32 devices in a mesh: ctx: 4 (over z), uly: 4 (over y, x), fsdp: 2 (over core).
Axes of the slice: x: 2, y: 2, z: 4, core: 2. Of those that a mesh axis runs over, the one named last changes fastest.
Arguments:
- tokens: bfloat16 [16384, 768], P(('ctx', 'uly', 'fsdp')), may hold values from -6 to 6
- teacher: bfloat16 [16384, 768], P(('ctx', 'uly', 'fsdp')), may hold values from -6 to 6
- cotangent: bfloat16 [16384, 768], P(('ctx', 'uly', 'fsdp')), may hold values from -6 to 6
- valid: int32 [16384], P(('ctx', 'uly', 'fsdp')), may hold values from 0 to 1, as said below
- teacher_ok: int32 [16384], P(('ctx', 'uly', 'fsdp')), may hold values 0 or 1
- doc_starts: int32 [34], replicated, may hold values from 0 to 16384, as said below
- w_query: bfloat16 [768, 768], P('fsdp'), may hold values from -0.21875 to 0.21875
- w_key: bfloat16 [768, 768], P('fsdp'), may hold values from -0.21875 to 0.21875
- w_value: bfloat16 [768, 768], P('fsdp'), may hold values from -0.21875 to 0.21875
- w_out: bfloat16 [768, 768], P('fsdp'), may hold values from -3 to 3
- w_in: bfloat16 [768, 3072], P('fsdp'), may hold values from -0.21875 to 0.21875
- w_back: bfloat16 [3072, 768], P('fsdp'), may hold values from -0.15625 to 0.15625
- bias_query: bfloat16 [768], P('fsdp'), may hold values from -1 to 1
- bias_value: bfloat16 [768], P('fsdp'), may hold values from -0.059814453 to 0.059814453
- bias_out: bfloat16 [768], P('fsdp'), may hold values from -0.3984375 to 0.3984375
- bias_in: bfloat16 [3072], P('fsdp'), may hold values from -1 to 1
- bias_back: bfloat16 [768], P('fsdp'), may hold values from -0.3984375 to 0.3984375
- norm1_gain: bfloat16 [768], P('fsdp'), may hold values from 0.25 to 1.75
- norm1_bias: bfloat16 [768], P('fsdp'), may hold values from -0.3984375 to 0.3984375
- norm2_gain: bfloat16 [768], P('fsdp'), may hold values from 0.25 to 1.75
- norm2_bias: bfloat16 [768], P('fsdp'), may hold values from -0.3984375 to 0.3984375
Outputs:
- out: bfloat16 [16384, 768], P(('ctx', 'uly', 'fsdp'))
- grad_tokens: float32 [16384, 768], P(('ctx', 'uly', 'fsdp'))
- grad_w_query: float32 [768, 768], P('fsdp')
- grad_w_key: float32 [768, 768], P('fsdp')
- grad_w_value: float32 [768, 768], P('fsdp')
- grad_w_out: float32 [768, 768], P('fsdp')
- grad_w_in: float32 [768, 3072], P('fsdp')
- grad_w_back: float32 [3072, 768], P('fsdp')
- grad_bias_query: float32 [768], P('fsdp')
- grad_bias_value: float32 [768], P('fsdp')
- grad_bias_out: float32 [768], P('fsdp')
- grad_bias_in: float32 [3072], P('fsdp')
- grad_bias_back: float32 [768], P('fsdp')
- grad_norm1_gain: float32 [768], P('fsdp')
- grad_norm1_bias: float32 [768], P('fsdp')
- grad_norm2_gain: float32 [768], P('fsdp')
- grad_norm2_bias: float32 [768], P('fsdp')
The draws below stay inside these ranges and needn't reach their ends.
Inputs may be any that keep to these rules, and one draw needn't show every extreme that they name: `doc_starts`: Ascending. The first entry is 0; each document runs from its start to the next start or to 16384; entries equal to 16384 start no document. Every document but the last has 512 to 2048 tokens, the last at most 2048; one has exactly 2048. `valid`: 1 at the first token of every document.
All inputs are finite; a program needn't handle non-finite values. No bound on the sum of `teacher_ok` on one device may be relied on, other than what follows from the above.
Results may differ from the reference program's by a relative error of at most 0.017.
Values may be sent and summed in bfloat16 or wider, within the bound.
No kernel may reach another device: no remote copies, remote signals or barrier semaphores. Data moves between devices by JAX's collectives and lax.ppermute only.
A program may use at most 448 MiB of HBM per device.

```python
import jax
import jax.numpy as jnp
from jax import lax

D = 768
HEADS = 12
HD = 64
FF = 3072
TOK_DEV = 512
DOC_MAX = 2048
TOKENS = 16384
NDOC = 34


def draw_layout(key):
    base_key = jax.random.fold_in(key, 11)
    lengths = jax.random.randint(jax.random.fold_in(base_key, 1), (NDOC,), DOC_MAX // 4, DOC_MAX + 1)
    chosen = jax.random.randint(jax.random.fold_in(base_key, 2), (), 0, TOKENS // DOC_MAX)
    lengths = jnp.where(jnp.arange(NDOC) == chosen, DOC_MAX, lengths)
    starts = jnp.cumsum(lengths) - lengths
    return jnp.minimum(starts, TOKENS).astype(jnp.int32)


def draw_doc_starts(key, part):
    return draw_layout(key)


def draw_valid(key, part):
    starts = draw_layout(key)
    positions = jnp.arange(TOKENS, dtype=jnp.int32)
    coin_draws = jax.random.randint(jax.random.fold_in(key, 23), (TOKENS,), 0, 4 * TOKENS)
    rising = (coin_draws < TOKENS + 2 * positions).astype(jnp.int32)
    first_rows = jnp.zeros((TOKENS,), jnp.int32).at[starts].max(1, mode='drop')
    return jnp.maximum(rising, first_rows)


def set_ends(values, own_key, low, top_value):
    shape = values.shape
    spot = [jax.random.randint(jax.random.fold_in(own_key, axis), (), 0, shape[axis]) for axis in range(len(shape))]
    values = values.at[tuple(spot)].set(low)
    longest = shape.index(max(shape))
    spot[longest] = (spot[longest] + 1) % shape[longest]
    return values.at[tuple(spot)].set(top_value)


def block_scale(own_key, shape, split, least, top_value):
    factor_of = 1.0
    for axis_at, parts in split:
        draws = jax.random.uniform(jax.random.fold_in(jax.random.fold_in(own_key, 6), axis_at), (parts,), jnp.float32, least / len(split), top_value / len(split))
        factor_of = factor_of * jnp.repeat(jnp.exp(draws), shape[axis_at] // parts).reshape((-1,) + (1,) * (len(shape) - 1 - axis_at))
    return factor_of


def bell_draw(stream_key, shape, deviation, reach, split=(), kind=jnp.bfloat16):
    loudness = block_scale(stream_key, shape, split, -0.22, 0.18) if split else 1.0
    values = jax.random.normal(stream_key, shape, jnp.float32) * deviation * loudness
    return jnp.minimum(jnp.maximum(values, -reach), reach).astype(kind)


def setup_inputs(seed: int = 0) -> dict:
    streams_of = jax.random.split(jax.random.key(seed), 22)
    tokens = bell_draw(streams_of[0], (TOKENS, D), 1.0, 6.0, ((0, 32),))
    teacher = bell_draw(streams_of[1], (TOKENS, D), 1.0, 6.0, ((0, 32),))
    cotangent = bell_draw(streams_of[2], (TOKENS, D), 1.0, 6.0, ((0, 32),))
    valid = draw_valid(jax.random.fold_in(streams_of[21], 71), 0)
    teacher_ok = set_ends((jax.random.randint(streams_of[4], (TOKENS,), 0, 4) < 3).astype(jnp.int32), jax.random.fold_in(streams_of[4], 1), 0, 1)
    doc_starts = draw_doc_starts(jax.random.fold_in(streams_of[21], 71), 0)
    w_query = bell_draw(streams_of[6], (D, D), D ** -0.5, 0.21875, ((0, 2),))
    w_key = bell_draw(streams_of[7], (D, D), D ** -0.5, 0.21875, ((0, 2),))
    w_value = bell_draw(streams_of[8], (D, D), D ** -0.5, 0.21875, ((0, 2),))
    w_out = bell_draw(streams_of[9], (D, D), 4 ** -0.5, 3.0, ((0, 2),))
    w_in = bell_draw(streams_of[10], (D, FF), D ** -0.5, 0.21875, ((0, 2),))
    w_back = bell_draw(streams_of[11], (FF, D), (FF // 2) ** -0.5, 0.15625, ((0, 2),))
    bias_query = bell_draw(streams_of[12], (D,), 0.2, 1.0, ((0, 2),))
    bias_value = bell_draw(streams_of[13], (D,), 0.015, 0.059814453, ((0, 2),))
    bias_out = bell_draw(streams_of[14], (D,), 0.1, 0.3984375, ((0, 2),))
    bias_in = bell_draw(streams_of[15], (FF,), 0.2, 1.0, ((0, 2),))
    bias_back = bell_draw(streams_of[16], (D,), 0.1, 0.3984375, ((0, 2),))
    norm1_gain = jnp.clip(1.0 + 0.15 * jax.random.normal(streams_of[17], (D,), jnp.float32), 0.25, 1.75).astype(jnp.bfloat16)
    norm1_bias = bell_draw(streams_of[18], (D,), 0.1, 0.3984375, ((0, 2),))
    norm2_gain = jnp.clip(1.0 + 0.15 * jax.random.normal(streams_of[19], (D,), jnp.float32), 0.25, 1.75).astype(jnp.bfloat16)
    norm2_bias = bell_draw(streams_of[20], (D,), 0.1, 0.3984375, ((0, 2),))
    return {"tokens": tokens, "teacher": teacher, "cotangent": cotangent, "valid": valid, "teacher_ok": teacher_ok, "doc_starts": doc_starts, "w_query": w_query, "w_key": w_key, "w_value": w_value, "w_out": w_out, "w_in": w_in, "w_back": w_back, "bias_query": bias_query, "bias_value": bias_value, "bias_out": bias_out, "bias_in": bias_in, "bias_back": bias_back, "norm1_gain": norm1_gain, "norm1_bias": norm1_bias, "norm2_gain": norm2_gain, "norm2_bias": norm2_bias}


@jax.custom_vjp
def low(v):
    return lax.optimization_barrier(v.astype(jnp.bfloat16)).astype(jnp.float32)

@jax.custom_vjp
def low_back(v):
    return v

def low_keep(v):
    return (low(v), None)

def low_pass(kept, grad):
    return (grad,)

def back_keep(v):
    return (v, None)

def back_low(kept, grad):
    return (low(grad),)
low.defvjp(low_keep, low_pass)
low_back.defvjp(back_keep, back_low)
MASKED = -1e+30

def matmul(left, right):
    return jnp.dot(left, right, precision=lax.Precision.HIGHEST)

def layer_norm(values, gain, shift):
    center = values - lax.optimization_barrier(jnp.mean(values, axis=-1, keepdims=True))
    spread = lax.optimization_barrier(jnp.mean(center * center, axis=-1, keepdims=True))
    return center * lax.rsqrt(spread + 1e-12) * gain + shift

def doc_index(positions, doc_starts):
    return lax.optimization_barrier(jnp.sum((doc_starts[None, :] <= positions[:, None]).astype(jnp.int32), axis=1)) - 1

def attention(queries, keys_all, values_all, doc_ids, valid):
    width = DOC_MAX
    window = TOK_DEV + 2 * width
    scale = HD ** (-0.5)
    q_three = queries.reshape(TOKENS, HEADS, HD)
    k_three = jnp.pad(keys_all.reshape(TOKENS, HEADS, HD), ((width, width), (0, 0), (0, 0)))
    v_three = jnp.pad(values_all.reshape(TOKENS, HEADS, HD), ((width, width), (0, 0), (0, 0)))
    ids_pad = jnp.pad(doc_ids, (width, width), constant_values=-2)
    valid_pad = jnp.pad(valid, (width, width))

    @jax.checkpoint
    def one_block(begin):
        q_blk = lax.dynamic_slice_in_dim(q_three, begin, TOK_DEV, 0)
        k_win = lax.dynamic_slice_in_dim(k_three, begin, window, 0)
        v_win = lax.dynamic_slice_in_dim(v_three, begin, window, 0)
        q_ids = lax.dynamic_slice_in_dim(doc_ids, begin, TOK_DEV, 0)
        k_ids = lax.dynamic_slice_in_dim(ids_pad, begin, window, 0)
        k_valid = lax.dynamic_slice_in_dim(valid_pad, begin, window, 0)
        allowed = (q_ids[:, None] == k_ids[None, :]) & (k_valid[None, :] > 0)
        scores = jnp.einsum('qhd,khd->hqk', q_blk, k_win, precision=lax.Precision.HIGHEST)
        scores = low_back(jnp.where(allowed[None], scale * scores, MASKED))
        attend = jax.nn.softmax(scores, axis=-1)
        return jnp.einsum('hqk,khd->qhd', low(attend), v_win, precision=lax.Precision.HIGHEST)
    begins = jnp.arange(TOKENS // TOK_DEV, dtype=jnp.int32) * TOK_DEV
    return lax.map(one_block, begins).reshape(TOKENS, D)

def reference(tokens, teacher, cotangent, valid, teacher_ok, doc_starts, w_query, w_key, w_value, w_out, w_in, w_back, bias_query, bias_value, bias_out, bias_in, bias_back, norm1_gain, norm1_bias, norm2_gain, norm2_bias):
    doc_ids = doc_index(jnp.arange(TOKENS, dtype=jnp.int32), doc_starts)
    count = jnp.sum(valid).astype(jnp.float32)
    loss_scale = jnp.float32(TOKENS) / count
    keep = (valid * teacher_ok).astype(jnp.float32)
    teacher_f = teacher.astype(jnp.float32)
    cot_f = cotangent.astype(jnp.float32)
    params = tuple((p.astype(jnp.float32) for p in (w_query, w_key, w_value, w_out, w_in, w_back, bias_query, bias_value, bias_out, bias_in, bias_back, norm1_gain, norm1_bias, norm2_gain, norm2_bias)))

    def forward(inputs, weights):
        wq_f, wk_f, wv_f, wo_f, win_f, wback_f, bq_f, bv_f, bo_f, bin_f, bback_f, gain_one, shift_one, gain_two, shift_two = weights
        queries = low_back(low(matmul(inputs, wq_f) + bq_f))
        keys_all = low_back(low(matmul(inputs, wk_f)))
        values_all = low_back(low(matmul(inputs, wv_f) + bv_f))
        attn = low_back(low(attention(queries, keys_all, values_all, doc_ids, valid)))
        proj = low_back(matmul(attn, wo_f) + bo_f)
        hidden = layer_norm(inputs + proj, gain_one, shift_one)
        pre_act = low_back(matmul(low(hidden), win_f) + bin_f)
        act_low = low(jax.nn.gelu(pre_act, approximate=False))
        branch = low_back(matmul(act_low, wback_f) + bback_f)
        result = layer_norm(hidden + branch, gain_two, shift_two)
        diff = result - teacher_f
        objective = jnp.sum(cot_f * result) + 0.5 * loss_scale * jnp.sum(keep[:, None] * diff * diff)
        return (objective, result)
    objective, pullback, result = jax.vjp(forward, tokens.astype(jnp.float32), params, has_aux=True)
    grad_in, grad_params = pullback(jnp.ones_like(objective))
    return (result.astype(jnp.bfloat16), grad_in) + tuple(grad_params)
```

```python
from functools import partial

import jax
import jax.numpy as jnp
from jax import lax
from jax.experimental import pallas as pl
from jax.experimental.pallas import tpu as pltpu
from jax.sharding import PartitionSpec as P

HEADS = 12
HD = 64
BLK = 512
TQ = 256
TK = 256
DOCS = 64
MASKED = -1e30
BF = jnp.bfloat16
F32 = jnp.float32
NT = (((1,), (1,)), ((), ()))
NN = (((1,), (0,)), ((), ()))
TN = (((0,), (0,)), ((), ()))


def mm(left, right, dims=NN):
    return lax.dot_general(left, right, dims, preferred_element_type=F32)


def layer_norm(values, gain, shift):
    center = values - jnp.mean(values, axis=-1, keepdims=True)
    spread = jnp.mean(center * center, axis=-1, keepdims=True)
    return center * lax.rsqrt(spread + 1e-12) * gain + shift


def lane_ids(rows):
    return lax.broadcasted_iota(jnp.int32, (rows, 128), 1)


def build_keys(sources, lo_ref, hi_ref, kaug, transposed, low_half):
    per = BLK // TK
    for at, kv in enumerate(sources):

        def one(j, _, at=at, kv=kv):
            rows = pl.ds(pl.multiple_of(j * TK, TK), TK)
            tile = at * (kv.shape[0] // TK) + j
            slot = at * (kv.shape[0] // BLK) + j // per
            out = pl.ds(pl.multiple_of(tile * TK, TK), TK)
            rank = lax.broadcasted_iota(jnp.int32, (TK, 128), 0) + lax.rem(j, per) * TK
            inside = (rank >= lo_ref[pl.ds(slot, 1), :]) & (rank < hi_ref[pl.ds(slot, 1), :])
            bias = jnp.where(inside, 0.0, MASKED).astype(BF)
            kaug[out, 0:128] = jnp.where(lane_ids(TK) < 64, bias, kv[rows, 128:256])
            kaug[out, 128:256] = kv[rows, 256:384]
            if low_half:
                transposed[tile] = kv[rows, 0:256].T[0:192]
            else:
                transposed[tile] = kaug[out, :].T[64:256]
            return 0

        lax.fori_loop(0, kv.shape[0] // TK, one, 0)


def stack_queries(q, first, slo_ref, shi_ref, qs):
    lane = lane_ids(TQ)
    spot = lax.broadcasted_iota(jnp.int32, (TQ, 128), 0) + first
    mine = ((spot >= slo_ref[...]) & (spot < shi_ref[...])).astype(F32).astype(BF)
    zero = jnp.zeros((TQ, 128), BF)
    low, high = q[:, 0:128], q[:, 128:256]
    mark = jnp.where(lane < 64, mine, zero)
    qs[0:TQ, 0:128] = jnp.where(lane < 64, mine, low)
    qs[TQ : 2 * TQ, 0:128] = mark
    qs[2 * TQ :, 0:128] = mark
    qs[0:TQ, 128:256] = zero
    qs[TQ : 2 * TQ, 128:256] = jnp.where(lane < 64, high, zero)
    qs[2 * TQ :, 128:256] = jnp.where(lane < 64, zero, high)


def attend_kernel(
    tlo, thi, qfirst, q_ref, kv0, kv1, kv2, kv3, lo_ref, hi_ref, slo_ref, shi_ref,
    o_ref, ot_ref, lse_ref, kaug, vt, qs, acc, m_s, l_s,
):
    build_keys((kv0, kv1, kv2, kv3), lo_ref, hi_ref, kaug, vt, True)
    slots = 4 * kv0.shape[0] // BLK
    per = BLK // TK

    def tile_loop(i, _):
        rows = pl.ds(pl.multiple_of(i * TQ, TQ), TQ)
        stack_queries(q_ref[rows, :], qfirst[i], slo_ref, shi_ref, qs)
        m_s[...] = jnp.full_like(m_s, 2 * MASKED)
        l_s[...] = jnp.zeros_like(l_s)
        acc[...] = jnp.zeros_like(acc)

        def slot_loop(s, _):
            def key_loop(t, _):
                tile = s * per + t
                keys = pl.ds(pl.multiple_of(tile * TK, TK), TK)
                st = mm(kaug[keys, :], qs[...], NT)
                m_old = m_s[...]
                m_new = jnp.maximum(m_old, jnp.max(st, axis=0, keepdims=True))
                fade = jnp.exp(m_old - m_new)
                p = jnp.exp(st - m_new)
                l_s[...] = l_s[...] * fade + jnp.sum(p, axis=0, keepdims=True)
                m_s[...] = m_new
                low = p.astype(BF)
                for h in range(3):
                    cols = slice(h * TQ, (h + 1) * TQ)
                    part = slice(h * HD, (h + 1) * HD)
                    acc[part, :] = acc[part, :] * fade[:, cols] + mm(vt[tile, part, :], low[:, cols])
                return 0

            return lax.fori_loop(tlo[i, s], thi[i, s], key_loop, 0)

        lax.fori_loop(0, slots, slot_loop, 0)
        total = l_s[...]
        for h in range(3):
            cols = slice(h * TQ, (h + 1) * TQ)
            part = slice(h * HD, (h + 1) * HD)
            acc[part, :] = acc[part, :] / total[:, cols]
        ot_ref[i] = acc[...]
        o_ref[rows, :] = acc[...].T.astype(BF)
        lse_ref[pl.ds(i, 1), :] = m_s[...] + jnp.log(total)
        return 0

    lax.fori_loop(0, q_ref.shape[0] // TQ, tile_loop, 0)


def whole(shape):
    return pl.BlockSpec(shape, lambda *_: (0,) * len(shape), pipeline_mode=pl.Buffered(1))


def attend(tables, q, sources):
    tlo, thi, qfirst, lo, hi, slo, shi = tables
    tiles = q.shape[0] // TQ
    keys = sum(s.shape[0] for s in sources)
    ins = (q, *sources, lo, hi, slo, shi)
    outs = (
        jax.ShapeDtypeStruct((q.shape[0], 3 * HD), BF),
        jax.ShapeDtypeStruct((tiles, 3 * HD, TQ), F32),
        jax.ShapeDtypeStruct((tiles, 3 * TQ), F32),
    )
    return pl.pallas_call(
        attend_kernel,
        out_shape=outs,
        grid_spec=pltpu.PrefetchScalarGridSpec(
            num_scalar_prefetch=3,
            grid=(1,),
            in_specs=[whole(x.shape) for x in ins],
            out_specs=tuple(whole(x.shape) for x in outs),
            scratch_shapes=[
                pltpu.VMEM((keys, 256), BF),
                pltpu.VMEM((keys // TK, 3 * HD, TK), BF),
                pltpu.VMEM((3 * TQ, 256), BF),
                pltpu.VMEM((3 * HD, TQ), F32),
                pltpu.VMEM((1, 3 * TQ), F32),
                pltpu.VMEM((1, 3 * TQ), F32),
            ],
        ),
        compiler_params=pltpu.CompilerParams(vmem_limit_bytes=48 << 20),
        cost_estimate=pl.CostEstimate(
            flops=12_000_000_000, bytes_accessed=12_000_000, transcendentals=10_000_000
        ),
        name="attend",
    )(tlo, thi, qfirst, *ins)


def attend_back_kernel(
    tlo, thi, qfirst, q_ref, do_ref, ot_ref, lse_ref, kv0, kv1, kv2, kv3, lo_ref, hi_ref, slo_ref, shi_ref,
    dq_ref, dkv0, dkv1, dkv2, dkv3, kaug, kt, vs, qs, dos, acc, dk_s, dv_s,
):
    sources = (kv0, kv1, kv2, kv3)
    build_keys(sources, lo_ref, hi_ref, kaug, kt, False)
    rows_each = kv0.shape[0]
    slots = 4 * rows_each // BLK
    per = BLK // TK
    for at, kv in enumerate(sources):
        vs[at * rows_each : (at + 1) * rows_each, :] = kv[:, 0:256]
    dk_s[...] = jnp.zeros_like(dk_s)
    dv_s[...] = jnp.zeros_like(dv_s)

    def tile_loop(i, _):
        rows = pl.ds(pl.multiple_of(i * TQ, TQ), TQ)
        stack_queries(q_ref[rows, :], qfirst[i], slo_ref, shi_ref, qs)
        do = do_ref[rows, :]
        lane = lane_ids(TQ)
        zero = jnp.zeros((TQ, 128), BF)
        dos[0:TQ, 0:128] = jnp.where(lane < 64, do[:, 0:128], zero)
        dos[TQ : 2 * TQ, 0:128] = jnp.where(lane < 64, zero, do[:, 0:128])
        dos[2 * TQ :, 0:128] = zero
        dos[0 : 2 * TQ, 128:256] = jnp.zeros((2 * TQ, 128), BF)
        dos[2 * TQ :, 128:192] = do[:, 128:192]
        dos[2 * TQ :, 192:256] = jnp.zeros((TQ, 64), BF)
        both = do.astype(F32).T * ot_ref[i]
        delta = jnp.concatenate(
            [jnp.sum(both[h * HD : (h + 1) * HD], axis=0, keepdims=True) for h in range(3)], axis=1
        )
        lse = lse_ref[pl.ds(i, 1), :]
        acc[...] = jnp.zeros_like(acc)

        def slot_loop(s, _):
            def key_loop(t, _):
                tile = s * per + t
                keys = pl.ds(pl.multiple_of(tile * TK, TK), TK)
                st = mm(kaug[keys, :], qs[...], NT)
                p = jnp.exp(st - lse)
                dp = mm(vs[keys, :], dos[...], NT)
                ds = (p * (dp - delta)).astype(BF)
                dv_s[keys, :] += mm(p.astype(BF), dos[...])
                dk_s[keys, :] += mm(ds, qs[...])
                for h in range(3):
                    cols = slice(h * TQ, (h + 1) * TQ)
                    acc[(h + 1) * HD : (h + 2) * HD, :] += mm(kt[tile, h * HD : (h + 1) * HD, :], ds[:, cols])
                return 0

            return lax.fori_loop(tlo[i, s], thi[i, s], key_loop, 0)

        lax.fori_loop(0, slots, slot_loop, 0)
        dq_ref[rows, :] = acc[...].T.astype(BF)
        return 0

    lax.fori_loop(0, q_ref.shape[0] // TQ, tile_loop, 0)
    for at, out in enumerate((dkv0, dkv1, dkv2, dkv3)):

        def finish(j, _, at=at, out=out):
            to = pl.ds(pl.multiple_of(j * TK, TK), TK)
            frm = pl.ds(pl.multiple_of(at * rows_each + j * TK, TK), TK)
            out[to, 0:128] = dv_s[frm, 0:128].astype(BF)
            out[to, 128:256] = jnp.where(lane_ids(TK) < 64, dv_s[frm, 128:256], dk_s[frm, 0:128]).astype(BF)
            out[to, 256:384] = dk_s[frm, 128:256].astype(BF)
            return 0

        lax.fori_loop(0, rows_each // TK, finish, 0)


def attend_back(tables, q, do, ot, lse, sources):
    tlo, thi, qfirst, lo, hi, slo, shi = tables
    keys = sum(s.shape[0] for s in sources)
    ins = (q, do, ot, lse, *sources, lo, hi, slo, shi)
    outs = (jax.ShapeDtypeStruct(q.shape, BF),) + tuple(jax.ShapeDtypeStruct(s.shape, BF) for s in sources)
    return pl.pallas_call(
        attend_back_kernel,
        out_shape=outs,
        grid_spec=pltpu.PrefetchScalarGridSpec(
            num_scalar_prefetch=3,
            grid=(1,),
            in_specs=[whole(x.shape) for x in ins],
            out_specs=tuple(whole(x.shape) for x in outs),
            scratch_shapes=[
                pltpu.VMEM((keys, 256), BF),
                pltpu.VMEM((keys // TK, 3 * HD, TK), BF),
                pltpu.VMEM((keys, 256), BF),
                pltpu.VMEM((3 * TQ, 256), BF),
                pltpu.VMEM((3 * TQ, 256), BF),
                pltpu.VMEM((256, TQ), F32),
                pltpu.VMEM((keys, 256), F32),
                pltpu.VMEM((keys, 256), F32),
            ],
        ),
        compiler_params=pltpu.CompilerParams(vmem_limit_bytes=62 << 20),
        cost_estimate=pl.CostEstimate(
            flops=30_000_000_000, bytes_accessed=24_000_000, transcendentals=10_000_000
        ),
        name="attend_back",
    )(tlo, thi, qfirst, *ins)


def swap(block, axis="fsdp"):
    return lax.ppermute(block, axis, [(0, 1), (1, 0)])


def shifted(block, axis, distance):
    devices = range(lax.axis_size(axis))
    route = [(i - distance, i) for i in devices if i - distance in devices]
    return lax.ppermute(block, axis, route)


def exchange(rows, axis):
    return lax.all_to_all(rows, axis, split_axis=0, concat_axis=0, tiled=True)


def spread_rows(rows, axis):
    count = lax.axis_size(axis)
    return exchange(jnp.broadcast_to(rows[None], (count, *rows.shape)).reshape(-1, rows.shape[1]), axis)


def sum_scatter(rows, axis):
    count = lax.axis_size(axis)
    got = exchange(rows, axis).reshape(count, -1, rows.shape[1])
    return sum(got[i].astype(F32) for i in range(count))


def pair_sum(grad, half):
    split = grad.astype(BF).reshape(2, -1, grad.shape[1])
    mine = lax.dynamic_index_in_dim(split, half, 0, keepdims=False)
    other = lax.dynamic_index_in_dim(split, 1 - half, 0, keepdims=False)
    return mine.astype(F32) + swap(other).astype(F32)


def reduce_all(grad, half):
    low = pair_sum(grad, half).astype(BF)
    low = sum_scatter(low, "uly").astype(BF)
    low = sum_scatter(low, "ctx").astype(BF)
    low = spread_rows(low, "ctx")
    return spread_rows(low, "uly").astype(F32)


def on_device(
    tokens, teacher, cotangent, valid, teacher_ok, doc_starts, w_query, w_key, w_value, w_out, w_in, w_back,
    bias_query, bias_value, bias_out, bias_in, bias_back, norm1_gain, norm1_bias, norm2_gain, norm2_bias,
):
    groups = lax.axis_size("uly")
    spans = lax.axis_size("ctx")
    rows, width = tokens.shape
    block = rows * groups * 2
    stream = block * spans
    ctx_index = lax.axis_index("ctx")
    uly_index = lax.axis_index("uly")
    half = lax.axis_index("fsdp")
    head_cols = width // groups
    half_groups = groups // 2

    valid_all = lax.all_gather(valid, ("ctx", "uly", "fsdp"), axis=0, tiled=True).reshape(-1, rows)
    x_plane = spread_rows(tokens, "uly")
    start_col = uly_index * head_cols
    cut = [lax.dynamic_slice_in_dim(w, start_col, head_cols, 1) for w in (w_query, w_value, w_key)]
    w_heads = lax.all_gather(
        jnp.concatenate([jnp.zeros((w_query.shape[0], 256 - head_cols), BF), *cut], axis=1), "fsdp", axis=0, tiled=True
    )
    wo_all = lax.all_gather(w_out, "fsdp", axis=0, tiled=True)
    win_all = lax.all_gather(w_in, "fsdp", axis=0, tiled=True)
    wback_all = lax.all_gather(w_back, "fsdp", axis=0, tiled=True)
    small = (bias_query, bias_value, bias_out, bias_in, bias_back, norm1_gain, norm1_bias, norm2_gain, norm2_bias)
    packed = jnp.concatenate([p.reshape(-1, 384) for p in small], axis=0)
    packed = jnp.stack([packed, swap(packed)])
    packed = jnp.stack([packed[half], packed[1 - half]], axis=0)
    vectors = []
    at = 0
    for p in small:
        n = p.shape[0] // 384
        vectors.append(packed[:, at : at + n].reshape(-1).astype(F32))
        at += n
    bq_all, bv_all, bo_all, bin_all, bback_all, gain_one, shift_one, gain_two, shift_two = vectors
    bias_heads = jnp.concatenate(
        [
            jnp.zeros((256 - head_cols,), F32),
            lax.dynamic_slice_in_dim(bq_all, start_col, head_cols, 0),
            lax.dynamic_slice_in_dim(bv_all, start_col, head_cols, 0),
            jnp.zeros((head_cols,), F32),
        ]
    )

    count = jnp.sum(valid_all).astype(F32)
    g_ids = jnp.arange(groups, dtype=jnp.int32)
    halo_plane = ctx_index + jnp.where(g_ids < half_groups, -1, 1)
    halo_group = jnp.where(g_ids < half_groups, g_ids + half_groups, g_ids - half_groups)
    plane_of = jnp.concatenate([jnp.full((2 * groups,), 1, jnp.int32) * ctx_index, halo_plane, halo_plane])
    group_of = jnp.concatenate([g_ids, g_ids, halo_group, halo_group])
    mine = jnp.full((groups,), 1, jnp.int32) * half
    core_of = jnp.concatenate([mine, 1 - mine, mine, 1 - mine])
    block_id = plane_of * (2 * groups) + group_of * 2 + core_of
    there = (plane_of >= 0) & (plane_of < spans)
    block_valid = jnp.take(valid_all, jnp.clip(block_id, 0, stream // rows - 1), axis=0) * there[:, None]
    spot = block_id[:, None] * rows + jnp.arange(rows, dtype=jnp.int32)[None, :]
    edges = jnp.concatenate([doc_starts, jnp.full((DOCS + 1,), stream, jnp.int32)])
    window_first = jnp.maximum(ctx_index * block - block // 2, 0)
    first_doc = jnp.sum((doc_starts <= window_first).astype(jnp.int32)) - 1
    near = lax.dynamic_slice_in_dim(edges, first_doc, DOCS + 1, 0)

    def counted(limits):
        return jnp.sum(block_valid[:, None, :] * (spot[:, None, :] < limits[None, :, None]), axis=-1)

    bounds = counted(near)
    pad64 = jnp.zeros((bounds.shape[0], 128 - DOCS), jnp.int32)
    lo_tab = jnp.concatenate([bounds[:, :DOCS], pad64], axis=1)
    hi_tab = jnp.concatenate([bounds[:, 1:], pad64], axis=1)
    slo_tab = jnp.concatenate([near[:DOCS], pad64[0]])[None, :]
    shi_tab = jnp.concatenate([near[1:], pad64[0]])[None, :]
    tiles = groups * rows // TQ
    tile_ids = jnp.arange(tiles, dtype=jnp.int32)
    per = rows // TQ
    qfirst = ctx_index * block + ((tile_ids // per) * 2 + half) * rows + lax.rem(tile_ids, per) * TQ
    started = near[None, :] <= qfirst[:, None]
    q_lo = jnp.max(jnp.where(started, near[None, :], 0), axis=1)
    q_hi = jnp.min(jnp.where(near[None, :] <= qfirst[:, None] + TQ - 1, stream, near[None, :]), axis=1)
    cnt_lo = counted(q_lo).T
    cnt_hi = counted(q_hi).T
    some = cnt_hi > cnt_lo
    tlo = jnp.where(some, cnt_lo // TK, 0)
    thi = jnp.where(some, (cnt_hi + TK - 1) // TK, 0)
    tables = (tlo, thi, qfirst, lo_tab, hi_tab, slo_tab, shi_tab)

    own_valid = block_valid[:groups]
    before = mm(own_valid.astype(BF), (jnp.arange(rows)[:, None] < jnp.arange(rows)[None, :]).astype(BF)).astype(jnp.int32)
    goes_to = jnp.where(own_valid > 0, before, rows)
    chosen = (goes_to[:, None, :] == jnp.arange(rows, dtype=jnp.int32)[None, :, None]).astype(BF)
    qvk = mm(x_plane, w_heads) + bias_heads
    q_low = qvk[:, :256].astype(BF) * jnp.asarray(HD ** (-0.5), BF)
    kv_tok = qvk[:, 256:].astype(BF).reshape(groups, rows, 2 * head_cols)
    kv_own = jnp.einsum("grt,gtk->grk", chosen, kv_tok, preferred_element_type=F32).astype(BF)
    kv_flat = kv_own.reshape(groups * rows, 2 * head_cols)
    middle = groups * rows // 2
    kv_pair = swap(kv_flat)
    kv_halo = jnp.concatenate([shifted(kv_flat[middle:], "ctx", 1), shifted(kv_flat[:middle], "ctx", -1)], axis=0)
    kv_halo_pair = swap(kv_halo)
    sources = (kv_flat, kv_pair, kv_halo, kv_halo_pair)
    o_heads, o_turned, lse = attend(tables, q_low, sources)
    o_parts = exchange(o_heads, "uly").reshape(groups, rows, head_cols)

    x_float = tokens.astype(F32)
    wo_parts = wo_all.reshape(groups, head_cols, width)
    proj = sum(mm(o_parts[i], wo_parts[i]) for i in range(groups))
    resid1 = x_float + proj + bo_all
    hidden = layer_norm(resid1, gain_one, shift_one)
    hidden_low = hidden.astype(BF)
    pre_act = mm(hidden_low, win_all) + bin_all
    gelu_exact = partial(jax.nn.gelu, approximate=False)
    act_low = gelu_exact(pre_act).astype(BF)
    resid2 = hidden + mm(act_low, wback_all) + bback_all
    result = layer_norm(resid2, gain_two, shift_two)
    loss_scale = jnp.float32(stream) / count
    keep = (valid * teacher_ok).astype(F32)
    grad_y = cotangent.astype(F32) + loss_scale * keep[:, None] * (result - teacher.astype(F32))
    d_resid2, d_gain_two, d_shift_two = jax.vjp(layer_norm, resid2, gain_two, shift_two)[1](grad_y)
    d_branch = d_resid2.astype(BF)
    d_bias_back = jnp.sum(d_branch.astype(F32), axis=0)
    d_w_back = mm(act_low, d_branch, TN)
    d_act = mm(d_branch, wback_all, NT)
    d_pre = jax.vjp(gelu_exact, pre_act)[1](d_act)[0].astype(BF)
    d_bias_in = jnp.sum(d_pre.astype(F32), axis=0)
    d_w_in = mm(hidden_low, d_pre, TN)
    d_hidden = d_resid2 + mm(d_pre, win_all, NT)
    d_resid1, d_gain_one, d_shift_one = jax.vjp(layer_norm, resid1, gain_one, shift_one)[1](d_hidden)
    d_proj = d_resid1.astype(BF)
    d_bias_out = jnp.sum(d_proj.astype(F32), axis=0)
    d_w_out = jnp.concatenate([mm(o_parts[i], d_proj, TN) for i in range(groups)], axis=0)
    d_parts = jnp.concatenate([mm(d_proj, wo_parts[i], NT).astype(BF) for i in range(groups)], axis=0)
    g_back = reduce_all(d_w_back, half)
    g_in = reduce_all(d_w_in, half)
    early = (d_bias_out, d_bias_in, d_bias_back, d_gain_one, d_shift_one, d_gain_two, d_shift_two)
    halves = jnp.concatenate([v.reshape(2, -1) for v in early], axis=1).reshape(2, -1, width)
    extra = jnp.pad(halves, ((0, 0), (0, 128 - halves.shape[1]), (0, 0)))
    out_pack = jnp.concatenate([d_w_out.reshape(2, -1, width), extra], axis=1).reshape(-1, width)
    g_out = reduce_all(out_pack, half)

    d_heads = exchange(d_parts, "uly")
    dq, dkv_own, dkv_pair, dkv_halo, dkv_halo_pair = attend_back(tables, q_low, d_heads, o_turned, lse, sources)
    halo_sum = (dkv_halo.astype(F32) + swap(dkv_halo_pair).astype(F32)).astype(BF)
    from_right = shifted(halo_sum[:middle], "ctx", -1)
    from_left = shifted(halo_sum[middle:], "ctx", 1)
    returned = jnp.concatenate([from_left, from_right], axis=0)
    dkv = (dkv_own.astype(F32) + swap(dkv_pair).astype(F32) + returned.astype(F32)).astype(BF)
    dkv_tok = jnp.einsum(
        "grt,grk->gtk", chosen, dkv.reshape(groups, rows, -1), preferred_element_type=F32
    ).astype(BF).reshape(groups * rows, -1)
    scale = jnp.asarray(HD ** (-0.5), BF)
    dq_low = dq * scale
    d_all = jnp.concatenate([dq_low, dkv_tok], axis=1)
    dx_part = mm(d_all, w_heads, NT).astype(BF)
    grad_in = d_resid1 + sum_scatter(dx_part, "uly")
    d_w_heads = mm(x_plane, d_all, TN)
    d_sums = jnp.sum(d_all.astype(F32), axis=0)
    n_cols = d_all.shape[1]
    sums_rows = jnp.pad(d_sums[None, None, :], ((0, 0), (0, 127), (0, 0)))
    pack = jnp.concatenate([d_w_heads.reshape(2, -1, n_cols), jnp.concatenate([sums_rows, sums_rows], 0)], axis=1)
    low = pair_sum(pack.reshape(-1, n_cols), half).astype(BF)
    low = sum_scatter(low, "ctx").astype(BF)
    low = spread_rows(low, "uly").reshape(groups, -1, n_cols)
    low = low.transpose(1, 0, 2).reshape(low.shape[1], groups * n_cols)
    g_heads = spread_rows(low, "ctx").reshape(-1, groups, n_cols)
    shard = w_query.shape[0]

    def columns(first, top, bottom):
        return g_heads[top:bottom, :, first : first + head_cols].reshape(bottom - top, width).astype(F32)

    g_query = columns(256 - head_cols, 0, shard)
    g_value = columns(256, 0, shard)
    g_key = columns(256 + head_cols, 0, shard)
    g_bias_q = lax.dynamic_slice_in_dim(columns(256 - head_cols, shard, shard + 1)[0], half * shard, shard, 0)
    g_bias_v = lax.dynamic_slice_in_dim(columns(256, shard, shard + 1)[0], half * shard, shard, 0)
    flat = g_out[shard:].reshape(-1)
    sizes = [v.shape[0] // 2 for v in early]
    cuts = [sum(sizes[:i]) for i in range(len(sizes))]
    g_bo, g_bin, g_bb, g_g1, g_s1, g_g2, g_s2 = [flat[a : a + n] for a, n in zip(cuts, sizes)]
    return (
        result.astype(BF), grad_in, g_query, g_key, g_value, g_out[:shard], g_in, g_back,
        g_bias_q, g_bias_v, g_bo, g_bin, g_bb, g_g1, g_s1, g_g2, g_s2,
    )


def solution(mesh):
    placed = (
        P(("ctx", "uly", "fsdp"), None),
        P(("ctx", "uly", "fsdp"), None),
        P(("ctx", "uly", "fsdp"), None),
        P(("ctx", "uly", "fsdp")),
        P(("ctx", "uly", "fsdp")),
        P(),
        P("fsdp", None),
        P("fsdp", None),
        P("fsdp", None),
        P("fsdp", None),
        P("fsdp", None),
        P("fsdp", None),
        P("fsdp"),
        P("fsdp"),
        P("fsdp"),
        P("fsdp"),
        P("fsdp"),
        P("fsdp"),
        P("fsdp"),
        P("fsdp"),
        P("fsdp"),
    )
    return jax.shard_map(
        on_device,
        mesh=mesh,
        in_specs=placed,
        out_specs=(
            P(("ctx", "uly", "fsdp"), None),
            P(("ctx", "uly", "fsdp"), None),
            P("fsdp", None),
            P("fsdp", None),
            P("fsdp", None),
            P("fsdp", None),
            P("fsdp", None),
            P("fsdp", None),
            P("fsdp"),
            P("fsdp"),
            P("fsdp"),
            P("fsdp"),
            P("fsdp"),
            P("fsdp"),
            P("fsdp"),
            P("fsdp"),
            P("fsdp"),
        ),
        check_vma=False,
    )
```

```python
import functools

import jax
import jax.numpy as jnp
from jax import lax
from jax.experimental import pallas as pl
from jax.experimental.pallas import tpu as pltpu
from jax.sharding import PartitionSpec as P

HEADS = 12
HD = 64
BLK = 512
TQ = 256
TK = 256
DOCS = 64
FFB = 768
MASKED = -1e30
BF = jnp.bfloat16
F32 = jnp.float32
NT = (((1,), (1,)), ((), ()))
NN = (((1,), (0,)), ((), ()))
TN = (((0,), (0,)), ((), ()))


def mm(left, right, dims=NN):
    return lax.dot_general(left, right, dims, preferred_element_type=F32)


def whole(shape):
    return pl.BlockSpec(shape, lambda *_: (0,) * len(shape), pipeline_mode=pl.Buffered(1))


def cost(flops, moved, special=0):
    return pl.CostEstimate(flops=flops, bytes_accessed=moved, transcendentals=special)


def lane_ids(rows):
    return lax.broadcasted_iota(jnp.int32, (rows, 128), 1)


def build_keys(sources, slot0, lo_ref, hi_ref, kaug, transposed, low_half):
    per = BLK // TK
    for at, kv in enumerate(sources):

        def one(j, _, at=at, kv=kv):
            rows = pl.ds(pl.multiple_of(j * TK, TK), TK)
            tile = at * (kv.shape[0] // TK) + j
            slot = slot0 + at * (kv.shape[0] // BLK) + j // per
            out = pl.ds(pl.multiple_of(tile * TK, TK), TK)
            rank = lax.broadcasted_iota(jnp.int32, (TK, 128), 0) + lax.rem(j, per) * TK
            inside = (rank >= lo_ref[pl.ds(slot, 1), :]) & (rank < hi_ref[pl.ds(slot, 1), :])
            bias = jnp.where(inside, 0.0, MASKED).astype(BF)
            kaug[out, 0:128] = jnp.where(lane_ids(TK) < 64, bias, kv[rows, 128:256])
            kaug[out, 128:256] = kv[rows, 256:384]
            if low_half:
                transposed[tile] = kv[rows, 0:256].T[0:192]
            else:
                transposed[tile] = kaug[out, :].T[64:256]
            return 0

        lax.fori_loop(0, kv.shape[0] // TK, one, 0)


def stack_queries(q, first, slo_ref, shi_ref, qs):
    lane = lane_ids(TQ)
    spot = lax.broadcasted_iota(jnp.int32, (TQ, 128), 0) + first
    mine = ((spot >= slo_ref[...]) & (spot < shi_ref[...])).astype(F32).astype(BF)
    zero = jnp.zeros((TQ, 128), BF)
    low, high = q[:, 0:128], q[:, 128:256]
    mark = jnp.where(lane < 64, mine, zero)
    qs[0:TQ, 0:128] = jnp.where(lane < 64, mine, low)
    qs[TQ : 2 * TQ, 0:128] = mark
    qs[2 * TQ :, 0:128] = mark
    qs[0:TQ, 128:256] = zero
    qs[TQ : 2 * TQ, 128:256] = jnp.where(lane < 64, high, zero)
    qs[2 * TQ :, 128:256] = jnp.where(lane < 64, zero, high)


def attend_kernel(*refs, slot0, count, resume, last):
    tlo, thi, qfirst, q_ref = refs[:4]
    sources = refs[4 : 4 + count]
    lo_ref, hi_ref, slo_ref, shi_ref = refs[4 + count : 8 + count]
    at = 8 + count
    if resume:
        acc_in, stat_in = refs[at : at + 2]
        at += 2
    if last:
        o_ref, ot_ref, lse_ref = refs[at : at + 3]
        at += 3
    else:
        acc_out, stat_out = refs[at : at + 2]
        at += 2
    kaug, vt, qs, acc, m_s, l_s = refs[at:]
    build_keys(sources, slot0, lo_ref, hi_ref, kaug, vt, True)
    slots = count * sources[0].shape[0] // BLK
    per = BLK // TK

    def tile_loop(i, _):
        rows = pl.ds(pl.multiple_of(i * TQ, TQ), TQ)
        stack_queries(q_ref[rows, :], qfirst[i], slo_ref, shi_ref, qs)
        if resume:
            m_s[...] = stat_in[i, 0:1, :]
            l_s[...] = stat_in[i, 1:2, :]
            acc[...] = acc_in[i]
        else:
            m_s[...] = jnp.full_like(m_s, 2 * MASKED)
            l_s[...] = jnp.zeros_like(l_s)
            acc[...] = jnp.zeros_like(acc)

        def slot_loop(s, _):
            def key_loop(t, _):
                tile = s * per + t
                keys = pl.ds(pl.multiple_of(tile * TK, TK), TK)
                st = mm(kaug[keys, :], qs[...], NT)
                m_old = m_s[...]
                m_new = jnp.maximum(m_old, jnp.max(st, axis=0, keepdims=True))
                fade = jnp.exp(m_old - m_new)
                p = jnp.exp(st - m_new)
                l_s[...] = l_s[...] * fade + jnp.sum(p, axis=0, keepdims=True)
                m_s[...] = m_new
                low = p.astype(BF)
                for h in range(3):
                    cols = slice(h * TQ, (h + 1) * TQ)
                    part = slice(h * HD, (h + 1) * HD)
                    acc[part, :] = acc[part, :] * fade[:, cols] + mm(vt[tile, part, :], low[:, cols])
                return 0

            return lax.fori_loop(tlo[i, slot0 + s], thi[i, slot0 + s], key_loop, 0)

        lax.fori_loop(0, slots, slot_loop, 0)
        if last:
            total = l_s[...]
            for h in range(3):
                cols = slice(h * TQ, (h + 1) * TQ)
                part = slice(h * HD, (h + 1) * HD)
                acc[part, :] = acc[part, :] / total[:, cols]
            ot_ref[i] = acc[...]
            o_ref[rows, :] = acc[...].T.astype(BF)
            lse_ref[pl.ds(i, 1), :] = m_s[...] + jnp.log(total)
        else:
            acc_out[i] = acc[...]
            stat_out[i, 0:1, :] = m_s[...]
            stat_out[i, 1:2, :] = l_s[...]
        return 0

    lax.fori_loop(0, q_ref.shape[0] // TQ, tile_loop, 0)


def attend(tables, q, sources, slot0, state=None, last=False):
    tlo, thi, qfirst, lo, hi, slo, shi = tables
    tiles = q.shape[0] // TQ
    keys = sum(s.shape[0] for s in sources)
    ins = (q, *sources, lo, hi, slo, shi) + (tuple(state) if state else ())
    if last:
        outs = (
            jax.ShapeDtypeStruct((q.shape[0], 3 * HD), BF),
            jax.ShapeDtypeStruct((tiles, 3 * HD, TQ), F32),
            jax.ShapeDtypeStruct((tiles, 3 * TQ), F32),
        )
    else:
        outs = (
            jax.ShapeDtypeStruct((tiles, 3 * HD, TQ), F32),
            jax.ShapeDtypeStruct((tiles, 2, 3 * TQ), F32),
        )
    return pl.pallas_call(
        functools.partial(attend_kernel, slot0=slot0, count=len(sources), resume=state is not None, last=last),
        out_shape=outs,
        grid_spec=pltpu.PrefetchScalarGridSpec(
            num_scalar_prefetch=3,
            grid=(1,),
            in_specs=[whole(x.shape) for x in ins],
            out_specs=tuple(whole(x.shape) for x in outs),
            scratch_shapes=[
                pltpu.VMEM((keys, 256), BF),
                pltpu.VMEM((keys // TK, 3 * HD, TK), BF),
                pltpu.VMEM((3 * TQ, 256), BF),
                pltpu.VMEM((3 * HD, TQ), F32),
                pltpu.VMEM((1, 3 * TQ), F32),
                pltpu.VMEM((1, 3 * TQ), F32),
            ],
        ),
        compiler_params=pltpu.CompilerParams(vmem_limit_bytes=40 << 20),
        cost_estimate=cost(12_000_000_000, 12_000_000, 10_000_000),
        name="attend_halo" if state else "attend_plane",
    )(tlo, thi, qfirst, *ins)


def attend_back_kernel(*refs, slot0, count, resume, last):
    tlo, thi, qfirst, q_ref, do_ref, ot_ref, lse_ref = refs[:7]
    sources = refs[7 : 7 + count]
    lo_ref, hi_ref, slo_ref, shi_ref = refs[7 + count : 11 + count]
    at = 11 + count
    if resume:
        acc_in = refs[at]
        at += 1
    dq_ref = refs[at]
    d_refs = refs[at + 1 : at + 1 + count]
    kaug, kt, vs, qs, dos, acc, dk_s, dv_s = refs[at + 1 + count :]
    build_keys(sources, slot0, lo_ref, hi_ref, kaug, kt, False)
    rows_each = sources[0].shape[0]
    slots = count * rows_each // BLK
    per = BLK // TK
    for j, kv in enumerate(sources):
        vs[j * rows_each : (j + 1) * rows_each, :] = kv[:, 0:256]
    dk_s[...] = jnp.zeros_like(dk_s)
    dv_s[...] = jnp.zeros_like(dv_s)

    def tile_loop(i, _):
        rows = pl.ds(pl.multiple_of(i * TQ, TQ), TQ)
        stack_queries(q_ref[rows, :], qfirst[i], slo_ref, shi_ref, qs)
        do = do_ref[rows, :]
        lane = lane_ids(TQ)
        zero = jnp.zeros((TQ, 128), BF)
        dos[0:TQ, 0:128] = jnp.where(lane < 64, do[:, 0:128], zero)
        dos[TQ : 2 * TQ, 0:128] = jnp.where(lane < 64, zero, do[:, 0:128])
        dos[2 * TQ :, 0:128] = zero
        dos[0 : 2 * TQ, 128:256] = jnp.zeros((2 * TQ, 128), BF)
        dos[2 * TQ :, 128:192] = do[:, 128:192]
        dos[2 * TQ :, 192:256] = jnp.zeros((TQ, 64), BF)
        both = do.astype(F32).T * ot_ref[i]
        delta = jnp.concatenate(
            [jnp.sum(both[h * HD : (h + 1) * HD], axis=0, keepdims=True) for h in range(3)], axis=1
        )
        lse = lse_ref[pl.ds(i, 1), :]
        if resume:
            acc[...] = acc_in[i]
        else:
            acc[...] = jnp.zeros_like(acc)

        def slot_loop(s, _):
            def key_loop(t, _):
                tile = s * per + t
                keys = pl.ds(pl.multiple_of(tile * TK, TK), TK)
                st = mm(kaug[keys, :], qs[...], NT)
                p = jnp.exp(st - lse)
                dp = mm(vs[keys, :], dos[...], NT)
                ds = (p * (dp - delta)).astype(BF)
                dv_s[keys, :] += mm(p.astype(BF), dos[...])
                dk_s[keys, :] += mm(ds, qs[...])
                for h in range(3):
                    cols = slice(h * TQ, (h + 1) * TQ)
                    acc[(h + 1) * HD : (h + 2) * HD, :] += mm(kt[tile, h * HD : (h + 1) * HD, :], ds[:, cols])
                return 0

            return lax.fori_loop(tlo[i, slot0 + s], thi[i, slot0 + s], key_loop, 0)

        lax.fori_loop(0, slots, slot_loop, 0)
        if last:
            dq_ref[rows, :] = acc[...].T.astype(BF)
        else:
            dq_ref[i] = acc[...]
        return 0

    lax.fori_loop(0, q_ref.shape[0] // TQ, tile_loop, 0)
    for j, out in enumerate(d_refs):

        def finish(k, _, j=j, out=out):
            to = pl.ds(pl.multiple_of(k * TK, TK), TK)
            frm = pl.ds(pl.multiple_of(j * rows_each + k * TK, TK), TK)
            out[to, 0:128] = dv_s[frm, 0:128].astype(BF)
            out[to, 128:256] = jnp.where(lane_ids(TK) < 64, dv_s[frm, 128:256], dk_s[frm, 0:128]).astype(BF)
            out[to, 256:384] = dk_s[frm, 128:256].astype(BF)
            return 0

        lax.fori_loop(0, rows_each // TK, finish, 0)


def attend_back(tables, q, do, ot, lse, sources, slot0, state=None, last=False, name="attend_back"):
    tlo, thi, qfirst, lo, hi, slo, shi = tables
    tiles = q.shape[0] // TQ
    keys = sum(s.shape[0] for s in sources)
    ins = (q, do, ot, lse, *sources, lo, hi, slo, shi) + ((state,) if state is not None else ())
    dq = jax.ShapeDtypeStruct(q.shape, BF) if last else jax.ShapeDtypeStruct((tiles, 256, TQ), F32)
    outs = (dq,) + tuple(jax.ShapeDtypeStruct(s.shape, BF) for s in sources)
    return pl.pallas_call(
        functools.partial(attend_back_kernel, slot0=slot0, count=len(sources), resume=state is not None, last=last),
        out_shape=outs,
        grid_spec=pltpu.PrefetchScalarGridSpec(
            num_scalar_prefetch=3,
            grid=(1,),
            in_specs=[whole(x.shape) for x in ins],
            out_specs=tuple(whole(x.shape) for x in outs),
            scratch_shapes=[
                pltpu.VMEM((keys, 256), BF),
                pltpu.VMEM((keys // TK, 3 * HD, TK), BF),
                pltpu.VMEM((keys, 256), BF),
                pltpu.VMEM((3 * TQ, 256), BF),
                pltpu.VMEM((3 * TQ, 256), BF),
                pltpu.VMEM((256, TQ), F32),
                pltpu.VMEM((keys, 256), F32),
                pltpu.VMEM((keys, 256), F32),
            ],
        ),
        compiler_params=pltpu.CompilerParams(vmem_limit_bytes=48 << 20),
        cost_estimate=cost(14_000_000_000, 16_000_000, 5_000_000),
        name=name,
    )(tlo, thi, qfirst, *ins)


def row_mean(v):
    return jnp.sum(v, axis=-1, keepdims=True) * (1.0 / v.shape[-1])

def dense_kernel(
    o_ref, wo_hbm, win_hbm, wback_hbm, x_ref, teacher_ref, cot_ref, keep_ref, vec_ref,
    out_ref, dres_ref, dparts_ref, act_ref, dbr_ref, dpre_ref, hid_ref, dproj_ref, sums_ref,
    wo, win, wback, xh, inv, hidden, gp, acc, sems, *, FB
):
    rows, width = x_ref.shape
    groups = o_ref.shape[0] // rows
    part = width // groups
    units = win.shape[1]
    loads = [pltpu.make_async_copy(a, b, sems.at[i]) for i, (a, b) in enumerate(((wo_hbm, wo), (win_hbm, win), (wback_hbm, wback)))]
    for load in loads:
        load.start()
    b_out, b_in, b_back = vec_ref[0:1, 0:width], vec_ref[1:2, :], vec_ref[2:3, 0:width]
    gain1, shift1, gain2, shift2 = (vec_ref[i : i + 1, 0:width] for i in range(3, 7))
    loads[0].wait()
    total = x_ref[...].astype(F32) + b_out
    for i in range(groups):
        total += mm(o_ref[i * rows : (i + 1) * rows, :], wo[i * part : (i + 1) * part, :])
    center = total - row_mean(total)
    scale = lax.rsqrt(row_mean(center * center) + 1e-12)
    inv[...] = scale
    unit = center * scale
    xh[...] = unit
    hid = unit * gain1 + shift1
    hidden[...] = hid
    hid_ref[...] = hid.astype(BF)
    acc[...] = jnp.zeros_like(acc)
    loads[1].wait()
    loads[2].wait()

    def up(n, _):
        cols = pl.ds(pl.multiple_of(n * FB, FB), FB)
        pre = mm(hid_ref[...], win[:, cols]) + vec_ref[1:2, cols]
        cdf = 0.5 + 0.5 * lax.erf(pre * 0.7071067811865476)
        act = (pre * cdf).astype(BF)
        act_ref[:, cols] = act
        gp[:, cols] = cdf + pre * (jnp.exp(pre * pre * -0.5) * 0.3989422804014327)
        acc[...] += mm(act, wback[cols, :])
        return 0

    lax.fori_loop(0, units // FB, up, 0, unroll=True)
    total = hidden[...] + acc[...] + b_back
    center = total - row_mean(total)
    scale = lax.rsqrt(row_mean(center * center) + 1e-12)
    unit = center * scale
    result = unit * gain2 + shift2
    out_ref[...] = result.astype(BF)
    grad = cot_ref[...].astype(F32) + keep_ref[...] * (result - teacher_ref[...].astype(F32))
    def put(row, value):
        sums_ref[row : row + 1, 0 : value.shape[1]] = value
    put(5, jnp.sum(grad * unit, axis=0, keepdims=True))
    put(6, jnp.sum(grad, axis=0, keepdims=True))
    grad = grad * gain2
    back = scale * (grad - row_mean(grad) - unit * row_mean(grad * unit))
    acc[...] = back
    low = back.astype(BF)
    dbr_ref[...] = low
    put(2, jnp.sum(low.astype(F32), axis=0, keepdims=True))

    def down(n, _):
        cols = pl.ds(pl.multiple_of(n * FB, FB), FB)
        dpre = (mm(dbr_ref[...], wback[cols, :], NT) * gp[:, cols]).astype(BF)
        dpre_ref[:, cols] = dpre
        sums_ref[1:2, cols] = jnp.sum(dpre.astype(F32), axis=0, keepdims=True)
        acc[...] += mm(dpre, win[:, cols], NT)
        return 0

    lax.fori_loop(0, units // FB, down, 0, unroll=True)
    grad = acc[...]
    unit = xh[...]
    put(3, jnp.sum(grad * unit, axis=0, keepdims=True))
    put(4, jnp.sum(grad, axis=0, keepdims=True))
    grad = grad * gain1
    back = inv[...] * (grad - row_mean(grad) - unit * row_mean(grad * unit))
    dres_ref[...] = back
    low = back.astype(BF)
    dproj_ref[...] = low
    put(0, jnp.sum(low.astype(F32), axis=0, keepdims=True))
    for i in range(groups):
        dparts_ref[i * rows : (i + 1) * rows, :] = mm(low, wo[i * part : (i + 1) * part, :], NT).astype(BF)


def dense(o, wo, win, wback, x, teacher, cot, keep, vec):
    rows, width = x.shape
    units = win.shape[1]
    sd = jax.ShapeDtypeStruct
    outs = (
        sd((rows, width), BF), sd((rows, width), F32), sd(o.shape, BF), sd((rows, units), BF), sd((rows, width), BF),
        sd((rows, units), BF), sd((rows, width), BF), sd((rows, width), BF), sd((8, units), F32),
    )
    ins = (o, wo, win, wback, x, teacher, cot, keep, vec)
    stay = pl.BlockSpec(memory_space=pl.ANY)
    return pl.pallas_call(
        functools.partial(dense_kernel, FB=FFB),
        out_shape=outs,
        grid=(1,),
        in_specs=[whole(o.shape), stay, stay, stay] + [whole(a.shape) for a in ins[4:]],
        out_specs=tuple(whole(a.shape) for a in outs),
        scratch_shapes=[
            pltpu.VMEM(wo.shape, BF), pltpu.VMEM(win.shape, BF), pltpu.VMEM(wback.shape, BF),
            pltpu.VMEM((rows, width), F32), pltpu.VMEM((rows, 1), F32), pltpu.VMEM((rows, width), F32),
            pltpu.VMEM((rows, units), F32), pltpu.VMEM((rows, width), F32), pltpu.SemaphoreType.DMA((3,)),
        ],
        compiler_params=pltpu.CompilerParams(vmem_limit_bytes=60 << 20),
        cost_estimate=cost(12_000_000_000, 30_000_000, 4_000_000),
        name="dense",
    )(*ins)


def back_grad_kernel(who, act_ref, dbr_ref, other_ref, mine_ref, *, each):
    value = mm(act_ref[...], dbr_ref[...], TN).astype(BF)
    step = pl.program_id(0)

    @pl.when(step < each)
    def _():
        other_ref[...] = value

    @pl.when(step >= each)
    def _():
        mine_ref[...] = value


def back_grad(half, act, dbr):
    rows, units = act.shape
    width = dbr.shape[1]
    tile = 512
    each = units // 2 // tile
    out = jax.ShapeDtypeStruct((units // 2, width), BF)
    return pl.pallas_call(
        functools.partial(back_grad_kernel, each=each),
        out_shape=(out, out),
        grid_spec=pltpu.PrefetchScalarGridSpec(
            num_scalar_prefetch=1,
            grid=(2 * each,),
            in_specs=[
                pl.BlockSpec((rows, tile), lambda j, who: (0, jnp.where(j < each, 1 - who[0], who[0]) * each + lax.rem(j, each))),
                pl.BlockSpec((rows, width), lambda j, who: (0, 0)),
            ],
            out_specs=(
                pl.BlockSpec((tile, width), lambda j, who: (jnp.minimum(j, each - 1), 0)),
                pl.BlockSpec((tile, width), lambda j, who: (jnp.maximum(j - each, 0), 0)),
            ),
        ),
        cost_estimate=cost(2_400_000_000, 9_000_000),
        name="back_grad",
    )(half, act, dbr)


def in_grad_kernel(who, hid_ref, dpre_ref, o_ref, dproj_ref, other_ref, mine_ref, *, each):
    step = pl.program_id(0)
    place = lax.rem(step, each)
    rows = dproj_ref.shape[0]
    part = o_ref.shape[1]

    def keep(low, high, value):
        @pl.when(step < each)
        def _():
            other_ref[low:high, :] = value

        @pl.when(step >= each)
        def _():
            mine_ref[low:high, :] = value

    @pl.when(place < each - 1)
    def _():
        keep(0, 2 * part, mm(hid_ref[...], dpre_ref[...], TN).astype(BF))

    @pl.when(place == each - 1)
    def _():
        half = jnp.where(step < each, 1 - who[0], who[0])
        for e in range(2):
            spot = (2 * half + e) ^ who[1]
            piece = o_ref[pl.ds(pl.multiple_of(spot * rows, rows), rows), :]
            keep(e * part, (e + 1) * part, mm(piece, dproj_ref[...], TN).astype(BF))


def in_grad(half, hid, dpre, o, dproj):
    rows, width = hid.shape
    blocks = dpre.shape[1] // width
    each = blocks + 1
    tall = width // 2
    out = jax.ShapeDtypeStruct((each * tall, width), BF)
    return pl.pallas_call(
        functools.partial(in_grad_kernel, each=each),
        out_shape=(out, out),
        grid_spec=pltpu.PrefetchScalarGridSpec(
            num_scalar_prefetch=1,
            grid=(2 * each,),
            in_specs=[
                pl.BlockSpec((rows, tall), lambda j, who: (0, jnp.where(j < each, 1 - who[0], who[0]))),
                pl.BlockSpec((rows, width), lambda j, who: (0, jnp.minimum(lax.rem(j, each), blocks - 1))),
                pl.BlockSpec(o.shape, lambda j, who: (0, 0)),
                pl.BlockSpec((rows, width), lambda j, who: (0, 0)),
            ],
            out_specs=(
                pl.BlockSpec((tall, width), lambda j, who: (jnp.minimum(j, each - 1), 0)),
                pl.BlockSpec((tall, width), lambda j, who: (jnp.maximum(j - each, 0), 0)),
            ),
        ),
        cost_estimate=cost(3_000_000_000, 12_000_000),
        name="in_grad",
    )(half, hid, dpre, o, dproj)


def swap(block, axis="fsdp"):
    return lax.ppermute(block, axis, [(0, 1), (1, 0)])


def shifted(block, axis, distance):
    devices = range(lax.axis_size(axis))
    route = [(i - distance, i) for i in devices if i - distance in devices]
    return lax.ppermute(block, axis, route)


def flip(block, bit, axis="uly"):
    return lax.ppermute(block, axis, [(i, i ^ bit) for i in range(lax.axis_size(axis))])


def exchange(rows, axis):
    return lax.all_to_all(rows, axis, split_axis=0, concat_axis=0, tiled=True)


def spread_rows(rows, axis):
    count = lax.axis_size(axis)
    return exchange(jnp.broadcast_to(rows[None], (count, *rows.shape)).reshape(-1, rows.shape[1]), axis)


def sum_scatter(rows, axis):
    count = lax.axis_size(axis)
    got = exchange(rows, axis).reshape(count, -1, rows.shape[1])
    return sum(got[i].astype(F32) for i in range(count)).astype(BF)


def add(left, right):
    return (left.astype(F32) + right.astype(F32)).astype(BF)


def sides(rows, bit):
    side = jnp.where((lax.axis_index("uly") & bit) > 0, 1, 0)
    split = rows.reshape(2, -1, rows.shape[1])
    return (
        lax.dynamic_index_in_dim(split, side, 0, keepdims=False),
        lax.dynamic_index_in_dim(split, 1 - side, 0, keepdims=False),
    )


def halve(rows, bit):
    mine, other = sides(rows, bit)
    return add(mine, flip(other, bit))


def double(rows, bit):
    low = (lax.axis_index("uly") & bit) == 0
    got = flip(rows, bit)
    return jnp.concatenate([jnp.where(low, rows, got), jnp.where(low, got, rows)], axis=0)


def halves(rows):
    middle = rows.shape[0] // 2
    return rows[:middle], rows[middle:]


def tie(*values):
    return lax.optimization_barrier(values)


def on_device(
    tokens, teacher, cotangent, valid, teacher_ok, doc_starts, w_query, w_key, w_value, w_out, w_in, w_back,
    bias_query, bias_value, bias_out, bias_in, bias_back, norm1_gain, norm1_bias, norm2_gain, norm2_bias,
):
    groups = lax.axis_size("uly")
    spans = lax.axis_size("ctx")
    rows, width = tokens.shape
    block = rows * groups * 2
    stream = block * spans
    ctx_index = lax.axis_index("ctx")
    uly = lax.axis_index("uly")
    half = lax.axis_index("fsdp")
    head_cols = width // groups
    shard = w_query.shape[0]
    middle = groups * rows // 2
    upper = uly // 2

    valid_one = valid[None, :]
    valid_own = jnp.concatenate([valid_one, flip(valid_one, 1), flip(valid_one, 2), flip(valid_one, 3)], axis=0)
    x_own, valid_own = tie(tokens, valid_own)
    x_x, x_y = flip(x_own, 1), flip(x_own, 2)
    x_top, x_bottom = flip(x_y[: rows // 2], 1), flip(x_x[rows // 2 :], 2)
    x_plane = (x_own, x_x, x_y, jnp.concatenate([x_top, x_bottom], axis=0))
    valid_pair = swap(valid_own)
    valid_both = jnp.stack([valid_own, valid_pair]).reshape(2, 2, 2, rows)
    valid_high = lax.dynamic_index_in_dim(valid_both, 1 - upper, 1, keepdims=False)
    valid_low = lax.dynamic_index_in_dim(valid_both, upper, 1, keepdims=False)
    halo = (shifted(valid_high, "ctx", 1), shifted(valid_low, "ctx", -1))
    block_valid = jnp.concatenate([valid_own, valid_pair, halo[0][0], halo[1][0], halo[0][1], halo[1][1]], axis=0)
    count = jnp.full((8, 128), jnp.sum(valid_both), jnp.int32)
    bit = 1
    while bit < spans:
        count = count + flip(count, bit, "ctx")
        bit *= 2
    count = count[0, 0].astype(F32)

    start_col = uly * head_cols
    cut = [lax.dynamic_slice_in_dim(w, start_col, head_cols, 1) for w in (w_query, w_value, w_key)]
    w_heads = lax.all_gather(
        jnp.concatenate([jnp.zeros((shard, 256 - head_cols), BF), *cut], axis=1), "fsdp", axis=0, tiled=True
    )
    wo_all = lax.all_gather(w_out, "fsdp", axis=0, tiled=True)
    win_all = lax.all_gather(w_in, "fsdp", axis=0, tiled=True)
    wback_all = lax.all_gather(w_back, "fsdp", axis=0, tiled=True)
    small = (bias_query, bias_value, bias_out, bias_in, bias_back, norm1_gain, norm1_bias, norm2_gain, norm2_bias)
    packed = jnp.concatenate([p.reshape(-1, shard) for p in small], axis=0)
    packed_pair = swap(packed)
    packed = jnp.stack([jnp.where(half == 0, packed, packed_pair), jnp.where(half == 0, packed_pair, packed)])
    vectors = []
    at = 0
    for p in small:
        n = p.shape[0] // shard
        vectors.append(packed[:, at : at + n].reshape(-1).astype(F32))
        at += n
    bq_all, bv_all = vectors[:2]
    vec = jnp.stack([jnp.pad(v, (0, w_in.shape[1] - v.shape[0])) for v in vectors[2:]] + [jnp.zeros((w_in.shape[1],), F32)])
    bias_heads = jnp.concatenate(
        [
            jnp.zeros((256 - head_cols,), F32),
            lax.dynamic_slice_in_dim(bq_all, start_col, head_cols, 0),
            lax.dynamic_slice_in_dim(bv_all, start_col, head_cols, 0),
            jnp.zeros((head_cols,), F32),
        ]
    )

    place = jnp.arange(groups, dtype=jnp.int32)
    two = jnp.arange(2, dtype=jnp.int32)
    in_plane = place ^ uly
    halo_group = jnp.concatenate([uly ^ (2 * (1 - upper) + two), uly ^ (2 * upper + two)])
    halo_plane = ctx_index + jnp.where(place < 2, -1, 1)
    plane_of = jnp.concatenate([jnp.full((2 * groups,), 1, jnp.int32) * ctx_index, halo_plane, halo_plane])
    group_of = jnp.concatenate([in_plane, in_plane, halo_group, halo_group])
    mine = jnp.full((groups,), 1, jnp.int32) * half
    core_of = jnp.concatenate([mine, 1 - mine, mine, 1 - mine])
    block_id = plane_of * (2 * groups) + group_of * 2 + core_of
    spot = block_id[:, None] * rows + jnp.arange(rows, dtype=jnp.int32)[None, :]
    edges = jnp.concatenate([doc_starts, jnp.full((DOCS + 1,), stream, jnp.int32)])
    window_first = jnp.maximum(ctx_index * block - block // 2, 0)
    first_doc = jnp.sum((doc_starts <= window_first).astype(jnp.int32)) - 1
    near = lax.dynamic_slice_in_dim(edges, first_doc, DOCS + 1, 0)
    tiles = groups * rows // TQ
    per = rows // TQ
    tile_ids = jnp.arange(tiles, dtype=jnp.int32)
    qfirst = ctx_index * block + (((tile_ids // per) ^ uly) * 2 + half) * rows + lax.rem(tile_ids, per) * TQ
    q_lo = jnp.max(jnp.where(near[None, :] <= qfirst[:, None], near[None, :], 0), axis=1)
    q_hi = jnp.min(jnp.where(near[None, :] <= qfirst[:, None] + TQ - 1, stream, near[None, :]), axis=1)
    limits = jnp.concatenate([near, q_lo, q_hi])
    counted = jnp.sum(block_valid[:, None, :] * (spot[:, None, :] < limits[None, :, None]), axis=-1)
    bounds = counted[:, : DOCS + 1]
    cnt_lo = counted[:, DOCS + 1 : DOCS + 1 + tiles].T
    cnt_hi = counted[:, DOCS + 1 + tiles :].T
    pad64 = jnp.zeros((bounds.shape[0], 128 - DOCS), jnp.int32)
    lo_tab = jnp.concatenate([bounds[:, :DOCS], pad64], axis=1)
    hi_tab = jnp.concatenate([bounds[:, 1:], pad64], axis=1)
    slo_tab = jnp.concatenate([near[:DOCS], pad64[0]])[None, :]
    shi_tab = jnp.concatenate([near[1:], pad64[0]])[None, :]
    some = cnt_hi > cnt_lo
    tlo = jnp.where(some, cnt_lo // TK, 0)
    thi = jnp.where(some, (cnt_hi + TK - 1) // TK, 0)
    tables = (tlo, thi, qfirst, lo_tab, hi_tab, slo_tab, shi_tab)
    before = mm(valid_own.astype(BF), (jnp.arange(rows)[:, None] < jnp.arange(rows)[None, :]).astype(BF)).astype(jnp.int32)
    goes_to = jnp.where(valid_own > 0, before, rows)
    chosen = (goes_to[:, None, :] == jnp.arange(rows, dtype=jnp.int32)[None, :, None]).astype(BF)
    loss_scale = jnp.float32(stream) / count
    keep = (loss_scale * (valid * teacher_ok).astype(F32))[:, None]
    wo_parts = jnp.take(wo_all.reshape(groups, head_cols, width), in_plane, axis=0).reshape(width, width)

    scale = jnp.asarray(HD ** (-0.5), BF)
    qvk = [mm(x, w_heads) + bias_heads for x in x_plane]
    q_low = jnp.concatenate([t[:, :256].astype(BF) for t in qvk], axis=0) * scale
    kv_own = jnp.concatenate([mm(chosen[d], qvk[d][:, 256:].astype(BF)).astype(BF) for d in range(groups)], axis=0)
    kv_split = kv_own.reshape(2, middle, 2 * head_cols)
    kv_halo = jnp.concatenate(
        [
            shifted(lax.dynamic_index_in_dim(kv_split, 1 - upper, 0, keepdims=False), "ctx", 1),
            shifted(lax.dynamic_index_in_dim(kv_split, upper, 0, keepdims=False), "ctx", -1),
        ],
        axis=0,
    )
    kv_pair = swap(kv_own)
    kv_halo_pair = swap(kv_halo)
    state = attend(tables, q_low, (kv_own, kv_pair), 0)
    o_heads, o_turned, lse = attend(tables, q_low, (kv_halo, kv_halo_pair), 2 * groups, state, last=True)
    o_rel = o_heads.reshape(groups, rows, head_cols)
    o_all = jnp.concatenate([o_rel[0]] + [flip(o_rel[d], d) for d in range(1, groups)], axis=0)

    out, d_resid1, d_parts, act, d_branch, d_pre, hidden_low, d_proj, sums = dense(
        o_all, wo_parts, win_all, wback_all, tokens, teacher, cotangent, keep, vec
    )
    d_rel = d_parts.reshape(groups, rows, head_cols)
    d_heads = jnp.concatenate([d_rel[0]] + [flip(d_rel[d], d) for d in range(1, groups)], axis=0)
    who = jnp.stack([half, uly])
    back_other, back_mine = back_grad(who, act, d_branch)
    in_other, in_mine = in_grad(who, hidden_low, d_pre, o_all, d_proj)
    vector_rows = jnp.concatenate(
        [sums[i, :width].reshape(2, -1) for i in (0, 2, 3, 4, 5, 6)] + [sums[1].reshape(2, -1)], axis=1
    ).reshape(2, -1, width)
    vector_rows = jnp.pad(vector_rows, ((0, 0), (0, 128 - vector_rows.shape[1]), (0, 0))).astype(BF)
    vec_mine = lax.dynamic_index_in_dim(vector_rows, half, 0, keepdims=False)
    vec_other = lax.dynamic_index_in_dim(vector_rows, 1 - half, 0, keepdims=False)
    back_sum = add(back_mine, swap(back_other))
    in_sum = jnp.concatenate([add(in_mine, swap(in_other)), add(vec_mine, swap(vec_other))], axis=0)

    d_heads, back_sum = tie(d_heads, back_sum)
    b1, b2 = halves(back_sum)
    b1, b2 = halve(b1, 1), halve(b2, 2)
    args = (tables, q_low, d_heads, o_turned, lse)
    dq_state, dkv_halo, dkv_halo_pair = attend_back(*args, (kv_halo, kv_halo_pair), 2 * groups, name="back_halo")
    dq_state, b1, b2, in_sum = tie(dq_state, b1, b2, in_sum)
    b1, b2 = halve(b1, 2), halve(b2, 1)
    i1, i2 = halves(in_sum)
    i1, i2 = halve(i1, 1), halve(i2, 2)
    halo_sum = add(dkv_halo, swap(dkv_halo_pair))
    dq_state, dkv_pair = attend_back(*args, (kv_pair,), groups, dq_state, name="back_pair")
    dq_state, b1, b2, i1, i2, halo_sum = tie(dq_state, b1, b2, i1, i2, halo_sum)
    back_line = sum_scatter(jnp.concatenate([b1, b2], axis=0), "ctx")
    i1, i2 = halve(i1, 2), halve(i2, 1)
    from_left = shifted(halo_sum[middle:], "ctx", 1)
    from_right = shifted(halo_sum[:middle], "ctx", -1)
    returned = jnp.stack([jnp.where(upper == 0, from_left, from_right), jnp.where(upper == 0, from_right, from_left)])
    pair_back = swap(dkv_pair)
    dq, dkv_own = attend_back(*args, (kv_own,), 0, dq_state, last=True, name="back_own")
    dkv = (
        dkv_own.astype(F32) + pair_back.astype(F32) + returned.reshape(dkv_own.shape).astype(F32)
    ).astype(BF).reshape(groups, rows, -1)
    d_all = [
        jnp.concatenate([dq[d * rows : (d + 1) * rows] * scale, mm(chosen[d], dkv[d], TN).astype(BF)], axis=1)
        for d in range(groups)
    ]

    d_w_heads = sum(mm(x_plane[d], d_all[d], TN) for d in range(groups))
    d_sums = sum(jnp.sum(d.astype(F32), axis=0) for d in d_all)
    n_cols = d_sums.shape[0]
    bottom = jnp.pad(d_sums[None, :], ((0, 63), (0, 0)))
    pack = jnp.stack([jnp.concatenate([d_w_heads[i * shard : (i + 1) * shard], bottom], axis=0) for i in range(2)]).astype(BF)
    heads_sum = add(
        lax.dynamic_index_in_dim(pack, half, 0, keepdims=False),
        swap(lax.dynamic_index_in_dim(pack, 1 - half, 0, keepdims=False)),
    )
    heads_sum = spread_rows(sum_scatter(heads_sum, "ctx"), "ctx")
    heads_all = jnp.stack([heads_sum] + [flip(heads_sum, d) for d in range(1, groups)])
    heads_all = jnp.take(heads_all, in_plane, axis=0)
    dx = [mm(d, w_heads, NT).astype(BF) for d in d_all]
    cut_at = width // 2
    give_x = flip(jnp.concatenate([dx[1][:, :cut_at], dx[3][:, :cut_at]], axis=0), 1)
    give_y = flip(jnp.concatenate([dx[2][:, cut_at:], dx[3][:, cut_at:]], axis=0), 2)
    left_own = dx[0][:, :cut_at].astype(F32) + give_x[:rows].astype(F32)
    right_own = dx[0][:, cut_at:].astype(F32) + give_y[:rows].astype(F32)
    left_next = flip(add(dx[2][:, :cut_at], give_x[rows:]), 2)
    right_next = flip(add(dx[1][:, cut_at:], give_y[rows:]), 1)
    grad_in = d_resid1 + jnp.concatenate(
        [left_own + left_next.astype(F32), right_own + right_next.astype(F32)], axis=1
    )

    b1, b2 = halves(spread_rows(back_line, "ctx"))
    b1, b2 = double(b1, 2), double(b2, 1)
    b1, b2 = double(b1, 1), double(b2, 2)
    g_back = jnp.concatenate([b1, b2], axis=0).astype(F32)
    in_line = spread_rows(sum_scatter(jnp.concatenate([i1, i2], axis=0), "ctx"), "ctx")
    i1, i2 = halves(in_line)
    i1, i2 = double(i1, 2), double(i2, 1)
    i1, i2 = double(i1, 1), double(i2, 2)
    in_all = jnp.concatenate([i1, i2], axis=0)
    n_in = w_in.shape[1] // width
    g_in = in_all[: n_in * shard].reshape(n_in, shard, width).transpose(1, 0, 2).reshape(shard, n_in * width).astype(F32)
    g_out = in_all[n_in * shard : (n_in + 1) * shard].astype(F32)
    flat = in_all[(n_in + 1) * shard :].reshape(-1).astype(F32)
    g_bo, g_bb, g_g1, g_s1, g_g2, g_s2 = [flat[i * shard : (i + 1) * shard] for i in range(6)]
    g_bin = flat[6 * shard : 6 * shard + bias_in.shape[0]]

    def columns(first, top, bottom):
        piece = heads_all[:, top:bottom, first : first + head_cols]
        return piece.transpose(1, 0, 2).reshape(bottom - top, width).astype(F32)

    g_query, g_value, g_key = [columns(256 - head_cols + i * head_cols, 0, shard) for i in range(3)]
    g_bias_q, g_bias_v = [
        lax.dynamic_slice_in_dim(columns(256 - head_cols + i * head_cols, shard, shard + 1)[0], half * shard, shard, 0)
        for i in range(2)
    ]
    return (
        out, grad_in, g_query, g_key, g_value, g_out, g_in, g_back,
        g_bias_q, g_bias_v, g_bo, g_bin, g_bb, g_g1, g_s1, g_g2, g_s2,
    )


def solution(mesh):
    placed = (
        P(("ctx", "uly", "fsdp"), None),
        P(("ctx", "uly", "fsdp"), None),
        P(("ctx", "uly", "fsdp"), None),
        P(("ctx", "uly", "fsdp")),
        P(("ctx", "uly", "fsdp")),
        P(),
        P("fsdp", None),
        P("fsdp", None),
        P("fsdp", None),
        P("fsdp", None),
        P("fsdp", None),
        P("fsdp", None),
        P("fsdp"),
        P("fsdp"),
        P("fsdp"),
        P("fsdp"),
        P("fsdp"),
        P("fsdp"),
        P("fsdp"),
        P("fsdp"),
        P("fsdp"),
    )
    return jax.shard_map(
        on_device,
        mesh=mesh,
        in_specs=placed,
        out_specs=(
            P(("ctx", "uly", "fsdp"), None),
            P(("ctx", "uly", "fsdp"), None),
            P("fsdp", None),
            P("fsdp", None),
            P("fsdp", None),
            P("fsdp", None),
            P("fsdp", None),
            P("fsdp", None),
            P("fsdp"),
            P("fsdp"),
            P("fsdp"),
            P("fsdp"),
            P("fsdp"),
            P("fsdp"),
            P("fsdp"),
            P("fsdp"),
            P("fsdp"),
        ),
        check_vma=False,
    )
```

```python
import functools

import jax
import jax.numpy as jnp
from jax import lax
from jax.experimental import pallas as pl
from jax.experimental.pallas import tpu as pltpu
from jax.sharding import PartitionSpec as P

HEADS = 12
HD = 64
BLK = 512
TQ = 256
TK = 256
DOCS = 64
FFB = 768
MASKED = -1e30
BF = jnp.bfloat16
F32 = jnp.float32
NT = (((1,), (1,)), ((), ()))
NN = (((1,), (0,)), ((), ()))
TN = (((0,), (0,)), ((), ()))


def mm(left, right, dims=NN):
    return lax.dot_general(left, right, dims, preferred_element_type=F32)


def whole(shape):
    return pl.BlockSpec(shape, lambda *_: (0,) * len(shape), pipeline_mode=pl.Buffered(1))


def cost(flops, moved, special=0):
    return pl.CostEstimate(flops=flops, bytes_accessed=moved, transcendentals=special)


def lane_ids(rows):
    return lax.broadcasted_iota(jnp.int32, (rows, 128), 1)


def build_keys(sources, slot0, lo_ref, hi_ref, kaug, transposed, low_half):
    per = BLK // TK
    for at, kv in enumerate(sources):

        def one(j, _, at=at, kv=kv):
            rows = pl.ds(pl.multiple_of(j * TK, TK), TK)
            tile = at * (kv.shape[0] // TK) + j
            slot = slot0 + at * (kv.shape[0] // BLK) + j // per
            out = pl.ds(pl.multiple_of(tile * TK, TK), TK)
            rank = lax.broadcasted_iota(jnp.int32, (TK, 128), 0) + lax.rem(j, per) * TK
            inside = (rank >= lo_ref[pl.ds(slot, 1), :]) & (rank < hi_ref[pl.ds(slot, 1), :])
            bias = jnp.where(inside, 0.0, MASKED).astype(BF)
            kaug[out, 0:128] = jnp.where(lane_ids(TK) < 64, bias, kv[rows, 128:256])
            kaug[out, 128:256] = kv[rows, 256:384]
            if low_half:
                transposed[tile] = kv[rows, 0:256].T[0:192]
            else:
                transposed[tile] = kaug[out, :].T[64:256]
            return 0

        lax.fori_loop(0, kv.shape[0] // TK, one, 0)


def stack_queries(q, first, slo_ref, shi_ref, qs):
    lane = lane_ids(TQ)
    spot = lax.broadcasted_iota(jnp.int32, (TQ, 128), 0) + first
    mine = ((spot >= slo_ref[...]) & (spot < shi_ref[...])).astype(F32).astype(BF)
    zero = jnp.zeros((TQ, 128), BF)
    low, high = q[:, 0:128], q[:, 128:256]
    mark = jnp.where(lane < 64, mine, zero)
    qs[0:TQ, 0:128] = jnp.where(lane < 64, mine, low)
    qs[TQ : 2 * TQ, 0:128] = mark
    qs[2 * TQ :, 0:128] = mark
    qs[0:TQ, 128:256] = zero
    qs[TQ : 2 * TQ, 128:256] = jnp.where(lane < 64, high, zero)
    qs[2 * TQ :, 128:256] = jnp.where(lane < 64, zero, high)


def attend_kernel(*refs, slot0, count, resume, last):
    tlo, thi, qfirst, q_ref = refs[:4]
    sources = refs[4 : 4 + count]
    lo_ref, hi_ref, slo_ref, shi_ref = refs[4 + count : 8 + count]
    at = 8 + count
    if resume:
        acc_in, stat_in = refs[at : at + 2]
        at += 2
    if last:
        o_ref, ot_ref, lse_ref = refs[at : at + 3]
        at += 3
    else:
        acc_out, stat_out = refs[at : at + 2]
        at += 2
    kaug, vt, qs, acc, m_s, l_s = refs[at:]
    build_keys(sources, slot0, lo_ref, hi_ref, kaug, vt, True)
    slots = count * sources[0].shape[0] // BLK
    per = BLK // TK

    def tile_loop(i, _):
        rows = pl.ds(pl.multiple_of(i * TQ, TQ), TQ)
        stack_queries(q_ref[rows, :], qfirst[i], slo_ref, shi_ref, qs)
        if resume:
            m_s[...] = stat_in[i, 0:1, :]
            l_s[...] = stat_in[i, 1:2, :]
            acc[...] = acc_in[i]
        else:
            m_s[...] = jnp.full_like(m_s, 2 * MASKED)
            l_s[...] = jnp.zeros_like(l_s)
            acc[...] = jnp.zeros_like(acc)

        def slot_loop(s, _):
            def key_loop(t, _):
                tile = s * per + t
                keys = pl.ds(pl.multiple_of(tile * TK, TK), TK)
                st = mm(kaug[keys, :], qs[...], NT)
                m_old = m_s[...]
                m_new = jnp.maximum(m_old, jnp.max(st, axis=0, keepdims=True))
                fade = jnp.exp(m_old - m_new)
                p = jnp.exp(st - m_new)
                l_s[...] = l_s[...] * fade + jnp.sum(p, axis=0, keepdims=True)
                m_s[...] = m_new
                low = p.astype(BF)
                for h in range(3):
                    cols = slice(h * TQ, (h + 1) * TQ)
                    part = slice(h * HD, (h + 1) * HD)
                    acc[part, :] = acc[part, :] * fade[:, cols] + mm(vt[tile, part, :], low[:, cols])
                return 0

            return lax.fori_loop(tlo[i, slot0 + s], thi[i, slot0 + s], key_loop, 0)

        lax.fori_loop(0, slots, slot_loop, 0)
        if last:
            total = l_s[...]
            for h in range(3):
                cols = slice(h * TQ, (h + 1) * TQ)
                part = slice(h * HD, (h + 1) * HD)
                acc[part, :] = acc[part, :] / total[:, cols]
            ot_ref[i] = acc[...]
            o_ref[rows, :] = acc[...].T.astype(BF)
            lse_ref[pl.ds(i, 1), :] = m_s[...] + jnp.log(total)
        else:
            acc_out[i] = acc[...]
            stat_out[i, 0:1, :] = m_s[...]
            stat_out[i, 1:2, :] = l_s[...]
        return 0

    lax.fori_loop(0, q_ref.shape[0] // TQ, tile_loop, 0)


def attend(tables, q, sources, slot0, state=None, last=False):
    tlo, thi, qfirst, lo, hi, slo, shi = tables
    tiles = q.shape[0] // TQ
    keys = sum(s.shape[0] for s in sources)
    ins = (q, *sources, lo, hi, slo, shi) + (tuple(state) if state else ())
    if last:
        outs = (
            jax.ShapeDtypeStruct((q.shape[0], 3 * HD), BF),
            jax.ShapeDtypeStruct((tiles, 3 * HD, TQ), F32),
            jax.ShapeDtypeStruct((tiles, 3 * TQ), F32),
        )
    else:
        outs = (
            jax.ShapeDtypeStruct((tiles, 3 * HD, TQ), F32),
            jax.ShapeDtypeStruct((tiles, 2, 3 * TQ), F32),
        )
    return pl.pallas_call(
        functools.partial(attend_kernel, slot0=slot0, count=len(sources), resume=state is not None, last=last),
        out_shape=outs,
        grid_spec=pltpu.PrefetchScalarGridSpec(
            num_scalar_prefetch=3,
            grid=(1,),
            in_specs=[whole(x.shape) for x in ins],
            out_specs=tuple(whole(x.shape) for x in outs),
            scratch_shapes=[
                pltpu.VMEM((keys, 256), BF),
                pltpu.VMEM((keys // TK, 3 * HD, TK), BF),
                pltpu.VMEM((3 * TQ, 256), BF),
                pltpu.VMEM((3 * HD, TQ), F32),
                pltpu.VMEM((1, 3 * TQ), F32),
                pltpu.VMEM((1, 3 * TQ), F32),
            ],
        ),
        compiler_params=pltpu.CompilerParams(vmem_limit_bytes=40 << 20),
        cost_estimate=cost(12_000_000_000, 12_000_000, 10_000_000),
        name="attend",
    )(tlo, thi, qfirst, *ins)


def attend_back_kernel(*refs, slot0, count, resume, last):
    tlo, thi, qfirst, q_ref, do_ref, ot_ref, lse_ref = refs[:7]
    sources = refs[7 : 7 + count]
    lo_ref, hi_ref, slo_ref, shi_ref = refs[7 + count : 11 + count]
    at = 11 + count
    if resume:
        acc_in = refs[at]
        at += 1
    dq_ref = refs[at]
    d_refs = refs[at + 1 : at + 1 + count]
    kaug, kt, vs, qs, dos, acc, dk_s, dv_s = refs[at + 1 + count :]
    build_keys(sources, slot0, lo_ref, hi_ref, kaug, kt, False)
    rows_each = sources[0].shape[0]
    slots = count * rows_each // BLK
    per = BLK // TK
    for j, kv in enumerate(sources):
        vs[j * rows_each : (j + 1) * rows_each, :] = kv[:, 0:256]
    dk_s[...] = jnp.zeros_like(dk_s)
    dv_s[...] = jnp.zeros_like(dv_s)

    def tile_loop(i, _):
        rows = pl.ds(pl.multiple_of(i * TQ, TQ), TQ)
        stack_queries(q_ref[rows, :], qfirst[i], slo_ref, shi_ref, qs)
        do = do_ref[rows, :]
        lane = lane_ids(TQ)
        zero = jnp.zeros((TQ, 128), BF)
        dos[0:TQ, 0:128] = jnp.where(lane < 64, do[:, 0:128], zero)
        dos[TQ : 2 * TQ, 0:128] = jnp.where(lane < 64, zero, do[:, 0:128])
        dos[2 * TQ :, 0:128] = zero
        dos[0 : 2 * TQ, 128:256] = jnp.zeros((2 * TQ, 128), BF)
        dos[2 * TQ :, 128:192] = do[:, 128:192]
        dos[2 * TQ :, 192:256] = jnp.zeros((TQ, 64), BF)
        both = do.astype(F32).T * ot_ref[i]
        delta = jnp.concatenate(
            [jnp.sum(both[h * HD : (h + 1) * HD], axis=0, keepdims=True) for h in range(3)], axis=1
        )
        lse = lse_ref[pl.ds(i, 1), :]
        if resume:
            acc[...] = acc_in[i]
        else:
            acc[...] = jnp.zeros_like(acc)

        def slot_loop(s, _):
            def key_loop(t, _):
                tile = s * per + t
                keys = pl.ds(pl.multiple_of(tile * TK, TK), TK)
                st = mm(kaug[keys, :], qs[...], NT)
                p = jnp.exp(st - lse)
                dp = mm(vs[keys, :], dos[...], NT)
                ds = (p * (dp - delta)).astype(BF)
                dv_s[keys, :] += mm(p.astype(BF), dos[...])
                dk_s[keys, :] += mm(ds, qs[...])
                for h in range(3):
                    cols = slice(h * TQ, (h + 1) * TQ)
                    acc[(h + 1) * HD : (h + 2) * HD, :] += mm(kt[tile, h * HD : (h + 1) * HD, :], ds[:, cols])
                return 0

            return lax.fori_loop(tlo[i, slot0 + s], thi[i, slot0 + s], key_loop, 0)

        lax.fori_loop(0, slots, slot_loop, 0)
        if last:
            dq_ref[rows, :] = (acc[...] * HD ** (-0.5)).T.astype(BF)
        else:
            dq_ref[i] = acc[...]
        return 0

    lax.fori_loop(0, q_ref.shape[0] // TQ, tile_loop, 0)
    for j, out in enumerate(d_refs):

        def finish(k, _, j=j, out=out):
            to = pl.ds(pl.multiple_of(k * TK, TK), TK)
            frm = pl.ds(pl.multiple_of(j * rows_each + k * TK, TK), TK)
            out[to, 0:128] = dv_s[frm, 0:128].astype(BF)
            out[to, 128:256] = jnp.where(lane_ids(TK) < 64, dv_s[frm, 128:256], dk_s[frm, 0:128]).astype(BF)
            out[to, 256:384] = dk_s[frm, 128:256].astype(BF)
            return 0

        lax.fori_loop(0, rows_each // TK, finish, 0)


def attend_back(tables, q, do, ot, lse, sources, slot0, state=None, last=False, name="attend_back"):
    tlo, thi, qfirst, lo, hi, slo, shi = tables
    tiles = q.shape[0] // TQ
    keys = sum(s.shape[0] for s in sources)
    ins = (q, do, ot, lse, *sources, lo, hi, slo, shi) + ((state,) if state is not None else ())
    dq = jax.ShapeDtypeStruct(q.shape, BF) if last else jax.ShapeDtypeStruct((tiles, 256, TQ), F32)
    outs = (dq,) + tuple(jax.ShapeDtypeStruct(s.shape, BF) for s in sources)
    return pl.pallas_call(
        functools.partial(attend_back_kernel, slot0=slot0, count=len(sources), resume=state is not None, last=last),
        out_shape=outs,
        grid_spec=pltpu.PrefetchScalarGridSpec(
            num_scalar_prefetch=3,
            grid=(1,),
            in_specs=[whole(x.shape) for x in ins],
            out_specs=tuple(whole(x.shape) for x in outs),
            scratch_shapes=[
                pltpu.VMEM((keys, 256), BF),
                pltpu.VMEM((keys // TK, 3 * HD, TK), BF),
                pltpu.VMEM((keys, 256), BF),
                pltpu.VMEM((3 * TQ, 256), BF),
                pltpu.VMEM((3 * TQ, 256), BF),
                pltpu.VMEM((256, TQ), F32),
                pltpu.VMEM((keys, 256), F32),
                pltpu.VMEM((keys, 256), F32),
            ],
        ),
        compiler_params=pltpu.CompilerParams(vmem_limit_bytes=48 << 20),
        cost_estimate=cost(14_000_000_000, 16_000_000, 5_000_000),
        name=name,
    )(tlo, thi, qfirst, *ins)


def row_mean(v):
    return jnp.sum(v, axis=-1, keepdims=True) * (1.0 / v.shape[-1])

def dense_kernel(
    who, o_ref, wo_a, wo_b, win_a, win_b, wback_a, wback_b, x_ref, teacher_ref, cot_ref, keep_ref, vec_ref,
    out_ref, dres_ref, dparts_ref, act_ref, dbr_ref, dpre_ref, hid_ref, dproj_ref, sums_ref,
    wo, win, wback, xh, inv, hidden, gp, acc, sems, *, FB
):
    rows, width = x_ref.shape
    groups = o_ref.shape[0] // rows
    part = width // groups
    units = win.shape[1]
    wo_loads, win_loads, wback_loads = [], [], []
    for i in range(2):
        side = who[0] if i == 0 else 1 - who[0]
        for e in range(groups // 2):
            to = pl.multiple_of(((side * (groups // 2) + e) ^ who[1]) * part, part)
            wo_loads.append(
                pltpu.make_async_copy((wo_a, wo_b)[i].at[pl.ds(e * part, part)], wo.at[pl.ds(to, part)], sems.at[2 * i + e])
            )
        for j, (pieces, target, held) in enumerate((((win_a, win_b), win, win_loads), ((wback_a, wback_b), wback, wback_loads))):
            tall = target.shape[0] // 2
            to = pl.multiple_of(side * tall, tall)
            held.append(pltpu.make_async_copy(pieces[i], target.at[pl.ds(to, tall)], sems.at[4 + 2 * i + j]))
    for load in wo_loads + win_loads + wback_loads:
        load.start()
    b_out, b_in, b_back = vec_ref[0:1, 0:width], vec_ref[1:2, :], vec_ref[2:3, 0:width]
    gain1, shift1, gain2, shift2 = (vec_ref[i : i + 1, 0:width] for i in range(3, 7))
    for load in wo_loads:
        load.wait()
    total = x_ref[...].astype(F32) + b_out
    for i in range(groups):
        total += mm(o_ref[i * rows : (i + 1) * rows, :], wo[i * part : (i + 1) * part, :])
    center = total - row_mean(total)
    scale = lax.rsqrt(row_mean(center * center) + 1e-12)
    inv[...] = scale
    unit = center * scale
    xh[...] = unit
    hid = unit * gain1 + shift1
    hidden[...] = hid
    hid_ref[...] = hid.astype(BF)
    acc[...] = jnp.zeros_like(acc)
    for load in win_loads + wback_loads:
        load.wait()

    def up(n, _):
        cols = pl.ds(pl.multiple_of(n * FB, FB), FB)
        pre = mm(hid_ref[...], win[:, cols]) + vec_ref[1:2, cols]
        cdf = 0.5 + 0.5 * lax.erf(pre * 0.7071067811865476)
        act = (pre * cdf).astype(BF)
        act_ref[:, cols] = act
        gp[:, cols] = cdf + pre * (jnp.exp(pre * pre * -0.5) * 0.3989422804014327)
        acc[...] += mm(act, wback[cols, :])
        return 0

    lax.fori_loop(0, units // FB, up, 0, unroll=True)
    total = hidden[...] + acc[...] + b_back
    center = total - row_mean(total)
    scale = lax.rsqrt(row_mean(center * center) + 1e-12)
    unit = center * scale
    result = unit * gain2 + shift2
    out_ref[...] = result.astype(BF)
    grad = cot_ref[...].astype(F32) + keep_ref[...] * (result - teacher_ref[...].astype(F32))
    def put(row, value):
        sums_ref[row : row + 1, 0 : value.shape[1]] = value
    put(5, jnp.sum(grad * unit, axis=0, keepdims=True))
    put(6, jnp.sum(grad, axis=0, keepdims=True))
    grad = grad * gain2
    back = scale * (grad - row_mean(grad) - unit * row_mean(grad * unit))
    acc[...] = back
    low = back.astype(BF)
    dbr_ref[...] = low
    put(2, jnp.sum(low.astype(F32), axis=0, keepdims=True))

    def down(n, _):
        cols = pl.ds(pl.multiple_of(n * FB, FB), FB)
        dpre = (mm(dbr_ref[...], wback[cols, :], NT) * gp[:, cols]).astype(BF)
        dpre_ref[:, cols] = dpre
        sums_ref[1:2, cols] = jnp.sum(dpre.astype(F32), axis=0, keepdims=True)
        acc[...] += mm(dpre, win[:, cols], NT)
        return 0

    lax.fori_loop(0, units // FB, down, 0, unroll=True)
    grad = acc[...]
    unit = xh[...]
    put(3, jnp.sum(grad * unit, axis=0, keepdims=True))
    put(4, jnp.sum(grad, axis=0, keepdims=True))
    grad = grad * gain1
    back = inv[...] * (grad - row_mean(grad) - unit * row_mean(grad * unit))
    dres_ref[...] = back
    low = back.astype(BF)
    dproj_ref[...] = low
    put(0, jnp.sum(low.astype(F32), axis=0, keepdims=True))
    for i in range(groups):
        dparts_ref[i * rows : (i + 1) * rows, :] = mm(low, wo[i * part : (i + 1) * part, :], NT).astype(BF)


def dense(who, o, weights, x, teacher, cot, keep, vec):
    rows, width = x.shape
    units = vec.shape[1]
    sd = jax.ShapeDtypeStruct
    outs = (
        sd((rows, width), BF), sd((rows, width), F32), sd(o.shape, BF), sd((rows, units), BF), sd((rows, width), BF),
        sd((rows, units), BF), sd((rows, width), BF), sd((rows, width), BF), sd((8, units), F32),
    )
    ins = (o, *weights, x, teacher, cot, keep, vec)
    stay = pl.BlockSpec(memory_space=pl.ANY)
    return pl.pallas_call(
        functools.partial(dense_kernel, FB=FFB),
        out_shape=outs,
        grid_spec=pltpu.PrefetchScalarGridSpec(
            num_scalar_prefetch=1,
            grid=(1,),
            in_specs=[whole(o.shape)] + [stay] * 6 + [whole(a.shape) for a in ins[7:]],
            out_specs=tuple(whole(a.shape) for a in outs),
            scratch_shapes=[
                pltpu.VMEM((width, width), BF), pltpu.VMEM((width, units), BF), pltpu.VMEM((units, width), BF),
                pltpu.VMEM((rows, width), F32), pltpu.VMEM((rows, 1), F32), pltpu.VMEM((rows, width), F32),
                pltpu.VMEM((rows, units), F32), pltpu.VMEM((rows, width), F32), pltpu.SemaphoreType.DMA((8,)),
            ],
        ),
        compiler_params=pltpu.CompilerParams(vmem_limit_bytes=60 << 20),
        cost_estimate=cost(12_000_000_000, 30_000_000, 4_000_000),
        name="dense",
    )(who, *ins)


def finish_kernel(who, dq_ref, own_ref, pair_ref, left_ref, right_ref, turn_ref, xt_ref, all_ref, mine_ref, other_ref, dw, sums):
    groups, rows = turn_ref.shape[:2]
    middle = groups * rows // 2
    sums[...] = jnp.zeros_like(sums)
    for d in range(groups):
        at = pl.ds(d * rows, rows)
        inner = pl.ds((d % (groups // 2)) * rows, rows)
        first = (d < groups // 2) == (who[2] == 0)
        back = own_ref[at, :].astype(F32) + pair_ref[at, :].astype(F32)
        back += jnp.where(first, left_ref[inner, :], right_ref[inner, :]).astype(F32)
        tok = mm(turn_ref[d], back.astype(BF)).astype(BF)
        dq = dq_ref[at, :]
        all_ref[at, 0:256] = dq
        all_ref[at, 256:640] = tok
        sums[0:1, 0:256] += jnp.sum(dq.astype(F32), axis=0, keepdims=True)
        sums[0:1, 256:640] += jnp.sum(tok.astype(F32), axis=0, keepdims=True)
    del middle
    dw[...] = mm(xt_ref[...], all_ref[...]).astype(BF)
    tall = dw.shape[0] // 2
    low = sums[...].astype(BF)
    for out, side in ((mine_ref, who[0]), (other_ref, 1 - who[0])):
        out[0:tall, :] = dw[pl.ds(pl.multiple_of(side * tall, tall), tall), :]
        out[tall:, :] = jnp.zeros((out.shape[0] - tall, out.shape[1]), BF)
        out[tall : tall + 16, :] = low


def finish(who, dq, own, pair, left, right, turn, xt):
    sd = jax.ShapeDtypeStruct
    cols = dq.shape[1] + own.shape[1]
    tall = xt.shape[0] // 2 + 64
    ins = (dq, own, pair, left, right, turn, xt)
    outs = (sd((dq.shape[0], cols), BF), sd((tall, cols), BF), sd((tall, cols), BF))
    return pl.pallas_call(
        finish_kernel,
        out_shape=outs,
        grid_spec=pltpu.PrefetchScalarGridSpec(
            num_scalar_prefetch=1,
            grid=(1,),
            in_specs=[whole(a.shape) for a in ins],
            out_specs=tuple(whole(a.shape) for a in outs),
            scratch_shapes=[pltpu.VMEM((xt.shape[0], cols), BF), pltpu.VMEM((16, cols), F32)],
        ),
        compiler_params=pltpu.CompilerParams(vmem_limit_bytes=32 << 20),
        cost_estimate=cost(3_000_000_000, 14_000_000),
        name="finish",
    )(who, *ins)


def spread_kernel(all_ref, w_ref, *outs):
    rows = outs[0].shape[0]
    for d, out in enumerate(outs):
        out[...] = mm(all_ref[d * rows : (d + 1) * rows, :], w_ref[...], NT).astype(BF)


def spread_x(d_all, w_heads, groups):
    out = jax.ShapeDtypeStruct((d_all.shape[0] // groups, w_heads.shape[0]), BF)
    return pl.pallas_call(
        spread_kernel,
        out_shape=(out,) * groups,
        grid=(1,),
        in_specs=[whole(d_all.shape), whole(w_heads.shape)],
        out_specs=(whole(out.shape),) * groups,
        compiler_params=pltpu.CompilerParams(vmem_limit_bytes=24 << 20),
        cost_estimate=cost(2_000_000_000, 7_000_000),
        name="spread_x",
    )(d_all, w_heads)


def place_kernel(who, a_near, a_far, b_near, b_far, back_ref, in_ref, out_ref, vec_ref, held, *, spans):
    fb, fi = 384 // spans, 128 // spans
    each = fb + 4 * fi
    s1, s2 = lax.rem(who[1], 2), who[1] // 2
    for color, pair in enumerate(((a_near, a_far), (b_near, b_far))):
        for i, ref in enumerate(pair):
            for j in range(2):
                if color == 0:
                    base = (s1 ^ i) * 2 + (s2 ^ j)
                else:
                    base = 4 + (s2 ^ i) * 2 + (s1 ^ j)
                for p in range(spans // 2):
                    frm = (j * (spans // 2) + p) * each
                    to = pl.multiple_of(base * 192 + p * fb, 8)
                    back_ref[pl.ds(to, fb), :] = ref[frm : frm + fb, :].astype(F32)
                    to = pl.multiple_of(base * 64 + p * fi, 8)
                    for k in range(4):
                        start = frm + fb + k * fi
                        held[pl.ds(to, fi), k * 768 : (k + 1) * 768] = ref[start : start + fi, :].astype(F32)
    in_ref[...] = held[0:384, :]
    for k in range(3):
        out_ref[k * 128 : (k + 1) * 128, :] = held[384:512, k * 768 : (k + 1) * 768]
    vec_ref[...] = held[384:392, 3 * 768 :]


def gather_out(who, pieces, spans):
    sd = jax.ShapeDtypeStruct
    outs = (sd((1536, 768), F32), sd((384, 3072), F32), sd((384, 768), F32), sd((8, 768), F32))
    return pl.pallas_call(
        functools.partial(place_kernel, spans=spans),
        out_shape=outs,
        grid_spec=pltpu.PrefetchScalarGridSpec(
            num_scalar_prefetch=1,
            grid=(1,),
            in_specs=[whole(a.shape) for a in pieces],
            out_specs=tuple(whole(a.shape) for a in outs),
            scratch_shapes=[pltpu.VMEM((512, 3072), F32)],
        ),
        compiler_params=pltpu.CompilerParams(vmem_limit_bytes=32 << 20),
        cost_estimate=cost(1_000_000, 18_000_000),
        name="gather_out",
    )(who, *pieces)


def heads_kernel(who, h0, h1, h2, h3, q_ref, k_ref, v_ref, bias_ref, held):
    tall = q_ref.shape[0]
    for d, ref in enumerate((h0, h1, h2, h3)):
        held[who[1] ^ d] = ref[...]
    for a in range(4):
        cols = slice(a * 192, (a + 1) * 192)
        q_ref[:, cols] = held[a, 0:tall, 64:256].astype(F32)
        v_ref[:, cols] = held[a, 0:tall, 256:448].astype(F32)
        k_ref[:, cols] = held[a, 0:tall, 448:640].astype(F32)
        bias_ref[0:8, cols] = held[a, tall : tall + 16, 64:256].astype(F32)[0:8]
        bias_ref[8:16, cols] = held[a, tall : tall + 16, 256:448].astype(F32)[0:8]


def heads_out(who, pieces):
    sd = jax.ShapeDtypeStruct
    outs = (sd((384, 768), F32),) * 3 + (sd((16, 768), F32),)
    return pl.pallas_call(
        heads_kernel,
        out_shape=outs,
        grid_spec=pltpu.PrefetchScalarGridSpec(
            num_scalar_prefetch=1,
            grid=(1,),
            in_specs=[whole(a.shape) for a in pieces],
            out_specs=tuple(whole(a.shape) for a in outs),
            scratch_shapes=[pltpu.VMEM((4, *pieces[0].shape), BF)],
        ),
        compiler_params=pltpu.CompilerParams(vmem_limit_bytes=24 << 20),
        cost_estimate=cost(1_000_000, 6_000_000),
        name="heads_out",
    )(who, *pieces)


def swap(block, axis="fsdp"):
    return lax.ppermute(block, axis, [(0, 1), (1, 0)])


def shifted(block, axis, distance):
    devices = range(lax.axis_size(axis))
    route = [(i - distance, i) for i in devices if i - distance in devices]
    return lax.ppermute(block, axis, route)


def flip(block, bit, axis="uly"):
    return lax.ppermute(block, axis, [(i, i ^ bit) for i in range(lax.axis_size(axis))])


def exchange(rows, axis):
    return lax.all_to_all(rows, axis, split_axis=0, concat_axis=0, tiled=True)


def spread_rows(rows, axis):
    count = lax.axis_size(axis)
    return exchange(jnp.broadcast_to(rows[None], (count, *rows.shape)).reshape(-1, rows.shape[1]), axis)


def sum_scatter(rows, axis):
    count = lax.axis_size(axis)
    got = exchange(rows, axis).reshape(count, -1, rows.shape[1])
    return sum(got[i].astype(F32) for i in range(count)).astype(BF)


def add(left, right):
    return (left.astype(F32) + right.astype(F32)).astype(BF)


def sides(rows, bit):
    side = jnp.where((lax.axis_index("uly") & bit) > 0, 1, 0)
    split = rows.reshape(2, -1, rows.shape[1])
    return (
        lax.dynamic_index_in_dim(split, side, 0, keepdims=False),
        lax.dynamic_index_in_dim(split, 1 - side, 0, keepdims=False),
    )


def halve(rows, bit):
    mine, other = sides(rows, bit)
    return add(mine, flip(other, bit))


def double(rows, bit, axis):
    low = (lax.axis_index(axis) & bit) == 0
    got = flip(rows, bit, axis)
    return jnp.concatenate([jnp.where(low, rows, got), jnp.where(low, got, rows)], axis=0)


def halves(rows):
    middle = rows.shape[0] // 2
    return rows[:middle], rows[middle:]


def line_gather(rows):
    bit = 1
    while bit < lax.axis_size("ctx"):
        rows = double(rows, bit, "ctx")
        bit *= 2
    return rows


def tie(*values):
    return lax.optimization_barrier(values)


def on_device(
    tokens, teacher, cotangent, valid, teacher_ok, doc_starts, w_query, w_key, w_value, w_out, w_in, w_back,
    bias_query, bias_value, bias_out, bias_in, bias_back, norm1_gain, norm1_bias, norm2_gain, norm2_bias,
):
    groups = lax.axis_size("uly")
    spans = lax.axis_size("ctx")
    rows, width = tokens.shape
    block = rows * groups * 2
    stream = block * spans
    ctx_index = lax.axis_index("ctx")
    uly = lax.axis_index("uly")
    half = lax.axis_index("fsdp")
    head_cols = width // groups
    shard = w_query.shape[0]
    middle = groups * rows // 2
    upper = uly // 2

    valid_one = valid[None, :]
    valid_own = jnp.concatenate([valid_one, flip(valid_one, 1), flip(valid_one, 2), flip(valid_one, 3)], axis=0)
    x_own, valid_own = tie(tokens, valid_own)
    x_x, x_y = flip(x_own, 1), flip(x_own, 2)
    x_top, x_bottom = flip(x_y[: rows // 2], 1), flip(x_x[rows // 2 :], 2)
    x_plane = (x_own, x_x, x_y, jnp.concatenate([x_top, x_bottom], axis=0))
    valid_pair = swap(valid_own)
    valid_both = jnp.stack([valid_own, valid_pair]).reshape(2, 2, 2, rows)
    valid_high = lax.dynamic_index_in_dim(valid_both, 1 - upper, 1, keepdims=False)
    valid_low = lax.dynamic_index_in_dim(valid_both, upper, 1, keepdims=False)
    halo = (shifted(valid_high, "ctx", 1), shifted(valid_low, "ctx", -1))
    block_valid = jnp.concatenate([valid_own, valid_pair, halo[0][0], halo[1][0], halo[0][1], halo[1][1]], axis=0)
    count = jnp.full((8, 128), jnp.sum(valid_both), jnp.int32)
    bit = 1
    while bit < spans:
        count = count + flip(count, bit, "ctx")
        bit *= 2
    count = count[0, 0].astype(F32)

    start_col = uly * head_cols
    cut = [lax.dynamic_slice_in_dim(w, start_col, head_cols, 1) for w in (w_query, w_value, w_key)]
    w_mine = jnp.concatenate([jnp.zeros((shard, 256 - head_cols), BF), *cut], axis=1)
    w_other = swap(w_mine)
    w_heads = jnp.concatenate(
        [jnp.where(half == 0, w_mine, w_other), jnp.where(half == 0, w_other, w_mine)], axis=0
    )
    weights = (w_out, swap(w_out), w_in, swap(w_in), w_back, swap(w_back))
    who = jnp.stack([half, uly, upper])
    small = (bias_query, bias_value, bias_out, bias_in, bias_back, norm1_gain, norm1_bias, norm2_gain, norm2_bias)
    packed = jnp.concatenate([p.reshape(-1, shard) for p in small], axis=0)
    packed_pair = swap(packed)
    packed = jnp.stack([jnp.where(half == 0, packed, packed_pair), jnp.where(half == 0, packed_pair, packed)])
    vectors = []
    at = 0
    for p in small:
        n = p.shape[0] // shard
        vectors.append(packed[:, at : at + n].reshape(-1).astype(F32))
        at += n
    bq_all, bv_all = vectors[:2]
    vec = jnp.stack([jnp.pad(v, (0, w_in.shape[1] - v.shape[0])) for v in vectors[2:]] + [jnp.zeros((w_in.shape[1],), F32)])
    bias_heads = jnp.concatenate(
        [
            jnp.zeros((256 - head_cols,), F32),
            lax.dynamic_slice_in_dim(bq_all, start_col, head_cols, 0),
            lax.dynamic_slice_in_dim(bv_all, start_col, head_cols, 0),
            jnp.zeros((head_cols,), F32),
        ]
    )

    place = jnp.arange(groups, dtype=jnp.int32)
    two = jnp.arange(2, dtype=jnp.int32)
    in_plane = place ^ uly
    halo_group = jnp.concatenate([uly ^ (2 * (1 - upper) + two), uly ^ (2 * upper + two)])
    halo_plane = ctx_index + jnp.where(place < 2, -1, 1)
    plane_of = jnp.concatenate([jnp.full((2 * groups,), 1, jnp.int32) * ctx_index, halo_plane, halo_plane])
    group_of = jnp.concatenate([in_plane, in_plane, halo_group, halo_group])
    mine = jnp.full((groups,), 1, jnp.int32) * half
    core_of = jnp.concatenate([mine, 1 - mine, mine, 1 - mine])
    block_id = plane_of * (2 * groups) + group_of * 2 + core_of
    spot = block_id[:, None] * rows + jnp.arange(rows, dtype=jnp.int32)[None, :]
    edges = jnp.concatenate([doc_starts, jnp.full((DOCS + 1,), stream, jnp.int32)])
    window_first = jnp.maximum(ctx_index * block - block // 2, 0)
    first_doc = jnp.sum((doc_starts <= window_first).astype(jnp.int32)) - 1
    near = lax.dynamic_slice_in_dim(edges, first_doc, DOCS + 1, 0)
    tiles = groups * rows // TQ
    per = rows // TQ
    tile_ids = jnp.arange(tiles, dtype=jnp.int32)
    qfirst = ctx_index * block + (((tile_ids // per) ^ uly) * 2 + half) * rows + lax.rem(tile_ids, per) * TQ
    q_lo = jnp.max(jnp.where(near[None, :] <= qfirst[:, None], near[None, :], 0), axis=1)
    q_hi = jnp.min(jnp.where(near[None, :] <= qfirst[:, None] + TQ - 1, stream, near[None, :]), axis=1)
    limits = jnp.concatenate([near, q_lo, q_hi])
    counted = jnp.sum(block_valid[:, None, :] * (spot[:, None, :] < limits[None, :, None]), axis=-1)
    bounds = counted[:, : DOCS + 1]
    cnt_lo = counted[:, DOCS + 1 : DOCS + 1 + tiles].T
    cnt_hi = counted[:, DOCS + 1 + tiles :].T
    pad64 = jnp.zeros((bounds.shape[0], 128 - DOCS), jnp.int32)
    lo_tab = jnp.concatenate([bounds[:, :DOCS], pad64], axis=1)
    hi_tab = jnp.concatenate([bounds[:, 1:], pad64], axis=1)
    slo_tab = jnp.concatenate([near[:DOCS], pad64[0]])[None, :]
    shi_tab = jnp.concatenate([near[1:], pad64[0]])[None, :]
    some = cnt_hi > cnt_lo
    tlo = jnp.where(some, cnt_lo // TK, 0)
    thi = jnp.where(some, (cnt_hi + TK - 1) // TK, 0)
    tables = (tlo, thi, qfirst, lo_tab, hi_tab, slo_tab, shi_tab)
    before = mm(valid_own.astype(BF), (jnp.arange(rows)[:, None] < jnp.arange(rows)[None, :]).astype(BF)).astype(jnp.int32)
    goes_to = jnp.where(valid_own > 0, before, rows)
    chosen = (goes_to[:, None, :] == jnp.arange(rows, dtype=jnp.int32)[None, :, None]).astype(BF)
    loss_scale = jnp.float32(stream) / count
    keep = (loss_scale * (valid * teacher_ok).astype(F32))[:, None]
    turned = (goes_to[:, :, None] == jnp.arange(rows, dtype=jnp.int32)[None, None, :]).astype(BF)
    x_turned = jnp.concatenate([x.T for x in x_plane], axis=1)

    scale = jnp.asarray(HD ** (-0.5), BF)
    qvk = [mm(x, w_heads) + bias_heads for x in x_plane]
    q_low = jnp.concatenate([t[:, :256].astype(BF) for t in qvk], axis=0) * scale
    kv_own = jnp.concatenate([mm(chosen[d], qvk[d][:, 256:].astype(BF)).astype(BF) for d in range(groups)], axis=0)
    kv_split = kv_own.reshape(2, middle, 2 * head_cols)
    kv_halo = jnp.concatenate(
        [
            shifted(lax.dynamic_index_in_dim(kv_split, 1 - upper, 0, keepdims=False), "ctx", 1),
            shifted(lax.dynamic_index_in_dim(kv_split, upper, 0, keepdims=False), "ctx", -1),
        ],
        axis=0,
    )
    kv_pair = swap(kv_own)
    state = attend(tables, q_low, (kv_own,), 0)
    kv_halo, kv_pair, *state = tie(kv_halo, kv_pair, *state)
    kv_halo_pair = swap(kv_halo)
    state = attend(tables, q_low, (kv_pair,), groups, state)
    o_heads, o_turned, lse = attend(tables, q_low, (kv_halo, kv_halo_pair), 2 * groups, state, last=True)
    o_rel = o_heads.reshape(groups, rows, head_cols)
    o_all = jnp.concatenate([o_rel[0]] + [flip(o_rel[d], d) for d in range(1, groups)], axis=0)

    out, d_resid1, d_parts, act, d_branch, d_pre, hidden_low, d_proj, sums = dense(
        who, o_all, weights, tokens, teacher, cotangent, keep, vec
    )
    d_rel = d_parts.reshape(groups, rows, head_cols)
    d_heads = jnp.concatenate([d_rel[0]] + [flip(d_rel[d], d) for d in range(1, groups)], axis=0)
    tall = w_back.shape[0]
    vector_rows = jnp.concatenate(
        [sums[i, :width].reshape(2, -1) for i in (0, 2, 3, 4, 5, 6)] + [sums[1].reshape(2, -1)], axis=1
    ).reshape(2, -1, width)
    vector_rows = jnp.pad(vector_rows, ((0, 0), (0, 128 - vector_rows.shape[1]), (0, 0))).astype(BF)
    o_rows = o_all.reshape(groups, rows, head_cols)

    def back_part(side):
        return mm(lax.dynamic_slice_in_dim(act, side * tall, tall, 1), d_branch, TN).astype(BF)

    def in_part(side):
        return mm(lax.dynamic_slice_in_dim(hidden_low, side * shard, shard, 1), d_pre, TN).astype(BF)

    def out_part(side):
        both = [
            mm(lax.dynamic_index_in_dim(o_rows, (2 * side + e) ^ uly, 0, keepdims=False), d_proj, TN).astype(BF)
            for e in range(2)
        ]
        stack = jnp.concatenate([*both, lax.dynamic_index_in_dim(vector_rows, side, 0, keepdims=False)], axis=0)
        return jnp.concatenate([stack[i * 128 : (i + 1) * 128] for i in range(4)], axis=1)

    back_sum = add(back_part(half), swap(back_part(1 - half)))
    in_sum = jnp.concatenate(
        [add(in_part(half), swap(in_part(1 - half))), add(out_part(half), swap(out_part(1 - half)))], axis=0
    )

    d_heads, back_sum = tie(d_heads, back_sum)
    b1, b2 = halves(back_sum)
    b1, b2 = halve(b1, 1), halve(b2, 2)
    args = (tables, q_low, d_heads, o_turned, lse)
    dq_state, dkv_halo, dkv_halo_pair = attend_back(*args, (kv_halo, kv_halo_pair), 2 * groups, name="back_halo")
    dq_state, b1, b2, in_sum = tie(dq_state, b1, b2, in_sum)
    b1, b2 = halve(b1, 2), halve(b2, 1)
    i1, i2 = halves(in_sum)
    i1, i2 = halve(i1, 1), halve(i2, 2)
    halo_sum = add(dkv_halo, swap(dkv_halo_pair))
    dq_state, dkv_pair = attend_back(*args, (kv_pair,), groups, dq_state, name="back_pair")
    dq_state, b1, b2, i1, i2, halo_sum = tie(dq_state, b1, b2, i1, i2, halo_sum)
    back_line = sum_scatter(jnp.concatenate([b1, b2], axis=0), "ctx")
    i1, i2 = halve(i1, 2), halve(i2, 1)
    from_left = shifted(halo_sum[middle:], "ctx", 1)
    from_right = shifted(halo_sum[:middle], "ctx", -1)
    pair_back = swap(dkv_pair)
    dq, dkv_own = attend_back(*args, (kv_own,), 0, dq_state, last=True, name="back_own")
    d_all, heads_mine, heads_other = finish(who, dq, dkv_own, pair_back, from_left, from_right, turned, x_turned)
    in_line = sum_scatter(jnp.concatenate([i1, i2], axis=0), "ctx")
    heads_sum = add(heads_mine, swap(heads_other))
    dx = spread_x(d_all, w_heads, groups)
    grad_in = d_resid1 + dx[0].astype(F32) + sum(flip(dx[d], d).astype(F32) for d in range(1, groups))

    in_line = jnp.concatenate([in_line[:, i * width : (i + 1) * width] for i in range(4)], axis=0)
    c1, c2 = halves(line_gather(jnp.concatenate([back_line, in_line], axis=0)))
    heads_sum = line_gather(sum_scatter(heads_sum, "ctx"))
    c1 = jnp.concatenate([c1, flip(c1, 2)], axis=0)
    c2 = jnp.concatenate([c2, flip(c2, 1)], axis=0)
    g_back, g_in, g_out, g_vec = gather_out(who, (c1, flip(c1, 1), c2, flip(c2, 2)), spans)
    g_query, g_key, g_value, g_bias = heads_out(who, [heads_sum] + [flip(heads_sum, d) for d in range(1, groups)])
    g_bias_q = lax.dynamic_slice_in_dim(g_bias[0], half * shard, shard, 0)
    g_bias_v = lax.dynamic_slice_in_dim(g_bias[8], half * shard, shard, 0)
    flat = g_vec.reshape(-1)
    g_bo, g_bb, g_g1, g_s1, g_g2, g_s2 = [flat[i * shard : (i + 1) * shard] for i in range(6)]
    g_bin = flat[6 * shard : 6 * shard + bias_in.shape[0]]
    return (
        out, grad_in, g_query, g_key, g_value, g_out, g_in, g_back,
        g_bias_q, g_bias_v, g_bo, g_bin, g_bb, g_g1, g_s1, g_g2, g_s2,
    )


def solution(mesh):
    placed = (
        P(("ctx", "uly", "fsdp"), None),
        P(("ctx", "uly", "fsdp"), None),
        P(("ctx", "uly", "fsdp"), None),
        P(("ctx", "uly", "fsdp")),
        P(("ctx", "uly", "fsdp")),
        P(),
        P("fsdp", None),
        P("fsdp", None),
        P("fsdp", None),
        P("fsdp", None),
        P("fsdp", None),
        P("fsdp", None),
        P("fsdp"),
        P("fsdp"),
        P("fsdp"),
        P("fsdp"),
        P("fsdp"),
        P("fsdp"),
        P("fsdp"),
        P("fsdp"),
        P("fsdp"),
    )
    return jax.shard_map(
        on_device,
        mesh=mesh,
        in_specs=placed,
        out_specs=(
            P(("ctx", "uly", "fsdp"), None),
            P(("ctx", "uly", "fsdp"), None),
            P("fsdp", None),
            P("fsdp", None),
            P("fsdp", None),
            P("fsdp", None),
            P("fsdp", None),
            P("fsdp", None),
            P("fsdp"),
            P("fsdp"),
            P("fsdp"),
            P("fsdp"),
            P("fsdp"),
            P("fsdp"),
            P("fsdp"),
            P("fsdp"),
            P("fsdp"),
        ),
        check_vma=False,
    )
```

```python
import functools

import jax
import jax.numpy as jnp
from jax import lax
from jax.experimental import pallas as pl
from jax.experimental.pallas import tpu as pltpu
from jax.sharding import PartitionSpec as P

HEADS = 12
HD = 64
BLK = 512
TQ = 256
TK = 256
DOCS = 64
FFB = 768
MASKED = -1e30
BF = jnp.bfloat16
F32 = jnp.float32
NT = (((1,), (1,)), ((), ()))
NN = (((1,), (0,)), ((), ()))
TN = (((0,), (0,)), ((), ()))


def mm(left, right, dims=NN):
    return lax.dot_general(left, right, dims, preferred_element_type=F32)


def whole(shape):
    return pl.BlockSpec(shape, lambda *_: (0,) * len(shape), pipeline_mode=pl.Buffered(1))


def cost(flops, moved, special=0):
    return pl.CostEstimate(flops=flops, bytes_accessed=moved, transcendentals=special)


def lane_ids(rows):
    return lax.broadcasted_iota(jnp.int32, (rows, 128), 1)


def build_keys(sources, slot0, lo_ref, hi_ref, kaug, transposed, low_half):
    per = BLK // TK
    for at, kv in enumerate(sources):

        def one(j, _, at=at, kv=kv):
            rows = pl.ds(pl.multiple_of(j * TK, TK), TK)
            tile = at * (kv.shape[0] // TK) + j
            slot = slot0 + at * (kv.shape[0] // BLK) + j // per
            out = pl.ds(pl.multiple_of(tile * TK, TK), TK)
            rank = lax.broadcasted_iota(jnp.int32, (TK, 128), 0) + lax.rem(j, per) * TK
            inside = (rank >= lo_ref[pl.ds(slot, 1), :]) & (rank < hi_ref[pl.ds(slot, 1), :])
            bias = jnp.where(inside, 0.0, MASKED).astype(BF)
            kaug[out, 0:128] = jnp.where(lane_ids(TK) < 64, bias, kv[rows, 128:256])
            kaug[out, 128:256] = kv[rows, 256:384]
            if low_half:
                transposed[tile] = kv[rows, 0:256].T[0:192]
            else:
                transposed[tile] = kaug[out, :].T[64:256]
            return 0

        lax.fori_loop(0, kv.shape[0] // TK, one, 0)


def stack_queries(q, first, slo_ref, shi_ref, qs):
    lane = lane_ids(TQ)
    spot = lax.broadcasted_iota(jnp.int32, (TQ, 128), 0) + first
    mine = ((spot >= slo_ref[...]) & (spot < shi_ref[...])).astype(F32).astype(BF)
    zero = jnp.zeros((TQ, 128), BF)
    low, high = q[:, 0:128], q[:, 128:256]
    mark = jnp.where(lane < 64, mine, zero)
    qs[0:TQ, 0:128] = jnp.where(lane < 64, mine, low)
    qs[TQ : 2 * TQ, 0:128] = mark
    qs[2 * TQ :, 0:128] = mark
    qs[0:TQ, 128:256] = zero
    qs[TQ : 2 * TQ, 128:256] = jnp.where(lane < 64, high, zero)
    qs[2 * TQ :, 128:256] = jnp.where(lane < 64, zero, high)


def attend_kernel(*refs, slot0, count, resume, last):
    tlo, thi, qfirst, q_ref = refs[:4]
    sources = refs[4 : 4 + count]
    lo_ref, hi_ref, slo_ref, shi_ref = refs[4 + count : 8 + count]
    at = 8 + count
    if resume:
        acc_in, stat_in = refs[at : at + 2]
        at += 2
    if last:
        o_ref, ot_ref, lse_ref = refs[at : at + 3]
        at += 3
    else:
        acc_out, stat_out = refs[at : at + 2]
        at += 2
    kaug, vt, qs, acc, m_s, l_s = refs[at:]
    build_keys(sources, slot0, lo_ref, hi_ref, kaug, vt, True)
    slots = count * sources[0].shape[0] // BLK
    per = BLK // TK

    def tile_loop(i, _):
        rows = pl.ds(pl.multiple_of(i * TQ, TQ), TQ)
        stack_queries(q_ref[rows, :], qfirst[i], slo_ref, shi_ref, qs)
        if resume:
            m_s[...] = stat_in[i, 0:1, :]
            l_s[...] = stat_in[i, 1:2, :]
            acc[...] = acc_in[i]
        else:
            m_s[...] = jnp.full_like(m_s, 2 * MASKED)
            l_s[...] = jnp.zeros_like(l_s)
            acc[...] = jnp.zeros_like(acc)

        def slot_loop(s, _):
            def key_loop(t, _):
                tile = s * per + t
                keys = pl.ds(pl.multiple_of(tile * TK, TK), TK)
                st = mm(kaug[keys, :], qs[...], NT)
                m_old = m_s[...]
                m_new = jnp.maximum(m_old, jnp.max(st, axis=0, keepdims=True))
                fade = jnp.exp(m_old - m_new)
                p = jnp.exp(st - m_new)
                l_s[...] = l_s[...] * fade + jnp.sum(p, axis=0, keepdims=True)
                m_s[...] = m_new
                low = p.astype(BF)
                for h in range(3):
                    cols = slice(h * TQ, (h + 1) * TQ)
                    part = slice(h * HD, (h + 1) * HD)
                    acc[part, :] = acc[part, :] * fade[:, cols] + mm(vt[tile, part, :], low[:, cols])
                return 0

            return lax.fori_loop(tlo[i, slot0 + s], thi[i, slot0 + s], key_loop, 0)

        lax.fori_loop(0, slots, slot_loop, 0)
        if last:
            total = l_s[...]
            for h in range(3):
                cols = slice(h * TQ, (h + 1) * TQ)
                part = slice(h * HD, (h + 1) * HD)
                acc[part, :] = acc[part, :] / total[:, cols]
            ot_ref[i] = acc[...]
            o_ref[rows, :] = acc[...].T.astype(BF)
            lse_ref[pl.ds(i, 1), :] = m_s[...] + jnp.log(total)
        else:
            acc_out[i] = acc[...]
            stat_out[i, 0:1, :] = m_s[...]
            stat_out[i, 1:2, :] = l_s[...]
        return 0

    lax.fori_loop(0, q_ref.shape[0] // TQ, tile_loop, 0)


def attend(tables, q, sources, slot0, state=None, last=False):
    tlo, thi, qfirst, lo, hi, slo, shi = tables
    tiles = q.shape[0] // TQ
    keys = sum(s.shape[0] for s in sources)
    ins = (q, *sources, lo, hi, slo, shi) + (tuple(state) if state else ())
    if last:
        outs = (
            jax.ShapeDtypeStruct((q.shape[0], 3 * HD), BF),
            jax.ShapeDtypeStruct((tiles, 3 * HD, TQ), F32),
            jax.ShapeDtypeStruct((tiles, 3 * TQ), F32),
        )
    else:
        outs = (
            jax.ShapeDtypeStruct((tiles, 3 * HD, TQ), F32),
            jax.ShapeDtypeStruct((tiles, 2, 3 * TQ), F32),
        )
    return pl.pallas_call(
        functools.partial(attend_kernel, slot0=slot0, count=len(sources), resume=state is not None, last=last),
        out_shape=outs,
        grid_spec=pltpu.PrefetchScalarGridSpec(
            num_scalar_prefetch=3,
            grid=(1,),
            in_specs=[whole(x.shape) for x in ins],
            out_specs=tuple(whole(x.shape) for x in outs),
            scratch_shapes=[
                pltpu.VMEM((keys, 256), BF),
                pltpu.VMEM((keys // TK, 3 * HD, TK), BF),
                pltpu.VMEM((3 * TQ, 256), BF),
                pltpu.VMEM((3 * HD, TQ), F32),
                pltpu.VMEM((1, 3 * TQ), F32),
                pltpu.VMEM((1, 3 * TQ), F32),
            ],
        ),
        compiler_params=pltpu.CompilerParams(vmem_limit_bytes=20 << 20),
        cost_estimate=cost(12_000_000_000, 12_000_000, 10_000_000),
        name="attend",
    )(tlo, thi, qfirst, *ins)


def attend_back_kernel(*refs, slot0, count, resume, last):
    tlo, thi, qfirst, q_ref, do_ref, ot_ref, lse_ref = refs[:7]
    sources = refs[7 : 7 + count]
    lo_ref, hi_ref, slo_ref, shi_ref = refs[7 + count : 11 + count]
    at = 11 + count
    if resume:
        acc_in = refs[at]
        at += 1
    dq_ref = refs[at]
    d_refs = refs[at + 1 : at + 1 + count]
    kaug, kt, vs, qs, dos, acc, dk_s, dv_s = refs[at + 1 + count :]
    build_keys(sources, slot0, lo_ref, hi_ref, kaug, kt, False)
    rows_each = sources[0].shape[0]
    slots = count * rows_each // BLK
    per = BLK // TK
    for j, kv in enumerate(sources):
        vs[j * rows_each : (j + 1) * rows_each, :] = kv[:, 0:256]
    dk_s[...] = jnp.zeros_like(dk_s)
    dv_s[...] = jnp.zeros_like(dv_s)

    def tile_loop(i, _):
        rows = pl.ds(pl.multiple_of(i * TQ, TQ), TQ)
        stack_queries(q_ref[rows, :], qfirst[i], slo_ref, shi_ref, qs)
        do = do_ref[rows, :]
        lane = lane_ids(TQ)
        zero = jnp.zeros((TQ, 128), BF)
        dos[0:TQ, 0:128] = jnp.where(lane < 64, do[:, 0:128], zero)
        dos[TQ : 2 * TQ, 0:128] = jnp.where(lane < 64, zero, do[:, 0:128])
        dos[2 * TQ :, 0:128] = zero
        dos[0 : 2 * TQ, 128:256] = jnp.zeros((2 * TQ, 128), BF)
        dos[2 * TQ :, 128:192] = do[:, 128:192]
        dos[2 * TQ :, 192:256] = jnp.zeros((TQ, 64), BF)
        both = do.astype(F32).T * ot_ref[i]
        delta = jnp.concatenate(
            [jnp.sum(both[h * HD : (h + 1) * HD], axis=0, keepdims=True) for h in range(3)], axis=1
        )
        lse = lse_ref[pl.ds(i, 1), :]
        if resume:
            acc[...] = acc_in[i]
        else:
            acc[...] = jnp.zeros_like(acc)

        def slot_loop(s, _):
            def key_loop(t, _):
                tile = s * per + t
                keys = pl.ds(pl.multiple_of(tile * TK, TK), TK)
                st = mm(kaug[keys, :], qs[...], NT)
                p = jnp.exp(st - lse)
                dp = mm(vs[keys, :], dos[...], NT)
                ds = (p * (dp - delta)).astype(BF)
                dv_s[keys, :] += mm(p.astype(BF), dos[...])
                dk_s[keys, :] += mm(ds, qs[...])
                for h in range(3):
                    cols = slice(h * TQ, (h + 1) * TQ)
                    acc[(h + 1) * HD : (h + 2) * HD, :] += mm(kt[tile, h * HD : (h + 1) * HD, :], ds[:, cols])
                return 0

            return lax.fori_loop(tlo[i, slot0 + s], thi[i, slot0 + s], key_loop, 0)

        lax.fori_loop(0, slots, slot_loop, 0)
        if last:
            dq_ref[rows, :] = (acc[...] * HD ** (-0.5)).T.astype(BF)
        else:
            dq_ref[i] = acc[...]
        return 0

    lax.fori_loop(0, q_ref.shape[0] // TQ, tile_loop, 0)
    for j, out in enumerate(d_refs):

        def finish(k, _, j=j, out=out):
            to = pl.ds(pl.multiple_of(k * TK, TK), TK)
            frm = pl.ds(pl.multiple_of(j * rows_each + k * TK, TK), TK)
            out[to, 0:128] = dv_s[frm, 0:128].astype(BF)
            out[to, 128:256] = jnp.where(lane_ids(TK) < 64, dv_s[frm, 128:256], dk_s[frm, 0:128]).astype(BF)
            out[to, 256:384] = dk_s[frm, 128:256].astype(BF)
            return 0

        lax.fori_loop(0, rows_each // TK, finish, 0)


def attend_back(tables, q, do, ot, lse, sources, slot0, state=None, last=False, name="attend_back", size=14_000_000_000):
    tlo, thi, qfirst, lo, hi, slo, shi = tables
    tiles = q.shape[0] // TQ
    keys = sum(s.shape[0] for s in sources)
    ins = (q, do, ot, lse, *sources, lo, hi, slo, shi) + ((state,) if state is not None else ())
    dq = jax.ShapeDtypeStruct(q.shape, BF) if last else jax.ShapeDtypeStruct((tiles, 256, TQ), F32)
    outs = (dq,) + tuple(jax.ShapeDtypeStruct(s.shape, BF) for s in sources)
    return pl.pallas_call(
        functools.partial(attend_back_kernel, slot0=slot0, count=len(sources), resume=state is not None, last=last),
        out_shape=outs,
        grid_spec=pltpu.PrefetchScalarGridSpec(
            num_scalar_prefetch=3,
            grid=(1,),
            in_specs=[whole(x.shape) for x in ins],
            out_specs=tuple(whole(x.shape) for x in outs),
            scratch_shapes=[
                pltpu.VMEM((keys, 256), BF),
                pltpu.VMEM((keys // TK, 3 * HD, TK), BF),
                pltpu.VMEM((keys, 256), BF),
                pltpu.VMEM((3 * TQ, 256), BF),
                pltpu.VMEM((3 * TQ, 256), BF),
                pltpu.VMEM((256, TQ), F32),
                pltpu.VMEM((keys, 256), F32),
                pltpu.VMEM((keys, 256), F32),
            ],
        ),
        compiler_params=pltpu.CompilerParams(vmem_limit_bytes=32 << 20),
        cost_estimate=cost(size, size // 1000, size // 3000),
        name=name,
    )(tlo, thi, qfirst, *ins)


def project_kernel(
    who, x0, x1, x2, x3_top, x3_bottom, w_mine, w_other, bias_ref, chosen, q_ref, kv_ref, up_ref, down_ref, w_ref
):
    tall = w_mine.shape[0]
    rows = x0.shape[0]
    w_ref[pl.ds(pl.multiple_of(who[0] * tall, tall), tall), :] = w_mine[...]
    w_ref[pl.ds(pl.multiple_of((1 - who[0]) * tall, tall), tall), :] = w_other[...]
    for d, x in enumerate((x0, x1, x2, (x3_top, x3_bottom))):
        if d < 3:
            value = mm(x[...], w_ref[...]) + bias_ref[...]
        else:
            value = jnp.concatenate([mm(x[0][...], w_ref[...]), mm(x[1][...], w_ref[...])], axis=0) + bias_ref[...]
        at = slice(d * rows, (d + 1) * rows)
        q_ref[at, :] = (value[:, :256].astype(BF).astype(F32) * HD ** (-0.5)).astype(BF)
        kv = mm(chosen[d], value[:, 256:].astype(BF)).astype(BF)
        kv_ref[at, :] = kv
        inner = slice((d % 2) * rows, (d % 2 + 1) * rows)

        @pl.when(who[2] == d // 2)
        def _(inner=inner, kv=kv):
            down_ref[inner, :] = kv

        @pl.when(who[2] != d // 2)
        def _(inner=inner, kv=kv):
            up_ref[inner, :] = kv


def project(who, xs, w_mine, w_other, bias, chosen):
    sd = jax.ShapeDtypeStruct
    rows, width = xs[0].shape
    cols = w_mine.shape[1]
    ins = (*xs, w_mine, w_other, bias, chosen)
    outs = (
        sd((4 * rows, 256), BF), sd((4 * rows, cols - 256), BF), sd((2 * rows, cols - 256), BF),
        sd((2 * rows, cols - 256), BF), sd((width, cols), BF),
    )
    return pl.pallas_call(
        project_kernel,
        out_shape=outs,
        grid_spec=pltpu.PrefetchScalarGridSpec(
            num_scalar_prefetch=1,
            grid=(1,),
            in_specs=[whole(a.shape) for a in ins],
            out_specs=tuple(whole(a.shape) for a in outs),
        ),
        compiler_params=pltpu.CompilerParams(vmem_limit_bytes=24 << 20),
        cost_estimate=cost(3_000_000_000, 12_000_000),
        name="project",
    )(who, *ins)


def row_mean(v):
    return jnp.sum(v, axis=-1, keepdims=True) * (1.0 / v.shape[-1])

def dense_kernel(
    who, o_ref, wo_a, wo_b, win_a, win_b, wback_a, wback_b, x_ref, teacher_ref, cot_ref, keep_ref, vec_ref,
    out_ref, dres_ref, dparts_ref, act_ref, dbr_ref, dpre_ref, hid_ref, dproj_ref, sums_ref,
    wo, win, wback, xh, inv, hidden, gp, acc, sems, *, FB
):
    rows, width = x_ref.shape
    groups = o_ref.shape[0] // rows
    part = width // groups
    units = win.shape[1]
    wo_loads, win_loads, wback_loads = [], [], []
    for i in range(2):
        side = who[0] if i == 0 else 1 - who[0]
        for e in range(groups // 2):
            to = pl.multiple_of(((side * (groups // 2) + e) ^ who[1]) * part, part)
            wo_loads.append(
                pltpu.make_async_copy((wo_a, wo_b)[i].at[pl.ds(e * part, part)], wo.at[pl.ds(to, part)], sems.at[2 * i + e])
            )
        for j, (pieces, target, held) in enumerate((((win_a, win_b), win, win_loads), ((wback_a, wback_b), wback, wback_loads))):
            tall = target.shape[0] // 2
            to = pl.multiple_of(side * tall, tall)
            held.append(pltpu.make_async_copy(pieces[i], target.at[pl.ds(to, tall)], sems.at[4 + 2 * i + j]))
    for load in wo_loads + win_loads + wback_loads:
        load.start()
    b_out, b_in, b_back = vec_ref[0:1, 0:width], vec_ref[1:2, :], vec_ref[2:3, 0:width]
    gain1, shift1, gain2, shift2 = (vec_ref[i : i + 1, 0:width] for i in range(3, 7))
    for load in wo_loads:
        load.wait()
    total = x_ref[...].astype(F32) + b_out
    for i in range(groups):
        total += mm(o_ref[i * rows : (i + 1) * rows, :], wo[i * part : (i + 1) * part, :])
    center = total - row_mean(total)
    scale = lax.rsqrt(row_mean(center * center) + 1e-12)
    inv[...] = scale
    unit = center * scale
    xh[...] = unit
    hid = unit * gain1 + shift1
    hidden[...] = hid
    hid_ref[...] = hid.astype(BF)
    acc[...] = jnp.zeros_like(acc)
    for load in win_loads + wback_loads:
        load.wait()

    def up(n, _):
        cols = pl.ds(pl.multiple_of(n * FB, FB), FB)
        pre = mm(hid_ref[...], win[:, cols]) + vec_ref[1:2, cols]
        cdf = 0.5 + 0.5 * lax.erf(pre * 0.7071067811865476)
        act = (pre * cdf).astype(BF)
        act_ref[:, cols] = act
        gp[:, cols] = cdf + pre * (jnp.exp(pre * pre * -0.5) * 0.3989422804014327)
        acc[...] += mm(act, wback[cols, :])
        return 0

    lax.fori_loop(0, units // FB, up, 0, unroll=True)
    total = hidden[...] + acc[...] + b_back
    center = total - row_mean(total)
    scale = lax.rsqrt(row_mean(center * center) + 1e-12)
    unit = center * scale
    result = unit * gain2 + shift2
    out_ref[...] = result.astype(BF)
    grad = cot_ref[...].astype(F32) + keep_ref[...] * (result - teacher_ref[...].astype(F32))
    def put(row, value):
        sums_ref[row : row + 1, 0 : value.shape[1]] = value
    put(5, jnp.sum(grad * unit, axis=0, keepdims=True))
    put(6, jnp.sum(grad, axis=0, keepdims=True))
    grad = grad * gain2
    back = scale * (grad - row_mean(grad) - unit * row_mean(grad * unit))
    acc[...] = back
    low = back.astype(BF)
    dbr_ref[...] = low
    put(2, jnp.sum(low.astype(F32), axis=0, keepdims=True))

    def down(n, _):
        cols = pl.ds(pl.multiple_of(n * FB, FB), FB)
        dpre = (mm(dbr_ref[...], wback[cols, :], NT) * gp[:, cols]).astype(BF)
        dpre_ref[:, cols] = dpre
        sums_ref[1:2, cols] = jnp.sum(dpre.astype(F32), axis=0, keepdims=True)
        acc[...] += mm(dpre, win[:, cols], NT)
        return 0

    lax.fori_loop(0, units // FB, down, 0, unroll=True)
    grad = acc[...]
    unit = xh[...]
    put(3, jnp.sum(grad * unit, axis=0, keepdims=True))
    put(4, jnp.sum(grad, axis=0, keepdims=True))
    grad = grad * gain1
    back = inv[...] * (grad - row_mean(grad) - unit * row_mean(grad * unit))
    dres_ref[...] = back
    low = back.astype(BF)
    dproj_ref[...] = low
    put(0, jnp.sum(low.astype(F32), axis=0, keepdims=True))
    for i in range(groups):
        dparts_ref[i * rows : (i + 1) * rows, :] = mm(low, wo[i * part : (i + 1) * part, :], NT).astype(BF)


def dense(who, o, weights, x, teacher, cot, keep, vec):
    rows, width = x.shape
    units = vec.shape[1]
    sd = jax.ShapeDtypeStruct
    outs = (
        sd((rows, width), BF), sd((rows, width), F32), sd(o.shape, BF), sd((rows, units), BF), sd((rows, width), BF),
        sd((rows, units), BF), sd((rows, width), BF), sd((rows, width), BF), sd((8, units), F32),
    )
    ins = (o, *weights, x, teacher, cot, keep, vec)
    stay = pl.BlockSpec(memory_space=pl.ANY)
    return pl.pallas_call(
        functools.partial(dense_kernel, FB=FFB),
        out_shape=outs,
        grid_spec=pltpu.PrefetchScalarGridSpec(
            num_scalar_prefetch=1,
            grid=(1,),
            in_specs=[whole(o.shape)] + [stay] * 6 + [whole(a.shape) for a in ins[7:]],
            out_specs=tuple(whole(a.shape) for a in outs),
            scratch_shapes=[
                pltpu.VMEM((width, width), BF), pltpu.VMEM((width, units), BF), pltpu.VMEM((units, width), BF),
                pltpu.VMEM((rows, width), F32), pltpu.VMEM((rows, 1), F32), pltpu.VMEM((rows, width), F32),
                pltpu.VMEM((rows, units), F32), pltpu.VMEM((rows, width), F32), pltpu.SemaphoreType.DMA((8,)),
            ],
        ),
        compiler_params=pltpu.CompilerParams(vmem_limit_bytes=50 << 20),
        cost_estimate=cost(12_000_000_000, 30_000_000, 4_000_000),
        name="dense",
    )(who, *ins)


def finish_kernel(who, dq_ref, own_ref, pair_ref, left_ref, right_ref, turn_ref, xt_ref, all_ref, mine_ref, other_ref, dw, sums):
    groups, rows = turn_ref.shape[:2]
    middle = groups * rows // 2
    sums[...] = jnp.zeros_like(sums)
    for d in range(groups):
        at = pl.ds(d * rows, rows)
        inner = pl.ds((d % (groups // 2)) * rows, rows)
        first = (d < groups // 2) == (who[2] == 0)
        back = own_ref[at, :].astype(F32) + pair_ref[at, :].astype(F32)
        back += jnp.where(first, left_ref[inner, :], right_ref[inner, :]).astype(F32)
        tok = mm(turn_ref[d], back.astype(BF)).astype(BF)
        dq = dq_ref[at, :]
        all_ref[at, 0:256] = dq
        all_ref[at, 256:640] = tok
        sums[0:1, 0:256] += jnp.sum(dq.astype(F32), axis=0, keepdims=True)
        sums[0:1, 256:640] += jnp.sum(tok.astype(F32), axis=0, keepdims=True)
    del middle
    dw[...] = mm(xt_ref[...], all_ref[...]).astype(BF)
    tall = dw.shape[0] // 2
    low = sums[...].astype(BF)
    for out, side in ((mine_ref, who[0]), (other_ref, 1 - who[0])):
        out[0:tall, :] = dw[pl.ds(pl.multiple_of(side * tall, tall), tall), :]
        for k in range(9):
            out[k : k + 1, 0:64] = low[0:1, 64 * (k + 1) : 64 * (k + 2)]


def finish(who, dq, own, pair, left, right, turn, xt):
    sd = jax.ShapeDtypeStruct
    cols = dq.shape[1] + own.shape[1]
    tall = xt.shape[0] // 2
    ins = (dq, own, pair, left, right, turn, xt)
    outs = (sd((dq.shape[0], cols), BF), sd((tall, cols), BF), sd((tall, cols), BF))
    return pl.pallas_call(
        finish_kernel,
        out_shape=outs,
        grid_spec=pltpu.PrefetchScalarGridSpec(
            num_scalar_prefetch=1,
            grid=(1,),
            in_specs=[whole(a.shape) for a in ins],
            out_specs=tuple(whole(a.shape) for a in outs),
            scratch_shapes=[pltpu.VMEM((xt.shape[0], cols), BF), pltpu.VMEM((16, cols), F32)],
        ),
        compiler_params=pltpu.CompilerParams(vmem_limit_bytes=32 << 20),
        cost_estimate=cost(3_000_000_000, 14_000_000),
        name="finish",
    )(who, *ins)


def spread_kernel(all_ref, w_ref, own_ref, gx_ref, gy_ref, left_ref, right_ref):
    rows, width = own_ref.shape
    cut = width // 2
    parts = [mm(all_ref[d * rows : (d + 1) * rows, :], w_ref[...], NT).astype(BF) for d in range(4)]
    own_ref[...] = parts[0]
    gx_ref[0:rows, :] = parts[1][:, :cut]
    right_ref[...] = parts[1][:, cut:]
    left_ref[...] = parts[2][:, :cut]
    gy_ref[0:rows, :] = parts[2][:, cut:]
    gx_ref[rows:, :] = parts[3][:, :cut]
    gy_ref[rows:, :] = parts[3][:, cut:]


def spread_x(d_all, w_heads):
    rows, width = d_all.shape[0] // 4, w_heads.shape[0]
    shapes = ((rows, width), (2 * rows, width // 2), (2 * rows, width // 2), (rows, width // 2), (rows, width // 2))
    return pl.pallas_call(
        spread_kernel,
        out_shape=tuple(jax.ShapeDtypeStruct(s, BF) for s in shapes),
        grid=(1,),
        in_specs=[whole(d_all.shape), whole(w_heads.shape)],
        out_specs=tuple(whole(s) for s in shapes),
        compiler_params=pltpu.CompilerParams(vmem_limit_bytes=24 << 20),
        cost_estimate=cost(2_000_000_000, 7_000_000),
        name="spread_x",
    )(d_all, w_heads)


def place_blocks(who, refs, put):
    s1, s2 = lax.rem(who[1], 2), who[1] // 2
    tall = refs[0].shape[0] // 2
    for at, ref in enumerate(refs):
        color, i = at // 2, at % 2
        for j in range(2):
            spot = (s1 ^ i) * 2 + (s2 ^ j) if color == 0 else 4 + (s2 ^ i) * 2 + (s1 ^ j)
            put(pl.ds(pl.multiple_of(spot * tall, 8), tall), ref[j * tall : (j + 1) * tall, :].astype(F32))


def back_out_kernel(who, a, b, c, d, out_ref):
    width = out_ref.shape[1]
    tall = out_ref.shape[0] // 4

    def put(at, value):
        for k in range(4):
            out_ref[pl.ds(k * tall + at.start, at.size), :] = value[:, k * width : (k + 1) * width]

    place_blocks(who, (a, b, c, d), put)


def in_out_kernel(who, a, b, c, d, in_ref, out_ref, vec_ref, held):
    def put(at, value):
        held[at, :] = value

    place_blocks(who, (a, b, c, d), put)
    tall, width = out_ref.shape
    in_ref[...] = held[0:tall, :]
    for k in range(3):
        out_ref[k * 128 : (k + 1) * 128, :] = held[tall:, k * width : (k + 1) * width]
    vec_ref[...] = held[tall : tall + 8, 3 * width :]


def out_call(kernel, who, pieces, shapes, scratch, name):
    return pl.pallas_call(
        kernel,
        out_shape=tuple(jax.ShapeDtypeStruct(s, F32) for s in shapes),
        grid_spec=pltpu.PrefetchScalarGridSpec(
            num_scalar_prefetch=1,
            grid=(1,),
            in_specs=[whole(a.shape) for a in pieces],
            out_specs=tuple(whole(s) for s in shapes),
            scratch_shapes=scratch,
        ),
        compiler_params=pltpu.CompilerParams(vmem_limit_bytes=24 << 20),
        cost_estimate=cost(1_000_000, 9_000_000),
        name=name,
    )(who, *pieces)


def heads_kernel(who, h0, h1, h2, h3, q_ref, k_ref, v_ref, bias_ref, held):
    tall = q_ref.shape[0]
    for d, ref in enumerate((h0, h1, h2, h3)):
        held[who[1] ^ d] = ref[...]
    for a in range(4):
        cols = slice(a * 192, (a + 1) * 192)
        q_ref[:, cols] = held[a, 0:tall, 64:256].astype(F32)
        v_ref[:, cols] = held[a, 0:tall, 256:448].astype(F32)
        k_ref[:, cols] = held[a, 0:tall, 448:640].astype(F32)
        line = held[a, 0:16, 0:64].astype(F32)
        for k in range(3):
            spot = slice(a * 192 + k * 64, a * 192 + (k + 1) * 64)
            bias_ref[0:1, spot] = line[k : k + 1]
            bias_ref[8:9, spot] = line[k + 3 : k + 4]


def heads_out(who, pieces):
    sd = jax.ShapeDtypeStruct
    outs = (sd((384, 768), F32),) * 3 + (sd((16, 768), F32),)
    return pl.pallas_call(
        heads_kernel,
        out_shape=outs,
        grid_spec=pltpu.PrefetchScalarGridSpec(
            num_scalar_prefetch=1,
            grid=(1,),
            in_specs=[whole(a.shape) for a in pieces],
            out_specs=tuple(whole(a.shape) for a in outs),
            scratch_shapes=[pltpu.VMEM((4, *pieces[0].shape), BF)],
        ),
        compiler_params=pltpu.CompilerParams(vmem_limit_bytes=24 << 20),
        cost_estimate=cost(1_000_000, 6_000_000),
        name="heads_out",
    )(who, *pieces)


def swap(block, axis="fsdp"):
    return lax.ppermute(block, axis, [(0, 1), (1, 0)])


def shifted(block, axis, distance):
    devices = range(lax.axis_size(axis))
    route = [(i - distance, i) for i in devices if i - distance in devices]
    return lax.ppermute(block, axis, route)


def flip(block, bit, axis="uly"):
    return lax.ppermute(block, axis, [(i, i ^ bit) for i in range(lax.axis_size(axis))])


def exchange(rows, axis):
    return lax.all_to_all(rows, axis, split_axis=0, concat_axis=0, tiled=True)


def spread_rows(rows, axis):
    count = lax.axis_size(axis)
    return exchange(jnp.broadcast_to(rows[None], (count, *rows.shape)).reshape(-1, rows.shape[1]), axis)


def sum_parts(rows, count):
    got = rows.reshape(count, -1, rows.shape[1])
    return sum(got[i].astype(F32) for i in range(count)).astype(BF)


def sum_scatter(rows, axis):
    return sum_parts(exchange(rows, axis), lax.axis_size(axis))


def add(left, right):
    return (left.astype(F32) + right.astype(F32)).astype(BF)


def sides(rows, bit):
    side = jnp.where((lax.axis_index("uly") & bit) > 0, 1, 0)
    split = rows.reshape(2, -1, rows.shape[1])
    return (
        lax.dynamic_index_in_dim(split, side, 0, keepdims=False),
        lax.dynamic_index_in_dim(split, 1 - side, 0, keepdims=False),
    )


def halve(rows, bit):
    mine, other = sides(rows, bit)
    return add(mine, flip(other, bit))


def halves(rows):
    middle = rows.shape[0] // 2
    return rows[:middle], rows[middle:]


def line_gather(rows):
    held = rows[None]
    bit = lax.axis_size("ctx") // 2
    while bit > 0:
        low = (lax.axis_index("ctx") & bit) == 0
        got = flip(held, bit, "ctx")
        held = jnp.stack([jnp.where(low, held, got), jnp.where(low, got, held)], axis=1).reshape(-1, *rows.shape)
        bit //= 2
    return held.reshape(-1, rows.shape[1])


def tie(*values):
    return lax.optimization_barrier(values)


def on_device(
    tokens, teacher, cotangent, valid, teacher_ok, doc_starts, w_query, w_key, w_value, w_out, w_in, w_back,
    bias_query, bias_value, bias_out, bias_in, bias_back, norm1_gain, norm1_bias, norm2_gain, norm2_bias,
):
    groups = lax.axis_size("uly")
    spans = lax.axis_size("ctx")
    rows, width = tokens.shape
    block = rows * groups * 2
    stream = block * spans
    ctx_index = lax.axis_index("ctx")
    uly = lax.axis_index("uly")
    half = lax.axis_index("fsdp")
    head_cols = width // groups
    shard = w_query.shape[0]
    middle = groups * rows // 2
    upper = uly // 2

    valid_one = valid[None, :]
    valid_own = jnp.concatenate([valid_one, flip(valid_one, 1), flip(valid_one, 2), flip(valid_one, 3)], axis=0)
    x_own, valid_own = tie(tokens, valid_own)
    x_x, x_y = flip(x_own, 1), flip(x_own, 2)
    valid_pair = swap(valid_own)
    valid_both = jnp.stack([valid_own, valid_pair]).reshape(2, 2, 2, rows)
    valid_high = lax.dynamic_index_in_dim(valid_both, 1 - upper, 1, keepdims=False)
    valid_low = lax.dynamic_index_in_dim(valid_both, upper, 1, keepdims=False)
    halo = (shifted(valid_high, "ctx", 1), shifted(valid_low, "ctx", -1))
    block_valid = jnp.concatenate([valid_own, valid_pair, halo[0][0], halo[1][0], halo[0][1], halo[1][1]], axis=0)
    count = jnp.full((8, 128), jnp.sum(valid_both), jnp.int32)
    bit = 1
    while bit < spans:
        count = count + flip(count, bit, "ctx")
        bit *= 2
    count = count[0, 0].astype(F32)

    start_col = uly * head_cols
    cut = [lax.dynamic_slice_in_dim(w, start_col, head_cols, 1) for w in (w_query, w_value, w_key)]
    w_mine = jnp.concatenate([jnp.zeros((shard, 256 - head_cols), BF), *cut], axis=1)
    w_other = swap(w_mine)
    who = jnp.stack([half, uly, upper])
    small = (bias_query, bias_value, bias_out, bias_in, bias_back, norm1_gain, norm1_bias, norm2_gain, norm2_bias)
    packed = jnp.concatenate([p.reshape(-1, shard) for p in small], axis=0)
    packed_pair = swap(packed)
    packed = jnp.stack([jnp.where(half == 0, packed, packed_pair), jnp.where(half == 0, packed_pair, packed)])
    vectors = []
    at = 0
    for p in small:
        n = p.shape[0] // shard
        vectors.append(packed[:, at : at + n].reshape(-1).astype(F32))
        at += n
    bq_all, bv_all = vectors[:2]
    vec = jnp.stack([jnp.pad(v, (0, w_in.shape[1] - v.shape[0])) for v in vectors[2:]] + [jnp.zeros((w_in.shape[1],), F32)])
    bias_heads = jnp.concatenate(
        [
            jnp.zeros((256 - head_cols,), F32),
            lax.dynamic_slice_in_dim(bq_all, start_col, head_cols, 0),
            lax.dynamic_slice_in_dim(bv_all, start_col, head_cols, 0),
            jnp.zeros((head_cols,), F32),
        ]
    )

    place = jnp.arange(groups, dtype=jnp.int32)
    two = jnp.arange(2, dtype=jnp.int32)
    in_plane = place ^ uly
    halo_group = jnp.concatenate([uly ^ (2 * (1 - upper) + two), uly ^ (2 * upper + two)])
    halo_plane = ctx_index + jnp.where(place < 2, -1, 1)
    plane_of = jnp.concatenate([jnp.full((2 * groups,), 1, jnp.int32) * ctx_index, halo_plane, halo_plane])
    group_of = jnp.concatenate([in_plane, in_plane, halo_group, halo_group])
    mine = jnp.full((groups,), 1, jnp.int32) * half
    core_of = jnp.concatenate([mine, 1 - mine, mine, 1 - mine])
    block_id = plane_of * (2 * groups) + group_of * 2 + core_of
    spot = block_id[:, None] * rows + jnp.arange(rows, dtype=jnp.int32)[None, :]
    edges = jnp.concatenate([doc_starts, jnp.full((DOCS + 1,), stream, jnp.int32)])
    window_first = jnp.maximum(ctx_index * block - block // 2, 0)
    first_doc = jnp.sum((doc_starts <= window_first).astype(jnp.int32)) - 1
    near = lax.dynamic_slice_in_dim(edges, first_doc, DOCS + 1, 0)
    tiles = groups * rows // TQ
    per = rows // TQ
    tile_ids = jnp.arange(tiles, dtype=jnp.int32)
    qfirst = ctx_index * block + (((tile_ids // per) ^ uly) * 2 + half) * rows + lax.rem(tile_ids, per) * TQ
    q_lo = jnp.max(jnp.where(near[None, :] <= qfirst[:, None], near[None, :], 0), axis=1)
    q_hi = jnp.min(jnp.where(near[None, :] <= qfirst[:, None] + TQ - 1, stream, near[None, :]), axis=1)
    limits = jnp.concatenate([near, q_lo, q_hi])
    counted = jnp.sum(block_valid[:, None, :] * (spot[:, None, :] < limits[None, :, None]), axis=-1)
    bounds = counted[:, : DOCS + 1]
    cnt_lo = counted[:, DOCS + 1 : DOCS + 1 + tiles].T
    cnt_hi = counted[:, DOCS + 1 + tiles :].T
    pad64 = jnp.zeros((bounds.shape[0], 128 - DOCS), jnp.int32)
    lo_tab = jnp.concatenate([bounds[:, :DOCS], pad64], axis=1)
    hi_tab = jnp.concatenate([bounds[:, 1:], pad64], axis=1)
    slo_tab = jnp.concatenate([near[:DOCS], pad64[0]])[None, :]
    shi_tab = jnp.concatenate([near[1:], pad64[0]])[None, :]
    some = cnt_hi > cnt_lo
    tlo = jnp.where(some, cnt_lo // TK, 0)
    thi = jnp.where(some, (cnt_hi + TK - 1) // TK, 0)
    tables = (tlo, thi, qfirst, lo_tab, hi_tab, slo_tab, shi_tab)
    before = mm(valid_own.astype(BF), (jnp.arange(rows)[:, None] < jnp.arange(rows)[None, :]).astype(BF)).astype(jnp.int32)
    goes_to = jnp.where(valid_own > 0, before, rows)
    chosen = (goes_to[:, None, :] == jnp.arange(rows, dtype=jnp.int32)[None, :, None]).astype(BF)
    loss_scale = jnp.float32(stream) / count
    keep = (loss_scale * (valid * teacher_ok).astype(F32))[:, None]
    turned = (goes_to[:, :, None] == jnp.arange(rows, dtype=jnp.int32)[None, None, :]).astype(BF)

    x_x, x_y, w_other, chosen, bias_heads, *tables = tie(x_x, x_y, w_other, chosen, bias_heads, *tables)
    x_top, x_bottom = flip(x_y[: rows // 2], 1), flip(x_x[rows // 2 :], 2)

    q_low, kv_own, kv_up, kv_down, w_heads = project(
        who, (tokens, x_x, x_y, x_top, x_bottom), w_mine, w_other, bias_heads[None, :], chosen
    )
    x_plane = (tokens, x_x, x_y, x_top, x_bottom)
    kv_from_left, kv_from_right = shifted(kv_up, "ctx", 1), shifted(kv_down, "ctx", -1)
    w_out, w_in, w_back, kv_own = tie(w_out, w_in, w_back, kv_own)
    weights = (w_out, swap(w_out), w_in, swap(w_in), w_back, swap(w_back))
    kv_pair = swap(kv_own)
    state = attend(tables, q_low, (kv_own,), 0)
    kv_halo = jnp.concatenate([kv_from_left, kv_from_right], axis=0)
    kv_halo, kv_pair, *state = tie(kv_halo, kv_pair, *state)
    kv_halo_pair = swap(kv_halo)
    state = attend(tables, q_low, (kv_pair,), groups, state)
    o_heads, o_turned, lse = attend(tables, q_low, (kv_halo, kv_halo_pair), 2 * groups, state, last=True)
    x_turned = jnp.concatenate([x.T for x in x_plane], axis=1)
    o_rel = o_heads.reshape(groups, rows, head_cols)
    o_all = jnp.concatenate([o_rel[0]] + [flip(o_rel[d], d) for d in range(1, groups)], axis=0)

    out, d_resid1, d_parts, act, d_branch, d_pre, hidden_low, d_proj, sums = dense(
        who, o_all, weights, tokens, teacher, cotangent, keep, vec
    )
    d_rel = d_parts.reshape(groups, rows, head_cols)
    d_heads = jnp.concatenate([d_rel[0]] + [flip(d_rel[d], d) for d in range(1, groups)], axis=0)
    tall = w_back.shape[0]
    vector_rows = jnp.concatenate(
        [sums[i, :width].reshape(2, -1) for i in (0, 2, 3, 4, 5, 6)] + [sums[1].reshape(2, -1)], axis=1
    ).reshape(2, -1, width)
    vector_rows = jnp.pad(vector_rows, ((0, 0), (0, 128 - vector_rows.shape[1]), (0, 0))).astype(BF)
    o_rows = o_all.reshape(groups, rows, head_cols)

    def back_part(side):
        return mm(lax.dynamic_slice_in_dim(act, side * tall, tall, 1), d_branch, TN).astype(BF)

    def in_part(side):
        return mm(lax.dynamic_slice_in_dim(hidden_low, side * shard, shard, 1), d_pre, TN).astype(BF)

    def out_part(side):
        both = [
            mm(lax.dynamic_index_in_dim(o_rows, (2 * side + e) ^ uly, 0, keepdims=False), d_proj, TN).astype(BF)
            for e in range(2)
        ]
        stack = jnp.concatenate([*both, lax.dynamic_index_in_dim(vector_rows, side, 0, keepdims=False)], axis=0)
        return jnp.concatenate([stack[i * 128 : (i + 1) * 128] for i in range(4)], axis=1)

    back_sum = add(back_part(half), swap(back_part(1 - half)))
    back_sum = jnp.concatenate([back_sum[i * shard : (i + 1) * shard] for i in range(4)], axis=1)
    in_sum = jnp.concatenate(
        [add(in_part(half), swap(in_part(1 - half))), add(out_part(half), swap(out_part(1 - half)))], axis=0
    )

    d_heads, back_sum = tie(d_heads, back_sum)
    b1, b2 = halves(back_sum)
    b1m, b1o = sides(b1, 1)
    b2m, b2o = sides(b2, 2)
    d_heads, b1m, b1o, b2m, b2o = tie(d_heads, b1m, b1o, b2m, b2o)
    b1g, b2g = flip(b1o, 1), flip(b2o, 2)
    args = (tables, q_low, d_heads, o_turned, lse)
    dq_state, dkv_halo_pair = attend_back(*args, (kv_halo_pair,), 3 * groups, name="back_halo_pair")
    dkv_halo_pair, dq_state = tie(dkv_halo_pair, dq_state)
    halo_got = swap(dkv_halo_pair)
    dq_state, dkv_halo = attend_back(*args, (kv_halo,), 2 * groups, dq_state, name="back_halo", size=1_000_000)
    dq_state, dkv_halo, halo_got, b1g, b2g = tie(dq_state, dkv_halo, halo_got, b1g, b2g)
    halo_sum = add(dkv_halo, halo_got)
    b1, b2 = add(b1m, b1g), add(b2m, b2g)
    b1m, b1o = sides(b1, 2)
    b2m, b2o = sides(b2, 1)
    i1, i2 = halves(in_sum)
    i1m, i1o = sides(i1, 1)
    i2m, i2o = sides(i2, 2)
    halo_lo, halo_hi = halves(halo_sum)
    dq_state, b1o, b2o, b1m, b2m, i1m, i2m, i1o, i2o, halo_lo, halo_hi = tie(
        dq_state, b1o, b2o, b1m, b2m, i1m, i2m, i1o, i2o, halo_lo, halo_hi
    )
    m1g = flip(jnp.concatenate([i1o, b2o], axis=0), 1)
    m2g = flip(jnp.concatenate([i2o, b1o], axis=0), 2)
    from_left, from_right = shifted(halo_hi, "ctx", 1), shifted(halo_lo, "ctx", -1)
    dq_state, dkv_pair = attend_back(*args, (kv_pair,), groups, dq_state, name="back_pair")
    dq_state, dkv_pair, m1g, m2g, from_left, from_right = tie(dq_state, dkv_pair, m1g, m2g, from_left, from_right)
    tall = i1o.shape[0]
    i1g, b2g, i2g, b1g = m1g[:tall], m1g[tall:], m2g[:tall], m2g[tall:]
    back_line = jnp.concatenate([add(b1m, b1g), add(b2m, b2g)], axis=0)
    i1, i2 = add(i1m, i1g), add(i2m, i2g)
    i1m, i1o = sides(i1, 2)
    i2m, i2o = sides(i2, 1)
    dq_state, dkv_pair, back_line, i1m, i2m, i1o, i2o = tie(dq_state, dkv_pair, back_line, i1m, i2m, i1o, i2o)
    i1g, i2g = flip(i1o, 2), flip(i2o, 1)
    back_line = exchange(back_line, "ctx")
    pair_back = swap(dkv_pair)
    dq, dkv_own = attend_back(*args, (kv_own,), 0, dq_state, last=True, name="back_own")
    dq, dkv_own, i1g, i2g, back_line, pair_back = tie(dq, dkv_own, i1g, i2g, back_line, pair_back)
    in_line = jnp.concatenate([add(i1m, i1g), add(i2m, i2g)], axis=0)

    back_line = sum_parts(back_line, spans)
    in_line = exchange(in_line, "ctx")
    d_all, heads_mine, heads_other = finish(who, dq, dkv_own, pair_back, from_left, from_right, turned, x_turned)
    heads_sum = add(heads_mine, swap(heads_other))
    dx_own, give_x, give_y, left_next, right_next = spread_x(d_all, w_heads)
    give_x, give_y = flip(give_x, 1), flip(give_y, 2)
    left_next = flip(add(left_next, give_x[rows:]), 2)
    right_next = flip(add(right_next, give_y[rows:]), 1)
    grad_in = d_resid1 + dx_own.astype(F32)
    grad_in = grad_in + jnp.concatenate([give_x[:rows].astype(F32), give_y[:rows].astype(F32)], axis=1)
    grad_in = grad_in + jnp.concatenate([left_next.astype(F32), right_next.astype(F32)], axis=1)

    b1, b2 = halves(line_gather(back_line))
    b1 = jnp.concatenate([b1, flip(b1, 2)], axis=0)
    b2 = jnp.concatenate([b2, flip(b2, 1)], axis=0)
    (g_back,) = out_call(back_out_kernel, who, (b1, flip(b1, 1), b2, flip(b2, 2)), (w_back.shape,), [], "back_out")
    i1, i2 = halves(line_gather(sum_parts(in_line, spans)))
    i1 = jnp.concatenate([i1, flip(i1, 2)], axis=0)
    i2 = jnp.concatenate([i2, flip(i2, 1)], axis=0)
    g_in, g_out, g_vec = out_call(
        in_out_kernel, who, (i1, flip(i1, 1), i2, flip(i2, 2)), (w_in.shape, w_out.shape, (8, width)),
        [pltpu.VMEM((shard + 128, w_in.shape[1]), F32)], "in_out",
    )
    heads_sum = line_gather(sum_scatter(heads_sum, "ctx"))
    g_query, g_key, g_value, g_bias = heads_out(who, [heads_sum] + [flip(heads_sum, d) for d in range(1, groups)])
    g_bias_q = lax.dynamic_slice_in_dim(g_bias[0], half * shard, shard, 0)
    g_bias_v = lax.dynamic_slice_in_dim(g_bias[8], half * shard, shard, 0)
    flat = g_vec.reshape(-1)
    g_bo, g_bb, g_g1, g_s1, g_g2, g_s2 = [flat[i * shard : (i + 1) * shard] for i in range(6)]
    g_bin = flat[6 * shard : 6 * shard + bias_in.shape[0]]
    return (
        out, grad_in, g_query, g_key, g_value, g_out, g_in, g_back,
        g_bias_q, g_bias_v, g_bo, g_bin, g_bb, g_g1, g_s1, g_g2, g_s2,
    )


def solution(mesh):
    placed = (
        P(("ctx", "uly", "fsdp"), None),
        P(("ctx", "uly", "fsdp"), None),
        P(("ctx", "uly", "fsdp"), None),
        P(("ctx", "uly", "fsdp")),
        P(("ctx", "uly", "fsdp")),
        P(),
        P("fsdp", None),
        P("fsdp", None),
        P("fsdp", None),
        P("fsdp", None),
        P("fsdp", None),
        P("fsdp", None),
        P("fsdp"),
        P("fsdp"),
        P("fsdp"),
        P("fsdp"),
        P("fsdp"),
        P("fsdp"),
        P("fsdp"),
        P("fsdp"),
        P("fsdp"),
    )
    return jax.shard_map(
        on_device,
        mesh=mesh,
        in_specs=placed,
        out_specs=(
            P(("ctx", "uly", "fsdp"), None),
            P(("ctx", "uly", "fsdp"), None),
            P("fsdp", None),
            P("fsdp", None),
            P("fsdp", None),
            P("fsdp", None),
            P("fsdp", None),
            P("fsdp", None),
            P("fsdp"),
            P("fsdp"),
            P("fsdp"),
            P("fsdp"),
            P("fsdp"),
            P("fsdp"),
            P("fsdp"),
            P("fsdp"),
            P("fsdp"),
        ),
        check_vma=False,
    )
```

```python
import functools

import jax
import jax.numpy as jnp
from jax import lax
from jax.experimental import pallas as pl
from jax.experimental.pallas import tpu as pltpu
from jax.sharding import PartitionSpec as P

HEADS = 12
HD = 64
BLK = 512
TQ = 256
TK = 256
DOCS = 64
FFB = 768
GRANT = 63 << 20
MASKED = -1e30
BF = jnp.bfloat16
F32 = jnp.float32
NT = (((1,), (1,)), ((), ()))
NN = (((1,), (0,)), ((), ()))
TN = (((0,), (0,)), ((), ()))


def mm(left, right, dims=NN):
    return lax.dot_general(left, right, dims, preferred_element_type=F32)


def whole(shape):
    return pl.BlockSpec(shape, lambda *_: (0,) * len(shape), pipeline_mode=pl.Buffered(1))


def cost(flops, moved, special=0):
    return pl.CostEstimate(flops=flops, bytes_accessed=moved, transcendentals=special)


def lane_ids(rows):
    return lax.broadcasted_iota(jnp.int32, (rows, 128), 1)


def build_keys(sources, slot0, lo_ref, hi_ref, kaug, transposed, low_half):
    per = BLK // TK
    for at, kv in enumerate(sources):

        def one(j, _, at=at, kv=kv):
            rows = pl.ds(pl.multiple_of(j * TK, TK), TK)
            tile = at * (kv.shape[0] // TK) + j
            slot = slot0 + at * (kv.shape[0] // BLK) + j // per
            out = pl.ds(pl.multiple_of(tile * TK, TK), TK)
            rank = lax.broadcasted_iota(jnp.int32, (TK, 128), 0) + lax.rem(j, per) * TK
            inside = (rank >= lo_ref[pl.ds(slot, 1), :]) & (rank < hi_ref[pl.ds(slot, 1), :])
            bias = jnp.where(inside, 0.0, MASKED).astype(BF)
            kaug[out, 0:128] = jnp.where(lane_ids(TK) < 64, bias, kv[rows, 128:256])
            kaug[out, 128:256] = kv[rows, 256:384]
            if low_half:
                transposed[tile] = kv[rows, 0:256].T[0:192]
            else:
                transposed[tile] = kaug[out, :].T[64:256]
            return 0

        lax.fori_loop(0, kv.shape[0] // TK, one, 0)


def stack_queries(q, first, slo_ref, shi_ref, qs):
    lane = lane_ids(TQ)
    spot = lax.broadcasted_iota(jnp.int32, (TQ, 128), 0) + first
    mine = ((spot >= slo_ref[...]) & (spot < shi_ref[...])).astype(F32).astype(BF)
    zero = jnp.zeros((TQ, 128), BF)
    low, high = q[:, 0:128], q[:, 128:256]
    mark = jnp.where(lane < 64, mine, zero)
    qs[0:TQ, 0:128] = jnp.where(lane < 64, mine, low)
    qs[TQ : 2 * TQ, 0:128] = mark
    qs[2 * TQ :, 0:128] = mark
    qs[0:TQ, 128:256] = zero
    qs[TQ : 2 * TQ, 128:256] = jnp.where(lane < 64, high, zero)
    qs[2 * TQ :, 128:256] = jnp.where(lane < 64, zero, high)


def attend_kernel(*refs, slot0, count, resume, last):
    tlo, thi, qfirst, q_ref = refs[:4]
    sources = refs[4 : 4 + count]
    lo_ref, hi_ref, slo_ref, shi_ref = refs[4 + count : 8 + count]
    at = 8 + count
    if resume:
        acc_in, stat_in = refs[at : at + 2]
        at += 2
    if last:
        o_ref, ot_ref, lse_ref = refs[at : at + 3]
        at += 3
    else:
        acc_out, stat_out = refs[at : at + 2]
        at += 2
    kaug, vt, qs, acc, m_s, l_s = refs[at:]
    build_keys(sources, slot0, lo_ref, hi_ref, kaug, vt, True)
    slots = count * sources[0].shape[0] // BLK
    per = BLK // TK

    def tile_loop(i, _):
        rows = pl.ds(pl.multiple_of(i * TQ, TQ), TQ)
        stack_queries(q_ref[rows, :], qfirst[i], slo_ref, shi_ref, qs)
        if resume:
            m_s[...] = stat_in[i, 0:1, :]
            l_s[...] = stat_in[i, 1:2, :]
            acc[...] = acc_in[i]
        else:
            m_s[...] = jnp.full_like(m_s, 2 * MASKED)
            l_s[...] = jnp.zeros_like(l_s)
            acc[...] = jnp.zeros_like(acc)

        def slot_loop(s, _):
            def key_loop(t, _):
                tile = s * per + t
                keys = pl.ds(pl.multiple_of(tile * TK, TK), TK)
                st = mm(kaug[keys, :], qs[...], NT)
                m_old = m_s[...]
                m_new = jnp.maximum(m_old, jnp.max(st, axis=0, keepdims=True))
                fade = jnp.exp(m_old - m_new)
                p = jnp.exp(st - m_new)
                l_s[...] = l_s[...] * fade + jnp.sum(p, axis=0, keepdims=True)
                m_s[...] = m_new
                low = p.astype(BF)
                for h in range(3):
                    cols = slice(h * TQ, (h + 1) * TQ)
                    part = slice(h * HD, (h + 1) * HD)
                    acc[part, :] = acc[part, :] * fade[:, cols] + mm(vt[tile, part, :], low[:, cols])
                return 0

            return lax.fori_loop(tlo[i, slot0 + s], thi[i, slot0 + s], key_loop, 0)

        lax.fori_loop(0, slots, slot_loop, 0)
        if last:
            total = l_s[...]
            for h in range(3):
                cols = slice(h * TQ, (h + 1) * TQ)
                part = slice(h * HD, (h + 1) * HD)
                acc[part, :] = acc[part, :] / total[:, cols]
            ot_ref[i] = acc[...]
            o_ref[rows, :] = acc[...].T.astype(BF)
            lse_ref[pl.ds(i, 1), :] = m_s[...] + jnp.log(total)
        else:
            acc_out[i] = acc[...]
            stat_out[i, 0:1, :] = m_s[...]
            stat_out[i, 1:2, :] = l_s[...]
        return 0

    lax.fori_loop(0, q_ref.shape[0] // TQ, tile_loop, 0)


def attend(tables, q, sources, slot0, state=None, last=False):
    tlo, thi, qfirst, lo, hi, slo, shi = tables
    tiles = q.shape[0] // TQ
    keys = sum(s.shape[0] for s in sources)
    ins = (q, *sources, lo, hi, slo, shi) + (tuple(state) if state else ())
    if last:
        outs = (
            jax.ShapeDtypeStruct((q.shape[0], 3 * HD), BF),
            jax.ShapeDtypeStruct((tiles, 3 * HD, TQ), F32),
            jax.ShapeDtypeStruct((tiles, 3 * TQ), F32),
        )
    else:
        outs = (
            jax.ShapeDtypeStruct((tiles, 3 * HD, TQ), F32),
            jax.ShapeDtypeStruct((tiles, 2, 3 * TQ), F32),
        )
    return pl.pallas_call(
        functools.partial(attend_kernel, slot0=slot0, count=len(sources), resume=state is not None, last=last),
        out_shape=outs,
        grid_spec=pltpu.PrefetchScalarGridSpec(
            num_scalar_prefetch=3,
            grid=(1,),
            in_specs=[whole(x.shape) for x in ins],
            out_specs=tuple(whole(x.shape) for x in outs),
            scratch_shapes=[
                pltpu.VMEM((keys, 256), BF),
                pltpu.VMEM((keys // TK, 3 * HD, TK), BF),
                pltpu.VMEM((3 * TQ, 256), BF),
                pltpu.VMEM((3 * HD, TQ), F32),
                pltpu.VMEM((1, 3 * TQ), F32),
                pltpu.VMEM((1, 3 * TQ), F32),
            ],
        ),
        compiler_params=pltpu.CompilerParams(vmem_limit_bytes=GRANT),
        cost_estimate=cost(12_000_000_000, 12_000_000, 10_000_000),
        name="attend",
    )(tlo, thi, qfirst, *ins)


def attend_back_kernel(*refs, slot0, count, resume, last):
    tlo, thi, qfirst, q_ref, do_ref, ot_ref, lse_ref = refs[:7]
    sources = refs[7 : 7 + count]
    lo_ref, hi_ref, slo_ref, shi_ref = refs[7 + count : 11 + count]
    at = 11 + count
    if resume:
        acc_in = refs[at]
        at += 1
    dq_ref = refs[at]
    d_refs = refs[at + 1 : at + 1 + count]
    kaug, kt, vs, qs, dos, acc, dk_s, dv_s = refs[at + 1 + count :]
    build_keys(sources, slot0, lo_ref, hi_ref, kaug, kt, False)
    rows_each = sources[0].shape[0]
    slots = count * rows_each // BLK
    per = BLK // TK
    for j, kv in enumerate(sources):
        vs[j * rows_each : (j + 1) * rows_each, :] = kv[:, 0:256]
    dk_s[...] = jnp.zeros_like(dk_s)
    dv_s[...] = jnp.zeros_like(dv_s)

    def tile_loop(i, _):
        rows = pl.ds(pl.multiple_of(i * TQ, TQ), TQ)
        stack_queries(q_ref[rows, :], qfirst[i], slo_ref, shi_ref, qs)
        do = do_ref[rows, :]
        lane = lane_ids(TQ)
        zero = jnp.zeros((TQ, 128), BF)
        dos[0:TQ, 0:128] = jnp.where(lane < 64, do[:, 0:128], zero)
        dos[TQ : 2 * TQ, 0:128] = jnp.where(lane < 64, zero, do[:, 0:128])
        dos[2 * TQ :, 0:128] = zero
        dos[0 : 2 * TQ, 128:256] = jnp.zeros((2 * TQ, 128), BF)
        dos[2 * TQ :, 128:192] = do[:, 128:192]
        dos[2 * TQ :, 192:256] = jnp.zeros((TQ, 64), BF)
        both = do.astype(F32).T * ot_ref[i]
        delta = jnp.concatenate(
            [jnp.sum(both[h * HD : (h + 1) * HD], axis=0, keepdims=True) for h in range(3)], axis=1
        )
        lse = lse_ref[pl.ds(i, 1), :]
        if resume:
            acc[...] = acc_in[i]
        else:
            acc[...] = jnp.zeros_like(acc)

        def slot_loop(s, _):
            def key_loop(t, _):
                tile = s * per + t
                keys = pl.ds(pl.multiple_of(tile * TK, TK), TK)
                st = mm(kaug[keys, :], qs[...], NT)
                p = jnp.exp(st - lse)
                dp = mm(vs[keys, :], dos[...], NT)
                ds = (p * (dp - delta)).astype(BF)
                dv_s[keys, :] += mm(p.astype(BF), dos[...])
                dk_s[keys, :] += mm(ds, qs[...])
                for h in range(3):
                    cols = slice(h * TQ, (h + 1) * TQ)
                    acc[(h + 1) * HD : (h + 2) * HD, :] += mm(kt[tile, h * HD : (h + 1) * HD, :], ds[:, cols])
                return 0

            return lax.fori_loop(tlo[i, slot0 + s], thi[i, slot0 + s], key_loop, 0)

        lax.fori_loop(0, slots, slot_loop, 0)
        if last:
            dq_ref[rows, :] = (acc[...] * HD ** (-0.5)).T.astype(BF)
        else:
            dq_ref[i] = acc[...]
        return 0

    lax.fori_loop(0, q_ref.shape[0] // TQ, tile_loop, 0)
    for j, out in enumerate(d_refs):

        def finish(k, _, j=j, out=out):
            to = pl.ds(pl.multiple_of(k * TK, TK), TK)
            frm = pl.ds(pl.multiple_of(j * rows_each + k * TK, TK), TK)
            out[to, 0:128] = dv_s[frm, 0:128].astype(BF)
            out[to, 128:256] = jnp.where(lane_ids(TK) < 64, dv_s[frm, 128:256], dk_s[frm, 0:128]).astype(BF)
            out[to, 256:384] = dk_s[frm, 128:256].astype(BF)
            return 0

        lax.fori_loop(0, rows_each // TK, finish, 0)


def attend_back(tables, q, do, ot, lse, source, slot0, part, parts, state=None, last=False, name="attend_back", size=9_000_000_000):
    tlo, thi, qfirst, lo, hi, slo, shi = tables
    tiles = q.shape[0] // TQ
    keys = source.shape[0] // parts
    tail = (lo, hi, slo, shi) + ((state,) if state is not None else ())
    dq = jax.ShapeDtypeStruct(q.shape, BF) if last else jax.ShapeDtypeStruct((tiles, 256, TQ), F32)
    outs = (dq, jax.ShapeDtypeStruct((keys, source.shape[1]), BF))
    return pl.pallas_call(
        functools.partial(
            attend_back_kernel, slot0=slot0 + part * (keys // BLK), count=1, resume=state is not None, last=last
        ),
        out_shape=outs,
        grid_spec=pltpu.PrefetchScalarGridSpec(
            num_scalar_prefetch=3,
            grid=(1,),
            in_specs=[whole(x.shape) for x in (q, do, ot, lse)]
            + [pl.BlockSpec((keys, source.shape[1]), lambda *_: (part, 0), pipeline_mode=pl.Buffered(1))]
            + [whole(x.shape) for x in tail],
            out_specs=tuple(whole(x.shape) for x in outs),
            scratch_shapes=[
                pltpu.VMEM((keys, 256), BF),
                pltpu.VMEM((keys // TK, 3 * HD, TK), BF),
                pltpu.VMEM((keys, 256), BF),
                pltpu.VMEM((3 * TQ, 256), BF),
                pltpu.VMEM((3 * TQ, 256), BF),
                pltpu.VMEM((256, TQ), F32),
                pltpu.VMEM((keys, 256), F32),
                pltpu.VMEM((keys, 256), F32),
            ],
        ),
        compiler_params=pltpu.CompilerParams(vmem_limit_bytes=GRANT),
        cost_estimate=cost(size, size // 1000, size // 3000),
        name=name,
    )(tlo, thi, qfirst, q, do, ot, lse, source, *tail)


def project_kernel(
    who, x0, x1, x2, x3_top, x3_bottom, w_mine, w_other, bias_ref, chosen, q_ref, kv_ref, up_ref, down_ref, w_ref, xt_ref
):
    tall = w_mine.shape[0]
    rows = x0.shape[0]
    w_ref[pl.ds(pl.multiple_of(who[0] * tall, tall), tall), :] = w_mine[...]
    w_ref[pl.ds(pl.multiple_of((1 - who[0]) * tall, tall), tall), :] = w_other[...]
    for d, x in enumerate((x0, x1, x2, (x3_top, x3_bottom))):
        if d < 3:
            value = mm(x[...], w_ref[...]) + bias_ref[...]
        else:
            value = jnp.concatenate([mm(x[0][...], w_ref[...]), mm(x[1][...], w_ref[...])], axis=0) + bias_ref[...]
        at = slice(d * rows, (d + 1) * rows)
        if d < 3:
            xt_ref[:, at] = x[...].T
        else:
            xt_ref[:, d * rows : d * rows + rows // 2] = x[0][...].T
            xt_ref[:, d * rows + rows // 2 : (d + 1) * rows] = x[1][...].T
        q_ref[at, :] = (value[:, :256].astype(BF).astype(F32) * HD ** (-0.5)).astype(BF)
        kv = mm(chosen[d], value[:, 256:].astype(BF)).astype(BF)
        kv_ref[at, :] = kv
        inner = slice((d % 2) * rows, (d % 2 + 1) * rows)

        @pl.when(who[2] == d // 2)
        def _(inner=inner, kv=kv):
            down_ref[inner, :] = kv

        @pl.when(who[2] != d // 2)
        def _(inner=inner, kv=kv):
            up_ref[inner, :] = kv


def project(who, xs, w_mine, w_other, bias, chosen):
    sd = jax.ShapeDtypeStruct
    rows, width = xs[0].shape
    cols = w_mine.shape[1]
    ins = (*xs, w_mine, w_other, bias, chosen)
    outs = (
        sd((4 * rows, 256), BF), sd((4 * rows, cols - 256), BF), sd((2 * rows, cols - 256), BF),
        sd((2 * rows, cols - 256), BF), sd((width, cols), BF), sd((width, 4 * rows), BF),
    )
    return pl.pallas_call(
        project_kernel,
        out_shape=outs,
        grid_spec=pltpu.PrefetchScalarGridSpec(
            num_scalar_prefetch=1,
            grid=(1,),
            in_specs=[whole(a.shape) for a in ins],
            out_specs=tuple(whole(a.shape) for a in outs),
        ),
        compiler_params=pltpu.CompilerParams(vmem_limit_bytes=GRANT),
        cost_estimate=cost(3_000_000_000, 12_000_000),
        name="project",
    )(who, *ins)


def row_mean(v):
    return jnp.sum(v, axis=-1, keepdims=True) * (1.0 / v.shape[-1])

def dense_kernel(
    who, o_ref, wo_a, wo_b, win_a, win_b, wback_a, wback_b, x_ref, teacher_ref, cot_ref, keep_ref, vec_ref,
    out_ref, dres_ref, dparts_ref, act_ref, dbr_ref, dpre_ref, hid_ref, dproj_ref, sums_ref,
    wo, win, wback, xh, inv, hidden, gp, acc, sems, *, FB
):
    rows, width = x_ref.shape
    groups = o_ref.shape[0] // rows
    part = width // groups
    units = win.shape[1]
    wo_loads, win_loads, wback_loads = [], [], []
    for i in range(2):
        side = who[0] if i == 0 else 1 - who[0]
        for e in range(groups // 2):
            to = pl.multiple_of(((side * (groups // 2) + e) ^ who[1]) * part, part)
            wo_loads.append(
                pltpu.make_async_copy((wo_a, wo_b)[i].at[pl.ds(e * part, part)], wo.at[pl.ds(to, part)], sems.at[2 * i + e])
            )
        for j, (pieces, target, held) in enumerate((((win_a, win_b), win, win_loads), ((wback_a, wback_b), wback, wback_loads))):
            tall = target.shape[0] // 2
            to = pl.multiple_of(side * tall, tall)
            held.append(pltpu.make_async_copy(pieces[i], target.at[pl.ds(to, tall)], sems.at[4 + 2 * i + j]))
    for load in wo_loads + win_loads + wback_loads:
        load.start()
    b_out, b_in, b_back = vec_ref[0:1, 0:width], vec_ref[1:2, :], vec_ref[2:3, 0:width]
    gain1, shift1, gain2, shift2 = (vec_ref[i : i + 1, 0:width] for i in range(3, 7))
    for load in wo_loads:
        load.wait()
    total = x_ref[...].astype(F32) + b_out
    for i in range(groups):
        total += mm(o_ref[i * rows : (i + 1) * rows, :], wo[i * part : (i + 1) * part, :])
    center = total - row_mean(total)
    scale = lax.rsqrt(row_mean(center * center) + 1e-12)
    inv[...] = scale
    unit = center * scale
    xh[...] = unit
    hid = unit * gain1 + shift1
    hidden[...] = hid
    hid_ref[...] = hid.astype(BF)
    acc[...] = jnp.zeros_like(acc)
    for load in win_loads + wback_loads:
        load.wait()

    def up(n, _):
        cols = pl.ds(pl.multiple_of(n * FB, FB), FB)
        pre = mm(hid_ref[...], win[:, cols]) + vec_ref[1:2, cols]
        cdf = 0.5 + 0.5 * lax.erf(pre * 0.7071067811865476)
        act = (pre * cdf).astype(BF)
        act_ref[:, cols] = act
        gp[:, cols] = cdf + pre * (jnp.exp(pre * pre * -0.5) * 0.3989422804014327)
        acc[...] += mm(act, wback[cols, :])
        return 0

    lax.fori_loop(0, units // FB, up, 0, unroll=True)
    total = hidden[...] + acc[...] + b_back
    center = total - row_mean(total)
    scale = lax.rsqrt(row_mean(center * center) + 1e-12)
    unit = center * scale
    result = unit * gain2 + shift2
    out_ref[...] = result.astype(BF)
    grad = cot_ref[...].astype(F32) + keep_ref[...] * (result - teacher_ref[...].astype(F32))
    def put(row, value):
        sums_ref[row : row + 1, 0 : value.shape[1]] = value
    put(5, jnp.sum(grad * unit, axis=0, keepdims=True))
    put(6, jnp.sum(grad, axis=0, keepdims=True))
    grad = grad * gain2
    back = scale * (grad - row_mean(grad) - unit * row_mean(grad * unit))
    acc[...] = back
    low = back.astype(BF)
    dbr_ref[...] = low
    put(2, jnp.sum(low.astype(F32), axis=0, keepdims=True))

    def down(n, _):
        cols = pl.ds(pl.multiple_of(n * FB, FB), FB)
        dpre = (mm(dbr_ref[...], wback[cols, :], NT) * gp[:, cols]).astype(BF)
        dpre_ref[:, cols] = dpre
        sums_ref[1:2, cols] = jnp.sum(dpre.astype(F32), axis=0, keepdims=True)
        acc[...] += mm(dpre, win[:, cols], NT)
        return 0

    lax.fori_loop(0, units // FB, down, 0, unroll=True)
    grad = acc[...]
    unit = xh[...]
    put(3, jnp.sum(grad * unit, axis=0, keepdims=True))
    put(4, jnp.sum(grad, axis=0, keepdims=True))
    grad = grad * gain1
    back = inv[...] * (grad - row_mean(grad) - unit * row_mean(grad * unit))
    dres_ref[...] = back
    low = back.astype(BF)
    dproj_ref[...] = low
    put(0, jnp.sum(low.astype(F32), axis=0, keepdims=True))
    for i in range(groups):
        dparts_ref[i * rows : (i + 1) * rows, :] = mm(low, wo[i * part : (i + 1) * part, :], NT).astype(BF)


def dense(who, o, weights, x, teacher, cot, keep, vec):
    rows, width = x.shape
    units = vec.shape[1]
    sd = jax.ShapeDtypeStruct
    outs = (
        sd((rows, width), BF), sd((rows, width), F32), sd(o.shape, BF), sd((rows, units), BF), sd((rows, width), BF),
        sd((rows, units), BF), sd((rows, width), BF), sd((rows, width), BF), sd((8, units), F32),
    )
    ins = (o, *weights, x, teacher, cot, keep, vec)
    stay = pl.BlockSpec(memory_space=pl.ANY)
    return pl.pallas_call(
        functools.partial(dense_kernel, FB=FFB),
        out_shape=outs,
        grid_spec=pltpu.PrefetchScalarGridSpec(
            num_scalar_prefetch=1,
            grid=(1,),
            in_specs=[whole(o.shape)] + [stay] * 6 + [whole(a.shape) for a in ins[7:]],
            out_specs=tuple(whole(a.shape) for a in outs),
            scratch_shapes=[
                pltpu.VMEM((width, width), BF), pltpu.VMEM((width, units), BF), pltpu.VMEM((units, width), BF),
                pltpu.VMEM((rows, width), F32), pltpu.VMEM((rows, 1), F32), pltpu.VMEM((rows, width), F32),
                pltpu.VMEM((rows, units), F32), pltpu.VMEM((rows, width), F32), pltpu.SemaphoreType.DMA((8,)),
            ],
        ),
        compiler_params=pltpu.CompilerParams(vmem_limit_bytes=GRANT),
        cost_estimate=cost(12_000_000_000, 30_000_000, 4_000_000),
        name="dense",
    )(who, *ins)


def finish_kernel(who, dq_ref, own_a, own_b, pair_a, pair_b, left_ref, right_ref, turn_ref, xt_ref, all_ref, mine_ref, other_ref, dw, sums):
    groups, rows = turn_ref.shape[:2]
    sums[...] = jnp.zeros_like(sums)
    for d in range(groups):
        at = pl.ds(d * rows, rows)
        inner = pl.ds((d % (groups // 2)) * rows, rows)
        first = (d < groups // 2) == (who[2] == 0)
        own_ref, pair_ref = ((own_a, pair_a), (own_b, pair_b))[d // (groups // 2)]
        back = own_ref[inner, :].astype(F32) + pair_ref[inner, :].astype(F32)
        back += jnp.where(first, left_ref[inner, :], right_ref[inner, :]).astype(F32)
        tok = mm(turn_ref[d], back.astype(BF)).astype(BF)
        dq = dq_ref[at, :]
        all_ref[at, 0:256] = dq
        all_ref[at, 256:640] = tok
        sums[0:1, 0:256] += jnp.sum(dq.astype(F32), axis=0, keepdims=True)
        sums[0:1, 256:640] += jnp.sum(tok.astype(F32), axis=0, keepdims=True)
    dw[...] = mm(xt_ref[...], all_ref[...]).astype(BF)
    tall = dw.shape[0] // 2
    low = sums[...].astype(BF)
    for out, side in ((mine_ref, who[0]), (other_ref, 1 - who[0])):
        out[0:tall, :] = dw[pl.ds(pl.multiple_of(side * tall, tall), tall), :]
        for k in range(9):
            out[k : k + 1, 0:64] = low[0:1, 64 * (k + 1) : 64 * (k + 2)]


def finish(who, dq, own_a, own_b, pair_a, pair_b, left, right, turn, xt):
    sd = jax.ShapeDtypeStruct
    cols = dq.shape[1] + own_a.shape[1]
    tall = xt.shape[0] // 2
    ins = (dq, own_a, own_b, pair_a, pair_b, left, right, turn, xt)
    outs = (sd((dq.shape[0], cols), BF), sd((tall, cols), BF), sd((tall, cols), BF))
    return pl.pallas_call(
        finish_kernel,
        out_shape=outs,
        grid_spec=pltpu.PrefetchScalarGridSpec(
            num_scalar_prefetch=1,
            grid=(1,),
            in_specs=[whole(a.shape) for a in ins],
            out_specs=tuple(whole(a.shape) for a in outs),
            scratch_shapes=[pltpu.VMEM((xt.shape[0], cols), BF), pltpu.VMEM((16, cols), F32)],
        ),
        compiler_params=pltpu.CompilerParams(vmem_limit_bytes=GRANT),
        cost_estimate=cost(3_000_000_000, 14_000_000),
        name="finish",
    )(who, *ins)


def spread_kernel(all_ref, w_ref, own_ref, gx_ref, gy_ref, left_ref, right_ref):
    rows, width = own_ref.shape
    cut = width // 2
    parts = [mm(all_ref[d * rows : (d + 1) * rows, :], w_ref[...], NT).astype(BF) for d in range(4)]
    own_ref[...] = parts[0]
    gx_ref[0:rows, :] = parts[1][:, :cut]
    right_ref[...] = parts[1][:, cut:]
    left_ref[...] = parts[2][:, :cut]
    gy_ref[0:rows, :] = parts[2][:, cut:]
    gx_ref[rows:, :] = parts[3][:, :cut]
    gy_ref[rows:, :] = parts[3][:, cut:]


def spread_x(d_all, w_heads):
    rows, width = d_all.shape[0] // 4, w_heads.shape[0]
    shapes = ((rows, width), (2 * rows, width // 2), (2 * rows, width // 2), (rows, width // 2), (rows, width // 2))
    return pl.pallas_call(
        spread_kernel,
        out_shape=tuple(jax.ShapeDtypeStruct(s, BF) for s in shapes),
        grid=(1,),
        in_specs=[whole(d_all.shape), whole(w_heads.shape)],
        out_specs=tuple(whole(s) for s in shapes),
        compiler_params=pltpu.CompilerParams(vmem_limit_bytes=GRANT),
        cost_estimate=cost(2_000_000_000, 7_000_000),
        name="spread_x",
    )(d_all, w_heads)


def place_blocks(who, refs, put):
    s1, s2 = lax.rem(who[1], 2), who[1] // 2
    tall = refs[0].shape[0] // 2
    for at, ref in enumerate(refs):
        color, i = at // 2, at % 2
        for j in range(2):
            spot = (s1 ^ i) * 2 + (s2 ^ j) if color == 0 else 4 + (s2 ^ i) * 2 + (s1 ^ j)
            put(pl.ds(pl.multiple_of(spot * tall, 8), tall), ref[j * tall : (j + 1) * tall, :].astype(F32))


def back_out_kernel(who, a, b, c, d, out_ref):
    width = out_ref.shape[1]

    def put(at, value):
        for k in range(4):
            to = pl.multiple_of(4 * at.start + k * at.size, 8)
            out_ref[pl.ds(to, at.size), :] = value[:, k * width : (k + 1) * width]

    place_blocks(who, (a, b, c, d), put)


def in_out_kernel(who, a, b, c, d, in_ref, out_ref, vec_ref, held):
    def put(at, value):
        held[at, :] = value

    place_blocks(who, (a, b, c, d), put)
    tall, width = out_ref.shape
    in_ref[...] = held[0:tall, :]
    for k in range(3):
        out_ref[k * 128 : (k + 1) * 128, :] = held[tall:, k * width : (k + 1) * width]
    vec_ref[...] = held[tall : tall + 8, 3 * width :]


def out_call(kernel, who, pieces, shapes, scratch, name):
    return pl.pallas_call(
        kernel,
        out_shape=tuple(jax.ShapeDtypeStruct(s, F32) for s in shapes),
        grid_spec=pltpu.PrefetchScalarGridSpec(
            num_scalar_prefetch=1,
            grid=(1,),
            in_specs=[whole(a.shape) for a in pieces],
            out_specs=tuple(whole(s) for s in shapes),
            scratch_shapes=scratch,
        ),
        compiler_params=pltpu.CompilerParams(vmem_limit_bytes=GRANT),
        cost_estimate=cost(1_000_000, 9_000_000),
        name=name,
    )(who, *pieces)


def heads_kernel(who, h0, h1, h2, h3, q_ref, k_ref, v_ref, bias_ref, held):
    tall = q_ref.shape[0]
    for d, ref in enumerate((h0, h1, h2, h3)):
        held[who[1] ^ d] = ref[...]
    for a in range(4):
        cols = slice(a * 192, (a + 1) * 192)
        q_ref[:, cols] = held[a, 0:tall, 64:256].astype(F32)
        v_ref[:, cols] = held[a, 0:tall, 256:448].astype(F32)
        k_ref[:, cols] = held[a, 0:tall, 448:640].astype(F32)
        line = held[a, 0:16, 0:64].astype(F32)
        for k in range(3):
            spot = slice(a * 192 + k * 64, a * 192 + (k + 1) * 64)
            bias_ref[0:1, spot] = line[k : k + 1]
            bias_ref[8:9, spot] = line[k + 3 : k + 4]


def heads_out(who, pieces):
    sd = jax.ShapeDtypeStruct
    outs = (sd((384, 768), F32),) * 3 + (sd((16, 768), F32),)
    return pl.pallas_call(
        heads_kernel,
        out_shape=outs,
        grid_spec=pltpu.PrefetchScalarGridSpec(
            num_scalar_prefetch=1,
            grid=(1,),
            in_specs=[whole(a.shape) for a in pieces],
            out_specs=tuple(whole(a.shape) for a in outs),
            scratch_shapes=[pltpu.VMEM((4, *pieces[0].shape), BF)],
        ),
        compiler_params=pltpu.CompilerParams(vmem_limit_bytes=GRANT),
        cost_estimate=cost(1_000_000, 6_000_000),
        name="heads_out",
    )(who, *pieces)


def swap(block, axis="fsdp"):
    return lax.ppermute(block, axis, [(0, 1), (1, 0)])


def shifted(block, axis, distance):
    devices = range(lax.axis_size(axis))
    route = [(i - distance, i) for i in devices if i - distance in devices]
    return lax.ppermute(block, axis, route)


def flip(block, bit, axis="uly"):
    return lax.ppermute(block, axis, [(i, i ^ bit) for i in range(lax.axis_size(axis))])


def exchange(rows, axis):
    return lax.all_to_all(rows, axis, split_axis=0, concat_axis=0, tiled=True)


def spread_rows(rows, axis):
    count = lax.axis_size(axis)
    return exchange(jnp.broadcast_to(rows[None], (count, *rows.shape)).reshape(-1, rows.shape[1]), axis)


def sum_parts(rows, count):
    got = rows.reshape(count, -1, rows.shape[1])
    return sum(got[i].astype(F32) for i in range(count)).astype(BF)


def sum_scatter(rows, axis):
    return sum_parts(exchange(rows, axis), lax.axis_size(axis))


def add(left, right):
    return (left.astype(F32) + right.astype(F32)).astype(BF)


def sides(rows, bit):
    side = jnp.where((lax.axis_index("uly") & bit) > 0, 1, 0)
    split = rows.reshape(2, -1, rows.shape[1])
    return (
        lax.dynamic_index_in_dim(split, side, 0, keepdims=False),
        lax.dynamic_index_in_dim(split, 1 - side, 0, keepdims=False),
    )


def halve(rows, bit):
    mine, other = sides(rows, bit)
    return add(mine, flip(other, bit))


def halves(rows):
    middle = rows.shape[0] // 2
    return rows[:middle], rows[middle:]


def wide(rows):
    tall = rows.shape[0] // 4
    return jnp.concatenate([rows[i * tall : (i + 1) * tall] for i in range(4)], axis=1)


def slim(rows):
    cols = rows.shape[1] // 4
    return jnp.concatenate([rows[:, i * cols : (i + 1) * cols] for i in range(4)], axis=0)


def line_step(held, bit):
    return flip(held, bit, "ctx")


def line_join(held, got, bit):
    low = (lax.axis_index("ctx") & bit) == 0
    return jnp.stack([jnp.where(low, held, got), jnp.where(low, got, held)], axis=1).reshape(-1, *held.shape[1:])


def line_rest(held, bit):
    while bit > 0:
        held = line_join(held, line_step(held, bit), bit)
        bit //= 2
    return held.reshape(-1, held.shape[2])


def tie(*values):
    return lax.optimization_barrier(values)


def on_device(
    tokens, teacher, cotangent, valid, teacher_ok, doc_starts, w_query, w_key, w_value, w_out, w_in, w_back,
    bias_query, bias_value, bias_out, bias_in, bias_back, norm1_gain, norm1_bias, norm2_gain, norm2_bias,
):
    groups = lax.axis_size("uly")
    spans = lax.axis_size("ctx")
    rows, width = tokens.shape
    block = rows * groups * 2
    stream = block * spans
    ctx_index = lax.axis_index("ctx")
    uly = lax.axis_index("uly")
    half = lax.axis_index("fsdp")
    head_cols = width // groups
    shard = w_query.shape[0]
    middle = groups * rows // 2
    upper = uly // 2

    valid_one = valid[None, :]
    valid_own = jnp.concatenate([valid_one, flip(valid_one, 1), flip(valid_one, 2), flip(valid_one, 3)], axis=0)
    x_own, valid_own = tie(tokens, valid_own)
    x_x, x_y = flip(x_own, 1), flip(x_own, 2)
    valid_pair = swap(valid_own)
    valid_both = jnp.stack([valid_own, valid_pair]).reshape(2, 2, 2, rows)
    valid_high = lax.dynamic_index_in_dim(valid_both, 1 - upper, 1, keepdims=False)
    valid_low = lax.dynamic_index_in_dim(valid_both, upper, 1, keepdims=False)
    halo = (shifted(valid_high, "ctx", 1), shifted(valid_low, "ctx", -1))
    block_valid = jnp.concatenate([valid_own, valid_pair, halo[0][0], halo[1][0], halo[0][1], halo[1][1]], axis=0)
    count = jnp.full((8, 128), jnp.sum(valid_both), jnp.int32)
    bit = 1
    while bit < spans:
        count = count + flip(count, bit, "ctx")
        bit *= 2
    count = count[0, 0].astype(F32)

    start_col = uly * head_cols
    cut = [lax.dynamic_slice_in_dim(w, start_col, head_cols, 1) for w in (w_query, w_value, w_key)]
    w_mine = jnp.concatenate([jnp.zeros((shard, 256 - head_cols), BF), *cut], axis=1)
    w_other = swap(w_mine)
    who = jnp.stack([half, uly, upper])
    small = (bias_query, bias_value, bias_out, bias_in, bias_back, norm1_gain, norm1_bias, norm2_gain, norm2_bias)
    packed = jnp.concatenate([p.reshape(-1, shard) for p in small], axis=0)
    packed_pair = swap(packed)
    packed = jnp.stack([jnp.where(half == 0, packed, packed_pair), jnp.where(half == 0, packed_pair, packed)])
    vectors = []
    at = 0
    for p in small:
        n = p.shape[0] // shard
        vectors.append(packed[:, at : at + n].reshape(-1).astype(F32))
        at += n
    bq_all, bv_all = vectors[:2]
    vec = jnp.stack([jnp.pad(v, (0, w_in.shape[1] - v.shape[0])) for v in vectors[2:]] + [jnp.zeros((w_in.shape[1],), F32)])
    bias_heads = jnp.concatenate(
        [
            jnp.zeros((256 - head_cols,), F32),
            lax.dynamic_slice_in_dim(bq_all, start_col, head_cols, 0),
            lax.dynamic_slice_in_dim(bv_all, start_col, head_cols, 0),
            jnp.zeros((head_cols,), F32),
        ]
    )

    place = jnp.arange(groups, dtype=jnp.int32)
    two = jnp.arange(2, dtype=jnp.int32)
    in_plane = place ^ uly
    halo_group = jnp.concatenate([uly ^ (2 * (1 - upper) + two), uly ^ (2 * upper + two)])
    halo_plane = ctx_index + jnp.where(place < 2, -1, 1)
    plane_of = jnp.concatenate([jnp.full((2 * groups,), 1, jnp.int32) * ctx_index, halo_plane, halo_plane])
    group_of = jnp.concatenate([in_plane, in_plane, halo_group, halo_group])
    mine = jnp.full((groups,), 1, jnp.int32) * half
    core_of = jnp.concatenate([mine, 1 - mine, mine, 1 - mine])
    block_id = plane_of * (2 * groups) + group_of * 2 + core_of
    spot = block_id[:, None] * rows + jnp.arange(rows, dtype=jnp.int32)[None, :]
    edges = jnp.concatenate([doc_starts, jnp.full((DOCS + 1,), stream, jnp.int32)])
    window_first = jnp.maximum(ctx_index * block - block // 2, 0)
    first_doc = jnp.sum((doc_starts <= window_first).astype(jnp.int32)) - 1
    near = lax.dynamic_slice_in_dim(edges, first_doc, DOCS + 1, 0)
    tiles = groups * rows // TQ
    per = rows // TQ
    tile_ids = jnp.arange(tiles, dtype=jnp.int32)
    qfirst = ctx_index * block + (((tile_ids // per) ^ uly) * 2 + half) * rows + lax.rem(tile_ids, per) * TQ
    q_lo = jnp.max(jnp.where(near[None, :] <= qfirst[:, None], near[None, :], 0), axis=1)
    q_hi = jnp.min(jnp.where(near[None, :] <= qfirst[:, None] + TQ - 1, stream, near[None, :]), axis=1)
    limits = jnp.concatenate([near, q_lo, q_hi])
    counted = jnp.sum(block_valid[:, None, :] * (spot[:, None, :] < limits[None, :, None]), axis=-1)
    bounds = counted[:, : DOCS + 1]
    cnt_lo = counted[:, DOCS + 1 : DOCS + 1 + tiles].T
    cnt_hi = counted[:, DOCS + 1 + tiles :].T
    pad64 = jnp.zeros((bounds.shape[0], 128 - DOCS), jnp.int32)
    lo_tab = jnp.concatenate([bounds[:, :DOCS], pad64], axis=1)
    hi_tab = jnp.concatenate([bounds[:, 1:], pad64], axis=1)
    slo_tab = jnp.concatenate([near[:DOCS], pad64[0]])[None, :]
    shi_tab = jnp.concatenate([near[1:], pad64[0]])[None, :]
    some = cnt_hi > cnt_lo
    tlo = jnp.where(some, cnt_lo // TK, 0)
    thi = jnp.where(some, (cnt_hi + TK - 1) // TK, 0)
    tables = (tlo, thi, qfirst, lo_tab, hi_tab, slo_tab, shi_tab)
    before = mm(valid_own.astype(BF), (jnp.arange(rows)[:, None] < jnp.arange(rows)[None, :]).astype(BF)).astype(jnp.int32)
    goes_to = jnp.where(valid_own > 0, before, rows)
    chosen = (goes_to[:, None, :] == jnp.arange(rows, dtype=jnp.int32)[None, :, None]).astype(BF)
    loss_scale = jnp.float32(stream) / count
    keep = (loss_scale * (valid * teacher_ok).astype(F32))[:, None]
    turned = (goes_to[:, :, None] == jnp.arange(rows, dtype=jnp.int32)[None, None, :]).astype(BF)

    x_x, x_y, w_other, chosen, bias_heads, *tables = tie(x_x, x_y, w_other, chosen, bias_heads, *tables)
    x_top, x_bottom = flip(x_y[: rows // 2], 1), flip(x_x[rows // 2 :], 2)

    q_low, kv_own, kv_up, kv_down, w_heads, x_turned = project(
        who, (tokens, x_x, x_y, x_top, x_bottom), w_mine, w_other, bias_heads[None, :], chosen
    )
    kv_from_left, kv_from_right = shifted(kv_up, "ctx", 1), shifted(kv_down, "ctx", -1)
    w_out, w_in, w_back, kv_own = tie(w_out, w_in, w_back, kv_own)
    weights = (w_out, swap(w_out), w_in, swap(w_in), w_back, swap(w_back))
    kv_pair = swap(kv_own)
    state = attend(tables, q_low, (kv_own,), 0)
    kv_halo = jnp.concatenate([kv_from_left, kv_from_right], axis=0)
    kv_halo, kv_pair, *state = tie(kv_halo, kv_pair, *state)
    kv_halo_pair = swap(kv_halo)
    state = attend(tables, q_low, (kv_pair,), groups, state)
    o_heads, o_turned, lse = attend(tables, q_low, (kv_halo, kv_halo_pair), 2 * groups, state, last=True)
    o_rel = o_heads.reshape(groups, rows, head_cols)
    o_all = jnp.concatenate([o_rel[0]] + [flip(o_rel[d], d) for d in range(1, groups)], axis=0)

    out, d_resid1, d_parts, act, d_branch, d_pre, hidden_low, d_proj, sums = dense(
        who, o_all, weights, tokens, teacher, cotangent, keep, vec
    )
    d_rel = d_parts.reshape(groups, rows, head_cols)
    tall = w_back.shape[0]
    vector_rows = jnp.concatenate(
        [sums[i, :width].reshape(2, -1) for i in (0, 2, 3, 4, 5, 6)] + [sums[1].reshape(2, -1)], axis=1
    ).reshape(2, -1, width)
    vector_rows = jnp.pad(vector_rows, ((0, 0), (0, 128 - vector_rows.shape[1]), (0, 0))).astype(BF)
    o_rows = o_all.reshape(groups, rows, head_cols)

    def back_part(side):
        return mm(lax.dynamic_slice_in_dim(act, side * tall, tall, 1), d_branch, TN).astype(BF)

    def in_part(side):
        return mm(lax.dynamic_slice_in_dim(hidden_low, side * shard, shard, 1), d_pre, TN).astype(BF)

    def out_part(side):
        both = [
            mm(lax.dynamic_index_in_dim(o_rows, (2 * side + e) ^ uly, 0, keepdims=False), d_proj, TN).astype(BF)
            for e in range(2)
        ]
        stack = jnp.concatenate([*both, lax.dynamic_index_in_dim(vector_rows, side, 0, keepdims=False)], axis=0)
        return jnp.concatenate([stack[i * 128 : (i + 1) * 128] for i in range(4)], axis=1)

    d_rest = [flip(d_rel[d], d) for d in range(1, groups)]
    back_got = swap(back_part(1 - half))
    in_other, out_other = in_part(1 - half), out_part(1 - half)
    back_sum = add(back_part(half), back_got)
    b1, b2 = halves(back_sum)
    (b1m, b1o), (b2m, b2o) = sides(b1, 1), sides(b2, 2)
    in_other, out_other, b1o, b2o, *d_rest = tie(in_other, out_other, b1o, b2o, *d_rest)
    b1g, b2g = flip(b1o, 1), flip(b2o, 2)
    in_got, out_got = swap(in_other), swap(out_other)
    in_mine, out_mine = in_part(half), out_part(half)
    in_sum = jnp.concatenate([add(in_mine, in_got), add(out_mine, out_got)], axis=0)
    i1, i2 = halves(in_sum)
    (i1m, i1o), (i2m, i2o) = sides(i1, 1), sides(i2, 2)
    d_heads = jnp.concatenate([d_rel[0], *d_rest], axis=0)
    d_heads, b1g, b2g, i1m, i1o, i2m, i2o = tie(d_heads, b1g, b2g, i1m, i1o, i2m, i2o)

    b1, b2 = add(b1m, b1g), add(b2m, b2g)
    (b1m, b1o), (b2m, b2o) = sides(b1, 2), sides(b2, 1)
    mix1 = jnp.concatenate([i1o, wide(b2o)], axis=0)
    mix2 = jnp.concatenate([i2o, wide(b1o)], axis=0)
    d_heads, mix1, mix2, b1m, b2m = tie(d_heads, mix1, mix2, b1m, b2m)
    args = (tables, q_low, d_heads, o_turned, lse)
    m1g, m2g = flip(mix1, 1), flip(mix2, 2)
    dq_state, dkv_halo_pair = attend_back(*args, kv_halo_pair, 3 * groups, 0, 1, name="back_halo_pair")
    dq_state, dkv_halo_pair = tie(dq_state, dkv_halo_pair)
    got_lo, got_hi = swap(dkv_halo_pair[:middle]), swap(dkv_halo_pair[middle:])
    dq_state, dkv_halo = attend_back(*args, kv_halo, 2 * groups, 0, 1, dq_state, name="back_halo", size=1_000_000)
    dq_state, dkv_halo, got_lo, got_hi, m1g, m2g = tie(dq_state, dkv_halo, got_lo, got_hi, m1g, m2g)

    halo_lo, halo_hi = add(dkv_halo[:middle], got_lo), add(dkv_halo[middle:], got_hi)
    tall = i1o.shape[0]
    back_line = jnp.concatenate([add(wide(b1m), m2g[tall:]), add(wide(b2m), m1g[tall:])], axis=0)
    i1, i2 = add(i1m, m1g[:tall]), add(i2m, m2g[:tall])
    (i1m, i1o), (i2m, i2o) = sides(i1, 2), sides(i2, 1)
    dq_state, halo_lo, halo_hi, back_line, i1m, i1o, i2m, i2o = tie(
        dq_state, halo_lo, halo_hi, back_line, i1m, i1o, i2m, i2o
    )
    i1g, i2g = flip(i1o, 2), flip(i2o, 1)
    from_left, from_right = shifted(halo_hi, "ctx", 1), shifted(halo_lo, "ctx", -1)
    back_line = exchange(back_line, "ctx")
    dq_state, dkv_pair_a = attend_back(*args, kv_pair, groups, 0, 2, dq_state, name="back_pair_a")
    dq_state, dkv_pair_a, i1g, i2g, back_line = tie(dq_state, dkv_pair_a, i1g, i2g, back_line)

    bit = spans // 2
    back_line = sum_parts(back_line, spans)[None]
    in_line = jnp.concatenate([add(i1m, i1g), add(i2m, i2g)], axis=0)
    dq_state, dkv_pair_a, back_line, in_line = tie(dq_state, dkv_pair_a, back_line, in_line)
    back_got = line_step(back_line, bit)
    in_line = exchange(in_line, "ctx")
    pair_a = swap(dkv_pair_a)
    dq_state, dkv_pair_b = attend_back(*args, kv_pair, groups, 1, 2, dq_state, name="back_pair_b")
    dq_state, dkv_pair_b, back_got, in_line, pair_a, from_left, from_right = tie(
        dq_state, dkv_pair_b, back_got, in_line, pair_a, from_left, from_right
    )

    back_line = line_join(back_line, back_got, bit)
    in_line = sum_parts(in_line, spans)[None]
    dq_state, dkv_pair_b, back_line, in_line = tie(dq_state, dkv_pair_b, back_line, in_line)
    in_got = line_step(in_line, bit)
    back_got = line_step(back_line, bit // 2)
    pair_b = swap(dkv_pair_b)
    dq_state, dkv_own_a = attend_back(*args, kv_own, 0, 0, 2, dq_state, name="back_own_a")
    dq_state, dkv_own_a, in_got, back_got, pair_b = tie(dq_state, dkv_own_a, in_got, back_got, pair_b)

    b1, b2 = halves(line_rest(line_join(back_line, back_got, bit // 2), bit // 4))
    in_line = line_join(in_line, in_got, bit)
    dq_state, b1, b2, in_line = tie(dq_state, b1, b2, in_line)
    b1g, b2g = flip(b1, 2), flip(b2, 1)
    in_got = line_step(in_line, bit // 2)
    dq, dkv_own_b = attend_back(*args, kv_own, 0, 1, 2, dq_state, last=True, name="back_own_b")
    dq, dkv_own_b, b1g, b2g, in_got = tie(dq, dkv_own_b, b1g, b2g, in_got)
    in_line = line_rest(line_join(in_line, in_got, bit // 2), bit // 4)

    b1, b2 = jnp.concatenate([b1, b1g], axis=0), jnp.concatenate([b2, b2g], axis=0)
    i1, i2 = halves(in_line)
    dq, b1, b2, i1, i2 = tie(dq, b1, b2, i1, i2)
    mix1 = flip(jnp.concatenate([b1, i2], axis=0), 1)
    mix2 = flip(jnp.concatenate([b2, i1], axis=0), 2)
    d_all, heads_mine, heads_other = finish(
        who, dq, dkv_own_a, dkv_own_b, pair_a, pair_b, from_left, from_right, turned, x_turned
    )
    d_all, heads_mine, heads_other = tie(d_all, heads_mine, heads_other)
    heads_got = swap(heads_other)
    dx_own, give_x, give_y, left_next, right_next = spread_x(d_all, w_heads)
    give_x, give_y, heads_got, mix1, mix2 = tie(give_x, give_y, heads_got, mix1, mix2)
    heads_line = exchange(add(heads_mine, heads_got), "ctx")
    give_x, give_y = flip(give_x, 1), flip(give_y, 2)
    tall = b1.shape[0]
    i1 = jnp.concatenate([i1, mix2[tall:]], axis=0)
    i2 = jnp.concatenate([i2, mix1[tall:]], axis=0)
    i1g, i2g = flip(i1, 1), flip(i2, 2)
    (g_back,) = out_call(back_out_kernel, who, (b1, mix1[:tall], b2, mix2[:tall]), (w_back.shape,), [], "back_out")
    heads_line = sum_parts(heads_line, spans)[None]
    left_next = flip(add(left_next, give_x[rows:]), 2)
    right_next = flip(add(right_next, give_y[rows:]), 1)
    heads_sum = line_rest(heads_line, bit)
    heads_all = [heads_sum] + [flip(heads_sum, d) for d in range(1, groups)]
    grad_in = d_resid1 + dx_own.astype(F32)
    grad_in = grad_in + jnp.concatenate([give_x[:rows].astype(F32), give_y[:rows].astype(F32)], axis=1)
    grad_in = grad_in + jnp.concatenate([left_next.astype(F32), right_next.astype(F32)], axis=1)
    g_in, g_out, g_vec = out_call(
        in_out_kernel, who, (i1, i1g, i2, i2g), (w_in.shape, w_out.shape, (8, width)),
        [pltpu.VMEM((shard + 128, w_in.shape[1]), F32)], "in_out",
    )
    g_query, g_key, g_value, g_bias = heads_out(who, heads_all)
    g_bias_q = lax.dynamic_slice_in_dim(g_bias[0], half * shard, shard, 0)
    g_bias_v = lax.dynamic_slice_in_dim(g_bias[8], half * shard, shard, 0)
    flat = g_vec.reshape(-1)
    g_bo, g_bb, g_g1, g_s1, g_g2, g_s2 = [flat[i * shard : (i + 1) * shard] for i in range(6)]
    g_bin = flat[6 * shard : 6 * shard + bias_in.shape[0]]
    return (
        out, grad_in, g_query, g_key, g_value, g_out, g_in, g_back,
        g_bias_q, g_bias_v, g_bo, g_bin, g_bb, g_g1, g_s1, g_g2, g_s2,
    )


def solution(mesh):
    placed = (
        P(("ctx", "uly", "fsdp"), None),
        P(("ctx", "uly", "fsdp"), None),
        P(("ctx", "uly", "fsdp"), None),
        P(("ctx", "uly", "fsdp")),
        P(("ctx", "uly", "fsdp")),
        P(),
        P("fsdp", None),
        P("fsdp", None),
        P("fsdp", None),
        P("fsdp", None),
        P("fsdp", None),
        P("fsdp", None),
        P("fsdp"),
        P("fsdp"),
        P("fsdp"),
        P("fsdp"),
        P("fsdp"),
        P("fsdp"),
        P("fsdp"),
        P("fsdp"),
        P("fsdp"),
    )
    return jax.shard_map(
        on_device,
        mesh=mesh,
        in_specs=placed,
        out_specs=(
            P(("ctx", "uly", "fsdp"), None),
            P(("ctx", "uly", "fsdp"), None),
            P("fsdp", None),
            P("fsdp", None),
            P("fsdp", None),
            P("fsdp", None),
            P("fsdp", None),
            P("fsdp", None),
            P("fsdp"),
            P("fsdp"),
            P("fsdp"),
            P("fsdp"),
            P("fsdp"),
            P("fsdp"),
            P("fsdp"),
            P("fsdp"),
            P("fsdp"),
        ),
        check_vma=False,
    )
```

```python
import functools

import jax
import jax.numpy as jnp
from jax import lax
from jax.experimental import pallas as pl
from jax.experimental.pallas import tpu as pltpu
from jax.sharding import PartitionSpec as P

HEADS = 12
HD = 64
BLK = 512
TQ = 256
TK = 256
DOCS = 64
FFB = 768
MASKED = -1e30
BF = jnp.bfloat16
F32 = jnp.float32
NT = (((1,), (1,)), ((), ()))
NN = (((1,), (0,)), ((), ()))
TN = (((0,), (0,)), ((), ()))


def mm(left, right, dims=NN):
    return lax.dot_general(left, right, dims, preferred_element_type=F32)


def whole(shape):
    return pl.BlockSpec(shape, lambda *_: (0,) * len(shape), pipeline_mode=pl.Buffered(1))


def cost(flops, moved, special=0):
    return pl.CostEstimate(flops=flops, bytes_accessed=moved, transcendentals=special)


def lane_ids(rows):
    return lax.broadcasted_iota(jnp.int32, (rows, 128), 1)


def build_keys(sources, slot0, lo_ref, hi_ref, kaug, transposed, low_half):
    per = BLK // TK
    for at, kv in enumerate(sources):

        def one(j, _, at=at, kv=kv):
            rows = pl.ds(pl.multiple_of(j * TK, TK), TK)
            tile = at * (kv.shape[0] // TK) + j
            slot = slot0 + at * (kv.shape[0] // BLK) + j // per
            out = pl.ds(pl.multiple_of(tile * TK, TK), TK)
            rank = lax.broadcasted_iota(jnp.int32, (TK, 128), 0) + lax.rem(j, per) * TK
            inside = (rank >= lo_ref[pl.ds(slot, 1), :]) & (rank < hi_ref[pl.ds(slot, 1), :])
            bias = jnp.where(inside, 0.0, MASKED).astype(BF)
            kaug[out, 0:128] = jnp.where(lane_ids(TK) < 64, bias, kv[rows, 128:256])
            kaug[out, 128:256] = kv[rows, 256:384]
            if low_half:
                transposed[tile] = kv[rows, 0:256].T[0:192]
            else:
                transposed[tile] = kaug[out, :].T[64:256]
            return 0

        lax.fori_loop(0, kv.shape[0] // TK, one, 0)


def stack_queries(q, first, slo_ref, shi_ref, qs):
    lane = lane_ids(TQ)
    spot = lax.broadcasted_iota(jnp.int32, (TQ, 128), 0) + first
    mine = ((spot >= slo_ref[...]) & (spot < shi_ref[...])).astype(F32).astype(BF)
    zero = jnp.zeros((TQ, 128), BF)
    low, high = q[:, 0:128], q[:, 128:256]
    mark = jnp.where(lane < 64, mine, zero)
    qs[0:TQ, 0:128] = jnp.where(lane < 64, mine, low)
    qs[TQ : 2 * TQ, 0:128] = mark
    qs[2 * TQ :, 0:128] = mark
    qs[0:TQ, 128:256] = zero
    qs[TQ : 2 * TQ, 128:256] = jnp.where(lane < 64, high, zero)
    qs[2 * TQ :, 128:256] = jnp.where(lane < 64, zero, high)


def attend_kernel(*refs, slot0, count, resume, last):
    tlo, thi, qfirst, q_ref = refs[:4]
    sources = refs[4 : 4 + count]
    lo_ref, hi_ref, slo_ref, shi_ref = refs[4 + count : 8 + count]
    at = 8 + count
    if resume:
        acc_in, stat_in = refs[at : at + 2]
        at += 2
    if last:
        o_ref, ot_ref, lse_ref = refs[at : at + 3]
        at += 3
    else:
        acc_out, stat_out = refs[at : at + 2]
        at += 2
    kaug, vt, qs, acc, m_s, l_s = refs[at:]
    build_keys(sources, slot0, lo_ref, hi_ref, kaug, vt, True)
    slots = count * sources[0].shape[0] // BLK
    per = BLK // TK

    def tile_loop(i, _):
        rows = pl.ds(pl.multiple_of(i * TQ, TQ), TQ)
        stack_queries(q_ref[rows, :], qfirst[i], slo_ref, shi_ref, qs)
        if resume:
            m_s[...] = stat_in[i, 0:1, :]
            l_s[...] = stat_in[i, 1:2, :]
            acc[...] = acc_in[i]
        else:
            m_s[...] = jnp.full_like(m_s, 2 * MASKED)
            l_s[...] = jnp.zeros_like(l_s)
            acc[...] = jnp.zeros_like(acc)

        def slot_loop(s, _):
            def key_loop(t, _):
                tile = s * per + t
                keys = pl.ds(pl.multiple_of(tile * TK, TK), TK)
                st = mm(kaug[keys, :], qs[...], NT)
                m_old = m_s[...]
                m_new = jnp.maximum(m_old, jnp.max(st, axis=0, keepdims=True))
                fade = jnp.exp(m_old - m_new)
                p = jnp.exp(st - m_new)
                l_s[...] = l_s[...] * fade + jnp.sum(p, axis=0, keepdims=True)
                m_s[...] = m_new
                low = p.astype(BF)
                for h in range(3):
                    cols = slice(h * TQ, (h + 1) * TQ)
                    part = slice(h * HD, (h + 1) * HD)
                    acc[part, :] = acc[part, :] * fade[:, cols] + mm(vt[tile, part, :], low[:, cols])
                return 0

            return lax.fori_loop(tlo[i, slot0 + s], thi[i, slot0 + s], key_loop, 0)

        lax.fori_loop(0, slots, slot_loop, 0)
        if last:
            total = l_s[...]
            for h in range(3):
                cols = slice(h * TQ, (h + 1) * TQ)
                part = slice(h * HD, (h + 1) * HD)
                acc[part, :] = acc[part, :] / total[:, cols]
            ot_ref[i] = acc[...]
            o_ref[rows, :] = acc[...].T.astype(BF)
            lse_ref[pl.ds(i, 1), :] = m_s[...] + jnp.log(total)
        else:
            acc_out[i] = acc[...]
            stat_out[i, 0:1, :] = m_s[...]
            stat_out[i, 1:2, :] = l_s[...]
        return 0

    lax.fori_loop(0, q_ref.shape[0] // TQ, tile_loop, 0)


def attend(tables, q, sources, slot0, state=None, last=False):
    tlo, thi, qfirst, lo, hi, slo, shi = tables
    tiles = q.shape[0] // TQ
    keys = sum(s.shape[0] for s in sources)
    ins = (q, *sources, lo, hi, slo, shi) + (tuple(state) if state else ())
    if last:
        outs = (
            jax.ShapeDtypeStruct((q.shape[0], 3 * HD), BF),
            jax.ShapeDtypeStruct((tiles, 3 * HD, TQ), F32),
            jax.ShapeDtypeStruct((tiles, 3 * TQ), F32),
        )
    else:
        outs = (
            jax.ShapeDtypeStruct((tiles, 3 * HD, TQ), F32),
            jax.ShapeDtypeStruct((tiles, 2, 3 * TQ), F32),
        )
    return pl.pallas_call(
        functools.partial(attend_kernel, slot0=slot0, count=len(sources), resume=state is not None, last=last),
        out_shape=outs,
        grid_spec=pltpu.PrefetchScalarGridSpec(
            num_scalar_prefetch=3,
            grid=(1,),
            in_specs=[whole(x.shape) for x in ins],
            out_specs=tuple(whole(x.shape) for x in outs),
            scratch_shapes=[
                pltpu.VMEM((keys, 256), BF),
                pltpu.VMEM((keys // TK, 3 * HD, TK), BF),
                pltpu.VMEM((3 * TQ, 256), BF),
                pltpu.VMEM((3 * HD, TQ), F32),
                pltpu.VMEM((1, 3 * TQ), F32),
                pltpu.VMEM((1, 3 * TQ), F32),
            ],
        ),
        compiler_params=pltpu.CompilerParams(vmem_limit_bytes=20 << 20),
        cost_estimate=cost(12_000_000_000, 12_000_000, 10_000_000),
        name="attend",
    )(tlo, thi, qfirst, *ins)


def attend_back_kernel(*refs, slot0, count, resume, last):
    tlo, thi, qfirst, q_ref, do_ref, ot_ref, lse_ref = refs[:7]
    sources = refs[7 : 7 + count]
    lo_ref, hi_ref, slo_ref, shi_ref = refs[7 + count : 11 + count]
    at = 11 + count
    if resume:
        acc_in = refs[at]
        at += 1
    dq_ref = refs[at]
    d_refs = refs[at + 1 : at + 1 + count]
    at += 1 + count
    if not resume:
        delta_ref = refs[at]
        at += 1
    kaug, kt, vs, qs, dos, acc, dk_s, dv_s = refs[at:]
    build_keys(sources, slot0, lo_ref, hi_ref, kaug, kt, False)
    rows_each = sources[0].shape[0]
    slots = count * rows_each // BLK
    per = BLK // TK
    for j, kv in enumerate(sources):
        vs[j * rows_each : (j + 1) * rows_each, :] = kv[:, 0:256]
    dk_s[...] = jnp.zeros_like(dk_s)
    dv_s[...] = jnp.zeros_like(dv_s)

    def tile_loop(i, _):
        rows = pl.ds(pl.multiple_of(i * TQ, TQ), TQ)
        stack_queries(q_ref[rows, :], qfirst[i], slo_ref, shi_ref, qs)
        do = do_ref[rows, :]
        lane = lane_ids(TQ)
        zero = jnp.zeros((TQ, 128), BF)
        dos[0:TQ, 0:128] = jnp.where(lane < 64, do[:, 0:128], zero)
        dos[TQ : 2 * TQ, 0:128] = jnp.where(lane < 64, zero, do[:, 0:128])
        dos[2 * TQ :, 0:128] = zero
        dos[0 : 2 * TQ, 128:256] = jnp.zeros((2 * TQ, 128), BF)
        dos[2 * TQ :, 128:192] = do[:, 128:192]
        dos[2 * TQ :, 192:256] = jnp.zeros((TQ, 64), BF)
        if resume:
            delta = ot_ref[pl.ds(i, 1), :]
        else:
            both = do.astype(F32).T * ot_ref[i]
            delta = jnp.concatenate(
                [jnp.sum(both[h * HD : (h + 1) * HD], axis=0, keepdims=True) for h in range(3)], axis=1
            )
            delta_ref[pl.ds(i, 1), :] = delta
        lse = lse_ref[pl.ds(i, 1), :]
        if resume:
            acc[...] = acc_in[i]
        else:
            acc[...] = jnp.zeros_like(acc)

        def slot_loop(s, _):
            def key_loop(t, _):
                tile = s * per + t
                keys = pl.ds(pl.multiple_of(tile * TK, TK), TK)
                st = mm(kaug[keys, :], qs[...], NT)
                p = jnp.exp(st - lse)
                dp = mm(vs[keys, :], dos[...], NT)
                ds = (p * (dp - delta)).astype(BF)
                dv_s[keys, :] += mm(p.astype(BF), dos[...])
                dk_s[keys, :] += mm(ds, qs[...])
                for h in range(3):
                    cols = slice(h * TQ, (h + 1) * TQ)
                    acc[(h + 1) * HD : (h + 2) * HD, :] += mm(kt[tile, h * HD : (h + 1) * HD, :], ds[:, cols])
                return 0

            return lax.fori_loop(tlo[i, slot0 + s], thi[i, slot0 + s], key_loop, 0)

        lax.fori_loop(0, slots, slot_loop, 0)
        if last:
            dq_ref[rows, :] = (acc[...] * HD ** (-0.5)).T.astype(BF)
        else:
            dq_ref[i] = acc[...]
        return 0

    lax.fori_loop(0, q_ref.shape[0] // TQ, tile_loop, 0)
    for j, out in enumerate(d_refs):

        def finish(k, _, j=j, out=out):
            to = pl.ds(pl.multiple_of(k * TK, TK), TK)
            frm = pl.ds(pl.multiple_of(j * rows_each + k * TK, TK), TK)
            out[to, 0:128] = dv_s[frm, 0:128].astype(BF)
            out[to, 128:256] = jnp.where(lane_ids(TK) < 64, dv_s[frm, 128:256], dk_s[frm, 0:128]).astype(BF)
            out[to, 256:384] = dk_s[frm, 128:256].astype(BF)
            return 0

        lax.fori_loop(0, rows_each // TK, finish, 0)


def attend_back(tables, q, do, ot, lse, source, slot0, part, parts, state=None, last=False, name="attend_back", size=9_000_000_000):
    tlo, thi, qfirst, lo, hi, slo, shi = tables
    tiles = q.shape[0] // TQ
    keys = source.shape[0] // parts
    tail = (lo, hi, slo, shi) + ((state,) if state is not None else ())
    dq = jax.ShapeDtypeStruct(q.shape, BF) if last else jax.ShapeDtypeStruct((tiles, 256, TQ), F32)
    outs = (dq, jax.ShapeDtypeStruct((keys, source.shape[1]), BF))
    if state is None:
        outs += (jax.ShapeDtypeStruct(lse.shape, F32),)
    return pl.pallas_call(
        functools.partial(
            attend_back_kernel, slot0=slot0 + part * (keys // BLK), count=1, resume=state is not None, last=last
        ),
        out_shape=outs,
        grid_spec=pltpu.PrefetchScalarGridSpec(
            num_scalar_prefetch=3,
            grid=(1,),
            in_specs=[whole(x.shape) for x in (q, do, ot, lse)]
            + [pl.BlockSpec((keys, source.shape[1]), lambda *_: (part, 0), pipeline_mode=pl.Buffered(1))]
            + [whole(x.shape) for x in tail],
            out_specs=tuple(whole(x.shape) for x in outs),
            scratch_shapes=[
                pltpu.VMEM((keys, 256), BF),
                pltpu.VMEM((keys // TK, 3 * HD, TK), BF),
                pltpu.VMEM((keys, 256), BF),
                pltpu.VMEM((3 * TQ, 256), BF),
                pltpu.VMEM((3 * TQ, 256), BF),
                pltpu.VMEM((256, TQ), F32),
                pltpu.VMEM((keys, 256), F32),
                pltpu.VMEM((keys, 256), F32),
            ],
        ),
        compiler_params=pltpu.CompilerParams(vmem_limit_bytes=28 << 20),
        cost_estimate=cost(size, size // 1000, size // 3000),
        name=name,
    )(tlo, thi, qfirst, q, do, ot, lse, source, *tail)


def project_kernel(
    who, x0, x1, x2, x3_top, x3_bottom, w_mine, w_other, bias_ref, chosen, q_ref, kv_ref, up_ref, down_ref, w_ref
):
    tall = w_mine.shape[0]
    rows = x0.shape[0]
    w_ref[pl.ds(pl.multiple_of(who[0] * tall, tall), tall), :] = w_mine[...]
    w_ref[pl.ds(pl.multiple_of((1 - who[0]) * tall, tall), tall), :] = w_other[...]
    for d, x in enumerate((x0, x1, x2, (x3_top, x3_bottom))):
        if d < 3:
            value = mm(x[...], w_ref[...]) + bias_ref[...]
        else:
            value = jnp.concatenate([mm(x[0][...], w_ref[...]), mm(x[1][...], w_ref[...])], axis=0) + bias_ref[...]
        at = slice(d * rows, (d + 1) * rows)
        q_ref[at, :] = (value[:, :256].astype(BF).astype(F32) * HD ** (-0.5)).astype(BF)
        kv = mm(chosen[d], value[:, 256:].astype(BF)).astype(BF)
        kv_ref[at, :] = kv
        inner = slice((d % 2) * rows, (d % 2 + 1) * rows)

        @pl.when(who[2] == d // 2)
        def _(inner=inner, kv=kv):
            down_ref[inner, :] = kv

        @pl.when(who[2] != d // 2)
        def _(inner=inner, kv=kv):
            up_ref[inner, :] = kv


def project(who, xs, w_mine, w_other, bias, chosen):
    sd = jax.ShapeDtypeStruct
    rows, width = xs[0].shape
    cols = w_mine.shape[1]
    ins = (*xs, w_mine, w_other, bias, chosen)
    outs = (
        sd((4 * rows, 256), BF), sd((4 * rows, cols - 256), BF), sd((2 * rows, cols - 256), BF),
        sd((2 * rows, cols - 256), BF), sd((width, cols), BF),
    )
    return pl.pallas_call(
        project_kernel,
        out_shape=outs,
        grid_spec=pltpu.PrefetchScalarGridSpec(
            num_scalar_prefetch=1,
            grid=(1,),
            in_specs=[whole(a.shape) for a in ins],
            out_specs=tuple(whole(a.shape) for a in outs),
        ),
        compiler_params=pltpu.CompilerParams(vmem_limit_bytes=24 << 20),
        cost_estimate=cost(3_000_000_000, 12_000_000),
        name="project",
    )(who, *ins)


def row_mean(v):
    return jnp.sum(v, axis=-1, keepdims=True) * (1.0 / v.shape[-1])

def dense_kernel(
    who, o_ref, wo_a, wo_b, win_hbm, wback_hbm, x_ref, teacher_ref, cot_ref, keep_ref, vec_ref,
    out_ref, dres_ref, dparts_ref, act_ref, dbr_ref, dpre_ref, hid_ref, dproj_ref, sums_ref,
    wo, win, wback, xh, inv, hidden, gp, acc, sems, *, FB
):
    rows, width = x_ref.shape
    groups = o_ref.shape[0] // rows
    part = width // groups
    units = win.shape[1]
    wo_loads, win_loads, wback_loads = [], [], []
    for i in range(2):
        side = who[0] if i == 0 else 1 - who[0]
        for e in range(groups // 2):
            to = pl.multiple_of(((side * (groups // 2) + e) ^ who[1]) * part, part)
            wo_loads.append(
                pltpu.make_async_copy((wo_a, wo_b)[i].at[pl.ds(e * part, part)], wo.at[pl.ds(to, part)], sems.at[2 * i + e])
            )
    for j, (source, target, held) in enumerate(((win_hbm, win, win_loads), (wback_hbm, wback, wback_loads))):
        held.append(pltpu.make_async_copy(source, target, sems.at[4 + j]))
    for load in wo_loads + win_loads + wback_loads:
        load.start()
    b_out, b_in, b_back = vec_ref[0:1, 0:width], vec_ref[1:2, :], vec_ref[2:3, 0:width]
    gain1, shift1, gain2, shift2 = (vec_ref[i : i + 1, 0:width] for i in range(3, 7))
    for load in wo_loads:
        load.wait()
    total = x_ref[...].astype(F32) + b_out
    for i in range(groups):
        total += mm(o_ref[i * rows : (i + 1) * rows, :], wo[i * part : (i + 1) * part, :])
    center = total - row_mean(total)
    scale = lax.rsqrt(row_mean(center * center) + 1e-12)
    inv[...] = scale
    unit = center * scale
    xh[...] = unit
    hid = unit * gain1 + shift1
    hidden[...] = hid
    hid_ref[...] = hid.astype(BF)
    acc[...] = jnp.zeros_like(acc)
    for load in win_loads + wback_loads:
        load.wait()

    def up(n, _):
        cols = pl.ds(pl.multiple_of(n * FB, FB), FB)
        pre = mm(hid_ref[...], win[:, cols]) + vec_ref[1:2, cols]
        cdf = 0.5 + 0.5 * lax.erf(pre * 0.7071067811865476)
        act = (pre * cdf).astype(BF)
        act_ref[:, cols] = act
        gp[:, cols] = cdf + pre * (jnp.exp(pre * pre * -0.5) * 0.3989422804014327)
        acc[...] += mm(act, wback[cols, :])
        return 0

    lax.fori_loop(0, units // FB, up, 0, unroll=True)
    total = hidden[...] + acc[...] + b_back
    center = total - row_mean(total)
    scale = lax.rsqrt(row_mean(center * center) + 1e-12)
    unit = center * scale
    result = unit * gain2 + shift2
    out_ref[...] = result.astype(BF)
    grad = cot_ref[...].astype(F32) + keep_ref[...] * (result - teacher_ref[...].astype(F32))
    def put(row, value):
        sums_ref[row : row + 1, 0 : value.shape[1]] = value
    put(5, jnp.sum(grad * unit, axis=0, keepdims=True))
    put(6, jnp.sum(grad, axis=0, keepdims=True))
    grad = grad * gain2
    back = scale * (grad - row_mean(grad) - unit * row_mean(grad * unit))
    acc[...] = back
    low = back.astype(BF)
    dbr_ref[...] = low
    put(2, jnp.sum(low.astype(F32), axis=0, keepdims=True))

    def down(n, _):
        cols = pl.ds(pl.multiple_of(n * FB, FB), FB)
        dpre = (mm(dbr_ref[...], wback[cols, :], NT) * gp[:, cols]).astype(BF)
        dpre_ref[:, cols] = dpre
        sums_ref[1:2, cols] = jnp.sum(dpre.astype(F32), axis=0, keepdims=True)
        acc[...] += mm(dpre, win[:, cols], NT)
        return 0

    lax.fori_loop(0, units // FB, down, 0, unroll=True)
    grad = acc[...]
    unit = xh[...]
    put(3, jnp.sum(grad * unit, axis=0, keepdims=True))
    put(4, jnp.sum(grad, axis=0, keepdims=True))
    grad = grad * gain1
    back = inv[...] * (grad - row_mean(grad) - unit * row_mean(grad * unit))
    dres_ref[...] = back
    low = back.astype(BF)
    dproj_ref[...] = low
    put(0, jnp.sum(low.astype(F32), axis=0, keepdims=True))
    for i in range(groups):
        dparts_ref[i * rows : (i + 1) * rows, :] = mm(low, wo[i * part : (i + 1) * part, :], NT).astype(BF)


def dense(who, o, weights, x, teacher, cot, keep, vec):
    rows, width = x.shape
    units = vec.shape[1]
    sd = jax.ShapeDtypeStruct
    outs = (
        sd((rows, width), BF), sd((rows, width), F32), sd(o.shape, BF), sd((rows, units), BF), sd((rows, width), BF),
        sd((rows, units), BF), sd((rows, width), BF), sd((rows, width), BF), sd((8, units), F32),
    )
    ins = (o, *weights, x, teacher, cot, keep, vec)
    stay = pl.BlockSpec(memory_space=pl.ANY)
    return pl.pallas_call(
        functools.partial(dense_kernel, FB=FFB),
        out_shape=outs,
        grid_spec=pltpu.PrefetchScalarGridSpec(
            num_scalar_prefetch=1,
            grid=(1,),
            in_specs=[whole(o.shape)] + [stay] * 4 + [whole(a.shape) for a in ins[5:]],
            out_specs=tuple(whole(a.shape) for a in outs),
            scratch_shapes=[
                pltpu.VMEM((width, width), BF), pltpu.VMEM((width, units), BF), pltpu.VMEM((units, width), BF),
                pltpu.VMEM((rows, width), F32), pltpu.VMEM((rows, 1), F32), pltpu.VMEM((rows, width), F32),
                pltpu.VMEM((rows, units), F32), pltpu.VMEM((rows, width), F32), pltpu.SemaphoreType.DMA((8,)),
            ],
        ),
        compiler_params=pltpu.CompilerParams(vmem_limit_bytes=50 << 20),
        cost_estimate=cost(12_000_000_000, 30_000_000, 4_000_000),
        name="dense",
    )(who, *ins)


def finish_kernel(who, dq_ref, own_a, own_b, pair_a, pair_b, left_ref, right_ref, turn_ref, all_ref, sums_ref):
    groups, rows = turn_ref.shape[:2]
    sums_ref[...] = jnp.zeros_like(sums_ref)
    for d in range(groups):
        at = pl.ds(d * rows, rows)
        inner = pl.ds((d % (groups // 2)) * rows, rows)
        first = (d < groups // 2) == (who[2] == 0)
        own_ref, pair_ref = ((own_a, pair_a), (own_b, pair_b))[d // (groups // 2)]
        back = own_ref[inner, :].astype(F32) + pair_ref[inner, :].astype(F32)
        back += jnp.where(first, left_ref[inner, :], right_ref[inner, :]).astype(F32)
        tok = mm(turn_ref[d], back.astype(BF)).astype(BF)
        dq = dq_ref[at, :]
        all_ref[at, 0:256] = dq
        all_ref[at, 256:640] = tok
        sums_ref[0:1, 0:256] += jnp.sum(dq.astype(F32), axis=0, keepdims=True)
        sums_ref[0:1, 256:640] += jnp.sum(tok.astype(F32), axis=0, keepdims=True)


def finish(who, dq, own_a, own_b, pair_a, pair_b, left, right, turn):
    sd = jax.ShapeDtypeStruct
    cols = dq.shape[1] + own_a.shape[1]
    ins = (dq, own_a, own_b, pair_a, pair_b, left, right, turn)
    outs = (sd((dq.shape[0], cols), BF), sd((8, cols), F32))
    return pl.pallas_call(
        finish_kernel,
        out_shape=outs,
        grid_spec=pltpu.PrefetchScalarGridSpec(
            num_scalar_prefetch=1,
            grid=(1,),
            in_specs=[whole(a.shape) for a in ins],
            out_specs=tuple(whole(a.shape) for a in outs),
        ),
        compiler_params=pltpu.CompilerParams(vmem_limit_bytes=20 << 20),
        cost_estimate=cost(1_000_000_000, 9_000_000),
        name="finish",
    )(who, *ins)


def spread_kernel(all_ref, w_ref, own_ref, gx_ref, gy_ref, left_ref, right_ref):
    rows, width = own_ref.shape
    cut = width // 2
    parts = [mm(all_ref[d * rows : (d + 1) * rows, :], w_ref[...], NT).astype(BF) for d in range(4)]
    own_ref[...] = parts[0]
    gx_ref[0:rows, :] = parts[1][:, :cut]
    right_ref[...] = parts[1][:, cut:]
    left_ref[...] = parts[2][:, :cut]
    gy_ref[0:rows, :] = parts[2][:, cut:]
    gx_ref[rows:, :] = parts[3][:, :cut]
    gy_ref[rows:, :] = parts[3][:, cut:]


def spread_x(d_all, w_heads):
    rows, width = d_all.shape[0] // 4, w_heads.shape[0]
    shapes = ((rows, width), (2 * rows, width // 2), (2 * rows, width // 2), (rows, width // 2), (rows, width // 2))
    return pl.pallas_call(
        spread_kernel,
        out_shape=tuple(jax.ShapeDtypeStruct(s, BF) for s in shapes),
        grid=(1,),
        in_specs=[whole(d_all.shape), whole(w_heads.shape)],
        out_specs=tuple(whole(s) for s in shapes),
        compiler_params=pltpu.CompilerParams(vmem_limit_bytes=24 << 20),
        cost_estimate=cost(2_000_000_000, 7_000_000),
        name="spread_x",
    )(d_all, w_heads)


def place_blocks(who, refs, put):
    s1, s2 = lax.rem(who[1], 2), who[1] // 2
    tall = refs[0].shape[0] // 2
    for at, ref in enumerate(refs):
        color, i = at // 2, at % 2
        for j in range(2):
            spot = (s1 ^ i) * 2 + (s2 ^ j) if color == 0 else 4 + (s2 ^ i) * 2 + (s1 ^ j)
            put(pl.ds(pl.multiple_of(spot * tall, 8), tall), ref[j * tall : (j + 1) * tall, :].astype(F32))


def back_out_kernel(who, a, b, c, d, out_ref):
    width = out_ref.shape[1]

    def put(at, value):
        for k in range(4):
            to = pl.multiple_of(4 * at.start + k * at.size, 8)
            out_ref[pl.ds(to, at.size), :] = value[:, k * width : (k + 1) * width]

    place_blocks(who, (a, b, c, d), put)


def in_out_kernel(who, a, b, c, d, in_ref, out_ref, vec_ref, held):
    def put(at, value):
        held[at, :] = value

    place_blocks(who, (a, b, c, d), put)
    tall, width = out_ref.shape
    in_ref[...] = held[0:tall, :]
    for k in range(3):
        out_ref[k * 128 : (k + 1) * 128, :] = held[tall:, k * width : (k + 1) * width]
    vec_ref[...] = held[tall : tall + 8, 3 * width :]


def out_call(kernel, who, pieces, shapes, scratch, name):
    return pl.pallas_call(
        kernel,
        out_shape=tuple(jax.ShapeDtypeStruct(s, F32) for s in shapes),
        grid_spec=pltpu.PrefetchScalarGridSpec(
            num_scalar_prefetch=1,
            grid=(1,),
            in_specs=[whole(a.shape) for a in pieces],
            out_specs=tuple(whole(s) for s in shapes),
            scratch_shapes=scratch,
        ),
        compiler_params=pltpu.CompilerParams(vmem_limit_bytes=24 << 20),
        cost_estimate=cost(1_000_000, 9_000_000),
        name=name,
    )(who, *pieces)


def heads_kernel(who, h0, h1, h2, h3, q_ref, k_ref, v_ref, bias_ref, held):
    tall = q_ref.shape[0]
    for d, ref in enumerate((h0, h1, h2, h3)):
        held[who[1] ^ d] = ref[...]
    for a in range(4):
        cols = slice(a * 192, (a + 1) * 192)
        q_ref[:, cols] = held[a, 0:tall, 64:256].astype(F32)
        v_ref[:, cols] = held[a, 0:tall, 256:448].astype(F32)
        k_ref[:, cols] = held[a, 0:tall, 448:640].astype(F32)
        line = held[a, 0:16, 0:64].astype(F32)
        for k in range(3):
            spot = slice(a * 192 + k * 64, a * 192 + (k + 1) * 64)
            bias_ref[0:1, spot] = line[k : k + 1]
            bias_ref[8:9, spot] = line[k + 3 : k + 4]


def heads_out(who, pieces):
    sd = jax.ShapeDtypeStruct
    outs = (sd((384, 768), F32),) * 3 + (sd((16, 768), F32),)
    return pl.pallas_call(
        heads_kernel,
        out_shape=outs,
        grid_spec=pltpu.PrefetchScalarGridSpec(
            num_scalar_prefetch=1,
            grid=(1,),
            in_specs=[whole(a.shape) for a in pieces],
            out_specs=tuple(whole(a.shape) for a in outs),
            scratch_shapes=[pltpu.VMEM((4, *pieces[0].shape), BF)],
        ),
        compiler_params=pltpu.CompilerParams(vmem_limit_bytes=24 << 20),
        cost_estimate=cost(1_000_000, 6_000_000),
        name="heads_out",
    )(who, *pieces)


def swap(block, axis="fsdp"):
    return lax.ppermute(block, axis, [(0, 1), (1, 0)])


def shifted(block, axis, distance):
    devices = range(lax.axis_size(axis))
    route = [(i - distance, i) for i in devices if i - distance in devices]
    return lax.ppermute(block, axis, route)


def flip(block, bit, axis="uly"):
    return lax.ppermute(block, axis, [(i, i ^ bit) for i in range(lax.axis_size(axis))])


def exchange(rows, axis):
    return lax.all_to_all(rows, axis, split_axis=0, concat_axis=0, tiled=True)


def spread_rows(rows, axis):
    count = lax.axis_size(axis)
    return exchange(jnp.broadcast_to(rows[None], (count, *rows.shape)).reshape(-1, rows.shape[1]), axis)


def sum_parts(rows, count):
    got = rows.reshape(count, -1, rows.shape[1])
    return sum(got[i].astype(F32) for i in range(count)).astype(BF)


def sum_scatter(rows, axis):
    return sum_parts(exchange(rows, axis), lax.axis_size(axis))


def add(left, right):
    return (left.astype(F32) + right.astype(F32)).astype(BF)


def sides(rows, bit):
    side = jnp.where((lax.axis_index("uly") & bit) > 0, 1, 0)
    split = rows.reshape(2, -1, rows.shape[1])
    return (
        lax.dynamic_index_in_dim(split, side, 0, keepdims=False),
        lax.dynamic_index_in_dim(split, 1 - side, 0, keepdims=False),
    )


def halve(rows, bit):
    mine, other = sides(rows, bit)
    return add(mine, flip(other, bit))


def halves(rows):
    middle = rows.shape[0] // 2
    return rows[:middle], rows[middle:]


def wide(rows):
    tall = rows.shape[0] // 4
    return jnp.concatenate([rows[i * tall : (i + 1) * tall] for i in range(4)], axis=1)


def slim(rows):
    cols = rows.shape[1] // 4
    return jnp.concatenate([rows[:, i * cols : (i + 1) * cols] for i in range(4)], axis=0)


def line_step(held, bit):
    return flip(held, bit, "ctx")


def line_join(held, got, bit):
    low = (lax.axis_index("ctx") & bit) == 0
    return jnp.stack([jnp.where(low, held, got), jnp.where(low, got, held)], axis=1).reshape(-1, *held.shape[1:])


def line_rest(held, bit):
    while bit > 0:
        held = line_join(held, line_step(held, bit), bit)
        bit //= 2
    return held.reshape(-1, held.shape[2])


def tie(*values):
    return lax.optimization_barrier(values)


def on_device(
    tokens, teacher, cotangent, valid, teacher_ok, doc_starts, w_query, w_key, w_value, w_out, w_in, w_back,
    bias_query, bias_value, bias_out, bias_in, bias_back, norm1_gain, norm1_bias, norm2_gain, norm2_bias,
):
    groups = lax.axis_size("uly")
    spans = lax.axis_size("ctx")
    rows, width = tokens.shape
    block = rows * groups * 2
    stream = block * spans
    ctx_index = lax.axis_index("ctx")
    uly = lax.axis_index("uly")
    half = lax.axis_index("fsdp")
    head_cols = width // groups
    shard = w_query.shape[0]
    middle = groups * rows // 2
    upper = uly // 2

    small = (bias_query, bias_value, bias_out, bias_in, bias_back, norm1_gain, norm1_bias, norm2_gain, norm2_bias)
    valid_one = valid[None, :]
    valid_own = jnp.concatenate([valid_one, flip(valid_one, 1), flip(valid_one, 2), flip(valid_one, 3)], axis=0)
    x_own, valid_own, *small = tie(tokens, valid_own, *small)
    x_x, x_y = flip(x_own, 1), flip(x_own, 2)
    valid_pair = swap(valid_own)
    valid_both = jnp.stack([valid_own, valid_pair]).reshape(2, 2, 2, rows)
    valid_high = lax.dynamic_index_in_dim(valid_both, 1 - upper, 1, keepdims=False)
    valid_low = lax.dynamic_index_in_dim(valid_both, upper, 1, keepdims=False)
    halo = (shifted(valid_high, "ctx", 1), shifted(valid_low, "ctx", -1))
    block_valid = jnp.concatenate([valid_own, valid_pair, halo[0][0], halo[1][0], halo[0][1], halo[1][1]], axis=0)
    count = jnp.full((8, 128), jnp.sum(valid_both), jnp.int32)
    bit = 1
    while bit < spans:
        count = count + flip(count, bit, "ctx")
        bit *= 2
    count = count[0, 0].astype(F32)

    start_col = uly * head_cols
    cut = [lax.dynamic_slice_in_dim(w, start_col, head_cols, 1) for w in (w_query, w_value, w_key)]
    w_mine = jnp.concatenate([jnp.zeros((shard, 256 - head_cols), BF), *cut], axis=1)
    w_other = swap(w_mine)
    who = jnp.stack([half, uly, upper])
    packed = jnp.concatenate(small)
    packed_pair = swap(packed)
    first, second = jnp.where(half == 0, packed, packed_pair), jnp.where(half == 0, packed_pair, packed)
    vectors = []
    at = 0
    for p in small:
        n = p.shape[0]
        vectors.append(jnp.concatenate([first[at : at + n], second[at : at + n]]).astype(F32))
        at += n
    bq_all, bv_all = vectors[:2]
    vec = jnp.stack([jnp.pad(v, (0, w_in.shape[1] - v.shape[0])) for v in vectors[2:]] + [jnp.zeros((w_in.shape[1],), F32)])
    bias_heads = jnp.concatenate(
        [
            jnp.zeros((256 - head_cols,), F32),
            lax.dynamic_slice_in_dim(bq_all, start_col, head_cols, 0),
            lax.dynamic_slice_in_dim(bv_all, start_col, head_cols, 0),
            jnp.zeros((head_cols,), F32),
        ]
    )

    place = jnp.arange(groups, dtype=jnp.int32)
    two = jnp.arange(2, dtype=jnp.int32)
    in_plane = place ^ uly
    halo_group = jnp.concatenate([uly ^ (2 * (1 - upper) + two), uly ^ (2 * upper + two)])
    halo_plane = ctx_index + jnp.where(place < 2, -1, 1)
    plane_of = jnp.concatenate([jnp.full((2 * groups,), 1, jnp.int32) * ctx_index, halo_plane, halo_plane])
    group_of = jnp.concatenate([in_plane, in_plane, halo_group, halo_group])
    mine = jnp.full((groups,), 1, jnp.int32) * half
    core_of = jnp.concatenate([mine, 1 - mine, mine, 1 - mine])
    block_id = plane_of * (2 * groups) + group_of * 2 + core_of
    spot = block_id[:, None] * rows + jnp.arange(rows, dtype=jnp.int32)[None, :]
    edges = jnp.concatenate([doc_starts, jnp.full((DOCS + 1,), stream, jnp.int32)])
    window_first = jnp.maximum(ctx_index * block - block // 2, 0)
    first_doc = jnp.sum((doc_starts <= window_first).astype(jnp.int32)) - 1
    near = lax.dynamic_slice_in_dim(edges, first_doc, DOCS + 1, 0)
    tiles = groups * rows // TQ
    per = rows // TQ
    tile_ids = jnp.arange(tiles, dtype=jnp.int32)
    qfirst = ctx_index * block + (((tile_ids // per) ^ uly) * 2 + half) * rows + lax.rem(tile_ids, per) * TQ
    q_lo = jnp.max(jnp.where(near[None, :] <= qfirst[:, None], near[None, :], 0), axis=1)
    q_hi = jnp.min(jnp.where(near[None, :] <= qfirst[:, None] + TQ - 1, stream, near[None, :]), axis=1)
    limits = jnp.concatenate([near, q_lo, q_hi])
    counted = jnp.sum(block_valid[:, None, :] * (spot[:, None, :] < limits[None, :, None]), axis=-1)
    bounds = counted[:, : DOCS + 1]
    cnt_lo = counted[:, DOCS + 1 : DOCS + 1 + tiles].T
    cnt_hi = counted[:, DOCS + 1 + tiles :].T
    pad64 = jnp.zeros((bounds.shape[0], 128 - DOCS), jnp.int32)
    lo_tab = jnp.concatenate([bounds[:, :DOCS], pad64], axis=1)
    hi_tab = jnp.concatenate([bounds[:, 1:], pad64], axis=1)
    slo_tab = jnp.concatenate([near[:DOCS], pad64[0]])[None, :]
    shi_tab = jnp.concatenate([near[1:], pad64[0]])[None, :]
    some = cnt_hi > cnt_lo
    tlo = jnp.where(some, cnt_lo // TK, 0)
    thi = jnp.where(some, (cnt_hi + TK - 1) // TK, 0)
    tables = (tlo, thi, qfirst, lo_tab, hi_tab, slo_tab, shi_tab)
    before = mm(valid_own.astype(BF), (jnp.arange(rows)[:, None] < jnp.arange(rows)[None, :]).astype(BF)).astype(jnp.int32)
    goes_to = jnp.where(valid_own > 0, before, rows)
    chosen = (goes_to[:, None, :] == jnp.arange(rows, dtype=jnp.int32)[None, :, None]).astype(BF)
    loss_scale = jnp.float32(stream) / count
    keep = (loss_scale * (valid * teacher_ok).astype(F32))[:, None]
    turned = (goes_to[:, :, None] == jnp.arange(rows, dtype=jnp.int32)[None, None, :]).astype(BF)

    x_x, x_y, w_other, chosen, bias_heads, *tables = tie(x_x, x_y, w_other, chosen, bias_heads, *tables)
    x_top, x_bottom = flip(x_y[: rows // 2], 1), flip(x_x[rows // 2 :], 2)

    q_low, kv_own, kv_up, kv_down, w_heads = project(
        who, (tokens, x_x, x_y, x_top, x_bottom), w_mine, w_other, bias_heads[None, :], chosen
    )
    kv_from_left, kv_from_right = shifted(kv_up, "ctx", 1), shifted(kv_down, "ctx", -1)
    w_out, w_in, w_back, kv_own = tie(w_out, w_in, w_back, kv_own)
    wo_pair, win_pair, wback_pair = swap(w_out), swap(w_in), swap(w_back)
    kv_pair = swap(kv_own)
    state = attend(tables, q_low, (kv_own,), 0)
    kv_halo = jnp.concatenate([kv_from_left, kv_from_right], axis=0)
    kv_halo, kv_pair, *state = tie(kv_halo, kv_pair, *state)
    kv_halo_pair = swap(kv_halo)
    state = attend(tables, q_low, (kv_pair,), groups, state)
    o_heads, o_turned, lse = attend(tables, q_low, (kv_halo, kv_halo_pair), 2 * groups, state, last=True)
    x_all = jnp.concatenate([tokens, x_x, x_y, x_top, x_bottom], axis=0)
    o_rel = o_heads.reshape(groups, rows, head_cols)
    o_rest = [flip(o_rel[d], d) for d in range(1, groups)]
    win_pair, wback_pair, o_heads = tie(win_pair, wback_pair, o_heads)

    def both(mine, other):
        return jnp.concatenate([jnp.where(half == 0, mine, other), jnp.where(half == 0, other, mine)], axis=0)

    win_all, wback_all, *o_rest = tie(both(w_in, win_pair), both(w_back, wback_pair), *o_rest)
    o_all = jnp.concatenate([o_rel[0], *o_rest], axis=0)

    out, d_resid1, d_parts, act, d_branch, d_pre, hidden_low, d_proj, sums = dense(
        who, o_all, (w_out, wo_pair, win_all, wback_all), tokens, teacher, cotangent, keep, vec
    )
    d_rel = d_parts.reshape(groups, rows, head_cols)
    tall = w_back.shape[0]
    vector_rows = jnp.concatenate(
        [sums[i, :width].reshape(2, -1) for i in (0, 2, 3, 4, 5, 6)] + [sums[1].reshape(2, -1)], axis=1
    ).reshape(2, -1, width)
    vector_rows = jnp.pad(vector_rows, ((0, 0), (0, 128 - vector_rows.shape[1]), (0, 0))).astype(BF)
    o_rows = o_all.reshape(groups, rows, head_cols)

    def back_part(side):
        return mm(lax.dynamic_slice_in_dim(act, side * tall, tall, 1), d_branch, TN).astype(BF)

    def in_part(side):
        return mm(lax.dynamic_slice_in_dim(hidden_low, side * shard, shard, 1), d_pre, TN).astype(BF)

    def out_part(side):
        both = [
            mm(lax.dynamic_index_in_dim(o_rows, (2 * side + e) ^ uly, 0, keepdims=False), d_proj, TN).astype(BF)
            for e in range(2)
        ]
        stack = jnp.concatenate([*both, lax.dynamic_index_in_dim(vector_rows, side, 0, keepdims=False)], axis=0)
        return jnp.concatenate([stack[i * 128 : (i + 1) * 128] for i in range(4)], axis=1)

    d_rest = [flip(d_rel[d], d) for d in range(1, groups)]
    back_got = swap(back_part(1 - half))
    in_other, out_other = in_part(1 - half), out_part(1 - half)
    back_sum = add(back_part(half), back_got)
    b1, b2 = halves(back_sum)
    (b1m, b1o), (b2m, b2o) = sides(b1, 1), sides(b2, 2)
    in_other, out_other, b1o, b2o, *d_rest = tie(in_other, out_other, b1o, b2o, *d_rest)
    b1g, b2g = flip(b1o, 1), flip(b2o, 2)
    in_got, out_got = swap(in_other), swap(out_other)
    in_mine, out_mine = in_part(half), out_part(half)
    in_sum = jnp.concatenate([add(in_mine, in_got), add(out_mine, out_got)], axis=0)
    i1, i2 = halves(in_sum)
    (i1m, i1o), (i2m, i2o) = sides(i1, 1), sides(i2, 2)
    d_heads = jnp.concatenate([d_rel[0], *d_rest], axis=0)
    d_heads, b1g, b2g, i1m, i1o, i2m, i2o = tie(d_heads, b1g, b2g, i1m, i1o, i2m, i2o)

    b1, b2 = add(b1m, b1g), add(b2m, b2g)
    (b1m, b1o), (b2m, b2o) = sides(b1, 2), sides(b2, 1)
    mix1 = jnp.concatenate([i1o, wide(b2o)], axis=0)
    mix2 = jnp.concatenate([i2o, wide(b1o)], axis=0)
    d_heads, mix1, mix2, b1m, b2m = tie(d_heads, mix1, mix2, b1m, b2m)
    args = (tables, q_low, d_heads, o_turned, lse)
    m1g, m2g = flip(mix1, 1), flip(mix2, 2)
    dq_state, dkv_halo_pair, delta = attend_back(*args, kv_halo_pair, 3 * groups, 0, 1, name="back_halo_pair")
    dq_state, dkv_halo_pair = tie(dq_state, dkv_halo_pair)
    args = (tables, q_low, d_heads, delta, lse)
    got_lo, got_hi = swap(dkv_halo_pair[:middle]), swap(dkv_halo_pair[middle:])
    dq_state, dkv_halo = attend_back(*args, kv_halo, 2 * groups, 0, 1, dq_state, name="back_halo", size=1_000_000)
    dq_state, dkv_halo, got_lo, got_hi, m1g, m2g = tie(dq_state, dkv_halo, got_lo, got_hi, m1g, m2g)

    halo_lo, halo_hi = add(dkv_halo[:middle], got_lo), add(dkv_halo[middle:], got_hi)
    tall = i1o.shape[0]
    back_line = jnp.concatenate([add(wide(b1m), m2g[tall:]), add(wide(b2m), m1g[tall:])], axis=0)
    i1, i2 = add(i1m, m1g[:tall]), add(i2m, m2g[:tall])
    (i1m, i1o), (i2m, i2o) = sides(i1, 2), sides(i2, 1)
    dq_state, halo_lo, halo_hi, back_line, i1m, i1o, i2m, i2o = tie(
        dq_state, halo_lo, halo_hi, back_line, i1m, i1o, i2m, i2o
    )
    i1g, i2g = flip(i1o, 2), flip(i2o, 1)
    from_left, from_right = shifted(halo_hi, "ctx", 1), shifted(halo_lo, "ctx", -1)
    back_line = exchange(back_line, "ctx")
    dq_state, dkv_pair_a = attend_back(*args, kv_pair, groups, 0, 2, dq_state, name="back_pair_a")
    dq_state, dkv_pair_a, i1g, i2g, back_line = tie(dq_state, dkv_pair_a, i1g, i2g, back_line)

    bit = spans // 2
    back_line = sum_parts(back_line, spans)[None]
    in_line = jnp.concatenate([add(i1m, i1g), add(i2m, i2g)], axis=0)
    dq_state, dkv_pair_a, back_line, in_line = tie(dq_state, dkv_pair_a, back_line, in_line)
    back_got = line_step(back_line, bit)
    in_line = exchange(in_line, "ctx")
    pair_a = swap(dkv_pair_a)
    dq_state, dkv_pair_b = attend_back(*args, kv_pair, groups, 1, 2, dq_state, name="back_pair_b")
    dq_state, dkv_pair_b, back_got, in_line, pair_a, from_left, from_right = tie(
        dq_state, dkv_pair_b, back_got, in_line, pair_a, from_left, from_right
    )

    back_line = line_join(back_line, back_got, bit)
    in_line = sum_parts(in_line, spans)[None]
    dq_state, dkv_pair_b, back_line, in_line = tie(dq_state, dkv_pair_b, back_line, in_line)
    in_got = line_step(in_line, bit)
    back_got = line_step(back_line, bit // 2)
    pair_b = swap(dkv_pair_b)
    dq_state, dkv_own_a = attend_back(*args, kv_own, 0, 0, 2, dq_state, name="back_own_a")
    dq_state, dkv_own_a, in_got, back_got, pair_b = tie(dq_state, dkv_own_a, in_got, back_got, pair_b)

    b1, b2 = halves(line_rest(line_join(back_line, back_got, bit // 2), bit // 4))
    in_line = line_join(in_line, in_got, bit)
    dq_state, b1, b2, in_line = tie(dq_state, b1, b2, in_line)
    b1g, b2g = flip(b1, 2), flip(b2, 1)
    in_got = line_step(in_line, bit // 2)
    dq, dkv_own_b = attend_back(*args, kv_own, 0, 1, 2, dq_state, last=True, name="back_own_b")
    dq, dkv_own_b, b1g, b2g, in_got = tie(dq, dkv_own_b, b1g, b2g, in_got)
    in_line = line_rest(line_join(in_line, in_got, bit // 2), bit // 4)

    b1, b2 = jnp.concatenate([b1, b1g], axis=0), jnp.concatenate([b2, b2g], axis=0)
    i1, i2 = halves(in_line)
    dq, b1, b2, i1, i2 = tie(dq, b1, b2, i1, i2)
    mix1 = flip(jnp.concatenate([b1, i2], axis=0), 1)
    mix2 = flip(jnp.concatenate([b2, i1], axis=0), 2)
    d_all, d_sums = finish(who, dq, dkv_own_a, dkv_own_b, pair_a, pair_b, from_left, from_right, turned)
    corner = d_sums[0, 64:].reshape(9, 64)

    def heads_part(side):
        grad = mm(lax.dynamic_slice_in_dim(x_all, side * shard, shard, 1), d_all, TN)
        return lax.dynamic_update_slice(grad, corner, (0, 0)).astype(BF)

    heads_other = heads_part(1 - half)
    heads_got = swap(heads_other)
    heads_mine = heads_part(half)
    dx_own, give_x, give_y, left_next, right_next = spread_x(d_all, w_heads)
    give_x, give_y, heads_got, mix1, mix2 = tie(give_x, give_y, heads_got, mix1, mix2)
    heads_line = exchange(add(heads_mine, heads_got), "ctx")
    give_x, give_y = flip(give_x, 1), flip(give_y, 2)
    tall = b1.shape[0]
    i1 = jnp.concatenate([i1, mix2[tall:]], axis=0)
    i2 = jnp.concatenate([i2, mix1[tall:]], axis=0)
    i1g, i2g = flip(i1, 1), flip(i2, 2)
    (g_back,) = out_call(back_out_kernel, who, (b1, mix1[:tall], b2, mix2[:tall]), (w_back.shape,), [], "back_out")
    heads_line = sum_parts(heads_line, spans)[None]
    left_next = flip(add(left_next, give_x[rows:]), 2)
    right_next = flip(add(right_next, give_y[rows:]), 1)
    heads_sum = line_rest(heads_line, bit)
    heads_all = [heads_sum] + [flip(heads_sum, d) for d in range(1, groups)]
    grad_in = d_resid1 + dx_own.astype(F32)
    grad_in = grad_in + jnp.concatenate([give_x[:rows].astype(F32), give_y[:rows].astype(F32)], axis=1)
    grad_in = grad_in + jnp.concatenate([left_next.astype(F32), right_next.astype(F32)], axis=1)
    g_in, g_out, g_vec = out_call(
        in_out_kernel, who, (i1, i1g, i2, i2g), (w_in.shape, w_out.shape, (8, width)),
        [pltpu.VMEM((shard + 128, w_in.shape[1]), F32)], "in_out",
    )
    g_query, g_key, g_value, g_bias = heads_out(who, heads_all)
    g_bias_q = lax.dynamic_slice_in_dim(g_bias[0], half * shard, shard, 0)
    g_bias_v = lax.dynamic_slice_in_dim(g_bias[8], half * shard, shard, 0)
    flat = g_vec.reshape(-1)
    g_bo, g_bb, g_g1, g_s1, g_g2, g_s2 = [flat[i * shard : (i + 1) * shard] for i in range(6)]
    g_bin = flat[6 * shard : 6 * shard + bias_in.shape[0]]
    return (
        out, grad_in, g_query, g_key, g_value, g_out, g_in, g_back,
        g_bias_q, g_bias_v, g_bo, g_bin, g_bb, g_g1, g_s1, g_g2, g_s2,
    )


def solution(mesh):
    placed = (
        P(("ctx", "uly", "fsdp"), None),
        P(("ctx", "uly", "fsdp"), None),
        P(("ctx", "uly", "fsdp"), None),
        P(("ctx", "uly", "fsdp")),
        P(("ctx", "uly", "fsdp")),
        P(),
        P("fsdp", None),
        P("fsdp", None),
        P("fsdp", None),
        P("fsdp", None),
        P("fsdp", None),
        P("fsdp", None),
        P("fsdp"),
        P("fsdp"),
        P("fsdp"),
        P("fsdp"),
        P("fsdp"),
        P("fsdp"),
        P("fsdp"),
        P("fsdp"),
        P("fsdp"),
    )
    return jax.shard_map(
        on_device,
        mesh=mesh,
        in_specs=placed,
        out_specs=(
            P(("ctx", "uly", "fsdp"), None),
            P(("ctx", "uly", "fsdp"), None),
            P("fsdp", None),
            P("fsdp", None),
            P("fsdp", None),
            P("fsdp", None),
            P("fsdp", None),
            P("fsdp", None),
            P("fsdp"),
            P("fsdp"),
            P("fsdp"),
            P("fsdp"),
            P("fsdp"),
            P("fsdp"),
            P("fsdp"),
            P("fsdp"),
            P("fsdp"),
        ),
        check_vma=False,
    )
```

```python
import functools

import jax
import jax.numpy as jnp
from jax import lax
from jax.experimental import pallas as pl
from jax.experimental.pallas import tpu as pltpu
from jax.sharding import PartitionSpec as P

HEADS = 12
HD = 64
BLK = 512
TQ = 256
TK = 256
DOCS = 64
FFB = 768
GRANT = 63 << 20
MASKED = -1e30
BF = jnp.bfloat16
F32 = jnp.float32
NT = (((1,), (1,)), ((), ()))
NN = (((1,), (0,)), ((), ()))
TN = (((0,), (0,)), ((), ()))


def mm(left, right, dims=NN):
    return lax.dot_general(left, right, dims, preferred_element_type=F32)


def whole(shape):
    return pl.BlockSpec(shape, lambda *_: (0,) * len(shape), pipeline_mode=pl.Buffered(1))


def cost(flops, moved, special=0):
    return pl.CostEstimate(flops=flops, bytes_accessed=moved, transcendentals=special)


def lane_ids(rows):
    return lax.broadcasted_iota(jnp.int32, (rows, 128), 1)


def build_keys(sources, slot0, lo_ref, hi_ref, kaug, transposed, low_half):
    per = BLK // TK
    for at, kv in enumerate(sources):

        def one(j, _, at=at, kv=kv):
            rows = pl.ds(pl.multiple_of(j * TK, TK), TK)
            tile = at * (kv.shape[0] // TK) + j
            slot = slot0 + at * (kv.shape[0] // BLK) + j // per
            out = pl.ds(pl.multiple_of(tile * TK, TK), TK)
            rank = lax.broadcasted_iota(jnp.int32, (TK, 128), 0) + lax.rem(j, per) * TK
            inside = (rank >= lo_ref[pl.ds(slot, 1), :]) & (rank < hi_ref[pl.ds(slot, 1), :])
            bias = jnp.where(inside, 0.0, MASKED).astype(BF)
            kaug[out, 0:128] = jnp.where(lane_ids(TK) < 64, bias, kv[rows, 128:256])
            kaug[out, 128:256] = kv[rows, 256:384]
            if low_half:
                transposed[tile] = kv[rows, 0:256].T[0:192]
            else:
                transposed[tile] = kaug[out, :].T[64:256]
            return 0

        lax.fori_loop(0, kv.shape[0] // TK, one, 0)


def stack_queries(q, first, slo_ref, shi_ref, qs):
    lane = lane_ids(TQ)
    spot = lax.broadcasted_iota(jnp.int32, (TQ, 128), 0) + first
    mine = ((spot >= slo_ref[...]) & (spot < shi_ref[...])).astype(F32).astype(BF)
    zero = jnp.zeros((TQ, 128), BF)
    low, high = q[:, 0:128], q[:, 128:256]
    mark = jnp.where(lane < 64, mine, zero)
    qs[0:TQ, 0:128] = jnp.where(lane < 64, mine, low)
    qs[TQ : 2 * TQ, 0:128] = mark
    qs[2 * TQ :, 0:128] = mark
    qs[0:TQ, 128:256] = zero
    qs[TQ : 2 * TQ, 128:256] = jnp.where(lane < 64, high, zero)
    qs[2 * TQ :, 128:256] = jnp.where(lane < 64, zero, high)


def attend_kernel(*refs, slot0, count, resume, last):
    tlo, thi, qfirst, q_ref = refs[:4]
    sources = refs[4 : 4 + count]
    lo_ref, hi_ref, slo_ref, shi_ref = refs[4 + count : 8 + count]
    at = 8 + count
    if resume:
        acc_in, stat_in = refs[at : at + 2]
        at += 2
    if last:
        o_ref, ot_ref, lse_ref = refs[at : at + 3]
        at += 3
    else:
        acc_out, stat_out = refs[at : at + 2]
        at += 2
    kaug, vt, qs, acc, m_s, l_s = refs[at:]
    i = pl.program_id(0)

    @pl.when(i == 0)
    def _():
        build_keys(sources, slot0, lo_ref, hi_ref, kaug, vt, True)

    slots = count * sources[0].shape[0] // BLK
    per = BLK // TK
    stack_queries(q_ref[...], qfirst[i], slo_ref, shi_ref, qs)
    if resume:
        m_s[...] = stat_in[0, 0:1, :]
        l_s[...] = stat_in[0, 1:2, :]
        acc[...] = acc_in[0]
    else:
        m_s[...] = jnp.full_like(m_s, 2 * MASKED)
        l_s[...] = jnp.zeros_like(l_s)
        acc[...] = jnp.zeros_like(acc)

    def slot_loop(s, _):
        def key_loop(t, _):
            tile = s * per + t
            keys = pl.ds(pl.multiple_of(tile * TK, TK), TK)
            st = mm(kaug[keys, :], qs[...], NT)
            m_old = m_s[...]
            m_new = jnp.maximum(m_old, jnp.max(st, axis=0, keepdims=True))
            fade = jnp.exp(m_old - m_new)
            p = jnp.exp(st - m_new)
            l_s[...] = l_s[...] * fade + jnp.sum(p, axis=0, keepdims=True)
            m_s[...] = m_new
            low = p.astype(BF)
            for h in range(3):
                cols = slice(h * TQ, (h + 1) * TQ)
                part = slice(h * HD, (h + 1) * HD)
                acc[part, :] = acc[part, :] * fade[:, cols] + mm(vt[tile, part, :], low[:, cols])
            return 0

        return lax.fori_loop(tlo[i, slot0 + s], thi[i, slot0 + s], key_loop, 0)

    lax.fori_loop(0, slots, slot_loop, 0)
    if last:
        total = l_s[...]
        for h in range(3):
            cols = slice(h * TQ, (h + 1) * TQ)
            part = slice(h * HD, (h + 1) * HD)
            acc[part, :] = acc[part, :] / total[:, cols]
        ot_ref[0] = acc[...]
        o_ref[...] = acc[...].T.astype(BF)
        lse_ref[0] = m_s[...] + jnp.log(total)
    else:
        acc_out[0] = acc[...]
        stat_out[0, 0:1, :] = m_s[...]
        stat_out[0, 1:2, :] = l_s[...]


def rows_spec(shape):
    return pl.BlockSpec((TQ, shape[1]), lambda i, *_: (i, 0))


def tile_spec(shape):
    return pl.BlockSpec((1, *shape[1:]), lambda i, *_: (i, 0, 0))


def attend(tables, q, sources, slot0, state=None, last=False):
    tlo, thi, qfirst, lo, hi, slo, shi = tables
    tiles = q.shape[0] // TQ
    keys = sum(s.shape[0] for s in sources)
    state = tuple(state) if state else ()
    sd = jax.ShapeDtypeStruct
    acc, stat = sd((tiles, 3 * HD, TQ), F32), sd((tiles, 2, 3 * TQ), F32)
    if last:
        o, lse = sd((q.shape[0], 3 * HD), BF), sd((tiles, 1, 3 * TQ), F32)
        outs, out_specs = (o, acc, lse), (rows_spec(o.shape), tile_spec(acc.shape), tile_spec(lse.shape))
    else:
        outs, out_specs = (acc, stat), (tile_spec(acc.shape), tile_spec(stat.shape))
    return pl.pallas_call(
        functools.partial(attend_kernel, slot0=slot0, count=len(sources), resume=bool(state), last=last),
        out_shape=outs,
        grid_spec=pltpu.PrefetchScalarGridSpec(
            num_scalar_prefetch=3,
            grid=(tiles,),
            in_specs=[rows_spec(q.shape)]
            + [whole(x.shape) for x in (*sources, lo, hi, slo, shi)]
            + [tile_spec(x.shape) for x in state],
            out_specs=out_specs,
            scratch_shapes=[
                pltpu.VMEM((keys, 256), BF),
                pltpu.VMEM((keys // TK, 3 * HD, TK), BF),
                pltpu.VMEM((3 * TQ, 256), BF),
                pltpu.VMEM((3 * HD, TQ), F32),
                pltpu.VMEM((1, 3 * TQ), F32),
                pltpu.VMEM((1, 3 * TQ), F32),
            ],
        ),
        compiler_params=pltpu.CompilerParams(vmem_limit_bytes=GRANT),
        cost_estimate=cost(12_000_000_000, 12_000_000, 10_000_000),
        name="attend",
    )(tlo, thi, qfirst, q, *sources, lo, hi, slo, shi, *state)


def attend_back_kernel(
    tlo, thi, qfirst, q_ref, do_ref, ot_ref, lse_ref, kv, lo_ref, hi_ref, slo_ref, shi_ref, dq_ref, dkv_ref, *rest,
    slot0, first,
):
    if first:
        delta_ref, *rest = rest
    kaug, kt, qs, dos, acc, dk_s, dv_s = rest
    keys_all = kv.shape[0]
    slots = keys_all // BLK
    per = BLK // TK
    i = pl.program_id(0)

    @pl.when(i == 0)
    def _():
        build_keys((kv,), slot0, lo_ref, hi_ref, kaug, kt, False)
        dk_s[...] = jnp.zeros_like(dk_s)
        dv_s[...] = jnp.zeros_like(dv_s)

    stack_queries(q_ref[...], qfirst[i], slo_ref, shi_ref, qs)
    do = do_ref[...]
    lane = lane_ids(TQ)
    zero = jnp.zeros((TQ, 128), BF)
    dos[0:TQ, 0:128] = jnp.where(lane < 64, do[:, 0:128], zero)
    dos[TQ : 2 * TQ, 0:128] = jnp.where(lane < 64, zero, do[:, 0:128])
    dos[2 * TQ :, 0:128] = zero
    dos[0 : 2 * TQ, 128:256] = jnp.zeros((2 * TQ, 128), BF)
    dos[2 * TQ :, 128:192] = do[:, 128:192]
    dos[2 * TQ :, 192:256] = jnp.zeros((TQ, 64), BF)
    if first:
        both = do.astype(F32).T * ot_ref[0]
        delta = jnp.concatenate(
            [jnp.sum(both[h * HD : (h + 1) * HD], axis=0, keepdims=True) for h in range(3)], axis=1
        )
        delta_ref[0] = delta
    else:
        delta = ot_ref[0]
    lse = lse_ref[0]
    acc[...] = jnp.zeros_like(acc)

    def slot_loop(s, _):
        def key_loop(t, _):
            tile = s * per + t
            keys = pl.ds(pl.multiple_of(tile * TK, TK), TK)
            st = mm(kaug[keys, :], qs[...], NT)
            p = jnp.exp(st - lse)
            dp = mm(kv[keys, 0:256], dos[...], NT)
            ds = (p * (dp - delta)).astype(BF)
            dv_s[keys, :] += mm(p.astype(BF), dos[...])
            dk_s[keys, :] += mm(ds, qs[...])
            for h in range(3):
                cols = slice(h * TQ, (h + 1) * TQ)
                acc[(h + 1) * HD : (h + 2) * HD, :] += mm(kt[tile, h * HD : (h + 1) * HD, :], ds[:, cols])
            return 0

        return lax.fori_loop(tlo[i, slot0 + s], thi[i, slot0 + s], key_loop, 0)

    lax.fori_loop(0, slots, slot_loop, 0)
    dq_ref[...] = (acc[...] * HD ** (-0.5)).T.astype(BF)

    @pl.when(i == pl.num_programs(0) - 1)
    def _():
        def finish_tile(k, _):
            at = pl.ds(pl.multiple_of(k * TK, TK), TK)
            dkv_ref[at, 0:128] = dv_s[at, 0:128].astype(BF)
            dkv_ref[at, 128:256] = jnp.where(lane_ids(TK) < 64, dv_s[at, 128:256], dk_s[at, 0:128]).astype(BF)
            dkv_ref[at, 256:384] = dk_s[at, 128:256].astype(BF)
            return 0

        lax.fori_loop(0, keys_all // TK, finish_tile, 0)


def attend_back(tables, q, do, ot, lse, source, slot0, first=False, name="attend_back", size=14_000_000_000):
    tlo, thi, qfirst, lo, hi, slo, shi = tables
    tiles = q.shape[0] // TQ
    keys = source.shape[0]
    sd = jax.ShapeDtypeStruct
    outs = (sd(q.shape, BF), sd(source.shape, BF))
    out_specs = (rows_spec(q.shape), whole(source.shape))
    if first:
        outs += (sd(lse.shape, F32),)
        out_specs += (tile_spec(lse.shape),)
    return pl.pallas_call(
        functools.partial(attend_back_kernel, slot0=slot0, first=first),
        out_shape=outs,
        grid_spec=pltpu.PrefetchScalarGridSpec(
            num_scalar_prefetch=3,
            grid=(tiles,),
            in_specs=[rows_spec(q.shape), rows_spec(do.shape), tile_spec(ot.shape), tile_spec(lse.shape)]
            + [whole(x.shape) for x in (source, lo, hi, slo, shi)],
            out_specs=out_specs,
            scratch_shapes=[
                pltpu.VMEM((keys, 256), BF),
                pltpu.VMEM((keys // TK, 3 * HD, TK), BF),
                pltpu.VMEM((3 * TQ, 256), BF),
                pltpu.VMEM((3 * TQ, 256), BF),
                pltpu.VMEM((256, TQ), F32),
                pltpu.VMEM((keys, 256), F32),
                pltpu.VMEM((keys, 256), F32),
            ],
        ),
        compiler_params=pltpu.CompilerParams(vmem_limit_bytes=GRANT),
        cost_estimate=cost(size, size // 1000, size // 3000),
        name=name,
    )(tlo, thi, qfirst, q, do, ot, lse, source, lo, hi, slo, shi)


def project_kernel(
    who, x0, x1, x2, x3_top, x3_bottom, w_mine, w_other, bias_ref, chosen, q_ref, kv_ref, up_ref, down_ref, w_ref
):
    tall = w_mine.shape[0]
    rows = x0.shape[0]
    w_ref[pl.ds(pl.multiple_of(who[0] * tall, tall), tall), :] = w_mine[...]
    w_ref[pl.ds(pl.multiple_of((1 - who[0]) * tall, tall), tall), :] = w_other[...]
    for d, x in enumerate((x0, x1, x2, (x3_top, x3_bottom))):
        if d < 3:
            value = mm(x[...], w_ref[...]) + bias_ref[...]
        else:
            value = jnp.concatenate([mm(x[0][...], w_ref[...]), mm(x[1][...], w_ref[...])], axis=0) + bias_ref[...]
        at = slice(d * rows, (d + 1) * rows)
        q_ref[at, :] = (value[:, :256].astype(BF).astype(F32) * HD ** (-0.5)).astype(BF)
        kv = mm(chosen[d], value[:, 256:].astype(BF)).astype(BF)
        kv_ref[at, :] = kv
        inner = slice((d % 2) * rows, (d % 2 + 1) * rows)

        @pl.when(who[2] == d // 2)
        def _(inner=inner, kv=kv):
            down_ref[inner, :] = kv

        @pl.when(who[2] != d // 2)
        def _(inner=inner, kv=kv):
            up_ref[inner, :] = kv


def project(who, xs, w_mine, w_other, bias, chosen):
    sd = jax.ShapeDtypeStruct
    rows, width = xs[0].shape
    cols = w_mine.shape[1]
    ins = (*xs, w_mine, w_other, bias, chosen)
    outs = (
        sd((4 * rows, 256), BF), sd((4 * rows, cols - 256), BF), sd((2 * rows, cols - 256), BF),
        sd((2 * rows, cols - 256), BF), sd((width, cols), BF),
    )
    return pl.pallas_call(
        project_kernel,
        out_shape=outs,
        grid_spec=pltpu.PrefetchScalarGridSpec(
            num_scalar_prefetch=1,
            grid=(1,),
            in_specs=[whole(a.shape) for a in ins],
            out_specs=tuple(whole(a.shape) for a in outs),
        ),
        compiler_params=pltpu.CompilerParams(vmem_limit_bytes=GRANT),
        cost_estimate=cost(3_000_000_000, 12_000_000),
        name="project",
    )(who, *ins)


def row_mean(v):
    return jnp.sum(v, axis=-1, keepdims=True) * (1.0 / v.shape[-1])

def dense_kernel(
    who, o_ref, wo_a, wo_b, win_hbm, wback_hbm, x_ref, teacher_ref, cot_ref, keep_ref, vec_ref,
    out_ref, dres_ref, dparts_ref, act_ref, dbr_ref, dpre_ref, hid_ref, dproj_ref, sums_ref,
    wo, win, wback, xh, inv, hidden, gp, acc, sems, *, FB
):
    rows, width = x_ref.shape
    groups = o_ref.shape[0] // rows
    part = width // groups
    units = win.shape[1]
    wo_loads, win_loads, wback_loads = [], [], []
    for i in range(2):
        side = who[0] if i == 0 else 1 - who[0]
        for e in range(groups // 2):
            to = pl.multiple_of(((side * (groups // 2) + e) ^ who[1]) * part, part)
            wo_loads.append(
                pltpu.make_async_copy((wo_a, wo_b)[i].at[pl.ds(e * part, part)], wo.at[pl.ds(to, part)], sems.at[2 * i + e])
            )
    for j, (source, target, held) in enumerate(((win_hbm, win, win_loads), (wback_hbm, wback, wback_loads))):
        held.append(pltpu.make_async_copy(source, target, sems.at[4 + j]))
    for load in wo_loads + win_loads + wback_loads:
        load.start()
    b_out, b_in, b_back = vec_ref[0:1, 0:width], vec_ref[1:2, :], vec_ref[2:3, 0:width]
    gain1, shift1, gain2, shift2 = (vec_ref[i : i + 1, 0:width] for i in range(3, 7))
    for load in wo_loads:
        load.wait()
    total = x_ref[...].astype(F32) + b_out
    for i in range(groups):
        total += mm(o_ref[i * rows : (i + 1) * rows, :], wo[i * part : (i + 1) * part, :])
    center = total - row_mean(total)
    scale = lax.rsqrt(row_mean(center * center) + 1e-12)
    inv[...] = scale
    unit = center * scale
    xh[...] = unit
    hid = unit * gain1 + shift1
    hidden[...] = hid
    hid_ref[...] = hid.astype(BF)
    acc[...] = jnp.zeros_like(acc)
    for load in win_loads + wback_loads:
        load.wait()

    def up(n, _):
        cols = pl.ds(pl.multiple_of(n * FB, FB), FB)
        pre = mm(hid_ref[...], win[:, cols]) + vec_ref[1:2, cols]
        cdf = 0.5 + 0.5 * lax.erf(pre * 0.7071067811865476)
        act = (pre * cdf).astype(BF)
        act_ref[:, cols] = act
        gp[:, cols] = cdf + pre * (jnp.exp(pre * pre * -0.5) * 0.3989422804014327)
        acc[...] += mm(act, wback[cols, :])
        return 0

    lax.fori_loop(0, units // FB, up, 0, unroll=True)
    total = hidden[...] + acc[...] + b_back
    center = total - row_mean(total)
    scale = lax.rsqrt(row_mean(center * center) + 1e-12)
    unit = center * scale
    result = unit * gain2 + shift2
    out_ref[...] = result.astype(BF)
    grad = cot_ref[...].astype(F32) + keep_ref[...] * (result - teacher_ref[...].astype(F32))
    def put(row, value):
        sums_ref[row : row + 1, 0 : value.shape[1]] = value
    put(5, jnp.sum(grad * unit, axis=0, keepdims=True))
    put(6, jnp.sum(grad, axis=0, keepdims=True))
    grad = grad * gain2
    back = scale * (grad - row_mean(grad) - unit * row_mean(grad * unit))
    acc[...] = back
    low = back.astype(BF)
    dbr_ref[...] = low
    put(2, jnp.sum(low.astype(F32), axis=0, keepdims=True))

    def down(n, _):
        cols = pl.ds(pl.multiple_of(n * FB, FB), FB)
        dpre = (mm(dbr_ref[...], wback[cols, :], NT) * gp[:, cols]).astype(BF)
        dpre_ref[:, cols] = dpre
        sums_ref[1:2, cols] = jnp.sum(dpre.astype(F32), axis=0, keepdims=True)
        acc[...] += mm(dpre, win[:, cols], NT)
        return 0

    lax.fori_loop(0, units // FB, down, 0, unroll=True)
    grad = acc[...]
    unit = xh[...]
    put(3, jnp.sum(grad * unit, axis=0, keepdims=True))
    put(4, jnp.sum(grad, axis=0, keepdims=True))
    grad = grad * gain1
    back = inv[...] * (grad - row_mean(grad) - unit * row_mean(grad * unit))
    dres_ref[...] = back
    low = back.astype(BF)
    dproj_ref[...] = low
    put(0, jnp.sum(low.astype(F32), axis=0, keepdims=True))
    for i in range(groups):
        dparts_ref[i * rows : (i + 1) * rows, :] = mm(low, wo[i * part : (i + 1) * part, :], NT).astype(BF)


def dense(who, o, weights, x, teacher, cot, keep, vec):
    rows, width = x.shape
    units = vec.shape[1]
    sd = jax.ShapeDtypeStruct
    outs = (
        sd((rows, width), BF), sd((rows, width), F32), sd(o.shape, BF), sd((rows, units), BF), sd((rows, width), BF),
        sd((rows, units), BF), sd((rows, width), BF), sd((rows, width), BF), sd((8, units), F32),
    )
    ins = (o, *weights, x, teacher, cot, keep, vec)
    stay = pl.BlockSpec(memory_space=pl.ANY)
    return pl.pallas_call(
        functools.partial(dense_kernel, FB=FFB),
        out_shape=outs,
        grid_spec=pltpu.PrefetchScalarGridSpec(
            num_scalar_prefetch=1,
            grid=(1,),
            in_specs=[whole(o.shape)] + [stay] * 4 + [whole(a.shape) for a in ins[5:]],
            out_specs=tuple(whole(a.shape) for a in outs),
            scratch_shapes=[
                pltpu.VMEM((width, width), BF), pltpu.VMEM((width, units), BF), pltpu.VMEM((units, width), BF),
                pltpu.VMEM((rows, width), F32), pltpu.VMEM((rows, 1), F32), pltpu.VMEM((rows, width), F32),
                pltpu.VMEM((rows, units), F32), pltpu.VMEM((rows, width), F32), pltpu.SemaphoreType.DMA((8,)),
            ],
        ),
        compiler_params=pltpu.CompilerParams(vmem_limit_bytes=GRANT),
        cost_estimate=cost(12_000_000_000, 30_000_000, 4_000_000),
        name="dense",
    )(who, *ins)


def finish_kernel(who, dq0, dq1, dq2, dq3, own_ref, pair_ref, left_ref, right_ref, turn_ref, all_ref, sums_ref):
    groups, rows = turn_ref.shape[:2]
    sums_ref[...] = jnp.zeros_like(sums_ref)
    for d in range(groups):
        at = pl.ds(d * rows, rows)
        inner = pl.ds((d % (groups // 2)) * rows, rows)
        first = (d < groups // 2) == (who[2] == 0)
        back = own_ref[at, :].astype(F32) + pair_ref[at, :].astype(F32)
        back += jnp.where(first, left_ref[inner, :], right_ref[inner, :]).astype(F32)
        tok = mm(turn_ref[d], back.astype(BF)).astype(BF)
        dq = sum(ref[at, :].astype(F32) for ref in (dq0, dq1, dq2, dq3)).astype(BF)
        all_ref[at, 0:256] = dq
        all_ref[at, 256:640] = tok
        sums_ref[0:1, 0:256] += jnp.sum(dq.astype(F32), axis=0, keepdims=True)
        sums_ref[0:1, 256:640] += jnp.sum(tok.astype(F32), axis=0, keepdims=True)


def finish(who, dqs, own, pair, left, right, turn):
    sd = jax.ShapeDtypeStruct
    cols = dqs[0].shape[1] + own.shape[1]
    ins = (*dqs, own, pair, left, right, turn)
    outs = (sd((dqs[0].shape[0], cols), BF), sd((8, cols), F32))
    return pl.pallas_call(
        finish_kernel,
        out_shape=outs,
        grid_spec=pltpu.PrefetchScalarGridSpec(
            num_scalar_prefetch=1,
            grid=(1,),
            in_specs=[whole(a.shape) for a in ins],
            out_specs=tuple(whole(a.shape) for a in outs),
        ),
        compiler_params=pltpu.CompilerParams(vmem_limit_bytes=GRANT),
        cost_estimate=cost(1_000_000_000, 9_000_000),
        name="finish",
    )(who, *ins)


def spread_kernel(all_ref, w_ref, own_ref, gx_ref, gy_ref, left_ref, right_ref):
    rows, width = own_ref.shape
    cut = width // 2
    parts = [mm(all_ref[d * rows : (d + 1) * rows, :], w_ref[...], NT).astype(BF) for d in range(4)]
    own_ref[...] = parts[0]
    gx_ref[0:rows, :] = parts[1][:, :cut]
    right_ref[...] = parts[1][:, cut:]
    left_ref[...] = parts[2][:, :cut]
    gy_ref[0:rows, :] = parts[2][:, cut:]
    gx_ref[rows:, :] = parts[3][:, :cut]
    gy_ref[rows:, :] = parts[3][:, cut:]


def spread_x(d_all, w_heads):
    rows, width = d_all.shape[0] // 4, w_heads.shape[0]
    shapes = ((rows, width), (2 * rows, width // 2), (2 * rows, width // 2), (rows, width // 2), (rows, width // 2))
    return pl.pallas_call(
        spread_kernel,
        out_shape=tuple(jax.ShapeDtypeStruct(s, BF) for s in shapes),
        grid=(1,),
        in_specs=[whole(d_all.shape), whole(w_heads.shape)],
        out_specs=tuple(whole(s) for s in shapes),
        compiler_params=pltpu.CompilerParams(vmem_limit_bytes=GRANT),
        cost_estimate=cost(2_000_000_000, 7_000_000),
        name="spread_x",
    )(d_all, w_heads)


def first_kernel(who, back_a, back_b, in_a, in_b, out_a, out_b, am, ao, bm, bo, held):
    width = back_a.shape[1]
    tall = in_a.shape[0]
    for k in range(4):
        at = slice(k * tall, (k + 1) * tall)
        value = back_a[at, :].astype(F32) + back_b[at, :].astype(F32)
        held[0:tall, k * width : (k + 1) * width] = value.astype(BF)
    held[tall : 2 * tall, :] = (in_a[...].astype(F32) + in_b[...].astype(F32)).astype(BF)
    held[2 * tall :, :] = (out_a[...].astype(F32) + out_b[...].astype(F32)).astype(BF)
    part_out(who, held, am, ao, bm, bo, (lax.rem(who[1], 2), who[1] // 2))


def part_out(who, held, am, ao, bm, bo, sides):
    part = am.shape[0]
    for mine, other, side, base in ((am, ao, sides[0], 0), (bm, bo, sides[1], 2 * part)):
        mine[...] = held[pl.ds(pl.multiple_of(base + side * part, 16), part), :]
        other[...] = held[pl.ds(pl.multiple_of(base + (1 - side) * part, 16), part), :]


def second_kernel(who, a_mine, a_got, b_mine, b_got, am, ao, bm, bo, held):
    part = a_mine.shape[0]
    held[0:part, :] = (a_mine[...].astype(F32) + a_got[...].astype(F32)).astype(BF)
    held[part:, :] = (b_mine[...].astype(F32) + b_got[...].astype(F32)).astype(BF)
    part_out(who, held, am, ao, bm, bo, (who[1] // 2, lax.rem(who[1], 2)))


def third_kernel(who, a_mine, a_got, b_mine, b_got, both):
    del who
    part = a_mine.shape[0]
    both[0:part, :] = (a_mine[...].astype(F32) + a_got[...].astype(F32)).astype(BF)
    both[part:, :] = (b_mine[...].astype(F32) + b_got[...].astype(F32)).astype(BF)


def join_kernel(who, a, b, c, d, back_ref, in_ref, out_ref, vec_ref, held):
    s1, s2 = lax.rem(who[1], 2), who[1] // 2
    part = a.shape[0] // 2
    for at, ref in enumerate((a, b, c, d)):
        color, i = at // 2, at % 2
        for j in range(2):
            spot = (s1 ^ i) * 2 + (s2 ^ j) if color == 0 else 4 + (s2 ^ i) * 2 + (s1 ^ j)
            held[pl.ds(pl.multiple_of(spot * part, 16), part), :] = ref[j * part : (j + 1) * part, :]
    tall, width = out_ref.shape
    for k in range(4):
        back_ref[k * tall : (k + 1) * tall, :] = held[0:tall, k * width : (k + 1) * width].astype(F32)
    in_ref[...] = held[tall : 2 * tall, :].astype(F32)
    for k in range(3):
        out_ref[k * 128 : (k + 1) * 128, :] = held[2 * tall :, k * width : (k + 1) * width].astype(F32)
    vec_ref[...] = held[2 * tall : 2 * tall + 16, 3 * width :].astype(F32)


def small_call(kernel, who, pieces, outs, scratch, name):
    return pl.pallas_call(
        kernel,
        out_shape=tuple(jax.ShapeDtypeStruct(*s) for s in outs),
        grid_spec=pltpu.PrefetchScalarGridSpec(
            num_scalar_prefetch=1,
            grid=(1,),
            in_specs=[whole(a.shape) for a in pieces],
            out_specs=tuple(whole(s[0]) for s in outs),
            scratch_shapes=scratch,
        ),
        compiler_params=pltpu.CompilerParams(vmem_limit_bytes=GRANT),
        cost_estimate=cost(1_000_000, 9_000_000),
        name=name,
    )(who, *pieces)


def heads_kernel(who, h0, h1, h2, h3, q_ref, k_ref, v_ref, bias_ref, held):
    tall = q_ref.shape[0]
    for d, ref in enumerate((h0, h1, h2, h3)):
        held[who[1] ^ d] = ref[...]
    for a in range(4):
        cols = slice(a * 192, (a + 1) * 192)
        q_ref[:, cols] = held[a, 0:tall, 64:256].astype(F32)
        v_ref[:, cols] = held[a, 0:tall, 256:448].astype(F32)
        k_ref[:, cols] = held[a, 0:tall, 448:640].astype(F32)
        line = held[a, 0:16, 0:64].astype(F32)
        for k in range(3):
            spot = slice(a * 192 + k * 64, a * 192 + (k + 1) * 64)
            bias_ref[0:1, spot] = line[k : k + 1]
            bias_ref[8:9, spot] = line[k + 3 : k + 4]


def heads_out(who, pieces):
    sd = jax.ShapeDtypeStruct
    outs = (sd((384, 768), F32),) * 3 + (sd((16, 768), F32),)
    return pl.pallas_call(
        heads_kernel,
        out_shape=outs,
        grid_spec=pltpu.PrefetchScalarGridSpec(
            num_scalar_prefetch=1,
            grid=(1,),
            in_specs=[whole(a.shape) for a in pieces],
            out_specs=tuple(whole(a.shape) for a in outs),
            scratch_shapes=[pltpu.VMEM((4, *pieces[0].shape), BF)],
        ),
        compiler_params=pltpu.CompilerParams(vmem_limit_bytes=GRANT),
        cost_estimate=cost(1_000_000, 6_000_000),
        name="heads_out",
    )(who, *pieces)


def swap(block, axis="fsdp"):
    return lax.ppermute(block, axis, [(0, 1), (1, 0)])


def shifted(block, axis, distance):
    devices = range(lax.axis_size(axis))
    route = [(i - distance, i) for i in devices if i - distance in devices]
    return lax.ppermute(block, axis, route)


def flip(block, bit, axis="uly"):
    return lax.ppermute(block, axis, [(i, i ^ bit) for i in range(lax.axis_size(axis))])


def exchange(rows, axis):
    return lax.all_to_all(rows, axis, split_axis=0, concat_axis=0, tiled=True)


def spread_rows(rows, axis):
    count = lax.axis_size(axis)
    return exchange(jnp.broadcast_to(rows[None], (count, *rows.shape)).reshape(-1, rows.shape[1]), axis)


def sum_parts(rows, count):
    got = rows.reshape(count, -1, rows.shape[1])
    return sum(got[i].astype(F32) for i in range(count)).astype(BF)


def sum_scatter(rows, axis):
    return sum_parts(exchange(rows, axis), lax.axis_size(axis))


def add(left, right):
    return (left.astype(F32) + right.astype(F32)).astype(BF)


def line_step(held, bit):
    return flip(held, bit, "ctx")


def line_join(held, got, bit):
    low = (lax.axis_index("ctx") & bit) == 0
    return jnp.stack([jnp.where(low, held, got), jnp.where(low, got, held)], axis=1).reshape(-1, *held.shape[1:])


def line_rest(held, bit):
    while bit > 0:
        held = line_join(held, line_step(held, bit), bit)
        bit //= 2
    return held.reshape(-1, held.shape[2])


def tie(*values):
    return lax.optimization_barrier(values)


def on_device(
    tokens, teacher, cotangent, valid, teacher_ok, doc_starts, w_query, w_key, w_value, w_out, w_in, w_back,
    bias_query, bias_value, bias_out, bias_in, bias_back, norm1_gain, norm1_bias, norm2_gain, norm2_bias,
):
    groups = lax.axis_size("uly")
    spans = lax.axis_size("ctx")
    rows, width = tokens.shape
    block = rows * groups * 2
    stream = block * spans
    ctx_index = lax.axis_index("ctx")
    uly = lax.axis_index("uly")
    half = lax.axis_index("fsdp")
    head_cols = width // groups
    shard = w_query.shape[0]
    middle = groups * rows // 2
    upper = uly // 2

    small = (bias_query, bias_value, bias_out, bias_in, bias_back, norm1_gain, norm1_bias, norm2_gain, norm2_bias)
    valid_one = valid[None, :]
    valid_own = jnp.concatenate([valid_one, flip(valid_one, 1), flip(valid_one, 2), flip(valid_one, 3)], axis=0)
    x_own, valid_own, *small = tie(tokens, valid_own, *small)
    x_x, x_y = flip(x_own, 1), flip(x_own, 2)
    valid_pair = swap(valid_own)
    valid_both = jnp.stack([valid_own, valid_pair]).reshape(2, 2, 2, rows)
    valid_high = lax.dynamic_index_in_dim(valid_both, 1 - upper, 1, keepdims=False)
    valid_low = lax.dynamic_index_in_dim(valid_both, upper, 1, keepdims=False)
    halo = (shifted(valid_high, "ctx", 1), shifted(valid_low, "ctx", -1))
    block_valid = jnp.concatenate([valid_own, valid_pair, halo[0][0], halo[1][0], halo[0][1], halo[1][1]], axis=0)
    count = jnp.full((8, 128), jnp.sum(valid_both), jnp.int32)
    bit = 1
    while bit < spans:
        count = count + flip(count, bit, "ctx")
        bit *= 2
    count = count[0, 0].astype(F32)

    start_col = uly * head_cols
    cut = [lax.dynamic_slice_in_dim(w, start_col, head_cols, 1) for w in (w_query, w_value, w_key)]
    w_mine = jnp.concatenate([jnp.zeros((shard, 256 - head_cols), BF), *cut], axis=1)
    w_other = swap(w_mine)
    who = jnp.stack([half, uly, upper])
    packed = jnp.concatenate(small)
    packed_pair = swap(packed)
    first, second = jnp.where(half == 0, packed, packed_pair), jnp.where(half == 0, packed_pair, packed)
    vectors = []
    at = 0
    for p in small:
        n = p.shape[0]
        vectors.append(jnp.concatenate([first[at : at + n], second[at : at + n]]).astype(F32))
        at += n
    bq_all, bv_all = vectors[:2]
    vec = jnp.stack([jnp.pad(v, (0, w_in.shape[1] - v.shape[0])) for v in vectors[2:]] + [jnp.zeros((w_in.shape[1],), F32)])
    bias_heads = jnp.concatenate(
        [
            jnp.zeros((256 - head_cols,), F32),
            lax.dynamic_slice_in_dim(bq_all, start_col, head_cols, 0),
            lax.dynamic_slice_in_dim(bv_all, start_col, head_cols, 0),
            jnp.zeros((head_cols,), F32),
        ]
    )

    place = jnp.arange(groups, dtype=jnp.int32)
    two = jnp.arange(2, dtype=jnp.int32)
    in_plane = place ^ uly
    halo_group = jnp.concatenate([uly ^ (2 * (1 - upper) + two), uly ^ (2 * upper + two)])
    halo_plane = ctx_index + jnp.where(place < 2, -1, 1)
    plane_of = jnp.concatenate([jnp.full((2 * groups,), 1, jnp.int32) * ctx_index, halo_plane, halo_plane])
    group_of = jnp.concatenate([in_plane, in_plane, halo_group, halo_group])
    mine = jnp.full((groups,), 1, jnp.int32) * half
    core_of = jnp.concatenate([mine, 1 - mine, mine, 1 - mine])
    block_id = plane_of * (2 * groups) + group_of * 2 + core_of
    spot = block_id[:, None] * rows + jnp.arange(rows, dtype=jnp.int32)[None, :]
    edges = jnp.concatenate([doc_starts, jnp.full((DOCS + 1,), stream, jnp.int32)])
    window_first = jnp.maximum(ctx_index * block - block // 2, 0)
    first_doc = jnp.sum((doc_starts <= window_first).astype(jnp.int32)) - 1
    near = lax.dynamic_slice_in_dim(edges, first_doc, DOCS + 1, 0)
    tiles = groups * rows // TQ
    per = rows // TQ
    tile_ids = jnp.arange(tiles, dtype=jnp.int32)
    qfirst = ctx_index * block + (((tile_ids // per) ^ uly) * 2 + half) * rows + lax.rem(tile_ids, per) * TQ
    q_lo = jnp.max(jnp.where(near[None, :] <= qfirst[:, None], near[None, :], 0), axis=1)
    q_hi = jnp.min(jnp.where(near[None, :] <= qfirst[:, None] + TQ - 1, stream, near[None, :]), axis=1)
    limits = jnp.concatenate([near, q_lo, q_hi])
    counted = jnp.sum(block_valid[:, None, :] * (spot[:, None, :] < limits[None, :, None]), axis=-1)
    bounds = counted[:, : DOCS + 1]
    cnt_lo = counted[:, DOCS + 1 : DOCS + 1 + tiles].T
    cnt_hi = counted[:, DOCS + 1 + tiles :].T
    pad64 = jnp.zeros((bounds.shape[0], 128 - DOCS), jnp.int32)
    lo_tab = jnp.concatenate([bounds[:, :DOCS], pad64], axis=1)
    hi_tab = jnp.concatenate([bounds[:, 1:], pad64], axis=1)
    slo_tab = jnp.concatenate([near[:DOCS], pad64[0]])[None, :]
    shi_tab = jnp.concatenate([near[1:], pad64[0]])[None, :]
    some = cnt_hi > cnt_lo
    tlo = jnp.where(some, cnt_lo // TK, 0)
    thi = jnp.where(some, (cnt_hi + TK - 1) // TK, 0)
    tables = (tlo, thi, qfirst, lo_tab, hi_tab, slo_tab, shi_tab)
    before = mm(valid_own.astype(BF), (jnp.arange(rows)[:, None] < jnp.arange(rows)[None, :]).astype(BF)).astype(jnp.int32)
    goes_to = jnp.where(valid_own > 0, before, rows)
    chosen = (goes_to[:, None, :] == jnp.arange(rows, dtype=jnp.int32)[None, :, None]).astype(BF)
    loss_scale = jnp.float32(stream) / count
    keep = (loss_scale * (valid * teacher_ok).astype(F32))[:, None]
    turned = (goes_to[:, :, None] == jnp.arange(rows, dtype=jnp.int32)[None, None, :]).astype(BF)

    x_x, x_y, w_other, chosen, bias_heads, *tables = tie(x_x, x_y, w_other, chosen, bias_heads, *tables)
    x_top, x_bottom = flip(x_y[: rows // 2], 1), flip(x_x[rows // 2 :], 2)

    q_low, kv_own, kv_up, kv_down, w_heads = project(
        who, (tokens, x_x, x_y, x_top, x_bottom), w_mine, w_other, bias_heads[None, :], chosen
    )
    kv_from_left, kv_from_right = shifted(kv_up, "ctx", 1), shifted(kv_down, "ctx", -1)
    w_out, w_in, w_back, kv_own = tie(w_out, w_in, w_back, kv_own)
    wo_pair, win_pair, wback_pair = swap(w_out), swap(w_in), swap(w_back)
    kv_pair = swap(kv_own)
    state = attend(tables, q_low, (kv_own,), 0)
    kv_halo = jnp.concatenate([kv_from_left, kv_from_right], axis=0)
    kv_halo, kv_pair, *state = tie(kv_halo, kv_pair, *state)
    kv_halo_pair = swap(kv_halo)
    state = attend(tables, q_low, (kv_pair,), groups, state)
    o_heads, o_turned, lse = attend(tables, q_low, (kv_halo, kv_halo_pair), 2 * groups, state, last=True)
    o_rel = o_heads.reshape(groups, rows, head_cols)
    o_rest = [flip(o_rel[d], d) for d in range(1, groups)]
    win_pair, wback_pair, o_heads, x_x, x_y, x_top, x_bottom = tie(
        win_pair, wback_pair, o_heads, x_x, x_y, x_top, x_bottom
    )
    x_all = jnp.concatenate([tokens, x_x, x_y, x_top, x_bottom], axis=0)

    def both(mine, other):
        return jnp.concatenate([jnp.where(half == 0, mine, other), jnp.where(half == 0, other, mine)], axis=0)

    win_all, wback_all, x_all, *o_rest = tie(both(w_in, win_pair), both(w_back, wback_pair), x_all, *o_rest)
    o_all = jnp.concatenate([o_rel[0], *o_rest], axis=0)

    out, d_resid1, d_parts, act, d_branch, d_pre, hidden_low, d_proj, sums = dense(
        who, o_all, (w_out, wo_pair, win_all, wback_all), tokens, teacher, cotangent, keep, vec
    )
    d_rel = d_parts.reshape(groups, rows, head_cols)
    tall = w_back.shape[0]
    vector_rows = jnp.concatenate(
        [sums[i, :width].reshape(2, -1) for i in (0, 2, 3, 4, 5, 6)] + [sums[1].reshape(2, -1)], axis=1
    ).reshape(2, -1, width)
    vector_rows = jnp.pad(vector_rows, ((0, 0), (0, 128 - vector_rows.shape[1]), (0, 0))).astype(BF)
    o_rows = o_all.reshape(groups, rows, head_cols)

    def back_part(side):
        return mm(lax.dynamic_slice_in_dim(act, side * tall, tall, 1), d_branch, TN).astype(BF)

    def in_part(side):
        return mm(lax.dynamic_slice_in_dim(hidden_low, side * shard, shard, 1), d_pre, TN).astype(BF)

    def out_part(side):
        both = [
            mm(lax.dynamic_index_in_dim(o_rows, (2 * side + e) ^ uly, 0, keepdims=False), d_proj, TN).astype(BF)
            for e in range(2)
        ]
        stack = jnp.concatenate([*both, lax.dynamic_index_in_dim(vector_rows, side, 0, keepdims=False)], axis=0)
        return jnp.concatenate([stack[i * 128 : (i + 1) * 128] for i in range(4)], axis=1)

    d_rest = [flip(d_rel[d], d) for d in range(1, groups)]
    back_got = swap(back_part(1 - half))
    in_got, out_got = swap(in_part(1 - half)), swap(out_part(1 - half))
    back_mine, in_mine, out_mine = back_part(half), in_part(half), out_part(half)
    back_got, in_got, out_got, back_mine, in_mine, out_mine, *d_rest = tie(
        back_got, in_got, out_got, back_mine, in_mine, out_mine, *d_rest
    )
    wide = w_in.shape[1]
    total = 2 * shard + 128
    am, ao, bm, bo = small_call(
        first_kernel, who, (back_mine, back_got, in_mine, in_got, out_mine, out_got),
        (((total // 4, wide), BF),) * 4, [pltpu.VMEM((total, wide), BF)], "first_stage",
    )
    d_heads = jnp.concatenate([d_rel[0], *d_rest], axis=0)
    d_heads, am, ao, bm, bo = tie(d_heads, am, ao, bm, bo)

    ag, bg = flip(ao, 1), flip(bo, 2)
    args = (tables, q_low, d_heads, o_turned, lse)
    dq0, dkv_halo_pair, delta = attend_back(*args, kv_halo_pair, 3 * groups, first=True, name="back_halo_pair")
    dkv_halo_pair, delta = tie(dkv_halo_pair, delta)
    args = (tables, q_low, d_heads, delta, lse)
    got_lo, got_hi = swap(dkv_halo_pair[:middle]), swap(dkv_halo_pair[middle:])
    dq1, dkv_halo = attend_back(*args, kv_halo, 2 * groups, name="back_halo", size=1_000_000)
    dkv_halo, got_lo, got_hi, ag, bg = tie(dkv_halo, got_lo, got_hi, ag, bg)

    halo_lo, halo_hi = add(dkv_halo[:middle], got_lo), add(dkv_halo[middle:], got_hi)
    am, ao, bm, bo = small_call(
        second_kernel, who, (am, ag, bm, bg), (((total // 8, wide), BF),) * 4,
        [pltpu.VMEM((total // 2, wide), BF)], "second_stage",
    )
    halo_lo, halo_hi, delta, am, ao, bm, bo = tie(halo_lo, halo_hi, delta, am, ao, bm, bo)
    args = (tables, q_low, d_heads, delta, lse)
    ag, bg = flip(ao, 2), flip(bo, 1)
    from_left, from_right = shifted(halo_hi, "ctx", 1), shifted(halo_lo, "ctx", -1)
    dq2, dkv_pair = attend_back(*args, kv_pair, groups, name="back_pair")
    dkv_pair, ag, bg, from_left, from_right = tie(dkv_pair, ag, bg, from_left, from_right)

    (line,) = small_call(third_kernel, who, (am, ag, bm, bg), (((total // 4, wide), BF),), [], "third_stage")
    line, dkv_pair, delta = tie(line, dkv_pair, delta)
    args = (tables, q_low, d_heads, delta, lse)
    line = exchange(line, "ctx")
    pair_got = swap(dkv_pair)
    dq3, dkv_own = attend_back(*args, kv_own, 0, name="back_own")
    dkv_own, line, pair_got = tie(dkv_own, line, pair_got)
    line = sum_parts(line, spans)
    line, dkv_own = tie(line, dkv_own)
    line = spread_rows(line, "ctx")

    d_all, d_sums = finish(who, (dq0, dq1, dq2, dq3), dkv_own, pair_got, from_left, from_right, turned)
    corner = d_sums[0, 64:].reshape(9, 64)

    def heads_part(side):
        grad = mm(lax.dynamic_slice_in_dim(x_all, side * shard, shard, 1), d_all, TN)
        return lax.dynamic_update_slice(grad, corner, (0, 0)).astype(BF)

    heads_other = heads_part(1 - half)
    heads_got = swap(heads_other)
    heads_mine = heads_part(half)
    dx_own, give_x, give_y, left_next, right_next = spread_x(d_all, w_heads)
    give_x, give_y = flip(give_x, 1), flip(give_y, 2)
    heads_sum = add(heads_mine, heads_got)
    line, heads_sum = tie(line, heads_sum)
    a_near, b_near = line[: total // 8], line[total // 8 :]
    a_near = jnp.concatenate([a_near, flip(a_near, 2)], axis=0)
    b_near = jnp.concatenate([b_near, flip(b_near, 1)], axis=0)
    a_far, b_far = flip(a_near, 1), flip(b_near, 2)
    left_next = flip(add(left_next, give_x[rows:]), 2)
    right_next = flip(add(right_next, give_y[rows:]), 1)
    heads_sum = spread_rows(sum_scatter(heads_sum, "ctx"), "ctx")
    heads_all = [heads_sum] + [flip(heads_sum, d) for d in range(1, groups)]
    grad_in = d_resid1 + dx_own.astype(F32)
    grad_in = grad_in + jnp.concatenate([give_x[:rows].astype(F32), give_y[:rows].astype(F32)], axis=1)
    grad_in = grad_in + jnp.concatenate([left_next.astype(F32), right_next.astype(F32)], axis=1)
    g_back, g_in, g_out, g_vec = small_call(
        join_kernel, who, (a_near, a_far, b_near, b_far),
        ((w_back.shape, F32), (w_in.shape, F32), (w_out.shape, F32), ((16, width), F32)),
        [pltpu.VMEM((total, wide), BF)], "join",
    )
    g_query, g_key, g_value, g_bias = heads_out(who, heads_all)
    g_bias_q = lax.dynamic_slice_in_dim(g_bias[0], half * shard, shard, 0)
    g_bias_v = lax.dynamic_slice_in_dim(g_bias[8], half * shard, shard, 0)
    flat = g_vec.reshape(-1)
    g_bo, g_bb, g_g1, g_s1, g_g2, g_s2 = [flat[i * shard : (i + 1) * shard] for i in range(6)]
    g_bin = flat[6 * shard : 6 * shard + bias_in.shape[0]]
    return (
        out, grad_in, g_query, g_key, g_value, g_out, g_in, g_back,
        g_bias_q, g_bias_v, g_bo, g_bin, g_bb, g_g1, g_s1, g_g2, g_s2,
    )


def solution(mesh):
    placed = (
        P(("ctx", "uly", "fsdp"), None),
        P(("ctx", "uly", "fsdp"), None),
        P(("ctx", "uly", "fsdp"), None),
        P(("ctx", "uly", "fsdp")),
        P(("ctx", "uly", "fsdp")),
        P(),
        P("fsdp", None),
        P("fsdp", None),
        P("fsdp", None),
        P("fsdp", None),
        P("fsdp", None),
        P("fsdp", None),
        P("fsdp"),
        P("fsdp"),
        P("fsdp"),
        P("fsdp"),
        P("fsdp"),
        P("fsdp"),
        P("fsdp"),
        P("fsdp"),
        P("fsdp"),
    )
    return jax.shard_map(
        on_device,
        mesh=mesh,
        in_specs=placed,
        out_specs=(
            P(("ctx", "uly", "fsdp"), None),
            P(("ctx", "uly", "fsdp"), None),
            P("fsdp", None),
            P("fsdp", None),
            P("fsdp", None),
            P("fsdp", None),
            P("fsdp", None),
            P("fsdp", None),
            P("fsdp"),
            P("fsdp"),
            P("fsdp"),
            P("fsdp"),
            P("fsdp"),
            P("fsdp"),
            P("fsdp"),
            P("fsdp"),
            P("fsdp"),
        ),
        check_vma=False,
    )
```

```python
import functools

import jax
import jax.numpy as jnp
from jax import lax
from jax.experimental import pallas as pl
from jax.experimental.pallas import tpu as pltpu
from jax.sharding import PartitionSpec as P

HEADS = 12
HD = 64
BLK = 512
TQ = 256
TK = 256
DOCS = 64
FFB = 768
GRANT = 63 << 20
MASKED = -1e30
BF = jnp.bfloat16
F32 = jnp.float32
NT = (((1,), (1,)), ((), ()))
NN = (((1,), (0,)), ((), ()))
TN = (((0,), (0,)), ((), ()))


def mm(left, right, dims=NN):
    return lax.dot_general(left, right, dims, preferred_element_type=F32)


def whole(shape):
    return pl.BlockSpec(shape, lambda *_: (0,) * len(shape), pipeline_mode=pl.Buffered(1))


def sweep(total, step, work):
    def one(i, _):
        work(pl.multiple_of(i * step, step))
        return 0

    lax.fori_loop(0, total // step, one, 0)


def cost(flops, moved, special=0):
    return pl.CostEstimate(flops=flops, bytes_accessed=moved, transcendentals=special)


def lane_ids(rows):
    return lax.broadcasted_iota(jnp.int32, (rows, 128), 1)


def build_keys(sources, slot0, lo_ref, hi_ref, kaug, transposed, low_half):
    per = BLK // TK
    for at, kv in enumerate(sources):

        def one(j, _, at=at, kv=kv):
            rows = pl.ds(pl.multiple_of(j * TK, TK), TK)
            tile = at * (kv.shape[0] // TK) + j
            slot = slot0 + at * (kv.shape[0] // BLK) + j // per
            out = pl.ds(pl.multiple_of(tile * TK, TK), TK)
            rank = lax.broadcasted_iota(jnp.int32, (TK, 128), 0) + lax.rem(j, per) * TK
            inside = (rank >= lo_ref[pl.ds(slot, 1), :]) & (rank < hi_ref[pl.ds(slot, 1), :])
            bias = jnp.where(inside, 0.0, MASKED).astype(BF)
            kaug[out, 0:128] = jnp.where(lane_ids(TK) < 64, bias, kv[rows, 128:256])
            kaug[out, 128:256] = kv[rows, 256:384]
            if low_half:
                transposed[tile] = kv[rows, 0:256].T[0:192]
            else:
                transposed[tile] = kaug[out, :].T[64:256]
            return 0

        lax.fori_loop(0, kv.shape[0] // TK, one, 0)


def stack_queries(q, first, slo_ref, shi_ref, qs):
    lane = lane_ids(TQ)
    spot = lax.broadcasted_iota(jnp.int32, (TQ, 128), 0) + first
    mine = ((spot >= slo_ref[...]) & (spot < shi_ref[...])).astype(F32).astype(BF)
    zero = jnp.zeros((TQ, 128), BF)
    low, high = q[:, 0:128], q[:, 128:256]
    mark = jnp.where(lane < 64, mine, zero)
    qs[0:TQ, 0:128] = jnp.where(lane < 64, mine, low)
    qs[TQ : 2 * TQ, 0:128] = mark
    qs[2 * TQ :, 0:128] = mark
    qs[0:TQ, 128:256] = zero
    qs[TQ : 2 * TQ, 128:256] = jnp.where(lane < 64, high, zero)
    qs[2 * TQ :, 128:256] = jnp.where(lane < 64, zero, high)


def attend_kernel(*refs, slot0, count, resume, last):
    tlo, thi, qfirst, q_ref = refs[:4]
    sources = refs[4 : 4 + count]
    lo_ref, hi_ref, slo_ref, shi_ref = refs[4 + count : 8 + count]
    at = 8 + count
    if resume:
        acc_in, stat_in = refs[at : at + 2]
        at += 2
    if last:
        o_ref, ot_ref, lse_ref = refs[at : at + 3]
        at += 3
    else:
        acc_out, stat_out = refs[at : at + 2]
        at += 2
    kaug, vt, qs, acc, m_s, l_s = refs[at:]
    i = pl.program_id(0)

    @pl.when(i == 0)
    def _():
        build_keys(sources, slot0, lo_ref, hi_ref, kaug, vt, True)

    slots = count * sources[0].shape[0] // BLK
    per = BLK // TK
    stack_queries(q_ref[...], qfirst[i], slo_ref, shi_ref, qs)
    if resume:
        m_s[...] = stat_in[0, 0:1, :]
        l_s[...] = stat_in[0, 1:2, :]
        acc[...] = acc_in[0]
    else:
        m_s[...] = jnp.full_like(m_s, 2 * MASKED)
        l_s[...] = jnp.zeros_like(l_s)
        acc[...] = jnp.zeros_like(acc)

    def slot_loop(s, _):
        def key_loop(t, _):
            tile = s * per + t
            keys = pl.ds(pl.multiple_of(tile * TK, TK), TK)
            st = mm(kaug[keys, :], qs[...], NT)
            m_old = m_s[...]
            m_new = jnp.maximum(m_old, jnp.max(st, axis=0, keepdims=True))
            fade = jnp.exp(m_old - m_new)
            p = jnp.exp(st - m_new)
            l_s[...] = l_s[...] * fade + jnp.sum(p, axis=0, keepdims=True)
            m_s[...] = m_new
            low = p.astype(BF)
            for h in range(3):
                cols = slice(h * TQ, (h + 1) * TQ)
                part = slice(h * HD, (h + 1) * HD)
                acc[part, :] = acc[part, :] * fade[:, cols] + mm(vt[tile, part, :], low[:, cols])
            return 0

        return lax.fori_loop(tlo[i, slot0 + s], thi[i, slot0 + s], key_loop, 0)

    lax.fori_loop(0, slots, slot_loop, 0)
    if last:
        total = l_s[...]
        for h in range(3):
            cols = slice(h * TQ, (h + 1) * TQ)
            part = slice(h * HD, (h + 1) * HD)
            acc[part, :] = acc[part, :] / total[:, cols]
        ot_ref[0] = acc[...]
        o_ref[...] = acc[...].T.astype(BF)
        lse_ref[0] = m_s[...] + jnp.log(total)
    else:
        acc_out[0] = acc[...]
        stat_out[0, 0:1, :] = m_s[...]
        stat_out[0, 1:2, :] = l_s[...]


def rows_spec(shape):
    return pl.BlockSpec((TQ, shape[1]), lambda i, *_: (i, 0))


def tile_spec(shape):
    return pl.BlockSpec((1, *shape[1:]), lambda i, *_: (i, 0, 0))


def attend(tables, q, sources, slot0, state=None, last=False):
    tlo, thi, qfirst, lo, hi, slo, shi = tables
    tiles = q.shape[0] // TQ
    keys = sum(s.shape[0] for s in sources)
    state = tuple(state) if state else ()
    sd = jax.ShapeDtypeStruct
    acc, stat = sd((tiles, 3 * HD, TQ), F32), sd((tiles, 2, 3 * TQ), F32)
    if last:
        o, lse = sd((q.shape[0], 3 * HD), BF), sd((tiles, 1, 3 * TQ), F32)
        outs, out_specs = (o, acc, lse), (rows_spec(o.shape), tile_spec(acc.shape), tile_spec(lse.shape))
    else:
        outs, out_specs = (acc, stat), (tile_spec(acc.shape), tile_spec(stat.shape))
    return pl.pallas_call(
        functools.partial(attend_kernel, slot0=slot0, count=len(sources), resume=bool(state), last=last),
        out_shape=outs,
        grid_spec=pltpu.PrefetchScalarGridSpec(
            num_scalar_prefetch=3,
            grid=(tiles,),
            in_specs=[rows_spec(q.shape)]
            + [whole(x.shape) for x in (*sources, lo, hi, slo, shi)]
            + [tile_spec(x.shape) for x in state],
            out_specs=out_specs,
            scratch_shapes=[
                pltpu.VMEM((keys, 256), BF),
                pltpu.VMEM((keys // TK, 3 * HD, TK), BF),
                pltpu.VMEM((3 * TQ, 256), BF),
                pltpu.VMEM((3 * HD, TQ), F32),
                pltpu.VMEM((1, 3 * TQ), F32),
                pltpu.VMEM((1, 3 * TQ), F32),
            ],
        ),
        compiler_params=pltpu.CompilerParams(vmem_limit_bytes=GRANT),
        cost_estimate=cost(12_000_000_000, 12_000_000, 10_000_000),
        name="attend",
    )(tlo, thi, qfirst, q, *sources, lo, hi, slo, shi, *state)


def attend_back_kernel(
    tlo, thi, qfirst, q_ref, do_ref, ot_ref, lse_ref, kv, lo_ref, hi_ref, slo_ref, shi_ref, dq_ref, dkv_ref, *rest,
    slot0, first,
):
    if first:
        delta_ref, *rest = rest
    kaug, kt, qs, dos, acc, dk_s, dv_s = rest
    keys_all = kv.shape[0]
    slots = keys_all // BLK
    per = BLK // TK
    i = pl.program_id(0)

    @pl.when(i == 0)
    def _():
        build_keys((kv,), slot0, lo_ref, hi_ref, kaug, kt, False)
        dk_s[...] = jnp.zeros_like(dk_s)
        dv_s[...] = jnp.zeros_like(dv_s)

    stack_queries(q_ref[...], qfirst[i], slo_ref, shi_ref, qs)
    do = do_ref[...]
    lane = lane_ids(TQ)
    zero = jnp.zeros((TQ, 128), BF)
    dos[0:TQ, 0:128] = jnp.where(lane < 64, do[:, 0:128], zero)
    dos[TQ : 2 * TQ, 0:128] = jnp.where(lane < 64, zero, do[:, 0:128])
    dos[2 * TQ :, 0:128] = zero
    dos[0 : 2 * TQ, 128:256] = jnp.zeros((2 * TQ, 128), BF)
    dos[2 * TQ :, 128:192] = do[:, 128:192]
    dos[2 * TQ :, 192:256] = jnp.zeros((TQ, 64), BF)
    if first:
        both = do.astype(F32).T * ot_ref[0]
        delta = jnp.concatenate(
            [jnp.sum(both[h * HD : (h + 1) * HD], axis=0, keepdims=True) for h in range(3)], axis=1
        )
        delta_ref[0] = delta
    else:
        delta = ot_ref[0]
    lse = lse_ref[0]
    acc[...] = jnp.zeros_like(acc)

    def slot_loop(s, _):
        def key_loop(t, _):
            tile = s * per + t
            keys = pl.ds(pl.multiple_of(tile * TK, TK), TK)
            st = mm(kaug[keys, :], qs[...], NT)
            p = jnp.exp(st - lse)
            dp = mm(kv[keys, 0:256], dos[...], NT)
            ds = (p * (dp - delta)).astype(BF)
            dv_s[keys, :] += mm(p.astype(BF), dos[...])
            dk_s[keys, :] += mm(ds, qs[...])
            for h in range(3):
                cols = slice(h * TQ, (h + 1) * TQ)
                acc[(h + 1) * HD : (h + 2) * HD, :] += mm(kt[tile, h * HD : (h + 1) * HD, :], ds[:, cols])
            return 0

        return lax.fori_loop(tlo[i, slot0 + s], thi[i, slot0 + s], key_loop, 0)

    lax.fori_loop(0, slots, slot_loop, 0)
    dq_ref[...] = (acc[...] * HD ** (-0.5)).T.astype(BF)

    @pl.when(i == pl.num_programs(0) - 1)
    def _():
        def finish_tile(k, _):
            at = pl.ds(pl.multiple_of(k * TK, TK), TK)
            dkv_ref[at, 0:128] = dv_s[at, 0:128].astype(BF)
            dkv_ref[at, 128:256] = jnp.where(lane_ids(TK) < 64, dv_s[at, 128:256], dk_s[at, 0:128]).astype(BF)
            dkv_ref[at, 256:384] = dk_s[at, 128:256].astype(BF)
            return 0

        lax.fori_loop(0, keys_all // TK, finish_tile, 0)


def attend_back(tables, q, do, ot, lse, source, slot0, first=False, name="attend_back", size=14_000_000_000):
    tlo, thi, qfirst, lo, hi, slo, shi = tables
    tiles = q.shape[0] // TQ
    keys = source.shape[0]
    sd = jax.ShapeDtypeStruct
    outs = (sd(q.shape, BF), sd(source.shape, BF))
    out_specs = (rows_spec(q.shape), whole(source.shape))
    if first:
        outs += (sd(lse.shape, F32),)
        out_specs += (tile_spec(lse.shape),)
    return pl.pallas_call(
        functools.partial(attend_back_kernel, slot0=slot0, first=first),
        out_shape=outs,
        grid_spec=pltpu.PrefetchScalarGridSpec(
            num_scalar_prefetch=3,
            grid=(tiles,),
            in_specs=[rows_spec(q.shape), rows_spec(do.shape), tile_spec(ot.shape), tile_spec(lse.shape)]
            + [whole(x.shape) for x in (source, lo, hi, slo, shi)],
            out_specs=out_specs,
            scratch_shapes=[
                pltpu.VMEM((keys, 256), BF),
                pltpu.VMEM((keys // TK, 3 * HD, TK), BF),
                pltpu.VMEM((3 * TQ, 256), BF),
                pltpu.VMEM((3 * TQ, 256), BF),
                pltpu.VMEM((256, TQ), F32),
                pltpu.VMEM((keys, 256), F32),
                pltpu.VMEM((keys, 256), F32),
            ],
        ),
        compiler_params=pltpu.CompilerParams(vmem_limit_bytes=GRANT),
        cost_estimate=cost(size, size // 1000, size // 3000),
        name=name,
    )(tlo, thi, qfirst, q, do, ot, lse, source, lo, hi, slo, shi)


def project_kernel(
    who, x0, x1, x2, x3_top, x3_bottom, w_mine, w_other, bias_ref, chosen, q_ref, kv_ref, up_ref, down_ref, w_ref
):
    tall = w_mine.shape[0]
    rows = x0.shape[0]
    w_ref[pl.ds(pl.multiple_of(who[0] * tall, tall), tall), :] = w_mine[...]
    w_ref[pl.ds(pl.multiple_of((1 - who[0]) * tall, tall), tall), :] = w_other[...]
    for d, x in enumerate((x0, x1, x2, (x3_top, x3_bottom))):
        if d < 3:
            value = mm(x[...], w_ref[...]) + bias_ref[...]
        else:
            value = jnp.concatenate([mm(x[0][...], w_ref[...]), mm(x[1][...], w_ref[...])], axis=0) + bias_ref[...]
        at = slice(d * rows, (d + 1) * rows)
        q_ref[at, :] = (value[:, :256].astype(BF).astype(F32) * HD ** (-0.5)).astype(BF)
        kv = mm(chosen[d], value[:, 256:].astype(BF)).astype(BF)
        kv_ref[at, :] = kv
        inner = slice((d % 2) * rows, (d % 2 + 1) * rows)

        @pl.when(who[2] == d // 2)
        def _(inner=inner, kv=kv):
            down_ref[inner, :] = kv

        @pl.when(who[2] != d // 2)
        def _(inner=inner, kv=kv):
            up_ref[inner, :] = kv


def project(who, xs, w_mine, w_other, bias, chosen):
    sd = jax.ShapeDtypeStruct
    rows, width = xs[0].shape
    cols = w_mine.shape[1]
    ins = (*xs, w_mine, w_other, bias, chosen)
    outs = (
        sd((4 * rows, 256), BF), sd((4 * rows, cols - 256), BF), sd((2 * rows, cols - 256), BF),
        sd((2 * rows, cols - 256), BF), sd((width, cols), BF),
    )
    return pl.pallas_call(
        project_kernel,
        out_shape=outs,
        grid_spec=pltpu.PrefetchScalarGridSpec(
            num_scalar_prefetch=1,
            grid=(1,),
            in_specs=[whole(a.shape) for a in ins],
            out_specs=tuple(whole(a.shape) for a in outs),
        ),
        compiler_params=pltpu.CompilerParams(vmem_limit_bytes=GRANT),
        cost_estimate=cost(3_000_000_000, 12_000_000),
        name="project",
    )(who, *ins)


def row_mean(v):
    return jnp.sum(v, axis=-1, keepdims=True) * (1.0 / v.shape[-1])

def dense_kernel(
    who, o_ref, wo_a, wo_b, win_a, win_b, wback_a, wback_b, x_ref, teacher_ref, cot_ref, keep_ref, vec_ref,
    out_ref, dres_ref, dparts_ref, act_ref, dbr_ref, dpre_ref, hid_ref, dproj_ref, sums_ref,
    wo, win, wback, xh, inv, hidden, gp, acc, sems, *, FB
):
    rows, width = x_ref.shape
    groups = o_ref.shape[0] // rows
    part = width // groups
    units = win.shape[1]
    wo_loads, win_loads, wback_loads = [], [], []
    for i in range(2):
        side = who[0] if i == 0 else 1 - who[0]
        for e in range(groups // 2):
            to = pl.multiple_of(((side * (groups // 2) + e) ^ who[1]) * part, part)
            wo_loads.append(
                pltpu.make_async_copy((wo_a, wo_b)[i].at[pl.ds(e * part, part)], wo.at[pl.ds(to, part)], sems.at[2 * i + e])
            )
        for j, (pieces, target, held) in enumerate((((win_a, win_b), win, win_loads), ((wback_a, wback_b), wback, wback_loads))):
            tall = target.shape[0] // 2
            to = pl.multiple_of(side * tall, tall)
            held.append(pltpu.make_async_copy(pieces[i], target.at[pl.ds(to, tall)], sems.at[4 + 2 * i + j]))
    for load in wo_loads + win_loads + wback_loads:
        load.start()
    b_out, b_in, b_back = vec_ref[0:1, 0:width], vec_ref[1:2, :], vec_ref[2:3, 0:width]
    gain1, shift1, gain2, shift2 = (vec_ref[i : i + 1, 0:width] for i in range(3, 7))
    for load in wo_loads:
        load.wait()
    total = x_ref[...].astype(F32) + b_out
    for i in range(groups):
        total += mm(o_ref[i * rows : (i + 1) * rows, :], wo[i * part : (i + 1) * part, :])
    center = total - row_mean(total)
    scale = lax.rsqrt(row_mean(center * center) + 1e-12)
    inv[...] = scale
    unit = center * scale
    xh[...] = unit
    hid = unit * gain1 + shift1
    hidden[...] = hid
    hid_ref[...] = hid.astype(BF)
    acc[...] = jnp.zeros_like(acc)
    for load in win_loads + wback_loads:
        load.wait()

    def up(n, _):
        cols = pl.ds(pl.multiple_of(n * FB, FB), FB)
        pre = mm(hid_ref[...], win[:, cols]) + vec_ref[1:2, cols]
        cdf = 0.5 + 0.5 * lax.erf(pre * 0.7071067811865476)
        act = (pre * cdf).astype(BF)
        act_ref[:, cols] = act
        gp[:, cols] = cdf + pre * (jnp.exp(pre * pre * -0.5) * 0.3989422804014327)
        acc[...] += mm(act, wback[cols, :])
        return 0

    lax.fori_loop(0, units // FB, up, 0, unroll=True)
    total = hidden[...] + acc[...] + b_back
    center = total - row_mean(total)
    scale = lax.rsqrt(row_mean(center * center) + 1e-12)
    unit = center * scale
    result = unit * gain2 + shift2
    out_ref[...] = result.astype(BF)
    grad = cot_ref[...].astype(F32) + keep_ref[...] * (result - teacher_ref[...].astype(F32))
    def put(row, value):
        sums_ref[row : row + 1, 0 : value.shape[1]] = value
    put(5, jnp.sum(grad * unit, axis=0, keepdims=True))
    put(6, jnp.sum(grad, axis=0, keepdims=True))
    grad = grad * gain2
    back = scale * (grad - row_mean(grad) - unit * row_mean(grad * unit))
    acc[...] = back
    low = back.astype(BF)
    dbr_ref[...] = low
    put(2, jnp.sum(low.astype(F32), axis=0, keepdims=True))

    def down(n, _):
        cols = pl.ds(pl.multiple_of(n * FB, FB), FB)
        dpre = (mm(dbr_ref[...], wback[cols, :], NT) * gp[:, cols]).astype(BF)
        dpre_ref[:, cols] = dpre
        sums_ref[1:2, cols] = jnp.sum(dpre.astype(F32), axis=0, keepdims=True)
        acc[...] += mm(dpre, win[:, cols], NT)
        return 0

    lax.fori_loop(0, units // FB, down, 0, unroll=True)
    grad = acc[...]
    unit = xh[...]
    put(3, jnp.sum(grad * unit, axis=0, keepdims=True))
    put(4, jnp.sum(grad, axis=0, keepdims=True))
    grad = grad * gain1
    back = inv[...] * (grad - row_mean(grad) - unit * row_mean(grad * unit))
    dres_ref[...] = back
    low = back.astype(BF)
    dproj_ref[...] = low
    put(0, jnp.sum(low.astype(F32), axis=0, keepdims=True))
    for i in range(groups):
        dparts_ref[i * rows : (i + 1) * rows, :] = mm(low, wo[i * part : (i + 1) * part, :], NT).astype(BF)


def dense(who, o, weights, x, teacher, cot, keep, vec):
    rows, width = x.shape
    units = vec.shape[1]
    sd = jax.ShapeDtypeStruct
    outs = (
        sd((rows, width), BF), sd((rows, width), F32), sd(o.shape, BF), sd((rows, units), BF), sd((rows, width), BF),
        sd((rows, units), BF), sd((rows, width), BF), sd((rows, width), BF), sd((8, units), F32),
    )
    ins = (o, *weights, x, teacher, cot, keep, vec)
    stay = pl.BlockSpec(memory_space=pl.ANY)
    return pl.pallas_call(
        functools.partial(dense_kernel, FB=FFB),
        out_shape=outs,
        grid_spec=pltpu.PrefetchScalarGridSpec(
            num_scalar_prefetch=1,
            grid=(1,),
            in_specs=[whole(o.shape)] + [stay] * 6 + [whole(a.shape) for a in ins[7:]],
            out_specs=tuple(whole(a.shape) for a in outs),
            scratch_shapes=[
                pltpu.VMEM((width, width), BF), pltpu.VMEM((width, units), BF), pltpu.VMEM((units, width), BF),
                pltpu.VMEM((rows, width), F32), pltpu.VMEM((rows, 1), F32), pltpu.VMEM((rows, width), F32),
                pltpu.VMEM((rows, units), F32), pltpu.VMEM((rows, width), F32), pltpu.SemaphoreType.DMA((8,)),
            ],
        ),
        compiler_params=pltpu.CompilerParams(vmem_limit_bytes=GRANT),
        cost_estimate=cost(12_000_000_000, 30_000_000, 4_000_000),
        name="dense",
    )(who, *ins)


def finish_kernel(who, dq0, dq1, dq2, dq3, own_ref, pair_ref, left_ref, right_ref, turn_ref, all_ref, sums_ref):
    groups, rows = turn_ref.shape[:2]
    sums_ref[...] = jnp.zeros_like(sums_ref)

    def work(r):
        d = r // rows
        at = pl.ds(r, rows)
        inner = pl.ds(pl.multiple_of(lax.rem(d, groups // 2) * rows, rows), rows)
        first = (d // (groups // 2)) == who[2]
        back = own_ref[at, :].astype(F32) + pair_ref[at, :].astype(F32)
        back += jnp.where(first, left_ref[inner, :], right_ref[inner, :]).astype(F32)
        tok = mm(turn_ref[d], back.astype(BF)).astype(BF)
        dq = sum(ref[at, :].astype(F32) for ref in (dq0, dq1, dq2, dq3)).astype(BF)
        all_ref[at, 0:256] = dq
        all_ref[at, 256:640] = tok
        sums_ref[0:1, 0:256] += jnp.sum(dq.astype(F32), axis=0, keepdims=True)
        sums_ref[0:1, 256:640] += jnp.sum(tok.astype(F32), axis=0, keepdims=True)

    sweep(groups * rows, rows, work)


def finish(who, dqs, own, pair, left, right, turn):
    sd = jax.ShapeDtypeStruct
    cols = dqs[0].shape[1] + own.shape[1]
    ins = (*dqs, own, pair, left, right, turn)
    outs = (sd((dqs[0].shape[0], cols), BF), sd((8, cols), F32))
    return pl.pallas_call(
        finish_kernel,
        out_shape=outs,
        grid_spec=pltpu.PrefetchScalarGridSpec(
            num_scalar_prefetch=1,
            grid=(1,),
            in_specs=[whole(a.shape) for a in ins],
            out_specs=tuple(whole(a.shape) for a in outs),
        ),
        compiler_params=pltpu.CompilerParams(vmem_limit_bytes=GRANT),
        cost_estimate=cost(1_000_000_000, 9_000_000),
        name="finish",
    )(who, *ins)


def spread_kernel(all_ref, w_ref, own_ref, gx_ref, gy_ref, left_ref, right_ref):
    rows, width = own_ref.shape
    cut = width // 2
    parts = [mm(all_ref[d * rows : (d + 1) * rows, :], w_ref[...], NT).astype(BF) for d in range(4)]
    own_ref[...] = parts[0]
    gx_ref[0:rows, :] = parts[1][:, :cut]
    right_ref[...] = parts[1][:, cut:]
    left_ref[...] = parts[2][:, :cut]
    gy_ref[0:rows, :] = parts[2][:, cut:]
    gx_ref[rows:, :] = parts[3][:, :cut]
    gy_ref[rows:, :] = parts[3][:, cut:]


def spread_x(d_all, w_heads):
    rows, width = d_all.shape[0] // 4, w_heads.shape[0]
    shapes = ((rows, width), (2 * rows, width // 2), (2 * rows, width // 2), (rows, width // 2), (rows, width // 2))
    return pl.pallas_call(
        spread_kernel,
        out_shape=tuple(jax.ShapeDtypeStruct(s, BF) for s in shapes),
        grid=(1,),
        in_specs=[whole(d_all.shape), whole(w_heads.shape)],
        out_specs=tuple(whole(s) for s in shapes),
        compiler_params=pltpu.CompilerParams(vmem_limit_bytes=GRANT),
        cost_estimate=cost(2_000_000_000, 7_000_000),
        name="spread_x",
    )(d_all, w_heads)


def part_out(who, held, am, ao, bm, bo, sides):
    part = am.shape[0]
    for mine, other, side, base in ((am, ao, sides[0], 0), (bm, bo, sides[1], 2 * part)):

        def move(r, mine=mine, other=other, side=side, base=base):
            mine[pl.ds(r, 16), :] = held[pl.ds(pl.multiple_of(base + side * part + r, 16), 16), :]
            other[pl.ds(r, 16), :] = held[pl.ds(pl.multiple_of(base + (1 - side) * part + r, 16), 16), :]

        sweep(part, 16, move)


def plus(left, right, at):
    return (left[at, :].astype(F32) + right[at, :].astype(F32)).astype(BF)


def first_kernel(who, back_a, back_b, in_a, in_b, out_a, out_b, am, ao, bm, bo, held):
    width = back_a.shape[1]
    tall = in_a.shape[0]

    def upper(r):
        at = pl.ds(r, 16)
        for k in range(4):
            held[at, k * width : (k + 1) * width] = plus(back_a, back_b, pl.ds(pl.multiple_of(k * tall + r, 16), 16))
        held[pl.ds(pl.multiple_of(tall + r, 16), 16), :] = plus(in_a, in_b, at)

    def lower(r):
        held[pl.ds(pl.multiple_of(2 * tall + r, 16), 16), :] = plus(out_a, out_b, pl.ds(r, 16))

    sweep(tall, 16, upper)
    sweep(out_a.shape[0], 16, lower)
    part_out(who, held, am, ao, bm, bo, (lax.rem(who[1], 2), who[1] // 2))


def both_kernel(who, a_mine, a_got, b_mine, b_got, both):
    del who
    part = a_mine.shape[0]

    def work(r):
        both[pl.ds(r, 16), :] = plus(a_mine, a_got, pl.ds(r, 16))
        both[pl.ds(pl.multiple_of(part + r, 16), 16), :] = plus(b_mine, b_got, pl.ds(r, 16))

    sweep(part, 16, work)


def second_kernel(who, a_mine, a_got, b_mine, b_got, am, ao, bm, bo, held):
    both_kernel(who, a_mine, a_got, b_mine, b_got, held)
    part_out(who, held, am, ao, bm, bo, (who[1] // 2, lax.rem(who[1], 2)))


def join_kernel(who, a, b, c, d, back_ref, in_ref, out_ref, vec_ref, held):
    s1, s2 = lax.rem(who[1], 2), who[1] // 2
    part = a.shape[0] // 2
    for at, ref in enumerate((a, b, c, d)):
        color, i = at // 2, at % 2
        for j in range(2):
            spot = (s1 ^ i) * 2 + (s2 ^ j) if color == 0 else 4 + (s2 ^ i) * 2 + (s1 ^ j)

            def move(r, spot=spot, ref=ref, j=j):
                frm = pl.ds(pl.multiple_of(j * part + r, 16), 16)
                held[pl.ds(pl.multiple_of(spot * part + r, 16), 16), :] = ref[frm, :]

            sweep(part, 16, move)
    tall, width = out_ref.shape

    def upper(r):
        at = pl.ds(r, 16)
        for k in range(4):
            to = pl.ds(pl.multiple_of(k * tall + r, 16), 16)
            back_ref[to, :] = held[at, k * width : (k + 1) * width].astype(F32)
        in_ref[at, :] = held[pl.ds(pl.multiple_of(tall + r, 16), 16), :].astype(F32)

    def lower(r):
        frm = pl.ds(pl.multiple_of(2 * tall + r, 16), 16)
        for k in range(3):
            to = pl.ds(pl.multiple_of(k * 128 + r, 16), 16)
            out_ref[to, :] = held[frm, k * width : (k + 1) * width].astype(F32)

    sweep(tall, 16, upper)
    sweep(128, 16, lower)
    vec_ref[...] = held[2 * tall : 2 * tall + 16, 3 * width :].astype(F32)


def small_call(kernel, who, pieces, outs, scratch, name):
    return pl.pallas_call(
        kernel,
        out_shape=tuple(jax.ShapeDtypeStruct(*s) for s in outs),
        grid_spec=pltpu.PrefetchScalarGridSpec(
            num_scalar_prefetch=1,
            grid=(1,),
            in_specs=[whole(a.shape) for a in pieces],
            out_specs=tuple(whole(s[0]) for s in outs),
            scratch_shapes=scratch,
        ),
        compiler_params=pltpu.CompilerParams(vmem_limit_bytes=GRANT),
        cost_estimate=cost(1_000_000, 9_000_000),
        name=name,
    )(who, *pieces)


def heads_kernel(who, h0, h1, h2, h3, q_ref, k_ref, v_ref, bias_ref, held):
    tall = q_ref.shape[0]
    for d, ref in enumerate((h0, h1, h2, h3)):
        held[who[1] ^ d] = ref[...]

    def work(r):
        at = pl.ds(r, 16)
        for a in range(4):
            cols = slice(a * 192, (a + 1) * 192)
            q_ref[at, cols] = held[a, at, 64:256].astype(F32)
            v_ref[at, cols] = held[a, at, 256:448].astype(F32)
            k_ref[at, cols] = held[a, at, 448:640].astype(F32)

    sweep(tall, 16, work)
    for a in range(4):
        line = held[a, 0:16, 0:64].astype(F32)
        for k in range(3):
            spot = slice(a * 192 + k * 64, a * 192 + (k + 1) * 64)
            bias_ref[0:1, spot] = line[k : k + 1]
            bias_ref[8:9, spot] = line[k + 3 : k + 4]


def heads_out(who, pieces):
    sd = jax.ShapeDtypeStruct
    outs = (sd((384, 768), F32),) * 3 + (sd((16, 768), F32),)
    return pl.pallas_call(
        heads_kernel,
        out_shape=outs,
        grid_spec=pltpu.PrefetchScalarGridSpec(
            num_scalar_prefetch=1,
            grid=(1,),
            in_specs=[whole(a.shape) for a in pieces],
            out_specs=tuple(whole(a.shape) for a in outs),
            scratch_shapes=[pltpu.VMEM((4, *pieces[0].shape), BF)],
        ),
        compiler_params=pltpu.CompilerParams(vmem_limit_bytes=GRANT),
        cost_estimate=cost(1_000_000, 6_000_000),
        name="heads_out",
    )(who, *pieces)


def swap(block, axis="fsdp"):
    return lax.ppermute(block, axis, [(0, 1), (1, 0)])


def shifted(block, axis, distance):
    devices = range(lax.axis_size(axis))
    route = [(i - distance, i) for i in devices if i - distance in devices]
    return lax.ppermute(block, axis, route)


def flip(block, bit, axis="uly"):
    return lax.ppermute(block, axis, [(i, i ^ bit) for i in range(lax.axis_size(axis))])


def exchange(rows, axis):
    return lax.all_to_all(rows, axis, split_axis=0, concat_axis=0, tiled=True)


def spread_rows(rows, axis):
    count = lax.axis_size(axis)
    return exchange(jnp.broadcast_to(rows[None], (count, *rows.shape)).reshape(-1, rows.shape[1]), axis)


def sum_parts(rows, count):
    got = rows.reshape(count, -1, rows.shape[1])
    return sum(got[i].astype(F32) for i in range(count)).astype(BF)


def sum_scatter(rows, axis):
    return sum_parts(exchange(rows, axis), lax.axis_size(axis))


def add(left, right):
    return (left.astype(F32) + right.astype(F32)).astype(BF)


def line_step(held, bit):
    return flip(held, bit, "ctx")


def line_join(held, got, bit):
    low = (lax.axis_index("ctx") & bit) == 0
    return jnp.stack([jnp.where(low, held, got), jnp.where(low, got, held)], axis=1).reshape(-1, *held.shape[1:])


def line_rest(held, bit):
    while bit > 0:
        held = line_join(held, line_step(held, bit), bit)
        bit //= 2
    return held.reshape(-1, held.shape[2])


def tie(*values):
    return lax.optimization_barrier(values)


def on_device(
    tokens, teacher, cotangent, valid, teacher_ok, doc_starts, w_query, w_key, w_value, w_out, w_in, w_back,
    bias_query, bias_value, bias_out, bias_in, bias_back, norm1_gain, norm1_bias, norm2_gain, norm2_bias,
):
    groups = lax.axis_size("uly")
    spans = lax.axis_size("ctx")
    rows, width = tokens.shape
    block = rows * groups * 2
    stream = block * spans
    ctx_index = lax.axis_index("ctx")
    uly = lax.axis_index("uly")
    half = lax.axis_index("fsdp")
    head_cols = width // groups
    shard = w_query.shape[0]
    middle = groups * rows // 2
    upper = uly // 2

    small = (bias_query, bias_value, bias_out, bias_in, bias_back, norm1_gain, norm1_bias, norm2_gain, norm2_bias)
    valid_one = valid[None, :]
    valid_own = jnp.concatenate([valid_one, flip(valid_one, 1), flip(valid_one, 2), flip(valid_one, 3)], axis=0)
    x_own, valid_own, *small = tie(tokens, valid_own, *small)
    x_x, x_y = flip(x_own, 1), flip(x_own, 2)
    valid_pair = swap(valid_own)
    valid_both = jnp.stack([valid_own, valid_pair]).reshape(2, 2, 2, rows)
    valid_high = lax.dynamic_index_in_dim(valid_both, 1 - upper, 1, keepdims=False)
    valid_low = lax.dynamic_index_in_dim(valid_both, upper, 1, keepdims=False)
    halo = (shifted(valid_high, "ctx", 1), shifted(valid_low, "ctx", -1))
    block_valid = jnp.concatenate([valid_own, valid_pair, halo[0][0], halo[1][0], halo[0][1], halo[1][1]], axis=0)
    count = jnp.full((8, 128), jnp.sum(valid_both), jnp.int32)
    bit = 1
    while bit < spans:
        count = count + flip(count, bit, "ctx")
        bit *= 2
    count = count[0, 0].astype(F32)

    start_col = uly * head_cols
    cut = [lax.dynamic_slice_in_dim(w, start_col, head_cols, 1) for w in (w_query, w_value, w_key)]
    w_mine = jnp.concatenate([jnp.zeros((shard, 256 - head_cols), BF), *cut], axis=1)
    w_other = swap(w_mine)
    who = jnp.stack([half, uly, upper])
    packed = jnp.concatenate(small)
    packed_pair = swap(packed)
    first, second = jnp.where(half == 0, packed, packed_pair), jnp.where(half == 0, packed_pair, packed)
    vectors = []
    at = 0
    for p in small:
        n = p.shape[0]
        vectors.append(jnp.concatenate([first[at : at + n], second[at : at + n]]).astype(F32))
        at += n
    bq_all, bv_all = vectors[:2]
    vec = jnp.stack([jnp.pad(v, (0, w_in.shape[1] - v.shape[0])) for v in vectors[2:]] + [jnp.zeros((w_in.shape[1],), F32)])
    bias_heads = jnp.concatenate(
        [
            jnp.zeros((256 - head_cols,), F32),
            lax.dynamic_slice_in_dim(bq_all, start_col, head_cols, 0),
            lax.dynamic_slice_in_dim(bv_all, start_col, head_cols, 0),
            jnp.zeros((head_cols,), F32),
        ]
    )

    place = jnp.arange(groups, dtype=jnp.int32)
    two = jnp.arange(2, dtype=jnp.int32)
    in_plane = place ^ uly
    halo_group = jnp.concatenate([uly ^ (2 * (1 - upper) + two), uly ^ (2 * upper + two)])
    halo_plane = ctx_index + jnp.where(place < 2, -1, 1)
    plane_of = jnp.concatenate([jnp.full((2 * groups,), 1, jnp.int32) * ctx_index, halo_plane, halo_plane])
    group_of = jnp.concatenate([in_plane, in_plane, halo_group, halo_group])
    mine = jnp.full((groups,), 1, jnp.int32) * half
    core_of = jnp.concatenate([mine, 1 - mine, mine, 1 - mine])
    block_id = plane_of * (2 * groups) + group_of * 2 + core_of
    spot = block_id[:, None] * rows + jnp.arange(rows, dtype=jnp.int32)[None, :]
    edges = jnp.concatenate([doc_starts, jnp.full((DOCS + 1,), stream, jnp.int32)])
    window_first = jnp.maximum(ctx_index * block - block // 2, 0)
    first_doc = jnp.sum((doc_starts <= window_first).astype(jnp.int32)) - 1
    near = lax.dynamic_slice_in_dim(edges, first_doc, DOCS + 1, 0)
    tiles = groups * rows // TQ
    per = rows // TQ
    tile_ids = jnp.arange(tiles, dtype=jnp.int32)
    qfirst = ctx_index * block + (((tile_ids // per) ^ uly) * 2 + half) * rows + lax.rem(tile_ids, per) * TQ
    q_lo = jnp.max(jnp.where(near[None, :] <= qfirst[:, None], near[None, :], 0), axis=1)
    q_hi = jnp.min(jnp.where(near[None, :] <= qfirst[:, None] + TQ - 1, stream, near[None, :]), axis=1)
    limits = jnp.concatenate([near, q_lo, q_hi])
    counted = jnp.sum(block_valid[:, None, :] * (spot[:, None, :] < limits[None, :, None]), axis=-1)
    bounds = counted[:, : DOCS + 1]
    cnt_lo = counted[:, DOCS + 1 : DOCS + 1 + tiles].T
    cnt_hi = counted[:, DOCS + 1 + tiles :].T
    pad64 = jnp.zeros((bounds.shape[0], 128 - DOCS), jnp.int32)
    lo_tab = jnp.concatenate([bounds[:, :DOCS], pad64], axis=1)
    hi_tab = jnp.concatenate([bounds[:, 1:], pad64], axis=1)
    slo_tab = jnp.concatenate([near[:DOCS], pad64[0]])[None, :]
    shi_tab = jnp.concatenate([near[1:], pad64[0]])[None, :]
    some = cnt_hi > cnt_lo
    tlo = jnp.where(some, cnt_lo // TK, 0)
    thi = jnp.where(some, (cnt_hi + TK - 1) // TK, 0)
    tables = (tlo, thi, qfirst, lo_tab, hi_tab, slo_tab, shi_tab)
    before = mm(valid_own.astype(BF), (jnp.arange(rows)[:, None] < jnp.arange(rows)[None, :]).astype(BF)).astype(jnp.int32)
    goes_to = jnp.where(valid_own > 0, before, rows)
    chosen = (goes_to[:, None, :] == jnp.arange(rows, dtype=jnp.int32)[None, :, None]).astype(BF)
    loss_scale = jnp.float32(stream) / count
    keep = (loss_scale * (valid * teacher_ok).astype(F32))[:, None]
    turned = (goes_to[:, :, None] == jnp.arange(rows, dtype=jnp.int32)[None, None, :]).astype(BF)

    x_x, x_y, w_other, chosen, bias_heads, *tables = tie(x_x, x_y, w_other, chosen, bias_heads, *tables)
    x_top, x_bottom = flip(x_y[: rows // 2], 1), flip(x_x[rows // 2 :], 2)

    q_low, kv_own, kv_up, kv_down, w_heads = project(
        who, (tokens, x_x, x_y, x_top, x_bottom), w_mine, w_other, bias_heads[None, :], chosen
    )
    kv_from_left, kv_from_right = shifted(kv_up, "ctx", 1), shifted(kv_down, "ctx", -1)
    w_out, w_in, w_back, kv_own = tie(w_out, w_in, w_back, kv_own)
    wo_pair, win_pair, wback_pair = swap(w_out), swap(w_in), swap(w_back)
    kv_pair = swap(kv_own)
    state = attend(tables, q_low, (kv_own,), 0)
    kv_halo = jnp.concatenate([kv_from_left, kv_from_right], axis=0)
    kv_halo, kv_pair, *state = tie(kv_halo, kv_pair, *state)
    kv_halo_pair = swap(kv_halo)
    state = attend(tables, q_low, (kv_pair,), groups, state)
    o_heads, o_turned, lse = attend(tables, q_low, (kv_halo, kv_halo_pair), 2 * groups, state, last=True)
    o_rel = o_heads.reshape(groups, rows, head_cols)
    o_rest = [flip(o_rel[d], d) for d in range(1, groups)]
    o_heads, x_x, x_y, x_top, x_bottom = tie(o_heads, x_x, x_y, x_top, x_bottom)
    x_all = jnp.concatenate([tokens, x_x, x_y, x_top, x_bottom], axis=0)

    x_all, *o_rest = tie(x_all, *o_rest)
    o_all = jnp.concatenate([o_rel[0], *o_rest], axis=0)

    out, d_resid1, d_parts, act, d_branch, d_pre, hidden_low, d_proj, sums = dense(
        who, o_all, (w_out, wo_pair, w_in, win_pair, w_back, wback_pair), tokens, teacher, cotangent, keep, vec
    )
    d_rel = d_parts.reshape(groups, rows, head_cols)
    tall = w_back.shape[0]
    vector_rows = jnp.concatenate(
        [sums[i, :width].reshape(2, -1) for i in (0, 2, 3, 4, 5, 6)] + [sums[1].reshape(2, -1)], axis=1
    ).reshape(2, -1, width)
    vector_rows = jnp.pad(vector_rows, ((0, 0), (0, 128 - vector_rows.shape[1]), (0, 0))).astype(BF)
    o_rows = o_all.reshape(groups, rows, head_cols)

    def back_part(side):
        return mm(lax.dynamic_slice_in_dim(act, side * tall, tall, 1), d_branch, TN).astype(BF)

    def in_part(side):
        return mm(lax.dynamic_slice_in_dim(hidden_low, side * shard, shard, 1), d_pre, TN).astype(BF)

    def out_part(side):
        both = [
            mm(lax.dynamic_index_in_dim(o_rows, (2 * side + e) ^ uly, 0, keepdims=False), d_proj, TN).astype(BF)
            for e in range(2)
        ]
        stack = jnp.concatenate([*both, lax.dynamic_index_in_dim(vector_rows, side, 0, keepdims=False)], axis=0)
        return jnp.concatenate([stack[i * 128 : (i + 1) * 128] for i in range(4)], axis=1)

    d_rest = [flip(d_rel[d], d) for d in range(1, groups)]
    back_got = swap(back_part(1 - half))
    in_got, out_got = swap(in_part(1 - half)), swap(out_part(1 - half))
    back_mine, in_mine, out_mine = back_part(half), in_part(half), out_part(half)
    back_got, in_got, out_got, back_mine, in_mine, out_mine, *d_rest = tie(
        back_got, in_got, out_got, back_mine, in_mine, out_mine, *d_rest
    )
    wide = w_in.shape[1]
    total = 2 * shard + 128
    am, ao, bm, bo = small_call(
        first_kernel, who, (back_mine, back_got, in_mine, in_got, out_mine, out_got),
        (((total // 4, wide), BF),) * 4, [pltpu.VMEM((total, wide), BF)], "first_stage",
    )
    d_heads = jnp.concatenate([d_rel[0], *d_rest], axis=0)
    d_heads, am, ao, bm, bo = tie(d_heads, am, ao, bm, bo)

    ag, bg = flip(ao, 1), flip(bo, 2)
    args = (tables, q_low, d_heads, o_turned, lse)
    dq0, dkv_halo_pair, delta = attend_back(*args, kv_halo_pair, 3 * groups, first=True, name="back_halo_pair")
    dkv_halo_pair, delta = tie(dkv_halo_pair, delta)
    args = (tables, q_low, d_heads, delta, lse)
    got_lo, got_hi = swap(dkv_halo_pair[:middle]), swap(dkv_halo_pair[middle:])
    dq1, dkv_halo = attend_back(*args, kv_halo, 2 * groups, name="back_halo", size=1_000_000)
    dkv_halo, got_lo, got_hi, ag, bg = tie(dkv_halo, got_lo, got_hi, ag, bg)

    halo_lo, halo_hi = add(dkv_halo[:middle], got_lo), add(dkv_halo[middle:], got_hi)
    am, ao, bm, bo = small_call(
        second_kernel, who, (am, ag, bm, bg), (((total // 8, wide), BF),) * 4,
        [pltpu.VMEM((total // 2, wide), BF)], "second_stage",
    )
    halo_lo, halo_hi, delta, am, ao, bm, bo = tie(halo_lo, halo_hi, delta, am, ao, bm, bo)
    args = (tables, q_low, d_heads, delta, lse)
    ag, bg = flip(ao, 2), flip(bo, 1)
    from_left, from_right = shifted(halo_hi, "ctx", 1), shifted(halo_lo, "ctx", -1)
    dq2, dkv_pair = attend_back(*args, kv_pair, groups, name="back_pair")
    dkv_pair, ag, bg, from_left, from_right = tie(dkv_pair, ag, bg, from_left, from_right)

    (line,) = small_call(both_kernel, who, (am, ag, bm, bg), (((total // 4, wide), BF),), [], "third_stage")
    line, dkv_pair, delta = tie(line, dkv_pair, delta)
    args = (tables, q_low, d_heads, delta, lse)
    line = exchange(line, "ctx")
    pair_got = swap(dkv_pair)
    dq3, dkv_own = attend_back(*args, kv_own, 0, name="back_own")
    dkv_own, line, pair_got = tie(dkv_own, line, pair_got)
    line = sum_parts(line, spans)
    line, dkv_own = tie(line, dkv_own)
    line = spread_rows(line, "ctx")

    d_all, d_sums = finish(who, (dq0, dq1, dq2, dq3), dkv_own, pair_got, from_left, from_right, turned)
    dx_own, give_x, give_y, left_next, right_next = spread_x(d_all, w_heads)
    d_all, give_x, give_y = tie(d_all, give_x, give_y)
    give_x, give_y = flip(give_x, 1), flip(give_y, 2)
    corner = d_sums[0, 64:].reshape(9, 64)

    def heads_part(side):
        grad = mm(lax.dynamic_slice_in_dim(x_all, side * shard, shard, 1), d_all, TN)
        return lax.dynamic_update_slice(grad, corner, (0, 0)).astype(BF)

    heads_other = heads_part(1 - half)
    heads_got = swap(heads_other)
    heads_mine = heads_part(half)
    heads_sum = add(heads_mine, heads_got)
    line, give_x, give_y, heads_sum = tie(line, give_x, give_y, heads_sum)
    a_near, b_near = line[: total // 8], line[total // 8 :]
    a_near = jnp.concatenate([a_near, flip(a_near, 2)], axis=0)
    b_near = jnp.concatenate([b_near, flip(b_near, 1)], axis=0)
    a_far, b_far = flip(a_near, 1), flip(b_near, 2)
    left_next = flip(add(left_next, give_x[rows:]), 2)
    right_next = flip(add(right_next, give_y[rows:]), 1)
    heads_sum = spread_rows(sum_scatter(heads_sum, "ctx"), "ctx")
    heads_all = [heads_sum] + [flip(heads_sum, d) for d in range(1, groups)]
    grad_in = d_resid1 + dx_own.astype(F32)
    grad_in = grad_in + jnp.concatenate([give_x[:rows].astype(F32), give_y[:rows].astype(F32)], axis=1)
    grad_in = grad_in + jnp.concatenate([left_next.astype(F32), right_next.astype(F32)], axis=1)
    g_back, g_in, g_out, g_vec = small_call(
        join_kernel, who, (a_near, a_far, b_near, b_far),
        ((w_back.shape, F32), (w_in.shape, F32), (w_out.shape, F32), ((16, width), F32)),
        [pltpu.VMEM((total, wide), BF)], "join",
    )
    g_query, g_key, g_value, g_bias = heads_out(who, heads_all)
    g_bias_q = lax.dynamic_slice_in_dim(g_bias[0], half * shard, shard, 0)
    g_bias_v = lax.dynamic_slice_in_dim(g_bias[8], half * shard, shard, 0)
    flat = g_vec.reshape(-1)
    g_bo, g_bb, g_g1, g_s1, g_g2, g_s2 = [flat[i * shard : (i + 1) * shard] for i in range(6)]
    g_bin = flat[6 * shard : 6 * shard + bias_in.shape[0]]
    return (
        out, grad_in, g_query, g_key, g_value, g_out, g_in, g_back,
        g_bias_q, g_bias_v, g_bo, g_bin, g_bb, g_g1, g_s1, g_g2, g_s2,
    )


def solution(mesh):
    placed = (
        P(("ctx", "uly", "fsdp"), None),
        P(("ctx", "uly", "fsdp"), None),
        P(("ctx", "uly", "fsdp"), None),
        P(("ctx", "uly", "fsdp")),
        P(("ctx", "uly", "fsdp")),
        P(),
        P("fsdp", None),
        P("fsdp", None),
        P("fsdp", None),
        P("fsdp", None),
        P("fsdp", None),
        P("fsdp", None),
        P("fsdp"),
        P("fsdp"),
        P("fsdp"),
        P("fsdp"),
        P("fsdp"),
        P("fsdp"),
        P("fsdp"),
        P("fsdp"),
        P("fsdp"),
    )
    return jax.shard_map(
        on_device,
        mesh=mesh,
        in_specs=placed,
        out_specs=(
            P(("ctx", "uly", "fsdp"), None),
            P(("ctx", "uly", "fsdp"), None),
            P("fsdp", None),
            P("fsdp", None),
            P("fsdp", None),
            P("fsdp", None),
            P("fsdp", None),
            P("fsdp", None),
            P("fsdp"),
            P("fsdp"),
            P("fsdp"),
            P("fsdp"),
            P("fsdp"),
            P("fsdp"),
            P("fsdp"),
            P("fsdp"),
            P("fsdp"),
        ),
        check_vma=False,
    )
```

```python
import functools

import jax
import jax.numpy as jnp
from jax import lax
from jax.experimental import pallas as pl
from jax.experimental.pallas import tpu as pltpu
from jax.sharding import PartitionSpec as P

HEADS = 12
HD = 64
BLK = 512
TQ = 256
TK = 256
DOCS = 64
FFB = 1536
GRANT = 63 << 20
MASKED = -1e30
BF = jnp.bfloat16
F32 = jnp.float32
NT = (((1,), (1,)), ((), ()))
NN = (((1,), (0,)), ((), ()))
TN = (((0,), (0,)), ((), ()))


def mm(left, right, dims=NN):
    return lax.dot_general(left, right, dims, preferred_element_type=F32)


def whole(shape):
    return pl.BlockSpec(shape, lambda *_: (0,) * len(shape), pipeline_mode=pl.Buffered(1))


def sweep(total, step, work):
    def one(i, _):
        work(pl.multiple_of(i * step, step))
        return 0

    lax.fori_loop(0, total // step, one, 0)


def cost(flops, moved, special=0):
    return pl.CostEstimate(flops=flops, bytes_accessed=moved, transcendentals=special)


def lane_ids(rows):
    return lax.broadcasted_iota(jnp.int32, (rows, 128), 1)


def build_keys(sources, slot0, lo_ref, hi_ref, kaug, transposed, low_half):
    per = BLK // TK
    for at, kv in enumerate(sources):

        def one(j, _, at=at, kv=kv):
            rows = pl.ds(pl.multiple_of(j * TK, TK), TK)
            tile = at * (kv.shape[0] // TK) + j
            slot = slot0 + at * (kv.shape[0] // BLK) + j // per
            out = pl.ds(pl.multiple_of(tile * TK, TK), TK)
            rank = lax.broadcasted_iota(jnp.int32, (TK, 128), 0) + lax.rem(j, per) * TK
            inside = (rank >= lo_ref[pl.ds(slot, 1), :]) & (rank < hi_ref[pl.ds(slot, 1), :])
            bias = jnp.where(inside, 0.0, MASKED).astype(BF)
            kaug[out, 0:128] = jnp.where(lane_ids(TK) < 64, bias, kv[rows, 128:256])
            kaug[out, 128:256] = kv[rows, 256:384]
            if low_half:
                transposed[tile] = kv[rows, 0:256].T[0:192]
            else:
                transposed[tile] = kaug[out, :].T[64:256]
            return 0

        lax.fori_loop(0, kv.shape[0] // TK, one, 0)


def stack_queries(q, first, slo_ref, shi_ref, qs):
    lane = lane_ids(TQ)
    spot = lax.broadcasted_iota(jnp.int32, (TQ, 128), 0) + first
    mine = ((spot >= slo_ref[...]) & (spot < shi_ref[...])).astype(F32).astype(BF)
    zero = jnp.zeros((TQ, 128), BF)
    low, high = q[:, 0:128], q[:, 128:256]
    mark = jnp.where(lane < 64, mine, zero)
    qs[0:TQ, 0:128] = jnp.where(lane < 64, mine, low)
    qs[TQ : 2 * TQ, 0:128] = mark
    qs[2 * TQ :, 0:128] = mark
    qs[0:TQ, 128:256] = zero
    qs[TQ : 2 * TQ, 128:256] = jnp.where(lane < 64, high, zero)
    qs[2 * TQ :, 128:256] = jnp.where(lane < 64, zero, high)


def attend_kernel(*refs, slot0, count, resume, last):
    tlo, thi, qfirst, q_ref = refs[:4]
    sources = refs[4 : 4 + count]
    lo_ref, hi_ref, slo_ref, shi_ref = refs[4 + count : 8 + count]
    at = 8 + count
    if resume:
        acc_in, stat_in = refs[at : at + 2]
        at += 2
    if last:
        o_ref, ot_ref, lse_ref = refs[at : at + 3]
        at += 3
    else:
        acc_out, stat_out = refs[at : at + 2]
        at += 2
    kaug, vt, qs, acc, m_s, l_s = refs[at:]
    i = pl.program_id(0)

    @pl.when(i == 0)
    def _():
        build_keys(sources, slot0, lo_ref, hi_ref, kaug, vt, True)

    slots = count * sources[0].shape[0] // BLK
    per = BLK // TK
    stack_queries(q_ref[...], qfirst[i], slo_ref, shi_ref, qs)
    if resume:
        m_s[...] = stat_in[0, 0:1, :]
        l_s[...] = stat_in[0, 1:2, :]
        acc[...] = acc_in[0]
    else:
        m_s[...] = jnp.full_like(m_s, 2 * MASKED)
        l_s[...] = jnp.zeros_like(l_s)
        acc[...] = jnp.zeros_like(acc)

    def slot_loop(s, _):
        def key_loop(t, _):
            tile = s * per + t
            keys = pl.ds(pl.multiple_of(tile * TK, TK), TK)
            st = mm(kaug[keys, :], qs[...], NT)
            m_old = m_s[...]
            m_new = jnp.maximum(m_old, jnp.max(st, axis=0, keepdims=True))
            fade = jnp.exp(m_old - m_new)
            p = jnp.exp(st - m_new)
            l_s[...] = l_s[...] * fade + jnp.sum(p, axis=0, keepdims=True)
            m_s[...] = m_new
            low = p.astype(BF)
            for h in range(3):
                cols = slice(h * TQ, (h + 1) * TQ)
                part = slice(h * HD, (h + 1) * HD)
                acc[part, :] = acc[part, :] * fade[:, cols] + mm(vt[tile, part, :], low[:, cols])
            return 0

        return lax.fori_loop(tlo[i, slot0 + s], thi[i, slot0 + s], key_loop, 0)

    lax.fori_loop(0, slots, slot_loop, 0)
    if last:
        total = l_s[...]
        for h in range(3):
            cols = slice(h * TQ, (h + 1) * TQ)
            part = slice(h * HD, (h + 1) * HD)
            acc[part, :] = acc[part, :] / total[:, cols]
        ot_ref[0] = acc[...]
        o_ref[...] = acc[...].T.astype(BF)
        lse_ref[0] = m_s[...] + jnp.log(total)
    else:
        acc_out[0] = acc[...]
        stat_out[0, 0:1, :] = m_s[...]
        stat_out[0, 1:2, :] = l_s[...]


def rows_spec(shape):
    return pl.BlockSpec((TQ, shape[1]), lambda i, *_: (i, 0))


def tile_spec(shape):
    return pl.BlockSpec((1, *shape[1:]), lambda i, *_: (i, 0, 0))


def attend(tables, q, sources, slot0, state=None, last=False):
    tlo, thi, qfirst, lo, hi, slo, shi = tables
    tiles = q.shape[0] // TQ
    keys = sum(s.shape[0] for s in sources)
    state = tuple(state) if state else ()
    sd = jax.ShapeDtypeStruct
    acc, stat = sd((tiles, 3 * HD, TQ), F32), sd((tiles, 2, 3 * TQ), F32)
    if last:
        o, lse = sd((q.shape[0], 3 * HD), BF), sd((tiles, 1, 3 * TQ), F32)
        outs, out_specs = (o, acc, lse), (rows_spec(o.shape), tile_spec(acc.shape), tile_spec(lse.shape))
    else:
        outs, out_specs = (acc, stat), (tile_spec(acc.shape), tile_spec(stat.shape))
    return pl.pallas_call(
        functools.partial(attend_kernel, slot0=slot0, count=len(sources), resume=bool(state), last=last),
        out_shape=outs,
        grid_spec=pltpu.PrefetchScalarGridSpec(
            num_scalar_prefetch=3,
            grid=(tiles,),
            in_specs=[rows_spec(q.shape)]
            + [whole(x.shape) for x in (*sources, lo, hi, slo, shi)]
            + [tile_spec(x.shape) for x in state],
            out_specs=out_specs,
            scratch_shapes=[
                pltpu.VMEM((keys, 256), BF),
                pltpu.VMEM((keys // TK, 3 * HD, TK), BF),
                pltpu.VMEM((3 * TQ, 256), BF),
                pltpu.VMEM((3 * HD, TQ), F32),
                pltpu.VMEM((1, 3 * TQ), F32),
                pltpu.VMEM((1, 3 * TQ), F32),
            ],
        ),
        compiler_params=pltpu.CompilerParams(vmem_limit_bytes=GRANT),
        cost_estimate=cost(12_000_000_000, 12_000_000, 10_000_000),
        name="attend",
    )(tlo, thi, qfirst, q, *sources, lo, hi, slo, shi, *state)


def attend_back_kernel(
    tlo, thi, qfirst, q_ref, do_ref, ot_ref, lse_ref, kv, lo_ref, hi_ref, slo_ref, shi_ref, dq_ref, *rest,
    slot0, first, cuts,
):
    dkv_refs, rest = rest[:cuts], rest[cuts:]
    if first:
        delta_ref, *rest = rest
    kaug, kt, qs, dos, acc, dk_s, dv_s = rest
    keys_all = kv.shape[0]
    slots = keys_all // BLK
    per = BLK // TK
    i = pl.program_id(0)

    @pl.when(i == 0)
    def _():
        build_keys((kv,), slot0, lo_ref, hi_ref, kaug, kt, False)
        dk_s[...] = jnp.zeros_like(dk_s)
        dv_s[...] = jnp.zeros_like(dv_s)

    stack_queries(q_ref[...], qfirst[i], slo_ref, shi_ref, qs)
    do = do_ref[...]
    lane = lane_ids(TQ)
    zero = jnp.zeros((TQ, 128), BF)
    dos[0:TQ, 0:128] = jnp.where(lane < 64, do[:, 0:128], zero)
    dos[TQ : 2 * TQ, 0:128] = jnp.where(lane < 64, zero, do[:, 0:128])
    dos[2 * TQ :, 0:128] = zero
    dos[0 : 2 * TQ, 128:256] = jnp.zeros((2 * TQ, 128), BF)
    dos[2 * TQ :, 128:192] = do[:, 128:192]
    dos[2 * TQ :, 192:256] = jnp.zeros((TQ, 64), BF)
    if first:
        both = do.astype(F32).T * ot_ref[0]
        delta = jnp.concatenate(
            [jnp.sum(both[h * HD : (h + 1) * HD], axis=0, keepdims=True) for h in range(3)], axis=1
        )
        delta_ref[0] = delta
    else:
        delta = ot_ref[0]
    lse = lse_ref[0]
    acc[...] = jnp.zeros_like(acc)

    def slot_loop(s, _):
        def key_loop(t, _):
            tile = s * per + t
            keys = pl.ds(pl.multiple_of(tile * TK, TK), TK)
            st = mm(kaug[keys, :], qs[...], NT)
            p = jnp.exp(st - lse)
            dp = mm(kv[keys, 0:256], dos[...], NT)
            ds = (p * (dp - delta)).astype(BF)
            dv_s[keys, :] += mm(p.astype(BF), dos[...])
            dk_s[keys, :] += mm(ds, qs[...])
            for h in range(3):
                cols = slice(h * TQ, (h + 1) * TQ)
                acc[(h + 1) * HD : (h + 2) * HD, :] += mm(kt[tile, h * HD : (h + 1) * HD, :], ds[:, cols])
            return 0

        return lax.fori_loop(tlo[i, slot0 + s], thi[i, slot0 + s], key_loop, 0)

    lax.fori_loop(0, slots, slot_loop, 0)
    dq_ref[...] = (acc[...] * HD ** (-0.5)).T.astype(BF)

    @pl.when(i == pl.num_programs(0) - 1)
    def _():
        share = keys_all // cuts
        for j, dkv_ref in enumerate(dkv_refs):

            def write(r, j=j, dkv_ref=dkv_ref):
                at = pl.ds(pl.multiple_of(j * share + r, TK), TK)
                to = pl.ds(r, TK)
                dkv_ref[to, 0:128] = dv_s[at, 0:128].astype(BF)
                dkv_ref[to, 128:256] = jnp.where(lane_ids(TK) < 64, dv_s[at, 128:256], dk_s[at, 0:128]).astype(BF)
                dkv_ref[to, 256:384] = dk_s[at, 128:256].astype(BF)

            sweep(share, TK, write)


def attend_back(tables, q, do, ot, lse, source, slot0, first=False, cuts=1, name="attend_back", size=14_000_000_000):
    tlo, thi, qfirst, lo, hi, slo, shi = tables
    tiles = q.shape[0] // TQ
    keys = source.shape[0]
    sd = jax.ShapeDtypeStruct
    piece = (keys // cuts, source.shape[1])
    outs = (sd(q.shape, BF),) + (sd(piece, BF),) * cuts
    out_specs = (rows_spec(q.shape),) + (whole(piece),) * cuts
    if first:
        outs += (sd(lse.shape, F32),)
        out_specs += (tile_spec(lse.shape),)
    return pl.pallas_call(
        functools.partial(attend_back_kernel, slot0=slot0, first=first, cuts=cuts),
        out_shape=outs,
        grid_spec=pltpu.PrefetchScalarGridSpec(
            num_scalar_prefetch=3,
            grid=(tiles,),
            in_specs=[rows_spec(q.shape), rows_spec(do.shape), tile_spec(ot.shape), tile_spec(lse.shape)]
            + [whole(x.shape) for x in (source, lo, hi, slo, shi)],
            out_specs=out_specs,
            scratch_shapes=[
                pltpu.VMEM((keys, 256), BF),
                pltpu.VMEM((keys // TK, 3 * HD, TK), BF),
                pltpu.VMEM((3 * TQ, 256), BF),
                pltpu.VMEM((3 * TQ, 256), BF),
                pltpu.VMEM((256, TQ), F32),
                pltpu.VMEM((keys, 256), F32),
                pltpu.VMEM((keys, 256), F32),
            ],
        ),
        compiler_params=pltpu.CompilerParams(vmem_limit_bytes=GRANT),
        cost_estimate=cost(size, size // 1000, size // 3000),
        name=name,
    )(tlo, thi, qfirst, q, do, ot, lse, source, lo, hi, slo, shi)


def project_kernel(
    who, x0, x1, x2, x3_top, x3_bottom, w_mine, w_other, bias_ref, chosen, q_ref, kv_ref, up_ref, down_ref, w_ref
):
    tall = w_mine.shape[0]
    rows = x0.shape[0]
    w_ref[pl.ds(pl.multiple_of(who[0] * tall, tall), tall), :] = w_mine[...]
    w_ref[pl.ds(pl.multiple_of((1 - who[0]) * tall, tall), tall), :] = w_other[...]
    for d, x in enumerate((x0, x1, x2, (x3_top, x3_bottom))):
        if d < 3:
            value = mm(x[...], w_ref[...]) + bias_ref[...]
        else:
            value = jnp.concatenate([mm(x[0][...], w_ref[...]), mm(x[1][...], w_ref[...])], axis=0) + bias_ref[...]
        at = slice(d * rows, (d + 1) * rows)
        q_ref[at, :] = (value[:, :256].astype(BF).astype(F32) * HD ** (-0.5)).astype(BF)
        kv = mm(chosen[d], value[:, 256:].astype(BF)).astype(BF)
        kv_ref[at, :] = kv
        inner = slice((d % 2) * rows, (d % 2 + 1) * rows)

        @pl.when(who[2] == d // 2)
        def _(inner=inner, kv=kv):
            down_ref[inner, :] = kv

        @pl.when(who[2] != d // 2)
        def _(inner=inner, kv=kv):
            up_ref[inner, :] = kv


def project(who, xs, w_mine, w_other, bias, chosen):
    sd = jax.ShapeDtypeStruct
    rows, width = xs[0].shape
    cols = w_mine.shape[1]
    ins = (*xs, w_mine, w_other, bias, chosen)
    outs = (
        sd((4 * rows, 256), BF), sd((4 * rows, cols - 256), BF), sd((2 * rows, cols - 256), BF),
        sd((2 * rows, cols - 256), BF), sd((width, cols), BF),
    )
    return pl.pallas_call(
        project_kernel,
        out_shape=outs,
        grid_spec=pltpu.PrefetchScalarGridSpec(
            num_scalar_prefetch=1,
            grid=(1,),
            in_specs=[whole(a.shape) for a in ins],
            out_specs=tuple(whole(a.shape) for a in outs),
        ),
        compiler_params=pltpu.CompilerParams(vmem_limit_bytes=24 << 20),
        cost_estimate=cost(3_000_000_000, 12_000_000),
        name="project",
    )(who, *ins)


def row_mean(v):
    return jnp.sum(v, axis=-1, keepdims=True) * (1.0 / v.shape[-1])

def dense_kernel(
    who, o_ref, wo_a, wo_b, win_a, win_b, wback_a, wback_b, x_ref, teacher_ref, cot_ref, keep_ref, vec_ref,
    out_ref, dres_ref, dparts_ref, act_ref, dbr_ref, dpre_ref, hid_ref, dproj_ref, sums_ref,
    wo, win, wback, xh, inv, hidden, gp, acc, sems, *, FB
):
    rows, width = x_ref.shape
    groups = o_ref.shape[0] // rows
    part = width // groups
    units = win.shape[1]
    wo_loads, win_loads, wback_loads = [], [], []
    for i in range(2):
        side = who[0] if i == 0 else 1 - who[0]
        for e in range(groups // 2):
            to = pl.multiple_of(((side * (groups // 2) + e) ^ who[1]) * part, part)
            wo_loads.append(
                pltpu.make_async_copy((wo_a, wo_b)[i].at[pl.ds(e * part, part)], wo.at[pl.ds(to, part)], sems.at[2 * i + e])
            )
        for j, (pieces, target, held) in enumerate((((win_a, win_b), win, win_loads), ((wback_a, wback_b), wback, wback_loads))):
            tall = target.shape[0] // 2
            to = pl.multiple_of(side * tall, tall)
            held.append(pltpu.make_async_copy(pieces[i], target.at[pl.ds(to, tall)], sems.at[4 + 2 * i + j]))
    for load in wo_loads + win_loads + wback_loads:
        load.start()
    b_out, b_in, b_back = vec_ref[0:1, 0:width], vec_ref[1:2, :], vec_ref[2:3, 0:width]
    gain1, shift1, gain2, shift2 = (vec_ref[i : i + 1, 0:width] for i in range(3, 7))
    for load in wo_loads:
        load.wait()
    total = x_ref[...].astype(F32) + b_out
    for i in range(groups):
        total += mm(o_ref[i * rows : (i + 1) * rows, :], wo[i * part : (i + 1) * part, :])
    center = total - row_mean(total)
    scale = lax.rsqrt(row_mean(center * center) + 1e-12)
    inv[...] = scale
    unit = center * scale
    xh[...] = unit
    hid = unit * gain1 + shift1
    hidden[...] = hid
    hid_ref[...] = hid.astype(BF)
    acc[...] = jnp.zeros_like(acc)
    for load in win_loads + wback_loads:
        load.wait()

    def up(n, _):
        cols = pl.ds(pl.multiple_of(n * FB, FB), FB)
        pre = mm(hid_ref[...], win[:, cols]) + vec_ref[1:2, cols]
        cdf = 0.5 + 0.5 * lax.erf(pre * 0.7071067811865476)
        act = (pre * cdf).astype(BF)
        act_ref[:, cols] = act
        gp[:, cols] = cdf + pre * (jnp.exp(pre * pre * -0.5) * 0.3989422804014327)
        acc[...] += mm(act, wback[cols, :])
        return 0

    lax.fori_loop(0, units // FB, up, 0, unroll=False)
    total = hidden[...] + acc[...] + b_back
    center = total - row_mean(total)
    scale = lax.rsqrt(row_mean(center * center) + 1e-12)
    unit = center * scale
    result = unit * gain2 + shift2
    out_ref[...] = result.astype(BF)
    grad = cot_ref[...].astype(F32) + keep_ref[...] * (result - teacher_ref[...].astype(F32))
    def put(row, value):
        sums_ref[row : row + 1, 0 : value.shape[1]] = value
    put(5, jnp.sum(grad * unit, axis=0, keepdims=True))
    put(6, jnp.sum(grad, axis=0, keepdims=True))
    grad = grad * gain2
    back = scale * (grad - row_mean(grad) - unit * row_mean(grad * unit))
    acc[...] = back
    low = back.astype(BF)
    dbr_ref[...] = low
    put(2, jnp.sum(low.astype(F32), axis=0, keepdims=True))

    def down(n, _):
        cols = pl.ds(pl.multiple_of(n * FB, FB), FB)
        dpre = (mm(dbr_ref[...], wback[cols, :], NT) * gp[:, cols]).astype(BF)
        dpre_ref[:, cols] = dpre
        sums_ref[1:2, cols] = jnp.sum(dpre.astype(F32), axis=0, keepdims=True)
        acc[...] += mm(dpre, win[:, cols], NT)
        return 0

    lax.fori_loop(0, units // FB, down, 0, unroll=False)
    grad = acc[...]
    unit = xh[...]
    put(3, jnp.sum(grad * unit, axis=0, keepdims=True))
    put(4, jnp.sum(grad, axis=0, keepdims=True))
    grad = grad * gain1
    back = inv[...] * (grad - row_mean(grad) - unit * row_mean(grad * unit))
    dres_ref[...] = back
    low = back.astype(BF)
    dproj_ref[...] = low
    put(0, jnp.sum(low.astype(F32), axis=0, keepdims=True))
    for i in range(groups):
        dparts_ref[i * rows : (i + 1) * rows, :] = mm(low, wo[i * part : (i + 1) * part, :], NT).astype(BF)


def dense(who, o, weights, x, teacher, cot, keep, vec):
    rows, width = x.shape
    units = vec.shape[1]
    sd = jax.ShapeDtypeStruct
    outs = (
        sd((rows, width), BF), sd((rows, width), F32), sd(o.shape, BF), sd((rows, units), BF), sd((rows, width), BF),
        sd((rows, units), BF), sd((rows, width), BF), sd((rows, width), BF), sd((8, units), F32),
    )
    ins = (o, *weights, x, teacher, cot, keep, vec)
    stay = pl.BlockSpec(memory_space=pl.ANY)
    return pl.pallas_call(
        functools.partial(dense_kernel, FB=FFB),
        out_shape=outs,
        grid_spec=pltpu.PrefetchScalarGridSpec(
            num_scalar_prefetch=1,
            grid=(1,),
            in_specs=[whole(o.shape)] + [stay] * 6 + [whole(a.shape) for a in ins[7:]],
            out_specs=tuple(whole(a.shape) for a in outs),
            scratch_shapes=[
                pltpu.VMEM((width, width), BF), pltpu.VMEM((width, units), BF), pltpu.VMEM((units, width), BF),
                pltpu.VMEM((rows, width), F32), pltpu.VMEM((rows, 1), F32), pltpu.VMEM((rows, width), F32),
                pltpu.VMEM((rows, units), F32), pltpu.VMEM((rows, width), F32), pltpu.SemaphoreType.DMA((8,)),
            ],
        ),
        compiler_params=pltpu.CompilerParams(vmem_limit_bytes=GRANT),
        cost_estimate=cost(12_000_000_000, 30_000_000, 4_000_000),
        name="dense",
    )(who, *ins)


def finish_kernel(
    who, dq0, dq1, dq2, dq3, own_ref, pair_ref, left_ref, right_ref, turn_ref, w_ref,
    all_ref, sums_ref, dx_ref, gx_ref, gy_ref, next_left, next_right,
):
    d = pl.program_id(0)
    rows, width = dx_ref.shape
    cut = width // 2

    @pl.when(d == 0)
    def _():
        sums_ref[...] = jnp.zeros_like(sums_ref)

    back = own_ref[...].astype(F32) + pair_ref[...].astype(F32)
    back += jnp.where((d // 2) == who[2], left_ref[...], right_ref[...]).astype(F32)
    tok = mm(turn_ref[0], back.astype(BF)).astype(BF)
    dq = sum(ref[...].astype(F32) for ref in (dq0, dq1, dq2, dq3)).astype(BF)
    all_ref[:, 0:256] = dq
    all_ref[:, 256:640] = tok
    sums_ref[0:1, 0:256] += jnp.sum(dq.astype(F32), axis=0, keepdims=True)
    sums_ref[0:1, 256:640] += jnp.sum(tok.astype(F32), axis=0, keepdims=True)
    part = mm(all_ref[...], w_ref[...], NT).astype(BF)

    @pl.when(d == 0)
    def _():
        dx_ref[...] = part

    @pl.when(d == 1)
    def _():
        gx_ref[0:rows, :] = part[:, :cut]
        next_right[...] = part[:, cut:]

    @pl.when(d == 2)
    def _():
        next_left[...] = part[:, :cut]
        gy_ref[0:rows, :] = part[:, cut:]

    @pl.when(d == 3)
    def _():
        gx_ref[rows:, :] = part[:, :cut]
        gy_ref[rows:, :] = part[:, cut:]


def finish(who, dqs, own, pair, left, right, turn, w_heads):
    sd = jax.ShapeDtypeStruct
    rows, width = turn.shape[1], w_heads.shape[0]
    cols = dqs[0].shape[1] + own.shape[1]
    ins = (*dqs, own, pair, left, right, turn, w_heads)
    shapes = ((rows, width), (2 * rows, width // 2), (2 * rows, width // 2), (rows, width // 2), (rows, width // 2))
    outs = (sd((4 * rows, cols), BF), sd((8, cols), F32)) + tuple(sd(s, BF) for s in shapes)

    def by_block(shape):
        return pl.BlockSpec((rows, shape[1]), lambda d, *_: (d, 0))

    def by_pair(shape):
        return pl.BlockSpec((rows, shape[1]), lambda d, *_: (lax.rem(d, 2), 0))

    return pl.pallas_call(
        finish_kernel,
        out_shape=outs,
        grid_spec=pltpu.PrefetchScalarGridSpec(
            num_scalar_prefetch=1,
            grid=(4,),
            in_specs=[by_block(a.shape) for a in ins[:6]]
            + [by_pair(a.shape) for a in ins[6:8]]
            + [pl.BlockSpec((1, rows, rows), lambda d, *_: (d, 0, 0)), whole(w_heads.shape)],
            out_specs=(by_block(outs[0].shape), whole(outs[1].shape)) + tuple(whole(s) for s in shapes),
        ),
        compiler_params=pltpu.CompilerParams(vmem_limit_bytes=GRANT),
        cost_estimate=cost(3_000_000_000, 16_000_000),
        name="finish",
    )(who, *ins)


def part_out(who, held, am, ao, bm, bo, sides):
    part = am.shape[0]
    for mine, other, side, base in ((am, ao, sides[0], 0), (bm, bo, sides[1], 2 * part)):

        def move(r, mine=mine, other=other, side=side, base=base):
            mine[pl.ds(r, 16), :] = held[pl.ds(pl.multiple_of(base + side * part + r, 16), 16), :]
            other[pl.ds(r, 16), :] = held[pl.ds(pl.multiple_of(base + (1 - side) * part + r, 16), 16), :]

        sweep(part, 16, move)


def plus(left, right, at):
    return (left[at, :].astype(F32) + right[at, :].astype(F32)).astype(BF)


def first_kernel(who, back_a, back_b, in_a, in_b, out_a, out_b, am, ao, bm, bo, held):
    width = back_a.shape[1]
    tall = in_a.shape[0]

    def upper(r):
        at = pl.ds(r, 16)
        for k in range(4):
            held[at, k * width : (k + 1) * width] = plus(back_a, back_b, pl.ds(pl.multiple_of(k * tall + r, 16), 16))
        held[pl.ds(pl.multiple_of(tall + r, 16), 16), :] = plus(in_a, in_b, at)

    def lower(r):
        held[pl.ds(pl.multiple_of(2 * tall + r, 16), 16), :] = plus(out_a, out_b, pl.ds(r, 16))

    sweep(tall, 16, upper)
    sweep(out_a.shape[0], 16, lower)
    part_out(who, held, am, ao, bm, bo, (lax.rem(who[1], 2), who[1] // 2))


def both_kernel(who, a_mine, a_got, b_mine, b_got, both):
    del who
    part = a_mine.shape[0]

    def work(r):
        both[pl.ds(r, 16), :] = plus(a_mine, a_got, pl.ds(r, 16))
        both[pl.ds(pl.multiple_of(part + r, 16), 16), :] = plus(b_mine, b_got, pl.ds(r, 16))

    sweep(part, 16, work)


def second_kernel(who, a_mine, a_got, b_mine, b_got, am, ao, bm, bo, held):
    both_kernel(who, a_mine, a_got, b_mine, b_got, held)
    part_out(who, held, am, ao, bm, bo, (who[1] // 2, lax.rem(who[1], 2)))


def join_kernel(who, a, b, c, d, back_ref, in_ref, out_ref, vec_ref, held):
    step = pl.program_id(0)

    @pl.when(step == 0)
    def _():
        gather_pieces(who, (a, b, c, d), held)

    tall = held.shape[0] - 128
    tall, width = tall // 2, back_ref.shape[1]
    cols = pl.ds(pl.multiple_of(step * width, 128), width)
    back_ref[...] = held[0:tall, cols].astype(F32)
    rows = in_ref.shape[0]
    in_ref[...] = held[pl.ds(pl.multiple_of(tall + step * rows, 16), rows), :].astype(F32)

    @pl.when(step < 3)
    def _():
        out_ref[...] = held[2 * tall :, cols].astype(F32)

    @pl.when(step == 3)
    def _():
        vec_ref[...] = held[2 * tall : 2 * tall + 16, 3 * width :].astype(F32)


def gather_pieces(who, pieces, held):
    s1, s2 = lax.rem(who[1], 2), who[1] // 2
    part = pieces[0].shape[0] // 2
    for at, ref in enumerate(pieces):
        color, i = at // 2, at % 2
        for j in range(2):
            spot = (s1 ^ i) * 2 + (s2 ^ j) if color == 0 else 4 + (s2 ^ i) * 2 + (s1 ^ j)

            def move(r, spot=spot, ref=ref, j=j):
                frm = pl.ds(pl.multiple_of(j * part + r, 16), 16)
                held[pl.ds(pl.multiple_of(spot * part + r, 16), 16), :] = ref[frm, :]

            sweep(part, 16, move)

def join(who, pieces, back, first, out, total):
    sd = jax.ShapeDtypeStruct
    tall, width = first[0], back[1]
    outs = (sd(back, F32), sd(first, F32), sd(out, F32), sd((16, width), F32))
    return pl.pallas_call(
        join_kernel,
        out_shape=outs,
        grid_spec=pltpu.PrefetchScalarGridSpec(
            num_scalar_prefetch=1,
            grid=(4,),
            in_specs=[whole(a.shape) for a in pieces],
            out_specs=(
                pl.BlockSpec((tall, width), lambda k, *_: (k, 0)),
                pl.BlockSpec((tall // 4, first[1]), lambda k, *_: (k, 0)),
                pl.BlockSpec((128, width), lambda k, *_: (jnp.minimum(k, 2), 0)),
                whole((16, width)),
            ),
            scratch_shapes=[pltpu.VMEM((total, first[1]), BF)],
        ),
        compiler_params=pltpu.CompilerParams(vmem_limit_bytes=GRANT),
        cost_estimate=cost(1_000_000, 16_000_000),
        name="join",
    )(who, *pieces)


def small_call(kernel, who, pieces, outs, scratch, name, grant=24 << 20):
    return pl.pallas_call(
        kernel,
        out_shape=tuple(jax.ShapeDtypeStruct(*s) for s in outs),
        grid_spec=pltpu.PrefetchScalarGridSpec(
            num_scalar_prefetch=1,
            grid=(1,),
            in_specs=[whole(a.shape) for a in pieces],
            out_specs=tuple(whole(s[0]) for s in outs),
            scratch_shapes=scratch,
        ),
        compiler_params=pltpu.CompilerParams(vmem_limit_bytes=grant),
        cost_estimate=cost(1_000_000, 9_000_000),
        name=name,
    )(who, *pieces)


def heads_kernel(who, in_ref, q_ref, k_ref, v_ref, bias_ref):
    tall = in_ref.shape[1]
    for c in range(in_ref.shape[0] // 4):
        at = slice(c * tall, (c + 1) * tall)
        for a in range(4):
            cols = slice(a * 192, (a + 1) * 192)
            block = in_ref[c * 4 + (who[1] ^ a)].astype(F32)
            q_ref[at, cols] = block[:, 64:256]
            v_ref[at, cols] = block[:, 256:448]
            k_ref[at, cols] = block[:, 448:640]
            if c == 0:
                for k in range(3):
                    spot = slice(a * 192 + k * 64, a * 192 + (k + 1) * 64)
                    bias_ref[0:1, spot] = block[k : k + 1, 0:64]
                    bias_ref[8:9, spot] = block[k + 3 : k + 4, 0:64]


def heads_out(who, gathered):
    outs = (((384, 768), F32),) * 3 + (((16, 768), F32),)
    return small_call(heads_kernel, who, (gathered,), outs, [], "heads_out")


def swap(block, axis="fsdp"):
    return lax.ppermute(block, axis, [(0, 1), (1, 0)])


def shifted(block, axis, distance):
    devices = range(lax.axis_size(axis))
    route = [(i - distance, i) for i in devices if i - distance in devices]
    return lax.ppermute(block, axis, route)


def flip(block, bit, axis="uly"):
    return lax.ppermute(block, axis, [(i, i ^ bit) for i in range(lax.axis_size(axis))])


def exchange(rows, axis):
    return lax.all_to_all(rows, axis, split_axis=0, concat_axis=0, tiled=True)


def spread_rows(rows, axis):
    count = lax.axis_size(axis)
    return exchange(jnp.broadcast_to(rows[None], (count, *rows.shape)).reshape(-1, rows.shape[1]), axis)


def sum_parts(rows, count):
    got = rows.reshape(count, -1, rows.shape[1])
    return sum(got[i].astype(F32) for i in range(count)).astype(BF)


def sum_scatter(rows, axis):
    return sum_parts(exchange(rows, axis), lax.axis_size(axis))


def add(left, right):
    return (left.astype(F32) + right.astype(F32)).astype(BF)


def line_step(held, bit):
    return flip(held, bit, "ctx")


def line_join(held, got, bit):
    low = (lax.axis_index("ctx") & bit) == 0
    return jnp.stack([jnp.where(low, held, got), jnp.where(low, got, held)], axis=1).reshape(-1, *held.shape[1:])


def line_rest(held, bit):
    while bit > 0:
        held = line_join(held, line_step(held, bit), bit)
        bit //= 2
    return held.reshape(-1, held.shape[2])


def chunks_of(rows, axis):
    count, me = lax.axis_size(axis), lax.axis_index(axis)
    split = rows.reshape(count, -1, rows.shape[1])
    picked = [lax.dynamic_index_in_dim(split, me ^ k, 0, keepdims=False) for k in range(count)]
    return [picked[0]] + [flip(picked[k], k, axis) for k in range(1, count)]


def tie(*values):
    return lax.optimization_barrier(values)


def on_device(
    tokens, teacher, cotangent, valid, teacher_ok, doc_starts, w_query, w_key, w_value, w_out, w_in, w_back,
    bias_query, bias_value, bias_out, bias_in, bias_back, norm1_gain, norm1_bias, norm2_gain, norm2_bias,
):
    groups = lax.axis_size("uly")
    spans = lax.axis_size("ctx")
    rows, width = tokens.shape
    block = rows * groups * 2
    stream = block * spans
    ctx_index = lax.axis_index("ctx")
    uly = lax.axis_index("uly")
    half = lax.axis_index("fsdp")
    head_cols = width // groups
    shard = w_query.shape[0]
    upper = uly // 2

    small = (bias_query, bias_value, bias_out, bias_in, bias_back, norm1_gain, norm1_bias, norm2_gain, norm2_bias)
    valid_one = valid[None, :]
    valid_own = jnp.concatenate([valid_one, flip(valid_one, 1), flip(valid_one, 2), flip(valid_one, 3)], axis=0)
    x_own, valid_own, *small = tie(tokens, valid_own, *small)
    x_x, x_y = flip(x_own, 1), flip(x_own, 2)
    valid_pair = swap(valid_own)
    valid_both = jnp.stack([valid_own, valid_pair]).reshape(2, 2, 2, rows)
    valid_high = lax.dynamic_index_in_dim(valid_both, 1 - upper, 1, keepdims=False)
    valid_low = lax.dynamic_index_in_dim(valid_both, upper, 1, keepdims=False)
    halo = (shifted(valid_high, "ctx", 1), shifted(valid_low, "ctx", -1))
    block_valid = jnp.concatenate([valid_own, valid_pair, halo[0][0], halo[1][0], halo[0][1], halo[1][1]], axis=0)
    count = jnp.full((8, 128), jnp.sum(valid_both), jnp.int32)
    bit = 1
    while bit < spans:
        count = count + flip(count, bit, "ctx")
        bit *= 2
    count = count[0, 0].astype(F32)

    start_col = uly * head_cols
    cut = [lax.dynamic_slice_in_dim(w, start_col, head_cols, 1) for w in (w_query, w_value, w_key)]
    w_mine = jnp.concatenate([jnp.zeros((shard, 256 - head_cols), BF), *cut], axis=1)
    w_other = swap(w_mine)
    who = jnp.stack([half, uly, upper])
    packed = jnp.concatenate(small)
    packed_pair = swap(packed)
    first, second = jnp.where(half == 0, packed, packed_pair), jnp.where(half == 0, packed_pair, packed)
    vectors = []
    at = 0
    for p in small:
        n = p.shape[0]
        vectors.append(jnp.concatenate([first[at : at + n], second[at : at + n]]).astype(F32))
        at += n
    bq_all, bv_all = vectors[:2]
    vec = jnp.stack([jnp.pad(v, (0, w_in.shape[1] - v.shape[0])) for v in vectors[2:]] + [jnp.zeros((w_in.shape[1],), F32)])
    bias_heads = jnp.concatenate(
        [
            jnp.zeros((256 - head_cols,), F32),
            lax.dynamic_slice_in_dim(bq_all, start_col, head_cols, 0),
            lax.dynamic_slice_in_dim(bv_all, start_col, head_cols, 0),
            jnp.zeros((head_cols,), F32),
        ]
    )

    place = jnp.arange(groups, dtype=jnp.int32)
    two = jnp.arange(2, dtype=jnp.int32)
    in_plane = place ^ uly
    halo_group = jnp.concatenate([uly ^ (2 * (1 - upper) + two), uly ^ (2 * upper + two)])
    halo_plane = ctx_index + jnp.where(place < 2, -1, 1)
    plane_of = jnp.concatenate([jnp.full((2 * groups,), 1, jnp.int32) * ctx_index, halo_plane, halo_plane])
    group_of = jnp.concatenate([in_plane, in_plane, halo_group, halo_group])
    mine = jnp.full((groups,), 1, jnp.int32) * half
    core_of = jnp.concatenate([mine, 1 - mine, mine, 1 - mine])
    block_id = plane_of * (2 * groups) + group_of * 2 + core_of
    spot = block_id[:, None] * rows + jnp.arange(rows, dtype=jnp.int32)[None, :]
    edges = jnp.concatenate([doc_starts, jnp.full((DOCS + 1,), stream, jnp.int32)])
    window_first = jnp.maximum(ctx_index * block - block // 2, 0)
    first_doc = jnp.sum((doc_starts <= window_first).astype(jnp.int32)) - 1
    near = lax.dynamic_slice_in_dim(edges, first_doc, DOCS + 1, 0)
    tiles = groups * rows // TQ
    per = rows // TQ
    tile_ids = jnp.arange(tiles, dtype=jnp.int32)
    qfirst = ctx_index * block + (((tile_ids // per) ^ uly) * 2 + half) * rows + lax.rem(tile_ids, per) * TQ
    q_lo = jnp.max(jnp.where(near[None, :] <= qfirst[:, None], near[None, :], 0), axis=1)
    q_hi = jnp.min(jnp.where(near[None, :] <= qfirst[:, None] + TQ - 1, stream, near[None, :]), axis=1)
    limits = jnp.concatenate([near, q_lo, q_hi])
    counted = jnp.sum(block_valid[:, None, :] * (spot[:, None, :] < limits[None, :, None]), axis=-1)
    bounds = counted[:, : DOCS + 1]
    cnt_lo = counted[:, DOCS + 1 : DOCS + 1 + tiles].T
    cnt_hi = counted[:, DOCS + 1 + tiles :].T
    pad64 = jnp.zeros((bounds.shape[0], 128 - DOCS), jnp.int32)
    lo_tab = jnp.concatenate([bounds[:, :DOCS], pad64], axis=1)
    hi_tab = jnp.concatenate([bounds[:, 1:], pad64], axis=1)
    slo_tab = jnp.concatenate([near[:DOCS], pad64[0]])[None, :]
    shi_tab = jnp.concatenate([near[1:], pad64[0]])[None, :]
    some = cnt_hi > cnt_lo
    tlo = jnp.where(some, cnt_lo // TK, 0)
    thi = jnp.where(some, (cnt_hi + TK - 1) // TK, 0)
    tables = (tlo, thi, qfirst, lo_tab, hi_tab, slo_tab, shi_tab)
    before = mm(valid_own.astype(BF), (jnp.arange(rows)[:, None] < jnp.arange(rows)[None, :]).astype(BF)).astype(jnp.int32)
    goes_to = jnp.where(valid_own > 0, before, rows)
    chosen = (goes_to[:, None, :] == jnp.arange(rows, dtype=jnp.int32)[None, :, None]).astype(BF)
    loss_scale = jnp.float32(stream) / count
    keep = (loss_scale * (valid * teacher_ok).astype(F32))[:, None]
    turned = (goes_to[:, :, None] == jnp.arange(rows, dtype=jnp.int32)[None, None, :]).astype(BF)

    x_x, x_y, w_other, chosen, bias_heads, *tables = tie(x_x, x_y, w_other, chosen, bias_heads, *tables)
    x_top, x_bottom = flip(x_y[: rows // 2], 1), flip(x_x[rows // 2 :], 2)

    q_low, kv_own, kv_up, kv_down, w_heads = project(
        who, (tokens, x_x, x_y, x_top, x_bottom), w_mine, w_other, bias_heads[None, :], chosen
    )
    kv_from_left, kv_from_right = shifted(kv_up, "ctx", 1), shifted(kv_down, "ctx", -1)
    w_out, w_in, w_back, kv_own = tie(w_out, w_in, w_back, kv_own)
    wo_pair, win_pair, wback_pair = swap(w_out), swap(w_in), swap(w_back)
    kv_pair = swap(kv_own)
    state = attend(tables, q_low, (kv_own,), 0)
    kv_halo = jnp.concatenate([kv_from_left, kv_from_right], axis=0)
    kv_halo, kv_pair, *state = tie(kv_halo, kv_pair, *state)
    kv_halo_pair = swap(kv_halo)
    state = attend(tables, q_low, (kv_pair,), groups, state)
    o_heads, o_turned, lse = attend(tables, q_low, (kv_halo, kv_halo_pair), 2 * groups, state, last=True)
    o_rel = o_heads.reshape(groups, rows, head_cols)
    o_rest = [flip(o_rel[d], d) for d in range(1, groups)]
    o_heads, x_x, x_y, x_top, x_bottom = tie(o_heads, x_x, x_y, x_top, x_bottom)
    x_all = jnp.concatenate([tokens, x_x, x_y, x_top, x_bottom], axis=0)

    x_all, *o_rest = tie(x_all, *o_rest)
    o_all = jnp.concatenate([o_rel[0], *o_rest], axis=0)

    out, d_resid1, d_parts, act, d_branch, d_pre, hidden_low, d_proj, sums = dense(
        who, o_all, (w_out, wo_pair, w_in, win_pair, w_back, wback_pair), tokens, teacher, cotangent, keep, vec
    )
    d_rel = d_parts.reshape(groups, rows, head_cols)
    tall = w_back.shape[0]
    vector_rows = jnp.concatenate(
        [sums[i, :width].reshape(2, -1) for i in (0, 2, 3, 4, 5, 6)] + [sums[1].reshape(2, -1)], axis=1
    ).reshape(2, -1, width)
    vector_rows = jnp.pad(vector_rows, ((0, 0), (0, 128 - vector_rows.shape[1]), (0, 0))).astype(BF)
    o_rows = o_all.reshape(groups, rows, head_cols)

    def back_part(side):
        return mm(lax.dynamic_slice_in_dim(act, side * tall, tall, 1), d_branch, TN).astype(BF)

    def in_part(side):
        return mm(lax.dynamic_slice_in_dim(hidden_low, side * shard, shard, 1), d_pre, TN).astype(BF)

    def out_part(side):
        both = [
            mm(lax.dynamic_index_in_dim(o_rows, (2 * side + e) ^ uly, 0, keepdims=False), d_proj, TN).astype(BF)
            for e in range(2)
        ]
        stack = jnp.concatenate([*both, lax.dynamic_index_in_dim(vector_rows, side, 0, keepdims=False)], axis=0)
        return jnp.concatenate([stack[i * 128 : (i + 1) * 128] for i in range(4)], axis=1)

    d_rest = [flip(d_rel[d], d) for d in range(1, groups)]
    back_got = swap(back_part(1 - half))
    in_got, out_got = swap(in_part(1 - half)), swap(out_part(1 - half))
    back_mine, in_mine, out_mine = back_part(half), in_part(half), out_part(half)
    back_got, in_got, out_got, back_mine, in_mine, out_mine, *d_rest = tie(
        back_got, in_got, out_got, back_mine, in_mine, out_mine, *d_rest
    )
    wide = w_in.shape[1]
    total = 2 * shard + 128
    am, ao, bm, bo = small_call(
        first_kernel, who, (back_mine, back_got, in_mine, in_got, out_mine, out_got),
        (((total // 4, wide), BF),) * 4, [pltpu.VMEM((total, wide), BF)], "first_stage",
    )
    d_heads = jnp.concatenate([d_rel[0], *d_rest], axis=0)
    d_heads, am, ao, bm, bo = tie(d_heads, am, ao, bm, bo)

    ag, bg = flip(ao, 1), flip(bo, 2)
    args = (tables, q_low, d_heads, o_turned, lse)
    dq0, got_lo, got_hi, delta = attend_back(
        *args, kv_halo_pair, 3 * groups, first=True, cuts=2, name="back_halo_pair"
    )
    got_lo, got_hi, delta = tie(got_lo, got_hi, delta)
    args = (tables, q_low, d_heads, delta, lse)
    got_lo, got_hi = swap(got_lo), swap(got_hi)
    dq1, halo_lo, halo_hi = attend_back(*args, kv_halo, 2 * groups, cuts=2, name="back_halo", size=1_000_000)
    halo_lo, halo_hi, got_lo, got_hi, ag, bg = tie(halo_lo, halo_hi, got_lo, got_hi, ag, bg)

    halo_lo, halo_hi = add(halo_lo, got_lo), add(halo_hi, got_hi)
    am, ao, bm, bo = small_call(
        second_kernel, who, (am, ag, bm, bg), (((total // 8, wide), BF),) * 4,
        [pltpu.VMEM((total // 2, wide), BF)], "second_stage", 12 << 20,
    )
    halo_lo, halo_hi, delta, am, ao, bm, bo = tie(halo_lo, halo_hi, delta, am, ao, bm, bo)
    args = (tables, q_low, d_heads, delta, lse)
    ag, bg = flip(ao, 2), flip(bo, 1)
    from_left, from_right = shifted(halo_hi, "ctx", 1), shifted(halo_lo, "ctx", -1)
    dq2, dkv_pair = attend_back(*args, kv_pair, groups, name="back_pair")
    dkv_pair, ag, bg, from_left, from_right = tie(dkv_pair, ag, bg, from_left, from_right)

    (line,) = small_call(both_kernel, who, (am, ag, bm, bg), (((total // 4, wide), BF),), [], "third_stage", 12 << 20)
    line, dkv_pair, delta = tie(line, dkv_pair, delta)
    args = (tables, q_low, d_heads, delta, lse)
    line = exchange(line, "ctx")
    pair_got = swap(dkv_pair)
    dq3, dkv_own = attend_back(*args, kv_own, 0, name="back_own")
    dkv_own, line, pair_got = tie(dkv_own, line, pair_got)
    line = sum_parts(line, spans)
    line, dkv_own = tie(line, dkv_own)
    line = spread_rows(line, "ctx")

    d_all, d_sums, dx_own, give_x, give_y, left_next, right_next = finish(
        who, (dq0, dq1, dq2, dq3), dkv_own, pair_got, from_left, from_right, turned, w_heads
    )
    d_all, give_x, give_y = tie(d_all, give_x, give_y)
    give_x, give_y = flip(give_x, 1), flip(give_y, 2)
    corner = d_sums[0, 64:].reshape(9, 64)

    def heads_part(side):
        grad = mm(lax.dynamic_slice_in_dim(x_all, side * shard, shard, 1), d_all, TN)
        return lax.dynamic_update_slice(grad, corner, (0, 0)).astype(BF)

    heads_other = heads_part(1 - half)
    heads_got = swap(heads_other)
    heads_mine = heads_part(half)
    heads_sum = add(heads_mine, heads_got)
    line, give_x, give_y, *heads_parts = tie(line, give_x, give_y, *chunks_of(heads_sum, "ctx"))
    heads_sum = sum(part.astype(F32) for part in heads_parts).astype(BF)
    a_near, b_near = line[: total // 8], line[total // 8 :]
    a_near = jnp.concatenate([a_near, flip(a_near, 2)], axis=0)
    b_near = jnp.concatenate([b_near, flip(b_near, 1)], axis=0)
    a_far, b_far = flip(a_near, 1), flip(b_near, 2)
    left_next = flip(add(left_next, give_x[rows:]), 2)
    right_next = flip(add(right_next, give_y[rows:]), 1)
    heads_sum = jnp.concatenate([heads_sum] + [flip(heads_sum, d) for d in range(1, groups)], axis=0)
    heads_all = spread_rows(heads_sum, "ctx").reshape(spans * groups, -1, heads_sum.shape[1])
    grad_in = d_resid1 + dx_own.astype(F32)
    grad_in = grad_in + jnp.concatenate([give_x[:rows].astype(F32), give_y[:rows].astype(F32)], axis=1)
    grad_in = grad_in + jnp.concatenate([left_next.astype(F32), right_next.astype(F32)], axis=1)
    g_back, g_in, g_out, g_vec = join(
        who, (a_near, a_far, b_near, b_far), w_back.shape, w_in.shape, w_out.shape, total
    )
    g_query, g_key, g_value, g_bias = heads_out(who, heads_all)
    g_bias_q = lax.dynamic_slice_in_dim(g_bias[0], half * shard, shard, 0)
    g_bias_v = lax.dynamic_slice_in_dim(g_bias[8], half * shard, shard, 0)
    flat = g_vec.reshape(-1)
    g_bo, g_bb, g_g1, g_s1, g_g2, g_s2 = [flat[i * shard : (i + 1) * shard] for i in range(6)]
    g_bin = flat[6 * shard : 6 * shard + bias_in.shape[0]]
    return (
        out, grad_in, g_query, g_key, g_value, g_out, g_in, g_back,
        g_bias_q, g_bias_v, g_bo, g_bin, g_bb, g_g1, g_s1, g_g2, g_s2,
    )


def solution(mesh):
    placed = (
        P(("ctx", "uly", "fsdp"), None),
        P(("ctx", "uly", "fsdp"), None),
        P(("ctx", "uly", "fsdp"), None),
        P(("ctx", "uly", "fsdp")),
        P(("ctx", "uly", "fsdp")),
        P(),
        P("fsdp", None),
        P("fsdp", None),
        P("fsdp", None),
        P("fsdp", None),
        P("fsdp", None),
        P("fsdp", None),
        P("fsdp"),
        P("fsdp"),
        P("fsdp"),
        P("fsdp"),
        P("fsdp"),
        P("fsdp"),
        P("fsdp"),
        P("fsdp"),
        P("fsdp"),
    )
    return jax.shard_map(
        on_device,
        mesh=mesh,
        in_specs=placed,
        out_specs=(
            P(("ctx", "uly", "fsdp"), None),
            P(("ctx", "uly", "fsdp"), None),
            P("fsdp", None),
            P("fsdp", None),
            P("fsdp", None),
            P("fsdp", None),
            P("fsdp", None),
            P("fsdp", None),
            P("fsdp"),
            P("fsdp"),
            P("fsdp"),
            P("fsdp"),
            P("fsdp"),
            P("fsdp"),
            P("fsdp"),
            P("fsdp"),
            P("fsdp"),
        ),
        check_vma=False,
    )
```

```python
import functools

import jax
import jax.numpy as jnp
from jax import lax
from jax.experimental import pallas as pl
from jax.experimental.pallas import tpu as pltpu
from jax.sharding import PartitionSpec as P

HEADS = 12
HD = 64
BLK = 512
TQ = 256
TK = 256
DOCS = 64
FFB = 1536
GRANT = 63 << 20
MASKED = -1e30
BF = jnp.bfloat16
F32 = jnp.float32
NT = (((1,), (1,)), ((), ()))
NN = (((1,), (0,)), ((), ()))
TN = (((0,), (0,)), ((), ()))


def mm(left, right, dims=NN):
    return lax.dot_general(left, right, dims, preferred_element_type=F32)


def whole(shape):
    return pl.BlockSpec(shape, lambda *_: (0,) * len(shape), pipeline_mode=pl.Buffered(1))


def sweep(total, step, work):
    def one(i, _):
        work(pl.multiple_of(i * step, step))
        return 0

    lax.fori_loop(0, total // step, one, 0)


def cost(flops, moved, special=0):
    return pl.CostEstimate(flops=flops, bytes_accessed=moved, transcendentals=special)


def lane_ids(rows):
    return lax.broadcasted_iota(jnp.int32, (rows, 128), 1)


def build_keys(sources, slot0, lo_ref, hi_ref, kaug, transposed, low_half):
    per = BLK // TK
    for at, kv in enumerate(sources):

        def one(j, _, at=at, kv=kv):
            rows = pl.ds(pl.multiple_of(j * TK, TK), TK)
            tile = at * (kv.shape[0] // TK) + j
            slot = slot0 + at * (kv.shape[0] // BLK) + j // per
            out = pl.ds(pl.multiple_of(tile * TK, TK), TK)
            rank = lax.broadcasted_iota(jnp.int32, (TK, 128), 0) + lax.rem(j, per) * TK
            inside = (rank >= lo_ref[pl.ds(slot, 1), :]) & (rank < hi_ref[pl.ds(slot, 1), :])
            bias = jnp.where(inside, 0.0, MASKED).astype(BF)
            kaug[out, 0:128] = jnp.where(lane_ids(TK) < 64, bias, kv[rows, 128:256])
            kaug[out, 128:256] = kv[rows, 256:384]
            if low_half:
                transposed[tile] = kv[rows, 0:256].T[0:192]
            else:
                transposed[tile] = kaug[out, :].T[64:256]
            return 0

        lax.fori_loop(0, kv.shape[0] // TK, one, 0)


def stack_queries(q, first, slo_ref, shi_ref, qs):
    lane = lane_ids(TQ)
    spot = lax.broadcasted_iota(jnp.int32, (TQ, 128), 0) + first
    mine = ((spot >= slo_ref[...]) & (spot < shi_ref[...])).astype(F32).astype(BF)
    zero = jnp.zeros((TQ, 128), BF)
    low, high = q[:, 0:128], q[:, 128:256]
    mark = jnp.where(lane < 64, mine, zero)
    qs[0:TQ, 0:128] = jnp.where(lane < 64, mine, low)
    qs[TQ : 2 * TQ, 0:128] = mark
    qs[2 * TQ :, 0:128] = mark
    qs[0:TQ, 128:256] = zero
    qs[TQ : 2 * TQ, 128:256] = jnp.where(lane < 64, high, zero)
    qs[2 * TQ :, 128:256] = jnp.where(lane < 64, zero, high)


def attend_kernel(*refs, slot0, count, resume, last):
    tlo, thi, qfirst, q_ref = refs[:4]
    sources = refs[4 : 4 + count]
    lo_ref, hi_ref, slo_ref, shi_ref = refs[4 + count : 8 + count]
    at = 8 + count
    if resume:
        acc_in, stat_in = refs[at : at + 2]
        at += 2
    if last:
        o_ref, ot_ref, lse_ref = refs[at : at + 3]
        at += 3
    else:
        acc_out, stat_out = refs[at : at + 2]
        at += 2
    kaug, vt, qs, acc, m_s, l_s = refs[at:]
    i = pl.program_id(0)

    @pl.when(i == 0)
    def _():
        build_keys(sources, slot0, lo_ref, hi_ref, kaug, vt, True)

    slots = count * sources[0].shape[0] // BLK
    per = BLK // TK
    stack_queries(q_ref[...], qfirst[i], slo_ref, shi_ref, qs)
    if resume:
        m_s[...] = stat_in[0, 0:1, :]
        l_s[...] = stat_in[0, 1:2, :]
        acc[...] = acc_in[0]
    else:
        m_s[...] = jnp.full_like(m_s, 2 * MASKED)
        l_s[...] = jnp.zeros_like(l_s)
        acc[...] = jnp.zeros_like(acc)

    def slot_loop(s, _):
        def key_loop(t, _):
            tile = s * per + t
            keys = pl.ds(pl.multiple_of(tile * TK, TK), TK)
            st = mm(kaug[keys, :], qs[...], NT)
            m_old = m_s[...]
            m_new = jnp.maximum(m_old, jnp.max(st, axis=0, keepdims=True))
            fade = jnp.exp(m_old - m_new)
            p = jnp.exp(st - m_new)
            l_s[...] = l_s[...] * fade + jnp.sum(p, axis=0, keepdims=True)
            m_s[...] = m_new
            low = p.astype(BF)
            for h in range(3):
                cols = slice(h * TQ, (h + 1) * TQ)
                part = slice(h * HD, (h + 1) * HD)
                acc[part, :] = acc[part, :] * fade[:, cols] + mm(vt[tile, part, :], low[:, cols])
            return 0

        return lax.fori_loop(tlo[i, slot0 + s], thi[i, slot0 + s], key_loop, 0)

    lax.fori_loop(0, slots, slot_loop, 0)
    if last:
        total = l_s[...]
        for h in range(3):
            cols = slice(h * TQ, (h + 1) * TQ)
            part = slice(h * HD, (h + 1) * HD)
            acc[part, :] = acc[part, :] / total[:, cols]
        ot_ref[0] = acc[...]
        o_ref[...] = acc[...].T.astype(BF)
        lse_ref[0] = m_s[...] + jnp.log(total)
    else:
        acc_out[0] = acc[...]
        stat_out[0, 0:1, :] = m_s[...]
        stat_out[0, 1:2, :] = l_s[...]


def rows_spec(shape):
    return pl.BlockSpec((TQ, shape[1]), lambda i, *_: (i, 0))


def tile_spec(shape):
    return pl.BlockSpec((1, *shape[1:]), lambda i, *_: (i, 0, 0))


def attend(tables, q, sources, slot0, state=None, last=False):
    tlo, thi, qfirst, lo, hi, slo, shi = tables
    tiles = q.shape[0] // TQ
    keys = sum(s.shape[0] for s in sources)
    state = tuple(state) if state else ()
    sd = jax.ShapeDtypeStruct
    acc, stat = sd((tiles, 3 * HD, TQ), F32), sd((tiles, 2, 3 * TQ), F32)
    if last:
        o, lse = sd((q.shape[0], 3 * HD), BF), sd((tiles, 1, 3 * TQ), F32)
        outs, out_specs = (o, acc, lse), (rows_spec(o.shape), tile_spec(acc.shape), tile_spec(lse.shape))
    else:
        outs, out_specs = (acc, stat), (tile_spec(acc.shape), tile_spec(stat.shape))
    return pl.pallas_call(
        functools.partial(attend_kernel, slot0=slot0, count=len(sources), resume=bool(state), last=last),
        out_shape=outs,
        grid_spec=pltpu.PrefetchScalarGridSpec(
            num_scalar_prefetch=3,
            grid=(tiles,),
            in_specs=[rows_spec(q.shape)]
            + [whole(x.shape) for x in (*sources, lo, hi, slo, shi)]
            + [tile_spec(x.shape) for x in state],
            out_specs=out_specs,
            scratch_shapes=[
                pltpu.VMEM((keys, 256), BF),
                pltpu.VMEM((keys // TK, 3 * HD, TK), BF),
                pltpu.VMEM((3 * TQ, 256), BF),
                pltpu.VMEM((3 * HD, TQ), F32),
                pltpu.VMEM((1, 3 * TQ), F32),
                pltpu.VMEM((1, 3 * TQ), F32),
            ],
        ),
        compiler_params=pltpu.CompilerParams(vmem_limit_bytes=GRANT),
        cost_estimate=cost(12_000_000_000, 12_000_000, 10_000_000),
        name="attend",
    )(tlo, thi, qfirst, q, *sources, lo, hi, slo, shi, *state)


def attend_back_kernel(
    tlo, thi, qfirst, q_ref, do_ref, ot_ref, lse_ref, kv, lo_ref, hi_ref, slo_ref, shi_ref, dq_ref, *rest,
    slot0, first, cuts,
):
    dkv_refs, rest = rest[:cuts], rest[cuts:]
    if first:
        delta_ref, *rest = rest
    kaug, kt, qs, dos, acc, dk_s, dv_s = rest
    keys_all = kv.shape[0]
    slots = keys_all // BLK
    per = BLK // TK
    i = pl.program_id(0)

    @pl.when(i == 0)
    def _():
        build_keys((kv,), slot0, lo_ref, hi_ref, kaug, kt, False)
        dk_s[...] = jnp.zeros_like(dk_s)
        dv_s[...] = jnp.zeros_like(dv_s)

    stack_queries(q_ref[...], qfirst[i], slo_ref, shi_ref, qs)
    do = do_ref[...]
    lane = lane_ids(TQ)
    zero = jnp.zeros((TQ, 128), BF)
    dos[0:TQ, 0:128] = jnp.where(lane < 64, do[:, 0:128], zero)
    dos[TQ : 2 * TQ, 0:128] = jnp.where(lane < 64, zero, do[:, 0:128])
    dos[2 * TQ :, 0:128] = zero
    dos[0 : 2 * TQ, 128:256] = jnp.zeros((2 * TQ, 128), BF)
    dos[2 * TQ :, 128:192] = do[:, 128:192]
    dos[2 * TQ :, 192:256] = jnp.zeros((TQ, 64), BF)
    if first:
        both = do.astype(F32).T * ot_ref[0]
        delta = jnp.concatenate(
            [jnp.sum(both[h * HD : (h + 1) * HD], axis=0, keepdims=True) for h in range(3)], axis=1
        )
        delta_ref[0] = delta
    else:
        delta = ot_ref[0]
    lse = lse_ref[0]
    acc[...] = jnp.zeros_like(acc)

    def slot_loop(s, _):
        def key_loop(t, _):
            tile = s * per + t
            keys = pl.ds(pl.multiple_of(tile * TK, TK), TK)
            st = mm(kaug[keys, :], qs[...], NT)
            p = jnp.exp(st - lse)
            dp = mm(kv[keys, 0:256], dos[...], NT)
            ds = (p * (dp - delta)).astype(BF)
            dv_s[keys, :] += mm(p.astype(BF), dos[...])
            dk_s[keys, :] += mm(ds, qs[...])
            for h in range(3):
                cols = slice(h * TQ, (h + 1) * TQ)
                acc[(h + 1) * HD : (h + 2) * HD, :] += mm(kt[tile, h * HD : (h + 1) * HD, :], ds[:, cols])
            return 0

        return lax.fori_loop(tlo[i, slot0 + s], thi[i, slot0 + s], key_loop, 0)

    lax.fori_loop(0, slots, slot_loop, 0)
    dq_ref[...] = (acc[...] * HD ** (-0.5)).T.astype(BF)

    @pl.when(i == pl.num_programs(0) - 1)
    def _():
        share = keys_all // cuts
        for j, dkv_ref in enumerate(dkv_refs):

            def write(r, j=j, dkv_ref=dkv_ref):
                at = pl.ds(pl.multiple_of(j * share + r, TK), TK)
                to = pl.ds(r, TK)
                dkv_ref[to, 0:128] = dv_s[at, 0:128].astype(BF)
                dkv_ref[to, 128:256] = jnp.where(lane_ids(TK) < 64, dv_s[at, 128:256], dk_s[at, 0:128]).astype(BF)
                dkv_ref[to, 256:384] = dk_s[at, 128:256].astype(BF)

            sweep(share, TK, write)


def attend_back(tables, q, do, ot, lse, source, slot0, first=False, cuts=1, name="attend_back", size=14_000_000_000):
    tlo, thi, qfirst, lo, hi, slo, shi = tables
    tiles = q.shape[0] // TQ
    keys = source.shape[0]
    sd = jax.ShapeDtypeStruct
    piece = (keys // cuts, source.shape[1])
    outs = (sd(q.shape, BF),) + (sd(piece, BF),) * cuts
    out_specs = (rows_spec(q.shape),) + (whole(piece),) * cuts
    if first:
        outs += (sd(lse.shape, F32),)
        out_specs += (tile_spec(lse.shape),)
    return pl.pallas_call(
        functools.partial(attend_back_kernel, slot0=slot0, first=first, cuts=cuts),
        out_shape=outs,
        grid_spec=pltpu.PrefetchScalarGridSpec(
            num_scalar_prefetch=3,
            grid=(tiles,),
            in_specs=[rows_spec(q.shape), rows_spec(do.shape), tile_spec(ot.shape), tile_spec(lse.shape)]
            + [whole(x.shape) for x in (source, lo, hi, slo, shi)],
            out_specs=out_specs,
            scratch_shapes=[
                pltpu.VMEM((keys, 256), BF),
                pltpu.VMEM((keys // TK, 3 * HD, TK), BF),
                pltpu.VMEM((3 * TQ, 256), BF),
                pltpu.VMEM((3 * TQ, 256), BF),
                pltpu.VMEM((256, TQ), F32),
                pltpu.VMEM((keys, 256), F32),
                pltpu.VMEM((keys, 256), F32),
            ],
        ),
        compiler_params=pltpu.CompilerParams(vmem_limit_bytes=GRANT),
        cost_estimate=cost(size, size // 1000, size // 3000),
        name=name,
    )(tlo, thi, qfirst, q, do, ot, lse, source, lo, hi, slo, shi)


def project_kernel(
    who, x0, x1, x2, x3_top, x3_bottom, w_mine, w_other, bias_ref, chosen, q_ref, kv_ref, up_ref, down_ref, w_ref
):
    tall = w_mine.shape[0]
    rows = x0.shape[0]
    w_ref[pl.ds(pl.multiple_of(who[0] * tall, tall), tall), :] = w_mine[...]
    w_ref[pl.ds(pl.multiple_of((1 - who[0]) * tall, tall), tall), :] = w_other[...]
    for d, x in enumerate((x0, x1, x2, (x3_top, x3_bottom))):
        if d < 3:
            value = mm(x[...], w_ref[...]) + bias_ref[...]
        else:
            value = jnp.concatenate([mm(x[0][...], w_ref[...]), mm(x[1][...], w_ref[...])], axis=0) + bias_ref[...]
        at = slice(d * rows, (d + 1) * rows)
        q_ref[at, :] = (value[:, :256].astype(BF).astype(F32) * HD ** (-0.5)).astype(BF)
        kv = mm(chosen[d], value[:, 256:].astype(BF)).astype(BF)
        kv_ref[at, :] = kv
        inner = slice((d % 2) * rows, (d % 2 + 1) * rows)

        @pl.when(who[2] == d // 2)
        def _(inner=inner, kv=kv):
            down_ref[inner, :] = kv

        @pl.when(who[2] != d // 2)
        def _(inner=inner, kv=kv):
            up_ref[inner, :] = kv


def project(who, xs, w_mine, w_other, bias, chosen):
    sd = jax.ShapeDtypeStruct
    rows, width = xs[0].shape
    cols = w_mine.shape[1]
    ins = (*xs, w_mine, w_other, bias, chosen)
    outs = (
        sd((4 * rows, 256), BF), sd((4 * rows, cols - 256), BF), sd((2 * rows, cols - 256), BF),
        sd((2 * rows, cols - 256), BF), sd((width, cols), BF),
    )
    return pl.pallas_call(
        project_kernel,
        out_shape=outs,
        grid_spec=pltpu.PrefetchScalarGridSpec(
            num_scalar_prefetch=1,
            grid=(1,),
            in_specs=[whole(a.shape) for a in ins],
            out_specs=tuple(whole(a.shape) for a in outs),
        ),
        compiler_params=pltpu.CompilerParams(vmem_limit_bytes=24 << 20),
        cost_estimate=cost(3_000_000_000, 12_000_000),
        name="project",
    )(who, *ins)


def row_mean(v):
    return jnp.sum(v, axis=-1, keepdims=True) * (1.0 / v.shape[-1])

def dense_kernel(
    who, o_ref, wo_a, wo_b, win_a, win_b, wback_a, wback_b, x_ref, teacher_ref, cot_ref, keep_ref, vec_ref,
    out_ref, dres_ref, dparts_ref, act_ref, dbr_ref, dpre_ref, hid_ref, dproj_ref, sums_ref,
    wo, win, wback, xh, inv, hidden, gp, acc, sems, *, FB
):
    rows, width = x_ref.shape
    groups = o_ref.shape[0] // rows
    part = width // groups
    units = win.shape[1]
    wo_loads, win_loads, wback_loads = [], [], []
    for i in range(2):
        side = who[0] if i == 0 else 1 - who[0]
        for e in range(groups // 2):
            to = pl.multiple_of(((side * (groups // 2) + e) ^ who[1]) * part, part)
            wo_loads.append(
                pltpu.make_async_copy((wo_a, wo_b)[i].at[pl.ds(e * part, part)], wo.at[pl.ds(to, part)], sems.at[2 * i + e])
            )
        for j, (pieces, target, held) in enumerate((((win_a, win_b), win, win_loads), ((wback_a, wback_b), wback, wback_loads))):
            tall = target.shape[0] // 2
            to = pl.multiple_of(side * tall, tall)
            held.append(pltpu.make_async_copy(pieces[i], target.at[pl.ds(to, tall)], sems.at[4 + 2 * i + j]))
    for load in wo_loads + win_loads + wback_loads:
        load.start()
    b_out, b_in, b_back = vec_ref[0:1, 0:width], vec_ref[1:2, :], vec_ref[2:3, 0:width]
    gain1, shift1, gain2, shift2 = (vec_ref[i : i + 1, 0:width] for i in range(3, 7))
    for load in wo_loads:
        load.wait()
    total = x_ref[...].astype(F32) + b_out
    for i in range(groups):
        total += mm(o_ref[i * rows : (i + 1) * rows, :], wo[i * part : (i + 1) * part, :])
    center = total - row_mean(total)
    scale = lax.rsqrt(row_mean(center * center) + 1e-12)
    inv[...] = scale
    unit = center * scale
    xh[...] = unit
    hid = unit * gain1 + shift1
    hidden[...] = hid
    hid_ref[...] = hid.astype(BF)
    acc[...] = jnp.zeros_like(acc)
    for load in win_loads + wback_loads:
        load.wait()

    def up(n, _):
        cols = pl.ds(pl.multiple_of(n * FB, FB), FB)
        pre = mm(hid_ref[...], win[:, cols]) + vec_ref[1:2, cols]
        cdf = 0.5 + 0.5 * lax.erf(pre * 0.7071067811865476)
        act = (pre * cdf).astype(BF)
        act_ref[:, cols] = act
        gp[:, cols] = cdf + pre * (jnp.exp(pre * pre * -0.5) * 0.3989422804014327)
        acc[...] += mm(act, wback[cols, :])
        return 0

    lax.fori_loop(0, units // FB, up, 0, unroll=False)
    total = hidden[...] + acc[...] + b_back
    center = total - row_mean(total)
    scale = lax.rsqrt(row_mean(center * center) + 1e-12)
    unit = center * scale
    result = unit * gain2 + shift2
    out_ref[...] = result.astype(BF)
    grad = cot_ref[...].astype(F32) + keep_ref[...] * (result - teacher_ref[...].astype(F32))
    def put(row, value):
        sums_ref[row : row + 1, 0 : value.shape[1]] = value
    put(5, jnp.sum(grad * unit, axis=0, keepdims=True))
    put(6, jnp.sum(grad, axis=0, keepdims=True))
    grad = grad * gain2
    back = scale * (grad - row_mean(grad) - unit * row_mean(grad * unit))
    acc[...] = back
    low = back.astype(BF)
    dbr_ref[...] = low
    put(2, jnp.sum(low.astype(F32), axis=0, keepdims=True))

    def down(n, _):
        cols = pl.ds(pl.multiple_of(n * FB, FB), FB)
        dpre = (mm(dbr_ref[...], wback[cols, :], NT) * gp[:, cols]).astype(BF)
        dpre_ref[:, cols] = dpre
        sums_ref[1:2, cols] = jnp.sum(dpre.astype(F32), axis=0, keepdims=True)
        acc[...] += mm(dpre, win[:, cols], NT)
        return 0

    lax.fori_loop(0, units // FB, down, 0, unroll=False)
    grad = acc[...]
    unit = xh[...]
    put(3, jnp.sum(grad * unit, axis=0, keepdims=True))
    put(4, jnp.sum(grad, axis=0, keepdims=True))
    grad = grad * gain1
    back = inv[...] * (grad - row_mean(grad) - unit * row_mean(grad * unit))
    dres_ref[...] = back
    low = back.astype(BF)
    dproj_ref[...] = low
    put(0, jnp.sum(low.astype(F32), axis=0, keepdims=True))
    for i in range(groups):
        dparts_ref[i * rows : (i + 1) * rows, :] = mm(low, wo[i * part : (i + 1) * part, :], NT).astype(BF)


def dense(who, o, weights, x, teacher, cot, keep, vec):
    rows, width = x.shape
    units = vec.shape[1]
    sd = jax.ShapeDtypeStruct
    outs = (
        sd((rows, width), BF), sd((rows, width), F32), sd(o.shape, BF), sd((rows, units), BF), sd((rows, width), BF),
        sd((rows, units), BF), sd((rows, width), BF), sd((rows, width), BF), sd((8, units), F32),
    )
    ins = (o, *weights, x, teacher, cot, keep, vec)
    stay = pl.BlockSpec(memory_space=pl.ANY)
    return pl.pallas_call(
        functools.partial(dense_kernel, FB=FFB),
        out_shape=outs,
        grid_spec=pltpu.PrefetchScalarGridSpec(
            num_scalar_prefetch=1,
            grid=(1,),
            in_specs=[whole(o.shape)] + [stay] * 6 + [whole(a.shape) for a in ins[7:]],
            out_specs=tuple(whole(a.shape) for a in outs),
            scratch_shapes=[
                pltpu.VMEM((width, width), BF), pltpu.VMEM((width, units), BF), pltpu.VMEM((units, width), BF),
                pltpu.VMEM((rows, width), F32), pltpu.VMEM((rows, 1), F32), pltpu.VMEM((rows, width), F32),
                pltpu.VMEM((rows, units), F32), pltpu.VMEM((rows, width), F32), pltpu.SemaphoreType.DMA((8,)),
            ],
        ),
        compiler_params=pltpu.CompilerParams(vmem_limit_bytes=GRANT),
        cost_estimate=cost(12_000_000_000, 30_000_000, 4_000_000),
        name="dense",
    )(who, *ins)


def finish_kernel(
    who, dq0, dq1, dq2, own_ref, pair_ref, left_ref, right_ref, turn_ref, w_ref,
    all_ref, sums_ref, dx_ref, gx_ref, gy_ref, next_left, next_right,
):
    d = pl.program_id(0)
    rows, width = dx_ref.shape
    cut = width // 2

    @pl.when(d == 0)
    def _():
        sums_ref[...] = jnp.zeros_like(sums_ref)

    back = own_ref[...].astype(F32) + pair_ref[...].astype(F32)
    back += jnp.where((d // 2) == who[2], left_ref[...], right_ref[...]).astype(F32)
    tok = mm(turn_ref[0], back.astype(BF)).astype(BF)
    dq = sum(ref[...].astype(F32) for ref in (dq0, dq1, dq2)).astype(BF)
    all_ref[:, 0:256] = dq
    all_ref[:, 256:640] = tok
    sums_ref[0:1, 0:256] += jnp.sum(dq.astype(F32), axis=0, keepdims=True)
    sums_ref[0:1, 256:640] += jnp.sum(tok.astype(F32), axis=0, keepdims=True)
    part = mm(all_ref[...], w_ref[...], NT).astype(BF)

    @pl.when(d == 0)
    def _():
        dx_ref[...] = part

    @pl.when(d == 1)
    def _():
        gx_ref[0:rows, :] = part[:, :cut]
        next_right[...] = part[:, cut:]

    @pl.when(d == 2)
    def _():
        next_left[...] = part[:, :cut]
        gy_ref[0:rows, :] = part[:, cut:]

    @pl.when(d == 3)
    def _():
        gx_ref[rows:, :] = part[:, :cut]
        gy_ref[rows:, :] = part[:, cut:]


def finish(who, dqs, own, pair, left, right, turn, w_heads):
    sd = jax.ShapeDtypeStruct
    rows, width = turn.shape[1], w_heads.shape[0]
    cols = dqs[0].shape[1] + own.shape[1]
    ins = (*dqs, own, pair, left, right, turn, w_heads)
    shapes = ((rows, width), (2 * rows, width // 2), (2 * rows, width // 2), (rows, width // 2), (rows, width // 2))
    outs = (sd((4 * rows, cols), BF), sd((8, cols), F32)) + tuple(sd(s, BF) for s in shapes)

    def by_block(shape):
        return pl.BlockSpec((rows, shape[1]), lambda d, *_: (d, 0))

    def by_pair(shape):
        return pl.BlockSpec((rows, shape[1]), lambda d, *_: (lax.rem(d, 2), 0))

    return pl.pallas_call(
        finish_kernel,
        out_shape=outs,
        grid_spec=pltpu.PrefetchScalarGridSpec(
            num_scalar_prefetch=1,
            grid=(4,),
            in_specs=[by_block(a.shape) for a in ins[:5]]
            + [by_pair(a.shape) for a in ins[5:7]]
            + [pl.BlockSpec((1, rows, rows), lambda d, *_: (d, 0, 0)), whole(w_heads.shape)],
            out_specs=(by_block(outs[0].shape), whole(outs[1].shape)) + tuple(whole(s) for s in shapes),
        ),
        compiler_params=pltpu.CompilerParams(vmem_limit_bytes=GRANT),
        cost_estimate=cost(3_000_000_000, 16_000_000),
        name="finish",
    )(who, *ins)


def part_out(who, held, am, ao, bm, bo, sides):
    part = am.shape[0]
    for mine, other, side, base in ((am, ao, sides[0], 0), (bm, bo, sides[1], 2 * part)):

        def move(r, mine=mine, other=other, side=side, base=base):
            mine[pl.ds(r, 16), :] = held[pl.ds(pl.multiple_of(base + side * part + r, 16), 16), :]
            other[pl.ds(r, 16), :] = held[pl.ds(pl.multiple_of(base + (1 - side) * part + r, 16), 16), :]

        sweep(part, 16, move)


def plus(left, right, at):
    return (left[at, :].astype(F32) + right[at, :].astype(F32)).astype(BF)


def back_first_kernel(who, left, right, am, ao, bm, bo, held):
    def work(r):
        held[pl.ds(r, 16), :] = plus(left, right, pl.ds(r, 16))

    sweep(held.shape[0], 16, work)
    part_out(who, held, am, ao, bm, bo, (lax.rem(who[1], 2), who[1] // 2))


def in_first_kernel(who, in_a, in_b, out_a, out_b, am, ao, bm, bo, held):
    tall = in_a.shape[0]

    def upper(r):
        held[pl.ds(r, 16), :] = plus(in_a, in_b, pl.ds(r, 16))

    def lower(r):
        held[pl.ds(pl.multiple_of(tall + r, 16), 16), :] = plus(out_a, out_b, pl.ds(r, 16))

    sweep(tall, 16, upper)
    sweep(out_a.shape[0], 16, lower)
    part_out(who, held, am, ao, bm, bo, (lax.rem(who[1], 2), who[1] // 2))


def both_kernel(who, a_mine, a_got, b_mine, b_got, both):
    del who
    part = a_mine.shape[0]

    def work(r):
        both[pl.ds(r, 16), :] = plus(a_mine, a_got, pl.ds(r, 16))
        both[pl.ds(pl.multiple_of(part + r, 16), 16), :] = plus(b_mine, b_got, pl.ds(r, 16))

    sweep(part, 16, work)


def second_kernel(who, fa, fag, fb, fbg, ia, iag, ib, ibg, am, ao, bm, bo):
    width = fa.shape[1]
    part = fa.shape[0] // 2
    low = part // 4
    rows = ia.shape[0] // 2
    s1, s2 = lax.rem(who[1], 2), who[1] // 2
    for mine, other, side, f, fg, i, ig in ((am, ao, s2, fa, fag, ia, iag), (bm, bo, s1, fb, fbg, ib, ibg)):
        for out, at in ((mine, side), (other, 1 - side)):

            def upper(r, out=out, at=at, f=f, fg=fg):
                for k in range(4):
                    frm = pl.ds(pl.multiple_of(at * part + k * low + r, 16), 16)
                    out[pl.ds(r, 16), k * width : (k + 1) * width] = plus(f, fg, frm)

            def lower(r, out=out, at=at, i=i, ig=ig):
                frm = pl.ds(pl.multiple_of(at * rows + r, 16), 16)
                out[pl.ds(pl.multiple_of(low + r, 16), 16), :] = plus(i, ig, frm)

            sweep(low, 16, upper)
            sweep(rows, 16, lower)


def join_kernel(who, a, b, c, d, back_ref, in_ref, out_ref, vec_ref, held, tall_held):
    step = pl.program_id(0)

    @pl.when(step == 0)
    def _():
        gather_pieces(who, (a, b, c, d), held, tall_held)

    tall, width = back_ref.shape
    cols = pl.ds(pl.multiple_of(step * width, 128), width)
    back_ref[...] = tall_held[pl.ds(pl.multiple_of(step * tall, 16), tall), :].astype(F32)
    rows = in_ref.shape[0]
    in_ref[...] = held[pl.ds(pl.multiple_of(step * rows, 16), rows), :].astype(F32)

    @pl.when(step < 3)
    def _():
        out_ref[...] = held[tall:, cols].astype(F32)

    @pl.when(step == 3)
    def _():
        vec_ref[...] = held[tall : tall + 16, 3 * width :].astype(F32)


def gather_pieces(who, pieces, held, tall_held):
    s1, s2 = lax.rem(who[1], 2), who[1] // 2
    part = pieces[0].shape[0] // 2
    width = tall_held.shape[1]
    low = tall_held.shape[0] // 32
    rows = held.shape[0] // 8
    for at, ref in enumerate(pieces):
        color, i = at // 2, at % 2
        for j in range(2):
            spot = (s1 ^ i) * 2 + (s2 ^ j) if color == 0 else 4 + (s2 ^ i) * 2 + (s1 ^ j)

            def upper(r, spot=spot, ref=ref, j=j):
                for k in range(4):
                    to = pl.ds(pl.multiple_of((spot * 4 + k) * low + r, 16), 16)
                    tall_held[to, :] = ref[pl.ds(pl.multiple_of(j * part + r, 16), 16), k * width : (k + 1) * width]

            def lower(r, spot=spot, ref=ref, j=j):
                frm = pl.ds(pl.multiple_of(j * part + low + r, 16), 16)
                held[pl.ds(pl.multiple_of(spot * rows + r, 16), 16), :] = ref[frm, :]

            sweep(low, 16, upper)
            sweep(rows, 16, lower)


def join(who, pieces, back, first, out):
    sd = jax.ShapeDtypeStruct
    tall, width = first[0], back[1]
    outs = (sd(back, F32), sd(first, F32), sd(out, F32), sd((16, width), F32))
    return pl.pallas_call(
        join_kernel,
        out_shape=outs,
        grid_spec=pltpu.PrefetchScalarGridSpec(
            num_scalar_prefetch=1,
            grid=(4,),
            in_specs=[whole(a.shape) for a in pieces],
            out_specs=(
                pl.BlockSpec((tall, width), lambda k, *_: (k, 0)),
                pl.BlockSpec((tall // 4, first[1]), lambda k, *_: (k, 0)),
                pl.BlockSpec((128, width), lambda k, *_: (jnp.minimum(k, 2), 0)),
                whole((16, width)),
            ),
            scratch_shapes=[pltpu.VMEM((tall + 128, first[1]), BF), pltpu.VMEM(back, BF)],
        ),
        compiler_params=pltpu.CompilerParams(vmem_limit_bytes=GRANT),
        cost_estimate=cost(1_000_000, 16_000_000),
        name="join",
    )(who, *pieces)


def small_call(kernel, who, pieces, outs, scratch, name, grant=24 << 20):
    return pl.pallas_call(
        kernel,
        out_shape=tuple(jax.ShapeDtypeStruct(*s) for s in outs),
        grid_spec=pltpu.PrefetchScalarGridSpec(
            num_scalar_prefetch=1,
            grid=(1,),
            in_specs=[whole(a.shape) for a in pieces],
            out_specs=tuple(whole(s[0]) for s in outs),
            scratch_shapes=scratch,
        ),
        compiler_params=pltpu.CompilerParams(vmem_limit_bytes=grant),
        cost_estimate=cost(1_000_000, 9_000_000),
        name=name,
    )(who, *pieces)


def heads_kernel(who, in_ref, q_ref, k_ref, v_ref, bias_ref):
    tall = in_ref.shape[1]
    for c in range(in_ref.shape[0] // 4):
        at = slice(c * tall, (c + 1) * tall)
        for a in range(4):
            cols = slice(a * 192, (a + 1) * 192)
            block = in_ref[c * 4 + (who[1] ^ a)].astype(F32)
            q_ref[at, cols] = block[:, 64:256]
            v_ref[at, cols] = block[:, 256:448]
            k_ref[at, cols] = block[:, 448:640]
            if c == 0:
                for k in range(3):
                    spot = slice(a * 192 + k * 64, a * 192 + (k + 1) * 64)
                    bias_ref[0:1, spot] = block[k : k + 1, 0:64]
                    bias_ref[8:9, spot] = block[k + 3 : k + 4, 0:64]


def heads_out(who, gathered):
    outs = (((384, 768), F32),) * 3 + (((16, 768), F32),)
    return small_call(heads_kernel, who, (gathered,), outs, [], "heads_out")


def swap(block, axis="fsdp"):
    return lax.ppermute(block, axis, [(0, 1), (1, 0)])


def shifted(block, axis, distance):
    devices = range(lax.axis_size(axis))
    route = [(i - distance, i) for i in devices if i - distance in devices]
    return lax.ppermute(block, axis, route)


def flip(block, bit, axis="uly"):
    return lax.ppermute(block, axis, [(i, i ^ bit) for i in range(lax.axis_size(axis))])


def exchange(rows, axis):
    return lax.all_to_all(rows, axis, split_axis=0, concat_axis=0, tiled=True)


def spread_rows(rows, axis):
    count = lax.axis_size(axis)
    return exchange(jnp.broadcast_to(rows[None], (count, *rows.shape)).reshape(-1, rows.shape[1]), axis)


def sum_parts(rows, count):
    got = rows.reshape(count, -1, rows.shape[1])
    return sum(got[i].astype(F32) for i in range(count)).astype(BF)


def sum_scatter(rows, axis):
    return sum_parts(exchange(rows, axis), lax.axis_size(axis))


def add(left, right):
    return (left.astype(F32) + right.astype(F32)).astype(BF)


def line_step(held, bit):
    return flip(held, bit, "ctx")


def line_join(held, got, bit):
    low = (lax.axis_index("ctx") & bit) == 0
    return jnp.stack([jnp.where(low, held, got), jnp.where(low, got, held)], axis=1).reshape(-1, *held.shape[1:])


def line_rest(held, bit):
    while bit > 0:
        held = line_join(held, line_step(held, bit), bit)
        bit //= 2
    return held.reshape(-1, held.shape[2])


def chunks_of(rows, axis):
    count, me = lax.axis_size(axis), lax.axis_index(axis)
    split = rows.reshape(count, -1, rows.shape[1])
    picked = [lax.dynamic_index_in_dim(split, me ^ k, 0, keepdims=False) for k in range(count)]
    return [picked[0]] + [flip(picked[k], k, axis) for k in range(1, count)]


def tie(*values):
    return lax.optimization_barrier(values)


def on_device(
    tokens, teacher, cotangent, valid, teacher_ok, doc_starts, w_query, w_key, w_value, w_out, w_in, w_back,
    bias_query, bias_value, bias_out, bias_in, bias_back, norm1_gain, norm1_bias, norm2_gain, norm2_bias,
):
    groups = lax.axis_size("uly")
    spans = lax.axis_size("ctx")
    rows, width = tokens.shape
    block = rows * groups * 2
    stream = block * spans
    ctx_index = lax.axis_index("ctx")
    uly = lax.axis_index("uly")
    half = lax.axis_index("fsdp")
    head_cols = width // groups
    shard = w_query.shape[0]
    upper = uly // 2

    small = (bias_query, bias_value, bias_out, bias_in, bias_back, norm1_gain, norm1_bias, norm2_gain, norm2_bias)
    valid_one = valid[None, :]
    valid_own = jnp.concatenate([valid_one, flip(valid_one, 1), flip(valid_one, 2), flip(valid_one, 3)], axis=0)
    x_own, valid_own, *small = tie(tokens, valid_own, *small)
    x_x, x_y = flip(x_own, 1), flip(x_own, 2)
    valid_pair = swap(valid_own)
    valid_both = jnp.stack([valid_own, valid_pair]).reshape(2, 2, 2, rows)
    valid_high = lax.dynamic_index_in_dim(valid_both, 1 - upper, 1, keepdims=False)
    valid_low = lax.dynamic_index_in_dim(valid_both, upper, 1, keepdims=False)
    halo = (shifted(valid_high, "ctx", 1), shifted(valid_low, "ctx", -1))
    block_valid = jnp.concatenate([valid_own, valid_pair, halo[0][0], halo[1][0], halo[0][1], halo[1][1]], axis=0)
    count = jnp.full((8, 128), jnp.sum(valid_both), jnp.int32)
    bit = 1
    while bit < spans:
        count = count + flip(count, bit, "ctx")
        bit *= 2
    count = count[0, 0].astype(F32)

    start_col = uly * head_cols
    cut = [lax.dynamic_slice_in_dim(w, start_col, head_cols, 1) for w in (w_query, w_value, w_key)]
    w_mine = jnp.concatenate([jnp.zeros((shard, 256 - head_cols), BF), *cut], axis=1)
    w_other = swap(w_mine)
    who = jnp.stack([half, uly, upper])
    packed = jnp.concatenate(small)
    packed_pair = swap(packed)
    first, second = jnp.where(half == 0, packed, packed_pair), jnp.where(half == 0, packed_pair, packed)
    vectors = []
    at = 0
    for p in small:
        n = p.shape[0]
        vectors.append(jnp.concatenate([first[at : at + n], second[at : at + n]]).astype(F32))
        at += n
    bq_all, bv_all = vectors[:2]
    vec = jnp.stack([jnp.pad(v, (0, w_in.shape[1] - v.shape[0])) for v in vectors[2:]] + [jnp.zeros((w_in.shape[1],), F32)])
    bias_heads = jnp.concatenate(
        [
            jnp.zeros((256 - head_cols,), F32),
            lax.dynamic_slice_in_dim(bq_all, start_col, head_cols, 0),
            lax.dynamic_slice_in_dim(bv_all, start_col, head_cols, 0),
            jnp.zeros((head_cols,), F32),
        ]
    )

    place = jnp.arange(groups, dtype=jnp.int32)
    two = jnp.arange(2, dtype=jnp.int32)
    in_plane = place ^ uly
    halo_group = jnp.concatenate([uly ^ (2 * (1 - upper) + two), uly ^ (2 * upper + two)])
    halo_plane = ctx_index + jnp.where(place < 2, -1, 1)
    plane_of = jnp.concatenate([jnp.full((2 * groups,), 1, jnp.int32) * ctx_index, halo_plane, halo_plane])
    group_of = jnp.concatenate([in_plane, in_plane, halo_group, halo_group])
    mine = jnp.full((groups,), 1, jnp.int32) * half
    core_of = jnp.concatenate([mine, 1 - mine, mine, 1 - mine])
    block_id = plane_of * (2 * groups) + group_of * 2 + core_of
    spot = block_id[:, None] * rows + jnp.arange(rows, dtype=jnp.int32)[None, :]
    edges = jnp.concatenate([doc_starts, jnp.full((DOCS + 1,), stream, jnp.int32)])
    window_first = jnp.maximum(ctx_index * block - block // 2, 0)
    first_doc = jnp.sum((doc_starts <= window_first).astype(jnp.int32)) - 1
    near = lax.dynamic_slice_in_dim(edges, first_doc, DOCS + 1, 0)
    tiles = groups * rows // TQ
    per = rows // TQ
    tile_ids = jnp.arange(tiles, dtype=jnp.int32)
    qfirst = ctx_index * block + (((tile_ids // per) ^ uly) * 2 + half) * rows + lax.rem(tile_ids, per) * TQ
    q_lo = jnp.max(jnp.where(near[None, :] <= qfirst[:, None], near[None, :], 0), axis=1)
    q_hi = jnp.min(jnp.where(near[None, :] <= qfirst[:, None] + TQ - 1, stream, near[None, :]), axis=1)
    limits = jnp.concatenate([near, q_lo, q_hi])
    counted = jnp.sum(block_valid[:, None, :] * (spot[:, None, :] < limits[None, :, None]), axis=-1)
    bounds = counted[:, : DOCS + 1]
    cnt_lo = counted[:, DOCS + 1 : DOCS + 1 + tiles].T
    cnt_hi = counted[:, DOCS + 1 + tiles :].T
    pad64 = jnp.zeros((bounds.shape[0], 128 - DOCS), jnp.int32)
    lo_tab = jnp.concatenate([bounds[:, :DOCS], pad64], axis=1)
    hi_tab = jnp.concatenate([bounds[:, 1:], pad64], axis=1)
    slo_tab = jnp.concatenate([near[:DOCS], pad64[0]])[None, :]
    shi_tab = jnp.concatenate([near[1:], pad64[0]])[None, :]
    some = cnt_hi > cnt_lo
    tlo = jnp.where(some, cnt_lo // TK, 0)
    thi = jnp.where(some, (cnt_hi + TK - 1) // TK, 0)
    tables = (tlo, thi, qfirst, lo_tab, hi_tab, slo_tab, shi_tab)
    before = mm(valid_own.astype(BF), (jnp.arange(rows)[:, None] < jnp.arange(rows)[None, :]).astype(BF)).astype(jnp.int32)
    goes_to = jnp.where(valid_own > 0, before, rows)
    chosen = (goes_to[:, None, :] == jnp.arange(rows, dtype=jnp.int32)[None, :, None]).astype(BF)
    loss_scale = jnp.float32(stream) / count
    keep = (loss_scale * (valid * teacher_ok).astype(F32))[:, None]
    turned = (goes_to[:, :, None] == jnp.arange(rows, dtype=jnp.int32)[None, None, :]).astype(BF)

    x_x, x_y, w_other, chosen, bias_heads, *tables = tie(x_x, x_y, w_other, chosen, bias_heads, *tables)
    x_top, x_bottom = flip(x_y[: rows // 2], 1), flip(x_x[rows // 2 :], 2)

    q_low, kv_own, kv_up, kv_down, w_heads = project(
        who, (tokens, x_x, x_y, x_top, x_bottom), w_mine, w_other, bias_heads[None, :], chosen
    )
    kv_from_left, kv_from_right = shifted(kv_up, "ctx", 1), shifted(kv_down, "ctx", -1)
    w_out, w_in, w_back, kv_own = tie(w_out, w_in, w_back, kv_own)
    wo_pair, win_pair, wback_pair = swap(w_out), swap(w_in), swap(w_back)
    kv_pair = swap(kv_own)
    state = attend(tables, q_low, (kv_own,), 0)
    kv_halo = jnp.concatenate([kv_from_left, kv_from_right], axis=0)
    kv_halo, kv_pair, *state = tie(kv_halo, kv_pair, *state)
    kv_halo_pair = swap(kv_halo)
    state = attend(tables, q_low, (kv_pair,), groups, state)
    o_heads, o_turned, lse = attend(tables, q_low, (kv_halo, kv_halo_pair), 2 * groups, state, last=True)
    o_rel = o_heads.reshape(groups, rows, head_cols)
    o_rest = [flip(o_rel[d], d) for d in range(1, groups)]
    o_heads, kv_from_left, kv_from_right, x_x, x_y, x_top, x_bottom = tie(
        o_heads, kv_from_left, kv_from_right, x_x, x_y, x_top, x_bottom
    )
    x_all = jnp.concatenate([tokens, x_x, x_y, x_top, x_bottom], axis=0)

    kv_halo_all = jnp.concatenate([kv_from_left, kv_from_right, kv_halo_pair], axis=0)
    x_all, kv_halo_all, *o_rest = tie(x_all, kv_halo_all, *o_rest)
    o_all = jnp.concatenate([o_rel[0], *o_rest], axis=0)

    out, d_resid1, d_parts, act, d_branch, d_pre, hidden_low, d_proj, sums = dense(
        who, o_all, (w_out, wo_pair, w_in, win_pair, w_back, wback_pair), tokens, teacher, cotangent, keep, vec
    )
    d_rel = d_parts.reshape(groups, rows, head_cols)
    tall = w_back.shape[0]
    vector_rows = jnp.concatenate(
        [sums[i, :width].reshape(2, -1) for i in (0, 2, 3, 4, 5, 6)] + [sums[1].reshape(2, -1)], axis=1
    ).reshape(2, -1, width)
    vector_rows = jnp.pad(vector_rows, ((0, 0), (0, 128 - vector_rows.shape[1]), (0, 0))).astype(BF)
    o_rows = o_all.reshape(groups, rows, head_cols)

    def back_part(side):
        return mm(lax.dynamic_slice_in_dim(act, side * tall, tall, 1), d_branch, TN).astype(BF)

    def in_part(side):
        return mm(lax.dynamic_slice_in_dim(hidden_low, side * shard, shard, 1), d_pre, TN).astype(BF)

    def out_part(side):
        both = [
            mm(lax.dynamic_index_in_dim(o_rows, (2 * side + e) ^ uly, 0, keepdims=False), d_proj, TN).astype(BF)
            for e in range(2)
        ]
        stack = jnp.concatenate([*both, lax.dynamic_index_in_dim(vector_rows, side, 0, keepdims=False)], axis=0)
        return jnp.concatenate([stack[i * 128 : (i + 1) * 128] for i in range(4)], axis=1)

    d_rest = [flip(d_rel[d], d) for d in range(1, groups)]
    wide = w_in.shape[1]
    total = 2 * shard + 128
    back_got = swap(back_part(1 - half))
    back_mine = back_part(half)
    in_other, out_other = in_part(1 - half), out_part(1 - half)
    back_got, back_mine, in_other, out_other, *d_rest = tie(back_got, back_mine, in_other, out_other, *d_rest)
    fam, fao, fbm, fbo = small_call(
        back_first_kernel, who, (back_mine, back_got), (((shard, width), BF),) * 4,
        [pltpu.VMEM(back_mine.shape, BF)], "back_first",
    )
    fao, fbo, in_other, out_other = tie(fao, fbo, in_other, out_other)
    fag, fbg = flip(fao, 1), flip(fbo, 2)
    in_got, out_got = swap(in_other), swap(out_other)
    in_mine, out_mine = in_part(half), out_part(half)
    d_heads = jnp.concatenate([d_rel[0], *d_rest], axis=0)
    in_got, out_got, in_mine, out_mine, d_heads, fag, fbg = tie(in_got, out_got, in_mine, out_mine, d_heads, fag, fbg)
    iam, iao, ibm, ibo = small_call(
        in_first_kernel, who, (in_mine, in_got, out_mine, out_got), ((((shard + 128) // 4, wide), BF),) * 4,
        [pltpu.VMEM((shard + 128, wide), BF)], "in_first",
    )
    d_heads, iao, ibo = tie(d_heads, iao, ibo)

    iag, ibg = flip(iao, 1), flip(ibo, 2)
    args = (tables, q_low, d_heads, o_turned, lse)
    dq0, halo_lo, halo_hi, got_lo, got_hi, delta = attend_back(
        *args, kv_halo_all, 2 * groups, first=True, cuts=4, name="back_halo"
    )
    halo_lo, halo_hi, got_lo, got_hi, delta, iag, ibg = tie(halo_lo, halo_hi, got_lo, got_hi, delta, iag, ibg)
    got_lo, got_hi = swap(got_lo), swap(got_hi)
    am, ao, bm, bo = small_call(
        second_kernel, who, (fam, fag, fbm, fbg, iam, iag, ibm, ibg), (((total // 8, wide), BF),) * 4, [],
        "second_stage", 20 << 20,
    )
    am, ao, bm, bo, got_lo, got_hi = tie(am, ao, bm, bo, got_lo, got_hi)
    halo_lo, halo_hi = add(halo_lo, got_lo), add(halo_hi, got_hi)
    halo_lo, halo_hi, delta, am, ao, bm, bo = tie(halo_lo, halo_hi, delta, am, ao, bm, bo)
    args = (tables, q_low, d_heads, delta, lse)
    ag, bg = flip(ao, 2), flip(bo, 1)
    from_left, from_right = shifted(halo_hi, "ctx", 1), shifted(halo_lo, "ctx", -1)
    dq1, dkv_pair = attend_back(*args, kv_pair, groups, name="back_pair")
    dkv_pair, ag, bg, from_left, from_right = tie(dkv_pair, ag, bg, from_left, from_right)

    (line,) = small_call(both_kernel, who, (am, ag, bm, bg), (((total // 4, wide), BF),), [], "third_stage", 12 << 20)
    line, dkv_pair, delta = tie(line, dkv_pair, delta)
    args = (tables, q_low, d_heads, delta, lse)
    line = exchange(line, "ctx")
    pair_got = swap(dkv_pair)
    dq2, dkv_own = attend_back(*args, kv_own, 0, name="back_own")
    dkv_own, line, pair_got = tie(dkv_own, line, pair_got)
    line = sum_parts(line, spans)
    line, dkv_own = tie(line, dkv_own)
    line = spread_rows(line, "ctx")

    d_all, d_sums, dx_own, give_x, give_y, left_next, right_next = finish(
        who, (dq0, dq1, dq2), dkv_own, pair_got, from_left, from_right, turned, w_heads
    )
    d_all, give_x, give_y = tie(d_all, give_x, give_y)
    give_x, give_y = flip(give_x, 1), flip(give_y, 2)
    corner = d_sums[0, 64:].reshape(9, 64)

    def heads_part(side):
        grad = mm(lax.dynamic_slice_in_dim(x_all, side * shard, shard, 1), d_all, TN)
        return lax.dynamic_update_slice(grad, corner, (0, 0)).astype(BF)

    heads_other = heads_part(1 - half)
    heads_got = swap(heads_other)
    heads_mine = heads_part(half)
    heads_sum = add(heads_mine, heads_got)
    heads_parts = chunks_of(heads_sum, "ctx")
    line, give_x, give_y = tie(line, give_x, give_y)
    heads_sum = sum(part.astype(F32) for part in heads_parts).astype(BF)
    a_near, b_near = line[: total // 8], line[total // 8 :]
    a_got, b_got = flip(a_near, 2), flip(b_near, 1)
    a_near = jnp.concatenate([a_near, a_got], axis=0)
    b_near = jnp.concatenate([b_near, b_got], axis=0)
    a_far, b_far = flip(a_near, 1), flip(b_near, 2)
    left_next = flip(add(left_next, give_x[rows:]), 2)
    right_next = flip(add(right_next, give_y[rows:]), 1)
    heads_sum = jnp.concatenate([heads_sum] + [flip(heads_sum, d) for d in range(1, groups)], axis=0)
    heads_all = spread_rows(heads_sum, "ctx").reshape(spans * groups, -1, heads_sum.shape[1])
    grad_in = d_resid1 + dx_own.astype(F32)
    grad_in = grad_in + jnp.concatenate([give_x[:rows].astype(F32), give_y[:rows].astype(F32)], axis=1)
    grad_in = grad_in + jnp.concatenate([left_next.astype(F32), right_next.astype(F32)], axis=1)
    g_back, g_in, g_out, g_vec = join(
        who, (a_near, a_far, b_near, b_far), w_back.shape, w_in.shape, w_out.shape
    )
    g_query, g_key, g_value, g_bias = heads_out(who, heads_all)
    g_bias_q = lax.dynamic_slice_in_dim(g_bias[0], half * shard, shard, 0)
    g_bias_v = lax.dynamic_slice_in_dim(g_bias[8], half * shard, shard, 0)
    flat = g_vec.reshape(-1)
    g_bo, g_bb, g_g1, g_s1, g_g2, g_s2 = [flat[i * shard : (i + 1) * shard] for i in range(6)]
    g_bin = flat[6 * shard : 6 * shard + bias_in.shape[0]]
    return (
        out, grad_in, g_query, g_key, g_value, g_out, g_in, g_back,
        g_bias_q, g_bias_v, g_bo, g_bin, g_bb, g_g1, g_s1, g_g2, g_s2,
    )


def solution(mesh):
    placed = (
        P(("ctx", "uly", "fsdp"), None),
        P(("ctx", "uly", "fsdp"), None),
        P(("ctx", "uly", "fsdp"), None),
        P(("ctx", "uly", "fsdp")),
        P(("ctx", "uly", "fsdp")),
        P(),
        P("fsdp", None),
        P("fsdp", None),
        P("fsdp", None),
        P("fsdp", None),
        P("fsdp", None),
        P("fsdp", None),
        P("fsdp"),
        P("fsdp"),
        P("fsdp"),
        P("fsdp"),
        P("fsdp"),
        P("fsdp"),
        P("fsdp"),
        P("fsdp"),
        P("fsdp"),
    )
    return jax.shard_map(
        on_device,
        mesh=mesh,
        in_specs=placed,
        out_specs=(
            P(("ctx", "uly", "fsdp"), None),
            P(("ctx", "uly", "fsdp"), None),
            P("fsdp", None),
            P("fsdp", None),
            P("fsdp", None),
            P("fsdp", None),
            P("fsdp", None),
            P("fsdp", None),
            P("fsdp"),
            P("fsdp"),
            P("fsdp"),
            P("fsdp"),
            P("fsdp"),
            P("fsdp"),
            P("fsdp"),
            P("fsdp"),
            P("fsdp"),
        ),
        check_vma=False,
    )
```

```python
import functools

import jax
import jax.numpy as jnp
from jax import lax
from jax.experimental import pallas as pl
from jax.experimental.pallas import tpu as pltpu
from jax.sharding import PartitionSpec as P

HEADS = 12
HD = 64
BLK = 1024
SPAN = 640
TQ = 512
TK = 256
DOCS = 64
FFB = 1536
GRANT = 63 << 20
MASKED = -1e30
BF = jnp.bfloat16
F32 = jnp.float32
NT = (((1,), (1,)), ((), ()))
NN = (((1,), (0,)), ((), ()))
TN = (((0,), (0,)), ((), ()))


def mm(left, right, dims=NN):
    return lax.dot_general(left, right, dims, preferred_element_type=F32)


def whole(shape):
    return pl.BlockSpec(shape, lambda *_: (0,) * len(shape), pipeline_mode=pl.Buffered(1))


def sweep(total, step, work):
    def one(i, _):
        work(pl.multiple_of(i * step, step))
        return 0

    lax.fori_loop(0, total // step, one, 0)


def cost(flops, moved, special=0):
    return pl.CostEstimate(flops=flops, bytes_accessed=moved, transcendentals=special)


def lane_ids(rows):
    return lax.broadcasted_iota(jnp.int32, (rows, 128), 1)


def build_keys(sources, slot0, lo_ref, hi_ref, kaug, transposed, low_half):
    per = BLK // TK
    for at, kv in enumerate(sources):

        def one(j, _, at=at, kv=kv):
            rows = pl.ds(pl.multiple_of(j * TK, TK), TK)
            tile = at * (kv.shape[0] // TK) + j
            slot = slot0 + at * (kv.shape[0] // BLK) + j // per
            out = pl.ds(pl.multiple_of(tile * TK, TK), TK)
            rank = lax.broadcasted_iota(jnp.int32, (TK, 128), 0) + lax.rem(j, per) * TK
            inside = (rank >= lo_ref[pl.ds(slot, 1), :]) & (rank < hi_ref[pl.ds(slot, 1), :])
            bias = jnp.where(inside, 0.0, MASKED).astype(BF)
            kaug[out, 0:128] = jnp.where(lane_ids(TK) < 64, bias, kv[rows, 128:256])
            kaug[out, 128:256] = kv[rows, 256:384]
            if low_half:
                transposed[tile] = kv[rows, 0:256].T[0:192]
            else:
                transposed[tile] = kaug[out, :].T[64:256]
            return 0

        lax.fori_loop(0, kv.shape[0] // TK, one, 0)


def stack_queries(q, first, slo_ref, shi_ref, qs):
    lane = lane_ids(TQ)
    spot = lax.broadcasted_iota(jnp.int32, (TQ, 128), 0) + first
    mine = ((spot >= slo_ref[...]) & (spot < shi_ref[...])).astype(F32).astype(BF)
    zero = jnp.zeros((TQ, 128), BF)
    low, high = q[:, 0:128], q[:, 128:256]
    mark = jnp.where(lane < 64, mine, zero)
    qs[0:TQ, 0:128] = jnp.where(lane < 64, mine, low)
    qs[TQ : 2 * TQ, 0:128] = mark
    qs[2 * TQ :, 0:128] = mark
    qs[0:TQ, 128:256] = zero
    qs[TQ : 2 * TQ, 128:256] = jnp.where(lane < 64, high, zero)
    qs[2 * TQ :, 128:256] = jnp.where(lane < 64, zero, high)


def attend_kernel(*refs, slot0, count, resume, last):
    tlo, thi, qfirst, q_ref = refs[:4]
    sources = refs[4 : 4 + count]
    lo_ref, hi_ref, slo_ref, shi_ref = refs[4 + count : 8 + count]
    at = 8 + count
    if resume:
        acc_in, stat_in = refs[at : at + 2]
        at += 2
    if last:
        o_ref, ot_ref, lse_ref = refs[at : at + 3]
        at += 3
    else:
        acc_out, stat_out = refs[at : at + 2]
        at += 2
    kaug, vt, qs, acc, m_s, l_s = refs[at:]
    i = pl.program_id(0)

    @pl.when(i == 0)
    def _():
        build_keys(sources, slot0, lo_ref, hi_ref, kaug, vt, True)

    slots = count * sources[0].shape[0] // BLK
    per = BLK // TK
    stack_queries(q_ref[...], qfirst[i], slo_ref, shi_ref, qs)
    if resume:
        m_s[...] = stat_in[0, 0:1, :]
        l_s[...] = stat_in[0, 1:2, :]
        acc[...] = acc_in[0]
    else:
        m_s[...] = jnp.full_like(m_s, 2 * MASKED)
        l_s[...] = jnp.zeros_like(l_s)
        acc[...] = jnp.zeros_like(acc)

    def slot_loop(s, _):
        def key_loop(t, _):
            tile = s * per + t
            keys = pl.ds(pl.multiple_of(tile * TK, TK), TK)
            st = mm(kaug[keys, :], qs[...], NT)
            m_old = m_s[...]
            m_new = jnp.maximum(m_old, jnp.max(st, axis=0, keepdims=True))
            fade = jnp.exp(m_old - m_new)
            p = jnp.exp(st - m_new)
            l_s[...] = l_s[...] * fade + jnp.sum(p, axis=0, keepdims=True)
            m_s[...] = m_new
            low = p.astype(BF)
            for h in range(3):
                cols = slice(h * TQ, (h + 1) * TQ)
                part = slice(h * HD, (h + 1) * HD)
                acc[part, :] = acc[part, :] * fade[:, cols] + mm(vt[tile, part, :], low[:, cols])
            return 0

        return lax.fori_loop(tlo[i, slot0 + s], thi[i, slot0 + s], key_loop, 0)

    lax.fori_loop(0, slots, slot_loop, 0)
    if last:
        total = l_s[...]
        for h in range(3):
            cols = slice(h * TQ, (h + 1) * TQ)
            part = slice(h * HD, (h + 1) * HD)
            acc[part, :] = acc[part, :] / total[:, cols]
        ot_ref[0] = acc[...]
        o_ref[...] = acc[...].T.astype(BF)
        lse_ref[0] = m_s[...] + jnp.log(total)
    else:
        acc_out[0] = acc[...]
        stat_out[0, 0:1, :] = m_s[...]
        stat_out[0, 1:2, :] = l_s[...]


def rows_spec(shape):
    return pl.BlockSpec((TQ, shape[1]), lambda i, *_: (i, 0))


def tile_spec(shape):
    return pl.BlockSpec((1, *shape[1:]), lambda i, *_: (i, 0, 0))


def attend(tables, q, sources, slot0, state=None, last=False):
    tlo, thi, qfirst, lo, hi, slo, shi = tables
    tiles = q.shape[0] // TQ
    keys = sum(s.shape[0] for s in sources)
    state = tuple(state) if state else ()
    sd = jax.ShapeDtypeStruct
    acc, stat = sd((tiles, 3 * HD, TQ), F32), sd((tiles, 2, 3 * TQ), F32)
    if last:
        o, lse = sd((q.shape[0], 3 * HD), BF), sd((tiles, 1, 3 * TQ), F32)
        outs, out_specs = (o, acc, lse), (rows_spec(o.shape), tile_spec(acc.shape), tile_spec(lse.shape))
    else:
        outs, out_specs = (acc, stat), (tile_spec(acc.shape), tile_spec(stat.shape))
    return pl.pallas_call(
        functools.partial(attend_kernel, slot0=slot0, count=len(sources), resume=bool(state), last=last),
        out_shape=outs,
        grid_spec=pltpu.PrefetchScalarGridSpec(
            num_scalar_prefetch=3,
            grid=(tiles,),
            in_specs=[rows_spec(q.shape)]
            + [whole(x.shape) for x in (*sources, lo, hi, slo, shi)]
            + [tile_spec(x.shape) for x in state],
            out_specs=out_specs,
            scratch_shapes=[
                pltpu.VMEM((keys, 256), BF),
                pltpu.VMEM((keys // TK, 3 * HD, TK), BF),
                pltpu.VMEM((3 * TQ, 256), BF),
                pltpu.VMEM((3 * HD, TQ), F32),
                pltpu.VMEM((1, 3 * TQ), F32),
                pltpu.VMEM((1, 3 * TQ), F32),
            ],
        ),
        compiler_params=pltpu.CompilerParams(vmem_limit_bytes=GRANT),
        cost_estimate=cost(12_000_000_000, 12_000_000, 10_000_000),
        name="attend",
    )(tlo, thi, qfirst, q, *sources, lo, hi, slo, shi, *state)


def attend_back_kernel(
    tlo, thi, qfirst, q_ref, do_ref, ot_ref, lse_ref, kv, lo_ref, hi_ref, slo_ref, shi_ref, dq_ref, *rest,
    slot0, first, cuts,
):
    dkv_refs, rest = rest[:cuts], rest[cuts:]
    if first:
        delta_ref, *rest = rest
    kaug, kt, qs, dos, acc, dk_s, dv_s = rest
    keys_all = kv.shape[0]
    slots = keys_all // BLK
    per = BLK // TK
    i = pl.program_id(0)

    @pl.when(i == 0)
    def _():
        build_keys((kv,), slot0, lo_ref, hi_ref, kaug, kt, False)
        dk_s[...] = jnp.zeros_like(dk_s)
        dv_s[...] = jnp.zeros_like(dv_s)

    stack_queries(q_ref[...], qfirst[i], slo_ref, shi_ref, qs)
    do = do_ref[...]
    lane = lane_ids(TQ)
    zero = jnp.zeros((TQ, 128), BF)
    dos[0:TQ, 0:128] = jnp.where(lane < 64, do[:, 0:128], zero)
    dos[TQ : 2 * TQ, 0:128] = jnp.where(lane < 64, zero, do[:, 0:128])
    dos[2 * TQ :, 0:128] = zero
    dos[0 : 2 * TQ, 128:256] = jnp.zeros((2 * TQ, 128), BF)
    dos[2 * TQ :, 128:192] = do[:, 128:192]
    dos[2 * TQ :, 192:256] = jnp.zeros((TQ, 64), BF)
    if first:
        both = do.astype(F32).T * ot_ref[0]
        delta = jnp.concatenate(
            [jnp.sum(both[h * HD : (h + 1) * HD], axis=0, keepdims=True) for h in range(3)], axis=1
        )
        delta_ref[0] = delta
    else:
        delta = ot_ref[0]
    lse = lse_ref[0]
    acc[...] = jnp.zeros_like(acc)

    def slot_loop(s, _):
        def key_loop(t, _):
            tile = s * per + t
            keys = pl.ds(pl.multiple_of(tile * TK, TK), TK)
            st = mm(kaug[keys, :], qs[...], NT)
            p = jnp.exp(st - lse)
            dp = mm(kv[keys, 0:256], dos[...], NT)
            ds = (p * (dp - delta)).astype(BF)
            dv_s[keys, :] += mm(p.astype(BF), dos[...])
            dk_s[keys, :] += mm(ds, qs[...])
            for h in range(3):
                cols = slice(h * TQ, (h + 1) * TQ)
                acc[(h + 1) * HD : (h + 2) * HD, :] += mm(kt[tile, h * HD : (h + 1) * HD, :], ds[:, cols])
            return 0

        return lax.fori_loop(tlo[i, slot0 + s], thi[i, slot0 + s], key_loop, 0)

    lax.fori_loop(0, slots, slot_loop, 0)
    dq_ref[...] = (acc[...] * HD ** (-0.5)).T.astype(BF)

    @pl.when(i == pl.num_programs(0) - 1)
    def _():
        share = keys_all // cuts
        for j, dkv_ref in enumerate(dkv_refs):

            def write(r, j=j, dkv_ref=dkv_ref):
                at = pl.ds(pl.multiple_of(j * share + r, TK), TK)
                to = pl.ds(r, TK)
                dkv_ref[to, 0:128] = dv_s[at, 0:128].astype(BF)
                dkv_ref[to, 128:256] = jnp.where(lane_ids(TK) < 64, dv_s[at, 128:256], dk_s[at, 0:128]).astype(BF)
                dkv_ref[to, 256:384] = dk_s[at, 128:256].astype(BF)

            sweep(share, TK, write)


def attend_back(tables, q, do, ot, lse, source, slot0, first=False, cuts=1, name="attend_back", size=14_000_000_000):
    tlo, thi, qfirst, lo, hi, slo, shi = tables
    tiles = q.shape[0] // TQ
    keys = source.shape[0]
    sd = jax.ShapeDtypeStruct
    piece = (keys // cuts, source.shape[1])
    outs = (sd(q.shape, BF),) + (sd(piece, BF),) * cuts
    out_specs = (rows_spec(q.shape),) + (whole(piece),) * cuts
    if first:
        outs += (sd(lse.shape, F32),)
        out_specs += (tile_spec(lse.shape),)
    return pl.pallas_call(
        functools.partial(attend_back_kernel, slot0=slot0, first=first, cuts=cuts),
        out_shape=outs,
        grid_spec=pltpu.PrefetchScalarGridSpec(
            num_scalar_prefetch=3,
            grid=(tiles,),
            in_specs=[rows_spec(q.shape), rows_spec(do.shape), tile_spec(ot.shape), tile_spec(lse.shape)]
            + [whole(x.shape) for x in (source, lo, hi, slo, shi)],
            out_specs=out_specs,
            scratch_shapes=[
                pltpu.VMEM((keys, 256), BF),
                pltpu.VMEM((keys // TK, 3 * HD, TK), BF),
                pltpu.VMEM((3 * TQ, 256), BF),
                pltpu.VMEM((3 * TQ, 256), BF),
                pltpu.VMEM((256, TQ), F32),
                pltpu.VMEM((keys, 256), F32),
                pltpu.VMEM((keys, 256), F32),
            ],
        ),
        compiler_params=pltpu.CompilerParams(vmem_limit_bytes=GRANT),
        cost_estimate=cost(size, size // 1000, size // 3000),
        name=name,
    )(tlo, thi, qfirst, q, do, ot, lse, source, lo, hi, slo, shi)


def project_kernel(
    who, x0, x1, x2, x3_top, x3_bottom, w_mine, w_other, bias_ref, chosen, q_ref, kv_ref, up_ref, down_ref, w_ref, held
):
    tall = w_mine.shape[0]
    rows = x0.shape[0]
    w_ref[pl.ds(pl.multiple_of(who[0] * tall, tall), tall), :] = w_mine[...]
    w_ref[pl.ds(pl.multiple_of((1 - who[0]) * tall, tall), tall), :] = w_other[...]
    held[...] = jnp.zeros_like(held)
    for d, x in enumerate((x0, x1, x2, (x3_top, x3_bottom))):
        if d < 3:
            value = mm(x[...], w_ref[...]) + bias_ref[...]
        else:
            value = jnp.concatenate([mm(x[0][...], w_ref[...]), mm(x[1][...], w_ref[...])], axis=0) + bias_ref[...]
        at = slice(d * rows, (d + 1) * rows)
        q_ref[at, :] = (value[:, :256].astype(BF).astype(F32) * HD ** (-0.5)).astype(BF)
        to = pl.ds(pl.multiple_of(who[3 + d], 16), SPAN)
        held[to, :] += mm(chosen[d], value[:, 256:].astype(BF))
    kv_ref[...] = held[0 : 2 * BLK, :].astype(BF)
    down_ref[...] = kv_ref[0:BLK, :]
    up_ref[...] = kv_ref[BLK:, :]


def project(who, xs, w_mine, w_other, bias, chosen):
    sd = jax.ShapeDtypeStruct
    rows, width = xs[0].shape
    cols = w_mine.shape[1]
    ins = (*xs, w_mine, w_other, bias, chosen)
    outs = (
        sd((4 * rows, 256), BF), sd((4 * rows, cols - 256), BF), sd((2 * rows, cols - 256), BF),
        sd((2 * rows, cols - 256), BF), sd((width, cols), BF),
    )
    return pl.pallas_call(
        project_kernel,
        out_shape=outs,
        grid_spec=pltpu.PrefetchScalarGridSpec(
            num_scalar_prefetch=1,
            grid=(1,),
            in_specs=[whole(a.shape) for a in ins],
            out_specs=tuple(whole(a.shape) for a in outs),
            scratch_shapes=[pltpu.VMEM((2 * BLK + 128, cols - 256), F32)],
        ),
        compiler_params=pltpu.CompilerParams(vmem_limit_bytes=24 << 20),
        cost_estimate=cost(3_000_000_000, 12_000_000),
        name="project",
    )(who, *ins)


def row_mean(v):
    return jnp.sum(v, axis=-1, keepdims=True) * (1.0 / v.shape[-1])

def dense_kernel(
    who, o_ref, wo_a, wo_b, win_a, win_b, wback_a, wback_b, x_ref, teacher_ref, cot_ref, keep_ref, vec_ref,
    out_ref, dres_ref, dparts_ref, act_ref, dbr_ref, dpre_ref, hid_ref, dproj_ref, sums_ref,
    wo, win, wback, xh, inv, hidden, gp, acc, sems, *, FB
):
    rows, width = x_ref.shape
    groups = o_ref.shape[0] // rows
    part = width // groups
    units = win.shape[1]
    wo_loads, win_loads, wback_loads = [], [], []
    for i in range(2):
        side = who[0] if i == 0 else 1 - who[0]
        for e in range(groups // 2):
            to = pl.multiple_of(((side * (groups // 2) + e) ^ who[1]) * part, part)
            wo_loads.append(
                pltpu.make_async_copy((wo_a, wo_b)[i].at[pl.ds(e * part, part)], wo.at[pl.ds(to, part)], sems.at[2 * i + e])
            )
        for j, (pieces, target, held) in enumerate((((win_a, win_b), win, win_loads), ((wback_a, wback_b), wback, wback_loads))):
            tall = target.shape[0] // 2
            to = pl.multiple_of(side * tall, tall)
            held.append(pltpu.make_async_copy(pieces[i], target.at[pl.ds(to, tall)], sems.at[4 + 2 * i + j]))
    for load in wo_loads + win_loads + wback_loads:
        load.start()
    b_out, b_in, b_back = vec_ref[0:1, 0:width], vec_ref[1:2, :], vec_ref[2:3, 0:width]
    gain1, shift1, gain2, shift2 = (vec_ref[i : i + 1, 0:width] for i in range(3, 7))
    for load in wo_loads:
        load.wait()
    total = x_ref[...].astype(F32) + b_out
    for i in range(groups):
        total += mm(o_ref[i * rows : (i + 1) * rows, :], wo[i * part : (i + 1) * part, :])
    center = total - row_mean(total)
    scale = lax.rsqrt(row_mean(center * center) + 1e-12)
    inv[...] = scale
    unit = center * scale
    xh[...] = unit
    hid = unit * gain1 + shift1
    hidden[...] = hid
    hid_ref[...] = hid.astype(BF)
    acc[...] = jnp.zeros_like(acc)
    for load in win_loads + wback_loads:
        load.wait()

    def up(n, _):
        cols = pl.ds(pl.multiple_of(n * FB, FB), FB)
        pre = mm(hid_ref[...], win[:, cols]) + vec_ref[1:2, cols]
        cdf = 0.5 + 0.5 * lax.erf(pre * 0.7071067811865476)
        act = (pre * cdf).astype(BF)
        act_ref[:, cols] = act
        gp[:, cols] = cdf + pre * (jnp.exp(pre * pre * -0.5) * 0.3989422804014327)
        acc[...] += mm(act, wback[cols, :])
        return 0

    lax.fori_loop(0, units // FB, up, 0, unroll=False)
    total = hidden[...] + acc[...] + b_back
    center = total - row_mean(total)
    scale = lax.rsqrt(row_mean(center * center) + 1e-12)
    unit = center * scale
    result = unit * gain2 + shift2
    out_ref[...] = result.astype(BF)
    grad = cot_ref[...].astype(F32) + keep_ref[...] * (result - teacher_ref[...].astype(F32))
    def put(row, value):
        sums_ref[row : row + 1, 0 : value.shape[1]] = value
    put(5, jnp.sum(grad * unit, axis=0, keepdims=True))
    put(6, jnp.sum(grad, axis=0, keepdims=True))
    grad = grad * gain2
    back = scale * (grad - row_mean(grad) - unit * row_mean(grad * unit))
    acc[...] = back
    low = back.astype(BF)
    dbr_ref[...] = low
    put(2, jnp.sum(low.astype(F32), axis=0, keepdims=True))

    def down(n, _):
        cols = pl.ds(pl.multiple_of(n * FB, FB), FB)
        dpre = (mm(dbr_ref[...], wback[cols, :], NT) * gp[:, cols]).astype(BF)
        dpre_ref[:, cols] = dpre
        sums_ref[1:2, cols] = jnp.sum(dpre.astype(F32), axis=0, keepdims=True)
        acc[...] += mm(dpre, win[:, cols], NT)
        return 0

    lax.fori_loop(0, units // FB, down, 0, unroll=False)
    grad = acc[...]
    unit = xh[...]
    put(3, jnp.sum(grad * unit, axis=0, keepdims=True))
    put(4, jnp.sum(grad, axis=0, keepdims=True))
    grad = grad * gain1
    back = inv[...] * (grad - row_mean(grad) - unit * row_mean(grad * unit))
    dres_ref[...] = back
    low = back.astype(BF)
    dproj_ref[...] = low
    put(0, jnp.sum(low.astype(F32), axis=0, keepdims=True))
    for i in range(groups):
        dparts_ref[i * rows : (i + 1) * rows, :] = mm(low, wo[i * part : (i + 1) * part, :], NT).astype(BF)


def dense(who, o, weights, x, teacher, cot, keep, vec):
    rows, width = x.shape
    units = vec.shape[1]
    sd = jax.ShapeDtypeStruct
    outs = (
        sd((rows, width), BF), sd((rows, width), F32), sd(o.shape, BF), sd((rows, units), BF), sd((rows, width), BF),
        sd((rows, units), BF), sd((rows, width), BF), sd((rows, width), BF), sd((8, units), F32),
    )
    ins = (o, *weights, x, teacher, cot, keep, vec)
    stay = pl.BlockSpec(memory_space=pl.ANY)
    return pl.pallas_call(
        functools.partial(dense_kernel, FB=FFB),
        out_shape=outs,
        grid_spec=pltpu.PrefetchScalarGridSpec(
            num_scalar_prefetch=1,
            grid=(1,),
            in_specs=[whole(o.shape)] + [stay] * 6 + [whole(a.shape) for a in ins[7:]],
            out_specs=tuple(whole(a.shape) for a in outs),
            scratch_shapes=[
                pltpu.VMEM((width, width), BF), pltpu.VMEM((width, units), BF), pltpu.VMEM((units, width), BF),
                pltpu.VMEM((rows, width), F32), pltpu.VMEM((rows, 1), F32), pltpu.VMEM((rows, width), F32),
                pltpu.VMEM((rows, units), F32), pltpu.VMEM((rows, width), F32), pltpu.SemaphoreType.DMA((8,)),
            ],
        ),
        compiler_params=pltpu.CompilerParams(vmem_limit_bytes=GRANT),
        cost_estimate=cost(12_000_000_000, 30_000_000, 4_000_000),
        name="dense",
    )(who, *ins)


def finish_kernel(
    who, dq0, dq1, dq2, dq3, own_ref, pair_ref, left_ref, right_ref, turn_ref, w_ref,
    all_ref, sums_ref, dx_ref, gx_ref, gy_ref, next_left, next_right, held,
):
    d = pl.program_id(0)
    rows, width = dx_ref.shape
    cut = width // 2

    @pl.when(d == 0)
    def _():
        sums_ref[...] = jnp.zeros_like(sums_ref)
        held[2 * BLK :, :] = jnp.zeros((held.shape[0] - 2 * BLK, held.shape[1]), BF)
        for base, extra in ((0, left_ref), (BLK, right_ref)):

            def gather(r, base=base, extra=extra):
                at = pl.ds(pl.multiple_of(base + r, 128), 128)
                value = own_ref[at, :].astype(F32) + pair_ref[at, :].astype(F32)
                held[at, :] = (value + extra[pl.ds(r, 128), :].astype(F32)).astype(BF)

            sweep(BLK, 128, gather)

    tok = mm(turn_ref[0], held[pl.ds(pl.multiple_of(who[3 + d], 16), SPAN), :]).astype(BF)
    dq = sum(ref[...].astype(F32) for ref in (dq0, dq1, dq2, dq3)).astype(BF)
    all_ref[:, 0:256] = dq
    all_ref[:, 256:640] = tok
    sums_ref[0:1, 0:256] += jnp.sum(dq.astype(F32), axis=0, keepdims=True)
    sums_ref[0:1, 256:640] += jnp.sum(tok.astype(F32), axis=0, keepdims=True)
    part = mm(all_ref[...], w_ref[...], NT).astype(BF)

    @pl.when(d == 0)
    def _():
        dx_ref[...] = part

    @pl.when(d == 1)
    def _():
        gx_ref[0:rows, :] = part[:, :cut]
        next_right[...] = part[:, cut:]

    @pl.when(d == 2)
    def _():
        next_left[...] = part[:, :cut]
        gy_ref[0:rows, :] = part[:, cut:]

    @pl.when(d == 3)
    def _():
        gx_ref[rows:, :] = part[:, :cut]
        gy_ref[rows:, :] = part[:, cut:]


def finish(who, dqs, own, pair, left, right, turn, w_heads):
    sd = jax.ShapeDtypeStruct
    rows, width = turn.shape[1], w_heads.shape[0]
    cols = dqs[0].shape[1] + own.shape[1]
    ins = (*dqs, own, pair, left, right, turn, w_heads)
    shapes = ((rows, width), (2 * rows, width // 2), (2 * rows, width // 2), (rows, width // 2), (rows, width // 2))
    outs = (sd((4 * rows, cols), BF), sd((8, cols), F32)) + tuple(sd(s, BF) for s in shapes)

    def by_block(shape):
        return pl.BlockSpec((rows, shape[1]), lambda d, *_: (d, 0))

    return pl.pallas_call(
        finish_kernel,
        out_shape=outs,
        grid_spec=pltpu.PrefetchScalarGridSpec(
            num_scalar_prefetch=1,
            grid=(4,),
            in_specs=[by_block(a.shape) for a in ins[:4]]
            + [whole(a.shape) for a in ins[4:8]]
            + [pl.BlockSpec((1, *turn.shape[1:]), lambda d, *_: (d, 0, 0)), whole(w_heads.shape)],
            out_specs=(by_block(outs[0].shape), whole(outs[1].shape)) + tuple(whole(s) for s in shapes),
            scratch_shapes=[pltpu.VMEM((2 * BLK + 128, own.shape[1]), BF)],
        ),
        compiler_params=pltpu.CompilerParams(vmem_limit_bytes=GRANT),
        cost_estimate=cost(3_000_000_000, 16_000_000),
        name="finish",
    )(who, *ins)


def part_out(who, held, am, ao, bm, bo, sides):
    part = am.shape[0]
    for mine, other, side, base in ((am, ao, sides[0], 0), (bm, bo, sides[1], 2 * part)):

        def move(r, mine=mine, other=other, side=side, base=base):
            mine[pl.ds(r, 16), :] = held[pl.ds(pl.multiple_of(base + side * part + r, 16), 16), :]
            other[pl.ds(r, 16), :] = held[pl.ds(pl.multiple_of(base + (1 - side) * part + r, 16), 16), :]

        sweep(part, 16, move)


def plus(left, right, at):
    return (left[at, :].astype(F32) + right[at, :].astype(F32)).astype(BF)


def first_kernel(who, back_a, back_b, in_a, in_b, out_a, out_b, am, ao, bm, bo, held):
    width = back_a.shape[1]
    tall = in_a.shape[0]

    def upper(r):
        at = pl.ds(r, 16)
        for k in range(4):
            held[at, k * width : (k + 1) * width] = plus(back_a, back_b, pl.ds(pl.multiple_of(k * tall + r, 16), 16))
        held[pl.ds(pl.multiple_of(tall + r, 16), 16), :] = plus(in_a, in_b, at)

    def lower(r):
        held[pl.ds(pl.multiple_of(2 * tall + r, 16), 16), :] = plus(out_a, out_b, pl.ds(r, 16))

    sweep(tall, 16, upper)
    sweep(out_a.shape[0], 16, lower)
    part_out(who, held, am, ao, bm, bo, (lax.rem(who[1], 2), who[1] // 2))


def both_kernel(who, a_mine, a_got, b_mine, b_got, both):
    del who
    part = a_mine.shape[0]

    def work(r):
        both[pl.ds(r, 16), :] = plus(a_mine, a_got, pl.ds(r, 16))
        both[pl.ds(pl.multiple_of(part + r, 16), 16), :] = plus(b_mine, b_got, pl.ds(r, 16))

    sweep(part, 16, work)


def second_kernel(who, a_mine, a_got, b_mine, b_got, am, ao, bm, bo, held):
    both_kernel(who, a_mine, a_got, b_mine, b_got, held)
    part_out(who, held, am, ao, bm, bo, (who[1] // 2, lax.rem(who[1], 2)))


def join_kernel(who, a, b, c, d, back_ref, in_ref, out_ref, vec_ref, held):
    step = pl.program_id(0)

    @pl.when(step == 0)
    def _():
        gather_pieces(who, (a, b, c, d), held)

    tall = held.shape[0] - 128
    tall, width = tall // 2, back_ref.shape[1]
    cols = pl.ds(pl.multiple_of(step * width, 128), width)
    back_ref[...] = held[0:tall, cols].astype(F32)
    rows = in_ref.shape[0]
    in_ref[...] = held[pl.ds(pl.multiple_of(tall + step * rows, 16), rows), :].astype(F32)

    @pl.when(step < 3)
    def _():
        out_ref[...] = held[2 * tall :, cols].astype(F32)

    @pl.when(step == 3)
    def _():
        vec_ref[...] = held[2 * tall : 2 * tall + 16, 3 * width :].astype(F32)


def gather_pieces(who, pieces, held):
    s1, s2 = lax.rem(who[1], 2), who[1] // 2
    part = pieces[0].shape[0] // 2
    for at, ref in enumerate(pieces):
        color, i = at // 2, at % 2
        for j in range(2):
            spot = (s1 ^ i) * 2 + (s2 ^ j) if color == 0 else 4 + (s2 ^ i) * 2 + (s1 ^ j)

            def move(r, spot=spot, ref=ref, j=j):
                frm = pl.ds(pl.multiple_of(j * part + r, 16), 16)
                held[pl.ds(pl.multiple_of(spot * part + r, 16), 16), :] = ref[frm, :]

            sweep(part, 16, move)

def join(who, pieces, back, first, out, total):
    sd = jax.ShapeDtypeStruct
    tall, width = first[0], back[1]
    outs = (sd(back, F32), sd(first, F32), sd(out, F32), sd((16, width), F32))
    return pl.pallas_call(
        join_kernel,
        out_shape=outs,
        grid_spec=pltpu.PrefetchScalarGridSpec(
            num_scalar_prefetch=1,
            grid=(4,),
            in_specs=[whole(a.shape) for a in pieces],
            out_specs=(
                pl.BlockSpec((tall, width), lambda k, *_: (k, 0)),
                pl.BlockSpec((tall // 4, first[1]), lambda k, *_: (k, 0)),
                pl.BlockSpec((128, width), lambda k, *_: (jnp.minimum(k, 2), 0)),
                whole((16, width)),
            ),
            scratch_shapes=[pltpu.VMEM((total, first[1]), BF)],
        ),
        compiler_params=pltpu.CompilerParams(vmem_limit_bytes=GRANT),
        cost_estimate=cost(1_000_000, 16_000_000),
        name="join",
    )(who, *pieces)


def small_call(kernel, who, pieces, outs, scratch, name, grant=24 << 20):
    return pl.pallas_call(
        kernel,
        out_shape=tuple(jax.ShapeDtypeStruct(*s) for s in outs),
        grid_spec=pltpu.PrefetchScalarGridSpec(
            num_scalar_prefetch=1,
            grid=(1,),
            in_specs=[whole(a.shape) for a in pieces],
            out_specs=tuple(whole(s[0]) for s in outs),
            scratch_shapes=scratch,
        ),
        compiler_params=pltpu.CompilerParams(vmem_limit_bytes=grant),
        cost_estimate=cost(1_000_000, 9_000_000),
        name=name,
    )(who, *pieces)


def heads_kernel(who, in_ref, q_ref, k_ref, v_ref, bias_ref):
    tall = in_ref.shape[1]
    for c in range(in_ref.shape[0] // 4):
        at = slice(c * tall, (c + 1) * tall)
        for a in range(4):
            cols = slice(a * 192, (a + 1) * 192)
            block = in_ref[c * 4 + (who[1] ^ a)].astype(F32)
            q_ref[at, cols] = block[:, 64:256]
            v_ref[at, cols] = block[:, 256:448]
            k_ref[at, cols] = block[:, 448:640]
            if c == 0:
                for k in range(3):
                    spot = slice(a * 192 + k * 64, a * 192 + (k + 1) * 64)
                    bias_ref[0:1, spot] = block[k : k + 1, 0:64]
                    bias_ref[8:9, spot] = block[k + 3 : k + 4, 0:64]


def heads_out(who, gathered):
    outs = (((384, 768), F32),) * 3 + (((16, 768), F32),)
    return small_call(heads_kernel, who, (gathered,), outs, [], "heads_out")


def swap(block, axis="fsdp"):
    return lax.ppermute(block, axis, [(0, 1), (1, 0)])


def shifted(block, axis, distance):
    devices = range(lax.axis_size(axis))
    route = [(i - distance, i) for i in devices if i - distance in devices]
    return lax.ppermute(block, axis, route)


def flip(block, bit, axis="uly"):
    return lax.ppermute(block, axis, [(i, i ^ bit) for i in range(lax.axis_size(axis))])


def exchange(rows, axis):
    return lax.all_to_all(rows, axis, split_axis=0, concat_axis=0, tiled=True)


def spread_rows(rows, axis):
    count = lax.axis_size(axis)
    return exchange(jnp.broadcast_to(rows[None], (count, *rows.shape)).reshape(-1, rows.shape[1]), axis)


def sum_parts(rows, count):
    got = rows.reshape(count, -1, rows.shape[1])
    return sum(got[i].astype(F32) for i in range(count)).astype(BF)


def sum_scatter(rows, axis):
    return sum_parts(exchange(rows, axis), lax.axis_size(axis))


def add(left, right):
    return (left.astype(F32) + right.astype(F32)).astype(BF)


def line_step(held, bit):
    return flip(held, bit, "ctx")


def line_join(held, got, bit):
    low = (lax.axis_index("ctx") & bit) == 0
    return jnp.stack([jnp.where(low, held, got), jnp.where(low, got, held)], axis=1).reshape(-1, *held.shape[1:])


def line_rest(held, bit):
    while bit > 0:
        held = line_join(held, line_step(held, bit), bit)
        bit //= 2
    return held.reshape(-1, held.shape[2])


def chunks_of(rows, axis):
    count, me = lax.axis_size(axis), lax.axis_index(axis)
    split = rows.reshape(count, -1, rows.shape[1])
    picked = [lax.dynamic_index_in_dim(split, me ^ k, 0, keepdims=False) for k in range(count)]
    return [picked[0]] + [flip(picked[k], k, axis) for k in range(1, count)]


def tie(*values):
    return lax.optimization_barrier(values)


def on_device(
    tokens, teacher, cotangent, valid, teacher_ok, doc_starts, w_query, w_key, w_value, w_out, w_in, w_back,
    bias_query, bias_value, bias_out, bias_in, bias_back, norm1_gain, norm1_bias, norm2_gain, norm2_bias,
):
    groups = lax.axis_size("uly")
    spans = lax.axis_size("ctx")
    rows, width = tokens.shape
    block = rows * groups * 2
    stream = block * spans
    ctx_index = lax.axis_index("ctx")
    uly = lax.axis_index("uly")
    half = lax.axis_index("fsdp")
    head_cols = width // groups
    shard = w_query.shape[0]
    upper = uly // 2

    small = (bias_query, bias_value, bias_out, bias_in, bias_back, norm1_gain, norm1_bias, norm2_gain, norm2_bias)
    valid_one = valid[None, :]
    valid_own = jnp.concatenate([valid_one, flip(valid_one, 1), flip(valid_one, 2), flip(valid_one, 3)], axis=0)
    x_own, valid_own, *small = tie(tokens, valid_own, *small)
    x_x, x_y = flip(x_own, 1), flip(x_own, 2)
    valid_pair = swap(valid_own)
    place = jnp.arange(groups, dtype=jnp.int32)
    in_plane = place ^ uly
    valid_mine = jnp.take(valid_own, in_plane, axis=0).reshape(2, BLK)
    valid_next = jnp.take(valid_pair, in_plane, axis=0).reshape(2, BLK)
    from_low = shifted(jnp.stack([valid_mine[1], valid_next[1]]), "ctx", 1)
    from_high = shifted(jnp.stack([valid_mine[0], valid_next[0]]), "ctx", -1)
    block_valid = jnp.concatenate(
        [valid_mine, valid_next, from_low[:1], from_high[:1], from_low[1:], from_high[1:]], axis=0
    )
    count = jnp.full((8, 128), jnp.sum(valid_mine) + jnp.sum(valid_next), jnp.int32)
    bit = 1
    while bit < spans:
        count = count + flip(count, bit, "ctx")
        bit *= 2
    count = count[0, 0].astype(F32)

    start_col = uly * head_cols
    cut = [lax.dynamic_slice_in_dim(w, start_col, head_cols, 1) for w in (w_query, w_value, w_key)]
    w_mine = jnp.concatenate([jnp.zeros((shard, 256 - head_cols), BF), *cut], axis=1)
    w_other = swap(w_mine)
    packed = jnp.concatenate(small)
    packed_pair = swap(packed)
    first, second = jnp.where(half == 0, packed, packed_pair), jnp.where(half == 0, packed_pair, packed)
    vectors = []
    at = 0
    for p in small:
        n = p.shape[0]
        vectors.append(jnp.concatenate([first[at : at + n], second[at : at + n]]).astype(F32))
        at += n
    bq_all, bv_all = vectors[:2]
    vec = jnp.stack([jnp.pad(v, (0, w_in.shape[1] - v.shape[0])) for v in vectors[2:]] + [jnp.zeros((w_in.shape[1],), F32)])
    bias_heads = jnp.concatenate(
        [
            jnp.zeros((256 - head_cols,), F32),
            lax.dynamic_slice_in_dim(bq_all, start_col, head_cols, 0),
            lax.dynamic_slice_in_dim(bv_all, start_col, head_cols, 0),
            jnp.zeros((head_cols,), F32),
        ]
    )

    step = jnp.asarray([0, 0, 0, 0, -1, 1, -1, 1], jnp.int32)
    side = jnp.asarray([0, 1, 0, 1, 1, 0, 1, 0], jnp.int32)
    swapped = jnp.asarray([0, 0, 1, 1, 0, 0, 1, 1], jnp.int32)
    inner = jnp.arange(BLK, dtype=jnp.int32)
    first_block = (ctx_index + step) * (2 * groups) + side * groups + (half ^ swapped)
    spot = (first_block[:, None] + 2 * (inner // rows)[None, :]) * rows + lax.rem(inner, rows)[None, :]
    edges = jnp.concatenate([doc_starts, jnp.full((DOCS + 1,), stream, jnp.int32)])
    window_first = jnp.maximum(ctx_index * block - block // 2, 0)
    first_doc = jnp.sum((doc_starts <= window_first).astype(jnp.int32)) - 1
    near = lax.dynamic_slice_in_dim(edges, first_doc, DOCS + 1, 0)
    tiles = groups * rows // TQ
    per = rows // TQ
    tile_ids = jnp.arange(tiles, dtype=jnp.int32)
    qfirst = ctx_index * block + (((tile_ids // per) ^ uly) * 2 + half) * rows + lax.rem(tile_ids, per) * TQ
    q_lo = jnp.max(jnp.where(near[None, :] <= qfirst[:, None], near[None, :], 0), axis=1)
    q_hi = jnp.min(jnp.where(near[None, :] <= qfirst[:, None] + TQ - 1, stream, near[None, :]), axis=1)
    limits = jnp.concatenate([near, q_lo, q_hi])
    counted = jnp.sum(block_valid[:, None, :] * (spot[:, None, :] < limits[None, :, None]), axis=-1)
    bounds = counted[:, : DOCS + 1]
    cnt_lo = counted[:, DOCS + 1 : DOCS + 1 + tiles].T
    cnt_hi = counted[:, DOCS + 1 + tiles :].T
    pad64 = jnp.zeros((bounds.shape[0], 128 - DOCS), jnp.int32)
    lo_tab = jnp.concatenate([bounds[:, :DOCS], pad64], axis=1)
    hi_tab = jnp.concatenate([bounds[:, 1:], pad64], axis=1)
    slo_tab = jnp.concatenate([near[:DOCS], pad64[0]])[None, :]
    shi_tab = jnp.concatenate([near[1:], pad64[0]])[None, :]
    some = cnt_hi > cnt_lo
    tlo = jnp.where(some, cnt_lo // TK, 0)
    thi = jnp.where(some, (cnt_hi + TK - 1) // TK, 0)
    tables = (tlo, thi, qfirst, lo_tab, hi_tab, slo_tab, shi_tab)
    before = mm(valid_own.astype(BF), (jnp.arange(rows)[:, None] < jnp.arange(rows)[None, :]).astype(BF)).astype(jnp.int32)
    filled = jnp.sum(valid_own, axis=1)
    shift = jnp.where(lax.rem(in_plane, 2) == 1, jnp.take(filled, place ^ 1), 0)
    base = (in_plane // 2) * BLK + (shift // 16) * 16
    goes_to = jnp.where(valid_own > 0, before + lax.rem(shift, 16)[:, None], 2 * BLK)
    ranks = jnp.arange(SPAN, dtype=jnp.int32)
    chosen = (goes_to[:, None, :] == ranks[None, :, None]).astype(BF)
    turned = (goes_to[:, :, None] == ranks[None, None, :]).astype(BF)
    who = jnp.concatenate([jnp.stack([half, uly, upper]).astype(jnp.int32), base])
    loss_scale = jnp.float32(stream) / count
    keep = (loss_scale * (valid * teacher_ok).astype(F32))[:, None]

    x_x, x_y, w_other, chosen, bias_heads, *tables = tie(x_x, x_y, w_other, chosen, bias_heads, *tables)
    x_top, x_bottom = flip(x_y[: rows // 2], 1), flip(x_x[rows // 2 :], 2)

    q_low, kv_own, kv_up, kv_down, w_heads = project(
        who, (tokens, x_x, x_y, x_top, x_bottom), w_mine, w_other, bias_heads[None, :], chosen
    )
    kv_from_left, kv_from_right = shifted(kv_up, "ctx", 1), shifted(kv_down, "ctx", -1)
    w_out, w_in, w_back, kv_own = tie(w_out, w_in, w_back, kv_own)
    wo_pair, win_pair, wback_pair = swap(w_out), swap(w_in), swap(w_back)
    kv_pair = swap(kv_own)
    state = attend(tables, q_low, (kv_own,), 0)
    kv_halo = jnp.concatenate([kv_from_left, kv_from_right], axis=0)
    kv_halo, kv_pair, *state = tie(kv_halo, kv_pair, *state)
    kv_halo_pair = swap(kv_halo)
    state = attend(tables, q_low, (kv_pair,), 2, state)
    o_heads, o_turned, lse = attend(tables, q_low, (kv_halo, kv_halo_pair), 4, state, last=True)
    o_rel = o_heads.reshape(groups, rows, head_cols)
    o_rest = [flip(o_rel[d], d) for d in range(1, groups)]
    o_heads, x_x, x_y, x_top, x_bottom = tie(o_heads, x_x, x_y, x_top, x_bottom)
    x_all = jnp.concatenate([tokens, x_x, x_y, x_top, x_bottom], axis=0)

    x_all, *o_rest = tie(x_all, *o_rest)
    o_all = jnp.concatenate([o_rel[0], *o_rest], axis=0)

    out, d_resid1, d_parts, act, d_branch, d_pre, hidden_low, d_proj, sums = dense(
        who, o_all, (w_out, wo_pair, w_in, win_pair, w_back, wback_pair), tokens, teacher, cotangent, keep, vec
    )
    d_rel = d_parts.reshape(groups, rows, head_cols)
    tall = w_back.shape[0]
    vector_rows = jnp.concatenate(
        [sums[i, :width].reshape(2, -1) for i in (0, 2, 3, 4, 5, 6)] + [sums[1].reshape(2, -1)], axis=1
    ).reshape(2, -1, width)
    vector_rows = jnp.pad(vector_rows, ((0, 0), (0, 128 - vector_rows.shape[1]), (0, 0))).astype(BF)
    o_rows = o_all.reshape(groups, rows, head_cols)

    def back_part(side):
        return mm(lax.dynamic_slice_in_dim(act, side * tall, tall, 1), d_branch, TN).astype(BF)

    def in_part(side):
        return mm(lax.dynamic_slice_in_dim(hidden_low, side * shard, shard, 1), d_pre, TN).astype(BF)

    def out_part(side):
        both = [
            mm(lax.dynamic_index_in_dim(o_rows, (2 * side + e) ^ uly, 0, keepdims=False), d_proj, TN).astype(BF)
            for e in range(2)
        ]
        stack = jnp.concatenate([*both, lax.dynamic_index_in_dim(vector_rows, side, 0, keepdims=False)], axis=0)
        return jnp.concatenate([stack[i * 128 : (i + 1) * 128] for i in range(4)], axis=1)

    d_rest = [flip(d_rel[d], d) for d in range(1, groups)]
    back_got = swap(back_part(1 - half))
    in_got, out_got = swap(in_part(1 - half)), swap(out_part(1 - half))
    back_mine, in_mine, out_mine = back_part(half), in_part(half), out_part(half)
    back_got, in_got, out_got, back_mine, in_mine, out_mine, *d_rest = tie(
        back_got, in_got, out_got, back_mine, in_mine, out_mine, *d_rest
    )
    wide = w_in.shape[1]
    total = 2 * shard + 128
    am, ao, bm, bo = small_call(
        first_kernel, who, (back_mine, back_got, in_mine, in_got, out_mine, out_got),
        (((total // 4, wide), BF),) * 4, [pltpu.VMEM((total, wide), BF)], "first_stage",
    )
    d_heads = jnp.concatenate([d_rel[0], *d_rest], axis=0)
    d_heads, am, ao, bm, bo = tie(d_heads, am, ao, bm, bo)

    ag, bg = flip(ao, 1), flip(bo, 2)
    args = (tables, q_low, d_heads, o_turned, lse)
    dq0, got_lo, got_hi, delta = attend_back(
        *args, kv_halo_pair, 6, first=True, cuts=2, name="back_halo_pair"
    )
    got_lo, got_hi, delta = tie(got_lo, got_hi, delta)
    args = (tables, q_low, d_heads, delta, lse)
    got_lo, got_hi = swap(got_lo), swap(got_hi)
    dq1, halo_lo, halo_hi = attend_back(*args, kv_halo, 4, cuts=2, name="back_halo", size=1_000_000)
    halo_lo, halo_hi, got_lo, got_hi, ag, bg = tie(halo_lo, halo_hi, got_lo, got_hi, ag, bg)

    halo_lo, halo_hi = add(halo_lo, got_lo), add(halo_hi, got_hi)
    am, ao, bm, bo = small_call(
        second_kernel, who, (am, ag, bm, bg), (((total // 8, wide), BF),) * 4,
        [pltpu.VMEM((total // 2, wide), BF)], "second_stage", 12 << 20,
    )
    halo_lo, halo_hi, delta, am, ao, bm, bo = tie(halo_lo, halo_hi, delta, am, ao, bm, bo)
    args = (tables, q_low, d_heads, delta, lse)
    ag, bg = flip(ao, 2), flip(bo, 1)
    from_left, from_right = shifted(halo_hi, "ctx", 1), shifted(halo_lo, "ctx", -1)
    dq2, dkv_pair = attend_back(*args, kv_pair, 2, name="back_pair")
    dkv_pair, ag, bg, from_left, from_right = tie(dkv_pair, ag, bg, from_left, from_right)

    (line,) = small_call(both_kernel, who, (am, ag, bm, bg), (((total // 4, wide), BF),), [], "third_stage", 12 << 20)
    line, dkv_pair, delta = tie(line, dkv_pair, delta)
    args = (tables, q_low, d_heads, delta, lse)
    line = exchange(line, "ctx")
    pair_got = swap(dkv_pair)
    dq3, dkv_own = attend_back(*args, kv_own, 0, name="back_own")
    dkv_own, line, pair_got = tie(dkv_own, line, pair_got)
    line = sum_parts(line, spans)
    line, dkv_own = tie(line, dkv_own)
    line = spread_rows(line, "ctx")

    d_all, d_sums, dx_own, give_x, give_y, left_next, right_next = finish(
        who, (dq0, dq1, dq2, dq3), dkv_own, pair_got, from_left, from_right, turned, w_heads
    )
    d_all, give_x, give_y = tie(d_all, give_x, give_y)
    give_x, give_y = flip(give_x, 1), flip(give_y, 2)
    corner = d_sums[0, 64:].reshape(9, 64)

    def heads_part(side):
        grad = mm(lax.dynamic_slice_in_dim(x_all, side * shard, shard, 1), d_all, TN)
        return lax.dynamic_update_slice(grad, corner, (0, 0)).astype(BF)

    heads_other = heads_part(1 - half)
    heads_got = swap(heads_other)
    heads_mine = heads_part(half)
    heads_sum = add(heads_mine, heads_got)
    line, give_x, give_y, *heads_parts = tie(line, give_x, give_y, *chunks_of(heads_sum, "ctx"))
    heads_sum = sum(part.astype(F32) for part in heads_parts).astype(BF)
    a_near, b_near = line[: total // 8], line[total // 8 :]
    a_near = jnp.concatenate([a_near, flip(a_near, 2)], axis=0)
    b_near = jnp.concatenate([b_near, flip(b_near, 1)], axis=0)
    a_far, b_far = flip(a_near, 1), flip(b_near, 2)
    left_next = flip(add(left_next, give_x[rows:]), 2)
    right_next = flip(add(right_next, give_y[rows:]), 1)
    heads_sum = jnp.concatenate([heads_sum] + [flip(heads_sum, d) for d in range(1, groups)], axis=0)
    heads_all = spread_rows(heads_sum, "ctx").reshape(spans * groups, -1, heads_sum.shape[1])
    grad_in = d_resid1 + dx_own.astype(F32)
    grad_in = grad_in + jnp.concatenate([give_x[:rows].astype(F32), give_y[:rows].astype(F32)], axis=1)
    grad_in = grad_in + jnp.concatenate([left_next.astype(F32), right_next.astype(F32)], axis=1)
    g_back, g_in, g_out, g_vec = join(
        who, (a_near, a_far, b_near, b_far), w_back.shape, w_in.shape, w_out.shape, total
    )
    g_query, g_key, g_value, g_bias = heads_out(who, heads_all)
    g_bias_q = lax.dynamic_slice_in_dim(g_bias[0], half * shard, shard, 0)
    g_bias_v = lax.dynamic_slice_in_dim(g_bias[8], half * shard, shard, 0)
    flat = g_vec.reshape(-1)
    g_bo, g_bb, g_g1, g_s1, g_g2, g_s2 = [flat[i * shard : (i + 1) * shard] for i in range(6)]
    g_bin = flat[6 * shard : 6 * shard + bias_in.shape[0]]
    return (
        out, grad_in, g_query, g_key, g_value, g_out, g_in, g_back,
        g_bias_q, g_bias_v, g_bo, g_bin, g_bb, g_g1, g_s1, g_g2, g_s2,
    )


def solution(mesh):
    placed = (
        P(("ctx", "uly", "fsdp"), None),
        P(("ctx", "uly", "fsdp"), None),
        P(("ctx", "uly", "fsdp"), None),
        P(("ctx", "uly", "fsdp")),
        P(("ctx", "uly", "fsdp")),
        P(),
        P("fsdp", None),
        P("fsdp", None),
        P("fsdp", None),
        P("fsdp", None),
        P("fsdp", None),
        P("fsdp", None),
        P("fsdp"),
        P("fsdp"),
        P("fsdp"),
        P("fsdp"),
        P("fsdp"),
        P("fsdp"),
        P("fsdp"),
        P("fsdp"),
        P("fsdp"),
    )
    return jax.shard_map(
        on_device,
        mesh=mesh,
        in_specs=placed,
        out_specs=(
            P(("ctx", "uly", "fsdp"), None),
            P(("ctx", "uly", "fsdp"), None),
            P("fsdp", None),
            P("fsdp", None),
            P("fsdp", None),
            P("fsdp", None),
            P("fsdp", None),
            P("fsdp", None),
            P("fsdp"),
            P("fsdp"),
            P("fsdp"),
            P("fsdp"),
            P("fsdp"),
            P("fsdp"),
            P("fsdp"),
            P("fsdp"),
            P("fsdp"),
        ),
        check_vma=False,
    )
```

```python
import functools

import jax
import jax.numpy as jnp
from jax import lax
from jax.experimental import pallas as pl
from jax.experimental.pallas import tpu as pltpu
from jax.sharding import PartitionSpec as P

HEADS = 12
HD = 64
BLK = 1024
SPAN = 640
TQ = 512
TK = 256
DOCS = 64
FFB = 1536
GRANT = 63 << 20
MASKED = -1e30
BF = jnp.bfloat16
F32 = jnp.float32
NT = (((1,), (1,)), ((), ()))
NN = (((1,), (0,)), ((), ()))
TN = (((0,), (0,)), ((), ()))


def mm(left, right, dims=NN):
    return lax.dot_general(left, right, dims, preferred_element_type=F32)


def whole(shape):
    return pl.BlockSpec(shape, lambda *_: (0,) * len(shape), pipeline_mode=pl.Buffered(1))


def sweep(total, step, work):
    def one(i, _):
        work(pl.multiple_of(i * step, step))
        return 0

    lax.fori_loop(0, total // step, one, 0)


def cost(flops, moved, special=0):
    return pl.CostEstimate(flops=flops, bytes_accessed=moved, transcendentals=special)


def lane_ids(rows):
    return lax.broadcasted_iota(jnp.int32, (rows, 128), 1)


def build_keys(sources, slot0, lo_ref, hi_ref, kaug, transposed, low_half):
    per = BLK // TK
    for at, kv in enumerate(sources):

        def one(j, _, at=at, kv=kv):
            rows = pl.ds(pl.multiple_of(j * TK, TK), TK)
            tile = at * (kv.shape[0] // TK) + j
            slot = slot0 + at * (kv.shape[0] // BLK) + j // per
            out = pl.ds(pl.multiple_of(tile * TK, TK), TK)
            rank = lax.broadcasted_iota(jnp.int32, (TK, 128), 0) + lax.rem(j, per) * TK
            inside = (rank >= lo_ref[pl.ds(slot, 1), :]) & (rank < hi_ref[pl.ds(slot, 1), :])
            bias = jnp.where(inside, 0.0, MASKED).astype(BF)
            kaug[out, 0:128] = jnp.where(lane_ids(TK) < 64, bias, kv[rows, 128:256])
            kaug[out, 128:256] = kv[rows, 256:384]
            if low_half:
                transposed[tile] = kv[rows, 0:256].T[0:192]
            else:
                transposed[tile] = kaug[out, :].T[64:256]
            return 0

        lax.fori_loop(0, kv.shape[0] // TK, one, 0)


def stack_queries(q, first, slo_ref, shi_ref, qs):
    lane = lane_ids(TQ)
    spot = lax.broadcasted_iota(jnp.int32, (TQ, 128), 0) + first
    mine = ((spot >= slo_ref[...]) & (spot < shi_ref[...])).astype(F32).astype(BF)
    zero = jnp.zeros((TQ, 128), BF)
    low, high = q[:, 0:128], q[:, 128:256]
    mark = jnp.where(lane < 64, mine, zero)
    qs[0:TQ, 0:128] = jnp.where(lane < 64, mine, low)
    qs[TQ : 2 * TQ, 0:128] = mark
    qs[2 * TQ :, 0:128] = mark
    qs[0:TQ, 128:256] = zero
    qs[TQ : 2 * TQ, 128:256] = jnp.where(lane < 64, high, zero)
    qs[2 * TQ :, 128:256] = jnp.where(lane < 64, zero, high)


def attend_kernel(*refs, slot0, count, resume, last):
    tlo, thi, qfirst, q_ref = refs[:4]
    sources = refs[4 : 4 + count]
    lo_ref, hi_ref, slo_ref, shi_ref = refs[4 + count : 8 + count]
    at = 8 + count
    if resume:
        acc_in, stat_in = refs[at : at + 2]
        at += 2
    if last:
        o_ref, ot_ref, lse_ref = refs[at : at + 3]
        at += 3
    else:
        acc_out, stat_out = refs[at : at + 2]
        at += 2
    kaug, vt, qs, acc, m_s, l_s = refs[at:]
    i = pl.program_id(0)

    @pl.when(i == 0)
    def _():
        build_keys(sources, slot0, lo_ref, hi_ref, kaug, vt, True)

    slots = count * sources[0].shape[0] // BLK
    per = BLK // TK
    stack_queries(q_ref[...], qfirst[i], slo_ref, shi_ref, qs)
    if resume:
        m_s[...] = stat_in[0, 0:1, :]
        l_s[...] = stat_in[0, 1:2, :]
        acc[...] = acc_in[0]
    else:
        m_s[...] = jnp.full_like(m_s, 2 * MASKED)
        l_s[...] = jnp.zeros_like(l_s)
        acc[...] = jnp.zeros_like(acc)

    def slot_loop(s, _):
        def key_loop(t, _):
            tile = s * per + t
            keys = pl.ds(pl.multiple_of(tile * TK, TK), TK)
            st = mm(kaug[keys, :], qs[...], NT)
            m_old = m_s[...]
            m_new = jnp.maximum(m_old, jnp.max(st, axis=0, keepdims=True))
            fade = jnp.exp(m_old - m_new)
            p = jnp.exp(st - m_new)
            l_s[...] = l_s[...] * fade + jnp.sum(p, axis=0, keepdims=True)
            m_s[...] = m_new
            low = p.astype(BF)
            for h in range(3):
                cols = slice(h * TQ, (h + 1) * TQ)
                part = slice(h * HD, (h + 1) * HD)
                acc[part, :] = acc[part, :] * fade[:, cols] + mm(vt[tile, part, :], low[:, cols])
            return 0

        return lax.fori_loop(tlo[i, slot0 + s], thi[i, slot0 + s], key_loop, 0)

    lax.fori_loop(0, slots, slot_loop, 0)
    if last:
        total = l_s[...]
        for h in range(3):
            cols = slice(h * TQ, (h + 1) * TQ)
            part = slice(h * HD, (h + 1) * HD)
            acc[part, :] = acc[part, :] / total[:, cols]
        ot_ref[0] = acc[...]
        o_ref[...] = acc[...].T.astype(BF)
        lse_ref[0] = m_s[...] + jnp.log(total)
    else:
        acc_out[0] = acc[...]
        stat_out[0, 0:1, :] = m_s[...]
        stat_out[0, 1:2, :] = l_s[...]


def rows_spec(shape):
    return pl.BlockSpec((TQ, shape[1]), lambda i, *_: (i, 0))


def tile_spec(shape):
    return pl.BlockSpec((1, *shape[1:]), lambda i, *_: (i, 0, 0))


def attend(tables, q, sources, slot0, state=None, last=False):
    tlo, thi, qfirst, lo, hi, slo, shi = tables
    tiles = q.shape[0] // TQ
    keys = sum(s.shape[0] for s in sources)
    state = tuple(state) if state else ()
    sd = jax.ShapeDtypeStruct
    acc, stat = sd((tiles, 3 * HD, TQ), F32), sd((tiles, 2, 3 * TQ), F32)
    if last:
        o, lse = sd((q.shape[0], 3 * HD), BF), sd((tiles, 1, 3 * TQ), F32)
        outs, out_specs = (o, acc, lse), (rows_spec(o.shape), tile_spec(acc.shape), tile_spec(lse.shape))
    else:
        outs, out_specs = (acc, stat), (tile_spec(acc.shape), tile_spec(stat.shape))
    return pl.pallas_call(
        functools.partial(attend_kernel, slot0=slot0, count=len(sources), resume=bool(state), last=last),
        out_shape=outs,
        grid_spec=pltpu.PrefetchScalarGridSpec(
            num_scalar_prefetch=3,
            grid=(tiles,),
            in_specs=[rows_spec(q.shape)]
            + [whole(x.shape) for x in (*sources, lo, hi, slo, shi)]
            + [tile_spec(x.shape) for x in state],
            out_specs=out_specs,
            scratch_shapes=[
                pltpu.VMEM((keys, 256), BF),
                pltpu.VMEM((keys // TK, 3 * HD, TK), BF),
                pltpu.VMEM((3 * TQ, 256), BF),
                pltpu.VMEM((3 * HD, TQ), F32),
                pltpu.VMEM((1, 3 * TQ), F32),
                pltpu.VMEM((1, 3 * TQ), F32),
            ],
        ),
        compiler_params=pltpu.CompilerParams(vmem_limit_bytes=GRANT),
        cost_estimate=cost(12_000_000_000, 12_000_000, 10_000_000),
        name="attend",
    )(tlo, thi, qfirst, q, *sources, lo, hi, slo, shi, *state)


def attend_back_kernel(
    tlo, thi, qfirst, q_ref, do_ref, ot_ref, lse_ref, kv, lo_ref, hi_ref, slo_ref, shi_ref, dq_ref, *rest,
    slot0, first, cuts,
):
    dkv_refs, rest = rest[:cuts], rest[cuts:]
    if first:
        delta_ref, *rest = rest
    kaug, kt, qs, dos, acc, dk_s, dv_s = rest
    keys_all = kv.shape[0]
    slots = keys_all // BLK
    per = BLK // TK
    i = pl.program_id(0)

    @pl.when(i == 0)
    def _():
        build_keys((kv,), slot0, lo_ref, hi_ref, kaug, kt, False)
        dk_s[...] = jnp.zeros_like(dk_s)
        dv_s[...] = jnp.zeros_like(dv_s)

    stack_queries(q_ref[...], qfirst[i], slo_ref, shi_ref, qs)
    do = do_ref[...]
    lane = lane_ids(TQ)
    zero = jnp.zeros((TQ, 128), BF)
    dos[0:TQ, 0:128] = jnp.where(lane < 64, do[:, 0:128], zero)
    dos[TQ : 2 * TQ, 0:128] = jnp.where(lane < 64, zero, do[:, 0:128])
    dos[2 * TQ :, 0:128] = zero
    dos[0 : 2 * TQ, 128:256] = jnp.zeros((2 * TQ, 128), BF)
    dos[2 * TQ :, 128:192] = do[:, 128:192]
    dos[2 * TQ :, 192:256] = jnp.zeros((TQ, 64), BF)
    if first:
        both = do.astype(F32).T * ot_ref[0]
        delta = jnp.concatenate(
            [jnp.sum(both[h * HD : (h + 1) * HD], axis=0, keepdims=True) for h in range(3)], axis=1
        )
        delta_ref[0] = delta
    else:
        delta = ot_ref[0]
    lse = lse_ref[0]
    acc[...] = jnp.zeros_like(acc)

    def slot_loop(s, _):
        def key_loop(t, _):
            tile = s * per + t
            keys = pl.ds(pl.multiple_of(tile * TK, TK), TK)
            st = mm(kaug[keys, :], qs[...], NT)
            p = jnp.exp(st - lse)
            dp = mm(kv[keys, 0:256], dos[...], NT)
            ds = (p * (dp - delta)).astype(BF)
            dv_s[keys, :] += mm(p.astype(BF), dos[...])
            dk_s[keys, :] += mm(ds, qs[...])
            for h in range(3):
                cols = slice(h * TQ, (h + 1) * TQ)
                acc[(h + 1) * HD : (h + 2) * HD, :] += mm(kt[tile, h * HD : (h + 1) * HD, :], ds[:, cols])
            return 0

        return lax.fori_loop(tlo[i, slot0 + s], thi[i, slot0 + s], key_loop, 0)

    lax.fori_loop(0, slots, slot_loop, 0)
    dq_ref[...] = (acc[...] * HD ** (-0.5)).T.astype(BF)

    @pl.when(i == pl.num_programs(0) - 1)
    def _():
        share = keys_all // cuts
        for j, dkv_ref in enumerate(dkv_refs):

            def write(r, j=j, dkv_ref=dkv_ref):
                at = pl.ds(pl.multiple_of(j * share + r, TK), TK)
                to = pl.ds(r, TK)
                dkv_ref[to, 0:128] = dv_s[at, 0:128].astype(BF)
                dkv_ref[to, 128:256] = jnp.where(lane_ids(TK) < 64, dv_s[at, 128:256], dk_s[at, 0:128]).astype(BF)
                dkv_ref[to, 256:384] = dk_s[at, 128:256].astype(BF)

            sweep(share, TK, write)


def attend_back(tables, q, do, ot, lse, source, slot0, first=False, cuts=1, name="attend_back", size=14_000_000_000):
    tlo, thi, qfirst, lo, hi, slo, shi = tables
    tiles = q.shape[0] // TQ
    keys = source.shape[0]
    sd = jax.ShapeDtypeStruct
    piece = (keys // cuts, source.shape[1])
    outs = (sd(q.shape, BF),) + (sd(piece, BF),) * cuts
    out_specs = (rows_spec(q.shape),) + (whole(piece),) * cuts
    if first:
        outs += (sd(lse.shape, F32),)
        out_specs += (tile_spec(lse.shape),)
    return pl.pallas_call(
        functools.partial(attend_back_kernel, slot0=slot0, first=first, cuts=cuts),
        out_shape=outs,
        grid_spec=pltpu.PrefetchScalarGridSpec(
            num_scalar_prefetch=3,
            grid=(tiles,),
            in_specs=[rows_spec(q.shape), rows_spec(do.shape), tile_spec(ot.shape), tile_spec(lse.shape)]
            + [whole(x.shape) for x in (source, lo, hi, slo, shi)],
            out_specs=out_specs,
            scratch_shapes=[
                pltpu.VMEM((keys, 256), BF),
                pltpu.VMEM((keys // TK, 3 * HD, TK), BF),
                pltpu.VMEM((3 * TQ, 256), BF),
                pltpu.VMEM((3 * TQ, 256), BF),
                pltpu.VMEM((256, TQ), F32),
                pltpu.VMEM((keys, 256), F32),
                pltpu.VMEM((keys, 256), F32),
            ],
        ),
        compiler_params=pltpu.CompilerParams(vmem_limit_bytes=GRANT),
        cost_estimate=cost(size, size // 1000, size // 3000),
        name=name,
    )(tlo, thi, qfirst, q, do, ot, lse, source, lo, hi, slo, shi)


def project_kernel(
    who, x0, x1, x2, x3_top, x3_bottom, w_mine, w_other, bias_ref, chosen, q_ref, kv_ref, up_ref, down_ref, w_ref, held
):
    tall = w_mine.shape[0]
    rows = x0.shape[0]
    w_ref[pl.ds(pl.multiple_of(who[0] * tall, tall), tall), :] = w_mine[...]
    w_ref[pl.ds(pl.multiple_of((1 - who[0]) * tall, tall), tall), :] = w_other[...]
    held[...] = jnp.zeros_like(held)
    for d, x in enumerate((x0, x1, x2, (x3_top, x3_bottom))):
        if d < 3:
            value = mm(x[...], w_ref[...]) + bias_ref[...]
        else:
            value = jnp.concatenate([mm(x[0][...], w_ref[...]), mm(x[1][...], w_ref[...])], axis=0) + bias_ref[...]
        at = slice(d * rows, (d + 1) * rows)
        q_ref[at, :] = (value[:, :256].astype(BF).astype(F32) * HD ** (-0.5)).astype(BF)
        to = pl.ds(pl.multiple_of(who[3 + d], 16), SPAN)
        held[to, :] += mm(chosen[d], value[:, 256:].astype(BF))
    kv_ref[...] = held[0 : 2 * BLK, :].astype(BF)
    down_ref[...] = kv_ref[0:BLK, :]
    up_ref[...] = kv_ref[BLK:, :]


def project(who, xs, w_mine, w_other, bias, chosen):
    sd = jax.ShapeDtypeStruct
    rows, width = xs[0].shape
    cols = w_mine.shape[1]
    ins = (*xs, w_mine, w_other, bias, chosen)
    outs = (
        sd((4 * rows, 256), BF), sd((4 * rows, cols - 256), BF), sd((2 * rows, cols - 256), BF),
        sd((2 * rows, cols - 256), BF), sd((width, cols), BF),
    )
    return pl.pallas_call(
        project_kernel,
        out_shape=outs,
        grid_spec=pltpu.PrefetchScalarGridSpec(
            num_scalar_prefetch=1,
            grid=(1,),
            in_specs=[whole(a.shape) for a in ins],
            out_specs=tuple(whole(a.shape) for a in outs),
            scratch_shapes=[pltpu.VMEM((2 * BLK + 128, cols - 256), F32)],
        ),
        compiler_params=pltpu.CompilerParams(vmem_limit_bytes=24 << 20),
        cost_estimate=cost(3_000_000_000, 12_000_000),
        name="project",
    )(who, *ins)


def row_mean(v):
    return jnp.sum(v, axis=-1, keepdims=True) * (1.0 / v.shape[-1])

def dense_kernel(
    who, o_ref, wo_a, wo_b, win_a, win_b, wback_a, wback_b, x_ref, teacher_ref, cot_ref, keep_ref, vec_ref,
    out_ref, dres_ref, dparts_ref, act_ref, dbr_ref, dpre_ref, hid_ref, dproj_ref, sums_ref,
    wo, win, wback, xh, inv, hidden, gp, acc, sems, *, FB
):
    rows, width = x_ref.shape
    groups = o_ref.shape[0] // rows
    part = width // groups
    units = win.shape[1]
    wo_loads, win_loads, wback_loads = [], [], []
    for i in range(2):
        side = who[0] if i == 0 else 1 - who[0]
        for e in range(groups // 2):
            to = pl.multiple_of(((side * (groups // 2) + e) ^ who[1]) * part, part)
            wo_loads.append(
                pltpu.make_async_copy((wo_a, wo_b)[i].at[pl.ds(e * part, part)], wo.at[pl.ds(to, part)], sems.at[2 * i + e])
            )
        for j, (pieces, target, held) in enumerate((((win_a, win_b), win, win_loads), ((wback_a, wback_b), wback, wback_loads))):
            tall = target.shape[0] // 2
            to = pl.multiple_of(side * tall, tall)
            held.append(pltpu.make_async_copy(pieces[i], target.at[pl.ds(to, tall)], sems.at[4 + 2 * i + j]))
    for load in wo_loads + win_loads + wback_loads:
        load.start()
    b_out, b_in, b_back = vec_ref[0:1, 0:width], vec_ref[1:2, :], vec_ref[2:3, 0:width]
    gain1, shift1, gain2, shift2 = (vec_ref[i : i + 1, 0:width] for i in range(3, 7))
    for load in wo_loads:
        load.wait()
    total = x_ref[...].astype(F32) + b_out
    for i in range(groups):
        total += mm(o_ref[i * rows : (i + 1) * rows, :], wo[i * part : (i + 1) * part, :])
    center = total - row_mean(total)
    scale = lax.rsqrt(row_mean(center * center) + 1e-12)
    inv[...] = scale
    unit = center * scale
    xh[...] = unit
    hid = unit * gain1 + shift1
    hidden[...] = hid
    hid_ref[...] = hid.astype(BF)
    acc[...] = jnp.zeros_like(acc)
    for load in win_loads + wback_loads:
        load.wait()

    def up(n, _):
        cols = pl.ds(pl.multiple_of(n * FB, FB), FB)
        pre = mm(hid_ref[...], win[:, cols]) + vec_ref[1:2, cols]
        cdf = 0.5 + 0.5 * lax.erf(pre * 0.7071067811865476)
        act = (pre * cdf).astype(BF)
        act_ref[:, cols] = act
        gp[:, cols] = cdf + pre * (jnp.exp(pre * pre * -0.5) * 0.3989422804014327)
        acc[...] += mm(act, wback[cols, :])
        return 0

    lax.fori_loop(0, units // FB, up, 0, unroll=False)
    total = hidden[...] + acc[...] + b_back
    center = total - row_mean(total)
    scale = lax.rsqrt(row_mean(center * center) + 1e-12)
    unit = center * scale
    result = unit * gain2 + shift2
    out_ref[...] = result.astype(BF)
    grad = cot_ref[...].astype(F32) + keep_ref[...] * (result - teacher_ref[...].astype(F32))
    def put(row, value):
        sums_ref[row : row + 1, 0 : value.shape[1]] = value
    put(5, jnp.sum(grad * unit, axis=0, keepdims=True))
    put(6, jnp.sum(grad, axis=0, keepdims=True))
    grad = grad * gain2
    back = scale * (grad - row_mean(grad) - unit * row_mean(grad * unit))
    acc[...] = back
    low = back.astype(BF)
    dbr_ref[...] = low
    put(2, jnp.sum(low.astype(F32), axis=0, keepdims=True))

    def down(n, _):
        cols = pl.ds(pl.multiple_of(n * FB, FB), FB)
        dpre = (mm(dbr_ref[...], wback[cols, :], NT) * gp[:, cols]).astype(BF)
        dpre_ref[:, cols] = dpre
        sums_ref[1:2, cols] = jnp.sum(dpre.astype(F32), axis=0, keepdims=True)
        acc[...] += mm(dpre, win[:, cols], NT)
        return 0

    lax.fori_loop(0, units // FB, down, 0, unroll=False)
    grad = acc[...]
    unit = xh[...]
    put(3, jnp.sum(grad * unit, axis=0, keepdims=True))
    put(4, jnp.sum(grad, axis=0, keepdims=True))
    grad = grad * gain1
    back = inv[...] * (grad - row_mean(grad) - unit * row_mean(grad * unit))
    dres_ref[...] = back
    low = back.astype(BF)
    dproj_ref[...] = low
    put(0, jnp.sum(low.astype(F32), axis=0, keepdims=True))
    for i in range(groups):
        dparts_ref[i * rows : (i + 1) * rows, :] = mm(low, wo[i * part : (i + 1) * part, :], NT).astype(BF)


def dense(who, o, weights, x, teacher, cot, keep, vec):
    rows, width = x.shape
    units = vec.shape[1]
    sd = jax.ShapeDtypeStruct
    outs = (
        sd((rows, width), BF), sd((rows, width), F32), sd(o.shape, BF), sd((rows, units), BF), sd((rows, width), BF),
        sd((rows, units), BF), sd((rows, width), BF), sd((rows, width), BF), sd((8, units), F32),
    )
    ins = (o, *weights, x, teacher, cot, keep, vec)
    stay = pl.BlockSpec(memory_space=pl.ANY)
    return pl.pallas_call(
        functools.partial(dense_kernel, FB=FFB),
        out_shape=outs,
        grid_spec=pltpu.PrefetchScalarGridSpec(
            num_scalar_prefetch=1,
            grid=(1,),
            in_specs=[whole(o.shape)] + [stay] * 6 + [whole(a.shape) for a in ins[7:]],
            out_specs=tuple(whole(a.shape) for a in outs),
            scratch_shapes=[
                pltpu.VMEM((width, width), BF), pltpu.VMEM((width, units), BF), pltpu.VMEM((units, width), BF),
                pltpu.VMEM((rows, width), F32), pltpu.VMEM((rows, 1), F32), pltpu.VMEM((rows, width), F32),
                pltpu.VMEM((rows, units), F32), pltpu.VMEM((rows, width), F32), pltpu.SemaphoreType.DMA((8,)),
            ],
        ),
        compiler_params=pltpu.CompilerParams(vmem_limit_bytes=GRANT),
        cost_estimate=cost(12_000_000_000, 30_000_000, 4_000_000),
        name="dense",
    )(who, *ins)


def finish_kernel(
    who, dq0, dq1, dq2, dq3, own_ref, pair_ref, left_ref, right_ref, turn_ref, w_ref,
    all_ref, sums_ref, dx_ref, gx_ref, gy_ref, next_left, next_right, held,
):
    d = pl.program_id(0)
    rows, width = dx_ref.shape
    cut = width // 2

    @pl.when(d == 0)
    def _():
        sums_ref[...] = jnp.zeros_like(sums_ref)
        held[2 * BLK :, :] = jnp.zeros((held.shape[0] - 2 * BLK, held.shape[1]), BF)
        for base, extra in ((0, left_ref), (BLK, right_ref)):

            def gather(r, base=base, extra=extra):
                at = pl.ds(pl.multiple_of(base + r, 128), 128)
                value = own_ref[at, :].astype(F32) + pair_ref[at, :].astype(F32)
                held[at, :] = (value + extra[pl.ds(r, 128), :].astype(F32)).astype(BF)

            sweep(BLK, 128, gather)

    tok = mm(turn_ref[0], held[pl.ds(pl.multiple_of(who[3 + d], 16), SPAN), :]).astype(BF)
    dq = sum(ref[...].astype(F32) for ref in (dq0, dq1, dq2, dq3)).astype(BF)
    all_ref[:, 0:256] = dq
    all_ref[:, 256:640] = tok
    sums_ref[0:1, 0:256] += jnp.sum(dq.astype(F32), axis=0, keepdims=True)
    sums_ref[0:1, 256:640] += jnp.sum(tok.astype(F32), axis=0, keepdims=True)
    part = mm(all_ref[...], w_ref[...], NT).astype(BF)

    @pl.when(d == 0)
    def _():
        dx_ref[...] = part

    @pl.when(d == 1)
    def _():
        gx_ref[0:rows, :] = part[:, :cut]
        next_right[...] = part[:, cut:]

    @pl.when(d == 2)
    def _():
        next_left[...] = part[:, :cut]
        gy_ref[0:rows, :] = part[:, cut:]

    @pl.when(d == 3)
    def _():
        gx_ref[rows:, :] = part[:, :cut]
        gy_ref[rows:, :] = part[:, cut:]


def finish(who, dqs, own, pair, left, right, turn, w_heads):
    sd = jax.ShapeDtypeStruct
    rows, width = turn.shape[1], w_heads.shape[0]
    cols = dqs[0].shape[1] + own.shape[1]
    ins = (*dqs, own, pair, left, right, turn, w_heads)
    shapes = ((rows, width), (2 * rows, width // 2), (2 * rows, width // 2), (rows, width // 2), (rows, width // 2))
    outs = (sd((4 * rows, cols), BF), sd((8, cols), F32)) + tuple(sd(s, BF) for s in shapes)

    def by_block(shape):
        return pl.BlockSpec((rows, shape[1]), lambda d, *_: (d, 0))

    return pl.pallas_call(
        finish_kernel,
        out_shape=outs,
        grid_spec=pltpu.PrefetchScalarGridSpec(
            num_scalar_prefetch=1,
            grid=(4,),
            in_specs=[by_block(a.shape) for a in ins[:4]]
            + [whole(a.shape) for a in ins[4:8]]
            + [pl.BlockSpec((1, *turn.shape[1:]), lambda d, *_: (d, 0, 0)), whole(w_heads.shape)],
            out_specs=(by_block(outs[0].shape), whole(outs[1].shape)) + tuple(whole(s) for s in shapes),
            scratch_shapes=[pltpu.VMEM((2 * BLK + 128, own.shape[1]), BF)],
        ),
        compiler_params=pltpu.CompilerParams(vmem_limit_bytes=GRANT),
        cost_estimate=cost(3_000_000_000, 16_000_000),
        name="finish",
    )(who, *ins)


def part_out(who, held, am, ao, bm, bo, sides):
    part = am.shape[0]
    for mine, other, side, base in ((am, ao, sides[0], 0), (bm, bo, sides[1], 2 * part)):

        def move(r, mine=mine, other=other, side=side, base=base):
            mine[pl.ds(r, 16), :] = held[pl.ds(pl.multiple_of(base + side * part + r, 16), 16), :]
            other[pl.ds(r, 16), :] = held[pl.ds(pl.multiple_of(base + (1 - side) * part + r, 16), 16), :]

        sweep(part, 16, move)


def plus(left, right, at):
    return (left[at, :].astype(F32) + right[at, :].astype(F32)).astype(BF)


def first_kernel(who, back_a, back_b, in_a, in_b, out_a, out_b, am, ao, bm, bo, held):
    width = back_a.shape[1]
    tall = in_a.shape[0]

    def upper(r):
        at = pl.ds(r, 16)
        for k in range(4):
            held[at, k * width : (k + 1) * width] = plus(back_a, back_b, pl.ds(pl.multiple_of(k * tall + r, 16), 16))
        held[pl.ds(pl.multiple_of(tall + r, 16), 16), :] = plus(in_a, in_b, at)

    def lower(r):
        held[pl.ds(pl.multiple_of(2 * tall + r, 16), 16), :] = plus(out_a, out_b, pl.ds(r, 16))

    sweep(tall, 16, upper)
    sweep(out_a.shape[0], 16, lower)
    part_out(who, held, am, ao, bm, bo, (lax.rem(who[1], 2), who[1] // 2))


def both_kernel(who, a_mine, a_got, b_mine, b_got, both):
    del who
    part = a_mine.shape[0]

    def work(r):
        both[pl.ds(r, 16), :] = plus(a_mine, a_got, pl.ds(r, 16))
        both[pl.ds(pl.multiple_of(part + r, 16), 16), :] = plus(b_mine, b_got, pl.ds(r, 16))

    sweep(part, 16, work)


def second_kernel(who, a_mine, a_got, b_mine, b_got, am, ao, bm, bo, held):
    both_kernel(who, a_mine, a_got, b_mine, b_got, held)
    part_out(who, held, am, ao, bm, bo, (who[1] // 2, lax.rem(who[1], 2)))


def join_kernel(who, a, b, c, d, back_ref, in_ref, out_ref, vec_ref, held):
    step = pl.program_id(0)

    @pl.when(step == 0)
    def _():
        gather_pieces(who, (a, b, c, d), held)

    tall = held.shape[0] - 128
    tall, width = tall // 2, back_ref.shape[1]
    cols = pl.ds(pl.multiple_of(step * width, 128), width)
    back_ref[...] = held[0:tall, cols].astype(F32)
    rows = in_ref.shape[0]
    in_ref[...] = held[pl.ds(pl.multiple_of(tall + step * rows, 16), rows), :].astype(F32)

    @pl.when(step < 3)
    def _():
        out_ref[...] = held[2 * tall :, cols].astype(F32)

    @pl.when(step == 3)
    def _():
        vec_ref[...] = held[2 * tall : 2 * tall + 16, 3 * width :].astype(F32)


def gather_pieces(who, pieces, held):
    s1, s2 = lax.rem(who[1], 2), who[1] // 2
    part = pieces[0].shape[0] // 2
    for at, ref in enumerate(pieces):
        color, i = at // 2, at % 2
        for j in range(2):
            spot = (s1 ^ i) * 2 + (s2 ^ j) if color == 0 else 4 + (s2 ^ i) * 2 + (s1 ^ j)

            def move(r, spot=spot, ref=ref, j=j):
                frm = pl.ds(pl.multiple_of(j * part + r, 16), 16)
                held[pl.ds(pl.multiple_of(spot * part + r, 16), 16), :] = ref[frm, :]

            sweep(part, 16, move)

def join(who, pieces, back, first, out, total):
    sd = jax.ShapeDtypeStruct
    tall, width = first[0], back[1]
    outs = (sd(back, F32), sd(first, F32), sd(out, F32), sd((16, width), F32))
    return pl.pallas_call(
        join_kernel,
        out_shape=outs,
        grid_spec=pltpu.PrefetchScalarGridSpec(
            num_scalar_prefetch=1,
            grid=(4,),
            in_specs=[whole(a.shape) for a in pieces],
            out_specs=(
                pl.BlockSpec((tall, width), lambda k, *_: (k, 0)),
                pl.BlockSpec((tall // 4, first[1]), lambda k, *_: (k, 0)),
                pl.BlockSpec((128, width), lambda k, *_: (jnp.minimum(k, 2), 0)),
                whole((16, width)),
            ),
            scratch_shapes=[pltpu.VMEM((total, first[1]), BF)],
        ),
        compiler_params=pltpu.CompilerParams(vmem_limit_bytes=GRANT),
        cost_estimate=cost(1_000_000, 16_000_000),
        name="join",
    )(who, *pieces)


def small_call(kernel, who, pieces, outs, scratch, name, grant=24 << 20):
    return pl.pallas_call(
        kernel,
        out_shape=tuple(jax.ShapeDtypeStruct(*s) for s in outs),
        grid_spec=pltpu.PrefetchScalarGridSpec(
            num_scalar_prefetch=1,
            grid=(1,),
            in_specs=[whole(a.shape) for a in pieces],
            out_specs=tuple(whole(s[0]) for s in outs),
            scratch_shapes=scratch,
        ),
        compiler_params=pltpu.CompilerParams(vmem_limit_bytes=grant),
        cost_estimate=cost(1_000_000, 9_000_000),
        name=name,
    )(who, *pieces)


def heads_kernel(who, in_ref, q_ref, k_ref, v_ref, bias_ref):
    tall = in_ref.shape[1]
    for c in range(in_ref.shape[0] // 4):
        at = slice(c * tall, (c + 1) * tall)
        for a in range(4):
            cols = slice(a * 192, (a + 1) * 192)
            block = in_ref[c * 4 + (who[1] ^ a)].astype(F32)
            q_ref[at, cols] = block[:, 64:256]
            v_ref[at, cols] = block[:, 256:448]
            k_ref[at, cols] = block[:, 448:640]
            if c == 0:
                for k in range(3):
                    spot = slice(a * 192 + k * 64, a * 192 + (k + 1) * 64)
                    bias_ref[0:1, spot] = block[k : k + 1, 0:64]
                    bias_ref[8:9, spot] = block[k + 3 : k + 4, 0:64]


def heads_out(who, gathered):
    outs = (((384, 768), F32),) * 3 + (((16, 768), F32),)
    return small_call(heads_kernel, who, (gathered,), outs, [], "heads_out")


def swap(block, axis="fsdp"):
    return lax.ppermute(block, axis, [(0, 1), (1, 0)])


def shifted(block, axis, distance):
    devices = range(lax.axis_size(axis))
    route = [(i - distance, i) for i in devices if i - distance in devices]
    return lax.ppermute(block, axis, route)


def flip(block, bit, axis="uly"):
    return lax.ppermute(block, axis, [(i, i ^ bit) for i in range(lax.axis_size(axis))])


def exchange(rows, axis):
    return lax.all_to_all(rows, axis, split_axis=0, concat_axis=0, tiled=True)


def spread_rows(rows, axis):
    count = lax.axis_size(axis)
    return exchange(jnp.broadcast_to(rows[None], (count, *rows.shape)).reshape(-1, rows.shape[1]), axis)


def sum_parts(rows, count):
    got = rows.reshape(count, -1, rows.shape[1])
    return sum(got[i].astype(F32) for i in range(count)).astype(BF)


def sum_scatter(rows, axis):
    return sum_parts(exchange(rows, axis), lax.axis_size(axis))


def add(left, right):
    return (left.astype(F32) + right.astype(F32)).astype(BF)


def line_step(held, bit):
    return flip(held, bit, "ctx")


def line_join(held, got, bit):
    low = (lax.axis_index("ctx") & bit) == 0
    return jnp.stack([jnp.where(low, held, got), jnp.where(low, got, held)], axis=1).reshape(-1, *held.shape[1:])


def line_rest(held, bit):
    while bit > 0:
        held = line_join(held, line_step(held, bit), bit)
        bit //= 2
    return held.reshape(-1, held.shape[2])


def chunks_of(rows, axis):
    count, me = lax.axis_size(axis), lax.axis_index(axis)
    split = rows.reshape(count, -1, rows.shape[1])
    picked = [lax.dynamic_index_in_dim(split, me ^ k, 0, keepdims=False) for k in range(count)]
    return [picked[0]] + [flip(picked[k], k, axis) for k in range(1, count)]


def tie(*values):
    return lax.optimization_barrier(values)


def on_device(
    tokens, teacher, cotangent, valid, teacher_ok, doc_starts, w_query, w_key, w_value, w_out, w_in, w_back,
    bias_query, bias_value, bias_out, bias_in, bias_back, norm1_gain, norm1_bias, norm2_gain, norm2_bias,
):
    groups = lax.axis_size("uly")
    spans = lax.axis_size("ctx")
    rows, width = tokens.shape
    block = rows * groups * 2
    stream = block * spans
    ctx_index = lax.axis_index("ctx")
    uly = lax.axis_index("uly")
    half = lax.axis_index("fsdp")
    head_cols = width // groups
    shard = w_query.shape[0]
    upper = uly // 2

    small = (bias_query, bias_value, bias_out, bias_in, bias_back, norm1_gain, norm1_bias, norm2_gain, norm2_bias)
    valid_one = valid[None, :]
    valid_own = jnp.concatenate([valid_one, flip(valid_one, 1), flip(valid_one, 2), flip(valid_one, 3)], axis=0)
    x_own, valid_own, *small = tie(tokens, valid_own, *small)
    x_x, x_y = flip(x_own, 1), flip(x_own, 2)
    valid_pair = swap(valid_own)
    place = jnp.arange(groups, dtype=jnp.int32)
    in_plane = place ^ uly
    valid_mine = jnp.take(valid_own, in_plane, axis=0).reshape(2, BLK)
    valid_next = jnp.take(valid_pair, in_plane, axis=0).reshape(2, BLK)
    from_low = shifted(jnp.stack([valid_mine[1], valid_next[1]]), "ctx", 1)
    from_high = shifted(jnp.stack([valid_mine[0], valid_next[0]]), "ctx", -1)
    block_valid = jnp.concatenate(
        [valid_mine, valid_next, from_low[:1], from_high[:1], from_low[1:], from_high[1:]], axis=0
    )
    count = jnp.full((8, 128), jnp.sum(valid_mine) + jnp.sum(valid_next), jnp.int32)
    bit = 1
    while bit < spans:
        count = count + flip(count, bit, "ctx")
        bit *= 2
    count = count[0, 0].astype(F32)

    start_col = uly * head_cols
    cut = [lax.dynamic_slice_in_dim(w, start_col, head_cols, 1) for w in (w_query, w_value, w_key)]
    w_mine = jnp.concatenate([jnp.zeros((shard, 256 - head_cols), BF), *cut], axis=1)
    w_other = swap(w_mine)
    packed = jnp.concatenate(small)
    packed_pair = swap(packed)
    first, second = jnp.where(half == 0, packed, packed_pair), jnp.where(half == 0, packed_pair, packed)
    vectors = []
    at = 0
    for p in small:
        n = p.shape[0]
        vectors.append(jnp.concatenate([first[at : at + n], second[at : at + n]]).astype(F32))
        at += n
    bq_all, bv_all = vectors[:2]
    vec = jnp.stack([jnp.pad(v, (0, w_in.shape[1] - v.shape[0])) for v in vectors[2:]] + [jnp.zeros((w_in.shape[1],), F32)])
    bias_heads = jnp.concatenate(
        [
            jnp.zeros((256 - head_cols,), F32),
            lax.dynamic_slice_in_dim(bq_all, start_col, head_cols, 0),
            lax.dynamic_slice_in_dim(bv_all, start_col, head_cols, 0),
            jnp.zeros((head_cols,), F32),
        ]
    )

    step = jnp.asarray([0, 0, 0, 0, -1, 1, -1, 1], jnp.int32)
    side = jnp.asarray([0, 1, 0, 1, 1, 0, 1, 0], jnp.int32)
    swapped = jnp.asarray([0, 0, 1, 1, 0, 0, 1, 1], jnp.int32)
    inner = jnp.arange(BLK, dtype=jnp.int32)
    first_block = (ctx_index + step) * (2 * groups) + side * groups + (half ^ swapped)
    spot = (first_block[:, None] + 2 * (inner // rows)[None, :]) * rows + lax.rem(inner, rows)[None, :]
    x_x, x_y, block_valid = tie(x_x, x_y, block_valid)
    edges = jnp.concatenate([doc_starts, jnp.full((DOCS + 1,), stream, jnp.int32)])
    window_first = jnp.maximum(ctx_index * block - block // 2, 0)
    first_doc = jnp.sum((doc_starts <= window_first).astype(jnp.int32)) - 1
    near = lax.dynamic_slice_in_dim(edges, first_doc, DOCS + 1, 0)
    tiles = groups * rows // TQ
    per = rows // TQ
    tile_ids = jnp.arange(tiles, dtype=jnp.int32)
    qfirst = ctx_index * block + (((tile_ids // per) ^ uly) * 2 + half) * rows + lax.rem(tile_ids, per) * TQ
    q_lo = jnp.max(jnp.where(near[None, :] <= qfirst[:, None], near[None, :], 0), axis=1)
    q_hi = jnp.min(jnp.where(near[None, :] <= qfirst[:, None] + TQ - 1, stream, near[None, :]), axis=1)
    limits = jnp.concatenate([near, q_lo, q_hi])
    counted = jnp.sum(block_valid[:, None, :] * (spot[:, None, :] < limits[None, :, None]), axis=-1)
    bounds = counted[:, : DOCS + 1]
    cnt_lo = counted[:, DOCS + 1 : DOCS + 1 + tiles].T
    cnt_hi = counted[:, DOCS + 1 + tiles :].T
    pad64 = jnp.zeros((bounds.shape[0], 128 - DOCS), jnp.int32)
    lo_tab = jnp.concatenate([bounds[:, :DOCS], pad64], axis=1)
    hi_tab = jnp.concatenate([bounds[:, 1:], pad64], axis=1)
    slo_tab = jnp.concatenate([near[:DOCS], pad64[0]])[None, :]
    shi_tab = jnp.concatenate([near[1:], pad64[0]])[None, :]
    some = cnt_hi > cnt_lo
    tlo = jnp.where(some, cnt_lo // TK, 0)
    thi = jnp.where(some, (cnt_hi + TK - 1) // TK, 0)
    tables = (tlo, thi, qfirst, lo_tab, hi_tab, slo_tab, shi_tab)
    before = mm(valid_own.astype(BF), (jnp.arange(rows)[:, None] < jnp.arange(rows)[None, :]).astype(BF)).astype(jnp.int32)
    filled = jnp.sum(valid_own, axis=1)
    shift = jnp.where(lax.rem(in_plane, 2) == 1, jnp.take(filled, place ^ 1), 0)
    base = (in_plane // 2) * BLK + (shift // 16) * 16
    goes_to = jnp.where(valid_own > 0, before + lax.rem(shift, 16)[:, None], 2 * BLK)
    ranks = jnp.arange(SPAN, dtype=jnp.int32)
    chosen = (goes_to[:, None, :] == ranks[None, :, None]).astype(BF)
    turned = (goes_to[:, :, None] == ranks[None, None, :]).astype(BF)
    who = jnp.concatenate([jnp.stack([half, uly, upper]).astype(jnp.int32), base])
    loss_scale = jnp.float32(stream) / count
    keep = (loss_scale * (valid * teacher_ok).astype(F32))[:, None]

    x_x, x_y, w_other = tie(x_x, x_y, w_other)
    x_top, x_bottom = flip(x_y[: rows // 2], 1), flip(x_x[rows // 2 :], 2)
    x_top, x_bottom, chosen, bias_heads, *tables = tie(x_top, x_bottom, chosen, bias_heads, *tables)

    q_low, kv_own, kv_up, kv_down, w_heads = project(
        who, (tokens, x_x, x_y, x_top, x_bottom), w_mine, w_other, bias_heads[None, :], chosen
    )
    kv_from_left, kv_from_right = shifted(kv_up, "ctx", 1), shifted(kv_down, "ctx", -1)
    w_out, w_in, w_back, kv_own = tie(w_out, w_in, w_back, kv_own)
    wo_pair, win_pair, wback_pair = swap(w_out), swap(w_in), swap(w_back)
    kv_pair = swap(kv_own)
    state = attend(tables, q_low, (kv_own,), 0)
    kv_halo = jnp.concatenate([kv_from_left, kv_from_right], axis=0)
    kv_halo, kv_pair, *state = tie(kv_halo, kv_pair, *state)
    kv_halo_pair = swap(kv_halo)
    state = attend(tables, q_low, (kv_pair,), 2, state)
    o_heads, o_turned, lse = attend(tables, q_low, (kv_halo, kv_halo_pair), 4, state, last=True)
    o_rel = o_heads.reshape(groups, rows, head_cols)
    o_rest = [flip(o_rel[d], d) for d in range(1, groups)]
    o_heads, x_x, x_y, x_top, x_bottom = tie(o_heads, x_x, x_y, x_top, x_bottom)
    x_all = jnp.concatenate([tokens, x_x, x_y, x_top, x_bottom], axis=0)

    x_all, *o_rest = tie(x_all, *o_rest)
    o_all = jnp.concatenate([o_rel[0], *o_rest], axis=0)

    out, d_resid1, d_parts, act, d_branch, d_pre, hidden_low, d_proj, sums = dense(
        who, o_all, (w_out, wo_pair, w_in, win_pair, w_back, wback_pair), tokens, teacher, cotangent, keep, vec
    )
    d_rel = d_parts.reshape(groups, rows, head_cols)
    tall = w_back.shape[0]
    vector_rows = jnp.concatenate(
        [sums[i, :width].reshape(2, -1) for i in (0, 2, 3, 4, 5, 6)] + [sums[1].reshape(2, -1)], axis=1
    ).reshape(2, -1, width)
    vector_rows = jnp.pad(vector_rows, ((0, 0), (0, 128 - vector_rows.shape[1]), (0, 0))).astype(BF)
    o_rows = o_all.reshape(groups, rows, head_cols)

    def back_part(side):
        return mm(lax.dynamic_slice_in_dim(act, side * tall, tall, 1), d_branch, TN).astype(BF)

    def in_part(side):
        return mm(lax.dynamic_slice_in_dim(hidden_low, side * shard, shard, 1), d_pre, TN).astype(BF)

    def out_part(side):
        both = [
            mm(lax.dynamic_index_in_dim(o_rows, (2 * side + e) ^ uly, 0, keepdims=False), d_proj, TN).astype(BF)
            for e in range(2)
        ]
        stack = jnp.concatenate([*both, lax.dynamic_index_in_dim(vector_rows, side, 0, keepdims=False)], axis=0)
        return jnp.concatenate([stack[i * 128 : (i + 1) * 128] for i in range(4)], axis=1)

    d_rest = [flip(d_rel[d], d) for d in range(1, groups)]
    back_got, in_got, out_got, *d_rest = tie(back_part(1 - half), in_part(1 - half), out_part(1 - half), *d_rest)
    back_got, in_got, out_got = swap(back_got), swap(in_got), swap(out_got)
    back_mine, in_mine, out_mine = back_part(half), in_part(half), out_part(half)
    back_got, in_got, out_got, back_mine, in_mine, out_mine = tie(
        back_got, in_got, out_got, back_mine, in_mine, out_mine
    )
    wide = w_in.shape[1]
    total = 2 * shard + 128
    am, ao, bm, bo = small_call(
        first_kernel, who, (back_mine, back_got, in_mine, in_got, out_mine, out_got),
        (((total // 4, wide), BF),) * 4, [pltpu.VMEM((total, wide), BF)], "first_stage",
    )
    d_heads = jnp.concatenate([d_rel[0], *d_rest], axis=0)
    d_heads, am, ao, bm, bo = tie(d_heads, am, ao, bm, bo)

    ag, bg = flip(ao, 1), flip(bo, 2)
    args = (tables, q_low, d_heads, o_turned, lse)
    dq0, got_lo, got_hi, delta = attend_back(
        *args, kv_halo_pair, 6, first=True, cuts=2, name="back_halo_pair"
    )
    got_lo, got_hi, delta = tie(got_lo, got_hi, delta)
    args = (tables, q_low, d_heads, delta, lse)
    got_lo, got_hi = swap(got_lo), swap(got_hi)
    dq1, halo_lo, halo_hi = attend_back(*args, kv_halo, 4, cuts=2, name="back_halo", size=1_000_000)
    halo_lo, halo_hi, got_lo, got_hi, ag, bg = tie(halo_lo, halo_hi, got_lo, got_hi, ag, bg)

    halo_lo, halo_hi = add(halo_lo, got_lo), add(halo_hi, got_hi)
    am, ao, bm, bo = small_call(
        second_kernel, who, (am, ag, bm, bg), (((total // 8, wide), BF),) * 4,
        [pltpu.VMEM((total // 2, wide), BF)], "second_stage", 12 << 20,
    )
    halo_lo, halo_hi, delta, am, ao, bm, bo = tie(halo_lo, halo_hi, delta, am, ao, bm, bo)
    args = (tables, q_low, d_heads, delta, lse)
    ag, bg = flip(ao, 2), flip(bo, 1)
    from_left, from_right = shifted(halo_hi, "ctx", 1), shifted(halo_lo, "ctx", -1)
    dq2, dkv_pair = attend_back(*args, kv_pair, 2, name="back_pair")
    dkv_pair, ag, bg, from_left, from_right = tie(dkv_pair, ag, bg, from_left, from_right)

    (line,) = small_call(both_kernel, who, (am, ag, bm, bg), (((total // 4, wide), BF),), [], "third_stage", 12 << 20)
    line, dkv_pair, delta = tie(line, dkv_pair, delta)
    args = (tables, q_low, d_heads, delta, lse)
    line = exchange(line, "ctx")
    pair_got = swap(dkv_pair)
    dq3, dkv_own = attend_back(*args, kv_own, 0, name="back_own")
    dkv_own, line, pair_got = tie(dkv_own, line, pair_got)
    line = sum_parts(line, spans)
    line, dkv_own = tie(line, dkv_own)
    line = spread_rows(line, "ctx")

    d_all, d_sums, dx_own, give_x, give_y, left_next, right_next = finish(
        who, (dq0, dq1, dq2, dq3), dkv_own, pair_got, from_left, from_right, turned, w_heads
    )
    d_all, give_x, give_y = tie(d_all, give_x, give_y)
    give_x, give_y = flip(give_x, 1), flip(give_y, 2)
    corner = d_sums[0, 64:].reshape(9, 64)

    def heads_part(side):
        grad = mm(lax.dynamic_slice_in_dim(x_all, side * shard, shard, 1), d_all, TN)
        return lax.dynamic_update_slice(grad, corner, (0, 0)).astype(BF)

    heads_other = heads_part(1 - half)
    heads_got = swap(heads_other)
    heads_mine = heads_part(half)
    heads_sum = add(heads_mine, heads_got)
    line, give_x, give_y, *heads_parts = tie(line, give_x, give_y, *chunks_of(heads_sum, "ctx"))
    heads_sum = sum(part.astype(F32) for part in heads_parts).astype(BF)
    a_near, b_near = line[: total // 8], line[total // 8 :]
    a_got, b_got, *heads_rest = tie(
        flip(a_near, 2), flip(b_near, 1), *[flip(heads_sum, d) for d in range(1, groups)]
    )
    a_near = jnp.concatenate([a_near, a_got], axis=0)
    b_near = jnp.concatenate([b_near, b_got], axis=0)
    a_far, b_far = flip(a_near, 1), flip(b_near, 2)
    left_next = flip(add(left_next, give_x[rows:]), 2)
    right_next = flip(add(right_next, give_y[rows:]), 1)
    heads_sum = jnp.concatenate([heads_sum, *heads_rest], axis=0)
    heads_all = spread_rows(heads_sum, "ctx").reshape(spans * groups, -1, heads_sum.shape[1])
    grad_in = d_resid1 + dx_own.astype(F32)
    grad_in = grad_in + jnp.concatenate([give_x[:rows].astype(F32), give_y[:rows].astype(F32)], axis=1)
    grad_in = grad_in + jnp.concatenate([left_next.astype(F32), right_next.astype(F32)], axis=1)
    g_back, g_in, g_out, g_vec = join(
        who, (a_near, a_far, b_near, b_far), w_back.shape, w_in.shape, w_out.shape, total
    )
    g_query, g_key, g_value, g_bias = heads_out(who, heads_all)
    g_bias_q = lax.dynamic_slice_in_dim(g_bias[0], half * shard, shard, 0)
    g_bias_v = lax.dynamic_slice_in_dim(g_bias[8], half * shard, shard, 0)
    flat = g_vec.reshape(-1)
    g_bo, g_bb, g_g1, g_s1, g_g2, g_s2 = [flat[i * shard : (i + 1) * shard] for i in range(6)]
    g_bin = flat[6 * shard : 6 * shard + bias_in.shape[0]]
    return (
        out, grad_in, g_query, g_key, g_value, g_out, g_in, g_back,
        g_bias_q, g_bias_v, g_bo, g_bin, g_bb, g_g1, g_s1, g_g2, g_s2,
    )


def solution(mesh):
    placed = (
        P(("ctx", "uly", "fsdp"), None),
        P(("ctx", "uly", "fsdp"), None),
        P(("ctx", "uly", "fsdp"), None),
        P(("ctx", "uly", "fsdp")),
        P(("ctx", "uly", "fsdp")),
        P(),
        P("fsdp", None),
        P("fsdp", None),
        P("fsdp", None),
        P("fsdp", None),
        P("fsdp", None),
        P("fsdp", None),
        P("fsdp"),
        P("fsdp"),
        P("fsdp"),
        P("fsdp"),
        P("fsdp"),
        P("fsdp"),
        P("fsdp"),
        P("fsdp"),
        P("fsdp"),
    )
    return jax.shard_map(
        on_device,
        mesh=mesh,
        in_specs=placed,
        out_specs=(
            P(("ctx", "uly", "fsdp"), None),
            P(("ctx", "uly", "fsdp"), None),
            P("fsdp", None),
            P("fsdp", None),
            P("fsdp", None),
            P("fsdp", None),
            P("fsdp", None),
            P("fsdp", None),
            P("fsdp"),
            P("fsdp"),
            P("fsdp"),
            P("fsdp"),
            P("fsdp"),
            P("fsdp"),
            P("fsdp"),
            P("fsdp"),
            P("fsdp"),
        ),
        check_vma=False,
    )
```

```python
import functools

import jax
import jax.numpy as jnp
from jax import lax
from jax.experimental import pallas as pl
from jax.experimental.pallas import tpu as pltpu
from jax.sharding import PartitionSpec as P

HEADS = 12
HD = 64
BLK = 1024
SPAN = 640
TQ = 512
TK = 256
DOCS = 64
FFB = 1536
GRANT = 63 << 20
MASKED = -1e30
BF = jnp.bfloat16
F32 = jnp.float32
NT = (((1,), (1,)), ((), ()))
NN = (((1,), (0,)), ((), ()))
TN = (((0,), (0,)), ((), ()))


def mm(left, right, dims=NN):
    return lax.dot_general(left, right, dims, preferred_element_type=F32)


def whole(shape):
    return pl.BlockSpec(shape, lambda *_: (0,) * len(shape), pipeline_mode=pl.Buffered(1))


def sweep(total, step, work):
    def one(i, _):
        work(pl.multiple_of(i * step, step))
        return 0

    lax.fori_loop(0, total // step, one, 0)


def cost(flops, moved, special=0):
    return pl.CostEstimate(flops=flops, bytes_accessed=moved, transcendentals=special)


def lane_ids(rows):
    return lax.broadcasted_iota(jnp.int32, (rows, 128), 1)


def build_keys(sources, slot0, lo_ref, hi_ref, kaug, transposed, low_half):
    per = BLK // TK
    for at, kv in enumerate(sources):

        def one(j, _, at=at, kv=kv):
            rows = pl.ds(pl.multiple_of(j * TK, TK), TK)
            tile = at * (kv.shape[0] // TK) + j
            slot = slot0 + at * (kv.shape[0] // BLK) + j // per
            out = pl.ds(pl.multiple_of(tile * TK, TK), TK)
            rank = lax.broadcasted_iota(jnp.int32, (TK, 128), 0) + lax.rem(j, per) * TK
            inside = (rank >= lo_ref[pl.ds(slot, 1), :]) & (rank < hi_ref[pl.ds(slot, 1), :])
            bias = jnp.where(inside, 0.0, MASKED).astype(BF)
            kaug[out, 0:128] = jnp.where(lane_ids(TK) < 64, bias, kv[rows, 128:256])
            kaug[out, 128:256] = kv[rows, 256:384]
            if low_half:
                transposed[tile] = kv[rows, 0:256].T[0:192]
            else:
                transposed[tile] = kaug[out, :].T[64:256]
            return 0

        lax.fori_loop(0, kv.shape[0] // TK, one, 0)


def stack_queries(q, first, slo_ref, shi_ref, qs):
    lane = lane_ids(TQ)
    spot = lax.broadcasted_iota(jnp.int32, (TQ, 128), 0) + first
    mine = ((spot >= slo_ref[...]) & (spot < shi_ref[...])).astype(F32).astype(BF)
    zero = jnp.zeros((TQ, 128), BF)
    low, high = q[:, 0:128], q[:, 128:256]
    mark = jnp.where(lane < 64, mine, zero)
    qs[0:TQ, 0:128] = jnp.where(lane < 64, mine, low)
    qs[TQ : 2 * TQ, 0:128] = mark
    qs[2 * TQ :, 0:128] = mark
    qs[0:TQ, 128:256] = zero
    qs[TQ : 2 * TQ, 128:256] = jnp.where(lane < 64, high, zero)
    qs[2 * TQ :, 128:256] = jnp.where(lane < 64, zero, high)


def attend_kernel(*refs, slot0, count, resume, last):
    tlo, thi, qfirst, q_ref = refs[:4]
    sources = refs[4 : 4 + count]
    lo_ref, hi_ref, slo_ref, shi_ref = refs[4 + count : 8 + count]
    at = 8 + count
    if resume:
        acc_in, stat_in = refs[at : at + 2]
        at += 2
    if last:
        o_ref, ot_ref, lse_ref = refs[at : at + 3]
        at += 3
    else:
        acc_out, stat_out = refs[at : at + 2]
        at += 2
    kaug, vt, qs, acc, m_s, l_s = refs[at:]
    i = pl.program_id(0)

    @pl.when(i == 0)
    def _():
        build_keys(sources, slot0, lo_ref, hi_ref, kaug, vt, True)

    slots = count * sources[0].shape[0] // BLK
    per = BLK // TK
    stack_queries(q_ref[...], qfirst[i], slo_ref, shi_ref, qs)
    if resume:
        m_s[...] = stat_in[0, 0:1, :]
        l_s[...] = stat_in[0, 1:2, :]
        acc[...] = acc_in[0]
    else:
        m_s[...] = jnp.full_like(m_s, 2 * MASKED)
        l_s[...] = jnp.zeros_like(l_s)
        acc[...] = jnp.zeros_like(acc)

    def slot_loop(s, _):
        def key_loop(t, _):
            tile = s * per + t
            keys = pl.ds(pl.multiple_of(tile * TK, TK), TK)
            st = mm(kaug[keys, :], qs[...], NT)
            m_old = m_s[...]
            m_new = jnp.maximum(m_old, jnp.max(st, axis=0, keepdims=True))
            fade = jnp.exp(m_old - m_new)
            p = jnp.exp(st - m_new)
            l_s[...] = l_s[...] * fade + jnp.sum(p, axis=0, keepdims=True)
            m_s[...] = m_new
            low = p.astype(BF)
            for h in range(3):
                cols = slice(h * TQ, (h + 1) * TQ)
                part = slice(h * HD, (h + 1) * HD)
                acc[part, :] = acc[part, :] * fade[:, cols] + mm(vt[tile, part, :], low[:, cols])
            return 0

        return lax.fori_loop(tlo[i, slot0 + s], thi[i, slot0 + s], key_loop, 0)

    lax.fori_loop(0, slots, slot_loop, 0)
    if last:
        total = l_s[...]
        for h in range(3):
            cols = slice(h * TQ, (h + 1) * TQ)
            part = slice(h * HD, (h + 1) * HD)
            acc[part, :] = acc[part, :] / total[:, cols]
        ot_ref[0] = acc[...]
        o_ref[...] = acc[...].T.astype(BF)
        lse_ref[0] = m_s[...] + jnp.log(total)
    else:
        acc_out[0] = acc[...]
        stat_out[0, 0:1, :] = m_s[...]
        stat_out[0, 1:2, :] = l_s[...]


def rows_spec(shape):
    return pl.BlockSpec((TQ, shape[1]), lambda i, *_: (i, 0))


def tile_spec(shape):
    return pl.BlockSpec((1, *shape[1:]), lambda i, *_: (i, 0, 0))


def attend(tables, q, sources, slot0, state=None, last=False):
    tlo, thi, qfirst, lo, hi, slo, shi = tables
    tiles = q.shape[0] // TQ
    keys = sum(s.shape[0] for s in sources)
    state = tuple(state) if state else ()
    sd = jax.ShapeDtypeStruct
    acc, stat = sd((tiles, 3 * HD, TQ), F32), sd((tiles, 2, 3 * TQ), F32)
    if last:
        o, lse = sd((q.shape[0], 3 * HD), BF), sd((tiles, 1, 3 * TQ), F32)
        outs, out_specs = (o, acc, lse), (rows_spec(o.shape), tile_spec(acc.shape), tile_spec(lse.shape))
    else:
        outs, out_specs = (acc, stat), (tile_spec(acc.shape), tile_spec(stat.shape))
    return pl.pallas_call(
        functools.partial(attend_kernel, slot0=slot0, count=len(sources), resume=bool(state), last=last),
        out_shape=outs,
        grid_spec=pltpu.PrefetchScalarGridSpec(
            num_scalar_prefetch=3,
            grid=(tiles,),
            in_specs=[rows_spec(q.shape)]
            + [whole(x.shape) for x in (*sources, lo, hi, slo, shi)]
            + [tile_spec(x.shape) for x in state],
            out_specs=out_specs,
            scratch_shapes=[
                pltpu.VMEM((keys, 256), BF),
                pltpu.VMEM((keys // TK, 3 * HD, TK), BF),
                pltpu.VMEM((3 * TQ, 256), BF),
                pltpu.VMEM((3 * HD, TQ), F32),
                pltpu.VMEM((1, 3 * TQ), F32),
                pltpu.VMEM((1, 3 * TQ), F32),
            ],
        ),
        compiler_params=pltpu.CompilerParams(vmem_limit_bytes=GRANT),
        cost_estimate=cost(12_000_000_000, 12_000_000, 10_000_000),
        name="attend",
    )(tlo, thi, qfirst, q, *sources, lo, hi, slo, shi, *state)


def attend_back_kernel(
    tlo, thi, qfirst, q_ref, do_ref, ot_ref, lse_ref, kv, lo_ref, hi_ref, slo_ref, shi_ref, dq_ref, *rest,
    slot0, first, cuts,
):
    dkv_refs, rest = rest[:cuts], rest[cuts:]
    if first:
        delta_ref, *rest = rest
    kaug, kt, qs, dos, acc, dk_s, dv_s = rest
    keys_all = kv.shape[0]
    slots = keys_all // BLK
    per = BLK // TK
    i = pl.program_id(0)

    @pl.when(i == 0)
    def _():
        build_keys((kv,), slot0, lo_ref, hi_ref, kaug, kt, False)
        dk_s[...] = jnp.zeros_like(dk_s)
        dv_s[...] = jnp.zeros_like(dv_s)

    stack_queries(q_ref[...], qfirst[i], slo_ref, shi_ref, qs)
    do = do_ref[...]
    lane = lane_ids(TQ)
    zero = jnp.zeros((TQ, 128), BF)
    dos[0:TQ, 0:128] = jnp.where(lane < 64, do[:, 0:128], zero)
    dos[TQ : 2 * TQ, 0:128] = jnp.where(lane < 64, zero, do[:, 0:128])
    dos[2 * TQ :, 0:128] = zero
    dos[0 : 2 * TQ, 128:256] = jnp.zeros((2 * TQ, 128), BF)
    dos[2 * TQ :, 128:192] = do[:, 128:192]
    dos[2 * TQ :, 192:256] = jnp.zeros((TQ, 64), BF)
    if first:
        both = do.astype(F32).T * ot_ref[0]
        delta = jnp.concatenate(
            [jnp.sum(both[h * HD : (h + 1) * HD], axis=0, keepdims=True) for h in range(3)], axis=1
        )
        delta_ref[0] = delta
    else:
        delta = ot_ref[0]
    lse = lse_ref[0]
    acc[...] = jnp.zeros_like(acc)

    def slot_loop(s, _):
        def key_loop(t, _):
            tile = s * per + t
            keys = pl.ds(pl.multiple_of(tile * TK, TK), TK)
            st = mm(kaug[keys, :], qs[...], NT)
            p = jnp.exp(st - lse)
            dp = mm(kv[keys, 0:256], dos[...], NT)
            ds = (p * (dp - delta)).astype(BF)
            dv_s[keys, :] += mm(p.astype(BF), dos[...])
            dk_s[keys, :] += mm(ds, qs[...])
            for h in range(3):
                cols = slice(h * TQ, (h + 1) * TQ)
                acc[(h + 1) * HD : (h + 2) * HD, :] += mm(kt[tile, h * HD : (h + 1) * HD, :], ds[:, cols])
            return 0

        return lax.fori_loop(tlo[i, slot0 + s], thi[i, slot0 + s], key_loop, 0)

    lax.fori_loop(0, slots, slot_loop, 0)
    dq_ref[...] = (acc[...] * HD ** (-0.5)).T.astype(BF)

    @pl.when(i == pl.num_programs(0) - 1)
    def _():
        share = keys_all // cuts
        for j, dkv_ref in enumerate(dkv_refs):

            def write(r, j=j, dkv_ref=dkv_ref):
                at = pl.ds(pl.multiple_of(j * share + r, TK), TK)
                to = pl.ds(r, TK)
                dkv_ref[to, 0:128] = dv_s[at, 0:128].astype(BF)
                dkv_ref[to, 128:256] = jnp.where(lane_ids(TK) < 64, dv_s[at, 128:256], dk_s[at, 0:128]).astype(BF)
                dkv_ref[to, 256:384] = dk_s[at, 128:256].astype(BF)

            sweep(share, TK, write)


def attend_back(tables, q, do, ot, lse, source, slot0, first=False, cuts=1, name="attend_back", size=14_000_000_000):
    tlo, thi, qfirst, lo, hi, slo, shi = tables
    tiles = q.shape[0] // TQ
    keys = source.shape[0]
    sd = jax.ShapeDtypeStruct
    piece = (keys // cuts, source.shape[1])
    outs = (sd(q.shape, BF),) + (sd(piece, BF),) * cuts
    out_specs = (rows_spec(q.shape),) + (whole(piece),) * cuts
    if first:
        outs += (sd(lse.shape, F32),)
        out_specs += (tile_spec(lse.shape),)
    return pl.pallas_call(
        functools.partial(attend_back_kernel, slot0=slot0, first=first, cuts=cuts),
        out_shape=outs,
        grid_spec=pltpu.PrefetchScalarGridSpec(
            num_scalar_prefetch=3,
            grid=(tiles,),
            in_specs=[rows_spec(q.shape), rows_spec(do.shape), tile_spec(ot.shape), tile_spec(lse.shape)]
            + [whole(x.shape) for x in (source, lo, hi, slo, shi)],
            out_specs=out_specs,
            scratch_shapes=[
                pltpu.VMEM((keys, 256), BF),
                pltpu.VMEM((keys // TK, 3 * HD, TK), BF),
                pltpu.VMEM((3 * TQ, 256), BF),
                pltpu.VMEM((3 * TQ, 256), BF),
                pltpu.VMEM((256, TQ), F32),
                pltpu.VMEM((keys, 256), F32),
                pltpu.VMEM((keys, 256), F32),
            ],
        ),
        compiler_params=pltpu.CompilerParams(vmem_limit_bytes=GRANT),
        cost_estimate=cost(size, size // 1000, size // 3000),
        name=name,
    )(tlo, thi, qfirst, q, do, ot, lse, source, lo, hi, slo, shi)


def project_kernel(
    who, x0, x1, x2, x3_top, x3_bottom, w_mine, w_other, bias_ref, chosen, q_ref, kv_ref, up_ref, down_ref, w_ref, held
):
    tall = w_mine.shape[0]
    rows = x0.shape[0]
    w_ref[pl.ds(pl.multiple_of(who[0] * tall, tall), tall), :] = w_mine[...]
    w_ref[pl.ds(pl.multiple_of((1 - who[0]) * tall, tall), tall), :] = w_other[...]
    held[...] = jnp.zeros_like(held)
    for d, x in enumerate((x0, x1, x2, (x3_top, x3_bottom))):
        if d < 3:
            value = mm(x[...], w_ref[...]) + bias_ref[...]
        else:
            value = jnp.concatenate([mm(x[0][...], w_ref[...]), mm(x[1][...], w_ref[...])], axis=0) + bias_ref[...]
        at = slice(d * rows, (d + 1) * rows)
        q_ref[at, :] = (value[:, :256].astype(BF).astype(F32) * HD ** (-0.5)).astype(BF)
        to = pl.ds(pl.multiple_of(who[3 + d], 16), SPAN)
        held[to, :] += mm(chosen[d], value[:, 256:].astype(BF))
    kv_ref[...] = held[0 : 2 * BLK, :].astype(BF)
    down_ref[...] = kv_ref[0:BLK, :]
    up_ref[...] = kv_ref[BLK:, :]


def project(who, xs, w_mine, w_other, bias, chosen):
    sd = jax.ShapeDtypeStruct
    rows, width = xs[0].shape
    cols = w_mine.shape[1]
    ins = (*xs, w_mine, w_other, bias, chosen)
    outs = (
        sd((4 * rows, 256), BF), sd((4 * rows, cols - 256), BF), sd((2 * rows, cols - 256), BF),
        sd((2 * rows, cols - 256), BF), sd((width, cols), BF),
    )
    return pl.pallas_call(
        project_kernel,
        out_shape=outs,
        grid_spec=pltpu.PrefetchScalarGridSpec(
            num_scalar_prefetch=1,
            grid=(1,),
            in_specs=[whole(a.shape) for a in ins],
            out_specs=tuple(whole(a.shape) for a in outs),
            scratch_shapes=[pltpu.VMEM((2 * BLK + 128, cols - 256), F32)],
        ),
        compiler_params=pltpu.CompilerParams(vmem_limit_bytes=24 << 20),
        cost_estimate=cost(3_000_000_000, 12_000_000),
        name="project",
    )(who, *ins)


def row_mean(v):
    return jnp.sum(v, axis=-1, keepdims=True) * (1.0 / v.shape[-1])

def dense_kernel(
    who, o_ref, wo_a, wo_b, win_a, win_b, wback_a, wback_b, x_ref, teacher_ref, cot_ref, keep_ref, vec_ref,
    out_ref, dres_ref, dparts_ref, act_ref, dbr_ref, dpre_ref, hid_ref, dproj_ref, sums_ref,
    wo, win, wback, xh, inv, hidden, gp, acc, sems, *, FB
):
    rows, width = x_ref.shape
    groups = o_ref.shape[0] // rows
    part = width // groups
    units = win.shape[1]
    wo_loads, win_loads, wback_loads = [], [], []
    for i in range(2):
        side = who[0] if i == 0 else 1 - who[0]
        for e in range(groups // 2):
            to = pl.multiple_of(((side * (groups // 2) + e) ^ who[1]) * part, part)
            wo_loads.append(
                pltpu.make_async_copy((wo_a, wo_b)[i].at[pl.ds(e * part, part)], wo.at[pl.ds(to, part)], sems.at[2 * i + e])
            )
        for j, (pieces, target, held) in enumerate((((win_a, win_b), win, win_loads), ((wback_a, wback_b), wback, wback_loads))):
            tall = target.shape[0] // 2
            to = pl.multiple_of(side * tall, tall)
            held.append(pltpu.make_async_copy(pieces[i], target.at[pl.ds(to, tall)], sems.at[4 + 2 * i + j]))
    for load in wo_loads + win_loads + wback_loads:
        load.start()
    b_out, b_in, b_back = vec_ref[0:1, 0:width], vec_ref[1:2, :], vec_ref[2:3, 0:width]
    gain1, shift1, gain2, shift2 = (vec_ref[i : i + 1, 0:width] for i in range(3, 7))
    for load in wo_loads:
        load.wait()
    total = x_ref[...].astype(F32) + b_out
    for i in range(groups):
        total += mm(o_ref[i * rows : (i + 1) * rows, :], wo[i * part : (i + 1) * part, :])
    center = total - row_mean(total)
    scale = lax.rsqrt(row_mean(center * center) + 1e-12)
    inv[...] = scale
    unit = center * scale
    xh[...] = unit
    hid = unit * gain1 + shift1
    hidden[...] = hid
    hid_ref[...] = hid.astype(BF)
    acc[...] = jnp.zeros_like(acc)
    for load in win_loads + wback_loads:
        load.wait()

    def up(n, _):
        cols = pl.ds(pl.multiple_of(n * FB, FB), FB)
        pre = mm(hid_ref[...], win[:, cols]) + vec_ref[1:2, cols]
        cdf = 0.5 + 0.5 * lax.erf(pre * 0.7071067811865476)
        act = (pre * cdf).astype(BF)
        act_ref[:, cols] = act
        gp[:, cols] = cdf + pre * (jnp.exp(pre * pre * -0.5) * 0.3989422804014327)
        acc[...] += mm(act, wback[cols, :])
        return 0

    lax.fori_loop(0, units // FB, up, 0, unroll=False)
    total = hidden[...] + acc[...] + b_back
    center = total - row_mean(total)
    scale = lax.rsqrt(row_mean(center * center) + 1e-12)
    unit = center * scale
    result = unit * gain2 + shift2
    out_ref[...] = result.astype(BF)
    grad = cot_ref[...].astype(F32) + keep_ref[...] * (result - teacher_ref[...].astype(F32))
    def put(row, value):
        sums_ref[row : row + 1, 0 : value.shape[1]] = value
    put(5, jnp.sum(grad * unit, axis=0, keepdims=True))
    put(6, jnp.sum(grad, axis=0, keepdims=True))
    grad = grad * gain2
    back = scale * (grad - row_mean(grad) - unit * row_mean(grad * unit))
    acc[...] = back
    low = back.astype(BF)
    dbr_ref[...] = low
    put(2, jnp.sum(low.astype(F32), axis=0, keepdims=True))

    def down(n, _):
        cols = pl.ds(pl.multiple_of(n * FB, FB), FB)
        dpre = (mm(dbr_ref[...], wback[cols, :], NT) * gp[:, cols]).astype(BF)
        dpre_ref[:, cols] = dpre
        sums_ref[1:2, cols] = jnp.sum(dpre.astype(F32), axis=0, keepdims=True)
        acc[...] += mm(dpre, win[:, cols], NT)
        return 0

    lax.fori_loop(0, units // FB, down, 0, unroll=False)
    grad = acc[...]
    unit = xh[...]
    put(3, jnp.sum(grad * unit, axis=0, keepdims=True))
    put(4, jnp.sum(grad, axis=0, keepdims=True))
    grad = grad * gain1
    back = inv[...] * (grad - row_mean(grad) - unit * row_mean(grad * unit))
    dres_ref[...] = back
    low = back.astype(BF)
    dproj_ref[...] = low
    put(0, jnp.sum(low.astype(F32), axis=0, keepdims=True))
    for i in range(groups):
        dparts_ref[i * rows : (i + 1) * rows, :] = mm(low, wo[i * part : (i + 1) * part, :], NT).astype(BF)


def dense(who, o, weights, x, teacher, cot, keep, vec):
    rows, width = x.shape
    units = vec.shape[1]
    sd = jax.ShapeDtypeStruct
    outs = (
        sd((rows, width), BF), sd((rows, width), F32), sd(o.shape, BF), sd((rows, units), BF), sd((rows, width), BF),
        sd((rows, units), BF), sd((rows, width), BF), sd((rows, width), BF), sd((8, units), F32),
    )
    ins = (o, *weights, x, teacher, cot, keep, vec)
    stay = pl.BlockSpec(memory_space=pl.ANY)
    return pl.pallas_call(
        functools.partial(dense_kernel, FB=FFB),
        out_shape=outs,
        grid_spec=pltpu.PrefetchScalarGridSpec(
            num_scalar_prefetch=1,
            grid=(1,),
            in_specs=[whole(o.shape)] + [stay] * 6 + [whole(a.shape) for a in ins[7:]],
            out_specs=tuple(whole(a.shape) for a in outs),
            scratch_shapes=[
                pltpu.VMEM((width, width), BF), pltpu.VMEM((width, units), BF), pltpu.VMEM((units, width), BF),
                pltpu.VMEM((rows, width), F32), pltpu.VMEM((rows, 1), F32), pltpu.VMEM((rows, width), F32),
                pltpu.VMEM((rows, units), F32), pltpu.VMEM((rows, width), F32), pltpu.SemaphoreType.DMA((8,)),
            ],
        ),
        compiler_params=pltpu.CompilerParams(vmem_limit_bytes=GRANT),
        cost_estimate=cost(12_000_000_000, 30_000_000, 4_000_000),
        name="dense",
    )(who, *ins)


def finish_kernel(
    who, dq0, dq1, dq2, dq3, own_ref, pair_ref, left_ref, right_ref, turn_ref, w_ref,
    all_ref, sums_ref, dx_ref, gx_ref, gy_ref, next_left, next_right, held,
):
    d = pl.program_id(0)
    rows, width = dx_ref.shape
    cut = width // 2

    @pl.when(d == 0)
    def _():
        sums_ref[...] = jnp.zeros_like(sums_ref)
        held[2 * BLK :, :] = jnp.zeros((held.shape[0] - 2 * BLK, held.shape[1]), BF)
        for base, extra in ((0, left_ref), (BLK, right_ref)):

            def gather(r, base=base, extra=extra):
                at = pl.ds(pl.multiple_of(base + r, 128), 128)
                value = own_ref[at, :].astype(F32) + pair_ref[at, :].astype(F32)
                held[at, :] = (value + extra[pl.ds(r, 128), :].astype(F32)).astype(BF)

            sweep(BLK, 128, gather)

    tok = mm(turn_ref[0], held[pl.ds(pl.multiple_of(who[3 + d], 16), SPAN), :]).astype(BF)
    dq = sum(ref[...].astype(F32) for ref in (dq0, dq1, dq2, dq3)).astype(BF)
    all_ref[:, 0:256] = dq
    all_ref[:, 256:640] = tok
    sums_ref[0:1, 0:256] += jnp.sum(dq.astype(F32), axis=0, keepdims=True)
    sums_ref[0:1, 256:640] += jnp.sum(tok.astype(F32), axis=0, keepdims=True)
    part = mm(all_ref[...], w_ref[...], NT).astype(BF)

    @pl.when(d == 0)
    def _():
        dx_ref[...] = part

    @pl.when(d == 1)
    def _():
        gx_ref[0:rows, :] = part[:, :cut]
        next_right[...] = part[:, cut:]

    @pl.when(d == 2)
    def _():
        next_left[...] = part[:, :cut]
        gy_ref[0:rows, :] = part[:, cut:]

    @pl.when(d == 3)
    def _():
        gx_ref[rows:, :] = part[:, :cut]
        gy_ref[rows:, :] = part[:, cut:]


def finish(who, dqs, own, pair, left, right, turn, w_heads):
    sd = jax.ShapeDtypeStruct
    rows, width = turn.shape[1], w_heads.shape[0]
    cols = dqs[0].shape[1] + own.shape[1]
    ins = (*dqs, own, pair, left, right, turn, w_heads)
    shapes = ((rows, width), (2 * rows, width // 2), (2 * rows, width // 2), (rows, width // 2), (rows, width // 2))
    outs = (sd((4 * rows, cols), BF), sd((8, cols), F32)) + tuple(sd(s, BF) for s in shapes)

    def by_block(shape):
        return pl.BlockSpec((rows, shape[1]), lambda d, *_: (d, 0))

    return pl.pallas_call(
        finish_kernel,
        out_shape=outs,
        grid_spec=pltpu.PrefetchScalarGridSpec(
            num_scalar_prefetch=1,
            grid=(4,),
            in_specs=[by_block(a.shape) for a in ins[:4]]
            + [whole(a.shape) for a in ins[4:8]]
            + [pl.BlockSpec((1, *turn.shape[1:]), lambda d, *_: (d, 0, 0)), whole(w_heads.shape)],
            out_specs=(by_block(outs[0].shape), whole(outs[1].shape)) + tuple(whole(s) for s in shapes),
            scratch_shapes=[pltpu.VMEM((2 * BLK + 128, own.shape[1]), BF)],
        ),
        compiler_params=pltpu.CompilerParams(vmem_limit_bytes=GRANT),
        cost_estimate=cost(3_000_000_000, 16_000_000),
        name="finish",
    )(who, *ins)


def part_out(who, held, am, ao, bm, bo, sides):
    part = am.shape[0]
    for mine, other, side, base in ((am, ao, sides[0], 0), (bm, bo, sides[1], 2 * part)):

        def move(r, mine=mine, other=other, side=side, base=base):
            mine[pl.ds(r, 16), :] = held[pl.ds(pl.multiple_of(base + side * part + r, 16), 16), :]
            other[pl.ds(r, 16), :] = held[pl.ds(pl.multiple_of(base + (1 - side) * part + r, 16), 16), :]

        sweep(part, 16, move)


def plus(left, right, at):
    return (left[at, :].astype(F32) + right[at, :].astype(F32)).astype(BF)


def first_kernel(who, back_a, back_b, in_a, in_b, out_a, out_b, am, ao, bm, bo, held):
    width = back_a.shape[1]
    tall = in_a.shape[0]

    def upper(r):
        at = pl.ds(r, 16)
        for k in range(4):
            held[at, k * width : (k + 1) * width] = plus(back_a, back_b, pl.ds(pl.multiple_of(k * tall + r, 16), 16))
        held[pl.ds(pl.multiple_of(tall + r, 16), 16), :] = plus(in_a, in_b, at)

    def lower(r):
        held[pl.ds(pl.multiple_of(2 * tall + r, 16), 16), :] = plus(out_a, out_b, pl.ds(r, 16))

    sweep(tall, 16, upper)
    sweep(out_a.shape[0], 16, lower)
    part_out(who, held, am, ao, bm, bo, (lax.rem(who[1], 2), who[1] // 2))


def both_kernel(who, a_mine, a_got, b_mine, b_got, both):
    del who
    part = a_mine.shape[0]

    def work(r):
        both[pl.ds(r, 16), :] = plus(a_mine, a_got, pl.ds(r, 16))
        both[pl.ds(pl.multiple_of(part + r, 16), 16), :] = plus(b_mine, b_got, pl.ds(r, 16))

    sweep(part, 16, work)


def second_kernel(who, a_mine, a_got, b_mine, b_got, am, ao, bm, bo, held):
    both_kernel(who, a_mine, a_got, b_mine, b_got, held)
    part_out(who, held, am, ao, bm, bo, (who[1] // 2, lax.rem(who[1], 2)))


def join_kernel(who, a, b, c, d, back_ref, in_ref, out_ref, vec_ref, held):
    step = pl.program_id(0)

    @pl.when(step == 0)
    def _():
        gather_pieces(who, (a, b, c, d), held)

    tall = held.shape[0] - 128
    tall, width = tall // 2, back_ref.shape[1]
    cols = pl.ds(pl.multiple_of(step * width, 128), width)
    back_ref[...] = held[0:tall, cols].astype(F32)
    rows = in_ref.shape[0]
    in_ref[...] = held[pl.ds(pl.multiple_of(tall + step * rows, 16), rows), :].astype(F32)

    @pl.when(step < 3)
    def _():
        out_ref[...] = held[2 * tall :, cols].astype(F32)

    @pl.when(step == 3)
    def _():
        vec_ref[...] = held[2 * tall : 2 * tall + 16, 3 * width :].astype(F32)


def gather_pieces(who, pieces, held):
    s1, s2 = lax.rem(who[1], 2), who[1] // 2
    part = pieces[0].shape[0] // 2
    for at, ref in enumerate(pieces):
        color, i = at // 2, at % 2
        for j in range(2):
            spot = (s1 ^ i) * 2 + (s2 ^ j) if color == 0 else 4 + (s2 ^ i) * 2 + (s1 ^ j)

            def move(r, spot=spot, ref=ref, j=j):
                frm = pl.ds(pl.multiple_of(j * part + r, 16), 16)
                held[pl.ds(pl.multiple_of(spot * part + r, 16), 16), :] = ref[frm, :]

            sweep(part, 16, move)

def join(who, pieces, back, first, out, total):
    sd = jax.ShapeDtypeStruct
    tall, width = first[0], back[1]
    outs = (sd(back, F32), sd(first, F32), sd(out, F32), sd((16, width), F32))
    return pl.pallas_call(
        join_kernel,
        out_shape=outs,
        grid_spec=pltpu.PrefetchScalarGridSpec(
            num_scalar_prefetch=1,
            grid=(4,),
            in_specs=[whole(a.shape) for a in pieces],
            out_specs=(
                pl.BlockSpec((tall, width), lambda k, *_: (k, 0)),
                pl.BlockSpec((tall // 4, first[1]), lambda k, *_: (k, 0)),
                pl.BlockSpec((128, width), lambda k, *_: (jnp.minimum(k, 2), 0)),
                whole((16, width)),
            ),
            scratch_shapes=[pltpu.VMEM((total, first[1]), BF)],
        ),
        compiler_params=pltpu.CompilerParams(vmem_limit_bytes=GRANT),
        cost_estimate=cost(1_000_000, 16_000_000),
        name="join",
    )(who, *pieces)


def small_call(kernel, who, pieces, outs, scratch, name, grant=24 << 20):
    return pl.pallas_call(
        kernel,
        out_shape=tuple(jax.ShapeDtypeStruct(*s) for s in outs),
        grid_spec=pltpu.PrefetchScalarGridSpec(
            num_scalar_prefetch=1,
            grid=(1,),
            in_specs=[whole(a.shape) for a in pieces],
            out_specs=tuple(whole(s[0]) for s in outs),
            scratch_shapes=scratch,
        ),
        compiler_params=pltpu.CompilerParams(vmem_limit_bytes=grant),
        cost_estimate=cost(1_000_000, 9_000_000),
        name=name,
    )(who, *pieces)


def heads_kernel(who, in_ref, q_ref, k_ref, v_ref, bias_ref):
    tall = in_ref.shape[1]
    for c in range(in_ref.shape[0] // 4):
        at = slice(c * tall, (c + 1) * tall)
        for a in range(4):
            cols = slice(a * 192, (a + 1) * 192)
            block = in_ref[c * 4 + (who[1] ^ a)].astype(F32)
            q_ref[at, cols] = block[:, 64:256]
            v_ref[at, cols] = block[:, 256:448]
            k_ref[at, cols] = block[:, 448:640]
            if c == 0:
                for k in range(3):
                    spot = slice(a * 192 + k * 64, a * 192 + (k + 1) * 64)
                    bias_ref[0:1, spot] = block[k : k + 1, 0:64]
                    bias_ref[8:9, spot] = block[k + 3 : k + 4, 0:64]


def heads_out(who, gathered):
    outs = (((384, 768), F32),) * 3 + (((16, 768), F32),)
    return small_call(heads_kernel, who, (gathered,), outs, [], "heads_out")


def swap(block, axis="fsdp"):
    return lax.ppermute(block, axis, [(0, 1), (1, 0)])


def shifted(block, axis, distance):
    devices = range(lax.axis_size(axis))
    route = [(i - distance, i) for i in devices if i - distance in devices]
    return lax.ppermute(block, axis, route)


def flip(block, bit, axis="uly"):
    return lax.ppermute(block, axis, [(i, i ^ bit) for i in range(lax.axis_size(axis))])


def exchange(rows, axis):
    return lax.all_to_all(rows, axis, split_axis=0, concat_axis=0, tiled=True)


def spread_rows(rows, axis):
    count = lax.axis_size(axis)
    return exchange(jnp.broadcast_to(rows[None], (count, *rows.shape)).reshape(-1, rows.shape[1]), axis)


def sum_parts(rows, count):
    got = rows.reshape(count, -1, rows.shape[1])
    return sum(got[i].astype(F32) for i in range(count)).astype(BF)


def sum_scatter(rows, axis):
    return sum_parts(exchange(rows, axis), lax.axis_size(axis))


def add(left, right):
    return (left.astype(F32) + right.astype(F32)).astype(BF)


def line_step(held, bit):
    return flip(held, bit, "ctx")


def line_join(held, got, bit):
    low = (lax.axis_index("ctx") & bit) == 0
    return jnp.stack([jnp.where(low, held, got), jnp.where(low, got, held)], axis=1).reshape(-1, *held.shape[1:])


def line_rest(held, bit):
    while bit > 0:
        held = line_join(held, line_step(held, bit), bit)
        bit //= 2
    return held.reshape(-1, held.shape[2])


def chunks_of(rows, axis):
    count, me = lax.axis_size(axis), lax.axis_index(axis)
    split = rows.reshape(count, -1, rows.shape[1])
    picked = [lax.dynamic_index_in_dim(split, me ^ k, 0, keepdims=False) for k in range(count)]
    return [picked[0]] + [flip(picked[k], k, axis) for k in range(1, count)]


def tie(*values):
    return lax.optimization_barrier(values)


def on_device(
    tokens, teacher, cotangent, valid, teacher_ok, doc_starts, w_query, w_key, w_value, w_out, w_in, w_back,
    bias_query, bias_value, bias_out, bias_in, bias_back, norm1_gain, norm1_bias, norm2_gain, norm2_bias,
):
    groups = lax.axis_size("uly")
    spans = lax.axis_size("ctx")
    rows, width = tokens.shape
    block = rows * groups * 2
    stream = block * spans
    ctx_index = lax.axis_index("ctx")
    uly = lax.axis_index("uly")
    half = lax.axis_index("fsdp")
    head_cols = width // groups
    shard = w_query.shape[0]
    upper = uly // 2

    small = (bias_query, bias_value, bias_out, bias_in, bias_back, norm1_gain, norm1_bias, norm2_gain, norm2_bias)
    valid_one = valid[None, :]
    valid_own = jnp.concatenate([valid_one, flip(valid_one, 1), flip(valid_one, 2), flip(valid_one, 3)], axis=0)
    x_own, valid_own, w_query, w_key, w_value, *small = tie(tokens, valid_own, w_query, w_key, w_value, *small)
    x_x, x_y = flip(x_own, 1), flip(x_own, 2)
    valid_pair = swap(valid_own)
    place = jnp.arange(groups, dtype=jnp.int32)
    in_plane = place ^ uly
    valid_mine = jnp.take(valid_own, in_plane, axis=0).reshape(2, BLK)
    valid_next = jnp.take(valid_pair, in_plane, axis=0).reshape(2, BLK)
    from_low = shifted(jnp.stack([valid_mine[1], valid_next[1]]), "ctx", 1)
    from_high = shifted(jnp.stack([valid_mine[0], valid_next[0]]), "ctx", -1)
    block_valid = jnp.concatenate(
        [valid_mine, valid_next, from_low[:1], from_high[:1], from_low[1:], from_high[1:]], axis=0
    )
    count = jnp.full((8, 128), jnp.sum(valid_mine) + jnp.sum(valid_next), jnp.int32)
    bit = 1
    while bit < spans:
        count = count + flip(count, bit, "ctx")
        bit *= 2
    count = count[0, 0].astype(F32)

    start_col = uly * head_cols
    cut = [lax.dynamic_slice_in_dim(w, start_col, head_cols, 1) for w in (w_query, w_value, w_key)]
    w_mine = jnp.concatenate([jnp.zeros((shard, 256 - head_cols), BF), *cut], axis=1)
    w_other = swap(w_mine)
    packed = jnp.concatenate(small)
    packed_pair = swap(packed)
    first, second = jnp.where(half == 0, packed, packed_pair), jnp.where(half == 0, packed_pair, packed)
    vectors = []
    at = 0
    for p in small:
        n = p.shape[0]
        vectors.append(jnp.concatenate([first[at : at + n], second[at : at + n]]).astype(F32))
        at += n
    bq_all, bv_all = vectors[:2]
    vec = jnp.stack([jnp.pad(v, (0, w_in.shape[1] - v.shape[0])) for v in vectors[2:]] + [jnp.zeros((w_in.shape[1],), F32)])
    bias_heads = jnp.concatenate(
        [
            jnp.zeros((256 - head_cols,), F32),
            lax.dynamic_slice_in_dim(bq_all, start_col, head_cols, 0),
            lax.dynamic_slice_in_dim(bv_all, start_col, head_cols, 0),
            jnp.zeros((head_cols,), F32),
        ]
    )

    step = jnp.asarray([0, 0, 0, 0, -1, 1, -1, 1], jnp.int32)
    side = jnp.asarray([0, 1, 0, 1, 1, 0, 1, 0], jnp.int32)
    swapped = jnp.asarray([0, 0, 1, 1, 0, 0, 1, 1], jnp.int32)
    inner = jnp.arange(BLK, dtype=jnp.int32)
    first_block = (ctx_index + step) * (2 * groups) + side * groups + (half ^ swapped)
    spot = (first_block[:, None] + 2 * (inner // rows)[None, :]) * rows + lax.rem(inner, rows)[None, :]
    x_x, x_y, block_valid = tie(x_x, x_y, block_valid)
    edges = jnp.concatenate([doc_starts, jnp.full((DOCS + 1,), stream, jnp.int32)])
    window_first = jnp.maximum(ctx_index * block - block // 2, 0)
    first_doc = jnp.sum((doc_starts <= window_first).astype(jnp.int32)) - 1
    near = lax.dynamic_slice_in_dim(edges, first_doc, DOCS + 1, 0)
    tiles = groups * rows // TQ
    per = rows // TQ
    tile_ids = jnp.arange(tiles, dtype=jnp.int32)
    qfirst = ctx_index * block + (((tile_ids // per) ^ uly) * 2 + half) * rows + lax.rem(tile_ids, per) * TQ
    q_lo = jnp.max(jnp.where(near[None, :] <= qfirst[:, None], near[None, :], 0), axis=1)
    q_hi = jnp.min(jnp.where(near[None, :] <= qfirst[:, None] + TQ - 1, stream, near[None, :]), axis=1)
    limits = jnp.concatenate([near, q_lo, q_hi])
    counted = jnp.sum(block_valid[:, None, :] * (spot[:, None, :] < limits[None, :, None]), axis=-1)
    bounds = counted[:, : DOCS + 1]
    cnt_lo = counted[:, DOCS + 1 : DOCS + 1 + tiles].T
    cnt_hi = counted[:, DOCS + 1 + tiles :].T
    pad64 = jnp.zeros((bounds.shape[0], 128 - DOCS), jnp.int32)
    lo_tab = jnp.concatenate([bounds[:, :DOCS], pad64], axis=1)
    hi_tab = jnp.concatenate([bounds[:, 1:], pad64], axis=1)
    slo_tab = jnp.concatenate([near[:DOCS], pad64[0]])[None, :]
    shi_tab = jnp.concatenate([near[1:], pad64[0]])[None, :]
    some = cnt_hi > cnt_lo
    tlo = jnp.where(some, cnt_lo // TK, 0)
    thi = jnp.where(some, (cnt_hi + TK - 1) // TK, 0)
    tables = (tlo, thi, qfirst, lo_tab, hi_tab, slo_tab, shi_tab)
    before = mm(valid_own.astype(BF), (jnp.arange(rows)[:, None] < jnp.arange(rows)[None, :]).astype(BF)).astype(jnp.int32)
    filled = jnp.sum(valid_own, axis=1)
    shift = jnp.where(lax.rem(in_plane, 2) == 1, jnp.take(filled, place ^ 1), 0)
    base = (in_plane // 2) * BLK + (shift // 16) * 16
    goes_to = jnp.where(valid_own > 0, before + lax.rem(shift, 16)[:, None], 2 * BLK)
    ranks = jnp.arange(SPAN, dtype=jnp.int32)
    chosen = (goes_to[:, None, :] == ranks[None, :, None]).astype(BF)
    turned = (goes_to[:, :, None] == ranks[None, None, :]).astype(BF)
    who = jnp.concatenate([jnp.stack([half, uly, upper]).astype(jnp.int32), base])
    loss_scale = jnp.float32(stream) / count
    keep = (loss_scale * (valid * teacher_ok).astype(F32))[:, None]

    x_x, x_y, w_other = tie(x_x, x_y, w_other)
    x_top, x_bottom = flip(x_y[: rows // 2], 1), flip(x_x[rows // 2 :], 2)
    x_top, x_bottom, chosen, bias_heads, *tables = tie(x_top, x_bottom, chosen, bias_heads, *tables)

    q_low, kv_own, kv_up, kv_down, w_heads = project(
        who, (tokens, x_x, x_y, x_top, x_bottom), w_mine, w_other, bias_heads[None, :], chosen
    )
    kv_from_left, kv_from_right = shifted(kv_up, "ctx", 1), shifted(kv_down, "ctx", -1)
    w_out, w_in, w_back, kv_own = tie(w_out, w_in, w_back, kv_own)
    wo_pair, win_pair, wback_pair = swap(w_out), swap(w_in), swap(w_back)
    kv_pair = swap(kv_own)
    state = attend(tables, q_low, (kv_own,), 0)
    kv_halo = jnp.concatenate([kv_from_left, kv_from_right], axis=0)
    kv_halo, kv_pair, *state = tie(kv_halo, kv_pair, *state)
    kv_halo_pair = swap(kv_halo)
    state = attend(tables, q_low, (kv_pair,), 2, state)
    o_heads, o_turned, lse = attend(tables, q_low, (kv_halo, kv_halo_pair), 4, state, last=True)
    o_rel = o_heads.reshape(groups, rows, head_cols)
    o_rest = [flip(o_rel[d], d) for d in range(1, groups)]
    o_heads, x_late, x_x, x_y, x_top, x_bottom = tie(o_heads, tokens, x_x, x_y, x_top, x_bottom)
    x_all = jnp.concatenate([x_late, x_x, x_y, x_top, x_bottom], axis=0)

    x_all, turned, *o_rest = tie(x_all, turned, *o_rest)
    o_all = jnp.concatenate([o_rel[0], *o_rest], axis=0)

    out, d_resid1, d_parts, act, d_branch, d_pre, hidden_low, d_proj, sums = dense(
        who, o_all, (w_out, wo_pair, w_in, win_pair, w_back, wback_pair), tokens, teacher, cotangent, keep, vec
    )
    d_rel = d_parts.reshape(groups, rows, head_cols)
    tall = w_back.shape[0]
    vector_rows = jnp.concatenate(
        [sums[i, :width].reshape(2, -1) for i in (0, 2, 3, 4, 5, 6)] + [sums[1].reshape(2, -1)], axis=1
    ).reshape(2, -1, width)
    vector_rows = jnp.pad(vector_rows, ((0, 0), (0, 128 - vector_rows.shape[1]), (0, 0))).astype(BF)
    o_rows = o_all.reshape(groups, rows, head_cols)

    def back_part(side):
        return mm(lax.dynamic_slice_in_dim(act, side * tall, tall, 1), d_branch, TN).astype(BF)

    def in_part(side):
        return mm(lax.dynamic_slice_in_dim(hidden_low, side * shard, shard, 1), d_pre, TN).astype(BF)

    def out_part(side):
        both = [
            mm(lax.dynamic_index_in_dim(o_rows, (2 * side + e) ^ uly, 0, keepdims=False), d_proj, TN).astype(BF)
            for e in range(2)
        ]
        stack = jnp.concatenate([*both, lax.dynamic_index_in_dim(vector_rows, side, 0, keepdims=False)], axis=0)
        return jnp.concatenate([stack[i * 128 : (i + 1) * 128] for i in range(4)], axis=1)

    d_rest = [flip(d_rel[d], d) for d in range(1, groups)]
    back_got, in_got, out_got, *d_rest = tie(back_part(1 - half), in_part(1 - half), out_part(1 - half), *d_rest)
    back_got, in_got, out_got = swap(back_got), swap(in_got), swap(out_got)
    back_mine, in_mine, out_mine = back_part(half), in_part(half), out_part(half)
    back_got, in_got, out_got, back_mine, in_mine, out_mine = tie(
        back_got, in_got, out_got, back_mine, in_mine, out_mine
    )
    wide = w_in.shape[1]
    total = 2 * shard + 128
    am, ao, bm, bo = small_call(
        first_kernel, who, (back_mine, back_got, in_mine, in_got, out_mine, out_got),
        (((total // 4, wide), BF),) * 4, [pltpu.VMEM((total, wide), BF)], "first_stage",
    )
    d_heads = jnp.concatenate([d_rel[0], *d_rest], axis=0)
    d_heads, am, ao, bm, bo = tie(d_heads, am, ao, bm, bo)

    ag, bg = flip(ao, 1), flip(bo, 2)
    args = (tables, q_low, d_heads, o_turned, lse)
    dq0, got_lo, got_hi, delta = attend_back(
        *args, kv_halo_pair, 6, first=True, cuts=2, name="back_halo_pair"
    )
    got_lo, got_hi, delta = tie(got_lo, got_hi, delta)
    args = (tables, q_low, d_heads, delta, lse)
    got_lo, got_hi = swap(got_lo), swap(got_hi)
    dq1, halo_lo, halo_hi = attend_back(*args, kv_halo, 4, cuts=2, name="back_halo", size=1_000_000)
    halo_lo, halo_hi, got_lo, got_hi, ag, bg = tie(halo_lo, halo_hi, got_lo, got_hi, ag, bg)

    halo_lo, halo_hi = add(halo_lo, got_lo), add(halo_hi, got_hi)
    am, ao, bm, bo = small_call(
        second_kernel, who, (am, ag, bm, bg), (((total // 8, wide), BF),) * 4,
        [pltpu.VMEM((total // 2, wide), BF)], "second_stage", 12 << 20,
    )
    halo_lo, halo_hi, delta, am, ao, bm, bo = tie(halo_lo, halo_hi, delta, am, ao, bm, bo)
    args = (tables, q_low, d_heads, delta, lse)
    ag, bg = flip(ao, 2), flip(bo, 1)
    from_left, from_right = shifted(halo_hi, "ctx", 1), shifted(halo_lo, "ctx", -1)
    dq2, dkv_pair = attend_back(*args, kv_pair, 2, name="back_pair")
    dkv_pair, ag, bg, from_left, from_right = tie(dkv_pair, ag, bg, from_left, from_right)

    (line,) = small_call(both_kernel, who, (am, ag, bm, bg), (((total // 4, wide), BF),), [], "third_stage", 12 << 20)
    line, dkv_pair, delta = tie(line, dkv_pair, delta)
    args = (tables, q_low, d_heads, delta, lse)
    line = exchange(line, "ctx")
    pair_got = swap(dkv_pair)
    dq3, dkv_own = attend_back(*args, kv_own, 0, name="back_own")
    dkv_own, line, pair_got = tie(dkv_own, line, pair_got)
    line = sum_parts(line, spans)
    line, dkv_own = tie(line, dkv_own)
    line = spread_rows(line, "ctx")

    d_all, d_sums, dx_own, give_x, give_y, left_next, right_next = finish(
        who, (dq0, dq1, dq2, dq3), dkv_own, pair_got, from_left, from_right, turned, w_heads
    )
    d_all, give_x, give_y = tie(d_all, give_x, give_y)
    give_x, give_y = flip(give_x, 1), flip(give_y, 2)
    corner = d_sums[0, 64:].reshape(9, 64)

    def heads_part(side):
        grad = mm(lax.dynamic_slice_in_dim(x_all, side * shard, shard, 1), d_all, TN)
        return lax.dynamic_update_slice(grad, corner, (0, 0)).astype(BF)

    heads_other = heads_part(1 - half)
    heads_got = swap(heads_other)
    heads_mine = heads_part(half)
    heads_sum = add(heads_mine, heads_got)
    line, give_x, give_y, *heads_parts = tie(line, give_x, give_y, *chunks_of(heads_sum, "ctx"))
    heads_sum = sum(part.astype(F32) for part in heads_parts).astype(BF)
    a_near, b_near = line[: total // 8], line[total // 8 :]
    a_got, b_got, *heads_rest = tie(
        flip(a_near, 2), flip(b_near, 1), *[flip(heads_sum, d) for d in range(1, groups)]
    )
    a_near = jnp.concatenate([a_near, a_got], axis=0)
    b_near = jnp.concatenate([b_near, b_got], axis=0)
    a_far, b_far = flip(a_near, 1), flip(b_near, 2)
    left_next = flip(add(left_next, give_x[rows:]), 2)
    right_next = flip(add(right_next, give_y[rows:]), 1)
    heads_sum = jnp.concatenate([heads_sum, *heads_rest], axis=0)
    heads_all = spread_rows(heads_sum, "ctx").reshape(spans * groups, -1, heads_sum.shape[1])
    grad_in = d_resid1 + dx_own.astype(F32)
    grad_in = grad_in + jnp.concatenate([give_x[:rows].astype(F32), give_y[:rows].astype(F32)], axis=1)
    grad_in = grad_in + jnp.concatenate([left_next.astype(F32), right_next.astype(F32)], axis=1)
    g_back, g_in, g_out, g_vec = join(
        who, (a_near, a_far, b_near, b_far), w_back.shape, w_in.shape, w_out.shape, total
    )
    g_query, g_key, g_value, g_bias = heads_out(who, heads_all)
    g_bias_q = lax.dynamic_slice_in_dim(g_bias[0], half * shard, shard, 0)
    g_bias_v = lax.dynamic_slice_in_dim(g_bias[8], half * shard, shard, 0)
    flat = g_vec.reshape(-1)
    g_bo, g_bb, g_g1, g_s1, g_g2, g_s2 = [flat[i * shard : (i + 1) * shard] for i in range(6)]
    g_bin = flat[6 * shard : 6 * shard + bias_in.shape[0]]
    return (
        out, grad_in, g_query, g_key, g_value, g_out, g_in, g_back,
        g_bias_q, g_bias_v, g_bo, g_bin, g_bb, g_g1, g_s1, g_g2, g_s2,
    )


def solution(mesh):
    placed = (
        P(("ctx", "uly", "fsdp"), None),
        P(("ctx", "uly", "fsdp"), None),
        P(("ctx", "uly", "fsdp"), None),
        P(("ctx", "uly", "fsdp")),
        P(("ctx", "uly", "fsdp")),
        P(),
        P("fsdp", None),
        P("fsdp", None),
        P("fsdp", None),
        P("fsdp", None),
        P("fsdp", None),
        P("fsdp", None),
        P("fsdp"),
        P("fsdp"),
        P("fsdp"),
        P("fsdp"),
        P("fsdp"),
        P("fsdp"),
        P("fsdp"),
        P("fsdp"),
        P("fsdp"),
    )
    return jax.shard_map(
        on_device,
        mesh=mesh,
        in_specs=placed,
        out_specs=(
            P(("ctx", "uly", "fsdp"), None),
            P(("ctx", "uly", "fsdp"), None),
            P("fsdp", None),
            P("fsdp", None),
            P("fsdp", None),
            P("fsdp", None),
            P("fsdp", None),
            P("fsdp", None),
            P("fsdp"),
            P("fsdp"),
            P("fsdp"),
            P("fsdp"),
            P("fsdp"),
            P("fsdp"),
            P("fsdp"),
            P("fsdp"),
            P("fsdp"),
        ),
        check_vma=False,
    )
```

```python
import functools

import jax
import jax.numpy as jnp
from jax import lax
from jax.experimental import pallas as pl
from jax.experimental.pallas import tpu as pltpu
from jax.sharding import PartitionSpec as P

HEADS = 12
HD = 64
BLK = 1024
SPAN = 640
TQ = 512
TK = 256
DOCS = 64
FFB = 1536
GRANT = 63 << 20
MASKED = -1e30
BF = jnp.bfloat16
F32 = jnp.float32
NT = (((1,), (1,)), ((), ()))
NN = (((1,), (0,)), ((), ()))
TN = (((0,), (0,)), ((), ()))


def mm(left, right, dims=NN):
    return lax.dot_general(left, right, dims, preferred_element_type=F32)


def whole(shape):
    return pl.BlockSpec(shape, lambda *_: (0,) * len(shape), pipeline_mode=pl.Buffered(1))


def sweep(total, step, work):
    def one(i, _):
        work(pl.multiple_of(i * step, step))
        return 0

    lax.fori_loop(0, total // step, one, 0)


def cost(flops, moved, special=0):
    return pl.CostEstimate(flops=flops, bytes_accessed=moved, transcendentals=special)


def lane_ids(rows):
    return lax.broadcasted_iota(jnp.int32, (rows, 128), 1)


def build_keys(sources, slot0, lo_ref, hi_ref, kaug, transposed, low_half):
    per = BLK // TK
    for at, kv in enumerate(sources):

        def one(j, _, at=at, kv=kv):
            rows = pl.ds(pl.multiple_of(j * TK, TK), TK)
            tile = at * (kv.shape[0] // TK) + j
            slot = slot0 + at * (kv.shape[0] // BLK) + j // per
            out = pl.ds(pl.multiple_of(tile * TK, TK), TK)
            rank = lax.broadcasted_iota(jnp.int32, (TK, 128), 0) + lax.rem(j, per) * TK
            inside = (rank >= lo_ref[pl.ds(slot, 1), :]) & (rank < hi_ref[pl.ds(slot, 1), :])
            bias = jnp.where(inside, 0.0, MASKED).astype(BF)
            kaug[out, 0:128] = jnp.where(lane_ids(TK) < 64, bias, kv[rows, 128:256])
            kaug[out, 128:256] = kv[rows, 256:384]
            if low_half:
                transposed[tile] = kv[rows, 0:256].T[0:192]
            else:
                transposed[tile] = kaug[out, :].T[64:256]
            return 0

        lax.fori_loop(0, kv.shape[0] // TK, one, 0)


def stack_queries(q, first, slo_ref, shi_ref, qs):
    lane = lane_ids(TQ)
    spot = lax.broadcasted_iota(jnp.int32, (TQ, 128), 0) + first
    mine = ((spot >= slo_ref[...]) & (spot < shi_ref[...])).astype(F32).astype(BF)
    zero = jnp.zeros((TQ, 128), BF)
    low, high = q[:, 0:128], q[:, 128:256]
    mark = jnp.where(lane < 64, mine, zero)
    qs[0:TQ, 0:128] = jnp.where(lane < 64, mine, low)
    qs[TQ : 2 * TQ, 0:128] = mark
    qs[2 * TQ :, 0:128] = mark
    qs[0:TQ, 128:256] = zero
    qs[TQ : 2 * TQ, 128:256] = jnp.where(lane < 64, high, zero)
    qs[2 * TQ :, 128:256] = jnp.where(lane < 64, zero, high)


def attend_kernel(*refs, slot0, count, resume, last):
    tlo, thi, qfirst, q_ref = refs[:4]
    sources = refs[4 : 4 + count]
    lo_ref, hi_ref, slo_ref, shi_ref = refs[4 + count : 8 + count]
    at = 8 + count
    if resume:
        acc_in, stat_in = refs[at : at + 2]
        at += 2
    if last:
        o_ref, ot_ref, lse_ref = refs[at : at + 3]
        at += 3
    else:
        acc_out, stat_out = refs[at : at + 2]
        at += 2
    kaug, vt, qs, acc, m_s, l_s = refs[at:]
    i = pl.program_id(0)

    @pl.when(i == 0)
    def _():
        build_keys(sources, slot0, lo_ref, hi_ref, kaug, vt, True)

    slots = count * sources[0].shape[0] // BLK
    per = BLK // TK
    stack_queries(q_ref[...], qfirst[i], slo_ref, shi_ref, qs)
    if resume:
        m_s[...] = stat_in[0, 0:1, :]
        l_s[...] = stat_in[0, 1:2, :]
        acc[...] = acc_in[0]
    else:
        m_s[...] = jnp.full_like(m_s, 2 * MASKED)
        l_s[...] = jnp.zeros_like(l_s)
        acc[...] = jnp.zeros_like(acc)

    def slot_loop(s, _):
        def key_loop(t, _):
            tile = s * per + t
            keys = pl.ds(pl.multiple_of(tile * TK, TK), TK)
            st = mm(kaug[keys, :], qs[...], NT)
            m_old = m_s[...]
            m_new = jnp.maximum(m_old, jnp.max(st, axis=0, keepdims=True))
            fade = jnp.exp(m_old - m_new)
            p = jnp.exp(st - m_new)
            l_s[...] = l_s[...] * fade + jnp.sum(p, axis=0, keepdims=True)
            m_s[...] = m_new
            low = p.astype(BF)
            for h in range(3):
                cols = slice(h * TQ, (h + 1) * TQ)
                part = slice(h * HD, (h + 1) * HD)
                acc[part, :] = acc[part, :] * fade[:, cols] + mm(vt[tile, part, :], low[:, cols])
            return 0

        return lax.fori_loop(tlo[i, slot0 + s], thi[i, slot0 + s], key_loop, 0)

    lax.fori_loop(0, slots, slot_loop, 0)
    if last:
        total = l_s[...]
        for h in range(3):
            cols = slice(h * TQ, (h + 1) * TQ)
            part = slice(h * HD, (h + 1) * HD)
            acc[part, :] = acc[part, :] / total[:, cols]
        ot_ref[0] = acc[...]
        o_ref[...] = acc[...].T.astype(BF)
        lse_ref[0] = m_s[...] + jnp.log(total)
    else:
        acc_out[0] = acc[...]
        stat_out[0, 0:1, :] = m_s[...]
        stat_out[0, 1:2, :] = l_s[...]


def rows_spec(shape):
    return pl.BlockSpec((TQ, shape[1]), lambda i, *_: (i, 0))


def tile_spec(shape):
    return pl.BlockSpec((1, *shape[1:]), lambda i, *_: (i, 0, 0))


def attend(tables, q, sources, slot0, state=None, last=False):
    tlo, thi, qfirst, lo, hi, slo, shi = tables
    tiles = q.shape[0] // TQ
    keys = sum(s.shape[0] for s in sources)
    state = tuple(state) if state else ()
    sd = jax.ShapeDtypeStruct
    acc, stat = sd((tiles, 3 * HD, TQ), F32), sd((tiles, 2, 3 * TQ), F32)
    if last:
        o, lse = sd((q.shape[0], 3 * HD), BF), sd((tiles, 1, 3 * TQ), F32)
        outs, out_specs = (o, acc, lse), (rows_spec(o.shape), tile_spec(acc.shape), tile_spec(lse.shape))
    else:
        outs, out_specs = (acc, stat), (tile_spec(acc.shape), tile_spec(stat.shape))
    return pl.pallas_call(
        functools.partial(attend_kernel, slot0=slot0, count=len(sources), resume=bool(state), last=last),
        out_shape=outs,
        grid_spec=pltpu.PrefetchScalarGridSpec(
            num_scalar_prefetch=3,
            grid=(tiles,),
            in_specs=[rows_spec(q.shape)]
            + [whole(x.shape) for x in (*sources, lo, hi, slo, shi)]
            + [tile_spec(x.shape) for x in state],
            out_specs=out_specs,
            scratch_shapes=[
                pltpu.VMEM((keys, 256), BF),
                pltpu.VMEM((keys // TK, 3 * HD, TK), BF),
                pltpu.VMEM((3 * TQ, 256), BF),
                pltpu.VMEM((3 * HD, TQ), F32),
                pltpu.VMEM((1, 3 * TQ), F32),
                pltpu.VMEM((1, 3 * TQ), F32),
            ],
        ),
        compiler_params=pltpu.CompilerParams(vmem_limit_bytes=GRANT),
        cost_estimate=cost(12_000_000_000, 12_000_000, 10_000_000),
        name="attend",
    )(tlo, thi, qfirst, q, *sources, lo, hi, slo, shi, *state)


def attend_back_kernel(
    tlo, thi, qfirst, q_ref, do_ref, ot_ref, lse_ref, kv, lo_ref, hi_ref, slo_ref, shi_ref, dq_ref, *rest,
    slot0, first, cuts,
):
    dkv_refs, rest = rest[:cuts], rest[cuts:]
    if first:
        delta_ref, *rest = rest
    kaug, kt, qs, dos, acc, dk_s, dv_s = rest
    keys_all = kv.shape[0]
    slots = keys_all // BLK
    per = BLK // TK
    i = pl.program_id(0)

    @pl.when(i == 0)
    def _():
        build_keys((kv,), slot0, lo_ref, hi_ref, kaug, kt, False)
        dk_s[...] = jnp.zeros_like(dk_s)
        dv_s[...] = jnp.zeros_like(dv_s)

    stack_queries(q_ref[...], qfirst[i], slo_ref, shi_ref, qs)
    do = do_ref[...]
    lane = lane_ids(TQ)
    zero = jnp.zeros((TQ, 128), BF)
    dos[0:TQ, 0:128] = jnp.where(lane < 64, do[:, 0:128], zero)
    dos[TQ : 2 * TQ, 0:128] = jnp.where(lane < 64, zero, do[:, 0:128])
    dos[2 * TQ :, 0:128] = zero
    dos[0 : 2 * TQ, 128:256] = jnp.zeros((2 * TQ, 128), BF)
    dos[2 * TQ :, 128:192] = do[:, 128:192]
    dos[2 * TQ :, 192:256] = jnp.zeros((TQ, 64), BF)
    if first:
        both = do.astype(F32).T * ot_ref[0]
        delta = jnp.concatenate(
            [jnp.sum(both[h * HD : (h + 1) * HD], axis=0, keepdims=True) for h in range(3)], axis=1
        )
        delta_ref[0] = delta
    else:
        delta = ot_ref[0]
    lse = lse_ref[0]
    acc[...] = jnp.zeros_like(acc)

    def slot_loop(s, _):
        def key_loop(t, _):
            tile = s * per + t
            keys = pl.ds(pl.multiple_of(tile * TK, TK), TK)
            st = mm(kaug[keys, :], qs[...], NT)
            p = jnp.exp(st - lse)
            dp = mm(kv[keys, 0:256], dos[...], NT)
            ds = (p * (dp - delta)).astype(BF)
            dv_s[keys, :] += mm(p.astype(BF), dos[...])
            dk_s[keys, :] += mm(ds, qs[...])
            for h in range(3):
                cols = slice(h * TQ, (h + 1) * TQ)
                acc[(h + 1) * HD : (h + 2) * HD, :] += mm(kt[tile, h * HD : (h + 1) * HD, :], ds[:, cols])
            return 0

        return lax.fori_loop(tlo[i, slot0 + s], thi[i, slot0 + s], key_loop, 0)

    lax.fori_loop(0, slots, slot_loop, 0)
    dq_ref[...] = (acc[...] * HD ** (-0.5)).T.astype(BF)

    @pl.when(i == pl.num_programs(0) - 1)
    def _():
        share = keys_all // cuts
        for j, dkv_ref in enumerate(dkv_refs):

            def write(r, j=j, dkv_ref=dkv_ref):
                at = pl.ds(pl.multiple_of(j * share + r, TK), TK)
                to = pl.ds(r, TK)
                dkv_ref[to, 0:128] = dv_s[at, 0:128].astype(BF)
                dkv_ref[to, 128:256] = jnp.where(lane_ids(TK) < 64, dv_s[at, 128:256], dk_s[at, 0:128]).astype(BF)
                dkv_ref[to, 256:384] = dk_s[at, 128:256].astype(BF)

            sweep(share, TK, write)


def attend_back(tables, q, do, ot, lse, source, slot0, first=False, cuts=1, name="attend_back", size=14_000_000_000):
    tlo, thi, qfirst, lo, hi, slo, shi = tables
    tiles = q.shape[0] // TQ
    keys = source.shape[0]
    sd = jax.ShapeDtypeStruct
    piece = (keys // cuts, source.shape[1])
    outs = (sd(q.shape, BF),) + (sd(piece, BF),) * cuts
    out_specs = (rows_spec(q.shape),) + (whole(piece),) * cuts
    if first:
        outs += (sd(lse.shape, F32),)
        out_specs += (tile_spec(lse.shape),)
    return pl.pallas_call(
        functools.partial(attend_back_kernel, slot0=slot0, first=first, cuts=cuts),
        out_shape=outs,
        grid_spec=pltpu.PrefetchScalarGridSpec(
            num_scalar_prefetch=3,
            grid=(tiles,),
            in_specs=[rows_spec(q.shape), rows_spec(do.shape), tile_spec(ot.shape), tile_spec(lse.shape)]
            + [whole(x.shape) for x in (source, lo, hi, slo, shi)],
            out_specs=out_specs,
            scratch_shapes=[
                pltpu.VMEM((keys, 256), BF),
                pltpu.VMEM((keys // TK, 3 * HD, TK), BF),
                pltpu.VMEM((3 * TQ, 256), BF),
                pltpu.VMEM((3 * TQ, 256), BF),
                pltpu.VMEM((256, TQ), F32),
                pltpu.VMEM((keys, 256), F32),
                pltpu.VMEM((keys, 256), F32),
            ],
        ),
        compiler_params=pltpu.CompilerParams(vmem_limit_bytes=GRANT),
        cost_estimate=cost(size, size // 1000, size // 3000),
        name=name,
    )(tlo, thi, qfirst, q, do, ot, lse, source, lo, hi, slo, shi)


def project_kernel(
    who, x0, x1, x2, x3_top, x3_bottom, w_mine, w_other, bias_ref, chosen, q_ref, kv_ref, up_ref, down_ref, w_ref, held
):
    tall = w_mine.shape[0]
    rows = x0.shape[0]
    w_ref[pl.ds(pl.multiple_of(who[0] * tall, tall), tall), :] = w_mine[...]
    w_ref[pl.ds(pl.multiple_of((1 - who[0]) * tall, tall), tall), :] = w_other[...]
    held[...] = jnp.zeros_like(held)
    for d, x in enumerate((x0, x1, x2, (x3_top, x3_bottom))):
        if d < 3:
            value = mm(x[...], w_ref[...]) + bias_ref[...]
        else:
            value = jnp.concatenate([mm(x[0][...], w_ref[...]), mm(x[1][...], w_ref[...])], axis=0) + bias_ref[...]
        at = slice(d * rows, (d + 1) * rows)
        q_ref[at, :] = (value[:, :256].astype(BF).astype(F32) * HD ** (-0.5)).astype(BF)
        to = pl.ds(pl.multiple_of(who[3 + d], 16), SPAN)
        held[to, :] += mm(chosen[d], value[:, 256:].astype(BF))
    kv_ref[...] = held[0 : 2 * BLK, :].astype(BF)
    down_ref[...] = kv_ref[0:BLK, :]
    up_ref[...] = kv_ref[BLK:, :]


def project(who, xs, w_mine, w_other, bias, chosen):
    sd = jax.ShapeDtypeStruct
    rows, width = xs[0].shape
    cols = w_mine.shape[1]
    ins = (*xs, w_mine, w_other, bias, chosen)
    outs = (
        sd((4 * rows, 256), BF), sd((4 * rows, cols - 256), BF), sd((2 * rows, cols - 256), BF),
        sd((2 * rows, cols - 256), BF), sd((width, cols), BF),
    )
    return pl.pallas_call(
        project_kernel,
        out_shape=outs,
        grid_spec=pltpu.PrefetchScalarGridSpec(
            num_scalar_prefetch=1,
            grid=(1,),
            in_specs=[whole(a.shape) for a in ins],
            out_specs=tuple(whole(a.shape) for a in outs),
            scratch_shapes=[pltpu.VMEM((2 * BLK + 128, cols - 256), F32)],
        ),
        compiler_params=pltpu.CompilerParams(vmem_limit_bytes=24 << 20),
        cost_estimate=cost(3_000_000_000, 12_000_000),
        name="project",
    )(who, *ins)


def row_mean(v):
    return jnp.sum(v, axis=-1, keepdims=True) * (1.0 / v.shape[-1])

def dense_kernel(
    who, o_ref, wo_a, wo_b, win_a, win_b, wback_a, wback_b, x_ref, teacher_ref, cot_ref, keep_ref, vec_ref,
    out_ref, dres_ref, dparts_ref, act_ref, dbr_ref, dpre_ref, hid_ref, dproj_ref, sums_ref,
    wo, win, wback, xh, inv, hidden, gp, acc, sems, *, FB
):
    rows, width = x_ref.shape
    groups = o_ref.shape[0] // rows
    part = width // groups
    units = win.shape[1]
    wo_loads, win_loads, wback_loads = [], [], []
    for i in range(2):
        side = who[0] if i == 0 else 1 - who[0]
        for e in range(groups // 2):
            to = pl.multiple_of(((side * (groups // 2) + e) ^ who[1]) * part, part)
            wo_loads.append(
                pltpu.make_async_copy((wo_a, wo_b)[i].at[pl.ds(e * part, part)], wo.at[pl.ds(to, part)], sems.at[2 * i + e])
            )
        for j, (pieces, target, held) in enumerate((((win_a, win_b), win, win_loads), ((wback_a, wback_b), wback, wback_loads))):
            tall = target.shape[0] // 2
            to = pl.multiple_of(side * tall, tall)
            held.append(pltpu.make_async_copy(pieces[i], target.at[pl.ds(to, tall)], sems.at[4 + 2 * i + j]))
    for load in wo_loads + win_loads + wback_loads:
        load.start()
    b_out, b_in, b_back = vec_ref[0:1, 0:width], vec_ref[1:2, :], vec_ref[2:3, 0:width]
    gain1, shift1, gain2, shift2 = (vec_ref[i : i + 1, 0:width] for i in range(3, 7))
    for load in wo_loads:
        load.wait()
    total = x_ref[...].astype(F32) + b_out
    for i in range(groups):
        total += mm(o_ref[i * rows : (i + 1) * rows, :], wo[i * part : (i + 1) * part, :])
    center = total - row_mean(total)
    scale = lax.rsqrt(row_mean(center * center) + 1e-12)
    inv[...] = scale
    unit = center * scale
    xh[...] = unit
    hid = unit * gain1 + shift1
    hidden[...] = hid
    hid_ref[...] = hid.astype(BF)
    acc[...] = jnp.zeros_like(acc)
    for load in win_loads + wback_loads:
        load.wait()

    def up(n, _):
        cols = pl.ds(pl.multiple_of(n * FB, FB), FB)
        pre = mm(hid_ref[...], win[:, cols]) + vec_ref[1:2, cols]
        cdf = 0.5 + 0.5 * lax.erf(pre * 0.7071067811865476)
        act = (pre * cdf).astype(BF)
        act_ref[:, cols] = act
        gp[:, cols] = cdf + pre * (jnp.exp(pre * pre * -0.5) * 0.3989422804014327)
        acc[...] += mm(act, wback[cols, :])
        return 0

    lax.fori_loop(0, units // FB, up, 0, unroll=False)
    total = hidden[...] + acc[...] + b_back
    center = total - row_mean(total)
    scale = lax.rsqrt(row_mean(center * center) + 1e-12)
    unit = center * scale
    result = unit * gain2 + shift2
    out_ref[...] = result.astype(BF)
    grad = cot_ref[...].astype(F32) + keep_ref[...] * (result - teacher_ref[...].astype(F32))
    def put(row, value):
        sums_ref[row : row + 1, 0 : value.shape[1]] = value
    put(5, jnp.sum(grad * unit, axis=0, keepdims=True))
    put(6, jnp.sum(grad, axis=0, keepdims=True))
    grad = grad * gain2
    back = scale * (grad - row_mean(grad) - unit * row_mean(grad * unit))
    acc[...] = back
    low = back.astype(BF)
    dbr_ref[...] = low
    put(2, jnp.sum(low.astype(F32), axis=0, keepdims=True))

    def down(n, _):
        cols = pl.ds(pl.multiple_of(n * FB, FB), FB)
        dpre = (mm(dbr_ref[...], wback[cols, :], NT) * gp[:, cols]).astype(BF)
        dpre_ref[:, cols] = dpre
        sums_ref[1:2, cols] = jnp.sum(dpre.astype(F32), axis=0, keepdims=True)
        acc[...] += mm(dpre, win[:, cols], NT)
        return 0

    lax.fori_loop(0, units // FB, down, 0, unroll=False)
    grad = acc[...]
    unit = xh[...]
    put(3, jnp.sum(grad * unit, axis=0, keepdims=True))
    put(4, jnp.sum(grad, axis=0, keepdims=True))
    grad = grad * gain1
    back = inv[...] * (grad - row_mean(grad) - unit * row_mean(grad * unit))
    dres_ref[...] = back
    low = back.astype(BF)
    dproj_ref[...] = low
    put(0, jnp.sum(low.astype(F32), axis=0, keepdims=True))
    for i in range(groups):
        dparts_ref[i * rows : (i + 1) * rows, :] = mm(low, wo[i * part : (i + 1) * part, :], NT).astype(BF)


def dense(who, o, weights, x, teacher, cot, keep, vec):
    rows, width = x.shape
    units = vec.shape[1]
    sd = jax.ShapeDtypeStruct
    outs = (
        sd((rows, width), BF), sd((rows, width), F32), sd(o.shape, BF), sd((rows, units), BF), sd((rows, width), BF),
        sd((rows, units), BF), sd((rows, width), BF), sd((rows, width), BF), sd((8, units), F32),
    )
    ins = (o, *weights, x, teacher, cot, keep, vec)
    stay = pl.BlockSpec(memory_space=pl.ANY)
    return pl.pallas_call(
        functools.partial(dense_kernel, FB=FFB),
        out_shape=outs,
        grid_spec=pltpu.PrefetchScalarGridSpec(
            num_scalar_prefetch=1,
            grid=(1,),
            in_specs=[whole(o.shape)] + [stay] * 6 + [whole(a.shape) for a in ins[7:]],
            out_specs=tuple(whole(a.shape) for a in outs),
            scratch_shapes=[
                pltpu.VMEM((width, width), BF), pltpu.VMEM((width, units), BF), pltpu.VMEM((units, width), BF),
                pltpu.VMEM((rows, width), F32), pltpu.VMEM((rows, 1), F32), pltpu.VMEM((rows, width), F32),
                pltpu.VMEM((rows, units), F32), pltpu.VMEM((rows, width), F32), pltpu.SemaphoreType.DMA((8,)),
            ],
        ),
        compiler_params=pltpu.CompilerParams(vmem_limit_bytes=GRANT),
        cost_estimate=cost(12_000_000_000, 30_000_000, 4_000_000),
        name="dense",
    )(who, *ins)


def finish_kernel(
    who, dq0, dq1, dq2, dq3, own_ref, pair_ref, left_ref, right_ref, turn_ref, w_ref,
    all_ref, sums_ref, dx_ref, gx_ref, gy_ref, next_left, next_right, held,
):
    d = pl.program_id(0)
    rows, width = dx_ref.shape
    cut = width // 2

    @pl.when(d == 0)
    def _():
        sums_ref[...] = jnp.zeros_like(sums_ref)
        held[2 * BLK :, :] = jnp.zeros((held.shape[0] - 2 * BLK, held.shape[1]), BF)
        for base, extra in ((0, left_ref), (BLK, right_ref)):

            def gather(r, base=base, extra=extra):
                at = pl.ds(pl.multiple_of(base + r, 128), 128)
                value = own_ref[at, :].astype(F32) + pair_ref[at, :].astype(F32)
                held[at, :] = (value + extra[pl.ds(r, 128), :].astype(F32)).astype(BF)

            sweep(BLK, 128, gather)

    tok = mm(turn_ref[0], held[pl.ds(pl.multiple_of(who[3 + d], 16), SPAN), :]).astype(BF)
    dq = sum(ref[...].astype(F32) for ref in (dq0, dq1, dq2, dq3)).astype(BF)
    all_ref[:, 0:256] = dq
    all_ref[:, 256:640] = tok
    sums_ref[0:1, 0:256] += jnp.sum(dq.astype(F32), axis=0, keepdims=True)
    sums_ref[0:1, 256:640] += jnp.sum(tok.astype(F32), axis=0, keepdims=True)
    part = mm(all_ref[...], w_ref[...], NT).astype(BF)

    @pl.when(d == 0)
    def _():
        dx_ref[...] = part

    @pl.when(d == 1)
    def _():
        gx_ref[0:rows, :] = part[:, :cut]
        next_right[...] = part[:, cut:]

    @pl.when(d == 2)
    def _():
        next_left[...] = part[:, :cut]
        gy_ref[0:rows, :] = part[:, cut:]

    @pl.when(d == 3)
    def _():
        gx_ref[rows:, :] = part[:, :cut]
        gy_ref[rows:, :] = part[:, cut:]


def finish(who, dqs, own, pair, left, right, turn, w_heads):
    sd = jax.ShapeDtypeStruct
    rows, width = turn.shape[1], w_heads.shape[0]
    cols = dqs[0].shape[1] + own.shape[1]
    ins = (*dqs, own, pair, left, right, turn, w_heads)
    shapes = ((rows, width), (2 * rows, width // 2), (2 * rows, width // 2), (rows, width // 2), (rows, width // 2))
    outs = (sd((4 * rows, cols), BF), sd((8, cols), F32)) + tuple(sd(s, BF) for s in shapes)

    def by_block(shape):
        return pl.BlockSpec((rows, shape[1]), lambda d, *_: (d, 0))

    return pl.pallas_call(
        finish_kernel,
        out_shape=outs,
        grid_spec=pltpu.PrefetchScalarGridSpec(
            num_scalar_prefetch=1,
            grid=(4,),
            in_specs=[by_block(a.shape) for a in ins[:4]]
            + [whole(a.shape) for a in ins[4:8]]
            + [pl.BlockSpec((1, *turn.shape[1:]), lambda d, *_: (d, 0, 0)), whole(w_heads.shape)],
            out_specs=(by_block(outs[0].shape), whole(outs[1].shape)) + tuple(whole(s) for s in shapes),
            scratch_shapes=[pltpu.VMEM((2 * BLK + 128, own.shape[1]), BF)],
        ),
        compiler_params=pltpu.CompilerParams(vmem_limit_bytes=GRANT),
        cost_estimate=cost(3_000_000_000, 16_000_000),
        name="finish",
    )(who, *ins)


def part_out(who, held, am, ao, bm, bo, sides):
    part = am.shape[0]
    for mine, other, side, base in ((am, ao, sides[0], 0), (bm, bo, sides[1], 2 * part)):

        def move(r, mine=mine, other=other, side=side, base=base):
            mine[pl.ds(r, 16), :] = held[pl.ds(pl.multiple_of(base + side * part + r, 16), 16), :]
            other[pl.ds(r, 16), :] = held[pl.ds(pl.multiple_of(base + (1 - side) * part + r, 16), 16), :]

        sweep(part, 16, move)


def plus(left, right, at):
    return (left[at, :].astype(F32) + right[at, :].astype(F32)).astype(BF)


def first_kernel(who, back_a, back_b, in_a, in_b, out_a, out_b, am, ao, bm, bo, held):
    width = back_a.shape[1]
    tall = in_a.shape[0]

    def upper(r):
        at = pl.ds(r, 16)
        for k in range(4):
            held[at, k * width : (k + 1) * width] = plus(back_a, back_b, pl.ds(pl.multiple_of(k * tall + r, 16), 16))
        held[pl.ds(pl.multiple_of(tall + r, 16), 16), :] = plus(in_a, in_b, at)

    def lower(r):
        held[pl.ds(pl.multiple_of(2 * tall + r, 16), 16), :] = plus(out_a, out_b, pl.ds(r, 16))

    sweep(tall, 16, upper)
    sweep(out_a.shape[0], 16, lower)
    part_out(who, held, am, ao, bm, bo, (lax.rem(who[1], 2), who[1] // 2))


def both_kernel(who, a_mine, a_got, b_mine, b_got, both):
    del who
    part = a_mine.shape[0]

    def work(r):
        both[pl.ds(r, 16), :] = plus(a_mine, a_got, pl.ds(r, 16))
        both[pl.ds(pl.multiple_of(part + r, 16), 16), :] = plus(b_mine, b_got, pl.ds(r, 16))

    sweep(part, 16, work)


def second_kernel(who, a_mine, a_got, b_mine, b_got, am, ao, bm, bo, held):
    both_kernel(who, a_mine, a_got, b_mine, b_got, held)
    part_out(who, held, am, ao, bm, bo, (who[1] // 2, lax.rem(who[1], 2)))


def join_kernel(who, a, b, c, d, back_ref, in_ref, out_ref, vec_ref, held):
    step = pl.program_id(0)

    @pl.when(step == 0)
    def _():
        gather_pieces(who, (a, b, c, d), held)

    tall = held.shape[0] - 128
    tall, width = tall // 2, back_ref.shape[1]
    cols = pl.ds(pl.multiple_of(step * width, 128), width)
    back_ref[...] = held[0:tall, cols].astype(F32)
    rows = in_ref.shape[0]
    in_ref[...] = held[pl.ds(pl.multiple_of(tall + step * rows, 16), rows), :].astype(F32)

    @pl.when(step < 3)
    def _():
        out_ref[...] = held[2 * tall :, cols].astype(F32)

    @pl.when(step == 3)
    def _():
        vec_ref[...] = held[2 * tall : 2 * tall + 16, 3 * width :].astype(F32)


def gather_pieces(who, pieces, held):
    s1, s2 = lax.rem(who[1], 2), who[1] // 2
    part = pieces[0].shape[0] // 2
    for at, ref in enumerate(pieces):
        color, i = at // 2, at % 2
        for j in range(2):
            spot = (s1 ^ i) * 2 + (s2 ^ j) if color == 0 else 4 + (s2 ^ i) * 2 + (s1 ^ j)

            def move(r, spot=spot, ref=ref, j=j):
                frm = pl.ds(pl.multiple_of(j * part + r, 16), 16)
                held[pl.ds(pl.multiple_of(spot * part + r, 16), 16), :] = ref[frm, :]

            sweep(part, 16, move)

def join(who, pieces, back, first, out, total):
    sd = jax.ShapeDtypeStruct
    tall, width = first[0], back[1]
    outs = (sd(back, F32), sd(first, F32), sd(out, F32), sd((16, width), F32))
    return pl.pallas_call(
        join_kernel,
        out_shape=outs,
        grid_spec=pltpu.PrefetchScalarGridSpec(
            num_scalar_prefetch=1,
            grid=(4,),
            in_specs=[whole(a.shape) for a in pieces],
            out_specs=(
                pl.BlockSpec((tall, width), lambda k, *_: (k, 0)),
                pl.BlockSpec((tall // 4, first[1]), lambda k, *_: (k, 0)),
                pl.BlockSpec((128, width), lambda k, *_: (jnp.minimum(k, 2), 0)),
                whole((16, width)),
            ),
            scratch_shapes=[pltpu.VMEM((total, first[1]), BF)],
        ),
        compiler_params=pltpu.CompilerParams(vmem_limit_bytes=GRANT),
        cost_estimate=cost(1_000_000, 16_000_000),
        name="join",
    )(who, *pieces)


def small_call(kernel, who, pieces, outs, scratch, name, grant=24 << 20):
    return pl.pallas_call(
        kernel,
        out_shape=tuple(jax.ShapeDtypeStruct(*s) for s in outs),
        grid_spec=pltpu.PrefetchScalarGridSpec(
            num_scalar_prefetch=1,
            grid=(1,),
            in_specs=[whole(a.shape) for a in pieces],
            out_specs=tuple(whole(s[0]) for s in outs),
            scratch_shapes=scratch,
        ),
        compiler_params=pltpu.CompilerParams(vmem_limit_bytes=grant),
        cost_estimate=cost(1_000_000, 9_000_000),
        name=name,
    )(who, *pieces)


def heads_kernel(who, in_ref, q_ref, k_ref, v_ref, bias_ref):
    tall = in_ref.shape[1]
    for c in range(in_ref.shape[0] // 4):
        at = slice(c * tall, (c + 1) * tall)
        for a in range(4):
            cols = slice(a * 192, (a + 1) * 192)
            block = in_ref[c * 4 + (who[1] ^ a)].astype(F32)
            q_ref[at, cols] = block[:, 64:256]
            v_ref[at, cols] = block[:, 256:448]
            k_ref[at, cols] = block[:, 448:640]
            if c == 0:
                for k in range(3):
                    spot = slice(a * 192 + k * 64, a * 192 + (k + 1) * 64)
                    bias_ref[0:1, spot] = block[k : k + 1, 0:64]
                    bias_ref[8:9, spot] = block[k + 3 : k + 4, 0:64]


def heads_out(who, gathered):
    outs = (((384, 768), F32),) * 3 + (((16, 768), F32),)
    return small_call(heads_kernel, who, (gathered,), outs, [], "heads_out")


def swap(block, axis="fsdp"):
    return lax.ppermute(block, axis, [(0, 1), (1, 0)])


def shifted(block, axis, distance):
    devices = range(lax.axis_size(axis))
    route = [(i - distance, i) for i in devices if i - distance in devices]
    return lax.ppermute(block, axis, route)


def flip(block, bit, axis="uly"):
    return lax.ppermute(block, axis, [(i, i ^ bit) for i in range(lax.axis_size(axis))])


def exchange(rows, axis):
    return lax.all_to_all(rows, axis, split_axis=0, concat_axis=0, tiled=True)


def spread_rows(rows, axis):
    count = lax.axis_size(axis)
    return exchange(jnp.broadcast_to(rows[None], (count, *rows.shape)).reshape(-1, rows.shape[1]), axis)


def sum_parts(rows, count):
    got = rows.reshape(count, -1, rows.shape[1])
    return sum(got[i].astype(F32) for i in range(count)).astype(BF)


def sum_scatter(rows, axis):
    return sum_parts(exchange(rows, axis), lax.axis_size(axis))


def add(left, right):
    return (left.astype(F32) + right.astype(F32)).astype(BF)


def line_step(held, bit):
    return flip(held, bit, "ctx")


def line_join(held, got, bit):
    low = (lax.axis_index("ctx") & bit) == 0
    return jnp.stack([jnp.where(low, held, got), jnp.where(low, got, held)], axis=1).reshape(-1, *held.shape[1:])


def line_rest(held, bit):
    while bit > 0:
        held = line_join(held, line_step(held, bit), bit)
        bit //= 2
    return held.reshape(-1, held.shape[2])


def chunks_of(rows, axis):
    count, me = lax.axis_size(axis), lax.axis_index(axis)
    split = rows.reshape(count, -1, rows.shape[1])
    picked = [lax.dynamic_index_in_dim(split, me ^ k, 0, keepdims=False) for k in range(count)]
    return [picked[0]] + [flip(picked[k], k, axis) for k in range(1, count)]


def tie(*values):
    return lax.optimization_barrier(values)


def on_device(
    tokens, teacher, cotangent, valid, teacher_ok, doc_starts, w_query, w_key, w_value, w_out, w_in, w_back,
    bias_query, bias_value, bias_out, bias_in, bias_back, norm1_gain, norm1_bias, norm2_gain, norm2_bias,
):
    groups = lax.axis_size("uly")
    spans = lax.axis_size("ctx")
    rows, width = tokens.shape
    block = rows * groups * 2
    stream = block * spans
    ctx_index = lax.axis_index("ctx")
    uly = lax.axis_index("uly")
    half = lax.axis_index("fsdp")
    head_cols = width // groups
    shard = w_query.shape[0]

    small = (bias_query, bias_value, bias_out, bias_in, bias_back, norm1_gain, norm1_bias, norm2_gain, norm2_bias)
    valid_one = valid[None, :]
    valid_own = jnp.concatenate([valid_one, flip(valid_one, 1), flip(valid_one, 2), flip(valid_one, 3)], axis=0)
    x_own, valid_own, doc_starts, ctx_index, uly, half, *small = tie(
        tokens, valid_own, doc_starts, ctx_index, uly, half, *small
    )
    x_x, x_y = flip(x_own, 1), flip(x_own, 2)
    valid_pair = swap(valid_own)
    upper = uly // 2
    place = jnp.arange(groups, dtype=jnp.int32)
    in_plane = place ^ uly
    valid_mine = jnp.take(valid_own, in_plane, axis=0).reshape(2, BLK)
    valid_next = jnp.take(valid_pair, in_plane, axis=0).reshape(2, BLK)
    from_low = shifted(jnp.stack([valid_mine[1], valid_next[1]]), "ctx", 1)
    from_high = shifted(jnp.stack([valid_mine[0], valid_next[0]]), "ctx", -1)
    block_valid = jnp.concatenate(
        [valid_mine, valid_next, from_low[:1], from_high[:1], from_low[1:], from_high[1:]], axis=0
    )
    count = jnp.full((8, 128), jnp.sum(valid_mine) + jnp.sum(valid_next), jnp.int32)
    bit = 1
    while bit < spans:
        count = count + flip(count, bit, "ctx")
        bit *= 2
    count = count[0, 0].astype(F32)

    start_col = uly * head_cols
    cut = [lax.dynamic_slice_in_dim(w, start_col, head_cols, 1) for w in (w_query, w_value, w_key)]
    w_mine = jnp.concatenate([jnp.zeros((shard, 256 - head_cols), BF), *cut], axis=1)
    w_other = swap(w_mine)
    packed = jnp.concatenate(small)
    packed_pair = swap(packed)
    first, second = jnp.where(half == 0, packed, packed_pair), jnp.where(half == 0, packed_pair, packed)
    vectors = []
    at = 0
    for p in small:
        n = p.shape[0]
        vectors.append(jnp.concatenate([first[at : at + n], second[at : at + n]]).astype(F32))
        at += n
    bq_all, bv_all = vectors[:2]
    vec = jnp.stack([jnp.pad(v, (0, w_in.shape[1] - v.shape[0])) for v in vectors[2:]] + [jnp.zeros((w_in.shape[1],), F32)])
    bias_heads = jnp.concatenate(
        [
            jnp.zeros((256 - head_cols,), F32),
            lax.dynamic_slice_in_dim(bq_all, start_col, head_cols, 0),
            lax.dynamic_slice_in_dim(bv_all, start_col, head_cols, 0),
            jnp.zeros((head_cols,), F32),
        ]
    )

    step = jnp.asarray([0, 0, 0, 0, -1, 1, -1, 1], jnp.int32)
    side = jnp.asarray([0, 1, 0, 1, 1, 0, 1, 0], jnp.int32)
    swapped = jnp.asarray([0, 0, 1, 1, 0, 0, 1, 1], jnp.int32)
    inner = jnp.arange(BLK, dtype=jnp.int32)
    first_block = (ctx_index + step) * (2 * groups) + side * groups + (half ^ swapped)
    spot = (first_block[:, None] + 2 * (inner // rows)[None, :]) * rows + lax.rem(inner, rows)[None, :]
    x_x, x_y, block_valid = tie(x_x, x_y, block_valid)
    edges = jnp.concatenate([doc_starts, jnp.full((DOCS + 1,), stream, jnp.int32)])
    window_first = jnp.maximum(ctx_index * block - block // 2, 0)
    first_doc = jnp.sum((doc_starts <= window_first).astype(jnp.int32)) - 1
    near = lax.dynamic_slice_in_dim(edges, first_doc, DOCS + 1, 0)
    tiles = groups * rows // TQ
    per = rows // TQ
    tile_ids = jnp.arange(tiles, dtype=jnp.int32)
    qfirst = ctx_index * block + (((tile_ids // per) ^ uly) * 2 + half) * rows + lax.rem(tile_ids, per) * TQ
    q_lo = jnp.max(jnp.where(near[None, :] <= qfirst[:, None], near[None, :], 0), axis=1)
    q_hi = jnp.min(jnp.where(near[None, :] <= qfirst[:, None] + TQ - 1, stream, near[None, :]), axis=1)
    limits = jnp.concatenate([near, q_lo, q_hi])
    counted = jnp.sum(block_valid[:, None, :] * (spot[:, None, :] < limits[None, :, None]), axis=-1)
    bounds = counted[:, : DOCS + 1]
    cnt_lo = counted[:, DOCS + 1 : DOCS + 1 + tiles].T
    cnt_hi = counted[:, DOCS + 1 + tiles :].T
    pad64 = jnp.zeros((bounds.shape[0], 128 - DOCS), jnp.int32)
    lo_tab = jnp.concatenate([bounds[:, :DOCS], pad64], axis=1)
    hi_tab = jnp.concatenate([bounds[:, 1:], pad64], axis=1)
    slo_tab = jnp.concatenate([near[:DOCS], pad64[0]])[None, :]
    shi_tab = jnp.concatenate([near[1:], pad64[0]])[None, :]
    some = cnt_hi > cnt_lo
    tlo = jnp.where(some, cnt_lo // TK, 0)
    thi = jnp.where(some, (cnt_hi + TK - 1) // TK, 0)
    tables = (tlo, thi, qfirst, lo_tab, hi_tab, slo_tab, shi_tab)
    before = mm(valid_own.astype(BF), (jnp.arange(rows)[:, None] < jnp.arange(rows)[None, :]).astype(BF)).astype(jnp.int32)
    filled = jnp.sum(valid_own, axis=1)
    shift = jnp.where(lax.rem(in_plane, 2) == 1, jnp.take(filled, place ^ 1), 0)
    base = (in_plane // 2) * BLK + (shift // 16) * 16
    goes_to = jnp.where(valid_own > 0, before + lax.rem(shift, 16)[:, None], 2 * BLK)
    ranks = jnp.arange(SPAN, dtype=jnp.int32)
    chosen = (goes_to[:, None, :] == ranks[None, :, None]).astype(BF)
    turned = (goes_to[:, :, None] == ranks[None, None, :]).astype(BF)
    who = jnp.concatenate([jnp.stack([half, uly, upper]).astype(jnp.int32), base])
    loss_scale = jnp.float32(stream) / count
    keep = (loss_scale * (valid * teacher_ok).astype(F32))[:, None]

    x_x, x_y, w_other = tie(x_x, x_y, w_other)
    x_top, x_bottom = flip(x_y[: rows // 2], 1), flip(x_x[rows // 2 :], 2)
    x_top, x_bottom, chosen, bias_heads, *tables = tie(x_top, x_bottom, chosen, bias_heads, *tables)

    q_low, kv_own, kv_up, kv_down, w_heads = project(
        who, (tokens, x_x, x_y, x_top, x_bottom), w_mine, w_other, bias_heads[None, :], chosen
    )
    kv_from_left, kv_from_right = shifted(kv_up, "ctx", 1), shifted(kv_down, "ctx", -1)
    w_out, w_in, w_back, kv_own = tie(w_out, w_in, w_back, kv_own)
    wo_pair, win_pair, wback_pair = swap(w_out), swap(w_in), swap(w_back)
    kv_pair = swap(kv_own)
    state = attend(tables, q_low, (kv_own,), 0)
    kv_halo = jnp.concatenate([kv_from_left, kv_from_right], axis=0)
    kv_halo, kv_pair, *state = tie(kv_halo, kv_pair, *state)
    kv_halo_pair = swap(kv_halo)
    state = attend(tables, q_low, (kv_pair,), 2, state)
    o_heads, o_turned, lse = attend(tables, q_low, (kv_halo, kv_halo_pair), 4, state, last=True)
    o_rel = o_heads.reshape(groups, rows, head_cols)
    o_rest = [flip(o_rel[d], d) for d in range(1, groups)]
    o_heads, x_x, x_y, x_top, x_bottom = tie(o_heads, x_x, x_y, x_top, x_bottom)
    x_all = jnp.concatenate([x_own, x_x, x_y, x_top, x_bottom], axis=0)

    x_all, *o_rest = tie(x_all, *o_rest)
    o_all = jnp.concatenate([o_rel[0], *o_rest], axis=0)

    out, d_resid1, d_parts, act, d_branch, d_pre, hidden_low, d_proj, sums = dense(
        who, o_all, (w_out, wo_pair, w_in, win_pair, w_back, wback_pair), tokens, teacher, cotangent, keep, vec
    )
    d_rel = d_parts.reshape(groups, rows, head_cols)
    tall = w_back.shape[0]
    vector_rows = jnp.concatenate(
        [sums[i, :width].reshape(2, -1) for i in (0, 2, 3, 4, 5, 6)] + [sums[1].reshape(2, -1)], axis=1
    ).reshape(2, -1, width)
    vector_rows = jnp.pad(vector_rows, ((0, 0), (0, 128 - vector_rows.shape[1]), (0, 0))).astype(BF)
    o_rows = o_all.reshape(groups, rows, head_cols)

    def back_part(side):
        return mm(lax.dynamic_slice_in_dim(act, side * tall, tall, 1), d_branch, TN).astype(BF)

    def in_part(side):
        return mm(lax.dynamic_slice_in_dim(hidden_low, side * shard, shard, 1), d_pre, TN).astype(BF)

    def out_part(side):
        both = [
            mm(lax.dynamic_index_in_dim(o_rows, (2 * side + e) ^ uly, 0, keepdims=False), d_proj, TN).astype(BF)
            for e in range(2)
        ]
        stack = jnp.concatenate([*both, lax.dynamic_index_in_dim(vector_rows, side, 0, keepdims=False)], axis=0)
        return jnp.concatenate([stack[i * 128 : (i + 1) * 128] for i in range(4)], axis=1)

    d_rest = [flip(d_rel[d], d) for d in range(1, groups)]
    back_got, in_got, out_got, *d_rest = tie(back_part(1 - half), in_part(1 - half), out_part(1 - half), *d_rest)
    back_got, in_got, out_got = swap(back_got), swap(in_got), swap(out_got)
    back_mine, in_mine, out_mine = back_part(half), in_part(half), out_part(half)
    back_got, in_got, out_got, back_mine, in_mine, out_mine = tie(
        back_got, in_got, out_got, back_mine, in_mine, out_mine
    )
    wide = w_in.shape[1]
    total = 2 * shard + 128
    am, ao, bm, bo = small_call(
        first_kernel, who, (back_mine, back_got, in_mine, in_got, out_mine, out_got),
        (((total // 4, wide), BF),) * 4, [pltpu.VMEM((total, wide), BF)], "first_stage",
    )
    d_heads = jnp.concatenate([d_rel[0], *d_rest], axis=0)
    d_heads, am, ao, bm, bo = tie(d_heads, am, ao, bm, bo)

    ag, bg = flip(ao, 1), flip(bo, 2)
    args = (tables, q_low, d_heads, o_turned, lse)
    dq0, got_lo, got_hi, delta = attend_back(
        *args, kv_halo_pair, 6, first=True, cuts=2, name="back_halo_pair"
    )
    got_lo, got_hi, delta = tie(got_lo, got_hi, delta)
    args = (tables, q_low, d_heads, delta, lse)
    got_lo, got_hi = swap(got_lo), swap(got_hi)
    dq1, halo_lo, halo_hi = attend_back(*args, kv_halo, 4, cuts=2, name="back_halo", size=1_000_000)
    halo_lo, halo_hi, got_lo, got_hi, ag, bg = tie(halo_lo, halo_hi, got_lo, got_hi, ag, bg)

    halo_lo, halo_hi = add(halo_lo, got_lo), add(halo_hi, got_hi)
    am, ao, bm, bo = small_call(
        second_kernel, who, (am, ag, bm, bg), (((total // 8, wide), BF),) * 4,
        [pltpu.VMEM((total // 2, wide), BF)], "second_stage", 12 << 20,
    )
    halo_lo, halo_hi, delta, am, ao, bm, bo = tie(halo_lo, halo_hi, delta, am, ao, bm, bo)
    args = (tables, q_low, d_heads, delta, lse)
    ag, bg = flip(ao, 2), flip(bo, 1)
    from_left, from_right = shifted(halo_hi, "ctx", 1), shifted(halo_lo, "ctx", -1)
    dq2, dkv_pair = attend_back(*args, kv_pair, 2, name="back_pair")
    dkv_pair, ag, bg, from_left, from_right = tie(dkv_pair, ag, bg, from_left, from_right)

    (line,) = small_call(both_kernel, who, (am, ag, bm, bg), (((total // 4, wide), BF),), [], "third_stage", 12 << 20)
    line, dkv_pair, delta = tie(line, dkv_pair, delta)
    args = (tables, q_low, d_heads, delta, lse)
    line = exchange(line, "ctx")
    pair_got = swap(dkv_pair)
    dq3, dkv_own = attend_back(*args, kv_own, 0, name="back_own")
    dkv_own, line, pair_got = tie(dkv_own, line, pair_got)
    line = sum_parts(line, spans)
    line, dkv_own = tie(line, dkv_own)
    line = spread_rows(line, "ctx")

    d_all, d_sums, dx_own, give_x, give_y, left_next, right_next = finish(
        who, (dq0, dq1, dq2, dq3), dkv_own, pair_got, from_left, from_right, turned, w_heads
    )
    d_all, give_x, give_y = tie(d_all, give_x, give_y)
    give_x, give_y = flip(give_x, 1), flip(give_y, 2)
    corner = d_sums[0, 64:].reshape(9, 64)

    def heads_part(side):
        grad = mm(lax.dynamic_slice_in_dim(x_all, side * shard, shard, 1), d_all, TN)
        return lax.dynamic_update_slice(grad, corner, (0, 0)).astype(BF)

    heads_other = heads_part(1 - half)
    heads_got = swap(heads_other)
    heads_mine = heads_part(half)
    heads_sum = add(heads_mine, heads_got)
    line, give_x, give_y, *heads_parts = tie(line, give_x, give_y, *chunks_of(heads_sum, "ctx"))
    heads_sum = sum(part.astype(F32) for part in heads_parts).astype(BF)
    a_near, b_near = line[: total // 8], line[total // 8 :]
    a_got, b_got, *heads_rest = tie(
        flip(a_near, 2), flip(b_near, 1), *[flip(heads_sum, d) for d in range(1, groups)]
    )
    a_near = jnp.concatenate([a_near, a_got], axis=0)
    b_near = jnp.concatenate([b_near, b_got], axis=0)
    a_far, b_far = flip(a_near, 1), flip(b_near, 2)
    left_next = flip(add(left_next, give_x[rows:]), 2)
    right_next = flip(add(right_next, give_y[rows:]), 1)
    heads_sum = jnp.concatenate([heads_sum, *heads_rest], axis=0)
    heads_all = spread_rows(heads_sum, "ctx").reshape(spans * groups, -1, heads_sum.shape[1])
    grad_in = d_resid1 + dx_own.astype(F32)
    grad_in = grad_in + jnp.concatenate([give_x[:rows].astype(F32), give_y[:rows].astype(F32)], axis=1)
    grad_in = grad_in + jnp.concatenate([left_next.astype(F32), right_next.astype(F32)], axis=1)
    g_back, g_in, g_out, g_vec = join(
        who, (a_near, a_far, b_near, b_far), w_back.shape, w_in.shape, w_out.shape, total
    )
    g_query, g_key, g_value, g_bias = heads_out(who, heads_all)
    g_bias_q = lax.dynamic_slice_in_dim(g_bias[0], half * shard, shard, 0)
    g_bias_v = lax.dynamic_slice_in_dim(g_bias[8], half * shard, shard, 0)
    flat = g_vec.reshape(-1)
    g_bo, g_bb, g_g1, g_s1, g_g2, g_s2 = [flat[i * shard : (i + 1) * shard] for i in range(6)]
    g_bin = flat[6 * shard : 6 * shard + bias_in.shape[0]]
    return (
        out, grad_in, g_query, g_key, g_value, g_out, g_in, g_back,
        g_bias_q, g_bias_v, g_bo, g_bin, g_bb, g_g1, g_s1, g_g2, g_s2,
    )


def solution(mesh):
    placed = (
        P(("ctx", "uly", "fsdp"), None),
        P(("ctx", "uly", "fsdp"), None),
        P(("ctx", "uly", "fsdp"), None),
        P(("ctx", "uly", "fsdp")),
        P(("ctx", "uly", "fsdp")),
        P(),
        P("fsdp", None),
        P("fsdp", None),
        P("fsdp", None),
        P("fsdp", None),
        P("fsdp", None),
        P("fsdp", None),
        P("fsdp"),
        P("fsdp"),
        P("fsdp"),
        P("fsdp"),
        P("fsdp"),
        P("fsdp"),
        P("fsdp"),
        P("fsdp"),
        P("fsdp"),
    )
    return jax.shard_map(
        on_device,
        mesh=mesh,
        in_specs=placed,
        out_specs=(
            P(("ctx", "uly", "fsdp"), None),
            P(("ctx", "uly", "fsdp"), None),
            P("fsdp", None),
            P("fsdp", None),
            P("fsdp", None),
            P("fsdp", None),
            P("fsdp", None),
            P("fsdp", None),
            P("fsdp"),
            P("fsdp"),
            P("fsdp"),
            P("fsdp"),
            P("fsdp"),
            P("fsdp"),
            P("fsdp"),
            P("fsdp"),
            P("fsdp"),
        ),
        check_vma=False,
    )
```

```python
import functools

import jax
import jax.numpy as jnp
from jax import lax
from jax.experimental import pallas as pl
from jax.experimental.pallas import tpu as pltpu
from jax.sharding import PartitionSpec as P

HEADS = 12
HD = 64
BLK = 1024
SPAN = 640
TQ = 512
TK = 256
DOCS = 64
FFB = 1536
GRANT = 63 << 20
MASKED = -1e30
BF = jnp.bfloat16
F32 = jnp.float32
NT = (((1,), (1,)), ((), ()))
NN = (((1,), (0,)), ((), ()))
TN = (((0,), (0,)), ((), ()))


def mm(left, right, dims=NN):
    return lax.dot_general(left, right, dims, preferred_element_type=F32)


def whole(shape):
    return pl.BlockSpec(shape, lambda *_: (0,) * len(shape), pipeline_mode=pl.Buffered(1))


def sweep(total, step, work):
    def one(i, _):
        work(pl.multiple_of(i * step, step))
        return 0

    lax.fori_loop(0, total // step, one, 0)


def cost(flops, moved, special=0):
    return pl.CostEstimate(flops=flops, bytes_accessed=moved, transcendentals=special)


def lane_ids(rows):
    return lax.broadcasted_iota(jnp.int32, (rows, 128), 1)


def build_keys(sources, slot0, lo_ref, hi_ref, kaug, transposed, low_half):
    per = BLK // TK
    for at, kv in enumerate(sources):

        def one(j, _, at=at, kv=kv):
            rows = pl.ds(pl.multiple_of(j * TK, TK), TK)
            tile = at * (kv.shape[0] // TK) + j
            slot = slot0 + at * (kv.shape[0] // BLK) + j // per
            out = pl.ds(pl.multiple_of(tile * TK, TK), TK)
            rank = lax.broadcasted_iota(jnp.int32, (TK, 128), 0) + lax.rem(j, per) * TK
            inside = (rank >= lo_ref[pl.ds(slot, 1), :]) & (rank < hi_ref[pl.ds(slot, 1), :])
            bias = jnp.where(inside, 0.0, MASKED).astype(BF)
            kaug[out, 0:128] = jnp.where(lane_ids(TK) < 64, bias, kv[rows, 128:256])
            kaug[out, 128:256] = kv[rows, 256:384]
            if low_half:
                transposed[tile] = kv[rows, 0:256].T[0:192]
            else:
                transposed[tile] = kaug[out, :].T[64:256]
            return 0

        lax.fori_loop(0, kv.shape[0] // TK, one, 0)


def stack_queries(q, first, slo_ref, shi_ref, qs):
    lane = lane_ids(TQ)
    spot = lax.broadcasted_iota(jnp.int32, (TQ, 128), 0) + first
    mine = ((spot >= slo_ref[...]) & (spot < shi_ref[...])).astype(F32).astype(BF)
    zero = jnp.zeros((TQ, 128), BF)
    low, high = q[:, 0:128], q[:, 128:256]
    mark = jnp.where(lane < 64, mine, zero)
    qs[0:TQ, 0:128] = jnp.where(lane < 64, mine, low)
    qs[TQ : 2 * TQ, 0:128] = mark
    qs[2 * TQ :, 0:128] = mark
    qs[0:TQ, 128:256] = zero
    qs[TQ : 2 * TQ, 128:256] = jnp.where(lane < 64, high, zero)
    qs[2 * TQ :, 128:256] = jnp.where(lane < 64, zero, high)


def attend_kernel(*refs, slot0, count, resume, last):
    tlo, thi, qfirst, q_ref = refs[:4]
    sources = refs[4 : 4 + count]
    lo_ref, hi_ref, slo_ref, shi_ref = refs[4 + count : 8 + count]
    at = 8 + count
    if resume:
        acc_in, stat_in = refs[at : at + 2]
        at += 2
    if last:
        o_ref, ot_ref, lse_ref = refs[at : at + 3]
        at += 3
    else:
        acc_out, stat_out = refs[at : at + 2]
        at += 2
    kaug, vt, qs, acc, m_s, l_s = refs[at:]
    i = pl.program_id(0)

    @pl.when(i == 0)
    def _():
        build_keys(sources, slot0, lo_ref, hi_ref, kaug, vt, True)

    slots = count * sources[0].shape[0] // BLK
    per = BLK // TK
    stack_queries(q_ref[...], qfirst[i], slo_ref, shi_ref, qs)
    if resume:
        m_s[...] = stat_in[0, 0:1, :]
        l_s[...] = stat_in[0, 1:2, :]
        acc[...] = acc_in[0]
    else:
        m_s[...] = jnp.full_like(m_s, 2 * MASKED)
        l_s[...] = jnp.zeros_like(l_s)
        acc[...] = jnp.zeros_like(acc)

    def slot_loop(s, _):
        def key_loop(t, _):
            tile = s * per + t
            keys = pl.ds(pl.multiple_of(tile * TK, TK), TK)
            st = mm(kaug[keys, :], qs[...], NT)
            m_old = m_s[...]
            m_new = jnp.maximum(m_old, jnp.max(st, axis=0, keepdims=True))
            fade = jnp.exp(m_old - m_new)
            p = jnp.exp(st - m_new)
            l_s[...] = l_s[...] * fade + jnp.sum(p, axis=0, keepdims=True)
            m_s[...] = m_new
            low = p.astype(BF)
            for h in range(3):
                cols = slice(h * TQ, (h + 1) * TQ)
                part = slice(h * HD, (h + 1) * HD)
                acc[part, :] = acc[part, :] * fade[:, cols] + mm(vt[tile, part, :], low[:, cols])
            return 0

        return lax.fori_loop(tlo[i, slot0 + s], thi[i, slot0 + s], key_loop, 0)

    lax.fori_loop(0, slots, slot_loop, 0)
    if last:
        total = l_s[...]
        for h in range(3):
            cols = slice(h * TQ, (h + 1) * TQ)
            part = slice(h * HD, (h + 1) * HD)
            acc[part, :] = acc[part, :] / total[:, cols]
        ot_ref[0] = acc[...]
        o_ref[...] = acc[...].T.astype(BF)
        lse_ref[0] = m_s[...] + jnp.log(total)
    else:
        acc_out[0] = acc[...]
        stat_out[0, 0:1, :] = m_s[...]
        stat_out[0, 1:2, :] = l_s[...]


def rows_spec(shape):
    return pl.BlockSpec((TQ, shape[1]), lambda i, *_: (i, 0))


def tile_spec(shape):
    return pl.BlockSpec((1, *shape[1:]), lambda i, *_: (i, 0, 0))


def attend(tables, q, sources, slot0, state=None, last=False):
    tlo, thi, qfirst, lo, hi, slo, shi = tables
    tiles = q.shape[0] // TQ
    keys = sum(s.shape[0] for s in sources)
    state = tuple(state) if state else ()
    sd = jax.ShapeDtypeStruct
    acc, stat = sd((tiles, 3 * HD, TQ), F32), sd((tiles, 2, 3 * TQ), F32)
    if last:
        o, lse = sd((q.shape[0], 3 * HD), BF), sd((tiles, 1, 3 * TQ), F32)
        outs, out_specs = (o, acc, lse), (rows_spec(o.shape), tile_spec(acc.shape), tile_spec(lse.shape))
    else:
        outs, out_specs = (acc, stat), (tile_spec(acc.shape), tile_spec(stat.shape))
    return pl.pallas_call(
        functools.partial(attend_kernel, slot0=slot0, count=len(sources), resume=bool(state), last=last),
        out_shape=outs,
        grid_spec=pltpu.PrefetchScalarGridSpec(
            num_scalar_prefetch=3,
            grid=(tiles,),
            in_specs=[rows_spec(q.shape)]
            + [whole(x.shape) for x in (*sources, lo, hi, slo, shi)]
            + [tile_spec(x.shape) for x in state],
            out_specs=out_specs,
            scratch_shapes=[
                pltpu.VMEM((keys, 256), BF),
                pltpu.VMEM((keys // TK, 3 * HD, TK), BF),
                pltpu.VMEM((3 * TQ, 256), BF),
                pltpu.VMEM((3 * HD, TQ), F32),
                pltpu.VMEM((1, 3 * TQ), F32),
                pltpu.VMEM((1, 3 * TQ), F32),
            ],
        ),
        compiler_params=pltpu.CompilerParams(vmem_limit_bytes=GRANT),
        cost_estimate=cost(12_000_000_000, 12_000_000, 10_000_000),
        name="attend",
    )(tlo, thi, qfirst, q, *sources, lo, hi, slo, shi, *state)


def attend_back_kernel(
    tlo, thi, qfirst, q_ref, do_ref, ot_ref, lse_ref, kv, lo_ref, hi_ref, slo_ref, shi_ref, dq_ref, *rest,
    slot0, first, cuts,
):
    dkv_refs, rest = rest[:cuts], rest[cuts:]
    if first:
        delta_ref, *rest = rest
    kaug, kt, qs, dos, acc, dk_s, dv_s = rest
    keys_all = kv.shape[0]
    slots = keys_all // BLK
    per = BLK // TK
    i = pl.program_id(0)

    @pl.when(i == 0)
    def _():
        build_keys((kv,), slot0, lo_ref, hi_ref, kaug, kt, False)
        dk_s[...] = jnp.zeros_like(dk_s)
        dv_s[...] = jnp.zeros_like(dv_s)

    stack_queries(q_ref[...], qfirst[i], slo_ref, shi_ref, qs)
    do = do_ref[...]
    lane = lane_ids(TQ)
    zero = jnp.zeros((TQ, 128), BF)
    dos[0:TQ, 0:128] = jnp.where(lane < 64, do[:, 0:128], zero)
    dos[TQ : 2 * TQ, 0:128] = jnp.where(lane < 64, zero, do[:, 0:128])
    dos[2 * TQ :, 0:128] = zero
    dos[0 : 2 * TQ, 128:256] = jnp.zeros((2 * TQ, 128), BF)
    dos[2 * TQ :, 128:192] = do[:, 128:192]
    dos[2 * TQ :, 192:256] = jnp.zeros((TQ, 64), BF)
    if first:
        both = do.astype(F32).T * ot_ref[0]
        delta = jnp.concatenate(
            [jnp.sum(both[h * HD : (h + 1) * HD], axis=0, keepdims=True) for h in range(3)], axis=1
        )
        delta_ref[0] = delta
    else:
        delta = ot_ref[0]
    lse = lse_ref[0]
    acc[...] = jnp.zeros_like(acc)

    def slot_loop(s, _):
        def key_loop(t, _):
            tile = s * per + t
            keys = pl.ds(pl.multiple_of(tile * TK, TK), TK)
            st = mm(kaug[keys, :], qs[...], NT)
            p = jnp.exp(st - lse)
            dp = mm(kv[keys, 0:256], dos[...], NT)
            ds = (p * (dp - delta)).astype(BF)
            dv_s[keys, :] += mm(p.astype(BF), dos[...])
            dk_s[keys, :] += mm(ds, qs[...])
            for h in range(3):
                cols = slice(h * TQ, (h + 1) * TQ)
                acc[(h + 1) * HD : (h + 2) * HD, :] += mm(kt[tile, h * HD : (h + 1) * HD, :], ds[:, cols])
            return 0

        return lax.fori_loop(tlo[i, slot0 + s], thi[i, slot0 + s], key_loop, 0)

    lax.fori_loop(0, slots, slot_loop, 0)
    dq_ref[...] = (acc[...] * HD ** (-0.5)).T.astype(BF)

    @pl.when(i == pl.num_programs(0) - 1)
    def _():
        share = keys_all // cuts
        for j, dkv_ref in enumerate(dkv_refs):

            def write(r, j=j, dkv_ref=dkv_ref):
                at = pl.ds(pl.multiple_of(j * share + r, TK), TK)
                to = pl.ds(r, TK)
                dkv_ref[to, 0:128] = dv_s[at, 0:128].astype(BF)
                dkv_ref[to, 128:256] = jnp.where(lane_ids(TK) < 64, dv_s[at, 128:256], dk_s[at, 0:128]).astype(BF)
                dkv_ref[to, 256:384] = dk_s[at, 128:256].astype(BF)

            sweep(share, TK, write)


def attend_back(tables, q, do, ot, lse, source, slot0, first=False, cuts=1, name="attend_back", size=14_000_000_000):
    tlo, thi, qfirst, lo, hi, slo, shi = tables
    tiles = q.shape[0] // TQ
    keys = source.shape[0]
    sd = jax.ShapeDtypeStruct
    piece = (keys // cuts, source.shape[1])
    outs = (sd(q.shape, BF),) + (sd(piece, BF),) * cuts
    out_specs = (rows_spec(q.shape),) + (whole(piece),) * cuts
    if first:
        outs += (sd(lse.shape, F32),)
        out_specs += (tile_spec(lse.shape),)
    return pl.pallas_call(
        functools.partial(attend_back_kernel, slot0=slot0, first=first, cuts=cuts),
        out_shape=outs,
        grid_spec=pltpu.PrefetchScalarGridSpec(
            num_scalar_prefetch=3,
            grid=(tiles,),
            in_specs=[rows_spec(q.shape), rows_spec(do.shape), tile_spec(ot.shape), tile_spec(lse.shape)]
            + [whole(x.shape) for x in (source, lo, hi, slo, shi)],
            out_specs=out_specs,
            scratch_shapes=[
                pltpu.VMEM((keys, 256), BF),
                pltpu.VMEM((keys // TK, 3 * HD, TK), BF),
                pltpu.VMEM((3 * TQ, 256), BF),
                pltpu.VMEM((3 * TQ, 256), BF),
                pltpu.VMEM((256, TQ), F32),
                pltpu.VMEM((keys, 256), F32),
                pltpu.VMEM((keys, 256), F32),
            ],
        ),
        compiler_params=pltpu.CompilerParams(vmem_limit_bytes=GRANT),
        cost_estimate=cost(size, size // 1000, size // 3000),
        name=name,
    )(tlo, thi, qfirst, q, do, ot, lse, source, lo, hi, slo, shi)


def project_kernel(
    who, x0, x1, x2, x3_top, x3_bottom, w_mine, w_other, bias_ref, chosen, q_ref, kv_ref, up_ref, down_ref, w_ref, held
):
    tall = w_mine.shape[0]
    rows = x0.shape[0]
    w_ref[pl.ds(pl.multiple_of(who[0] * tall, tall), tall), :] = w_mine[...]
    w_ref[pl.ds(pl.multiple_of((1 - who[0]) * tall, tall), tall), :] = w_other[...]
    held[...] = jnp.zeros_like(held)
    for d, x in enumerate((x0, x1, x2, (x3_top, x3_bottom))):
        if d < 3:
            value = mm(x[...], w_ref[...]) + bias_ref[...]
        else:
            value = jnp.concatenate([mm(x[0][...], w_ref[...]), mm(x[1][...], w_ref[...])], axis=0) + bias_ref[...]
        at = slice(d * rows, (d + 1) * rows)
        q_ref[at, :] = (value[:, :256].astype(BF).astype(F32) * HD ** (-0.5)).astype(BF)
        to = pl.ds(pl.multiple_of(who[3 + d], 16), SPAN)
        held[to, :] += mm(chosen[d], value[:, 256:].astype(BF))
    kv_ref[...] = held[0 : 2 * BLK, :].astype(BF)
    down_ref[...] = kv_ref[0:BLK, :]
    up_ref[...] = kv_ref[BLK:, :]


def project(who, xs, w_mine, w_other, bias, chosen):
    sd = jax.ShapeDtypeStruct
    rows, width = xs[0].shape
    cols = w_mine.shape[1]
    ins = (*xs, w_mine, w_other, bias, chosen)
    outs = (
        sd((4 * rows, 256), BF), sd((4 * rows, cols - 256), BF), sd((2 * rows, cols - 256), BF),
        sd((2 * rows, cols - 256), BF), sd((width, cols), BF),
    )
    return pl.pallas_call(
        project_kernel,
        out_shape=outs,
        grid_spec=pltpu.PrefetchScalarGridSpec(
            num_scalar_prefetch=1,
            grid=(1,),
            in_specs=[whole(a.shape) for a in ins],
            out_specs=tuple(whole(a.shape) for a in outs),
            scratch_shapes=[pltpu.VMEM((2 * BLK + 128, cols - 256), F32)],
        ),
        compiler_params=pltpu.CompilerParams(vmem_limit_bytes=24 << 20),
        cost_estimate=cost(3_000_000_000, 12_000_000),
        name="project",
    )(who, *ins)


def row_mean(v):
    return jnp.sum(v, axis=-1, keepdims=True) * (1.0 / v.shape[-1])

def dense_kernel(
    who, o_ref, wo_a, wo_b, win_a, win_b, wback_a, wback_b, x_ref, teacher_ref, cot_ref, keep_ref, vec_ref,
    out_ref, dres_ref, dparts_ref, act_ref, dbr_ref, dpre_ref, hid_ref, dproj_ref, sums_ref,
    wo, win, wback, xh, inv, hidden, gp, acc, sems, *, FB
):
    rows, width = x_ref.shape
    groups = o_ref.shape[0] // rows
    part = width // groups
    units = win.shape[1]
    wo_loads, win_loads, wback_loads = [], [], []
    for i in range(2):
        side = who[0] if i == 0 else 1 - who[0]
        for e in range(groups // 2):
            to = pl.multiple_of(((side * (groups // 2) + e) ^ who[1]) * part, part)
            wo_loads.append(
                pltpu.make_async_copy((wo_a, wo_b)[i].at[pl.ds(e * part, part)], wo.at[pl.ds(to, part)], sems.at[2 * i + e])
            )
        for j, (pieces, target, held) in enumerate((((win_a, win_b), win, win_loads), ((wback_a, wback_b), wback, wback_loads))):
            tall = target.shape[0] // 2
            to = pl.multiple_of(side * tall, tall)
            held.append(pltpu.make_async_copy(pieces[i], target.at[pl.ds(to, tall)], sems.at[4 + 2 * i + j]))
    for load in wo_loads + win_loads + wback_loads:
        load.start()
    b_out, b_in, b_back = vec_ref[0:1, 0:width], vec_ref[1:2, :], vec_ref[2:3, 0:width]
    gain1, shift1, gain2, shift2 = (vec_ref[i : i + 1, 0:width] for i in range(3, 7))
    for load in wo_loads:
        load.wait()
    total = x_ref[...].astype(F32) + b_out
    for i in range(groups):
        total += mm(o_ref[i * rows : (i + 1) * rows, :], wo[i * part : (i + 1) * part, :])
    center = total - row_mean(total)
    scale = lax.rsqrt(row_mean(center * center) + 1e-12)
    inv[...] = scale
    unit = center * scale
    xh[...] = unit
    hid = unit * gain1 + shift1
    hidden[...] = hid
    hid_ref[...] = hid.astype(BF)
    acc[...] = jnp.zeros_like(acc)
    for load in win_loads + wback_loads:
        load.wait()

    def up(n, _):
        cols = pl.ds(pl.multiple_of(n * FB, FB), FB)
        pre = mm(hid_ref[...], win[:, cols]) + vec_ref[1:2, cols]
        cdf = 0.5 + 0.5 * lax.erf(pre * 0.7071067811865476)
        act = (pre * cdf).astype(BF)
        act_ref[:, cols] = act
        gp[:, cols] = cdf + pre * (jnp.exp(pre * pre * -0.5) * 0.3989422804014327)
        acc[...] += mm(act, wback[cols, :])
        return 0

    lax.fori_loop(0, units // FB, up, 0, unroll=False)
    total = hidden[...] + acc[...] + b_back
    center = total - row_mean(total)
    scale = lax.rsqrt(row_mean(center * center) + 1e-12)
    unit = center * scale
    result = unit * gain2 + shift2
    out_ref[...] = result.astype(BF)
    grad = cot_ref[...].astype(F32) + keep_ref[...] * (result - teacher_ref[...].astype(F32))
    def put(row, value):
        sums_ref[row : row + 1, 0 : value.shape[1]] = value
    put(5, jnp.sum(grad * unit, axis=0, keepdims=True))
    put(6, jnp.sum(grad, axis=0, keepdims=True))
    grad = grad * gain2
    back = scale * (grad - row_mean(grad) - unit * row_mean(grad * unit))
    acc[...] = back
    low = back.astype(BF)
    dbr_ref[...] = low
    put(2, jnp.sum(low.astype(F32), axis=0, keepdims=True))

    def down(n, _):
        cols = pl.ds(pl.multiple_of(n * FB, FB), FB)
        dpre = (mm(dbr_ref[...], wback[cols, :], NT) * gp[:, cols]).astype(BF)
        dpre_ref[:, cols] = dpre
        sums_ref[1:2, cols] = jnp.sum(dpre.astype(F32), axis=0, keepdims=True)
        acc[...] += mm(dpre, win[:, cols], NT)
        return 0

    lax.fori_loop(0, units // FB, down, 0, unroll=False)
    grad = acc[...]
    unit = xh[...]
    put(3, jnp.sum(grad * unit, axis=0, keepdims=True))
    put(4, jnp.sum(grad, axis=0, keepdims=True))
    grad = grad * gain1
    back = inv[...] * (grad - row_mean(grad) - unit * row_mean(grad * unit))
    dres_ref[...] = back
    low = back.astype(BF)
    dproj_ref[...] = low
    put(0, jnp.sum(low.astype(F32), axis=0, keepdims=True))
    for i in range(groups):
        dparts_ref[i * rows : (i + 1) * rows, :] = mm(low, wo[i * part : (i + 1) * part, :], NT).astype(BF)


def dense(who, o, weights, x, teacher, cot, keep, vec):
    rows, width = x.shape
    units = vec.shape[1]
    sd = jax.ShapeDtypeStruct
    outs = (
        sd((rows, width), BF), sd((rows, width), F32), sd(o.shape, BF), sd((rows, units), BF), sd((rows, width), BF),
        sd((rows, units), BF), sd((rows, width), BF), sd((rows, width), BF), sd((8, units), F32),
    )
    ins = (o, *weights, x, teacher, cot, keep, vec)
    stay = pl.BlockSpec(memory_space=pl.ANY)
    return pl.pallas_call(
        functools.partial(dense_kernel, FB=FFB),
        out_shape=outs,
        grid_spec=pltpu.PrefetchScalarGridSpec(
            num_scalar_prefetch=1,
            grid=(1,),
            in_specs=[whole(o.shape)] + [stay] * 6 + [whole(a.shape) for a in ins[7:]],
            out_specs=tuple(whole(a.shape) for a in outs),
            scratch_shapes=[
                pltpu.VMEM((width, width), BF), pltpu.VMEM((width, units), BF), pltpu.VMEM((units, width), BF),
                pltpu.VMEM((rows, width), F32), pltpu.VMEM((rows, 1), F32), pltpu.VMEM((rows, width), F32),
                pltpu.VMEM((rows, units), F32), pltpu.VMEM((rows, width), F32), pltpu.SemaphoreType.DMA((8,)),
            ],
        ),
        compiler_params=pltpu.CompilerParams(vmem_limit_bytes=GRANT),
        cost_estimate=cost(12_000_000_000, 30_000_000, 4_000_000),
        name="dense",
    )(who, *ins)


def finish_kernel(
    who, dq0, dq1, dq2, dq3, own_ref, pair_ref, left_ref, right_ref, turn_ref, w_ref,
    all_ref, sums_ref, dx_ref, gx_ref, gy_ref, next_left, next_right, held,
):
    d = pl.program_id(0)
    rows, width = dx_ref.shape
    cut = width // 2

    @pl.when(d == 0)
    def _():
        sums_ref[...] = jnp.zeros_like(sums_ref)
        held[2 * BLK :, :] = jnp.zeros((held.shape[0] - 2 * BLK, held.shape[1]), BF)
        for base, extra in ((0, left_ref), (BLK, right_ref)):

            def gather(r, base=base, extra=extra):
                at = pl.ds(pl.multiple_of(base + r, 128), 128)
                value = own_ref[at, :].astype(F32) + pair_ref[at, :].astype(F32)
                held[at, :] = (value + extra[pl.ds(r, 128), :].astype(F32)).astype(BF)

            sweep(BLK, 128, gather)

    tok = mm(turn_ref[0], held[pl.ds(pl.multiple_of(who[3 + d], 16), SPAN), :]).astype(BF)
    dq = sum(ref[...].astype(F32) for ref in (dq0, dq1, dq2, dq3)).astype(BF)
    all_ref[:, 0:256] = dq
    all_ref[:, 256:640] = tok
    sums_ref[0:1, 0:256] += jnp.sum(dq.astype(F32), axis=0, keepdims=True)
    sums_ref[0:1, 256:640] += jnp.sum(tok.astype(F32), axis=0, keepdims=True)
    part = mm(all_ref[...], w_ref[...], NT).astype(BF)

    @pl.when(d == 0)
    def _():
        dx_ref[...] = part

    @pl.when(d == 1)
    def _():
        gx_ref[0:rows, :] = part[:, :cut]
        next_right[...] = part[:, cut:]

    @pl.when(d == 2)
    def _():
        next_left[...] = part[:, :cut]
        gy_ref[0:rows, :] = part[:, cut:]

    @pl.when(d == 3)
    def _():
        gx_ref[rows:, :] = part[:, :cut]
        gy_ref[rows:, :] = part[:, cut:]


def finish(who, dqs, own, pair, left, right, turn, w_heads):
    sd = jax.ShapeDtypeStruct
    rows, width = turn.shape[1], w_heads.shape[0]
    cols = dqs[0].shape[1] + own.shape[1]
    ins = (*dqs, own, pair, left, right, turn, w_heads)
    shapes = ((rows, width), (2 * rows, width // 2), (2 * rows, width // 2), (rows, width // 2), (rows, width // 2))
    outs = (sd((4 * rows, cols), BF), sd((8, cols), F32)) + tuple(sd(s, BF) for s in shapes)

    def by_block(shape):
        return pl.BlockSpec((rows, shape[1]), lambda d, *_: (d, 0))

    return pl.pallas_call(
        finish_kernel,
        out_shape=outs,
        grid_spec=pltpu.PrefetchScalarGridSpec(
            num_scalar_prefetch=1,
            grid=(4,),
            in_specs=[by_block(a.shape) for a in ins[:4]]
            + [whole(a.shape) for a in ins[4:8]]
            + [pl.BlockSpec((1, *turn.shape[1:]), lambda d, *_: (d, 0, 0)), whole(w_heads.shape)],
            out_specs=(by_block(outs[0].shape), whole(outs[1].shape)) + tuple(whole(s) for s in shapes),
            scratch_shapes=[pltpu.VMEM((2 * BLK + 128, own.shape[1]), BF)],
        ),
        compiler_params=pltpu.CompilerParams(vmem_limit_bytes=GRANT),
        cost_estimate=cost(3_000_000_000, 16_000_000),
        name="finish",
    )(who, *ins)


def part_out(who, held, am, ao, bm, bo, sides):
    part = am.shape[0]
    for mine, other, side, base in ((am, ao, sides[0], 0), (bm, bo, sides[1], 2 * part)):

        def move(r, mine=mine, other=other, side=side, base=base):
            mine[pl.ds(r, 16), :] = held[pl.ds(pl.multiple_of(base + side * part + r, 16), 16), :]
            other[pl.ds(r, 16), :] = held[pl.ds(pl.multiple_of(base + (1 - side) * part + r, 16), 16), :]

        sweep(part, 16, move)


def plus(left, right, at):
    return (left[at, :].astype(F32) + right[at, :].astype(F32)).astype(BF)


def first_kernel(who, back_a, back_b, in_a, in_b, out_a, out_b, am, ao, bm, bo, held):
    width = back_a.shape[1]
    tall = in_a.shape[0]

    def upper(r):
        at = pl.ds(r, 16)
        for k in range(4):
            held[at, k * width : (k + 1) * width] = plus(back_a, back_b, pl.ds(pl.multiple_of(k * tall + r, 16), 16))
        held[pl.ds(pl.multiple_of(tall + r, 16), 16), :] = plus(in_a, in_b, at)

    def lower(r):
        held[pl.ds(pl.multiple_of(2 * tall + r, 16), 16), :] = plus(out_a, out_b, pl.ds(r, 16))

    sweep(tall, 16, upper)
    sweep(out_a.shape[0], 16, lower)
    part_out(who, held, am, ao, bm, bo, (lax.rem(who[1], 2), who[1] // 2))


def both_kernel(who, a_mine, a_got, b_mine, b_got, both):
    del who
    part = a_mine.shape[0]

    def work(r):
        both[pl.ds(r, 16), :] = plus(a_mine, a_got, pl.ds(r, 16))
        both[pl.ds(pl.multiple_of(part + r, 16), 16), :] = plus(b_mine, b_got, pl.ds(r, 16))

    sweep(part, 16, work)


def second_kernel(who, a_mine, a_got, b_mine, b_got, am, ao, bm, bo, held):
    both_kernel(who, a_mine, a_got, b_mine, b_got, held)
    part_out(who, held, am, ao, bm, bo, (who[1] // 2, lax.rem(who[1], 2)))


def join_kernel(who, a, b, c, d, back_ref, in_ref, out_ref, vec_ref, held):
    step = pl.program_id(0)

    @pl.when(step == 0)
    def _():
        gather_pieces(who, (a, b, c, d), held)

    tall = held.shape[0] - 128
    tall, width = tall // 2, back_ref.shape[1]
    cols = pl.ds(pl.multiple_of(step * width, 128), width)
    back_ref[...] = held[0:tall, cols].astype(F32)
    rows = in_ref.shape[0]
    in_ref[...] = held[pl.ds(pl.multiple_of(tall + step * rows, 16), rows), :].astype(F32)

    @pl.when(step < 3)
    def _():
        out_ref[...] = held[2 * tall :, cols].astype(F32)

    @pl.when(step == 3)
    def _():
        vec_ref[...] = held[2 * tall : 2 * tall + 16, 3 * width :].astype(F32)


def gather_pieces(who, pieces, held):
    s1, s2 = lax.rem(who[1], 2), who[1] // 2
    part = pieces[0].shape[0] // 2
    for at, ref in enumerate(pieces):
        color, i = at // 2, at % 2
        for j in range(2):
            spot = (s1 ^ i) * 2 + (s2 ^ j) if color == 0 else 4 + (s2 ^ i) * 2 + (s1 ^ j)

            def move(r, spot=spot, ref=ref, j=j):
                frm = pl.ds(pl.multiple_of(j * part + r, 16), 16)
                held[pl.ds(pl.multiple_of(spot * part + r, 16), 16), :] = ref[frm, :]

            sweep(part, 16, move)

def join(who, pieces, back, first, out, total):
    sd = jax.ShapeDtypeStruct
    tall, width = first[0], back[1]
    outs = (sd(back, F32), sd(first, F32), sd(out, F32), sd((16, width), F32))
    return pl.pallas_call(
        join_kernel,
        out_shape=outs,
        grid_spec=pltpu.PrefetchScalarGridSpec(
            num_scalar_prefetch=1,
            grid=(4,),
            in_specs=[whole(a.shape) for a in pieces],
            out_specs=(
                pl.BlockSpec((tall, width), lambda k, *_: (k, 0)),
                pl.BlockSpec((tall // 4, first[1]), lambda k, *_: (k, 0)),
                pl.BlockSpec((128, width), lambda k, *_: (jnp.minimum(k, 2), 0)),
                whole((16, width)),
            ),
            scratch_shapes=[pltpu.VMEM((total, first[1]), BF)],
        ),
        compiler_params=pltpu.CompilerParams(vmem_limit_bytes=GRANT),
        cost_estimate=cost(1_000_000, 16_000_000),
        name="join",
    )(who, *pieces)


def small_call(kernel, who, pieces, outs, scratch, name, grant=24 << 20):
    return pl.pallas_call(
        kernel,
        out_shape=tuple(jax.ShapeDtypeStruct(*s) for s in outs),
        grid_spec=pltpu.PrefetchScalarGridSpec(
            num_scalar_prefetch=1,
            grid=(1,),
            in_specs=[whole(a.shape) for a in pieces],
            out_specs=tuple(whole(s[0]) for s in outs),
            scratch_shapes=scratch,
        ),
        compiler_params=pltpu.CompilerParams(vmem_limit_bytes=grant),
        cost_estimate=cost(1_000_000, 9_000_000),
        name=name,
    )(who, *pieces)


def heads_kernel(who, in_ref, q_ref, k_ref, v_ref, bias_ref):
    tall = in_ref.shape[1]
    for c in range(in_ref.shape[0] // 4):
        at = slice(c * tall, (c + 1) * tall)
        for a in range(4):
            cols = slice(a * 192, (a + 1) * 192)
            block = in_ref[c * 4 + (who[1] ^ a)].astype(F32)
            q_ref[at, cols] = block[:, 64:256]
            v_ref[at, cols] = block[:, 256:448]
            k_ref[at, cols] = block[:, 448:640]
            if c == 0:
                for k in range(3):
                    spot = slice(a * 192 + k * 64, a * 192 + (k + 1) * 64)
                    bias_ref[0:1, spot] = block[k : k + 1, 0:64]
                    bias_ref[8:9, spot] = block[k + 3 : k + 4, 0:64]


def heads_out(who, gathered):
    outs = (((384, 768), F32),) * 3 + (((16, 768), F32),)
    return small_call(heads_kernel, who, (gathered,), outs, [], "heads_out")


def swap(block, axis="fsdp"):
    return lax.ppermute(block, axis, [(0, 1), (1, 0)])


def shifted(block, axis, distance):
    devices = range(lax.axis_size(axis))
    route = [(i - distance, i) for i in devices if i - distance in devices]
    return lax.ppermute(block, axis, route)


def flip(block, bit, axis="uly"):
    return lax.ppermute(block, axis, [(i, i ^ bit) for i in range(lax.axis_size(axis))])


def exchange(rows, axis):
    return lax.all_to_all(rows, axis, split_axis=0, concat_axis=0, tiled=True)


def spread_rows(rows, axis):
    count = lax.axis_size(axis)
    return exchange(jnp.broadcast_to(rows[None], (count, *rows.shape)).reshape(-1, rows.shape[1]), axis)


def sum_parts(rows, count):
    got = rows.reshape(count, -1, rows.shape[1])
    return sum(got[i].astype(F32) for i in range(count)).astype(BF)


def sum_scatter(rows, axis):
    return sum_parts(exchange(rows, axis), lax.axis_size(axis))


def add(left, right):
    return (left.astype(F32) + right.astype(F32)).astype(BF)


def line_step(held, bit):
    return flip(held, bit, "ctx")


def line_join(held, got, bit):
    low = (lax.axis_index("ctx") & bit) == 0
    return jnp.stack([jnp.where(low, held, got), jnp.where(low, got, held)], axis=1).reshape(-1, *held.shape[1:])


def line_rest(held, bit):
    while bit > 0:
        held = line_join(held, line_step(held, bit), bit)
        bit //= 2
    return held.reshape(-1, held.shape[2])


def chunks_of(rows, axis):
    count, me = lax.axis_size(axis), lax.axis_index(axis)
    split = rows.reshape(count, -1, rows.shape[1])
    picked = [lax.dynamic_index_in_dim(split, me ^ k, 0, keepdims=False) for k in range(count)]
    return [picked[0]] + [flip(picked[k], k, axis) for k in range(1, count)]


def tie(*values):
    return lax.optimization_barrier(values)


def on_device(
    tokens, teacher, cotangent, valid, teacher_ok, doc_starts, w_query, w_key, w_value, w_out, w_in, w_back,
    bias_query, bias_value, bias_out, bias_in, bias_back, norm1_gain, norm1_bias, norm2_gain, norm2_bias,
):
    groups = lax.axis_size("uly")
    spans = lax.axis_size("ctx")
    rows, width = tokens.shape
    block = rows * groups * 2
    stream = block * spans
    ctx_index = lax.axis_index("ctx")
    uly = lax.axis_index("uly")
    half = lax.axis_index("fsdp")
    head_cols = width // groups
    shard = w_query.shape[0]
    upper = uly // 2

    small = (bias_query, bias_value, bias_out, bias_in, bias_back, norm1_gain, norm1_bias, norm2_gain, norm2_bias)
    valid_one = valid[None, :]
    valid_own = jnp.concatenate([valid_one, flip(valid_one, 1), flip(valid_one, 2), flip(valid_one, 3)], axis=0)
    x_own, valid_own, *small = tie(tokens, valid_own, *small)
    x_x, x_y = flip(x_own, 1), flip(x_own, 2)
    valid_pair = swap(valid_own)
    place = jnp.arange(groups, dtype=jnp.int32)
    in_plane = place ^ uly
    valid_mine = jnp.take(valid_own, in_plane, axis=0).reshape(2, BLK)
    valid_next = jnp.take(valid_pair, in_plane, axis=0).reshape(2, BLK)
    from_low = shifted(jnp.stack([valid_mine[1], valid_next[1]]), "ctx", 1)
    from_high = shifted(jnp.stack([valid_mine[0], valid_next[0]]), "ctx", -1)
    block_valid = jnp.concatenate(
        [valid_mine, valid_next, from_low[:1], from_high[:1], from_low[1:], from_high[1:]], axis=0
    )
    count = jnp.full((8, 128), jnp.sum(valid_mine) + jnp.sum(valid_next), jnp.int32)
    bit = 1
    while bit < spans:
        count = count + flip(count, bit, "ctx")
        bit *= 2
    count = count[0, 0].astype(F32)

    start_col = uly * head_cols
    cut = [lax.dynamic_slice_in_dim(w, start_col, head_cols, 1) for w in (w_query, w_value, w_key)]
    w_mine = jnp.concatenate([jnp.zeros((shard, 256 - head_cols), BF), *cut], axis=1)
    w_other = swap(w_mine)
    packed = jnp.concatenate(small)
    packed_pair = swap(packed)
    first, second = jnp.where(half == 0, packed, packed_pair), jnp.where(half == 0, packed_pair, packed)
    vectors = []
    at = 0
    for p in small:
        n = p.shape[0]
        vectors.append(jnp.concatenate([first[at : at + n], second[at : at + n]]).astype(F32))
        at += n
    bq_all, bv_all = vectors[:2]
    vec = jnp.stack([jnp.pad(v, (0, w_in.shape[1] - v.shape[0])) for v in vectors[2:]] + [jnp.zeros((w_in.shape[1],), F32)])
    bias_heads = jnp.concatenate(
        [
            jnp.zeros((256 - head_cols,), F32),
            lax.dynamic_slice_in_dim(bq_all, start_col, head_cols, 0),
            lax.dynamic_slice_in_dim(bv_all, start_col, head_cols, 0),
            jnp.zeros((head_cols,), F32),
        ]
    )

    step = jnp.asarray([0, 0, 0, 0, -1, 1, -1, 1], jnp.int32)
    side = jnp.asarray([0, 1, 0, 1, 1, 0, 1, 0], jnp.int32)
    swapped = jnp.asarray([0, 0, 1, 1, 0, 0, 1, 1], jnp.int32)
    inner = jnp.arange(BLK, dtype=jnp.int32)
    first_block = (ctx_index + step) * (2 * groups) + side * groups + (half ^ swapped)
    spot = (first_block[:, None] + 2 * (inner // rows)[None, :]) * rows + lax.rem(inner, rows)[None, :]
    x_x, x_y, block_valid = tie(x_x, x_y, block_valid)
    edges = jnp.concatenate([doc_starts, jnp.full((DOCS + 1,), stream, jnp.int32)])
    window_first = jnp.maximum(ctx_index * block - block // 2, 0)
    first_doc = jnp.sum((doc_starts <= window_first).astype(jnp.int32)) - 1
    near = lax.dynamic_slice_in_dim(edges, first_doc, DOCS + 1, 0)
    tiles = groups * rows // TQ
    per = rows // TQ
    tile_ids = jnp.arange(tiles, dtype=jnp.int32)
    qfirst = ctx_index * block + (((tile_ids // per) ^ uly) * 2 + half) * rows + lax.rem(tile_ids, per) * TQ
    q_lo = jnp.max(jnp.where(near[None, :] <= qfirst[:, None], near[None, :], 0), axis=1)
    q_hi = jnp.min(jnp.where(near[None, :] <= qfirst[:, None] + TQ - 1, stream, near[None, :]), axis=1)
    limits = jnp.concatenate([near, q_lo, q_hi])
    counted = jnp.sum(block_valid[:, None, :] * (spot[:, None, :] < limits[None, :, None]), axis=-1)
    bounds = counted[:, : DOCS + 1]
    cnt_lo = counted[:, DOCS + 1 : DOCS + 1 + tiles].T
    cnt_hi = counted[:, DOCS + 1 + tiles :].T
    pad64 = jnp.zeros((bounds.shape[0], 128 - DOCS), jnp.int32)
    lo_tab = jnp.concatenate([bounds[:, :DOCS], pad64], axis=1)
    hi_tab = jnp.concatenate([bounds[:, 1:], pad64], axis=1)
    slo_tab = jnp.concatenate([near[:DOCS], pad64[0]])[None, :]
    shi_tab = jnp.concatenate([near[1:], pad64[0]])[None, :]
    some = cnt_hi > cnt_lo
    tlo = jnp.where(some, cnt_lo // TK, 0)
    thi = jnp.where(some, (cnt_hi + TK - 1) // TK, 0)
    tables = (tlo, thi, qfirst, lo_tab, hi_tab, slo_tab, shi_tab)
    before = mm(valid_own.astype(BF), (jnp.arange(rows)[:, None] < jnp.arange(rows)[None, :]).astype(BF)).astype(jnp.int32)
    filled = jnp.sum(valid_own, axis=1)
    shift = jnp.where(lax.rem(in_plane, 2) == 1, jnp.take(filled, place ^ 1), 0)
    base = (in_plane // 2) * BLK + (shift // 16) * 16
    goes_to = jnp.where(valid_own > 0, before + lax.rem(shift, 16)[:, None], 2 * BLK)
    ranks = jnp.arange(SPAN, dtype=jnp.int32)
    chosen = (goes_to[:, None, :] == ranks[None, :, None]).astype(BF)
    who = jnp.concatenate([jnp.stack([half, uly, upper]).astype(jnp.int32), base])
    loss_scale = jnp.float32(stream) / count
    keep = (loss_scale * (valid * teacher_ok).astype(F32))[:, None]

    x_x, x_y, w_other = tie(x_x, x_y, w_other)
    x_top, x_bottom = flip(x_y[: rows // 2], 1), flip(x_x[rows // 2 :], 2)
    x_top, x_bottom, chosen, bias_heads, *tables = tie(x_top, x_bottom, chosen, bias_heads, *tables)

    q_low, kv_own, kv_up, kv_down, w_heads = project(
        who, (tokens, x_x, x_y, x_top, x_bottom), w_mine, w_other, bias_heads[None, :], chosen
    )
    kv_from_left, kv_from_right = shifted(kv_up, "ctx", 1), shifted(kv_down, "ctx", -1)
    w_out, w_in, w_back, kv_own = tie(w_out, w_in, w_back, kv_own)
    wo_pair, win_pair, wback_pair = swap(w_out), swap(w_in), swap(w_back)
    kv_pair = swap(kv_own)
    state = attend(tables, q_low, (kv_own,), 0)
    kv_halo = jnp.concatenate([kv_from_left, kv_from_right], axis=0)
    kv_halo, kv_pair, *state = tie(kv_halo, kv_pair, *state)
    kv_halo_pair = swap(kv_halo)
    state = attend(tables, q_low, (kv_pair,), 2, state)
    o_heads, o_turned, lse = attend(tables, q_low, (kv_halo, kv_halo_pair), 4, state, last=True)
    o_rel = o_heads.reshape(groups, rows, head_cols)
    o_rest = [flip(o_rel[d], d) for d in range(1, groups)]
    o_heads, x_late, goes_late, x_x, x_y, x_top, x_bottom = tie(o_heads, tokens, goes_to, x_x, x_y, x_top, x_bottom)
    turned = (goes_late[:, :, None] == ranks[None, None, :]).astype(BF)
    x_all = jnp.concatenate([x_late, x_x, x_y, x_top, x_bottom], axis=0)

    x_all, turned, *o_rest = tie(x_all, turned, *o_rest)
    o_all = jnp.concatenate([o_rel[0], *o_rest], axis=0)

    out, d_resid1, d_parts, act, d_branch, d_pre, hidden_low, d_proj, sums = dense(
        who, o_all, (w_out, wo_pair, w_in, win_pair, w_back, wback_pair), tokens, teacher, cotangent, keep, vec
    )
    d_rel = d_parts.reshape(groups, rows, head_cols)
    tall = w_back.shape[0]
    vector_rows = jnp.concatenate(
        [sums[i, :width].reshape(2, -1) for i in (0, 2, 3, 4, 5, 6)] + [sums[1].reshape(2, -1)], axis=1
    ).reshape(2, -1, width)
    vector_rows = jnp.pad(vector_rows, ((0, 0), (0, 128 - vector_rows.shape[1]), (0, 0))).astype(BF)
    o_rows = o_all.reshape(groups, rows, head_cols)

    def back_part(side):
        return mm(lax.dynamic_slice_in_dim(act, side * tall, tall, 1), d_branch, TN).astype(BF)

    def in_part(side):
        return mm(lax.dynamic_slice_in_dim(hidden_low, side * shard, shard, 1), d_pre, TN).astype(BF)

    def out_part(side):
        both = [
            mm(lax.dynamic_index_in_dim(o_rows, (2 * side + e) ^ uly, 0, keepdims=False), d_proj, TN).astype(BF)
            for e in range(2)
        ]
        stack = jnp.concatenate([*both, lax.dynamic_index_in_dim(vector_rows, side, 0, keepdims=False)], axis=0)
        return jnp.concatenate([stack[i * 128 : (i + 1) * 128] for i in range(4)], axis=1)

    d_rest = [flip(d_rel[d], d) for d in range(1, groups)]
    back_got, in_got, out_got, *d_rest = tie(back_part(1 - half), in_part(1 - half), out_part(1 - half), *d_rest)
    back_got, in_got, out_got = swap(back_got), swap(in_got), swap(out_got)
    back_mine, in_mine, out_mine = back_part(half), in_part(half), out_part(half)
    back_got, in_got, out_got, back_mine, in_mine, out_mine = tie(
        back_got, in_got, out_got, back_mine, in_mine, out_mine
    )
    wide = w_in.shape[1]
    total = 2 * shard + 128
    am, ao, bm, bo = small_call(
        first_kernel, who, (back_mine, back_got, in_mine, in_got, out_mine, out_got),
        (((total // 4, wide), BF),) * 4, [pltpu.VMEM((total, wide), BF)], "first_stage",
    )
    d_heads = jnp.concatenate([d_rel[0], *d_rest], axis=0)
    d_heads, am, ao, bm, bo = tie(d_heads, am, ao, bm, bo)

    ag, bg = flip(ao, 1), flip(bo, 2)
    args = (tables, q_low, d_heads, o_turned, lse)
    dq0, got_lo, got_hi, delta = attend_back(
        *args, kv_halo_pair, 6, first=True, cuts=2, name="back_halo_pair"
    )
    got_lo, got_hi, delta = tie(got_lo, got_hi, delta)
    args = (tables, q_low, d_heads, delta, lse)
    got_lo, got_hi = swap(got_lo), swap(got_hi)
    dq1, halo_lo, halo_hi = attend_back(*args, kv_halo, 4, cuts=2, name="back_halo", size=1_000_000)
    halo_lo, halo_hi, got_lo, got_hi = tie(halo_lo, halo_hi, got_lo, got_hi)
    halo_lo, halo_hi = add(halo_lo, got_lo), add(halo_hi, got_hi)
    halo_lo, halo_hi, ag, bg = tie(halo_lo, halo_hi, ag, bg)

    am, ao, bm, bo = small_call(
        second_kernel, who, (am, ag, bm, bg), (((total // 8, wide), BF),) * 4,
        [pltpu.VMEM((total // 2, wide), BF)], "second_stage", 12 << 20,
    )
    halo_lo, halo_hi, delta, am, ao, bm, bo = tie(halo_lo, halo_hi, delta, am, ao, bm, bo)
    args = (tables, q_low, d_heads, delta, lse)
    ag, bg = flip(ao, 2), flip(bo, 1)
    from_left, from_right = shifted(halo_hi, "ctx", 1), shifted(halo_lo, "ctx", -1)
    dq2, dkv_pair = attend_back(*args, kv_pair, 2, name="back_pair")
    dkv_pair, ag, bg, from_left, from_right = tie(dkv_pair, ag, bg, from_left, from_right)

    (line,) = small_call(both_kernel, who, (am, ag, bm, bg), (((total // 4, wide), BF),), [], "third_stage", 12 << 20)
    line, dkv_pair, delta = tie(line, dkv_pair, delta)
    args = (tables, q_low, d_heads, delta, lse)
    line = exchange(line, "ctx")
    pair_got = swap(dkv_pair)
    dq3, dkv_own = attend_back(*args, kv_own, 0, name="back_own")
    dkv_own, line, pair_got = tie(dkv_own, line, pair_got)
    line = sum_parts(line, spans)
    line, dkv_own = tie(line, dkv_own)
    line = spread_rows(line, "ctx")

    d_all, d_sums, dx_own, give_x, give_y, left_next, right_next = finish(
        who, (dq0, dq1, dq2, dq3), dkv_own, pair_got, from_left, from_right, turned, w_heads
    )
    d_all, give_x, give_y = tie(d_all, give_x, give_y)
    give_x, give_y = flip(give_x, 1), flip(give_y, 2)
    corner = d_sums[0, 64:].reshape(9, 64)

    def heads_part(side):
        grad = mm(lax.dynamic_slice_in_dim(x_all, side * shard, shard, 1), d_all, TN)
        return lax.dynamic_update_slice(grad, corner, (0, 0)).astype(BF)

    heads_other = heads_part(1 - half)
    heads_got = swap(heads_other)
    heads_mine = heads_part(half)
    heads_sum = add(heads_mine, heads_got)
    line, give_x, give_y, *heads_parts = tie(line, give_x, give_y, *chunks_of(heads_sum, "ctx"))
    heads_sum = sum(part.astype(F32) for part in heads_parts).astype(BF)
    a_near, b_near = line[: total // 8], line[total // 8 :]
    a_got, b_got, *heads_rest = tie(
        flip(a_near, 2), flip(b_near, 1), *[flip(heads_sum, d) for d in range(1, groups)]
    )
    a_near = jnp.concatenate([a_near, a_got], axis=0)
    b_near = jnp.concatenate([b_near, b_got], axis=0)
    a_far, b_far = flip(a_near, 1), flip(b_near, 2)
    left_next = flip(add(left_next, give_x[rows:]), 2)
    right_next = flip(add(right_next, give_y[rows:]), 1)
    heads_sum = jnp.concatenate([heads_sum, *heads_rest], axis=0)
    heads_all = spread_rows(heads_sum, "ctx").reshape(spans * groups, -1, heads_sum.shape[1])
    grad_in = d_resid1 + dx_own.astype(F32)
    grad_in = grad_in + jnp.concatenate([give_x[:rows].astype(F32), give_y[:rows].astype(F32)], axis=1)
    grad_in = grad_in + jnp.concatenate([left_next.astype(F32), right_next.astype(F32)], axis=1)
    g_back, g_in, g_out, g_vec = join(
        who, (a_near, a_far, b_near, b_far), w_back.shape, w_in.shape, w_out.shape, total
    )
    g_query, g_key, g_value, g_bias = heads_out(who, heads_all)
    g_bias_q = lax.dynamic_slice_in_dim(g_bias[0], half * shard, shard, 0)
    g_bias_v = lax.dynamic_slice_in_dim(g_bias[8], half * shard, shard, 0)
    flat = g_vec.reshape(-1)
    g_bo, g_bb, g_g1, g_s1, g_g2, g_s2 = [flat[i * shard : (i + 1) * shard] for i in range(6)]
    g_bin = flat[6 * shard : 6 * shard + bias_in.shape[0]]
    return (
        out, grad_in, g_query, g_key, g_value, g_out, g_in, g_back,
        g_bias_q, g_bias_v, g_bo, g_bin, g_bb, g_g1, g_s1, g_g2, g_s2,
    )


def solution(mesh):
    placed = (
        P(("ctx", "uly", "fsdp"), None),
        P(("ctx", "uly", "fsdp"), None),
        P(("ctx", "uly", "fsdp"), None),
        P(("ctx", "uly", "fsdp")),
        P(("ctx", "uly", "fsdp")),
        P(),
        P("fsdp", None),
        P("fsdp", None),
        P("fsdp", None),
        P("fsdp", None),
        P("fsdp", None),
        P("fsdp", None),
        P("fsdp"),
        P("fsdp"),
        P("fsdp"),
        P("fsdp"),
        P("fsdp"),
        P("fsdp"),
        P("fsdp"),
        P("fsdp"),
        P("fsdp"),
    )
    return jax.shard_map(
        on_device,
        mesh=mesh,
        in_specs=placed,
        out_specs=(
            P(("ctx", "uly", "fsdp"), None),
            P(("ctx", "uly", "fsdp"), None),
            P("fsdp", None),
            P("fsdp", None),
            P("fsdp", None),
            P("fsdp", None),
            P("fsdp", None),
            P("fsdp", None),
            P("fsdp"),
            P("fsdp"),
            P("fsdp"),
            P("fsdp"),
            P("fsdp"),
            P("fsdp"),
            P("fsdp"),
            P("fsdp"),
            P("fsdp"),
        ),
        check_vma=False,
    )
```

```python
import functools

import jax
import jax.numpy as jnp
from jax import lax
from jax.experimental import pallas as pl
from jax.experimental.pallas import tpu as pltpu
from jax.sharding import PartitionSpec as P

HEADS = 12
HD = 64
BLK = 1024
SPAN = 640
TQ = 512
TK = 256
DOCS = 64
FFB = 1536
GRANT = 63 << 20
MASKED = -1e30
BF = jnp.bfloat16
F32 = jnp.float32
NT = (((1,), (1,)), ((), ()))
NN = (((1,), (0,)), ((), ()))
TN = (((0,), (0,)), ((), ()))


def mm(left, right, dims=NN):
    return lax.dot_general(left, right, dims, preferred_element_type=F32)


def whole(shape):
    return pl.BlockSpec(shape, lambda *_: (0,) * len(shape), pipeline_mode=pl.Buffered(1))


def sweep(total, step, work):
    def one(i, _):
        work(pl.multiple_of(i * step, step))
        return 0

    lax.fori_loop(0, total // step, one, 0)


def cost(flops, moved, special=0):
    return pl.CostEstimate(flops=flops, bytes_accessed=moved, transcendentals=special)


def lane_ids(rows):
    return lax.broadcasted_iota(jnp.int32, (rows, 128), 1)


def build_keys(sources, slot0, lo_ref, hi_ref, kaug, transposed, low_half):
    per = BLK // TK
    for at, kv in enumerate(sources):

        def one(j, _, at=at, kv=kv):
            rows = pl.ds(pl.multiple_of(j * TK, TK), TK)
            tile = at * (kv.shape[0] // TK) + j
            slot = slot0 + at * (kv.shape[0] // BLK) + j // per
            out = pl.ds(pl.multiple_of(tile * TK, TK), TK)
            rank = lax.broadcasted_iota(jnp.int32, (TK, 128), 0) + lax.rem(j, per) * TK
            inside = (rank >= lo_ref[pl.ds(slot, 1), :]) & (rank < hi_ref[pl.ds(slot, 1), :])
            bias = jnp.where(inside, 0.0, MASKED).astype(BF)
            kaug[out, 0:128] = jnp.where(lane_ids(TK) < 64, bias, kv[rows, 128:256])
            kaug[out, 128:256] = kv[rows, 256:384]
            if low_half:
                transposed[tile] = kv[rows, 0:256].T[0:192]
            else:
                transposed[tile] = kaug[out, :].T[64:256]
            return 0

        lax.fori_loop(0, kv.shape[0] // TK, one, 0)


def stack_queries(q, first, slo_ref, shi_ref, qs):
    lane = lane_ids(TQ)
    spot = lax.broadcasted_iota(jnp.int32, (TQ, 128), 0) + first
    mine = ((spot >= slo_ref[...]) & (spot < shi_ref[...])).astype(F32).astype(BF)
    zero = jnp.zeros((TQ, 128), BF)
    low, high = q[:, 0:128], q[:, 128:256]
    mark = jnp.where(lane < 64, mine, zero)
    qs[0:TQ, 0:128] = jnp.where(lane < 64, mine, low)
    qs[TQ : 2 * TQ, 0:128] = mark
    qs[2 * TQ :, 0:128] = mark
    qs[0:TQ, 128:256] = zero
    qs[TQ : 2 * TQ, 128:256] = jnp.where(lane < 64, high, zero)
    qs[2 * TQ :, 128:256] = jnp.where(lane < 64, zero, high)


def attend_kernel(*refs, slot0, count, resume, last):
    tlo, thi, qfirst, q_ref = refs[:4]
    sources = refs[4 : 4 + count]
    lo_ref, hi_ref, slo_ref, shi_ref = refs[4 + count : 8 + count]
    at = 8 + count
    if resume:
        acc_in, stat_in = refs[at : at + 2]
        at += 2
    if last:
        o_ref, ot_ref, lse_ref = refs[at : at + 3]
        at += 3
    else:
        acc_out, stat_out = refs[at : at + 2]
        at += 2
    kaug, vt, qs, acc, m_s, l_s = refs[at:]
    i = pl.program_id(0)

    @pl.when(i == 0)
    def _():
        build_keys(sources, slot0, lo_ref, hi_ref, kaug, vt, True)

    slots = count * sources[0].shape[0] // BLK
    per = BLK // TK
    stack_queries(q_ref[...], qfirst[i], slo_ref, shi_ref, qs)
    if resume:
        m_s[...] = stat_in[0, 0:1, :]
        l_s[...] = stat_in[0, 1:2, :]
        acc[...] = acc_in[0]
    else:
        m_s[...] = jnp.full_like(m_s, 2 * MASKED)
        l_s[...] = jnp.zeros_like(l_s)
        acc[...] = jnp.zeros_like(acc)

    def slot_loop(s, _):
        def key_loop(t, _):
            tile = s * per + t
            keys = pl.ds(pl.multiple_of(tile * TK, TK), TK)
            st = mm(kaug[keys, :], qs[...], NT)
            m_old = m_s[...]
            m_new = jnp.maximum(m_old, jnp.max(st, axis=0, keepdims=True))
            fade = jnp.exp(m_old - m_new)
            p = jnp.exp(st - m_new)
            l_s[...] = l_s[...] * fade + jnp.sum(p, axis=0, keepdims=True)
            m_s[...] = m_new
            low = p.astype(BF)
            for h in range(3):
                cols = slice(h * TQ, (h + 1) * TQ)
                part = slice(h * HD, (h + 1) * HD)
                acc[part, :] = acc[part, :] * fade[:, cols] + mm(vt[tile, part, :], low[:, cols])
            return 0

        return lax.fori_loop(tlo[i, slot0 + s], thi[i, slot0 + s], key_loop, 0)

    lax.fori_loop(0, slots, slot_loop, 0)
    if last:
        total = l_s[...]
        for h in range(3):
            cols = slice(h * TQ, (h + 1) * TQ)
            part = slice(h * HD, (h + 1) * HD)
            acc[part, :] = acc[part, :] / total[:, cols]
        ot_ref[0] = acc[...]
        o_ref[...] = acc[...].T.astype(BF)
        lse_ref[0] = m_s[...] + jnp.log(total)
    else:
        acc_out[0] = acc[...]
        stat_out[0, 0:1, :] = m_s[...]
        stat_out[0, 1:2, :] = l_s[...]


def rows_spec(shape):
    return pl.BlockSpec((TQ, shape[1]), lambda i, *_: (i, 0))


def tile_spec(shape):
    return pl.BlockSpec((1, *shape[1:]), lambda i, *_: (i, 0, 0))


def attend(tables, q, sources, slot0, state=None, last=False):
    tlo, thi, qfirst, lo, hi, slo, shi = tables
    tiles = q.shape[0] // TQ
    keys = sum(s.shape[0] for s in sources)
    state = tuple(state) if state else ()
    sd = jax.ShapeDtypeStruct
    acc, stat = sd((tiles, 3 * HD, TQ), F32), sd((tiles, 2, 3 * TQ), F32)
    if last:
        o, lse = sd((q.shape[0], 3 * HD), BF), sd((tiles, 1, 3 * TQ), F32)
        outs, out_specs = (o, acc, lse), (rows_spec(o.shape), tile_spec(acc.shape), tile_spec(lse.shape))
    else:
        outs, out_specs = (acc, stat), (tile_spec(acc.shape), tile_spec(stat.shape))
    return pl.pallas_call(
        functools.partial(attend_kernel, slot0=slot0, count=len(sources), resume=bool(state), last=last),
        out_shape=outs,
        grid_spec=pltpu.PrefetchScalarGridSpec(
            num_scalar_prefetch=3,
            grid=(tiles,),
            in_specs=[rows_spec(q.shape)]
            + [whole(x.shape) for x in (*sources, lo, hi, slo, shi)]
            + [tile_spec(x.shape) for x in state],
            out_specs=out_specs,
            scratch_shapes=[
                pltpu.VMEM((keys, 256), BF),
                pltpu.VMEM((keys // TK, 3 * HD, TK), BF),
                pltpu.VMEM((3 * TQ, 256), BF),
                pltpu.VMEM((3 * HD, TQ), F32),
                pltpu.VMEM((1, 3 * TQ), F32),
                pltpu.VMEM((1, 3 * TQ), F32),
            ],
        ),
        compiler_params=pltpu.CompilerParams(vmem_limit_bytes=GRANT),
        cost_estimate=cost(12_000_000_000, 12_000_000, 10_000_000),
        name="attend",
    )(tlo, thi, qfirst, q, *sources, lo, hi, slo, shi, *state)


def attend_back_kernel(
    tlo, thi, qfirst, q_ref, do_ref, ot_ref, lse_ref, kv, lo_ref, hi_ref, slo_ref, shi_ref, dq_ref, *rest,
    slot0, first, cuts,
):
    dkv_refs, rest = rest[:cuts], rest[cuts:]
    if first:
        delta_ref, *rest = rest
    kaug, kt, qs, dos, acc, dk_s, dv_s = rest
    keys_all = kv.shape[0]
    slots = keys_all // BLK
    per = BLK // TK
    i = pl.program_id(0)

    @pl.when(i == 0)
    def _():
        build_keys((kv,), slot0, lo_ref, hi_ref, kaug, kt, False)
        dk_s[...] = jnp.zeros_like(dk_s)
        dv_s[...] = jnp.zeros_like(dv_s)

    stack_queries(q_ref[...], qfirst[i], slo_ref, shi_ref, qs)
    do = do_ref[...]
    lane = lane_ids(TQ)
    zero = jnp.zeros((TQ, 128), BF)
    dos[0:TQ, 0:128] = jnp.where(lane < 64, do[:, 0:128], zero)
    dos[TQ : 2 * TQ, 0:128] = jnp.where(lane < 64, zero, do[:, 0:128])
    dos[2 * TQ :, 0:128] = zero
    dos[0 : 2 * TQ, 128:256] = jnp.zeros((2 * TQ, 128), BF)
    dos[2 * TQ :, 128:192] = do[:, 128:192]
    dos[2 * TQ :, 192:256] = jnp.zeros((TQ, 64), BF)
    if first:
        both = do.astype(F32).T * ot_ref[0]
        delta = jnp.concatenate(
            [jnp.sum(both[h * HD : (h + 1) * HD], axis=0, keepdims=True) for h in range(3)], axis=1
        )
        delta_ref[0] = delta
    else:
        delta = ot_ref[0]
    lse = lse_ref[0]
    acc[...] = jnp.zeros_like(acc)

    def slot_loop(s, _):
        def key_loop(t, _):
            tile = s * per + t
            keys = pl.ds(pl.multiple_of(tile * TK, TK), TK)
            st = mm(kaug[keys, :], qs[...], NT)
            p = jnp.exp(st - lse)
            dp = mm(kv[keys, 0:256], dos[...], NT)
            ds = (p * (dp - delta)).astype(BF)
            dv_s[keys, :] += mm(p.astype(BF), dos[...])
            dk_s[keys, :] += mm(ds, qs[...])
            for h in range(3):
                cols = slice(h * TQ, (h + 1) * TQ)
                acc[(h + 1) * HD : (h + 2) * HD, :] += mm(kt[tile, h * HD : (h + 1) * HD, :], ds[:, cols])
            return 0

        return lax.fori_loop(tlo[i, slot0 + s], thi[i, slot0 + s], key_loop, 0)

    lax.fori_loop(0, slots, slot_loop, 0)
    dq_ref[...] = (acc[...] * HD ** (-0.5)).T.astype(BF)

    @pl.when(i == pl.num_programs(0) - 1)
    def _():
        share = keys_all // cuts
        for j, dkv_ref in enumerate(dkv_refs):

            def write(r, j=j, dkv_ref=dkv_ref):
                at = pl.ds(pl.multiple_of(j * share + r, TK), TK)
                to = pl.ds(r, TK)
                dkv_ref[to, 0:128] = dv_s[at, 0:128].astype(BF)
                dkv_ref[to, 128:256] = jnp.where(lane_ids(TK) < 64, dv_s[at, 128:256], dk_s[at, 0:128]).astype(BF)
                dkv_ref[to, 256:384] = dk_s[at, 128:256].astype(BF)

            sweep(share, TK, write)


def attend_back(tables, q, do, ot, lse, source, slot0, first=False, cuts=1, name="attend_back", size=14_000_000_000):
    tlo, thi, qfirst, lo, hi, slo, shi = tables
    tiles = q.shape[0] // TQ
    keys = source.shape[0]
    sd = jax.ShapeDtypeStruct
    piece = (keys // cuts, source.shape[1])
    outs = (sd(q.shape, BF),) + (sd(piece, BF),) * cuts
    out_specs = (rows_spec(q.shape),) + (whole(piece),) * cuts
    if first:
        outs += (sd(lse.shape, F32),)
        out_specs += (tile_spec(lse.shape),)
    return pl.pallas_call(
        functools.partial(attend_back_kernel, slot0=slot0, first=first, cuts=cuts),
        out_shape=outs,
        grid_spec=pltpu.PrefetchScalarGridSpec(
            num_scalar_prefetch=3,
            grid=(tiles,),
            in_specs=[rows_spec(q.shape), rows_spec(do.shape), tile_spec(ot.shape), tile_spec(lse.shape)]
            + [whole(x.shape) for x in (source, lo, hi, slo, shi)],
            out_specs=out_specs,
            scratch_shapes=[
                pltpu.VMEM((keys, 256), BF),
                pltpu.VMEM((keys // TK, 3 * HD, TK), BF),
                pltpu.VMEM((3 * TQ, 256), BF),
                pltpu.VMEM((3 * TQ, 256), BF),
                pltpu.VMEM((256, TQ), F32),
                pltpu.VMEM((keys, 256), F32),
                pltpu.VMEM((keys, 256), F32),
            ],
        ),
        compiler_params=pltpu.CompilerParams(vmem_limit_bytes=GRANT),
        cost_estimate=cost(size, size // 1000, size // 3000),
        name=name,
    )(tlo, thi, qfirst, q, do, ot, lse, source, lo, hi, slo, shi)


def project_kernel(
    who, x0, x1, x2, x3_top, x3_bottom, w_mine, w_other, bias_ref, chosen, q_ref, kv_ref, up_ref, down_ref, w_ref, held
):
    tall = w_mine.shape[0]
    rows = x0.shape[0]
    w_ref[pl.ds(pl.multiple_of(who[0] * tall, tall), tall), :] = w_mine[...]
    w_ref[pl.ds(pl.multiple_of((1 - who[0]) * tall, tall), tall), :] = w_other[...]
    held[...] = jnp.zeros_like(held)
    for d, x in enumerate((x0, x1, x2, (x3_top, x3_bottom))):
        if d < 3:
            value = mm(x[...], w_ref[...]) + bias_ref[...]
        else:
            value = jnp.concatenate([mm(x[0][...], w_ref[...]), mm(x[1][...], w_ref[...])], axis=0) + bias_ref[...]
        at = slice(d * rows, (d + 1) * rows)
        q_ref[at, :] = (value[:, :256].astype(BF).astype(F32) * HD ** (-0.5)).astype(BF)
        to = pl.ds(pl.multiple_of(who[3 + d], 16), SPAN)
        held[to, :] += mm(chosen[d], value[:, 256:].astype(BF))
    kv_ref[...] = held[0 : 2 * BLK, :].astype(BF)
    down_ref[...] = kv_ref[0:BLK, :]
    up_ref[...] = kv_ref[BLK:, :]


def project(who, xs, w_mine, w_other, bias, chosen):
    sd = jax.ShapeDtypeStruct
    rows, width = xs[0].shape
    cols = w_mine.shape[1]
    ins = (*xs, w_mine, w_other, bias, chosen)
    outs = (
        sd((4 * rows, 256), BF), sd((4 * rows, cols - 256), BF), sd((2 * rows, cols - 256), BF),
        sd((2 * rows, cols - 256), BF), sd((width, cols), BF),
    )
    return pl.pallas_call(
        project_kernel,
        out_shape=outs,
        grid_spec=pltpu.PrefetchScalarGridSpec(
            num_scalar_prefetch=1,
            grid=(1,),
            in_specs=[whole(a.shape) for a in ins],
            out_specs=tuple(whole(a.shape) for a in outs),
            scratch_shapes=[pltpu.VMEM((2 * BLK + 128, cols - 256), F32)],
        ),
        compiler_params=pltpu.CompilerParams(vmem_limit_bytes=24 << 20),
        cost_estimate=cost(3_000_000_000, 12_000_000),
        name="project",
    )(who, *ins)


def row_mean(v):
    return jnp.sum(v, axis=-1, keepdims=True) * (1.0 / v.shape[-1])

def dense_kernel(
    who, o_ref, wo_a, wo_b, win_a, win_b, wback_a, wback_b, x_ref, teacher_ref, cot_ref, keep_ref, vec_ref,
    out_ref, dres_ref, dparts_ref, act_ref, dbr_ref, dpre_ref, hid_ref, dproj_ref, sums_ref,
    wo, win, wback, xh, inv, hidden, gp, acc, sems, *, FB
):
    rows, width = x_ref.shape
    groups = o_ref.shape[0] // rows
    part = width // groups
    units = win.shape[1]
    wo_loads, win_loads, wback_loads = [], [], []
    for i in range(2):
        side = who[0] if i == 0 else 1 - who[0]
        for e in range(groups // 2):
            to = pl.multiple_of(((side * (groups // 2) + e) ^ who[1]) * part, part)
            wo_loads.append(
                pltpu.make_async_copy((wo_a, wo_b)[i].at[pl.ds(e * part, part)], wo.at[pl.ds(to, part)], sems.at[2 * i + e])
            )
        for j, (pieces, target, held) in enumerate((((win_a, win_b), win, win_loads), ((wback_a, wback_b), wback, wback_loads))):
            tall = target.shape[0] // 2
            to = pl.multiple_of(side * tall, tall)
            held.append(pltpu.make_async_copy(pieces[i], target.at[pl.ds(to, tall)], sems.at[4 + 2 * i + j]))
    for load in wo_loads + win_loads + wback_loads:
        load.start()
    b_out, b_in, b_back = vec_ref[0:1, 0:width], vec_ref[1:2, :], vec_ref[2:3, 0:width]
    gain1, shift1, gain2, shift2 = (vec_ref[i : i + 1, 0:width] for i in range(3, 7))
    for load in wo_loads:
        load.wait()
    total = x_ref[...].astype(F32) + b_out
    for i in range(groups):
        total += mm(o_ref[i * rows : (i + 1) * rows, :], wo[i * part : (i + 1) * part, :])
    center = total - row_mean(total)
    scale = lax.rsqrt(row_mean(center * center) + 1e-12)
    inv[...] = scale
    unit = center * scale
    xh[...] = unit
    hid = unit * gain1 + shift1
    hidden[...] = hid
    hid_ref[...] = hid.astype(BF)
    acc[...] = jnp.zeros_like(acc)
    for load in win_loads + wback_loads:
        load.wait()

    def up(n, _):
        cols = pl.ds(pl.multiple_of(n * FB, FB), FB)
        pre = mm(hid_ref[...], win[:, cols]) + vec_ref[1:2, cols]
        cdf = 0.5 + 0.5 * lax.erf(pre * 0.7071067811865476)
        act = (pre * cdf).astype(BF)
        act_ref[:, cols] = act
        gp[:, cols] = cdf + pre * (jnp.exp(pre * pre * -0.5) * 0.3989422804014327)
        acc[...] += mm(act, wback[cols, :])
        return 0

    lax.fori_loop(0, units // FB, up, 0, unroll=False)
    total = hidden[...] + acc[...] + b_back
    center = total - row_mean(total)
    scale = lax.rsqrt(row_mean(center * center) + 1e-12)
    unit = center * scale
    result = unit * gain2 + shift2
    out_ref[...] = result.astype(BF)
    grad = cot_ref[...].astype(F32) + keep_ref[...] * (result - teacher_ref[...].astype(F32))
    def put(row, value):
        sums_ref[row : row + 1, 0 : value.shape[1]] = value
    put(5, jnp.sum(grad * unit, axis=0, keepdims=True))
    put(6, jnp.sum(grad, axis=0, keepdims=True))
    grad = grad * gain2
    back = scale * (grad - row_mean(grad) - unit * row_mean(grad * unit))
    acc[...] = back
    low = back.astype(BF)
    dbr_ref[...] = low
    put(2, jnp.sum(low.astype(F32), axis=0, keepdims=True))

    def down(n, _):
        cols = pl.ds(pl.multiple_of(n * FB, FB), FB)
        dpre = (mm(dbr_ref[...], wback[cols, :], NT) * gp[:, cols]).astype(BF)
        dpre_ref[:, cols] = dpre
        sums_ref[1:2, cols] = jnp.sum(dpre.astype(F32), axis=0, keepdims=True)
        acc[...] += mm(dpre, win[:, cols], NT)
        return 0

    lax.fori_loop(0, units // FB, down, 0, unroll=False)
    grad = acc[...]
    unit = xh[...]
    put(3, jnp.sum(grad * unit, axis=0, keepdims=True))
    put(4, jnp.sum(grad, axis=0, keepdims=True))
    grad = grad * gain1
    back = inv[...] * (grad - row_mean(grad) - unit * row_mean(grad * unit))
    dres_ref[...] = back
    low = back.astype(BF)
    dproj_ref[...] = low
    put(0, jnp.sum(low.astype(F32), axis=0, keepdims=True))
    for i in range(groups):
        dparts_ref[i * rows : (i + 1) * rows, :] = mm(low, wo[i * part : (i + 1) * part, :], NT).astype(BF)


def dense(who, o, weights, x, teacher, cot, keep, vec):
    rows, width = x.shape
    units = vec.shape[1]
    sd = jax.ShapeDtypeStruct
    outs = (
        sd((rows, width), BF), sd((rows, width), F32), sd(o.shape, BF), sd((rows, units), BF), sd((rows, width), BF),
        sd((rows, units), BF), sd((rows, width), BF), sd((rows, width), BF), sd((8, units), F32),
    )
    ins = (o, *weights, x, teacher, cot, keep, vec)
    stay = pl.BlockSpec(memory_space=pl.ANY)
    return pl.pallas_call(
        functools.partial(dense_kernel, FB=FFB),
        out_shape=outs,
        grid_spec=pltpu.PrefetchScalarGridSpec(
            num_scalar_prefetch=1,
            grid=(1,),
            in_specs=[whole(o.shape)] + [stay] * 6 + [whole(a.shape) for a in ins[7:]],
            out_specs=tuple(whole(a.shape) for a in outs),
            scratch_shapes=[
                pltpu.VMEM((width, width), BF), pltpu.VMEM((width, units), BF), pltpu.VMEM((units, width), BF),
                pltpu.VMEM((rows, width), F32), pltpu.VMEM((rows, 1), F32), pltpu.VMEM((rows, width), F32),
                pltpu.VMEM((rows, units), F32), pltpu.VMEM((rows, width), F32), pltpu.SemaphoreType.DMA((8,)),
            ],
        ),
        compiler_params=pltpu.CompilerParams(vmem_limit_bytes=GRANT),
        cost_estimate=cost(12_000_000_000, 30_000_000, 4_000_000),
        name="dense",
    )(who, *ins)


def finish_kernel(
    who, dq0, dq1, dq2, dq3, own_ref, pair_ref, left_ref, right_ref, turn_ref, w_ref,
    all_ref, sums_ref, dx_ref, gx_ref, gy_ref, next_left, next_right, held,
):
    d = pl.program_id(0)
    rows, width = dx_ref.shape
    cut = width // 2

    @pl.when(d == 0)
    def _():
        sums_ref[...] = jnp.zeros_like(sums_ref)
        held[2 * BLK :, :] = jnp.zeros((held.shape[0] - 2 * BLK, held.shape[1]), BF)
        for base, extra in ((0, left_ref), (BLK, right_ref)):

            def gather(r, base=base, extra=extra):
                at = pl.ds(pl.multiple_of(base + r, 128), 128)
                value = own_ref[at, :].astype(F32) + pair_ref[at, :].astype(F32)
                held[at, :] = (value + extra[pl.ds(r, 128), :].astype(F32)).astype(BF)

            sweep(BLK, 128, gather)

    tok = mm(turn_ref[0], held[pl.ds(pl.multiple_of(who[3 + d], 16), SPAN), :]).astype(BF)
    dq = sum(ref[...].astype(F32) for ref in (dq0, dq1, dq2, dq3)).astype(BF)
    all_ref[:, 0:256] = dq
    all_ref[:, 256:640] = tok
    sums_ref[0:1, 0:256] += jnp.sum(dq.astype(F32), axis=0, keepdims=True)
    sums_ref[0:1, 256:640] += jnp.sum(tok.astype(F32), axis=0, keepdims=True)
    part = mm(all_ref[...], w_ref[...], NT).astype(BF)

    @pl.when(d == 0)
    def _():
        dx_ref[...] = part

    @pl.when(d == 1)
    def _():
        gx_ref[0:rows, :] = part[:, :cut]
        next_right[...] = part[:, cut:]

    @pl.when(d == 2)
    def _():
        next_left[...] = part[:, :cut]
        gy_ref[0:rows, :] = part[:, cut:]

    @pl.when(d == 3)
    def _():
        gx_ref[rows:, :] = part[:, :cut]
        gy_ref[rows:, :] = part[:, cut:]


def finish(who, dqs, own, pair, left, right, turn, w_heads):
    sd = jax.ShapeDtypeStruct
    rows, width = turn.shape[1], w_heads.shape[0]
    cols = dqs[0].shape[1] + own.shape[1]
    ins = (*dqs, own, pair, left, right, turn, w_heads)
    shapes = ((rows, width), (2 * rows, width // 2), (2 * rows, width // 2), (rows, width // 2), (rows, width // 2))
    outs = (sd((4 * rows, cols), BF), sd((8, cols), F32)) + tuple(sd(s, BF) for s in shapes)

    def by_block(shape):
        return pl.BlockSpec((rows, shape[1]), lambda d, *_: (d, 0))

    return pl.pallas_call(
        finish_kernel,
        out_shape=outs,
        grid_spec=pltpu.PrefetchScalarGridSpec(
            num_scalar_prefetch=1,
            grid=(4,),
            in_specs=[by_block(a.shape) for a in ins[:4]]
            + [whole(a.shape) for a in ins[4:8]]
            + [pl.BlockSpec((1, *turn.shape[1:]), lambda d, *_: (d, 0, 0)), whole(w_heads.shape)],
            out_specs=(by_block(outs[0].shape), whole(outs[1].shape)) + tuple(whole(s) for s in shapes),
            scratch_shapes=[pltpu.VMEM((2 * BLK + 128, own.shape[1]), BF)],
        ),
        compiler_params=pltpu.CompilerParams(vmem_limit_bytes=GRANT),
        cost_estimate=cost(3_000_000_000, 16_000_000),
        name="finish",
    )(who, *ins)


def part_out(who, held, am, ao, bm, bo, sides):
    part = am.shape[0]
    for mine, other, side, base in ((am, ao, sides[0], 0), (bm, bo, sides[1], 2 * part)):

        def move(r, mine=mine, other=other, side=side, base=base):
            mine[pl.ds(r, 16), :] = held[pl.ds(pl.multiple_of(base + side * part + r, 16), 16), :]
            other[pl.ds(r, 16), :] = held[pl.ds(pl.multiple_of(base + (1 - side) * part + r, 16), 16), :]

        sweep(part, 16, move)


def plus(left, right, at):
    return (left[at, :].astype(F32) + right[at, :].astype(F32)).astype(BF)


def first_kernel(who, back_a, back_b, in_a, in_b, out_a, out_b, am, ao, bm, bo, held):
    width = back_a.shape[1]
    tall = in_a.shape[0]

    def upper(r):
        at = pl.ds(r, 16)
        for k in range(4):
            held[at, k * width : (k + 1) * width] = plus(back_a, back_b, pl.ds(pl.multiple_of(k * tall + r, 16), 16))
        held[pl.ds(pl.multiple_of(tall + r, 16), 16), :] = plus(in_a, in_b, at)

    def lower(r):
        held[pl.ds(pl.multiple_of(2 * tall + r, 16), 16), :] = plus(out_a, out_b, pl.ds(r, 16))

    sweep(tall, 16, upper)
    sweep(out_a.shape[0], 16, lower)
    part_out(who, held, am, ao, bm, bo, (lax.rem(who[1], 2), who[1] // 2))


def both_kernel(who, a_mine, a_got, b_mine, b_got, both):
    del who
    part = a_mine.shape[0]

    def work(r):
        both[pl.ds(r, 16), :] = plus(a_mine, a_got, pl.ds(r, 16))
        both[pl.ds(pl.multiple_of(part + r, 16), 16), :] = plus(b_mine, b_got, pl.ds(r, 16))

    sweep(part, 16, work)


def second_kernel(who, a_mine, a_got, b_mine, b_got, am, ao, bm, bo, held):
    both_kernel(who, a_mine, a_got, b_mine, b_got, held)
    part_out(who, held, am, ao, bm, bo, (who[1] // 2, lax.rem(who[1], 2)))


def join_kernel(who, a, b, c, d, back_ref, in_ref, out_ref, vec_ref, held):
    step = pl.program_id(0)

    @pl.when(step == 0)
    def _():
        gather_pieces(who, (a, b, c, d), held)

    tall = held.shape[0] - 128
    tall, width = tall // 2, back_ref.shape[1]
    cols = pl.ds(pl.multiple_of(step * width, 128), width)
    back_ref[...] = held[0:tall, cols].astype(F32)
    rows = in_ref.shape[0]
    in_ref[...] = held[pl.ds(pl.multiple_of(tall + step * rows, 16), rows), :].astype(F32)

    @pl.when(step < 3)
    def _():
        out_ref[...] = held[2 * tall :, cols].astype(F32)

    @pl.when(step == 3)
    def _():
        vec_ref[...] = held[2 * tall : 2 * tall + 16, 3 * width :].astype(F32)


def gather_pieces(who, pieces, held):
    s1, s2 = lax.rem(who[1], 2), who[1] // 2
    part = pieces[0].shape[0] // 2
    for at, ref in enumerate(pieces):
        color, i = at // 2, at % 2
        for j in range(2):
            spot = (s1 ^ i) * 2 + (s2 ^ j) if color == 0 else 4 + (s2 ^ i) * 2 + (s1 ^ j)

            def move(r, spot=spot, ref=ref, j=j):
                frm = pl.ds(pl.multiple_of(j * part + r, 16), 16)
                held[pl.ds(pl.multiple_of(spot * part + r, 16), 16), :] = ref[frm, :]

            sweep(part, 16, move)

def join(who, pieces, back, first, out, total):
    sd = jax.ShapeDtypeStruct
    tall, width = first[0], back[1]
    outs = (sd(back, F32), sd(first, F32), sd(out, F32), sd((16, width), F32))
    return pl.pallas_call(
        join_kernel,
        out_shape=outs,
        grid_spec=pltpu.PrefetchScalarGridSpec(
            num_scalar_prefetch=1,
            grid=(4,),
            in_specs=[whole(a.shape) for a in pieces],
            out_specs=(
                pl.BlockSpec((tall, width), lambda k, *_: (k, 0)),
                pl.BlockSpec((tall // 4, first[1]), lambda k, *_: (k, 0)),
                pl.BlockSpec((128, width), lambda k, *_: (jnp.minimum(k, 2), 0)),
                whole((16, width)),
            ),
            scratch_shapes=[pltpu.VMEM((total, first[1]), BF)],
        ),
        compiler_params=pltpu.CompilerParams(vmem_limit_bytes=GRANT),
        cost_estimate=cost(1_000_000, 16_000_000),
        name="join",
    )(who, *pieces)


def small_call(kernel, who, pieces, outs, scratch, name, grant=24 << 20):
    return pl.pallas_call(
        kernel,
        out_shape=tuple(jax.ShapeDtypeStruct(*s) for s in outs),
        grid_spec=pltpu.PrefetchScalarGridSpec(
            num_scalar_prefetch=1,
            grid=(1,),
            in_specs=[whole(a.shape) for a in pieces],
            out_specs=tuple(whole(s[0]) for s in outs),
            scratch_shapes=scratch,
        ),
        compiler_params=pltpu.CompilerParams(vmem_limit_bytes=grant),
        cost_estimate=cost(1_000_000, 9_000_000),
        name=name,
    )(who, *pieces)


def heads_kernel(who, in_ref, q_ref, k_ref, v_ref, bias_ref):
    tall = in_ref.shape[1]
    for c in range(in_ref.shape[0] // 4):
        at = slice(c * tall, (c + 1) * tall)
        for a in range(4):
            cols = slice(a * 192, (a + 1) * 192)
            block = in_ref[c * 4 + (who[1] ^ a)].astype(F32)
            q_ref[at, cols] = block[:, 64:256]
            v_ref[at, cols] = block[:, 256:448]
            k_ref[at, cols] = block[:, 448:640]
            if c == 0:
                for k in range(3):
                    spot = slice(a * 192 + k * 64, a * 192 + (k + 1) * 64)
                    bias_ref[0:1, spot] = block[k : k + 1, 0:64]
                    bias_ref[8:9, spot] = block[k + 3 : k + 4, 0:64]


def heads_out(who, gathered):
    outs = (((384, 768), F32),) * 3 + (((16, 768), F32),)
    return small_call(heads_kernel, who, (gathered,), outs, [], "heads_out")


def swap(block, axis="fsdp"):
    return lax.ppermute(block, axis, [(0, 1), (1, 0)])


def shifted(block, axis, distance):
    devices = range(lax.axis_size(axis))
    route = [(i - distance, i) for i in devices if i - distance in devices]
    return lax.ppermute(block, axis, route)


def flip(block, bit, axis="uly"):
    return lax.ppermute(block, axis, [(i, i ^ bit) for i in range(lax.axis_size(axis))])


def exchange(rows, axis):
    return lax.all_to_all(rows, axis, split_axis=0, concat_axis=0, tiled=True)


def spread_rows(rows, axis):
    count = lax.axis_size(axis)
    return exchange(jnp.broadcast_to(rows[None], (count, *rows.shape)).reshape(-1, rows.shape[1]), axis)


def sum_parts(rows, count):
    got = rows.reshape(count, -1, rows.shape[1])
    return sum(got[i].astype(F32) for i in range(count)).astype(BF)


def sum_scatter(rows, axis):
    return sum_parts(exchange(rows, axis), lax.axis_size(axis))


def add(left, right):
    return (left.astype(F32) + right.astype(F32)).astype(BF)


def line_step(held, bit):
    return flip(held, bit, "ctx")


def line_join(held, got, bit):
    low = (lax.axis_index("ctx") & bit) == 0
    return jnp.stack([jnp.where(low, held, got), jnp.where(low, got, held)], axis=1).reshape(-1, *held.shape[1:])


def line_rest(held, bit):
    while bit > 0:
        held = line_join(held, line_step(held, bit), bit)
        bit //= 2
    return held.reshape(-1, held.shape[2])


def chunks_of(rows, axis):
    count, me = lax.axis_size(axis), lax.axis_index(axis)
    split = rows.reshape(count, -1, rows.shape[1])
    picked = [lax.dynamic_index_in_dim(split, me ^ k, 0, keepdims=False) for k in range(count)]
    return [picked[0]] + [flip(picked[k], k, axis) for k in range(1, count)]


def tie(*values):
    return lax.optimization_barrier(values)


def on_device(
    tokens, teacher, cotangent, valid, teacher_ok, doc_starts, w_query, w_key, w_value, w_out, w_in, w_back,
    bias_query, bias_value, bias_out, bias_in, bias_back, norm1_gain, norm1_bias, norm2_gain, norm2_bias,
):
    groups = lax.axis_size("uly")
    spans = lax.axis_size("ctx")
    rows, width = tokens.shape
    block = rows * groups * 2
    stream = block * spans
    ctx_index = lax.axis_index("ctx")
    uly = lax.axis_index("uly")
    half = lax.axis_index("fsdp")
    head_cols = width // groups
    shard = w_query.shape[0]
    upper = uly // 2

    small = (bias_query, bias_value, bias_out, bias_in, bias_back, norm1_gain, norm1_bias, norm2_gain, norm2_bias)
    valid_one = valid[None, :]
    valid_own = jnp.concatenate([valid_one, flip(valid_one, 1), flip(valid_one, 2), flip(valid_one, 3)], axis=0)
    x_own, valid_own, *small = tie(tokens, valid_own, *small)
    x_x, x_y = flip(x_own, 1), flip(x_own, 2)
    valid_pair = swap(valid_own)
    place = jnp.arange(groups, dtype=jnp.int32)
    in_plane = place ^ uly
    valid_mine = jnp.take(valid_own, in_plane, axis=0).reshape(2, BLK)
    valid_next = jnp.take(valid_pair, in_plane, axis=0).reshape(2, BLK)
    from_low = shifted(jnp.stack([valid_mine[1], valid_next[1]]), "ctx", 1)
    from_high = shifted(jnp.stack([valid_mine[0], valid_next[0]]), "ctx", -1)
    block_valid = jnp.concatenate(
        [valid_mine, valid_next, from_low[:1], from_high[:1], from_low[1:], from_high[1:]], axis=0
    )
    count = jnp.full((8, 128), jnp.sum(valid_mine) + jnp.sum(valid_next), jnp.int32)
    bit = 1
    while bit < spans:
        count = count + flip(count, bit, "ctx")
        bit *= 2
    count = count[0, 0].astype(F32)

    start_col = uly * head_cols
    cut = [lax.dynamic_slice_in_dim(w, start_col, head_cols, 1) for w in (w_query, w_value, w_key)]
    w_mine = jnp.concatenate([jnp.zeros((shard, 256 - head_cols), BF), *cut], axis=1)
    w_other = swap(w_mine)
    packed = jnp.concatenate(small)
    packed_pair = swap(packed)
    first, second = jnp.where(half == 0, packed, packed_pair), jnp.where(half == 0, packed_pair, packed)
    vectors = []
    at = 0
    for p in small:
        n = p.shape[0]
        vectors.append(jnp.concatenate([first[at : at + n], second[at : at + n]]).astype(F32))
        at += n
    bq_all, bv_all = vectors[:2]
    vec = jnp.stack([jnp.pad(v, (0, w_in.shape[1] - v.shape[0])) for v in vectors[2:]] + [jnp.zeros((w_in.shape[1],), F32)])
    bias_heads = jnp.concatenate(
        [
            jnp.zeros((256 - head_cols,), F32),
            lax.dynamic_slice_in_dim(bq_all, start_col, head_cols, 0),
            lax.dynamic_slice_in_dim(bv_all, start_col, head_cols, 0),
            jnp.zeros((head_cols,), F32),
        ]
    )

    step = jnp.asarray([0, 0, 0, 0, -1, 1, -1, 1], jnp.int32)
    side = jnp.asarray([0, 1, 0, 1, 1, 0, 1, 0], jnp.int32)
    swapped = jnp.asarray([0, 0, 1, 1, 0, 0, 1, 1], jnp.int32)
    inner = jnp.arange(BLK, dtype=jnp.int32)
    first_block = (ctx_index + step) * (2 * groups) + side * groups + (half ^ swapped)
    spot = (first_block[:, None] + 2 * (inner // rows)[None, :]) * rows + lax.rem(inner, rows)[None, :]
    x_x, x_y, block_valid = tie(x_x, x_y, block_valid)
    edges = jnp.concatenate([doc_starts, jnp.full((DOCS + 1,), stream, jnp.int32)])
    window_first = jnp.maximum(ctx_index * block - block // 2, 0)
    first_doc = jnp.sum((doc_starts <= window_first).astype(jnp.int32)) - 1
    near = lax.dynamic_slice_in_dim(edges, first_doc, DOCS + 1, 0)
    tiles = groups * rows // TQ
    per = rows // TQ
    tile_ids = jnp.arange(tiles, dtype=jnp.int32)
    qfirst = ctx_index * block + (((tile_ids // per) ^ uly) * 2 + half) * rows + lax.rem(tile_ids, per) * TQ
    q_lo = jnp.max(jnp.where(near[None, :] <= qfirst[:, None], near[None, :], 0), axis=1)
    q_hi = jnp.min(jnp.where(near[None, :] <= qfirst[:, None] + TQ - 1, stream, near[None, :]), axis=1)
    limits = jnp.concatenate([near, q_lo, q_hi])
    counted = jnp.sum(block_valid[:, None, :] * (spot[:, None, :] < limits[None, :, None]), axis=-1)
    bounds = counted[:, : DOCS + 1]
    cnt_lo = counted[:, DOCS + 1 : DOCS + 1 + tiles].T
    cnt_hi = counted[:, DOCS + 1 + tiles :].T
    pad64 = jnp.zeros((bounds.shape[0], 128 - DOCS), jnp.int32)
    lo_tab = jnp.concatenate([bounds[:, :DOCS], pad64], axis=1)
    hi_tab = jnp.concatenate([bounds[:, 1:], pad64], axis=1)
    slo_tab = jnp.concatenate([near[:DOCS], pad64[0]])[None, :]
    shi_tab = jnp.concatenate([near[1:], pad64[0]])[None, :]
    some = cnt_hi > cnt_lo
    tlo = jnp.where(some, cnt_lo // TK, 0)
    thi = jnp.where(some, (cnt_hi + TK - 1) // TK, 0)
    tables = (tlo, thi, qfirst, lo_tab, hi_tab, slo_tab, shi_tab)
    before = mm(valid_own.astype(BF), (jnp.arange(rows)[:, None] < jnp.arange(rows)[None, :]).astype(BF)).astype(jnp.int32)
    filled = jnp.sum(valid_own, axis=1)
    shift = jnp.where(lax.rem(in_plane, 2) == 1, jnp.take(filled, place ^ 1), 0)
    base = (in_plane // 2) * BLK + (shift // 16) * 16
    goes_to = jnp.where(valid_own > 0, before + lax.rem(shift, 16)[:, None], 2 * BLK)
    ranks = jnp.arange(SPAN, dtype=jnp.int32)
    chosen = (goes_to[:, None, :] == ranks[None, :, None]).astype(BF)
    who = jnp.concatenate([jnp.stack([half, uly, upper]).astype(jnp.int32), base])
    loss_scale = jnp.float32(stream) / count
    keep = (loss_scale * (valid * teacher_ok).astype(F32))[:, None]

    x_x, x_y, w_other = tie(x_x, x_y, w_other)
    x_top, x_bottom = flip(x_y[: rows // 2], 1), flip(x_x[rows // 2 :], 2)
    x_top, x_bottom, chosen, bias_heads, *tables = tie(x_top, x_bottom, chosen, bias_heads, *tables)

    q_low, kv_own, kv_up, kv_down, w_heads = project(
        who, (tokens, x_x, x_y, x_top, x_bottom), w_mine, w_other, bias_heads[None, :], chosen
    )
    kv_from_left, kv_from_right = shifted(kv_up, "ctx", 1), shifted(kv_down, "ctx", -1)
    w_out, w_in, w_back, kv_own = tie(w_out, w_in, w_back, kv_own)
    wo_pair, win_pair, wback_pair = swap(w_out), swap(w_in), swap(w_back)
    kv_pair = swap(kv_own)
    state = attend(tables, q_low, (kv_own, kv_pair), 0)
    kv_from_left, kv_from_right, wo_pair, win_pair, wback_pair, *state = tie(
        kv_from_left, kv_from_right, wo_pair, win_pair, wback_pair, *state
    )
    pair_left, pair_right = swap(kv_from_left), swap(kv_from_right)
    o_heads, o_turned, lse = attend(
        tables, q_low, (kv_from_left, kv_from_right, pair_left, pair_right), 4, state, last=True
    )
    o_rel = o_heads.reshape(groups, rows, head_cols)
    o_rest = [flip(o_rel[d], d) for d in range(1, groups)]
    o_heads, x_late, goes_late, x_x, x_y, x_top, x_bottom = tie(o_heads, tokens, goes_to, x_x, x_y, x_top, x_bottom)
    turned = (goes_late[:, :, None] == ranks[None, None, :]).astype(BF)
    x_all = jnp.concatenate([x_late, x_x, x_y, x_top, x_bottom], axis=0)

    kv_halo = jnp.concatenate([kv_from_left, kv_from_right], axis=0)
    kv_halo_pair = jnp.concatenate([pair_left, pair_right], axis=0)
    x_all, turned, kv_halo, kv_halo_pair, *o_rest = tie(x_all, turned, kv_halo, kv_halo_pair, *o_rest)
    o_all = jnp.concatenate([o_rel[0], *o_rest], axis=0)

    out, d_resid1, d_parts, act, d_branch, d_pre, hidden_low, d_proj, sums = dense(
        who, o_all, (w_out, wo_pair, w_in, win_pair, w_back, wback_pair), tokens, teacher, cotangent, keep, vec
    )
    d_rel = d_parts.reshape(groups, rows, head_cols)
    tall = w_back.shape[0]
    vector_rows = jnp.concatenate(
        [sums[i, :width].reshape(2, -1) for i in (0, 2, 3, 4, 5, 6)] + [sums[1].reshape(2, -1)], axis=1
    ).reshape(2, -1, width)
    vector_rows = jnp.pad(vector_rows, ((0, 0), (0, 128 - vector_rows.shape[1]), (0, 0))).astype(BF)
    o_rows = o_all.reshape(groups, rows, head_cols)

    def back_part(side):
        return mm(lax.dynamic_slice_in_dim(act, side * tall, tall, 1), d_branch, TN).astype(BF)

    def in_part(side):
        return mm(lax.dynamic_slice_in_dim(hidden_low, side * shard, shard, 1), d_pre, TN).astype(BF)

    def out_part(side):
        both = [
            mm(lax.dynamic_index_in_dim(o_rows, (2 * side + e) ^ uly, 0, keepdims=False), d_proj, TN).astype(BF)
            for e in range(2)
        ]
        stack = jnp.concatenate([*both, lax.dynamic_index_in_dim(vector_rows, side, 0, keepdims=False)], axis=0)
        return jnp.concatenate([stack[i * 128 : (i + 1) * 128] for i in range(4)], axis=1)

    d_rest = [flip(d_rel[d], d) for d in range(1, groups)]
    back_got, in_got, out_got, *d_rest = tie(back_part(1 - half), in_part(1 - half), out_part(1 - half), *d_rest)
    back_got, in_got, out_got = swap(back_got), swap(in_got), swap(out_got)
    back_mine, in_mine, out_mine = back_part(half), in_part(half), out_part(half)
    back_got, in_got, out_got, back_mine, in_mine, out_mine = tie(
        back_got, in_got, out_got, back_mine, in_mine, out_mine
    )
    wide = w_in.shape[1]
    total = 2 * shard + 128
    am, ao, bm, bo = small_call(
        first_kernel, who, (back_mine, back_got, in_mine, in_got, out_mine, out_got),
        (((total // 4, wide), BF),) * 4, [pltpu.VMEM((total, wide), BF)], "first_stage",
    )
    d_heads = jnp.concatenate([d_rel[0], *d_rest], axis=0)
    d_heads, am, ao, bm, bo = tie(d_heads, am, ao, bm, bo)

    ag, bg = flip(ao, 1), flip(bo, 2)
    args = (tables, q_low, d_heads, o_turned, lse)
    dq0, got_lo, got_hi, delta = attend_back(
        *args, kv_halo_pair, 6, first=True, cuts=2, name="back_halo_pair"
    )
    got_lo, got_hi, delta = tie(got_lo, got_hi, delta)
    args = (tables, q_low, d_heads, delta, lse)
    got_lo, got_hi = swap(got_lo), swap(got_hi)
    dq1, halo_lo, halo_hi = attend_back(*args, kv_halo, 4, cuts=2, name="back_halo", size=1_000_000)
    halo_lo, halo_hi, got_lo, got_hi = tie(halo_lo, halo_hi, got_lo, got_hi)
    halo_lo, halo_hi = add(halo_lo, got_lo), add(halo_hi, got_hi)
    halo_lo, halo_hi, ag, bg = tie(halo_lo, halo_hi, ag, bg)

    am, ao, bm, bo = small_call(
        second_kernel, who, (am, ag, bm, bg), (((total // 8, wide), BF),) * 4,
        [pltpu.VMEM((total // 2, wide), BF)], "second_stage", 12 << 20,
    )
    halo_lo, halo_hi, delta, am, ao, bm, bo = tie(halo_lo, halo_hi, delta, am, ao, bm, bo)
    args = (tables, q_low, d_heads, delta, lse)
    ag, bg = flip(ao, 2), flip(bo, 1)
    from_left, from_right = shifted(halo_hi, "ctx", 1), shifted(halo_lo, "ctx", -1)
    dq2, dkv_pair = attend_back(*args, kv_pair, 2, name="back_pair")
    dkv_pair, ag, bg, from_left, from_right = tie(dkv_pair, ag, bg, from_left, from_right)

    (line,) = small_call(both_kernel, who, (am, ag, bm, bg), (((total // 4, wide), BF),), [], "third_stage", 12 << 20)
    line, dkv_pair, delta = tie(line, dkv_pair, delta)
    args = (tables, q_low, d_heads, delta, lse)
    line = exchange(line, "ctx")
    pair_got = swap(dkv_pair)
    dq3, dkv_own = attend_back(*args, kv_own, 0, name="back_own")
    dkv_own, line, pair_got = tie(dkv_own, line, pair_got)
    line = sum_parts(line, spans)
    line, dkv_own = tie(line, dkv_own)
    line = spread_rows(line, "ctx")

    d_all, d_sums, dx_own, give_x, give_y, left_next, right_next = finish(
        who, (dq0, dq1, dq2, dq3), dkv_own, pair_got, from_left, from_right, turned, w_heads
    )
    d_all, give_x, give_y = tie(d_all, give_x, give_y)
    give_x, give_y = flip(give_x, 1), flip(give_y, 2)
    corner = d_sums[0, 64:].reshape(9, 64)

    def heads_part(side):
        grad = mm(lax.dynamic_slice_in_dim(x_all, side * shard, shard, 1), d_all, TN)
        return lax.dynamic_update_slice(grad, corner, (0, 0)).astype(BF)

    heads_other = heads_part(1 - half)
    heads_got = swap(heads_other)
    heads_mine = heads_part(half)
    heads_sum = add(heads_mine, heads_got)
    line, give_x, give_y, *heads_parts = tie(line, give_x, give_y, *chunks_of(heads_sum, "ctx"))
    heads_sum = sum(part.astype(F32) for part in heads_parts).astype(BF)
    a_near, b_near = line[: total // 8], line[total // 8 :]
    a_got, b_got, *heads_rest = tie(
        flip(a_near, 2), flip(b_near, 1), *[flip(heads_sum, d) for d in range(1, groups)]
    )
    a_near = jnp.concatenate([a_near, a_got], axis=0)
    b_near = jnp.concatenate([b_near, b_got], axis=0)
    a_far, b_far = flip(a_near, 1), flip(b_near, 2)
    left_next = flip(add(left_next, give_x[rows:]), 2)
    right_next = flip(add(right_next, give_y[rows:]), 1)
    heads_sum = jnp.concatenate([heads_sum, *heads_rest], axis=0)
    heads_all = spread_rows(heads_sum, "ctx").reshape(spans * groups, -1, heads_sum.shape[1])
    grad_in = d_resid1 + dx_own.astype(F32)
    grad_in = grad_in + jnp.concatenate([give_x[:rows].astype(F32), give_y[:rows].astype(F32)], axis=1)
    grad_in = grad_in + jnp.concatenate([left_next.astype(F32), right_next.astype(F32)], axis=1)
    g_back, g_in, g_out, g_vec = join(
        who, (a_near, a_far, b_near, b_far), w_back.shape, w_in.shape, w_out.shape, total
    )
    g_query, g_key, g_value, g_bias = heads_out(who, heads_all)
    g_bias_q = lax.dynamic_slice_in_dim(g_bias[0], half * shard, shard, 0)
    g_bias_v = lax.dynamic_slice_in_dim(g_bias[8], half * shard, shard, 0)
    flat = g_vec.reshape(-1)
    g_bo, g_bb, g_g1, g_s1, g_g2, g_s2 = [flat[i * shard : (i + 1) * shard] for i in range(6)]
    g_bin = flat[6 * shard : 6 * shard + bias_in.shape[0]]
    return (
        out, grad_in, g_query, g_key, g_value, g_out, g_in, g_back,
        g_bias_q, g_bias_v, g_bo, g_bin, g_bb, g_g1, g_s1, g_g2, g_s2,
    )


def solution(mesh):
    placed = (
        P(("ctx", "uly", "fsdp"), None),
        P(("ctx", "uly", "fsdp"), None),
        P(("ctx", "uly", "fsdp"), None),
        P(("ctx", "uly", "fsdp")),
        P(("ctx", "uly", "fsdp")),
        P(),
        P("fsdp", None),
        P("fsdp", None),
        P("fsdp", None),
        P("fsdp", None),
        P("fsdp", None),
        P("fsdp", None),
        P("fsdp"),
        P("fsdp"),
        P("fsdp"),
        P("fsdp"),
        P("fsdp"),
        P("fsdp"),
        P("fsdp"),
        P("fsdp"),
        P("fsdp"),
    )
    return jax.shard_map(
        on_device,
        mesh=mesh,
        in_specs=placed,
        out_specs=(
            P(("ctx", "uly", "fsdp"), None),
            P(("ctx", "uly", "fsdp"), None),
            P("fsdp", None),
            P("fsdp", None),
            P("fsdp", None),
            P("fsdp", None),
            P("fsdp", None),
            P("fsdp", None),
            P("fsdp"),
            P("fsdp"),
            P("fsdp"),
            P("fsdp"),
            P("fsdp"),
            P("fsdp"),
            P("fsdp"),
            P("fsdp"),
            P("fsdp"),
        ),
        check_vma=False,
    )
```

```python
import functools

import jax
import jax.numpy as jnp
from jax import lax
from jax.experimental import pallas as pl
from jax.experimental.pallas import tpu as pltpu
from jax.sharding import PartitionSpec as P

HEADS = 12
HD = 64
BLK = 1024
SPAN = 640
TQ = 512
TK = 256
DOCS = 64
FFB = 1536
GRANT = 63 << 20
MASKED = -1e30
BF = jnp.bfloat16
F32 = jnp.float32
NT = (((1,), (1,)), ((), ()))
NN = (((1,), (0,)), ((), ()))
TN = (((0,), (0,)), ((), ()))


def mm(left, right, dims=NN):
    return lax.dot_general(left, right, dims, preferred_element_type=F32)


def whole(shape):
    return pl.BlockSpec(shape, lambda *_: (0,) * len(shape), pipeline_mode=pl.Buffered(1))


def sweep(total, step, work):
    def one(i, _):
        work(pl.multiple_of(i * step, step))
        return 0

    lax.fori_loop(0, total // step, one, 0)


def cost(flops, moved, special=0):
    return pl.CostEstimate(flops=flops, bytes_accessed=moved, transcendentals=special)


def lane_ids(rows):
    return lax.broadcasted_iota(jnp.int32, (rows, 128), 1)


def build_keys(sources, slot0, lo_ref, hi_ref, kaug, transposed, low_half):
    per = BLK // TK
    for at, kv in enumerate(sources):

        def one(j, _, at=at, kv=kv):
            rows = pl.ds(pl.multiple_of(j * TK, TK), TK)
            tile = at * (kv.shape[0] // TK) + j
            slot = slot0 + at * (kv.shape[0] // BLK) + j // per
            out = pl.ds(pl.multiple_of(tile * TK, TK), TK)
            rank = lax.broadcasted_iota(jnp.int32, (TK, 128), 0) + lax.rem(j, per) * TK
            inside = (rank >= lo_ref[pl.ds(slot, 1), :]) & (rank < hi_ref[pl.ds(slot, 1), :])
            bias = jnp.where(inside, 0.0, MASKED).astype(BF)
            kaug[out, 0:128] = jnp.where(lane_ids(TK) < 64, bias, kv[rows, 128:256])
            kaug[out, 128:256] = kv[rows, 256:384]
            if low_half:
                transposed[tile] = kv[rows, 0:256].T[0:192]
            else:
                transposed[tile] = kaug[out, :].T[64:256]
            return 0

        lax.fori_loop(0, kv.shape[0] // TK, one, 0)


def stack_queries(q, first, slo_ref, shi_ref, qs):
    lane = lane_ids(TQ)
    spot = lax.broadcasted_iota(jnp.int32, (TQ, 128), 0) + first
    mine = ((spot >= slo_ref[...]) & (spot < shi_ref[...])).astype(F32).astype(BF)
    zero = jnp.zeros((TQ, 128), BF)
    low, high = q[:, 0:128], q[:, 128:256]
    mark = jnp.where(lane < 64, mine, zero)
    qs[0:TQ, 0:128] = jnp.where(lane < 64, mine, low)
    qs[TQ : 2 * TQ, 0:128] = mark
    qs[2 * TQ :, 0:128] = mark
    qs[0:TQ, 128:256] = zero
    qs[TQ : 2 * TQ, 128:256] = jnp.where(lane < 64, high, zero)
    qs[2 * TQ :, 128:256] = jnp.where(lane < 64, zero, high)


def attend_kernel(*refs, slot0, count, resume, last):
    tlo, thi, qfirst, q_ref = refs[:4]
    sources = refs[4 : 4 + count]
    lo_ref, hi_ref, slo_ref, shi_ref = refs[4 + count : 8 + count]
    at = 8 + count
    if resume:
        acc_in, stat_in = refs[at : at + 2]
        at += 2
    if last:
        o_ref, ot_ref, lse_ref = refs[at : at + 3]
        at += 3
    else:
        acc_out, stat_out = refs[at : at + 2]
        at += 2
    kaug, vt, qs, acc, m_s, l_s = refs[at:]
    i = pl.program_id(0)

    @pl.when(i == 0)
    def _():
        build_keys(sources, slot0, lo_ref, hi_ref, kaug, vt, True)

    slots = count * sources[0].shape[0] // BLK
    per = BLK // TK
    stack_queries(q_ref[...], qfirst[i], slo_ref, shi_ref, qs)
    if resume:
        m_s[...] = stat_in[0, 0:1, :]
        l_s[...] = stat_in[0, 1:2, :]
        acc[...] = acc_in[0]
    else:
        m_s[...] = jnp.full_like(m_s, 2 * MASKED)
        l_s[...] = jnp.zeros_like(l_s)
        acc[...] = jnp.zeros_like(acc)

    def slot_loop(s, _):
        def key_loop(t, _):
            tile = s * per + t
            keys = pl.ds(pl.multiple_of(tile * TK, TK), TK)
            st = mm(kaug[keys, :], qs[...], NT)
            m_old = m_s[...]
            m_new = jnp.maximum(m_old, jnp.max(st, axis=0, keepdims=True))
            fade = jnp.exp(m_old - m_new)
            p = jnp.exp(st - m_new)
            l_s[...] = l_s[...] * fade + jnp.sum(p, axis=0, keepdims=True)
            m_s[...] = m_new
            low = p.astype(BF)
            for h in range(3):
                cols = slice(h * TQ, (h + 1) * TQ)
                part = slice(h * HD, (h + 1) * HD)
                acc[part, :] = acc[part, :] * fade[:, cols] + mm(vt[tile, part, :], low[:, cols])
            return 0

        return lax.fori_loop(tlo[i, slot0 + s], thi[i, slot0 + s], key_loop, 0)

    lax.fori_loop(0, slots, slot_loop, 0)
    if last:
        total = l_s[...]
        for h in range(3):
            cols = slice(h * TQ, (h + 1) * TQ)
            part = slice(h * HD, (h + 1) * HD)
            acc[part, :] = acc[part, :] / total[:, cols]
        ot_ref[0] = acc[...]
        o_ref[...] = acc[...].T.astype(BF)
        lse_ref[0] = m_s[...] + jnp.log(total)
    else:
        acc_out[0] = acc[...]
        stat_out[0, 0:1, :] = m_s[...]
        stat_out[0, 1:2, :] = l_s[...]


def rows_spec(shape):
    return pl.BlockSpec((TQ, shape[1]), lambda i, *_: (i, 0))


def tile_spec(shape):
    return pl.BlockSpec((1, *shape[1:]), lambda i, *_: (i, 0, 0))


def attend(tables, q, sources, slot0, state=None, last=False):
    tlo, thi, qfirst, lo, hi, slo, shi = tables
    tiles = q.shape[0] // TQ
    keys = sum(s.shape[0] for s in sources)
    state = tuple(state) if state else ()
    sd = jax.ShapeDtypeStruct
    acc, stat = sd((tiles, 3 * HD, TQ), F32), sd((tiles, 2, 3 * TQ), F32)
    if last:
        o, lse = sd((q.shape[0], 3 * HD), BF), sd((tiles, 1, 3 * TQ), F32)
        outs, out_specs = (o, acc, lse), (rows_spec(o.shape), tile_spec(acc.shape), tile_spec(lse.shape))
    else:
        outs, out_specs = (acc, stat), (tile_spec(acc.shape), tile_spec(stat.shape))
    return pl.pallas_call(
        functools.partial(attend_kernel, slot0=slot0, count=len(sources), resume=bool(state), last=last),
        out_shape=outs,
        grid_spec=pltpu.PrefetchScalarGridSpec(
            num_scalar_prefetch=3,
            grid=(tiles,),
            in_specs=[rows_spec(q.shape)]
            + [whole(x.shape) for x in (*sources, lo, hi, slo, shi)]
            + [tile_spec(x.shape) for x in state],
            out_specs=out_specs,
            scratch_shapes=[
                pltpu.VMEM((keys, 256), BF),
                pltpu.VMEM((keys // TK, 3 * HD, TK), BF),
                pltpu.VMEM((3 * TQ, 256), BF),
                pltpu.VMEM((3 * HD, TQ), F32),
                pltpu.VMEM((1, 3 * TQ), F32),
                pltpu.VMEM((1, 3 * TQ), F32),
            ],
        ),
        compiler_params=pltpu.CompilerParams(vmem_limit_bytes=GRANT),
        cost_estimate=cost(12_000_000_000, 12_000_000, 10_000_000),
        name="attend",
    )(tlo, thi, qfirst, q, *sources, lo, hi, slo, shi, *state)


def attend_back_kernel(
    tlo, thi, qfirst, q_ref, do_ref, ot_ref, lse_ref, kv, lo_ref, hi_ref, slo_ref, shi_ref, dq_ref, *rest,
    slot0, first, cuts,
):
    dkv_refs, rest = rest[:cuts], rest[cuts:]
    if first:
        delta_ref, *rest = rest
    kaug, kt, qs, dos, acc, dk_s, dv_s = rest
    keys_all = kv.shape[0]
    slots = keys_all // BLK
    per = BLK // TK
    i = pl.program_id(0)

    @pl.when(i == 0)
    def _():
        build_keys((kv,), slot0, lo_ref, hi_ref, kaug, kt, False)
        dk_s[...] = jnp.zeros_like(dk_s)
        dv_s[...] = jnp.zeros_like(dv_s)

    stack_queries(q_ref[...], qfirst[i], slo_ref, shi_ref, qs)
    do = do_ref[...]
    lane = lane_ids(TQ)
    zero = jnp.zeros((TQ, 128), BF)
    dos[0:TQ, 0:128] = jnp.where(lane < 64, do[:, 0:128], zero)
    dos[TQ : 2 * TQ, 0:128] = jnp.where(lane < 64, zero, do[:, 0:128])
    dos[2 * TQ :, 0:128] = zero
    dos[0 : 2 * TQ, 128:256] = jnp.zeros((2 * TQ, 128), BF)
    dos[2 * TQ :, 128:192] = do[:, 128:192]
    dos[2 * TQ :, 192:256] = jnp.zeros((TQ, 64), BF)
    if first:
        both = do.astype(F32).T * ot_ref[0]
        delta = jnp.concatenate(
            [jnp.sum(both[h * HD : (h + 1) * HD], axis=0, keepdims=True) for h in range(3)], axis=1
        )
        delta_ref[0] = delta
    else:
        delta = ot_ref[0]
    lse = lse_ref[0]
    acc[...] = jnp.zeros_like(acc)

    def slot_loop(s, _):
        def key_loop(t, _):
            tile = s * per + t
            keys = pl.ds(pl.multiple_of(tile * TK, TK), TK)
            st = mm(kaug[keys, :], qs[...], NT)
            p = jnp.exp(st - lse)
            dp = mm(kv[keys, 0:256], dos[...], NT)
            ds = (p * (dp - delta)).astype(BF)
            dv_s[keys, :] += mm(p.astype(BF), dos[...])
            dk_s[keys, :] += mm(ds, qs[...])
            for h in range(3):
                cols = slice(h * TQ, (h + 1) * TQ)
                acc[(h + 1) * HD : (h + 2) * HD, :] += mm(kt[tile, h * HD : (h + 1) * HD, :], ds[:, cols])
            return 0

        return lax.fori_loop(tlo[i, slot0 + s], thi[i, slot0 + s], key_loop, 0)

    lax.fori_loop(0, slots, slot_loop, 0)
    dq_ref[...] = (acc[...] * HD ** (-0.5)).T.astype(BF)

    @pl.when(i == pl.num_programs(0) - 1)
    def _():
        share = keys_all // cuts
        for j, dkv_ref in enumerate(dkv_refs):

            def write(r, j=j, dkv_ref=dkv_ref):
                at = pl.ds(pl.multiple_of(j * share + r, TK), TK)
                to = pl.ds(r, TK)
                dkv_ref[to, 0:128] = dv_s[at, 0:128].astype(BF)
                dkv_ref[to, 128:256] = jnp.where(lane_ids(TK) < 64, dv_s[at, 128:256], dk_s[at, 0:128]).astype(BF)
                dkv_ref[to, 256:384] = dk_s[at, 128:256].astype(BF)

            sweep(share, TK, write)


def attend_back(tables, q, do, ot, lse, source, slot0, first=False, cuts=1, name="attend_back", size=14_000_000_000):
    tlo, thi, qfirst, lo, hi, slo, shi = tables
    tiles = q.shape[0] // TQ
    keys = source.shape[0]
    sd = jax.ShapeDtypeStruct
    piece = (keys // cuts, source.shape[1])
    outs = (sd(q.shape, BF),) + (sd(piece, BF),) * cuts
    out_specs = (rows_spec(q.shape),) + (whole(piece),) * cuts
    if first:
        outs += (sd(lse.shape, F32),)
        out_specs += (tile_spec(lse.shape),)
    return pl.pallas_call(
        functools.partial(attend_back_kernel, slot0=slot0, first=first, cuts=cuts),
        out_shape=outs,
        grid_spec=pltpu.PrefetchScalarGridSpec(
            num_scalar_prefetch=3,
            grid=(tiles,),
            in_specs=[rows_spec(q.shape), rows_spec(do.shape), tile_spec(ot.shape), tile_spec(lse.shape)]
            + [whole(x.shape) for x in (source, lo, hi, slo, shi)],
            out_specs=out_specs,
            scratch_shapes=[
                pltpu.VMEM((keys, 256), BF),
                pltpu.VMEM((keys // TK, 3 * HD, TK), BF),
                pltpu.VMEM((3 * TQ, 256), BF),
                pltpu.VMEM((3 * TQ, 256), BF),
                pltpu.VMEM((256, TQ), F32),
                pltpu.VMEM((keys, 256), F32),
                pltpu.VMEM((keys, 256), F32),
            ],
        ),
        compiler_params=pltpu.CompilerParams(vmem_limit_bytes=GRANT),
        cost_estimate=cost(size, size // 1000, size // 3000),
        name=name,
    )(tlo, thi, qfirst, q, do, ot, lse, source, lo, hi, slo, shi)


def project_kernel(
    who, x0, x1, x2, x3_top, x3_bottom, w_mine, w_other, bias_ref, chosen, q_ref, kv_ref, up_ref, down_ref, w_ref, held
):
    tall = w_mine.shape[0]
    rows = x0.shape[0]
    w_ref[pl.ds(pl.multiple_of(who[0] * tall, tall), tall), :] = w_mine[...]
    w_ref[pl.ds(pl.multiple_of((1 - who[0]) * tall, tall), tall), :] = w_other[...]
    held[...] = jnp.zeros_like(held)
    for d, x in enumerate((x0, x1, x2, (x3_top, x3_bottom))):
        if d < 3:
            value = mm(x[...], w_ref[...]) + bias_ref[...]
        else:
            value = jnp.concatenate([mm(x[0][...], w_ref[...]), mm(x[1][...], w_ref[...])], axis=0) + bias_ref[...]
        at = slice(d * rows, (d + 1) * rows)
        q_ref[at, :] = (value[:, :256].astype(BF).astype(F32) * HD ** (-0.5)).astype(BF)
        to = pl.ds(pl.multiple_of(who[3 + d], 16), SPAN)
        held[to, :] += mm(chosen[d], value[:, 256:].astype(BF))
    kv_ref[...] = held[0 : 2 * BLK, :].astype(BF)
    down_ref[...] = kv_ref[0:BLK, :]
    up_ref[...] = kv_ref[BLK:, :]


def project(who, xs, w_mine, w_other, bias, chosen):
    sd = jax.ShapeDtypeStruct
    rows, width = xs[0].shape
    cols = w_mine.shape[1]
    ins = (*xs, w_mine, w_other, bias, chosen)
    outs = (
        sd((4 * rows, 256), BF), sd((4 * rows, cols - 256), BF), sd((2 * rows, cols - 256), BF),
        sd((2 * rows, cols - 256), BF), sd((width, cols), BF),
    )
    return pl.pallas_call(
        project_kernel,
        out_shape=outs,
        grid_spec=pltpu.PrefetchScalarGridSpec(
            num_scalar_prefetch=1,
            grid=(1,),
            in_specs=[whole(a.shape) for a in ins],
            out_specs=tuple(whole(a.shape) for a in outs),
            scratch_shapes=[pltpu.VMEM((2 * BLK + 128, cols - 256), F32)],
        ),
        compiler_params=pltpu.CompilerParams(vmem_limit_bytes=24 << 20),
        cost_estimate=cost(3_000_000_000, 12_000_000),
        name="project",
    )(who, *ins)


def row_mean(v):
    return jnp.sum(v, axis=-1, keepdims=True) * (1.0 / v.shape[-1])

def dense_kernel(
    who, o_ref, wo_a, wo_b, win_a, win_b, wback_a, wback_b, x_ref, teacher_ref, cot_ref, keep_ref, vec_ref,
    out_ref, dres_ref, dparts_ref, act_ref, dbr_ref, dpre_ref, hid_ref, dproj_ref, sums_ref,
    wo, win, wback, xh, inv, hidden, gp, acc, sems, *, FB
):
    rows, width = x_ref.shape
    groups = o_ref.shape[0] // rows
    part = width // groups
    units = win.shape[1]
    wo_loads, win_loads, wback_loads = [], [], []
    for i in range(2):
        side = who[0] if i == 0 else 1 - who[0]
        for e in range(groups // 2):
            to = pl.multiple_of(((side * (groups // 2) + e) ^ who[1]) * part, part)
            wo_loads.append(
                pltpu.make_async_copy((wo_a, wo_b)[i].at[pl.ds(e * part, part)], wo.at[pl.ds(to, part)], sems.at[2 * i + e])
            )
        for j, (pieces, target, held) in enumerate((((win_a, win_b), win, win_loads), ((wback_a, wback_b), wback, wback_loads))):
            tall = target.shape[0] // 2
            to = pl.multiple_of(side * tall, tall)
            held.append(pltpu.make_async_copy(pieces[i], target.at[pl.ds(to, tall)], sems.at[4 + 2 * i + j]))
    for load in wo_loads + win_loads + wback_loads:
        load.start()
    b_out, b_in, b_back = vec_ref[0:1, 0:width], vec_ref[1:2, :], vec_ref[2:3, 0:width]
    gain1, shift1, gain2, shift2 = (vec_ref[i : i + 1, 0:width] for i in range(3, 7))
    for load in wo_loads:
        load.wait()
    total = x_ref[...].astype(F32) + b_out
    for i in range(groups):
        total += mm(o_ref[i * rows : (i + 1) * rows, :], wo[i * part : (i + 1) * part, :])
    center = total - row_mean(total)
    scale = lax.rsqrt(row_mean(center * center) + 1e-12)
    inv[...] = scale
    unit = center * scale
    xh[...] = unit
    hid = unit * gain1 + shift1
    hidden[...] = hid
    hid_ref[...] = hid.astype(BF)
    acc[...] = jnp.zeros_like(acc)
    for load in win_loads + wback_loads:
        load.wait()

    def up(n, _):
        cols = pl.ds(pl.multiple_of(n * FB, FB), FB)
        pre = mm(hid_ref[...], win[:, cols]) + vec_ref[1:2, cols]
        cdf = 0.5 + 0.5 * lax.erf(pre * 0.7071067811865476)
        act = (pre * cdf).astype(BF)
        act_ref[:, cols] = act
        gp[:, cols] = cdf + pre * (jnp.exp(pre * pre * -0.5) * 0.3989422804014327)
        acc[...] += mm(act, wback[cols, :])
        return 0

    lax.fori_loop(0, units // FB, up, 0, unroll=False)
    total = hidden[...] + acc[...] + b_back
    center = total - row_mean(total)
    scale = lax.rsqrt(row_mean(center * center) + 1e-12)
    unit = center * scale
    result = unit * gain2 + shift2
    out_ref[...] = result.astype(BF)
    grad = cot_ref[...].astype(F32) + keep_ref[...] * (result - teacher_ref[...].astype(F32))
    def put(row, value):
        sums_ref[row : row + 1, 0 : value.shape[1]] = value
    put(5, jnp.sum(grad * unit, axis=0, keepdims=True))
    put(6, jnp.sum(grad, axis=0, keepdims=True))
    grad = grad * gain2
    back = scale * (grad - row_mean(grad) - unit * row_mean(grad * unit))
    acc[...] = back
    low = back.astype(BF)
    dbr_ref[...] = low
    put(2, jnp.sum(low.astype(F32), axis=0, keepdims=True))

    def down(n, _):
        cols = pl.ds(pl.multiple_of(n * FB, FB), FB)
        dpre = (mm(dbr_ref[...], wback[cols, :], NT) * gp[:, cols]).astype(BF)
        dpre_ref[:, cols] = dpre
        sums_ref[1:2, cols] = jnp.sum(dpre.astype(F32), axis=0, keepdims=True)
        acc[...] += mm(dpre, win[:, cols], NT)
        return 0

    lax.fori_loop(0, units // FB, down, 0, unroll=False)
    grad = acc[...]
    unit = xh[...]
    put(3, jnp.sum(grad * unit, axis=0, keepdims=True))
    put(4, jnp.sum(grad, axis=0, keepdims=True))
    grad = grad * gain1
    back = inv[...] * (grad - row_mean(grad) - unit * row_mean(grad * unit))
    dres_ref[...] = back
    low = back.astype(BF)
    dproj_ref[...] = low
    put(0, jnp.sum(low.astype(F32), axis=0, keepdims=True))
    for i in range(groups):
        dparts_ref[i * rows : (i + 1) * rows, :] = mm(low, wo[i * part : (i + 1) * part, :], NT).astype(BF)


def dense(who, o, weights, x, teacher, cot, keep, vec):
    rows, width = x.shape
    units = vec.shape[1]
    sd = jax.ShapeDtypeStruct
    outs = (
        sd((rows, width), BF), sd((rows, width), F32), sd(o.shape, BF), sd((rows, units), BF), sd((rows, width), BF),
        sd((rows, units), BF), sd((rows, width), BF), sd((rows, width), BF), sd((8, units), F32),
    )
    ins = (o, *weights, x, teacher, cot, keep, vec)
    stay = pl.BlockSpec(memory_space=pl.ANY)
    return pl.pallas_call(
        functools.partial(dense_kernel, FB=FFB),
        out_shape=outs,
        grid_spec=pltpu.PrefetchScalarGridSpec(
            num_scalar_prefetch=1,
            grid=(1,),
            in_specs=[whole(o.shape)] + [stay] * 6 + [whole(a.shape) for a in ins[7:]],
            out_specs=tuple(whole(a.shape) for a in outs),
            scratch_shapes=[
                pltpu.VMEM((width, width), BF), pltpu.VMEM((width, units), BF), pltpu.VMEM((units, width), BF),
                pltpu.VMEM((rows, width), F32), pltpu.VMEM((rows, 1), F32), pltpu.VMEM((rows, width), F32),
                pltpu.VMEM((rows, units), F32), pltpu.VMEM((rows, width), F32), pltpu.SemaphoreType.DMA((8,)),
            ],
        ),
        compiler_params=pltpu.CompilerParams(vmem_limit_bytes=GRANT),
        cost_estimate=cost(12_000_000_000, 30_000_000, 4_000_000),
        name="dense",
    )(who, *ins)


def finish_kernel(
    who, dq0, dq1, dq2, dq3, own_ref, pair_ref, left_ref, right_ref, turn_ref, w_ref,
    all_ref, sums_ref, dx_ref, gx_ref, gy_ref, next_left, next_right, held,
):
    d = pl.program_id(0)
    rows, width = dx_ref.shape
    cut = width // 2

    @pl.when(d == 0)
    def _():
        sums_ref[...] = jnp.zeros_like(sums_ref)
        held[2 * BLK :, :] = jnp.zeros((held.shape[0] - 2 * BLK, held.shape[1]), BF)
        for base, extra in ((0, left_ref), (BLK, right_ref)):

            def gather(r, base=base, extra=extra):
                at = pl.ds(pl.multiple_of(base + r, 128), 128)
                value = own_ref[at, :].astype(F32) + pair_ref[at, :].astype(F32)
                held[at, :] = (value + extra[pl.ds(r, 128), :].astype(F32)).astype(BF)

            sweep(BLK, 128, gather)

    tok = mm(turn_ref[0], held[pl.ds(pl.multiple_of(who[3 + d], 16), SPAN), :]).astype(BF)
    dq = sum(ref[...].astype(F32) for ref in (dq0, dq1, dq2, dq3)).astype(BF)
    all_ref[:, 0:256] = dq
    all_ref[:, 256:640] = tok
    sums_ref[0:1, 0:256] += jnp.sum(dq.astype(F32), axis=0, keepdims=True)
    sums_ref[0:1, 256:640] += jnp.sum(tok.astype(F32), axis=0, keepdims=True)
    part = mm(all_ref[...], w_ref[...], NT).astype(BF)

    @pl.when(d == 0)
    def _():
        dx_ref[...] = part

    @pl.when(d == 1)
    def _():
        gx_ref[0:rows, :] = part[:, :cut]
        next_right[...] = part[:, cut:]

    @pl.when(d == 2)
    def _():
        next_left[...] = part[:, :cut]
        gy_ref[0:rows, :] = part[:, cut:]

    @pl.when(d == 3)
    def _():
        gx_ref[rows:, :] = part[:, :cut]
        gy_ref[rows:, :] = part[:, cut:]


def finish(who, dqs, own, pair, left, right, turn, w_heads):
    sd = jax.ShapeDtypeStruct
    rows, width = turn.shape[1], w_heads.shape[0]
    cols = dqs[0].shape[1] + own.shape[1]
    ins = (*dqs, own, pair, left, right, turn, w_heads)
    shapes = ((rows, width), (2 * rows, width // 2), (2 * rows, width // 2), (rows, width // 2), (rows, width // 2))
    outs = (sd((4 * rows, cols), BF), sd((8, cols), F32)) + tuple(sd(s, BF) for s in shapes)

    def by_block(shape):
        return pl.BlockSpec((rows, shape[1]), lambda d, *_: (d, 0))

    return pl.pallas_call(
        finish_kernel,
        out_shape=outs,
        grid_spec=pltpu.PrefetchScalarGridSpec(
            num_scalar_prefetch=1,
            grid=(4,),
            in_specs=[by_block(a.shape) for a in ins[:4]]
            + [whole(a.shape) for a in ins[4:8]]
            + [pl.BlockSpec((1, *turn.shape[1:]), lambda d, *_: (d, 0, 0)), whole(w_heads.shape)],
            out_specs=(by_block(outs[0].shape), whole(outs[1].shape)) + tuple(whole(s) for s in shapes),
            scratch_shapes=[pltpu.VMEM((2 * BLK + 128, own.shape[1]), BF)],
        ),
        compiler_params=pltpu.CompilerParams(vmem_limit_bytes=GRANT),
        cost_estimate=cost(3_000_000_000, 16_000_000),
        name="finish",
    )(who, *ins)


def part_out(who, held, am, ao, bm, bo, sides):
    part = am.shape[0]
    for mine, other, side, base in ((am, ao, sides[0], 0), (bm, bo, sides[1], 2 * part)):

        def move(r, mine=mine, other=other, side=side, base=base):
            mine[pl.ds(r, 16), :] = held[pl.ds(pl.multiple_of(base + side * part + r, 16), 16), :]
            other[pl.ds(r, 16), :] = held[pl.ds(pl.multiple_of(base + (1 - side) * part + r, 16), 16), :]

        sweep(part, 16, move)


def plus(left, right, at):
    return (left[at, :].astype(F32) + right[at, :].astype(F32)).astype(BF)


def first_kernel(who, back_a, back_b, in_a, in_b, out_a, out_b, am, ao, bm, bo, held):
    width = back_a.shape[1]
    tall = in_a.shape[0]

    def upper(r):
        at = pl.ds(r, 16)
        for k in range(4):
            held[at, k * width : (k + 1) * width] = plus(back_a, back_b, pl.ds(pl.multiple_of(k * tall + r, 16), 16))
        held[pl.ds(pl.multiple_of(tall + r, 16), 16), :] = plus(in_a, in_b, at)

    def lower(r):
        held[pl.ds(pl.multiple_of(2 * tall + r, 16), 16), :] = plus(out_a, out_b, pl.ds(r, 16))

    sweep(tall, 16, upper)
    sweep(out_a.shape[0], 16, lower)
    part_out(who, held, am, ao, bm, bo, (lax.rem(who[1], 2), who[1] // 2))


def both_kernel(who, a_mine, a_got, b_mine, b_got, both):
    del who
    part = a_mine.shape[0]

    def work(r):
        both[pl.ds(r, 16), :] = plus(a_mine, a_got, pl.ds(r, 16))
        both[pl.ds(pl.multiple_of(part + r, 16), 16), :] = plus(b_mine, b_got, pl.ds(r, 16))

    sweep(part, 16, work)


def second_kernel(who, a_mine, a_got, b_mine, b_got, am, ao, bm, bo, held):
    both_kernel(who, a_mine, a_got, b_mine, b_got, held)
    part_out(who, held, am, ao, bm, bo, (who[1] // 2, lax.rem(who[1], 2)))


def join_kernel(who, a, b, c, d, back_ref, in_ref, out_ref, vec_ref, held):
    step = pl.program_id(0)

    @pl.when(step == 0)
    def _():
        gather_pieces(who, (a, b, c, d), held)

    tall = held.shape[0] - 128
    tall, width = tall // 2, back_ref.shape[1]
    cols = pl.ds(pl.multiple_of(step * width, 128), width)
    back_ref[...] = held[0:tall, cols].astype(F32)
    rows = in_ref.shape[0]
    in_ref[...] = held[pl.ds(pl.multiple_of(tall + step * rows, 16), rows), :].astype(F32)

    @pl.when(step < 3)
    def _():
        out_ref[...] = held[2 * tall :, cols].astype(F32)

    @pl.when(step == 3)
    def _():
        vec_ref[...] = held[2 * tall : 2 * tall + 16, 3 * width :].astype(F32)


def gather_pieces(who, pieces, held):
    s1, s2 = lax.rem(who[1], 2), who[1] // 2
    part = pieces[0].shape[0] // 2
    for at, ref in enumerate(pieces):
        color, i = at // 2, at % 2
        for j in range(2):
            spot = (s1 ^ i) * 2 + (s2 ^ j) if color == 0 else 4 + (s2 ^ i) * 2 + (s1 ^ j)

            def move(r, spot=spot, ref=ref, j=j):
                frm = pl.ds(pl.multiple_of(j * part + r, 16), 16)
                held[pl.ds(pl.multiple_of(spot * part + r, 16), 16), :] = ref[frm, :]

            sweep(part, 16, move)

def join(who, pieces, back, first, out, total):
    sd = jax.ShapeDtypeStruct
    tall, width = first[0], back[1]
    outs = (sd(back, F32), sd(first, F32), sd(out, F32), sd((16, width), F32))
    return pl.pallas_call(
        join_kernel,
        out_shape=outs,
        grid_spec=pltpu.PrefetchScalarGridSpec(
            num_scalar_prefetch=1,
            grid=(4,),
            in_specs=[whole(a.shape) for a in pieces],
            out_specs=(
                pl.BlockSpec((tall, width), lambda k, *_: (k, 0)),
                pl.BlockSpec((tall // 4, first[1]), lambda k, *_: (k, 0)),
                pl.BlockSpec((128, width), lambda k, *_: (jnp.minimum(k, 2), 0)),
                whole((16, width)),
            ),
            scratch_shapes=[pltpu.VMEM((total, first[1]), BF)],
        ),
        compiler_params=pltpu.CompilerParams(vmem_limit_bytes=GRANT),
        cost_estimate=cost(1_000_000, 16_000_000),
        name="join",
    )(who, *pieces)


def small_call(kernel, who, pieces, outs, scratch, name, grant=24 << 20):
    return pl.pallas_call(
        kernel,
        out_shape=tuple(jax.ShapeDtypeStruct(*s) for s in outs),
        grid_spec=pltpu.PrefetchScalarGridSpec(
            num_scalar_prefetch=1,
            grid=(1,),
            in_specs=[whole(a.shape) for a in pieces],
            out_specs=tuple(whole(s[0]) for s in outs),
            scratch_shapes=scratch,
        ),
        compiler_params=pltpu.CompilerParams(vmem_limit_bytes=grant),
        cost_estimate=cost(1_000_000, 9_000_000),
        name=name,
    )(who, *pieces)


def heads_kernel(who, in_ref, q_ref, k_ref, v_ref, bias_ref):
    tall = in_ref.shape[1]
    for c in range(in_ref.shape[0] // 4):
        at = slice(c * tall, (c + 1) * tall)
        for a in range(4):
            cols = slice(a * 192, (a + 1) * 192)
            block = in_ref[c * 4 + (who[1] ^ a)].astype(F32)
            q_ref[at, cols] = block[:, 64:256]
            v_ref[at, cols] = block[:, 256:448]
            k_ref[at, cols] = block[:, 448:640]
            if c == 0:
                for k in range(3):
                    spot = slice(a * 192 + k * 64, a * 192 + (k + 1) * 64)
                    bias_ref[0:1, spot] = block[k : k + 1, 0:64]
                    bias_ref[8:9, spot] = block[k + 3 : k + 4, 0:64]


def heads_out(who, gathered):
    outs = (((384, 768), F32),) * 3 + (((16, 768), F32),)
    return small_call(heads_kernel, who, (gathered,), outs, [], "heads_out")


def swap(block, axis="fsdp"):
    return lax.ppermute(block, axis, [(0, 1), (1, 0)])


def shifted(block, axis, distance):
    devices = range(lax.axis_size(axis))
    route = [(i - distance, i) for i in devices if i - distance in devices]
    return lax.ppermute(block, axis, route)


def flip(block, bit, axis="uly"):
    return lax.ppermute(block, axis, [(i, i ^ bit) for i in range(lax.axis_size(axis))])


def exchange(rows, axis):
    return lax.all_to_all(rows, axis, split_axis=0, concat_axis=0, tiled=True)


def spread_rows(rows, axis):
    count = lax.axis_size(axis)
    return exchange(jnp.broadcast_to(rows[None], (count, *rows.shape)).reshape(-1, rows.shape[1]), axis)


def sum_parts(rows, count):
    got = rows.reshape(count, -1, rows.shape[1])
    return sum(got[i].astype(F32) for i in range(count)).astype(BF)


def sum_scatter(rows, axis):
    return sum_parts(exchange(rows, axis), lax.axis_size(axis))


def add(left, right):
    return (left.astype(F32) + right.astype(F32)).astype(BF)


def line_step(held, bit):
    return flip(held, bit, "ctx")


def line_join(held, got, bit):
    low = (lax.axis_index("ctx") & bit) == 0
    return jnp.stack([jnp.where(low, held, got), jnp.where(low, got, held)], axis=1).reshape(-1, *held.shape[1:])


def line_rest(held, bit):
    while bit > 0:
        held = line_join(held, line_step(held, bit), bit)
        bit //= 2
    return held.reshape(-1, held.shape[2])


def chunks_of(rows, axis):
    count, me = lax.axis_size(axis), lax.axis_index(axis)
    split = rows.reshape(count, -1, rows.shape[1])
    picked = [lax.dynamic_index_in_dim(split, me ^ k, 0, keepdims=False) for k in range(count)]
    return [picked[0]] + [flip(picked[k], k, axis) for k in range(1, count)]


def tie(*values):
    return lax.optimization_barrier(values)


def on_device(
    tokens, teacher, cotangent, valid, teacher_ok, doc_starts, w_query, w_key, w_value, w_out, w_in, w_back,
    bias_query, bias_value, bias_out, bias_in, bias_back, norm1_gain, norm1_bias, norm2_gain, norm2_bias,
):
    groups = lax.axis_size("uly")
    spans = lax.axis_size("ctx")
    rows, width = tokens.shape
    block = rows * groups * 2
    stream = block * spans
    ctx_index = lax.axis_index("ctx")
    uly = lax.axis_index("uly")
    half = lax.axis_index("fsdp")
    head_cols = width // groups
    shard = w_query.shape[0]
    upper = uly // 2

    small = (bias_query, bias_value, bias_out, bias_in, bias_back, norm1_gain, norm1_bias, norm2_gain, norm2_bias)
    valid_one = valid[None, :]
    valid_own = jnp.concatenate([valid_one, flip(valid_one, 1), flip(valid_one, 2), flip(valid_one, 3)], axis=0)
    x_own, valid_own, *small = tie(tokens, valid_own, *small)
    x_x, x_y = flip(x_own, 1), flip(x_own, 2)
    valid_pair = swap(valid_own)
    place = jnp.arange(groups, dtype=jnp.int32)
    in_plane = place ^ uly
    valid_mine = jnp.take(valid_own, in_plane, axis=0).reshape(2, BLK)
    valid_next = jnp.take(valid_pair, in_plane, axis=0).reshape(2, BLK)
    from_low = shifted(jnp.stack([valid_mine[1], valid_next[1]]), "ctx", 1)
    from_high = shifted(jnp.stack([valid_mine[0], valid_next[0]]), "ctx", -1)
    block_valid = jnp.concatenate(
        [valid_mine, valid_next, from_low[:1], from_high[:1], from_low[1:], from_high[1:]], axis=0
    )
    count = jnp.full((8, 128), jnp.sum(valid_mine) + jnp.sum(valid_next), jnp.int32)

    start_col = uly * head_cols
    cut = [lax.dynamic_slice_in_dim(w, start_col, head_cols, 1) for w in (w_query, w_value, w_key)]
    w_mine = jnp.concatenate([jnp.zeros((shard, 256 - head_cols), BF), *cut], axis=1)
    w_other = swap(w_mine)
    packed = jnp.concatenate(small)
    packed_pair = swap(packed)
    first, second = jnp.where(half == 0, packed, packed_pair), jnp.where(half == 0, packed_pair, packed)
    vectors = []
    at = 0
    for p in small:
        n = p.shape[0]
        vectors.append(jnp.concatenate([first[at : at + n], second[at : at + n]]).astype(F32))
        at += n
    bq_all, bv_all = vectors[:2]
    vec = jnp.stack([jnp.pad(v, (0, w_in.shape[1] - v.shape[0])) for v in vectors[2:]] + [jnp.zeros((w_in.shape[1],), F32)])
    bias_heads = jnp.concatenate(
        [
            jnp.zeros((256 - head_cols,), F32),
            lax.dynamic_slice_in_dim(bq_all, start_col, head_cols, 0),
            lax.dynamic_slice_in_dim(bv_all, start_col, head_cols, 0),
            jnp.zeros((head_cols,), F32),
        ]
    )

    step = jnp.asarray([0, 0, 0, 0, -1, 1, -1, 1], jnp.int32)
    side = jnp.asarray([0, 1, 0, 1, 1, 0, 1, 0], jnp.int32)
    swapped = jnp.asarray([0, 0, 1, 1, 0, 0, 1, 1], jnp.int32)
    inner = jnp.arange(BLK, dtype=jnp.int32)
    first_block = (ctx_index + step) * (2 * groups) + side * groups + (half ^ swapped)
    spot = (first_block[:, None] + 2 * (inner // rows)[None, :]) * rows + lax.rem(inner, rows)[None, :]
    x_x, x_y, block_valid = tie(x_x, x_y, block_valid)
    edges = jnp.concatenate([doc_starts, jnp.full((DOCS + 1,), stream, jnp.int32)])
    window_first = jnp.maximum(ctx_index * block - block // 2, 0)
    first_doc = jnp.sum((doc_starts <= window_first).astype(jnp.int32)) - 1
    near = lax.dynamic_slice_in_dim(edges, first_doc, DOCS + 1, 0)
    tiles = groups * rows // TQ
    per = rows // TQ
    tile_ids = jnp.arange(tiles, dtype=jnp.int32)
    qfirst = ctx_index * block + (((tile_ids // per) ^ uly) * 2 + half) * rows + lax.rem(tile_ids, per) * TQ
    q_lo = jnp.max(jnp.where(near[None, :] <= qfirst[:, None], near[None, :], 0), axis=1)
    q_hi = jnp.min(jnp.where(near[None, :] <= qfirst[:, None] + TQ - 1, stream, near[None, :]), axis=1)
    limits = jnp.concatenate([near, q_lo, q_hi])
    counted = jnp.sum(block_valid[:, None, :] * (spot[:, None, :] < limits[None, :, None]), axis=-1)
    bounds = counted[:, : DOCS + 1]
    cnt_lo = counted[:, DOCS + 1 : DOCS + 1 + tiles].T
    cnt_hi = counted[:, DOCS + 1 + tiles :].T
    pad64 = jnp.zeros((bounds.shape[0], 128 - DOCS), jnp.int32)
    lo_tab = jnp.concatenate([bounds[:, :DOCS], pad64], axis=1)
    hi_tab = jnp.concatenate([bounds[:, 1:], pad64], axis=1)
    slo_tab = jnp.concatenate([near[:DOCS], pad64[0]])[None, :]
    shi_tab = jnp.concatenate([near[1:], pad64[0]])[None, :]
    some = cnt_hi > cnt_lo
    tlo = jnp.where(some, cnt_lo // TK, 0)
    thi = jnp.where(some, (cnt_hi + TK - 1) // TK, 0)
    tables = (tlo, thi, qfirst, lo_tab, hi_tab, slo_tab, shi_tab)
    before = mm(valid_own.astype(BF), (jnp.arange(rows)[:, None] < jnp.arange(rows)[None, :]).astype(BF)).astype(jnp.int32)
    filled = jnp.sum(valid_own, axis=1)
    shift = jnp.where(lax.rem(in_plane, 2) == 1, jnp.take(filled, place ^ 1), 0)
    base = (in_plane // 2) * BLK + (shift // 16) * 16
    goes_to = jnp.where(valid_own > 0, before + lax.rem(shift, 16)[:, None], 2 * BLK)
    ranks = jnp.arange(SPAN, dtype=jnp.int32)
    chosen = (goes_to[:, None, :] == ranks[None, :, None]).astype(BF)
    who = jnp.concatenate([jnp.stack([half, uly, upper]).astype(jnp.int32), base])

    x_x, x_y, w_other = tie(x_x, x_y, w_other)
    x_top, x_bottom = flip(x_y[: rows // 2], 1), flip(x_x[rows // 2 :], 2)
    x_top, x_bottom, chosen, bias_heads, vec, *tables = tie(x_top, x_bottom, chosen, bias_heads, vec, *tables)

    q_low, kv_own, kv_up, kv_down, w_heads = project(
        who, (tokens, x_x, x_y, x_top, x_bottom), w_mine, w_other, bias_heads[None, :], chosen
    )
    kv_from_left, kv_from_right = shifted(kv_up, "ctx", 1), shifted(kv_down, "ctx", -1)
    w_out, w_in, w_back, kv_own = tie(w_out, w_in, w_back, kv_own)
    wo_pair, win_pair, wback_pair = swap(w_out), swap(w_in), swap(w_back)
    kv_pair = swap(kv_own)
    state = attend(tables, q_low, (kv_own, kv_pair), 0)
    kv_from_left, kv_from_right, wo_pair, win_pair, wback_pair, count, *state = tie(
        kv_from_left, kv_from_right, wo_pair, win_pair, wback_pair, count, *state
    )
    pair_left, pair_right = swap(kv_from_left), swap(kv_from_right)
    bit = 1
    while bit < spans:
        count = count + flip(count, bit, "ctx")
        bit *= 2
    count = count[0, 0].astype(F32)
    loss_scale = jnp.float32(stream) / count
    keep = (loss_scale * (valid * teacher_ok).astype(F32))[:, None]
    o_heads, o_turned, lse = attend(
        tables, q_low, (kv_from_left, kv_from_right, pair_left, pair_right), 4, state, last=True
    )
    o_rel = o_heads.reshape(groups, rows, head_cols)
    o_rest = [flip(o_rel[d], d) for d in range(1, groups)]
    o_heads, x_late, goes_late, x_x, x_y, x_top, x_bottom = tie(o_heads, tokens, goes_to, x_x, x_y, x_top, x_bottom)
    turned = (goes_late[:, :, None] == ranks[None, None, :]).astype(BF)
    x_all = jnp.concatenate([x_late, x_x, x_y, x_top, x_bottom], axis=0)

    kv_halo = jnp.concatenate([kv_from_left, kv_from_right], axis=0)
    kv_halo_pair = jnp.concatenate([pair_left, pair_right], axis=0)
    x_all, turned, kv_halo, kv_halo_pair, *o_rest = tie(x_all, turned, kv_halo, kv_halo_pair, *o_rest)
    o_all = jnp.concatenate([o_rel[0], *o_rest], axis=0)

    out, d_resid1, d_parts, act, d_branch, d_pre, hidden_low, d_proj, sums = dense(
        who, o_all, (w_out, wo_pair, w_in, win_pair, w_back, wback_pair), tokens, teacher, cotangent, keep, vec
    )
    d_rel = d_parts.reshape(groups, rows, head_cols)
    tall = w_back.shape[0]
    vector_rows = jnp.concatenate(
        [sums[i, :width].reshape(2, -1) for i in (0, 2, 3, 4, 5, 6)] + [sums[1].reshape(2, -1)], axis=1
    ).reshape(2, -1, width)
    vector_rows = jnp.pad(vector_rows, ((0, 0), (0, 128 - vector_rows.shape[1]), (0, 0))).astype(BF)
    o_rows = o_all.reshape(groups, rows, head_cols)

    def back_part(side):
        return mm(lax.dynamic_slice_in_dim(act, side * tall, tall, 1), d_branch, TN).astype(BF)

    def in_part(side):
        return mm(lax.dynamic_slice_in_dim(hidden_low, side * shard, shard, 1), d_pre, TN).astype(BF)

    def out_part(side):
        both = [
            mm(lax.dynamic_index_in_dim(o_rows, (2 * side + e) ^ uly, 0, keepdims=False), d_proj, TN).astype(BF)
            for e in range(2)
        ]
        stack = jnp.concatenate([*both, lax.dynamic_index_in_dim(vector_rows, side, 0, keepdims=False)], axis=0)
        return jnp.concatenate([stack[i * 128 : (i + 1) * 128] for i in range(4)], axis=1)

    d_rest = [flip(d_rel[d], d) for d in range(1, groups)]
    back_got, in_got, out_got, *d_rest = tie(back_part(1 - half), in_part(1 - half), out_part(1 - half), *d_rest)
    back_got, in_got, out_got = swap(back_got), swap(in_got), swap(out_got)
    back_mine, in_mine, out_mine = back_part(half), in_part(half), out_part(half)
    back_got, in_got, out_got, back_mine, in_mine, out_mine = tie(
        back_got, in_got, out_got, back_mine, in_mine, out_mine
    )
    wide = w_in.shape[1]
    total = 2 * shard + 128
    am, ao, bm, bo = small_call(
        first_kernel, who, (back_mine, back_got, in_mine, in_got, out_mine, out_got),
        (((total // 4, wide), BF),) * 4, [pltpu.VMEM((total, wide), BF)], "first_stage",
    )
    d_heads = jnp.concatenate([d_rel[0], *d_rest], axis=0)
    d_heads, am, ao, bm, bo = tie(d_heads, am, ao, bm, bo)

    ag, bg = flip(ao, 1), flip(bo, 2)
    args = (tables, q_low, d_heads, o_turned, lse)
    dq0, got_lo, got_hi, delta = attend_back(
        *args, kv_halo_pair, 6, first=True, cuts=2, name="back_halo_pair"
    )
    got_lo, got_hi, delta = tie(got_lo, got_hi, delta)
    args = (tables, q_low, d_heads, delta, lse)
    got_lo, got_hi = swap(got_lo), swap(got_hi)
    dq1, halo_lo, halo_hi = attend_back(*args, kv_halo, 4, cuts=2, name="back_halo", size=1_000_000)
    halo_lo, halo_hi, got_lo, got_hi = tie(halo_lo, halo_hi, got_lo, got_hi)
    halo_lo, halo_hi = add(halo_lo, got_lo), add(halo_hi, got_hi)
    halo_lo, halo_hi, ag, bg = tie(halo_lo, halo_hi, ag, bg)

    am, ao, bm, bo = small_call(
        second_kernel, who, (am, ag, bm, bg), (((total // 8, wide), BF),) * 4,
        [pltpu.VMEM((total // 2, wide), BF)], "second_stage", 12 << 20,
    )
    halo_lo, halo_hi, delta, am, ao, bm, bo = tie(halo_lo, halo_hi, delta, am, ao, bm, bo)
    args = (tables, q_low, d_heads, delta, lse)
    ag, bg = flip(ao, 2), flip(bo, 1)
    from_left, from_right = shifted(halo_hi, "ctx", 1), shifted(halo_lo, "ctx", -1)
    dq2, dkv_pair = attend_back(*args, kv_pair, 2, name="back_pair")
    dkv_pair, ag, bg, from_left, from_right = tie(dkv_pair, ag, bg, from_left, from_right)

    (line,) = small_call(both_kernel, who, (am, ag, bm, bg), (((total // 4, wide), BF),), [], "third_stage", 12 << 20)
    line, dkv_pair, delta = tie(line, dkv_pair, delta)
    args = (tables, q_low, d_heads, delta, lse)
    line = exchange(line, "ctx")
    pair_got = swap(dkv_pair)
    dq3, dkv_own = attend_back(*args, kv_own, 0, name="back_own")
    dkv_own, line, pair_got = tie(dkv_own, line, pair_got)
    line = sum_parts(line, spans)
    line, dkv_own = tie(line, dkv_own)
    line = spread_rows(line, "ctx")

    d_all, d_sums, dx_own, give_x, give_y, left_next, right_next = finish(
        who, (dq0, dq1, dq2, dq3), dkv_own, pair_got, from_left, from_right, turned, w_heads
    )
    d_all, give_x, give_y = tie(d_all, give_x, give_y)
    give_x, give_y = flip(give_x, 1), flip(give_y, 2)
    corner = d_sums[0, 64:].reshape(9, 64)

    def heads_part(side):
        grad = mm(lax.dynamic_slice_in_dim(x_all, side * shard, shard, 1), d_all, TN)
        return lax.dynamic_update_slice(grad, corner, (0, 0)).astype(BF)

    heads_other = heads_part(1 - half)
    heads_got = swap(heads_other)
    heads_mine = heads_part(half)
    heads_sum = add(heads_mine, heads_got)
    line, give_x, give_y, *heads_parts = tie(line, give_x, give_y, *chunks_of(heads_sum, "ctx"))
    heads_sum = sum(part.astype(F32) for part in heads_parts).astype(BF)
    a_near, b_near = line[: total // 8], line[total // 8 :]
    a_got, b_got, *heads_rest = tie(
        flip(a_near, 2), flip(b_near, 1), *[flip(heads_sum, d) for d in range(1, groups)]
    )
    a_near = jnp.concatenate([a_near, a_got], axis=0)
    b_near = jnp.concatenate([b_near, b_got], axis=0)
    a_far, b_far = flip(a_near, 1), flip(b_near, 2)
    left_next = flip(add(left_next, give_x[rows:]), 2)
    right_next = flip(add(right_next, give_y[rows:]), 1)
    heads_sum = jnp.concatenate([heads_sum, *heads_rest], axis=0)
    heads_all = spread_rows(heads_sum, "ctx").reshape(spans * groups, -1, heads_sum.shape[1])
    grad_in = d_resid1 + dx_own.astype(F32)
    grad_in = grad_in + jnp.concatenate([give_x[:rows].astype(F32), give_y[:rows].astype(F32)], axis=1)
    grad_in = grad_in + jnp.concatenate([left_next.astype(F32), right_next.astype(F32)], axis=1)
    g_back, g_in, g_out, g_vec = join(
        who, (a_near, a_far, b_near, b_far), w_back.shape, w_in.shape, w_out.shape, total
    )
    g_query, g_key, g_value, g_bias = heads_out(who, heads_all)
    g_bias_q = lax.dynamic_slice_in_dim(g_bias[0], half * shard, shard, 0)
    g_bias_v = lax.dynamic_slice_in_dim(g_bias[8], half * shard, shard, 0)
    flat = g_vec.reshape(-1)
    g_bo, g_bb, g_g1, g_s1, g_g2, g_s2 = [flat[i * shard : (i + 1) * shard] for i in range(6)]
    g_bin = flat[6 * shard : 6 * shard + bias_in.shape[0]]
    return (
        out, grad_in, g_query, g_key, g_value, g_out, g_in, g_back,
        g_bias_q, g_bias_v, g_bo, g_bin, g_bb, g_g1, g_s1, g_g2, g_s2,
    )


def solution(mesh):
    placed = (
        P(("ctx", "uly", "fsdp"), None),
        P(("ctx", "uly", "fsdp"), None),
        P(("ctx", "uly", "fsdp"), None),
        P(("ctx", "uly", "fsdp")),
        P(("ctx", "uly", "fsdp")),
        P(),
        P("fsdp", None),
        P("fsdp", None),
        P("fsdp", None),
        P("fsdp", None),
        P("fsdp", None),
        P("fsdp", None),
        P("fsdp"),
        P("fsdp"),
        P("fsdp"),
        P("fsdp"),
        P("fsdp"),
        P("fsdp"),
        P("fsdp"),
        P("fsdp"),
        P("fsdp"),
    )
    return jax.shard_map(
        on_device,
        mesh=mesh,
        in_specs=placed,
        out_specs=(
            P(("ctx", "uly", "fsdp"), None),
            P(("ctx", "uly", "fsdp"), None),
            P("fsdp", None),
            P("fsdp", None),
            P("fsdp", None),
            P("fsdp", None),
            P("fsdp", None),
            P("fsdp", None),
            P("fsdp"),
            P("fsdp"),
            P("fsdp"),
            P("fsdp"),
            P("fsdp"),
            P("fsdp"),
            P("fsdp"),
            P("fsdp"),
            P("fsdp"),
        ),
        check_vma=False,
    )
```
